32 devices in a mesh: dp: 4 (over y, x), depth: 4 (over z), mp: 2 (over core).
Axes of the slice: x: 2, y: 2, z: 4, core: 2. Of those that a mesh axis runs over, the one named last changes fastest.
Arguments:
- history: bfloat16 [20, 8192, 2048], P('depth', 'dp', 'mp'), may hold values from -6 to 6
- slot_layer: int32 [20], P('depth'), may hold values from 0 to 18, as said below
- current: bfloat16 [8192, 2048], P(('dp', 'depth')), may hold values from -6 to 6
- positions: int32 [8192], P(('dp', 'depth')), may hold values from 0 to 1023, as said below
- doc_ids: int32 [8192], P('dp'), may hold values from 0 to 8191, as said below
- cotangent: bfloat16 [8192, 2048], P(('dp', 'depth'), 'mp'), may hold values from -6 to 6
- norm_gains: bfloat16 [5, 2048], P(None, ('dp', 'depth')), may hold values from 0.5 to 1.5
- generator_in: bfloat16 [2048, 72], P(('dp', 'depth')), may hold values from -0.125 to 0.125
- generator_out: bfloat16 [5184], P(('dp', 'depth')), may hold values from -0.75 to 0.75
- query_weight: bfloat16 [2048, 2048], P(('dp', 'depth'), 'mp'), may hold values from -0.125 to 0.125
- key_weight: bfloat16 [2048, 2048], P(('dp', 'depth'), 'mp'), may hold values from -0.125 to 0.125
- value_weight: bfloat16 [2048, 2048], P(('dp', 'depth'), 'mp'), may hold values from -0.125 to 0.125
- out_weight: bfloat16 [2048, 2048], P('mp', ('dp', 'depth')), may hold values from -0.75 to 0.75
- up_weight: bfloat16 [2048, 8192], P(('dp', 'depth'), 'mp'), may hold values from -0.125 to 0.125
- down_weight: bfloat16 [8192, 2048], P('mp', ('dp', 'depth')), may hold values from -0.0625 to 0.0625
Outputs:
- layer_out: bfloat16 [8192, 2048], P(('dp', 'depth'), 'mp')
- history_grad: bfloat16 [20, 8192, 2048], P('depth', 'dp', 'mp')
- current_grad: float32 [8192, 2048], P(('dp', 'depth'), 'mp')
- gains_grad: float32 [5, 2048], P(None, ('dp', 'depth'))
- gen_in_grad: float32 [2048, 72], P(('dp', 'depth'))
- gen_out_grad: float32 [5184], P(('dp', 'depth'))
- query_grad: float32 [2048, 2048], P(('dp', 'depth'), 'mp')
- key_grad: float32 [2048, 2048], P(('dp', 'depth'), 'mp')
- value_grad: float32 [2048, 2048], P(('dp', 'depth'), 'mp')
- out_grad: float32 [2048, 2048], P('mp', ('dp', 'depth'))
- up_grad: float32 [2048, 8192], P(('dp', 'depth'), 'mp')
- down_grad: float32 [8192, 2048], P('mp', ('dp', 'depth'))
The draws below stay inside these ranges and needn't reach their ends.
Inputs may be any that keep to these rules, and one draw needn't show every extreme that they name: `slot_layer`: each of the 17 history states sits in exactly one slot; the other slots hold 18 and are empty. `positions`: a token's place within its document; documents never cross sequences, and some sequence is one whole document. `doc_ids`: the tokens of one document stand consecutively within one sequence and share one number; different documents have different numbers.
All inputs are finite; a program needn't handle non-finite values.
Results may differ from the reference program's by a relative error of at most 0.012.
The reference program's roundings to bfloat16 on the way count: a program that leaves them out, or rounds other values in their place, can miss the bound.
Values may be sent and summed in bfloat16 or wider, within the bound.
No kernel may reach another device: no remote copies, remote signals or barrier semaphores. Data moves between devices by JAX's collectives and lax.ppermute only.
A program may use at most 704 MiB of HBM per device.

```python
import math
import jax
import jax.numpy as jnp
from jax import lax

D = 2048
HDIM = 128
FF = 8192
ROT = 32
GEN = 72
STATES = 17
MB = 2
HD = 2048
MIX = 18
MBT = 256
LENGTH = 1024
TOKENS = 8192
SLOTS = 20
N_DP = 4
N_DEPTH = 4


def document_layout(key):
    seq_count = N_DP * MB
    ordinal = jnp.arange(LENGTH)
    starts = jax.random.randint(key, (seq_count, LENGTH), 0, max(LENGTH // 4, 2)) == 0
    starts = starts | (ordinal == 0)[None, :]
    last_start = (jnp.arange(seq_count) == seq_count - 1)[:, None] & (ordinal == LENGTH - 1)[None, :]
    starts = starts | last_start
    single_doc = (jnp.arange(seq_count) == 0)[:, None] & (ordinal > 0)[None, :]
    starts = starts & jnp.logical_not(single_doc)
    begins = lax.cummax(jnp.where(starts, ordinal[None, :], 0), axis=1)
    places = ordinal[None, :] - begins
    doc_numbers = begins + (jnp.arange(seq_count) * LENGTH)[:, None]

    def reorder(values):
        shaped = values.reshape(N_DP, MB, N_DEPTH, MBT)
        return jnp.swapaxes(shaped, 1, 2).reshape(TOKENS).astype(jnp.int32)
    return (reorder(doc_numbers), reorder(places))


def draw_doc_ids(key, part):
    return document_layout(jax.random.fold_in(key, 11))[0]


def draw_positions(key, part):
    return document_layout(jax.random.fold_in(key, 11))[1]


def draw_slot_layer(key, part):
    shuffled = jax.random.permutation(jax.random.fold_in(key, 5), SLOTS)
    return jnp.where(shuffled < STATES, shuffled, STATES + 1).astype(jnp.int32)


def shard_levels(own_key, extent, cuts, smallest, high):
    loudness = 1.0
    for position, parts in cuts:
        draws = jax.random.uniform(jax.random.fold_in(jax.random.fold_in(own_key, 6), position), (parts,), jnp.float32, smallest / len(cuts), high / len(cuts))
        loudness = loudness * jnp.repeat(jnp.exp(draws), extent[position] // parts).reshape((-1,) + (1,) * (len(extent) - 1 - position))
    return loudness


def noise(own_key, extent, width, reach, shards=(), kind=jnp.bfloat16):
    entries = jax.random.normal(own_key, extent, jnp.float32) * width
    if len(shards) > 0:
        entries = shard_levels(own_key, extent, shards, -0.22, 0.18) * entries
    return jnp.clip(entries, min=-reach, max=reach).astype(kind)


def setup_inputs(seed: int = 0) -> dict:
    key_list = jax.random.split(jax.random.key(seed), 16)
    history = noise(key_list[0], (SLOTS, TOKENS, D), 1.0, 6.0, ((0, 4), (1, 4), (2, 2)))
    slot_layer = draw_slot_layer(jax.random.fold_in(key_list[15], 71), 0)
    current = noise(key_list[2], (TOKENS, D), 1.0, 6.0, ((0, 16),))
    positions = draw_positions(jax.random.fold_in(key_list[15], 71), 0)
    doc_ids = draw_doc_ids(jax.random.fold_in(key_list[15], 71), 0)
    cotangent = noise(key_list[5], (TOKENS, D), 1.0, 6.0, ((0, 16), (1, 2)))
    norm_gains = jnp.clip(1.0 + 0.1 * jax.random.normal(key_list[6], (5, D), jnp.float32), 0.5, 1.5).astype(jnp.bfloat16)
    generator_in = noise(key_list[7], (D, GEN), D ** -0.5, 0.125, ((0, 16),))
    generator_out = noise(key_list[8], (GEN * 4 * MIX,), GEN ** -0.5, 0.75, ((0, 16),))
    query_weight = noise(key_list[9], (D, HD), D ** -0.5, 0.125, ((0, 16), (1, 2)))
    key_weight = noise(key_list[10], (D, HD), D ** -0.5, 0.125, ((0, 16), (1, 2)))
    value_weight = noise(key_list[11], (D, HD), D ** -0.5, 0.125, ((0, 16), (1, 2)))
    out_weight = noise(key_list[12], (HD, D), (HD // 32) ** -0.5, 0.75, ((0, 2), (1, 16)))
    up_weight = noise(key_list[13], (D, FF), D ** -0.5, 0.125, ((0, 16), (1, 2)))
    down_weight = noise(key_list[14], (FF, D), FF ** -0.5, 0.0625, ((0, 2), (1, 16)))
    return dict(history=history, slot_layer=slot_layer, current=current, positions=positions, doc_ids=doc_ids, cotangent=cotangent, norm_gains=norm_gains, generator_in=generator_in, generator_out=generator_out, query_weight=query_weight, key_weight=key_weight, value_weight=value_weight, out_weight=out_weight, up_weight=up_weight, down_weight=down_weight)


@jax.custom_vjp
def low(v):
    return lax.optimization_barrier(v.astype(jnp.bfloat16)).astype(jnp.float32)

@jax.custom_vjp
def low_back(v):
    return v

def low_keep(v):
    return (low(v), None)

def low_pass(kept, grad):
    return (grad,)

def back_keep(v):
    return (v, None)

def back_low(kept, grad):
    return (low(grad),)
low.defvjp(low_keep, low_pass)
low_back.defvjp(back_keep, back_low)
PRECISE = lax.Precision.HIGHEST
NORM_EPSILON = 1e-05
RMS_EPSILON = 1e-06
MASKED = -1e+30

def matmul_exact(left_op, right_op):
    return jnp.dot(left_op, right_op, precision=PRECISE, preferred_element_type=jnp.float32)

def gelu_exact(values):
    return jax.nn.gelu(values, approximate=False)

def layer_norm(values, gain_vec):
    average = lax.optimization_barrier(jnp.mean(values, axis=-1, keepdims=True))
    centred = values - average
    variance = lax.optimization_barrier(jnp.mean(centred * centred, axis=-1, keepdims=True))
    return centred * lax.rsqrt(variance + NORM_EPSILON) * gain_vec

def rotary_tables(places):
    half_rot = ROT // 2
    inverse = jnp.exp(jnp.arange(half_rot, dtype=jnp.float32) * (-2.0 * math.log(10000.0) / ROT))
    angles = places.astype(jnp.float32)[:, None] * inverse[None, :]
    return (jnp.cos(angles)[:, None, :], jnp.sin(angles)[:, None, :])

def rotate(values, cosine, sine_part):
    half_rot = ROT // 2
    first_half = values[..., :half_rot]
    second_half = values[..., half_rot:ROT]
    return jnp.concatenate([first_half * cosine - second_half * sine_part, second_half * cosine + first_half * sine_part, values[..., ROT:]], axis=-1)

def generator(current_f, gain_vec, weight_in, weight_out):
    mean_square = lax.optimization_barrier(jnp.mean(current_f * current_f, axis=-1, keepdims=True))
    scaled = current_f * lax.rsqrt(mean_square + RMS_EPSILON)
    normed = low(scaled * gain_vec)
    gen_hidden = low(gelu_exact(matmul_exact(normed, weight_in)))
    dynamic = matmul_exact(gen_hidden, weight_out.reshape(GEN, 4 * MIX)).reshape(-1, 4, MIX)
    last_col = (jnp.arange(MIX) == MIX - 1).astype(jnp.float32)
    return low(dynamic + last_col)

def sequence_block(weights, inputs):
    gain_rows, query_w, key_w, value_w, out_w, up_w, down_w = weights
    stream_low, residual, places, documents = inputs
    length = residual.shape[0]
    head_count = query_w.shape[1] // HDIM
    normed = [low(layer_norm(stream_low[:, stream_at], gain_rows[stream_at])) for stream_at in range(4)]
    cosine, sine_part = rotary_tables(places)
    queries = low(rotate(low_back(matmul_exact(normed[0], query_w)).reshape(length, head_count, HDIM), cosine, sine_part))
    key_rows = low(rotate(low_back(matmul_exact(normed[1], key_w)).reshape(length, head_count, HDIM), cosine, sine_part))
    values = low(low_back(matmul_exact(normed[2], value_w))).reshape(length, head_count, HDIM)
    scores = low_back(jnp.einsum('qhd,khd->hqk', queries, key_rows, precision=PRECISE) * HDIM ** (-0.5))
    ordinal = jnp.arange(length)
    allowed = (documents[:, None] == documents[None, :]) & (ordinal[:, None] >= ordinal[None, :])
    scores = jnp.where(allowed[None], scores, MASKED)
    attention = low(low_back(jax.nn.softmax(scores, axis=-1)))
    attended = low(low_back(jnp.einsum('hqk,khd->qhd', attention, values, precision=PRECISE).reshape(length, head_count * HDIM)))
    up_pre = low_back(matmul_exact(normed[3], up_w))
    hidden = low(gelu_exact(up_pre))
    return residual + matmul_exact(attended, out_w) + matmul_exact(hidden, down_w)

def to_sequences(values):
    shaped = values.reshape((N_DP, N_DEPTH, MB, MBT) + values.shape[1:])
    return jnp.swapaxes(shaped, 1, 2).reshape((N_DP * MB, LENGTH) + values.shape[1:])

def from_sequences(values):
    shaped = values.reshape((N_DP, MB, N_DEPTH, MBT) + values.shape[2:])
    return jnp.swapaxes(shaped, 1, 2).reshape((TOKENS,) + values.shape[2:])

def reference(history, slot_layer, current, positions, doc_ids, cotangent, norm_gains, generator_in, generator_out, query_weight, key_weight, value_weight, out_weight, up_weight, down_weight):
    select = (slot_layer[:, None] == jnp.arange(MIX)[None, :]).astype(jnp.float32)
    places = to_sequences(positions)
    documents = to_sequences(doc_ids)

    def forward(history_f, current_f, gain_rows, gen_first, gen_second, query_w, key_w, value_w, out_w, up_w, down_w):
        mixing = generator(current_f, gain_rows[4], gen_first, gen_second)
        slot_mix = jnp.einsum('tsj,kj->tsk', mixing, select, precision=PRECISE)
        streams = jnp.einsum('tsk,ktd->tsd', slot_mix, history_f, precision=PRECISE) + mixing[:, :, MIX - 1:MIX] * current_f[:, None, :]
        streams = low_back(streams)
        stream_low = low(streams)
        weights = (gain_rows, query_w, key_w, value_w, out_w, up_w, down_w)

        def one_sequence(inputs):
            return sequence_block(weights, inputs)
        outputs = lax.map(jax.checkpoint(one_sequence), (to_sequences(stream_low), to_sequences(streams[:, 3]), places, documents))
        return from_sequences(outputs)
    floats = tuple((argument.astype(jnp.float32) for argument in (history, current, norm_gains, generator_in, generator_out, query_weight, key_weight, value_weight, out_weight, up_weight, down_weight)))
    layer_out, pullback = jax.vjp(forward, *floats)
    gradients = pullback(cotangent.astype(jnp.float32))
    return (layer_out.astype(jnp.bfloat16), gradients[0].astype(jnp.bfloat16), gradients[1], gradients[2], gradients[3], gradients[4], gradients[5], gradients[6], gradients[7], gradients[8], gradients[9], gradients[10])
```

```python
import functools
import math

import jax
import jax.numpy as jnp
from jax import lax
from jax.experimental import pallas as pl
from jax.experimental.pallas import tpu as pltpu
from jax.sharding import PartitionSpec as P

HDIM = 128
ROT = 32
GEN = 72
MB = 2
MIX = 18
STREAMS = 4

PRECISE = lax.Precision.HIGHEST
NORM_EPSILON = 1e-05
RMS_EPSILON = 1e-06
MASKED = -1e30

bf16 = jnp.bfloat16
f32 = jnp.float32


def dot_nn(a, b):
    return lax.dot_general(a, b, (((1,), (0,)), ((), ())), preferred_element_type=f32)


def dot_nt(a, b):
    return lax.dot_general(a, b, (((1,), (1,)), ((), ())), preferred_element_type=f32)


def dot_tn(a, b):
    return lax.dot_general(a, b, (((0,), (0,)), ((), ())), preferred_element_type=f32)


def dot_exact(a, b):
    return jnp.dot(a, b, precision=PRECISE, preferred_element_type=f32)


def gelu_exact(values):
    return jax.nn.gelu(values, approximate=False)


def gelu_slope(values):
    result, pullback = jax.vjp(gelu_exact, values)
    return pullback(jnp.ones_like(result))[0]


def bit_count(size):
    count = size.bit_length() - 1
    assert 1 << count == size
    return count


def swap_mask(values, axis, mask):
    size = lax.axis_size(axis)
    return lax.ppermute(values, axis, [(i, i ^ mask) for i in range(size)])


def gather_masked(values, axis, order):
    pieces = {0: values}
    for bit in order:
        arrived = {m | (1 << bit): swap_mask(v, axis, 1 << bit) for m, v in pieces.items()}
        pieces.update(arrived)
    return [pieces[m] for m in range(len(pieces))]


def scatter_masked(pieces, axis, order, link=bf16):
    pieces = dict(enumerate(pieces))
    for bit in order:
        flag = 1 << bit
        for m in [m for m in pieces if m & flag]:
            arrived = swap_mask(pieces.pop(m).astype(link), axis, flag)
            pieces[m ^ flag] = pieces[m ^ flag].astype(f32) + arrived.astype(f32)
    return pieces[0]


def reorder_masked(stacked, axis):
    count = bit_count(stacked.shape[0])
    here = lax.axis_index(axis)
    shape = stacked.shape
    values = stacked.reshape((2,) * count + shape[1:])
    for bit in range(count):
        turned = jnp.flip(values, count - 1 - bit)
        values = jnp.where(((here >> bit) & 1) == 1, turned, values)
    return values.reshape(shape)


def gather_small(values, axes):
    shape = values.shape
    values = values[None]
    for axis in reversed(axes):
        order = range(bit_count(lax.axis_size(axis)))
        stacked = jnp.stack(gather_masked(values, axis, order))
        values = reorder_masked(stacked, axis)
        values = values.reshape((-1,) + shape)
    return values


def scatter_small(values, axes):
    for axis in axes:
        size = lax.axis_size(axis)
        values = values.reshape((size, values.shape[0] // size) + values.shape[1:])
        turned = reorder_masked(values, axis)
        order = reversed(range(bit_count(size)))
        values = scatter_masked([turned[m] for m in range(size)], axis, order, f32)
    return values[0]


def other_core(values):
    return swap_mask(values, "mp", 1)


def join_kernel(model_ref, own_ref, other_ref, out_ref):
    width = own_ref.shape[1]
    own_at = pl.multiple_of(model_ref[0] * width, width)
    other_at = pl.multiple_of((1 - model_ref[0]) * width, width)
    out_ref[:, pl.ds(own_at, width)] = own_ref[...]
    out_ref[:, pl.ds(other_at, width)] = other_ref[...]


def join_halves(own, other, model_at):
    tall, width = own.shape
    rows = min(256, tall)
    return pl.pallas_call(
        join_kernel,
        grid_spec=pltpu.PrefetchScalarGridSpec(
            num_scalar_prefetch=1,
            grid=(tall // rows,),
            in_specs=[pl.BlockSpec((rows, width), lambda i, m: (i, 0))] * 2,
            out_specs=pl.BlockSpec((rows, 2 * width), lambda i, m: (i, 0)),
        ),
        out_shape=jax.ShapeDtypeStruct((tall, 2 * width), own.dtype),
        cost_estimate=pl.CostEstimate(
            flops=0, bytes_accessed=8 * tall * width, transcendentals=0
        ),
        name="join_halves",
    )(model_at.astype(jnp.int32)[None], own, other)


def mix_kernel(slots, mix_ref, hist_ref, out_ref):
    rows, width = hist_ref.shape[1], hist_ref.shape[2]
    part = 512 if width % 512 == 0 else width

    def step(at, carry):
        r0 = pl.multiple_of(at * 16, 16)
        weights = mix_ref[pl.ds(r0, 16), :]
        for c0 in range(0, width, part):
            sums = [None] * STREAMS
            for k in range(slots):
                state = hist_ref[k, pl.ds(r0, 16), c0 : c0 + part].astype(f32)
                for s in range(STREAMS):
                    term = weights[:, s * slots + k : s * slots + k + 1] * state
                    sums[s] = term if sums[s] is None else sums[s] + term
            for s in range(STREAMS):
                out_ref[pl.ds(r0, 16), s * width + c0 : s * width + c0 + part] = sums[s].astype(bf16)
        return carry

    lax.fori_loop(0, rows // 16, step, 0)


def mix_streams(slot_mix, history, micro_at, depth_count, rows_mb):
    slots, _, width = history.shape
    rows = min(128, rows_mb)
    per = rows_mb // rows

    def row_block(i):
        return ((i // per) * MB + micro_at) * per + i % per

    return pl.pallas_call(
        functools.partial(mix_kernel, slots),
        grid=(depth_count * per,),
        in_specs=[
            pl.BlockSpec((rows, slot_mix.shape[1]), lambda i: (row_block(i), 0)),
            pl.BlockSpec((slots, rows, width), lambda i: (0, row_block(i), 0)),
        ],
        out_specs=pl.BlockSpec((rows, STREAMS * width), lambda i: (i, 0)),
        out_shape=jax.ShapeDtypeStruct((depth_count * rows_mb, STREAMS * width), bf16),
        cost_estimate=pl.CostEstimate(
            flops=2 * slots * STREAMS * depth_count * rows_mb * width,
            bytes_accessed=2 * (slots + STREAMS) * depth_count * rows_mb * width,
            transcendentals=0,
        ),
        name="mix_streams",
    )(slot_mix, history)


def unmix_kernel(slots, mix_ref, hist_ref, grad_ref, *rest):
    hist_grad_ref, slot_grad_ref = rest[-2:]
    rows, width = hist_ref.shape[1], hist_ref.shape[2]
    part = 512 if width % 512 == 0 else width

    def step(at, carry):
        r0 = pl.multiple_of(at * 16, 16)
        weights = mix_ref[pl.ds(r0, 16), :]
        totals = [None] * (STREAMS * slots)
        for c0 in range(0, width, part):
            grads = [
                grad_ref[pl.ds(r0, 16), s * width + c0 : s * width + c0 + part].astype(f32)
                for s in range(STREAMS)
            ]
            for k in range(slots):
                state = hist_ref[k, pl.ds(r0, 16), c0 : c0 + part].astype(f32)
                back = None
                for s in range(STREAMS):
                    at_sk = s * slots + k
                    term = weights[:, at_sk : at_sk + 1] * grads[s]
                    back = term if back is None else back + term
                    product = state * grads[s]
                    folded = product[:, 0:128]
                    for l0 in range(128, part, 128):
                        folded = folded + product[:, l0 : l0 + 128]
                    totals[at_sk] = folded if totals[at_sk] is None else totals[at_sk] + folded
                hist_grad_ref[k, pl.ds(r0, 16), c0 : c0 + part] = back.astype(bf16)
        lane = lax.broadcasted_iota(jnp.int32, (16, 128), 1)
        packed = jnp.zeros((16, 128), f32)
        for at_sk in range(STREAMS * slots):
            column = jnp.sum(totals[at_sk], axis=1, keepdims=True)
            packed = jnp.where(lane == at_sk, column, packed)
        slot_grad_ref[pl.ds(r0, 16), :] = packed
        return carry

    lax.fori_loop(0, rows // 16, step, 0)


def unmix_streams(slot_mix, history, grads, micro_at, depth_count, rows_mb, earlier):
    slots, tokens, width = history.shape
    rows = min(128, rows_mb)
    per = rows_mb // rows

    def row_block(i):
        return ((i // per) * MB + micro_at) * per + i % per

    in_specs = [
        pl.BlockSpec((rows, slot_mix.shape[1]), lambda i: (row_block(i), 0)),
        pl.BlockSpec((slots, rows, width), lambda i: (0, row_block(i), 0)),
        pl.BlockSpec((rows, STREAMS * width), lambda i: (i, 0)),
    ]
    operands = [slot_mix, history, grads]
    aliases = {}
    if earlier is not None:
        in_specs.append(pl.BlockSpec(memory_space=pl.ANY))
        operands.append(earlier)
        aliases = {3: 0}
    return pl.pallas_call(
        functools.partial(unmix_kernel, slots),
        grid=(depth_count * per,),
        in_specs=in_specs,
        out_specs=[
            pl.BlockSpec((slots, rows, width), lambda i: (0, row_block(i), 0)),
            pl.BlockSpec((rows, 128), lambda i: (i, 0)),
        ],
        out_shape=[
            jax.ShapeDtypeStruct((slots, tokens, width), bf16),
            jax.ShapeDtypeStruct((depth_count * rows_mb, 128), f32),
        ],
        input_output_aliases=aliases,
        cost_estimate=pl.CostEstimate(
            flops=4 * slots * STREAMS * depth_count * rows_mb * width,
            bytes_accessed=2 * (2 * slots + STREAMS) * depth_count * rows_mb * width,
            transcendentals=0,
        ),
        name="unmix_streams",
    )(*operands)


def own_spans(model_ref, width):
    own_at = pl.multiple_of(model_ref[0] * width, width)
    other_at = pl.multiple_of((1 - model_ref[0]) * width, width)
    return pl.ds(own_at, width), pl.ds(other_at, width)


def total_kernel(part_ref, cur_ref, last_ref, low_ref, resid_ref):
    width = resid_ref.shape[1]
    current = cur_ref[...].astype(f32)
    for s in range(STREAMS):
        lanes = slice(s * width, (s + 1) * width)
        total = part_ref[0, :, lanes].astype(f32)
        for at in range(1, part_ref.shape[0]):
            total = total + part_ref[at, :, lanes].astype(f32)
        total = total + last_ref[:, s : s + 1] * current
        if s == STREAMS - 1:
            resid_ref[...] = total
        low_ref[:, lanes] = total.astype(bf16)


def total_streams(parts, current_half, last):
    count, tall, wide = parts.shape
    width = wide // STREAMS
    rows = min(64, tall)
    return pl.pallas_call(
        total_kernel,
        grid=(tall // rows,),
        in_specs=[
            pl.BlockSpec((count, rows, wide), lambda i: (0, i, 0)),
            pl.BlockSpec((rows, width), lambda i: (i, 0)),
            pl.BlockSpec((rows, 128), lambda i: (i, 0)),
        ],
        out_specs=[
            pl.BlockSpec((rows, wide), lambda i: (i, 0)),
            pl.BlockSpec((rows, width), lambda i: (i, 0)),
        ],
        out_shape=[
            jax.ShapeDtypeStruct((tall, wide), bf16),
            jax.ShapeDtypeStruct((tall, width), f32),
        ],
        cost_estimate=pl.CostEstimate(
            flops=(count + 2) * tall * wide,
            bytes_accessed=2 * (count + 2) * tall * wide,
            transcendentals=0,
        ),
        name="total_streams",
    )(parts, current_half, last)


def norm_kernel(model_ref, own_ref, other_ref, gain_ref, normed_ref, ff_ref, stat_ref):
    rows, width = ff_ref.shape
    model = 2 * width
    own_span, other_span = own_spans(model_ref, width)
    lane = lax.broadcasted_iota(jnp.int32, (rows, 128), 1)
    stats = jnp.zeros((rows, 128), f32)
    for s in range(STREAMS):
        lanes = slice(s * width, (s + 1) * width)
        own = own_ref[:, lanes].astype(f32)
        other = other_ref[:, lanes].astype(f32)
        average = (
            jnp.sum(own, axis=-1, keepdims=True) + jnp.sum(other, axis=-1, keepdims=True)
        ) / model
        own, other = own - average, other - average
        variance = (
            jnp.sum(own * own, axis=-1, keepdims=True)
            + jnp.sum(other * other, axis=-1, keepdims=True)
        ) / model
        inverse = lax.rsqrt(variance + NORM_EPSILON)
        stats = jnp.where(lane == 2 * s, average, stats)
        stats = jnp.where(lane == 2 * s + 1, inverse, stats)
        norm_own = (own * inverse * gain_ref[s : s + 1, own_span]).astype(bf16)
        if s == STREAMS - 1:
            ff_ref[...] = norm_own
        else:
            normed_ref[s, :, own_span] = norm_own
            norm_other = (other * inverse * gain_ref[s : s + 1, other_span]).astype(bf16)
            normed_ref[s, :, other_span] = norm_other
    stat_ref[...] = stats


def norm_streams(low, low_other, gains, which):
    tall, wide = low.shape
    width = wide // STREAMS
    rows = min(64, tall)
    row = lambda i, m: (i, 0)
    return pl.pallas_call(
        norm_kernel,
        grid_spec=pltpu.PrefetchScalarGridSpec(
            num_scalar_prefetch=1,
            grid=(tall // rows,),
            in_specs=[
                pl.BlockSpec((rows, wide), row),
                pl.BlockSpec((rows, wide), row),
                pl.BlockSpec(gains.shape, lambda i, m: (0, 0)),
            ],
            out_specs=[
                pl.BlockSpec((3, rows, 2 * width), lambda i, m: (0, i, 0)),
                pl.BlockSpec((rows, width), row),
                pl.BlockSpec((rows, 128), row),
            ],
        ),
        out_shape=[
            jax.ShapeDtypeStruct((3, tall, 2 * width), bf16),
            jax.ShapeDtypeStruct((tall, width), bf16),
            jax.ShapeDtypeStruct((tall, 128), f32),
        ],
        cost_estimate=pl.CostEstimate(
            flops=20 * tall * wide, bytes_accessed=8 * tall * wide, transcendentals=0
        ),
        name="norm_streams",
    )(which, low, low_other, gains)


def turn(values, cosine, sine_up, sine_down, sign):
    up = pltpu.roll(values, HDIM - ROT // 2, 1)
    down = pltpu.roll(values, ROT // 2, 1)
    return values * cosine + sign * (up * sine_up + down * sine_down)


def project_kernel(
    x_ref, cot_ref, wq_ref, wk_ref, wv_ref, wo_ref, cos_ref, up_ref, down_ref, out_ref
):
    span = wq_ref.shape[1]
    tables = cos_ref[...], up_ref[...], down_ref[...]
    for kind, w_ref in enumerate((wq_ref, wk_ref, wv_ref, wo_ref)):
        rows = cot_ref[...] if kind == 3 else x_ref[kind]
        product = dot_nn(rows, w_ref[...])
        for begin in range(0, span, HDIM):
            head = product[:, begin : begin + HDIM]
            if kind < 2:
                head = turn(head, *tables, 1.0)
            out_ref[0, :, kind * span + begin : kind * span + begin + HDIM] = head.astype(bf16)


def project_heads(normed, cot, weights, tables, depth_count):
    _, rows, model = normed.shape
    span = weights[0].shape[1] // depth_count
    whole = lambda j: (0, 0)
    return pl.pallas_call(
        project_kernel,
        grid=(depth_count,),
        in_specs=[
            pl.BlockSpec((3, rows, model), lambda j: (0, 0, 0)),
            pl.BlockSpec((rows, model), whole),
        ]
        + [pl.BlockSpec((model, span), lambda j: (0, j))] * 4
        + [pl.BlockSpec((rows, HDIM), whole)] * 3,
        out_specs=pl.BlockSpec((1, rows, 4 * span), lambda j: (j, 0, 0)),
        out_shape=jax.ShapeDtypeStruct((depth_count, rows, 4 * span), bf16),
        compiler_params=pltpu.CompilerParams(vmem_limit_bytes=40 << 20),
        cost_estimate=pl.CostEstimate(
            flops=8 * rows * model * span * depth_count,
            bytes_accessed=8 * model * span * depth_count + 8 * rows * model,
            transcendentals=0,
        ),
        name="project_heads",
    )(normed, cot, *weights, *tables)


def attend_kernel(
    block, q_ref, k_ref, v_ref, g_ref, doc_col_ref, doc_row_ref, cos_ref, up_ref, down_ref,
    out_ref, dk_sum, dv_sum,
):
    length = q_ref.shape[0]
    scale = HDIM**-0.5
    heads_each = out_ref.shape[1] // (4 * HDIM)

    def lanes(kind):
        return pl.ds(pl.multiple_of((kind * heads_each + pl.program_id(0)) * HDIM, HDIM), HDIM)

    for begin in range(0, length, block):
        end = begin + block
        rows = slice(begin, end)
        queries, grads = q_ref[rows, :], g_ref[rows, :]
        keys, values = k_ref[0:end, :], v_ref[0:end, :]
        scores = dot_nt(queries, keys) * scale
        place_q = begin + lax.broadcasted_iota(jnp.int32, scores.shape, 0)
        place_k = lax.broadcasted_iota(jnp.int32, scores.shape, 1)
        allowed = (doc_col_ref[rows, :] == doc_row_ref[:, 0:end]) & (place_q >= place_k)
        scores = jnp.where(allowed, scores, MASKED)
        highest = jnp.max(scores, axis=-1, keepdims=True)
        exponent = jnp.exp(scores - highest)
        totals = jnp.sum(exponent, axis=-1, keepdims=True)
        attention = exponent * (1.0 / totals)
        low = attention.astype(bf16)
        out_ref[rows, lanes(0)] = dot_nn(low, values).astype(bf16)
        grad_att = dot_nt(grads, values).astype(bf16).astype(f32)
        weighted = jnp.sum(attention * grad_att, axis=-1, keepdims=True)
        grad_scores = (attention * (grad_att - weighted)).astype(bf16)
        grad_q = dot_nn(grad_scores, keys) * scale
        out_ref[rows, lanes(1)] = turn(
            grad_q, cos_ref[rows, :], up_ref[rows, :], down_ref[rows, :], -1.0
        ).astype(bf16)
        part_k = dot_tn(grad_scores, queries)
        part_v = dot_tn(low, grads)
        if begin > 0:
            dk_sum[0:begin, :] += part_k[0:begin]
            dv_sum[0:begin, :] += part_v[0:begin]
        dk_sum[begin:end, :] = part_k[begin:end]
        dv_sum[begin:end, :] = part_v[begin:end]
    grad_k = dk_sum[...] * scale
    out_ref[:, lanes(2)] = turn(grad_k, cos_ref[...], up_ref[...], down_ref[...], -1.0).astype(bf16)
    out_ref[:, lanes(3)] = dv_sum[...].astype(bf16)


def attend(packed, documents, tables, heads_each):
    length = packed.shape[0]
    block = min(256, length)
    whole = lambda h: (0, 0)

    def kind(at):
        return pl.BlockSpec((length, HDIM), lambda h: (0, at * heads_each + h))

    return pl.pallas_call(
        functools.partial(attend_kernel, block),
        grid=(heads_each,),
        in_specs=[kind(0), kind(1), kind(2), kind(3)]
        + [pl.BlockSpec((length, 1), whole), pl.BlockSpec((1, length), whole)]
        + [pl.BlockSpec((length, HDIM), whole)] * 3,
        out_specs=pl.BlockSpec((length, 4 * heads_each * HDIM), whole),
        out_shape=jax.ShapeDtypeStruct((length, 4 * heads_each * HDIM), bf16),
        scratch_shapes=[pltpu.VMEM((length, HDIM), f32)] * 2,
        compiler_params=pltpu.CompilerParams(vmem_limit_bytes=48 << 20),
        cost_estimate=pl.CostEstimate(
            flops=9 * heads_each * length * length * HDIM,
            bytes_accessed=16 * length * heads_each * HDIM + 12 * length * HDIM,
            transcendentals=heads_each * length * length,
        ),
        name="attend",
    )(packed, packed, packed, packed, documents[:, None], documents[None, :], *tables)


def gelu_parts(values):
    cdf = 0.5 * (1.0 + lax.erf(values * (0.5**0.5)))
    density = jnp.exp(-0.5 * values * values) * (1.0 / math.sqrt(2.0 * math.pi))
    return values * cdf, cdf + values * density


def ff_kernel(
    model_ref, x_ref, cot_ref, up_ref, down_ref,
    hidden_ref, grad_ref, out_own_ref, out_other_ref, back_own_ref, back_other_ref,
):
    own_span, other_span = own_spans(model_ref, out_own_ref.shape[1])
    up_pre = dot_nn(x_ref[...], up_ref[...])
    hidden, slope = gelu_parts(up_pre)
    hidden = hidden.astype(bf16)
    grad_up = (dot_nn(cot_ref[...], down_ref[...]) * slope).astype(bf16)
    hidden_ref[...] = hidden
    grad_ref[...] = grad_up
    back_other_ref[...] = dot_nt(grad_up, up_ref[other_span, :]).astype(bf16)
    back_own_ref[...] = dot_nt(grad_up, up_ref[own_span, :])
    out_other_ref[...] = dot_nt(hidden, down_ref[other_span, :]).astype(bf16)
    out_own_ref[...] = dot_nt(hidden, down_ref[own_span, :])


def feed_forward(x, cot, up_w, down_wt, which):
    tall, model = x.shape
    part = up_w.shape[1]
    width = model // 2
    rows = min(256, tall)
    row = lambda i, m: (i, 0)
    whole = lambda i, m: (0, 0)
    resident = pl.BlockSpec((model, part), whole, pipeline_mode=pl.Buffered(1))
    return pl.pallas_call(
        ff_kernel,
        grid_spec=pltpu.PrefetchScalarGridSpec(
            num_scalar_prefetch=1,
            grid=(tall // rows,),
            in_specs=[
                pl.BlockSpec((rows, model), row),
                pl.BlockSpec((rows, model), row),
                resident,
                resident,
            ],
            out_specs=[pl.BlockSpec((rows, part), row)] * 2
            + [pl.BlockSpec((rows, width), row)] * 4,
        ),
        out_shape=[jax.ShapeDtypeStruct((tall, part), bf16)] * 2
        + [
            jax.ShapeDtypeStruct((tall, width), f32),
            jax.ShapeDtypeStruct((tall, width), bf16),
            jax.ShapeDtypeStruct((tall, width), f32),
            jax.ShapeDtypeStruct((tall, width), bf16),
        ],
        compiler_params=pltpu.CompilerParams(vmem_limit_bytes=48 << 20),
        cost_estimate=pl.CostEstimate(
            flops=8 * tall * model * part,
            bytes_accessed=4 * model * part + 16 * tall * model,
            transcendentals=2 * tall * part,
        ),
        name="feed_forward",
    )(which, x, cot, up_w, down_wt)


def back_kernel(half_ref, ans_ref, wo_ref, wq_ref, wk_ref, wv_ref, out_ref, *flat):
    count, _, wide = ans_ref.shape
    span = wide // 4
    for kind, w_ref in enumerate((wo_ref, wq_ref, wk_ref, wv_ref)):
        total = None
        for j in range(count):
            term = dot_nt(
                ans_ref[j, :, kind * span : (kind + 1) * span], w_ref[:, j * span : (j + 1) * span]
            )
            total = term if total is None else total + term
        out_ref[kind] = total.astype(out_ref.dtype)
    if flat:

        @pl.when(pl.program_id(0) == 0)
        def _():
            for kind in range(4):
                for j in range(count):
                    flat[0][kind, :, j * span : (j + 1) * span] = ans_ref[
                        j, :, kind * span : (kind + 1) * span
                    ]


def back_project(answer, weights, half, dtype, flat):
    count, rows, wide = answer.shape
    model, heads_width = weights[0].shape
    width = model // 2
    steps = 2
    part = width // steps
    out_specs = [pl.BlockSpec((4, rows, part), lambda i, m: (0, 0, i))]
    out_shape = [jax.ShapeDtypeStruct((4, rows, width), dtype)]
    if flat:
        out_specs.append(pl.BlockSpec((4, rows, heads_width), lambda i, m: (0, 0, 0)))
        out_shape.append(jax.ShapeDtypeStruct((4, rows, heads_width), bf16))
    return pl.pallas_call(
        back_kernel,
        grid_spec=pltpu.PrefetchScalarGridSpec(
            num_scalar_prefetch=1,
            grid=(steps,),
            in_specs=[pl.BlockSpec((count, rows, wide), lambda i, m: (0, 0, 0))]
            + [pl.BlockSpec((part, heads_width), lambda i, m: (m[0] * steps + i, 0))] * 4,
            out_specs=out_specs,
        ),
        out_shape=out_shape,
        compiler_params=pltpu.CompilerParams(vmem_limit_bytes=40 << 20),
        cost_estimate=pl.CostEstimate(
            flops=8 * rows * heads_width * width,
            bytes_accessed=8 * heads_width * width + 20 * rows * width,
            transcendentals=0,
        ),
        name="back_project",
    )(half, answer, *weights)


def slope_kernel(
    model_ref, own_ref, got_ref, ff_ref, low_ref, stat_ref, gain_ref, scaled_ref, sum_ref, gain_out_ref
):
    rows, width = ff_ref.shape
    own_span, _ = own_spans(model_ref, width)
    lane = lax.broadcasted_iota(jnp.int32, (rows, 128), 1)
    packed = jnp.zeros((rows, 128), f32)
    totals = []
    for s in range(STREAMS):
        lanes = slice(s * width, (s + 1) * width)
        if s < 3:
            grad = own_ref[s + 1] + got_ref[s + 1].astype(f32)
        else:
            grad = ff_ref[...]
        average, inverse = stat_ref[:, 2 * s : 2 * s + 1], stat_ref[:, 2 * s + 1 : 2 * s + 2]
        hat = (low_ref[:, lanes].astype(f32) - average) * inverse
        totals.append(jnp.sum(grad * hat, axis=0, keepdims=True))
        scaled = grad * gain_ref[s : s + 1, own_span]
        scaled_ref[:, lanes] = scaled
        packed = jnp.where(lane == 2 * s, jnp.sum(scaled, axis=-1, keepdims=True), packed)
        packed = jnp.where(
            lane == 2 * s + 1, jnp.sum(scaled * hat, axis=-1, keepdims=True), packed
        )
    sum_ref[...] = packed
    totals = jnp.concatenate(totals, axis=0)

    @pl.when(pl.program_id(0) == 0)
    def _():
        gain_out_ref[...] = totals

    @pl.when(pl.program_id(0) > 0)
    def _():
        gain_out_ref[...] += totals


def norm_slopes(own, got, ff_grad, low, stats, gains, which):
    tall, wide = low.shape
    width = wide // STREAMS
    rows = min(64, tall)
    row = lambda i, m: (i, 0)
    cube = pl.BlockSpec((4, rows, width), lambda i, m: (0, i, 0))
    return pl.pallas_call(
        slope_kernel,
        grid_spec=pltpu.PrefetchScalarGridSpec(
            num_scalar_prefetch=1,
            grid=(tall // rows,),
            in_specs=[
                cube,
                cube,
                pl.BlockSpec((rows, width), row),
                pl.BlockSpec((rows, wide), row),
                pl.BlockSpec((rows, 128), row),
                pl.BlockSpec(gains.shape, lambda i, m: (0, 0)),
            ],
            out_specs=[
                pl.BlockSpec((rows, wide), row),
                pl.BlockSpec((rows, 128), row),
                pl.BlockSpec((STREAMS, width), lambda i, m: (0, 0)),
            ],
        ),
        out_shape=[
            jax.ShapeDtypeStruct((tall, wide), f32),
            jax.ShapeDtypeStruct((tall, 128), f32),
            jax.ShapeDtypeStruct((STREAMS, width), f32),
        ],
        cost_estimate=pl.CostEstimate(
            flops=12 * tall * wide, bytes_accessed=12 * tall * wide, transcendentals=0
        ),
        name="norm_slopes",
    )(which, own, got, ff_grad, low, stats, gains)


def grads_kernel(
    scaled_ref, mine_ref, theirs_ref, low_ref, stat_ref, cot_ref, cur_ref, last_ref,
    grad_ref, mix_ref, dot_ref,
):
    rows, width = cot_ref.shape
    lane = lax.broadcasted_iota(jnp.int32, (rows, 128), 1)
    means = (mine_ref[...] + theirs_ref[...]) / (2 * width)
    current = cur_ref[...].astype(f32)
    packed = jnp.zeros((rows, 128), f32)
    mixed = None
    for s in range(STREAMS):
        lanes = slice(s * width, (s + 1) * width)
        average, inverse = stat_ref[:, 2 * s : 2 * s + 1], stat_ref[:, 2 * s + 1 : 2 * s + 2]
        hat = (low_ref[:, lanes].astype(f32) - average) * inverse
        grad = inverse * (
            scaled_ref[:, lanes]
            - means[:, 2 * s : 2 * s + 1]
            - hat * means[:, 2 * s + 1 : 2 * s + 2]
        )
        if s == STREAMS - 1:
            grad = grad + cot_ref[...].astype(f32)
        grad = grad.astype(bf16)
        grad_ref[:, lanes] = grad
        grad = grad.astype(f32)
        term = last_ref[:, s : s + 1] * grad
        mixed = term if mixed is None else mixed + term
        packed = jnp.where(lane == s, jnp.sum(grad * current, axis=-1, keepdims=True), packed)
    mix_ref[...] = mixed
    dot_ref[...] = packed


def stream_grads(scaled, mine, theirs, low, stats, cot, current_half, last):
    tall, wide = low.shape
    width = wide // STREAMS
    rows = min(64, tall)
    row = lambda i: (i, 0)
    return pl.pallas_call(
        grads_kernel,
        grid=(tall // rows,),
        in_specs=[
            pl.BlockSpec((rows, wide), row),
            pl.BlockSpec((rows, 128), row),
            pl.BlockSpec((rows, 128), row),
            pl.BlockSpec((rows, wide), row),
            pl.BlockSpec((rows, 128), row),
            pl.BlockSpec((rows, width), row),
            pl.BlockSpec((rows, width), row),
            pl.BlockSpec((rows, 128), row),
        ],
        out_specs=[
            pl.BlockSpec((rows, wide), row),
            pl.BlockSpec((rows, width), row),
            pl.BlockSpec((rows, 128), row),
        ],
        out_shape=[
            jax.ShapeDtypeStruct((tall, wide), bf16),
            jax.ShapeDtypeStruct((tall, width), f32),
            jax.ShapeDtypeStruct((tall, 128), f32),
        ],
        cost_estimate=pl.CostEstimate(
            flops=12 * tall * wide, bytes_accessed=10 * tall * wide, transcendentals=0
        ),
        name="stream_grads",
    )(scaled, mine, theirs, low, stats, cot, current_half, last)


def turning_tables(places):
    half = ROT // 2
    inverse = jnp.exp(jnp.arange(half, dtype=f32) * (-2.0 * math.log(10000.0) / ROT))
    angles = places.astype(f32)[:, None] * inverse[None, :]
    cosine, sine = jnp.cos(angles), jnp.sin(angles)
    rows = places.shape[0]
    rest = jnp.zeros((rows, HDIM - ROT), f32)
    blank = jnp.zeros((rows, half), f32)
    return (
        jnp.concatenate([cosine, cosine, rest + 1.0], axis=1),
        jnp.concatenate([-sine, blank, rest], axis=1),
        jnp.concatenate([blank, sine, rest], axis=1),
    )


def local(
    history,
    slot_layer,
    current,
    positions,
    doc_ids,
    cotangent,
    norm_gains,
    generator_in,
    generator_out,
    query_weight,
    key_weight,
    value_weight,
    out_weight,
    up_weight,
    down_weight,
):
    dp_count = lax.axis_size("dp")
    depth_count = lax.axis_size("depth")
    dp_at = lax.axis_index("dp")
    model_at = lax.axis_index("mp")
    dp_bits = list(range(bit_count(dp_count)))
    order_one, order_two = dp_bits, dp_bits[1:] + dp_bits[:1]
    back_one, back_two = order_one[::-1], order_two[::-1]
    slots, tokens_held, width = history.shape
    model = current.shape[1]
    rows_mb = current.shape[0] // MB
    length = depth_count * rows_mb
    heads_width = query_weight.shape[1]
    heads_each = heads_width // HDIM // depth_count
    own_rows = query_weight.shape[0]
    ff_width = up_weight.shape[1]
    ff_part = ff_width // dp_count
    both = ("dp", "depth")

    def half_of(values, axis, which):
        return lax.dynamic_slice_in_dim(values, which * width, width, axis)

    small_cols = jnp.concatenate(
        [generator_in, norm_gains.T, jnp.zeros((own_rows, 128 - GEN - 5), bf16)], axis=1
    )
    small_all = gather_small(small_cols, both).reshape(model, 128)
    gen_first = small_all[:, :GEN]
    gain_float = small_all[:, GEN : GEN + 5].astype(f32).T
    second_rows = generator_out.shape[0]
    second_pad = -second_rows % 128
    second_all = gather_small(jnp.pad(generator_out, (0, second_pad))[None], both)
    gen_second = second_all.reshape(-1, second_rows + second_pad)[:, :second_rows]
    second_low = gen_second.reshape(GEN, STREAMS * MIX)

    stacked = jnp.concatenate([query_weight, key_weight, value_weight, out_weight.T], axis=0)
    over_depth = lax.all_gather(stacked, "depth", axis=0, tiled=True)
    over_depth = over_depth.reshape(depth_count, 4, own_rows, heads_width)
    gathered = []
    for at in range(4):
        piece = over_depth[:, at].reshape(depth_count * own_rows, heads_width)
        pieces = gather_masked(piece, "dp", order_one if at % 2 == 0 else order_two)
        gathered.append(reorder_masked(jnp.stack(pieces), "dp").reshape(model, heads_width))
    query_w, key_w, value_w, out_wt = gathered

    current_f = current.astype(f32)
    current_half = half_of(current, 1, model_at)
    mean_square = jnp.mean(current_f * current_f, axis=-1, keepdims=True)
    inverse_rms = lax.rsqrt(mean_square + RMS_EPSILON)
    unit = current_f * inverse_rms
    gen_normed = (unit * gain_float[4]).astype(bf16)
    gen_pre = dot_nn(gen_normed, gen_first)
    gen_hidden = gelu_exact(gen_pre).astype(bf16)
    column = jnp.arange(STREAMS * MIX)
    last_col = (column % MIX == MIX - 1).astype(f32)
    mixing = (dot_nn(gen_hidden, second_low) + last_col).astype(bf16)
    pick_last = (column[:, None] == (jnp.arange(128) * MIX + MIX - 1)[None, :]).astype(bf16)
    last = dot_nn(mixing, pick_last)

    layer_of = jnp.tile(slot_layer, STREAMS)
    stream_of = jnp.repeat(jnp.arange(STREAMS), slots)
    from_col = jnp.where(layer_of < MIX, stream_of * MIX + layer_of, -1)
    pick = (column[:, None] == from_col[None, :]).astype(f32)
    mix_all = gather_small(mixing, ("depth",)).reshape(depth_count * MB * rows_mb, STREAMS * MIX)
    slot_mix = dot_nn(mix_all, pick.astype(bf16))

    ff_local = jnp.stack([up_weight, down_weight.T])
    ff_local, slot_mix = lax.optimization_barrier((ff_local, slot_mix))
    ff_pieces = [
        lax.dynamic_slice_in_dim(ff_local, (dp_at ^ m) * ff_part, ff_part, 2)
        for m in range(dp_count)
    ]
    ff_pieces = [ff_pieces[0]] + [swap_mask(ff_pieces[m], "dp", m) for m in range(1, dp_count)]
    ff_rows = reorder_masked(jnp.stack(ff_pieces), "dp")

    def ff_gather(at):
        flat = ff_rows[:, at].reshape(dp_count * own_rows, ff_part)
        full = lax.all_gather(flat, "depth", axis=0, tiled=True)
        full = full.reshape(depth_count, dp_count, own_rows, ff_part)
        return jnp.swapaxes(full, 0, 1).reshape(model, ff_part)

    up_w, down_wt = ff_gather(0), ff_gather(1)

    cotangent, slot_mix = lax.optimization_barrier((cotangent, slot_mix))
    cot_full = join_halves(cotangent, other_core(cotangent), model_at)
    cot_group = []
    for micro_at in range(MB):
        rows = cotangent[micro_at * rows_mb : (micro_at + 1) * rows_mb]
        order = order_one if micro_at % 2 == 0 else order_two
        mine = jnp.concatenate(gather_masked(rows, "dp", order), axis=0)
        cot_group.append(join_halves(mine, other_core(mine), model_at))

    places_all = gather_small(positions, ("depth",))
    document_view = doc_ids.reshape(depth_count, MB, rows_mb)
    own_tables = turning_tables(positions)
    which = model_at.astype(jnp.int32)[None]
    gains = gain_float

    saved = []
    for micro_at in range(MB):
        span = slice(micro_at * rows_mb, (micro_at + 1) * rows_mb)
        partial = mix_streams(slot_mix, history, micro_at, depth_count, rows_mb)
        parts = partial.reshape(depth_count, rows_mb, STREAMS * width)
        parts = lax.all_to_all(parts, "depth", 0, 0, tiled=True)
        low, resid = total_streams(parts, current_half[span], last[span])
        normed, ff_normed, stats = norm_streams(low, other_core(low), gains, which)

        packed = project_heads(
            normed,
            cot_full[span],
            [query_w, key_w, value_w, out_wt],
            [t[span] for t in own_tables],
            depth_count,
        )
        by_head = lax.all_to_all(packed, "depth", 0, 0, tiled=True)
        by_head = by_head.reshape(length, 4 * heads_each * HDIM)
        documents = document_view[:, micro_at].reshape(length)
        seq_places = places_all[:, span].reshape(length)
        answer = attend(by_head, documents, turning_tables(seq_places), heads_each)
        answer = answer.reshape(depth_count, rows_mb, 4 * heads_each * HDIM)
        answer = lax.all_to_all(answer, "depth", 0, 0, tiled=True)

        order = order_one if micro_at % 2 == 0 else order_two
        back = back_one if micro_at % 2 == 0 else back_two
        mine = jnp.concatenate(gather_masked(ff_normed, "dp", order), axis=0)
        group_normed = join_halves(mine, other_core(mine), model_at)
        hidden, grad_up, out_own, out_other, back_own, back_other = feed_forward(
            group_normed, cot_group[micro_at], up_w, down_wt, which
        )

        def reduce_group(own, other, back=back):
            total = own + other_core(other).astype(f32)
            return scatter_masked(jnp.split(total, dp_count, axis=0), "dp", back)

        grad_norm_ff = reduce_group(back_own, back_other)
        ff_out = reduce_group(out_own, out_other)

        weights = [out_wt, query_w, key_w, value_w]
        (theirs,) = back_project(answer, weights, 1 - which, bf16, False)
        got = other_core(theirs)
        own, flat = back_project(answer, weights, which, f32, True)
        layer_rows = (resid + own[0] + got[0].astype(f32) + ff_out).astype(bf16)
        scaled, sums, gain_part = norm_slopes(own, got, grad_norm_ff, low, stats, gains, which)
        grad_low, current_mix, last_dot = stream_grads(
            scaled, sums, other_core(sums), low, stats, cotangent[span], current_half[span], last[span]
        )
        grad_all = lax.all_gather(grad_low, "depth", axis=0, tiled=True)
        saved.append(
            dict(
                normed=normed,
                group_normed=group_normed,
                hidden=hidden,
                grad_up=grad_up,
                flat=flat,
                grad_all=grad_all,
                grad_low=grad_low,
                layer_rows=layer_rows,
                gain=gain_part,
                current_mix=current_mix,
                last_dot=last_dot,
            )
        )

    def rows_of(name, at=None):
        return jnp.concatenate([s[name] if at is None else s[name][at] for s in saved], axis=0)

    def over_depth_sum(values):
        arrived = lax.all_to_all(values, "depth", 0, 0, tiled=True).astype(f32)
        return jnp.sum(arrived, axis=0)

    left = [rows_of("normed", 0), rows_of("normed", 1), rows_of("normed", 2), cot_full]
    right = [rows_of("flat", 1), rows_of("flat", 2), rows_of("flat", 3), rows_of("flat", 0)]
    scattered = []
    for at in range(4):
        by_dp = dot_tn(left[at], right[at]).reshape(dp_count, model // dp_count, heads_width)
        pieces = [
            lax.dynamic_index_in_dim(by_dp, dp_at ^ m, 0, keepdims=False) for m in range(dp_count)
        ]
        total = scatter_masked(pieces, "dp", back_one if at % 2 == 0 else back_two)
        total = total.astype(bf16).reshape(depth_count, own_rows, heads_width)
        scattered.append(over_depth_sum(total))

    def ff_scatter(left, right):
        grads = dot_tn(left, right).astype(bf16)
        grads = grads.reshape(dp_count, depth_count, own_rows, ff_part)
        return over_depth_sum(jnp.swapaxes(grads, 0, 1))

    cot_group_all = jnp.concatenate(cot_group, axis=0)
    ff_grads = [
        ff_scatter(rows_of("group_normed"), rows_of("grad_up")),
        ff_scatter(cot_group_all, rows_of("hidden")),
    ]
    ff_grads = jnp.stack(ff_grads).astype(bf16)
    ff_pieces = [
        lax.dynamic_index_in_dim(ff_grads, dp_at ^ m, 1, keepdims=False) for m in range(dp_count)
    ]
    ff_pieces = [ff_pieces[0]] + [swap_mask(ff_pieces[m], "dp", m) for m in range(1, dp_count)]
    ff_cols = reorder_masked(jnp.stack(ff_pieces), "dp").astype(f32)
    up_grad = jnp.swapaxes(ff_cols[:, 0], 0, 1).reshape(own_rows, ff_width)
    down_grad = jnp.swapaxes(ff_cols[:, 1], 1, 2).reshape(ff_width, own_rows)

    history_grad = None
    slot_parts = []
    for micro_at in range(MB):
        history_grad, slot_part = unmix_streams(
            slot_mix, history, saved[micro_at]["grad_all"], micro_at, depth_count, rows_mb, history_grad
        )
        slot_parts.append(slot_part.reshape(depth_count, 1, rows_mb, 128))
    slot_grads = jnp.concatenate(slot_parts, axis=1).reshape(-1, 128)[:, : STREAMS * slots]
    mix_grads = dot_exact(slot_grads, pick.T).reshape(depth_count, MB * rows_mb, STREAMS * MIX)
    grad_mixing = scatter_small(mix_grads, ("depth",))
    last_dots = rows_of("last_dot")
    grad_mixing = grad_mixing + dot_exact(last_dots, pick_last.astype(f32).T)
    grad_mixing = grad_mixing + other_core(grad_mixing)

    second_float = second_low.astype(f32)
    grad_second = dot_exact(gen_hidden.astype(f32).T, grad_mixing)
    grad_pre = dot_exact(grad_mixing, second_float.T) * gelu_slope(gen_pre)
    grad_first = dot_exact(gen_normed.astype(f32).T, grad_pre)
    grad_gen_normed = dot_exact(grad_pre, gen_first.astype(f32).T)
    gain_gen = jnp.sum(grad_gen_normed * unit, axis=0)
    grad_unit = grad_gen_normed * gain_float[4]
    shared = jnp.mean(grad_unit * unit, axis=-1, keepdims=True)
    current_gen = half_of(inverse_rms * (grad_unit - unit * shared), 1, model_at)
    current_grad = rows_of("current_mix") + current_gen

    gain_own = sum(s["gain"] for s in saved)
    gain_other = other_core(gain_own)
    gain_all = jnp.where(
        model_at == 0,
        jnp.concatenate([gain_own, gain_other], axis=1),
        jnp.concatenate([gain_other, gain_own], axis=1),
    )
    gain_all = jnp.concatenate([gain_all, gain_gen[None]], axis=0)
    small_grads = jnp.concatenate(
        [grad_first, gain_all.T, jnp.zeros((model, 128 - GEN - 5), f32)], axis=1
    )
    small_grads = scatter_small(small_grads.reshape(-1, own_rows, 128), both)
    second_grads = jnp.pad(grad_second.reshape(-1, second_rows), ((0, 0), (0, second_pad)))
    second_grads = scatter_small(second_grads[:, None], both)

    return (
        rows_of("layer_rows"),
        history_grad,
        current_grad,
        small_grads[:, GEN : GEN + 5].T,
        small_grads[:, :GEN],
        second_grads[0, :second_rows],
        scattered[0],
        scattered[1],
        scattered[2],
        scattered[3].T,
        up_grad,
        down_grad,
    )


def solution(mesh):
    return jax.shard_map(
        local,
        mesh=mesh,
        in_specs=(
            P("depth", "dp", "mp"),
            P("depth"),
            P(("dp", "depth"), None),
            P(("dp", "depth")),
            P("dp"),
            P(("dp", "depth"), "mp"),
            P(None, ("dp", "depth")),
            P(("dp", "depth"), None),
            P(("dp", "depth")),
            P(("dp", "depth"), "mp"),
            P(("dp", "depth"), "mp"),
            P(("dp", "depth"), "mp"),
            P("mp", ("dp", "depth")),
            P(("dp", "depth"), "mp"),
            P("mp", ("dp", "depth")),
        ),
        out_specs=(
            P(("dp", "depth"), "mp"),
            P("depth", "dp", "mp"),
            P(("dp", "depth"), "mp"),
            P(None, ("dp", "depth")),
            P(("dp", "depth"), None),
            P(("dp", "depth")),
            P(("dp", "depth"), "mp"),
            P(("dp", "depth"), "mp"),
            P(("dp", "depth"), "mp"),
            P("mp", ("dp", "depth")),
            P(("dp", "depth"), "mp"),
            P("mp", ("dp", "depth")),
        ),
        check_vma=False,
    )
```

```python
import functools
import math

import jax
import jax.numpy as jnp
from jax import lax
from jax.experimental import pallas as pl
from jax.experimental.pallas import tpu as pltpu
from jax.sharding import PartitionSpec as P

HDIM = 128
ROT = 32
GEN = 72
MB = 2
MIX = 18
STREAMS = 4
COST = 1

PRECISE = lax.Precision.HIGHEST
NORM_EPSILON = 1e-05
RMS_EPSILON = 1e-06
MASKED = -1e30

bf16 = jnp.bfloat16
f32 = jnp.float32


def dot_nn(a, b):
    return lax.dot_general(a, b, (((1,), (0,)), ((), ())), preferred_element_type=f32)


def dot_nt(a, b):
    return lax.dot_general(a, b, (((1,), (1,)), ((), ())), preferred_element_type=f32)


def dot_tn(a, b):
    return lax.dot_general(a, b, (((0,), (0,)), ((), ())), preferred_element_type=f32)


def dot_exact(a, b):
    return jnp.dot(a, b, precision=PRECISE, preferred_element_type=f32)


def gelu_exact(values):
    return jax.nn.gelu(values, approximate=False)


def gelu_slope(values):
    result, pullback = jax.vjp(gelu_exact, values)
    return pullback(jnp.ones_like(result))[0]


def bit_count(size):
    count = size.bit_length() - 1
    assert 1 << count == size
    return count


def swap_mask(values, axis, mask):
    size = lax.axis_size(axis)
    return lax.ppermute(values, axis, [(i, i ^ mask) for i in range(size)])


def gather_masked(values, axis, order):
    pieces = {0: values}
    for bit in order:
        arrived = {m | (1 << bit): swap_mask(v, axis, 1 << bit) for m, v in pieces.items()}
        pieces.update(arrived)
    return [pieces[m] for m in range(len(pieces))]


def scatter_masked(pieces, axis, order, link=bf16):
    pieces = dict(enumerate(pieces))
    for bit in order:
        flag = 1 << bit
        for m in [m for m in pieces if m & flag]:
            arrived = swap_mask(pieces.pop(m).astype(link), axis, flag)
            pieces[m ^ flag] = pieces[m ^ flag].astype(f32) + arrived.astype(f32)
    return pieces[0]


def core_orders():
    bits = list(range(bit_count(lax.axis_size("dp"))))
    return bits, bits[1:] + bits[:1]


def place_mask(place):
    masks = []
    for order in core_orders():
        masks.append(sum(1 << bit for at, bit in enumerate(order) if (place >> at) & 1))
    return jnp.where(lax.axis_index("mp") % 2 == 0, masks[0], masks[1])


def place_index(place):
    return lax.axis_index("dp") ^ place_mask(place)


def core_hop(values, at):
    orders, cores = core_orders(), lax.axis_size("mp")
    pairs = []
    for i in range(lax.axis_size("dp")):
        for core in range(cores):
            partner = i ^ (1 << orders[core % 2][at])
            pairs.append((i * cores + core, partner * cores + core))
    return lax.ppermute(values, ("dp", "mp"), pairs)


def group_gather(values):
    pieces = values[None]
    for at in range(bit_count(lax.axis_size("dp"))):
        pieces = jnp.concatenate([pieces, core_hop(pieces, at)], axis=0)
    buffer = None
    for place in range(pieces.shape[0]):
        buffer = place_block(
            buffer, pieces[place][None], place_index(place), pieces.shape[0]
        )
    return buffer[0]


def group_scatter(blocks):
    count = blocks.shape[0]
    pieces = [
        lax.dynamic_index_in_dim(blocks, place_index(p), 0, keepdims=False) for p in range(count)
    ]
    for at in reversed(range(bit_count(count))):
        half = 1 << at
        arrived = core_hop(jnp.stack(pieces[half : 2 * half]).astype(bf16), at).astype(f32)
        pieces = [pieces[p] + arrived[p] for p in range(half)]
    return pieces[0]


def reorder_masked(stacked, axis):
    count = bit_count(stacked.shape[0])
    here = lax.axis_index(axis)
    shape = stacked.shape
    values = stacked.reshape((2,) * count + shape[1:])
    for bit in range(count):
        turned = jnp.flip(values, count - 1 - bit)
        values = jnp.where(((here >> bit) & 1) == 1, turned, values)
    return values.reshape(shape)


def gather_small(values, axes):
    shape = values.shape
    values = values[None]
    for axis in reversed(axes):
        order = range(bit_count(lax.axis_size(axis)))
        stacked = jnp.stack(gather_masked(values, axis, order))
        values = reorder_masked(stacked, axis)
        values = values.reshape((-1,) + shape)
    return values


def scatter_small(values, axes):
    for axis in axes:
        size = lax.axis_size(axis)
        values = values.reshape((size, values.shape[0] // size) + values.shape[1:])
        turned = reorder_masked(values, axis)
        order = reversed(range(bit_count(size)))
        values = scatter_masked([turned[m] for m in range(size)], axis, order, f32)
    return values[0]


def line_size():
    return lax.axis_size("depth"), lax.axis_index("depth")


def fence(*values):
    return lax.optimization_barrier(values)


class LineGather:

    def __init__(self, values):
        self.up, self.down = [values], [values]

    def step(self):
        size, _ = line_size()
        at = len(self.up)
        if at < size:
            up_pairs = [(i, i + 1) for i in range(at - 1, size - 1)]
            down_pairs = [(i, i - 1) for i in range(1, size - at + 1)]
            self.up.append(lax.ppermute(self.up[-1], "depth", up_pairs))
            self.down.append(lax.ppermute(self.down[-1], "depth", down_pairs))

    def hold(self, *others):
        kept = fence((self.up[1:], self.down[1:]), *others)
        (up, down), rest = kept[0], kept[1:]
        self.up, self.down = self.up[:1] + list(up), self.down[:1] + list(down)
        return rest

    def placed(self):
        size, here = line_size()
        buffer = place_block(None, self.up[0], here, size)
        for at in range(1, size):
            buffer = place_block(
                buffer,
                self.up[at],
                lax.rem(here - at + size, size),
                size,
                self.down[size - at],
                here >= at,
            )
        return buffer


class LineScatter:

    def __init__(self, terms):
        self.terms, self.at = terms, 0
        self.up = self.down = None

    def step(self):
        size, here = line_size()
        self.at += 1
        if self.at >= size:
            return
        goes_up, goes_down = hop_sums(
            self.terms,
            jnp.minimum(size - self.at + here, size - 1),
            jnp.maximum(here - size + self.at, 0),
            self.up,
            self.down,
        )
        up_pairs = [(i, i + 1) for i in range(min(self.at, size - 1))]
        down_pairs = [(size - 1 - i, size - 2 - i) for i in range(min(self.at, size - 1))]
        self.up = lax.ppermute(goes_up, "depth", up_pairs)
        self.down = lax.ppermute(goes_down, "depth", down_pairs)

    def hold(self, *others):
        (self.up, self.down), *rest = fence((self.up, self.down), *others)
        return rest


def other_core(values):
    return swap_mask(values, "mp", 1)


def join_kernel(model_ref, own_ref, other_ref, out_ref):
    width = own_ref.shape[1]
    own_at = pl.multiple_of(model_ref[0] * width, width)
    other_at = pl.multiple_of((1 - model_ref[0]) * width, width)
    out_ref[:, pl.ds(own_at, width)] = own_ref[...]
    out_ref[:, pl.ds(other_at, width)] = other_ref[...]


def join_halves(own, other, model_at):
    tall, width = own.shape
    rows = min(256, tall)
    return pl.pallas_call(
        join_kernel,
        grid_spec=pltpu.PrefetchScalarGridSpec(
            num_scalar_prefetch=1,
            grid=(tall // rows,),
            in_specs=[pl.BlockSpec((rows, width), lambda i, m: (i, 0))] * 2,
            out_specs=pl.BlockSpec((rows, 2 * width), lambda i, m: (i, 0)),
        ),
        out_shape=jax.ShapeDtypeStruct((tall, 2 * width), own.dtype),
        cost_estimate=spent(
            flops=0, bytes_accessed=8 * tall * width, transcendentals=0
        ),
        name="join_halves",
    )(model_at.astype(jnp.int32)[None], own, other)


def spent(flops, bytes_accessed, transcendentals):
    return pl.CostEstimate(
        flops=flops // COST, bytes_accessed=bytes_accessed // COST, transcendentals=transcendentals // COST
    )


def chunk_of(tall, wide):
    rows = tall
    while rows * wide > 1 << 19 and rows % 32 == 0:
        rows //= 2
    return rows


def place_kernel(at_ref, *refs):
    if len(refs) < 4:
        refs[-1][0, 0] = refs[0][0]
        return

    @pl.when(at_ref[1] == 1)
    def _():
        refs[-1][0, 0] = refs[0][0]

    @pl.when(at_ref[1] == 0)
    def _():
        refs[-1][0, 0] = refs[1][0]


def place_block(buffer, block, index, count, instead=None, first=None):
    lead, tall, wide = block.shape
    rows = chunk_of(tall, wide)
    spec = pl.BlockSpec((1, rows, wide), lambda l, i, m: (l, i, 0))
    blocks = [block] if instead is None else [block, instead]
    where = [index, 1 if first is None else first]
    where = jnp.stack([jnp.asarray(v).astype(jnp.int32) for v in where])
    in_specs, operands, aliases = [spec] * len(blocks), list(blocks), {}
    if buffer is not None or instead is not None:
        in_specs.append(pl.BlockSpec(memory_space=pl.ANY))
        operands.append(block if buffer is None else buffer)
        aliases = {} if buffer is None else {len(operands): 0}
    return pl.pallas_call(
        place_kernel,
        grid_spec=pltpu.PrefetchScalarGridSpec(
            num_scalar_prefetch=1,
            grid=(lead, tall // rows),
            in_specs=in_specs,
            out_specs=pl.BlockSpec((1, 1, rows, wide), lambda l, i, m: (l, m[0], i, 0)),
        ),
        out_shape=jax.ShapeDtypeStruct((lead, count, tall, wide), block.dtype),
        input_output_aliases=aliases,
        cost_estimate=spent(
            flops=0, bytes_accessed=4 * lead * tall * wide, transcendentals=0
        ),
        name="place_block",
    )(where, *operands)


def hop_kernel(at_ref, *refs):
    ins, outs = refs[:-2], refs[-2:]
    for way in range(2):
        term = ins[way][0, 0].astype(f32)
        if len(ins) > 2:
            term = term + ins[2 + way][0].astype(f32)
        outs[way][0] = term.astype(bf16)


def hop_sums(terms, up_at, down_at, up, down):
    lead, _, tall, wide = terms.shape
    rows = chunk_of(tall, wide)
    block = pl.BlockSpec((1, rows, wide), lambda l, i, m: (l, i, 0))
    in_specs = [
        pl.BlockSpec((1, 1, rows, wide), lambda l, i, m: (l, m[0], i, 0)),
        pl.BlockSpec((1, 1, rows, wide), lambda l, i, m: (l, m[1], i, 0)),
    ]
    operands = [terms, terms]
    if up is not None:
        in_specs += [block, block]
        operands += [up, down]
    return pl.pallas_call(
        hop_kernel,
        grid_spec=pltpu.PrefetchScalarGridSpec(
            num_scalar_prefetch=1,
            grid=(lead, tall // rows),
            in_specs=in_specs,
            out_specs=[block, block],
        ),
        out_shape=[jax.ShapeDtypeStruct((lead, tall, wide), bf16)] * 2,
        cost_estimate=spent(
            flops=2 * lead * tall * wide, bytes_accessed=12 * lead * tall * wide, transcendentals=0
        ),
        name="hop_sums",
    )(jnp.stack([up_at, down_at]).astype(jnp.int32), *operands)


def end_kernel(at_ref, term_ref, up_ref, down_ref, out_ref):
    total = term_ref[0, 0].astype(f32) + up_ref[0].astype(f32) + down_ref[0].astype(f32)
    out_ref[0] = total.astype(out_ref.dtype)


def end_sums(sums, dtype):
    lead, _, tall, wide = sums.terms.shape
    rows = chunk_of(tall, wide)
    block = pl.BlockSpec((1, rows, wide), lambda l, i, m: (l, i, 0))
    return pl.pallas_call(
        end_kernel,
        grid_spec=pltpu.PrefetchScalarGridSpec(
            num_scalar_prefetch=1,
            grid=(lead, tall // rows),
            in_specs=[
                pl.BlockSpec((1, 1, rows, wide), lambda l, i, m: (l, m[0], i, 0)),
                block,
                block,
            ],
            out_specs=block,
        ),
        out_shape=jax.ShapeDtypeStruct((lead, tall, wide), dtype),
        cost_estimate=spent(
            flops=2 * lead * tall * wide, bytes_accessed=10 * lead * tall * wide, transcendentals=0
        ),
        name="end_sums",
    )(lax.axis_index("depth").astype(jnp.int32)[None], sums.terms, sums.up, sums.down)


def attention_grad_kernel(
    at_ref, x0_ref, x1_ref, cot_ref, g0_ref, g1_ref, out_ref
):
    tall = x0_ref.shape[1]

    def store(total):
        out_ref[...] = total.reshape(out_ref.shape).astype(out_ref.dtype)

    @pl.when(pl.program_id(0) < 3)
    def _():
        store(dot_tn(x0_ref[0], g0_ref[0]) + dot_tn(x1_ref[0], g1_ref[0]))

    @pl.when(pl.program_id(0) == 3)
    def _():
        store(
            dot_tn(cot_ref[0:tall, :], g0_ref[0]) + dot_tn(cot_ref[tall : 2 * tall, :], g1_ref[0])
        )


def attention_grads(normed, cot, flat, place, depth_count, dp_count, dtype):
    _, tall, model = normed[0].shape
    heads_width = flat[0].shape[2]
    block = model // dp_count
    own_rows = block // depth_count
    normed_spec = pl.BlockSpec((1, tall, block), lambda k, m: (jnp.minimum(k, 2), 0, m[0]))
    flat_spec = pl.BlockSpec((1, tall, heads_width), lambda k, m: (lax.rem(k + 1, 4), 0, 0))
    return pl.pallas_call(
        attention_grad_kernel,
        grid_spec=pltpu.PrefetchScalarGridSpec(
            num_scalar_prefetch=1,
            grid=(4,),
            in_specs=[
                normed_spec,
                normed_spec,
                pl.BlockSpec((2 * tall, block), lambda k, m: (0, m[0])),
                flat_spec,
                flat_spec,
            ],
            out_specs=pl.BlockSpec(
                (depth_count, 1, own_rows, heads_width), lambda k, m: (0, k, 0, 0)
            ),
        ),
        out_shape=jax.ShapeDtypeStruct((depth_count, 4, own_rows, heads_width), dtype),
        compiler_params=pltpu.CompilerParams(vmem_limit_bytes=40 << 20),
        cost_estimate=spent(
            flops=16 * tall * block * heads_width,
            bytes_accessed=16 * block * heads_width,
            transcendentals=0,
        ),
        name="attention_grads",
    )(place, *normed, cot, *flat)


def hidden_grad_kernel(x0_ref, x1_ref, c0_ref, c1_ref, u0_ref, u1_ref, h0_ref, h1_ref, out_ref):
    def store(total):
        out_ref[...] = total.reshape(out_ref.shape)

    @pl.when(pl.program_id(0) == 0)
    def _():
        store(dot_tn(x0_ref[...], u0_ref[...]) + dot_tn(x1_ref[...], u1_ref[...]))

    @pl.when(pl.program_id(0) == 1)
    def _():
        store(dot_tn(c0_ref[0], h0_ref[...]) + dot_tn(c1_ref[0], h1_ref[...]))


def hidden_grads(x, cot, up_grads, hidden, dp_count, depth_count):
    tall, model = x[0].shape
    part = hidden[0].shape[1]
    block = model // dp_count
    cols = pl.BlockSpec((tall, block), lambda k, n: (0, n * (1 - k)))
    whole = pl.BlockSpec((tall, part), lambda k, n: (0, 0))
    return pl.pallas_call(
        hidden_grad_kernel,
        grid=(2, dp_count),
        in_specs=[cols, cols]
        + [
            pl.BlockSpec((1, tall, block), lambda k, n: (0, 0, n * k)),
            pl.BlockSpec((1, tall, block), lambda k, n: (1, 0, n * k)),
        ]
        + [whole] * 4,
        out_specs=pl.BlockSpec(
            (1, depth_count, block // depth_count, part), lambda k, n: (k * dp_count + n, 0, 0, 0)
        ),
        out_shape=jax.ShapeDtypeStruct(
            (2 * dp_count, depth_count, block // depth_count, part), f32
        ),
        compiler_params=pltpu.CompilerParams(vmem_limit_bytes=48 << 20),
        cost_estimate=spent(
            flops=8 * tall * model * part, bytes_accessed=8 * model * part, transcendentals=0
        ),
        name="hidden_grads",
    )(*x, cot, cot, *up_grads, *hidden)


def mix_kernel(slots, mix_ref, hist_ref, out_ref):
    rows, width = hist_ref.shape[1], hist_ref.shape[2]
    part = 512 if width % 512 == 0 else width

    def step(at, carry):
        r0 = pl.multiple_of(at * 16, 16)
        weights = mix_ref[pl.ds(r0, 16), :]
        for c0 in range(0, width, part):
            sums = [None] * STREAMS
            for k in range(slots):
                state = hist_ref[k, pl.ds(r0, 16), c0 : c0 + part].astype(f32)
                for s in range(STREAMS):
                    term = weights[:, s * slots + k : s * slots + k + 1] * state
                    sums[s] = term if sums[s] is None else sums[s] + term
            for s in range(STREAMS):
                out_ref[pl.ds(r0, 16), s * width + c0 : s * width + c0 + part] = sums[s].astype(bf16)
        return carry

    lax.fori_loop(0, rows // 16, step, 0)


def mix_streams(slot_mix, history, micro_at, depth_count, rows_mb):
    slots, _, width = history.shape
    rows = min(128, rows_mb)
    per = rows_mb // rows

    def row_block(i):
        return ((i // per) * MB + micro_at) * per + i % per

    return pl.pallas_call(
        functools.partial(mix_kernel, slots),
        grid=(depth_count * per,),
        in_specs=[
            pl.BlockSpec((rows, slot_mix.shape[1]), lambda i: (row_block(i), 0)),
            pl.BlockSpec((slots, rows, width), lambda i: (0, row_block(i), 0)),
        ],
        out_specs=pl.BlockSpec((rows, STREAMS * width), lambda i: (i, 0)),
        out_shape=jax.ShapeDtypeStruct((depth_count * rows_mb, STREAMS * width), bf16),
        cost_estimate=spent(
            flops=2 * slots * STREAMS * depth_count * rows_mb * width,
            bytes_accessed=2 * (slots + STREAMS) * depth_count * rows_mb * width,
            transcendentals=0,
        ),
        name="mix_streams",
    )(slot_mix, history)


def unmix_kernel(slots, mix_ref, hist_ref, grad_ref, *rest):
    hist_grad_ref, slot_grad_ref = rest[-2:]
    rows, width = hist_ref.shape[1], hist_ref.shape[2]
    part = 512 if width % 512 == 0 else width

    def step(at, carry):
        r0 = pl.multiple_of(at * 16, 16)
        weights = mix_ref[pl.ds(r0, 16), :]
        totals = [None] * (STREAMS * slots)
        for c0 in range(0, width, part):
            grads = [
                grad_ref[pl.ds(r0, 16), s * width + c0 : s * width + c0 + part].astype(f32)
                for s in range(STREAMS)
            ]
            for k in range(slots):
                state = hist_ref[k, pl.ds(r0, 16), c0 : c0 + part].astype(f32)
                back = None
                for s in range(STREAMS):
                    at_sk = s * slots + k
                    term = weights[:, at_sk : at_sk + 1] * grads[s]
                    back = term if back is None else back + term
                    product = state * grads[s]
                    folded = product[:, 0:128]
                    for l0 in range(128, part, 128):
                        folded = folded + product[:, l0 : l0 + 128]
                    totals[at_sk] = folded if totals[at_sk] is None else totals[at_sk] + folded
                hist_grad_ref[k, pl.ds(r0, 16), c0 : c0 + part] = back.astype(bf16)
        lane = lax.broadcasted_iota(jnp.int32, (16, 128), 1)
        packed = jnp.zeros((16, 128), f32)
        for at_sk in range(STREAMS * slots):
            column = jnp.sum(totals[at_sk], axis=1, keepdims=True)
            packed = jnp.where(lane == at_sk, column, packed)
        slot_grad_ref[pl.ds(r0, 16), :] = packed
        return carry

    lax.fori_loop(0, rows // 16, step, 0)


def unmix_streams(slot_mix, history, grads, micro_at, depth_count, rows_mb, earlier):
    slots, tokens, width = history.shape
    rows = min(128, rows_mb)
    per = rows_mb // rows

    def row_block(i):
        return ((i // per) * MB + micro_at) * per + i % per

    in_specs = [
        pl.BlockSpec((rows, slot_mix.shape[1]), lambda i: (row_block(i), 0)),
        pl.BlockSpec((slots, rows, width), lambda i: (0, row_block(i), 0)),
        pl.BlockSpec((rows, STREAMS * width), lambda i: (i, 0)),
    ]
    operands = [slot_mix, history, grads]
    aliases = {}
    if earlier is not None:
        in_specs.append(pl.BlockSpec(memory_space=pl.ANY))
        operands.append(earlier)
        aliases = {3: 0}
    return pl.pallas_call(
        functools.partial(unmix_kernel, slots),
        grid=(depth_count * per,),
        in_specs=in_specs,
        out_specs=[
            pl.BlockSpec((slots, rows, width), lambda i: (0, row_block(i), 0)),
            pl.BlockSpec((rows, 128), lambda i: (i, 0)),
        ],
        out_shape=[
            jax.ShapeDtypeStruct((slots, tokens, width), bf16),
            jax.ShapeDtypeStruct((depth_count * rows_mb, 128), f32),
        ],
        input_output_aliases=aliases,
        cost_estimate=spent(
            flops=4 * slots * STREAMS * depth_count * rows_mb * width,
            bytes_accessed=2 * (2 * slots + STREAMS) * depth_count * rows_mb * width,
            transcendentals=0,
        ),
        name="unmix_streams",
    )(*operands)


def own_spans(model_ref, width):
    own_at = pl.multiple_of(model_ref[0] * width, width)
    other_at = pl.multiple_of((1 - model_ref[0]) * width, width)
    return pl.ds(own_at, width), pl.ds(other_at, width)


def ff_split_kernel(at_ref, up_ref, down_ref, out_ref):
    out_ref[0, 0] = up_ref[...]
    out_ref[0, 1] = down_ref[...].T


def ff_split(up_weight, down_weight, partners):
    own_rows, ff_width = up_weight.shape
    count = partners.shape[0]
    part = ff_width // count
    return pl.pallas_call(
        ff_split_kernel,
        grid_spec=pltpu.PrefetchScalarGridSpec(
            num_scalar_prefetch=1,
            grid=(count,),
            in_specs=[
                pl.BlockSpec((own_rows, part), lambda i, m: (0, m[i])),
                pl.BlockSpec((part, own_rows), lambda i, m: (m[i], 0)),
            ],
            out_specs=pl.BlockSpec((1, 2, own_rows, part), lambda i, m: (i, 0, 0, 0)),
        ),
        out_shape=jax.ShapeDtypeStruct((count, 2, own_rows, part), bf16),
        cost_estimate=spent(flops=0, bytes_accessed=8 * own_rows * ff_width, transcendentals=0),
        name="ff_split",
    )(partners, up_weight, down_weight)


def ff_join_kernel(at_ref, piece_ref, up_ref, down_ref):
    up_ref[...] = piece_ref[0, 0].astype(f32)
    down_ref[...] = piece_ref[0, 1].astype(f32).T


def ff_join(pieces, partners):
    count, _, own_rows, part = pieces.shape
    return pl.pallas_call(
        ff_join_kernel,
        grid_spec=pltpu.PrefetchScalarGridSpec(
            num_scalar_prefetch=1,
            grid=(count,),
            in_specs=[pl.BlockSpec((1, 2, own_rows, part), lambda i, m: (i, 0, 0, 0))],
            out_specs=[
                pl.BlockSpec((own_rows, part), lambda i, m: (0, m[i])),
                pl.BlockSpec((part, own_rows), lambda i, m: (m[i], 0)),
            ],
        ),
        out_shape=[
            jax.ShapeDtypeStruct((own_rows, count * part), f32),
            jax.ShapeDtypeStruct((count * part, own_rows), f32),
        ],
        cost_estimate=spent(
            flops=0, bytes_accessed=12 * own_rows * count * part, transcendentals=0
        ),
        name="ff_join",
    )(partners, pieces)


def total_kernel(depth_ref, part_ref, up_ref, down_ref, cur_ref, last_ref, low_ref, resid_ref):
    width = resid_ref.shape[1]
    current = cur_ref[...].astype(f32)
    for s in range(STREAMS):
        lanes = slice(s * width, (s + 1) * width)
        total = part_ref[0, 0, :, lanes].astype(f32)
        total = total + up_ref[0, :, lanes].astype(f32) + down_ref[0, :, lanes].astype(f32)
        total = total + last_ref[:, s : s + 1] * current
        if s == STREAMS - 1:
            resid_ref[...] = total
        low_ref[:, lanes] = total.astype(bf16)


def total_streams(sums, current_half, last, depth_at):
    _, _, tall, wide = sums.terms.shape
    width = wide // STREAMS
    rows = min(64, tall)
    row = lambda i, d: (i, 0)
    return pl.pallas_call(
        total_kernel,
        grid_spec=pltpu.PrefetchScalarGridSpec(
            num_scalar_prefetch=1,
            grid=(tall // rows,),
            in_specs=[
                pl.BlockSpec((1, 1, rows, wide), lambda i, d: (0, d[0], i, 0)),
                pl.BlockSpec((1, rows, wide), lambda i, d: (0, i, 0)),
                pl.BlockSpec((1, rows, wide), lambda i, d: (0, i, 0)),
                pl.BlockSpec((rows, width), row),
                pl.BlockSpec((rows, 128), row),
            ],
            out_specs=[pl.BlockSpec((rows, wide), row), pl.BlockSpec((rows, width), row)],
        ),
        out_shape=[
            jax.ShapeDtypeStruct((tall, wide), bf16),
            jax.ShapeDtypeStruct((tall, width), f32),
        ],
        cost_estimate=spent(flops=5 * tall * wide, bytes_accessed=9 * tall * wide, transcendentals=0),
        name="total_streams",
    )(depth_at, sums.terms, sums.up, sums.down, current_half, last)


def norm_kernel(model_ref, own_ref, other_ref, gain_ref, normed_ref, ff_ref, stat_ref):
    rows, width = ff_ref.shape
    model = 2 * width
    own_span, other_span = own_spans(model_ref, width)
    lane = lax.broadcasted_iota(jnp.int32, (rows, 128), 1)
    stats = jnp.zeros((rows, 128), f32)
    for s in range(STREAMS):
        lanes = slice(s * width, (s + 1) * width)
        own = own_ref[:, lanes].astype(f32)
        other = other_ref[:, lanes].astype(f32)
        average = (
            jnp.sum(own, axis=-1, keepdims=True) + jnp.sum(other, axis=-1, keepdims=True)
        ) / model
        own, other = own - average, other - average
        variance = (
            jnp.sum(own * own, axis=-1, keepdims=True)
            + jnp.sum(other * other, axis=-1, keepdims=True)
        ) / model
        inverse = lax.rsqrt(variance + NORM_EPSILON)
        stats = jnp.where(lane == 2 * s, average, stats)
        stats = jnp.where(lane == 2 * s + 1, inverse, stats)
        norm_own = (own * inverse * gain_ref[s : s + 1, own_span]).astype(bf16)
        if s == STREAMS - 1:
            ff_ref[...] = norm_own
        else:
            normed_ref[s, :, own_span] = norm_own
            norm_other = (other * inverse * gain_ref[s : s + 1, other_span]).astype(bf16)
            normed_ref[s, :, other_span] = norm_other
    stat_ref[...] = stats


def norm_streams(low, low_other, gains, which):
    tall, wide = low.shape
    width = wide // STREAMS
    rows = min(64, tall)
    row = lambda i, m: (i, 0)
    return pl.pallas_call(
        norm_kernel,
        grid_spec=pltpu.PrefetchScalarGridSpec(
            num_scalar_prefetch=1,
            grid=(tall // rows,),
            in_specs=[
                pl.BlockSpec((rows, wide), row),
                pl.BlockSpec((rows, wide), row),
                pl.BlockSpec(gains.shape, lambda i, m: (0, 0)),
            ],
            out_specs=[
                pl.BlockSpec((3, rows, 2 * width), lambda i, m: (0, i, 0)),
                pl.BlockSpec((rows, width), row),
                pl.BlockSpec((rows, 128), row),
            ],
        ),
        out_shape=[
            jax.ShapeDtypeStruct((3, tall, 2 * width), bf16),
            jax.ShapeDtypeStruct((tall, width), bf16),
            jax.ShapeDtypeStruct((tall, 128), f32),
        ],
        cost_estimate=spent(
            flops=20 * tall * wide, bytes_accessed=8 * tall * wide, transcendentals=0
        ),
        name="norm_streams",
    )(which, low, low_other, gains)


def turn(values, cosine, sine_up, sine_down, sign):
    up = pltpu.roll(values, HDIM - ROT // 2, 1)
    down = pltpu.roll(values, ROT // 2, 1)
    return values * cosine + sign * (up * sine_up + down * sine_down)


def project_kernel(
    x_ref, cot_ref, wq_ref, wk_ref, wv_ref, wo_ref, cos_ref, up_ref, down_ref, out_ref
):
    span = wq_ref.shape[-1]
    tables = cos_ref[...], up_ref[...], down_ref[...]
    for kind, w_ref in enumerate((wq_ref, wk_ref, wv_ref, wo_ref)):
        rows = cot_ref[...] if kind == 3 else x_ref[kind]
        product = dot_nn(rows, w_ref[...].reshape(-1, span))
        for begin in range(0, span, HDIM):
            head = product[:, begin : begin + HDIM]
            if kind < 2:
                head = turn(head, *tables, 1.0)
            out_ref[0, :, kind * span + begin : kind * span + begin + HDIM] = head.astype(bf16)


def project_heads(normed, cot, weights, tables, depth_count):
    _, rows, model = normed.shape
    groups, _, _, own_rows, heads_width = weights.shape
    span = heads_width // depth_count
    whole = lambda j: (0, 0)

    def matrix(kind):
        shape = (groups, depth_count, 1, own_rows, span)
        return pl.BlockSpec(shape, lambda j: (0, 0, kind, 0, j))

    return pl.pallas_call(
        project_kernel,
        grid=(depth_count,),
        in_specs=[
            pl.BlockSpec((3, rows, model), lambda j: (0, 0, 0)),
            pl.BlockSpec((rows, model), whole),
        ]
        + [matrix(kind) for kind in range(4)]
        + [pl.BlockSpec((rows, HDIM), whole)] * 3,
        out_specs=pl.BlockSpec((1, rows, 4 * span), lambda j: (j, 0, 0)),
        out_shape=jax.ShapeDtypeStruct((depth_count, rows, 4 * span), bf16),
        compiler_params=pltpu.CompilerParams(vmem_limit_bytes=40 << 20),
        cost_estimate=spent(
            flops=8 * rows * model * span * depth_count,
            bytes_accessed=8 * model * span * depth_count + 8 * rows * model,
            transcendentals=0,
        ),
        name="project_heads",
    )(normed, cot, *[weights] * 4, *tables)


def attend_kernel(
    block, q_ref, k_ref, v_ref, g_ref, doc_col_ref, doc_row_ref, cos_ref, up_ref, down_ref,
    out_ref, dk_sum, dv_sum,
):
    length = q_ref.shape[0]
    scale = HDIM**-0.5
    heads_each = out_ref.shape[1] // (4 * HDIM)

    def lanes(kind):
        return pl.ds(pl.multiple_of((kind * heads_each + pl.program_id(0)) * HDIM, HDIM), HDIM)

    for begin in range(0, length, block):
        end = begin + block
        rows = slice(begin, end)
        queries, grads = q_ref[rows, :], g_ref[rows, :]
        keys, values = k_ref[0:end, :], v_ref[0:end, :]
        scores = dot_nt(queries, keys) * scale
        place_q = begin + lax.broadcasted_iota(jnp.int32, scores.shape, 0)
        place_k = lax.broadcasted_iota(jnp.int32, scores.shape, 1)
        allowed = (doc_col_ref[rows, :] == doc_row_ref[:, 0:end]) & (place_q >= place_k)
        scores = jnp.where(allowed, scores, MASKED)
        highest = jnp.max(scores, axis=-1, keepdims=True)
        exponent = jnp.exp(scores - highest)
        totals = jnp.sum(exponent, axis=-1, keepdims=True)
        attention = exponent * (1.0 / totals)
        low = attention.astype(bf16)
        out_ref[rows, lanes(0)] = dot_nn(low, values).astype(bf16)
        grad_att = dot_nt(grads, values).astype(bf16).astype(f32)
        weighted = jnp.sum(attention * grad_att, axis=-1, keepdims=True)
        grad_scores = (attention * (grad_att - weighted)).astype(bf16)
        grad_q = dot_nn(grad_scores, keys) * scale
        out_ref[rows, lanes(1)] = turn(
            grad_q, cos_ref[rows, :], up_ref[rows, :], down_ref[rows, :], -1.0
        ).astype(bf16)
        part_k = dot_tn(grad_scores, queries)
        part_v = dot_tn(low, grads)
        if begin > 0:
            dk_sum[0:begin, :] += part_k[0:begin]
            dv_sum[0:begin, :] += part_v[0:begin]
        dk_sum[begin:end, :] = part_k[begin:end]
        dv_sum[begin:end, :] = part_v[begin:end]
    grad_k = dk_sum[...] * scale
    out_ref[:, lanes(2)] = turn(grad_k, cos_ref[...], up_ref[...], down_ref[...], -1.0).astype(bf16)
    out_ref[:, lanes(3)] = dv_sum[...].astype(bf16)


def attend(packed, documents, tables, heads_each):
    length = packed.shape[0]
    block = min(256, length)
    whole = lambda h: (0, 0)

    def kind(at):
        return pl.BlockSpec((length, HDIM), lambda h: (0, at * heads_each + h))

    return pl.pallas_call(
        functools.partial(attend_kernel, block),
        grid=(heads_each,),
        in_specs=[kind(0), kind(1), kind(2), kind(3)]
        + [pl.BlockSpec((length, 1), whole), pl.BlockSpec((1, length), whole)]
        + [pl.BlockSpec((length, HDIM), whole)] * 3,
        out_specs=pl.BlockSpec((length, 4 * heads_each * HDIM), whole),
        out_shape=jax.ShapeDtypeStruct((length, 4 * heads_each * HDIM), bf16),
        scratch_shapes=[pltpu.VMEM((length, HDIM), f32)] * 2,
        compiler_params=pltpu.CompilerParams(vmem_limit_bytes=48 << 20),
        cost_estimate=spent(
            flops=9 * heads_each * length * length * HDIM,
            bytes_accessed=16 * length * heads_each * HDIM + 12 * length * HDIM,
            transcendentals=heads_each * length * length,
        ),
        name="attend",
    )(packed, packed, packed, packed, documents[:, None], documents[None, :], *tables)


def gelu_parts(values):
    cdf = 0.5 * (1.0 + lax.erf(values * (0.5**0.5)))
    density = jnp.exp(-0.5 * values * values) * (1.0 / math.sqrt(2.0 * math.pi))
    return values * cdf, cdf + values * density


def ff_kernel(
    model_ref, x_ref, cot_ref, up_ref, down_ref,
    hidden_ref, grad_ref, out_own_ref, out_other_ref, back_own_ref, back_other_ref,
):
    part = up_ref.shape[-1]
    half = up_ref.shape[1] // 2

    def rows_of(ref, which):
        return ref[0, pl.ds(which * half, half)].reshape(-1, part)

    own, other = model_ref[0], 1 - model_ref[0]
    up_pre = dot_nn(x_ref[...], up_ref[...].reshape(-1, part))
    hidden, slope = gelu_parts(up_pre)
    hidden = hidden.astype(bf16)
    grad_up = (dot_nn(cot_ref[0], down_ref[...].reshape(-1, part)) * slope).astype(bf16)
    hidden_ref[...] = hidden
    grad_ref[...] = grad_up
    back_other_ref[...] = dot_nt(grad_up, rows_of(up_ref, other)).astype(bf16)
    back_own_ref[...] = dot_nt(grad_up, rows_of(up_ref, own))
    out_other_ref[...] = dot_nt(hidden, rows_of(down_ref, other)).astype(bf16)
    out_own_ref[...] = dot_nt(hidden, rows_of(down_ref, own))


def feed_forward(x, cot, micro_at, weights, which):
    tall, model = x.shape
    part = weights.shape[-1]
    width = model // 2
    rows = min(256, tall)
    row = lambda i, m: (i, 0)

    def resident(kind):
        return pl.BlockSpec(
            (1,) + weights.shape[1:],
            lambda i, m: (kind, 0, 0, 0, 0),
            pipeline_mode=pl.Buffered(1),
        )

    return pl.pallas_call(
        ff_kernel,
        grid_spec=pltpu.PrefetchScalarGridSpec(
            num_scalar_prefetch=1,
            grid=(tall // rows,),
            in_specs=[
                pl.BlockSpec((rows, model), row),
                pl.BlockSpec((1, rows, model), lambda i, m: (micro_at, i, 0)),
                resident(0),
                resident(1),
            ],
            out_specs=[pl.BlockSpec((rows, part), row)] * 2
            + [pl.BlockSpec((rows, width), row)] * 4,
        ),
        out_shape=[jax.ShapeDtypeStruct((tall, part), bf16)] * 2
        + [
            jax.ShapeDtypeStruct((tall, width), f32),
            jax.ShapeDtypeStruct((tall, width), bf16),
            jax.ShapeDtypeStruct((tall, width), f32),
            jax.ShapeDtypeStruct((tall, width), bf16),
        ],
        compiler_params=pltpu.CompilerParams(vmem_limit_bytes=48 << 20),
        cost_estimate=spent(
            flops=8 * tall * model * part,
            bytes_accessed=4 * model * part + 16 * tall * model,
            transcendentals=2 * tall * part,
        ),
        name="feed_forward",
    )(which, x, cot, weights, weights)


def back_kernel(half_ref, ans_ref, wo_ref, wq_ref, wk_ref, wv_ref, out_ref, *flat):
    count, _, wide = ans_ref.shape
    span = wide // 4
    for kind, w_ref in enumerate((wo_ref, wq_ref, wk_ref, wv_ref)):
        total = None
        for j in range(count):
            term = dot_nt(
                ans_ref[j, :, kind * span : (kind + 1) * span],
                w_ref[:, :, :, :, j * span : (j + 1) * span].reshape(-1, span),
            )
            total = term if total is None else total + term
        out_ref[kind] = total.astype(out_ref.dtype)
    if flat:

        @pl.when(pl.program_id(0) == 0)
        def _():
            for kind in range(4):
                for j in range(count):
                    flat[0][kind, :, j * span : (j + 1) * span] = ans_ref[
                        j, :, kind * span : (kind + 1) * span
                    ]


def back_project(answer, weights, half, dtype, flat):
    count, rows, wide = answer.shape
    groups, _, _, own_rows, heads_width = weights.shape
    part = count * own_rows
    steps = groups // 2
    width = part * steps

    def matrix(kind):
        shape = (1, count, 1, own_rows, heads_width)
        return pl.BlockSpec(shape, lambda i, m: (m[0] * steps + i, 0, kind, 0, 0))

    out_specs = [pl.BlockSpec((4, rows, part), lambda i, m: (0, 0, i))]
    out_shape = [jax.ShapeDtypeStruct((4, rows, width), dtype)]
    if flat:
        out_specs.append(pl.BlockSpec((4, rows, heads_width), lambda i, m: (0, 0, 0)))
        out_shape.append(jax.ShapeDtypeStruct((4, rows, heads_width), bf16))
    return pl.pallas_call(
        back_kernel,
        grid_spec=pltpu.PrefetchScalarGridSpec(
            num_scalar_prefetch=1,
            grid=(steps,),
            in_specs=[pl.BlockSpec((count, rows, wide), lambda i, m: (0, 0, 0))]
            + [matrix(kind) for kind in (3, 0, 1, 2)],
            out_specs=out_specs,
        ),
        out_shape=out_shape,
        compiler_params=pltpu.CompilerParams(vmem_limit_bytes=40 << 20),
        cost_estimate=spent(
            flops=8 * rows * heads_width * width,
            bytes_accessed=8 * heads_width * width + 20 * rows * width,
            transcendentals=0,
        ),
        name="back_project",
    )(half, answer, *[weights] * 4)


def slope_kernel(
    model_ref, own_ref, got_ref, ff_ref, low_ref, stat_ref, gain_ref, scaled_ref, sum_ref, gain_out_ref
):
    rows, width = ff_ref.shape
    own_span, _ = own_spans(model_ref, width)
    lane = lax.broadcasted_iota(jnp.int32, (rows, 128), 1)
    packed = jnp.zeros((rows, 128), f32)
    totals = []
    for s in range(STREAMS):
        lanes = slice(s * width, (s + 1) * width)
        if s < 3:
            grad = own_ref[s + 1] + got_ref[s + 1].astype(f32)
        else:
            grad = ff_ref[...]
        average, inverse = stat_ref[:, 2 * s : 2 * s + 1], stat_ref[:, 2 * s + 1 : 2 * s + 2]
        hat = (low_ref[:, lanes].astype(f32) - average) * inverse
        totals.append(jnp.sum(grad * hat, axis=0, keepdims=True))
        scaled = grad * gain_ref[s : s + 1, own_span]
        scaled_ref[:, lanes] = scaled
        packed = jnp.where(lane == 2 * s, jnp.sum(scaled, axis=-1, keepdims=True), packed)
        packed = jnp.where(
            lane == 2 * s + 1, jnp.sum(scaled * hat, axis=-1, keepdims=True), packed
        )
    sum_ref[...] = packed
    totals = jnp.concatenate(totals, axis=0)

    @pl.when(pl.program_id(0) == 0)
    def _():
        gain_out_ref[...] = totals

    @pl.when(pl.program_id(0) > 0)
    def _():
        gain_out_ref[...] += totals


def norm_slopes(own, got, ff_grad, low, stats, gains, which):
    tall, wide = low.shape
    width = wide // STREAMS
    rows = min(64, tall)
    row = lambda i, m: (i, 0)
    cube = pl.BlockSpec((4, rows, width), lambda i, m: (0, i, 0))
    return pl.pallas_call(
        slope_kernel,
        grid_spec=pltpu.PrefetchScalarGridSpec(
            num_scalar_prefetch=1,
            grid=(tall // rows,),
            in_specs=[
                cube,
                cube,
                pl.BlockSpec((rows, width), row),
                pl.BlockSpec((rows, wide), row),
                pl.BlockSpec((rows, 128), row),
                pl.BlockSpec(gains.shape, lambda i, m: (0, 0)),
            ],
            out_specs=[
                pl.BlockSpec((rows, wide), row),
                pl.BlockSpec((rows, 128), row),
                pl.BlockSpec((STREAMS, width), lambda i, m: (0, 0)),
            ],
        ),
        out_shape=[
            jax.ShapeDtypeStruct((tall, wide), f32),
            jax.ShapeDtypeStruct((tall, 128), f32),
            jax.ShapeDtypeStruct((STREAMS, width), f32),
        ],
        cost_estimate=spent(
            flops=12 * tall * wide, bytes_accessed=12 * tall * wide, transcendentals=0
        ),
        name="norm_slopes",
    )(which, own, got, ff_grad, low, stats, gains)


def grads_kernel(
    scaled_ref, mine_ref, theirs_ref, low_ref, stat_ref, cot_ref, cur_ref, last_ref,
    grad_ref, mix_ref, dot_ref,
):
    rows, width = cot_ref.shape
    lane = lax.broadcasted_iota(jnp.int32, (rows, 128), 1)
    means = (mine_ref[...] + theirs_ref[...]) / (2 * width)
    current = cur_ref[...].astype(f32)
    packed = jnp.zeros((rows, 128), f32)
    mixed = None
    for s in range(STREAMS):
        lanes = slice(s * width, (s + 1) * width)
        average, inverse = stat_ref[:, 2 * s : 2 * s + 1], stat_ref[:, 2 * s + 1 : 2 * s + 2]
        hat = (low_ref[:, lanes].astype(f32) - average) * inverse
        grad = inverse * (
            scaled_ref[:, lanes]
            - means[:, 2 * s : 2 * s + 1]
            - hat * means[:, 2 * s + 1 : 2 * s + 2]
        )
        if s == STREAMS - 1:
            grad = grad + cot_ref[...].astype(f32)
        grad = grad.astype(bf16)
        grad_ref[:, lanes] = grad
        grad = grad.astype(f32)
        term = last_ref[:, s : s + 1] * grad
        mixed = term if mixed is None else mixed + term
        packed = jnp.where(lane == s, jnp.sum(grad * current, axis=-1, keepdims=True), packed)
    mix_ref[...] = mixed
    dot_ref[...] = packed


def stream_grads(scaled, mine, theirs, low, stats, cot, current_half, last):
    tall, wide = low.shape
    width = wide // STREAMS
    rows = min(64, tall)
    row = lambda i: (i, 0)
    return pl.pallas_call(
        grads_kernel,
        grid=(tall // rows,),
        in_specs=[
            pl.BlockSpec((rows, wide), row),
            pl.BlockSpec((rows, 128), row),
            pl.BlockSpec((rows, 128), row),
            pl.BlockSpec((rows, wide), row),
            pl.BlockSpec((rows, 128), row),
            pl.BlockSpec((rows, width), row),
            pl.BlockSpec((rows, width), row),
            pl.BlockSpec((rows, 128), row),
        ],
        out_specs=[
            pl.BlockSpec((rows, wide), row),
            pl.BlockSpec((rows, width), row),
            pl.BlockSpec((rows, 128), row),
        ],
        out_shape=[
            jax.ShapeDtypeStruct((tall, wide), bf16),
            jax.ShapeDtypeStruct((tall, width), f32),
            jax.ShapeDtypeStruct((tall, 128), f32),
        ],
        cost_estimate=spent(
            flops=12 * tall * wide, bytes_accessed=10 * tall * wide, transcendentals=0
        ),
        name="stream_grads",
    )(scaled, mine, theirs, low, stats, cot, current_half, last)


def turning_tables(places):
    half = ROT // 2
    inverse = jnp.exp(jnp.arange(half, dtype=f32) * (-2.0 * math.log(10000.0) / ROT))
    angles = places.astype(f32)[:, None] * inverse[None, :]
    cosine, sine = jnp.cos(angles), jnp.sin(angles)
    rows = places.shape[0]
    rest = jnp.zeros((rows, HDIM - ROT), f32)
    blank = jnp.zeros((rows, half), f32)
    return (
        jnp.concatenate([cosine, cosine, rest + 1.0], axis=1),
        jnp.concatenate([-sine, blank, rest], axis=1),
        jnp.concatenate([blank, sine, rest], axis=1),
    )


def local(
    history,
    slot_layer,
    current,
    positions,
    doc_ids,
    cotangent,
    norm_gains,
    generator_in,
    generator_out,
    query_weight,
    key_weight,
    value_weight,
    out_weight,
    up_weight,
    down_weight,
):
    dp_count = lax.axis_size("dp")
    depth_count = lax.axis_size("depth")
    dp_at = lax.axis_index("dp")
    model_at = lax.axis_index("mp")
    dp_bits = list(range(bit_count(dp_count)))
    slots, tokens_held, width = history.shape
    model = current.shape[1]
    rows_mb = current.shape[0] // MB
    length = depth_count * rows_mb
    heads_width = query_weight.shape[1]
    heads_each = heads_width // HDIM // depth_count
    own_rows = query_weight.shape[0]
    ff_width = up_weight.shape[1]
    ff_part = ff_width // dp_count
    both = ("dp", "depth")

    def half_of(values, axis, which):
        return lax.dynamic_slice_in_dim(values, which * width, width, axis)

    small_cols = jnp.concatenate(
        [generator_in, norm_gains.T, jnp.zeros((own_rows, 128 - GEN - 5), bf16)], axis=1
    )
    small_all = gather_small(small_cols, both).reshape(model, 128)
    gen_first = small_all[:, :GEN]
    gain_float = small_all[:, GEN : GEN + 5].astype(f32).T
    second_rows = generator_out.shape[0]
    second_pad = -second_rows % 128
    second_all = gather_small(jnp.pad(generator_out, (0, second_pad))[None], both)
    gen_second = second_all.reshape(-1, second_rows + second_pad)[:, :second_rows]
    second_low = gen_second.reshape(GEN, STREAMS * MIX)

    stacked = jnp.concatenate([query_weight, key_weight, value_weight, out_weight.T], axis=0)
    over_depth = lax.all_gather(stacked, "depth", axis=0, tiled=True)
    current_f = current.astype(f32)
    current_half = half_of(current, 1, model_at)
    mean_square = jnp.mean(current_f * current_f, axis=-1, keepdims=True)
    inverse_rms = lax.rsqrt(mean_square + RMS_EPSILON)
    unit = current_f * inverse_rms
    gen_normed = (unit * gain_float[4]).astype(bf16)
    gen_pre = dot_nn(gen_normed, gen_first)
    gen_hidden = gelu_exact(gen_pre).astype(bf16)
    column = jnp.arange(STREAMS * MIX)
    last_col = (column % MIX == MIX - 1).astype(f32)
    mixing = (dot_nn(gen_hidden, second_low) + last_col).astype(bf16)
    pick_last = (column[:, None] == (jnp.arange(128) * MIX + MIX - 1)[None, :]).astype(bf16)
    last = dot_nn(mixing, pick_last)

    layer_of = jnp.tile(slot_layer, STREAMS)
    stream_of = jnp.repeat(jnp.arange(STREAMS), slots)
    from_col = jnp.where(layer_of < MIX, stream_of * MIX + layer_of, -1)
    pick = (column[:, None] == from_col[None, :]).astype(f32)
    mix_all = gather_small(mixing, ("depth",)).reshape(depth_count * MB * rows_mb, STREAMS * MIX)
    slot_mix = dot_nn(mix_all, pick.astype(bf16))

    def over_depth_swap(values):
        return lax.all_to_all(values, "depth", 0, 0, tiled=True)

    def mix_part(micro_at, slot_mix):
        partial = mix_streams(slot_mix, history, micro_at, depth_count, rows_mb)
        return partial.reshape(1, depth_count, rows_mb, STREAMS * width)

    partners = jnp.stack([dp_at ^ m for m in range(dp_count)]).astype(jnp.int32)
    ff_local = ff_split(up_weight, down_weight, partners)
    ff_local, slot_mix = fence(ff_local, slot_mix)
    ff_rows = place_block(None, ff_local[0], partners[0], dp_count)
    for m in range(1, dp_count):
        arrived = swap_mask(ff_local[m], "dp", m)
        ff_rows = place_block(ff_rows, arrived, partners[m], dp_count)
    ff_rows = ff_rows.reshape(2 * dp_count, own_rows, ff_part)

    partial = mix_part(0, slot_mix)
    over_depth, partial, slot_mix, ff_rows, cotangent, positions = fence(
        over_depth, partial, slot_mix, ff_rows, cotangent, positions
    )

    weights_line = LineGather(ff_rows)
    weights_line.step()
    flat_rows = depth_count * 4 * own_rows
    pieces = [over_depth.reshape(flat_rows, heads_width)]
    pieces.append(core_hop(pieces[0], 0))
    weights = place_block(None, pieces[0][None], place_index(0), dp_count)
    partial_next = mix_part(1, slot_mix)
    pieces, partial, partial_next, weights, cotangent = weights_line.hold(
        pieces, partial, partial_next, weights, cotangent
    )
    hops_left = [(p, at) for at in range(1, len(dp_bits)) for p in range(1 << at)]
    placed = 1
    cot_other = cot_mine = None
    sums, sums_next = LineScatter(partial), LineScatter(partial_next)
    for hop in range(1, depth_count):
        sums.step()
        weights_line.step()
        last_hop = hop == depth_count - 1
        for place in range(placed, len(pieces)):
            weights = place_block(weights, pieces[place][None], place_index(place), dp_count)
        placed = len(pieces)
        while hops_left:
            place, at = hops_left.pop(0)
            pieces.append(core_hop(pieces[place], at))
            if len(hops_left) <= depth_count - 2 - hop:
                break
        if last_hop:
            cot_other = other_core(cotangent)
            cot_mine = group_gather(cotangent)
            sums_next.step()
        (state,) = weights_line.hold((sums.up, sums.down, pieces, weights, cotangent))
        sums.up, sums.down, pieces, weights, cotangent = state
    while sums_next.at < depth_count - 3:
        sums_next.hold()
        sums_next.step()
    for place in range(placed, len(pieces)):
        weights = place_block(weights, pieces[place][None], place_index(place), dp_count)
    weights = weights.reshape(dp_count, depth_count, 4, own_rows, heads_width)
    ff_weights = weights_line.placed().reshape(2, dp_count, depth_count, own_rows, ff_part)

    cot_full = join_halves(cotangent, cot_other, model_at)
    cot_mine = jnp.swapaxes(cot_mine.reshape(dp_count, MB, rows_mb, width), 0, 1)
    cot_mine = cot_mine.reshape(MB * dp_count * rows_mb, width)
    cot_group = join_halves(cot_mine, other_core(cot_mine), model_at)
    cot_group = cot_group.reshape(MB, dp_count * rows_mb, model)

    places_all = gather_small(positions, ("depth",))
    document_view = doc_ids.reshape(depth_count, MB, rows_mb)
    own_tables = turning_tables(positions)
    which = model_at.astype(jnp.int32)[None]
    depth_at = lax.axis_index("depth").astype(jnp.int32)[None]
    gains = gain_float

    def enter(micro_at, sums):
        span = slice(micro_at * rows_mb, (micro_at + 1) * rows_mb)
        low, resid = total_streams(sums, current_half[span], last[span], depth_at)
        normed, ff_normed, stats = norm_streams(low, other_core(low), gains, which)
        packed = project_heads(
            normed,
            cot_full[span],
            weights,
            [t[span] for t in own_tables],
            depth_count,
        )
        return dict(
            low=low, resid=resid, normed=normed, ff_normed=ff_normed, stats=stats, packed=packed
        )

    def attention(micro_at, by_head):
        span = slice(micro_at * rows_mb, (micro_at + 1) * rows_mb)
        documents = document_view[:, micro_at].reshape(length)
        seq_places = places_all[:, span].reshape(length)
        by_head = by_head.reshape(length, 4 * heads_each * HDIM)
        answer = attend(by_head, documents, turning_tables(seq_places), heads_each)
        return answer.reshape(depth_count, rows_mb, 4 * heads_each * HDIM)

    def group_rows(ff_normed):
        mine = group_gather(ff_normed).reshape(dp_count * rows_mb, width)
        return join_halves(mine, other_core(mine), model_at)

    def hidden_units(micro_at, group_normed):
        hidden, grad_up, out_own, out_other, back_own, back_other = feed_forward(
            group_normed, cot_group, micro_at, ff_weights, which
        )
        return (
            dict(group_normed=group_normed, hidden=hidden, grad_up=grad_up),
            ((back_own, other_core(back_other)), (out_own, other_core(out_other))),
        )

    def reduce_group(own, other):
        total = own + other.astype(f32)
        return group_scatter(total.reshape(dp_count, rows_mb, width))

    def back(kept, answer, ff_parts):
        (theirs,) = back_project(answer, weights, 1 - which, bf16, False)
        got = other_core(theirs)
        own, kept["flat"] = back_project(answer, weights, which, f32, True)
        grad_norm_ff = reduce_group(*ff_parts[0])
        ff_out = reduce_group(*ff_parts[1])
        kept["layer_rows"] = (kept["resid"] + own[0] + got[0].astype(f32) + ff_out).astype(bf16)
        return own, got, grad_norm_ff

    def leave(micro_at, kept, own, got, grad_norm_ff):
        span = slice(micro_at * rows_mb, (micro_at + 1) * rows_mb)
        low, stats = kept["low"], kept["stats"]
        scaled, sums, gain_part = norm_slopes(own, got, grad_norm_ff, low, stats, gains, which)
        grad_low, current_mix, last_dot = stream_grads(
            scaled, sums, other_core(sums), low, stats, cotangent[span], current_half[span], last[span]
        )
        kept.update(gain=gain_part, current_mix=current_mix, last_dot=last_dot)
        return grad_low

    sums_next.step()
    first = enter(0, sums)
    packed, ff_normed = sums_next.hold(first["packed"], first["ff_normed"])
    sums_next.step()
    by_head = over_depth_swap(packed)
    group_normed = group_rows(ff_normed)
    by_head, group_normed = sums_next.hold(by_head, group_normed)
    answer = attention(0, by_head)
    answer, group_normed = sums_next.hold(answer, group_normed)

    answer = over_depth_swap(answer)
    second = enter(1, sums_next)
    kept, ff_parts = hidden_units(0, group_normed)
    first.update(kept)
    answer, packed, ff_normed, ff_parts = fence(
        answer, second["packed"], second["ff_normed"], ff_parts
    )
    by_head = over_depth_swap(packed)
    group_normed = group_rows(ff_normed)
    ways = back(first, answer, ff_parts)
    by_head, group_normed, ways = fence(by_head, group_normed, ways)
    answer = attention(1, by_head)
    answer, group_normed, ways = fence(answer, group_normed, ways)

    answer = over_depth_swap(answer)
    grad_low = leave(0, first, *ways)
    kept, ff_parts = hidden_units(1, group_normed)
    second.update(kept)
    answer, grad_low, ff_parts = fence(answer, grad_low, ff_parts)
    saved = [first, second]

    def each(name):
        return [s[name] for s in saved]

    def rows_of(name):
        return jnp.concatenate(each(name), axis=0)

    grad_line = LineGather(grad_low[None])
    for hop in range(1, depth_count):
        grad_line.step()
        if hop == 1:
            ways = back(second, answer, ff_parts)
            (ways,) = grad_line.hold(ways)
        elif hop == 2:
            grad_low = leave(1, second, *ways)
            ff_products = hidden_grads(
                each("group_normed"), cot_group, each("grad_up"), each("hidden"), dp_count, depth_count
            )
            grad_low, ff_products = grad_line.hold(grad_low, ff_products)
        elif hop == 3:
            place_list = jnp.stack([place_index(p) for p in range(dp_count)]).astype(jnp.int32)
            pieces = [
                attention_grads(
                    each("normed"),
                    cot_full,
                    each("flat"),
                    place_list[p : p + 1],
                    depth_count,
                    dp_count,
                    bf16 if p >= dp_count // 2 else f32,
                )
                for p in range(dp_count)
            ]
            grad_low, ff_products, pieces = grad_line.hold(grad_low, ff_products, pieces)
        else:
            grad_low, ff_products, pieces = grad_line.hold(grad_low, ff_products, pieces)

    last_line = LineGather(grad_low[None])
    last_line.step()
    ff_sums = LineScatter(ff_products)
    hops_left = [
        (p, at) for at in reversed(range(len(dp_bits))) for p in range(1 << at, 2 << at)
    ]

    def sums_hop():
        place, at = hops_left.pop(0)
        arrived = core_hop(pieces[place].astype(bf16), at).astype(f32)
        pieces[place - (1 << at)] = pieces[place - (1 << at)] + arrived

    sums_hop()
    (pieces,) = last_line.hold(pieces)
    grad_first = grad_line.placed().reshape(length, -1)
    history_grad, slot_part = unmix_streams(
        slot_mix, history, grad_first, 0, depth_count, rows_mb, None
    )
    slot_parts = [slot_part.reshape(depth_count, 1, rows_mb, 128)]
    for hop in range(1, depth_count):
        last_line.step()
        ff_sums.step()
        if hops_left:
            sums_hop()
        if hop < depth_count - 1:
            (state,) = last_line.hold((ff_sums.up, ff_sums.down, pieces))
            ff_sums.up, ff_sums.down, pieces = state
    while hops_left:
        sums_hop()
    last_grads = last_line.placed().reshape(length, -1)
    totals = pieces[0].astype(bf16)
    history_grad, slot_part = unmix_streams(
        slot_mix, history, last_grads, 1, depth_count, rows_mb, history_grad
    )
    slot_parts.append(slot_part.reshape(depth_count, 1, rows_mb, 128))
    arrived = over_depth_swap(totals)

    slot_grads = jnp.concatenate(slot_parts, axis=1).reshape(-1, 128)[:, : STREAMS * slots]
    mix_grads = dot_exact(slot_grads, pick.T).reshape(depth_count, MB * rows_mb, STREAMS * MIX)
    grad_mixing = scatter_small(mix_grads, ("depth",))
    (grad_mixing,) = ff_sums.hold(grad_mixing)
    ff_grads = end_sums(ff_sums, bf16).reshape(2, dp_count, own_rows, ff_part)
    ff_pieces = [
        lax.dynamic_index_in_dim(ff_grads, partners[m], 1, keepdims=False) for m in range(dp_count)
    ]
    ff_pieces = [ff_pieces[0]] + [swap_mask(ff_pieces[m], "dp", m) for m in range(1, dp_count)]
    up_grad, down_grad = ff_join(jnp.stack(ff_pieces), partners)
    last_dots = rows_of("last_dot")
    grad_mixing = grad_mixing + dot_exact(last_dots, pick_last.astype(f32).T)
    grad_mixing = grad_mixing + other_core(grad_mixing)

    second_float = second_low.astype(f32)
    grad_second = dot_exact(gen_hidden.astype(f32).T, grad_mixing)
    grad_pre = dot_exact(grad_mixing, second_float.T) * gelu_slope(gen_pre)
    grad_first = dot_exact(gen_normed.astype(f32).T, grad_pre)
    grad_gen_normed = dot_exact(grad_pre, gen_first.astype(f32).T)
    gain_gen = jnp.sum(grad_gen_normed * unit, axis=0)
    gain_gen, arrived = fence(gain_gen, arrived)
    scattered = jnp.sum(arrived.astype(f32), axis=0)
    grad_unit = grad_gen_normed * gain_float[4]
    shared = jnp.mean(grad_unit * unit, axis=-1, keepdims=True)
    current_gen = half_of(inverse_rms * (grad_unit - unit * shared), 1, model_at)
    current_grad = rows_of("current_mix") + current_gen

    gain_own = sum(s["gain"] for s in saved)
    gain_other = other_core(gain_own)
    gain_all = jnp.where(
        model_at == 0,
        jnp.concatenate([gain_own, gain_other], axis=1),
        jnp.concatenate([gain_other, gain_own], axis=1),
    )
    gain_all = jnp.concatenate([gain_all, gain_gen[None]], axis=0)
    small_grads = jnp.concatenate(
        [grad_first, gain_all.T, jnp.zeros((model, 128 - GEN - 5), f32)], axis=1
    )
    small_grads = scatter_small(small_grads.reshape(-1, own_rows, 128), both)
    second_grads = jnp.pad(grad_second.reshape(-1, second_rows), ((0, 0), (0, second_pad)))
    second_grads = scatter_small(second_grads[:, None], both)

    return (
        rows_of("layer_rows"),
        history_grad,
        current_grad,
        small_grads[:, GEN : GEN + 5].T,
        small_grads[:, :GEN],
        second_grads[0, :second_rows],
        scattered[0],
        scattered[1],
        scattered[2],
        scattered[3].T,
        up_grad,
        down_grad,
    )


def solution(mesh):
    return jax.shard_map(
        local,
        mesh=mesh,
        in_specs=(
            P("depth", "dp", "mp"),
            P("depth"),
            P(("dp", "depth"), None),
            P(("dp", "depth")),
            P("dp"),
            P(("dp", "depth"), "mp"),
            P(None, ("dp", "depth")),
            P(("dp", "depth"), None),
            P(("dp", "depth")),
            P(("dp", "depth"), "mp"),
            P(("dp", "depth"), "mp"),
            P(("dp", "depth"), "mp"),
            P("mp", ("dp", "depth")),
            P(("dp", "depth"), "mp"),
            P("mp", ("dp", "depth")),
        ),
        out_specs=(
            P(("dp", "depth"), "mp"),
            P("depth", "dp", "mp"),
            P(("dp", "depth"), "mp"),
            P(None, ("dp", "depth")),
            P(("dp", "depth"), None),
            P(("dp", "depth")),
            P(("dp", "depth"), "mp"),
            P(("dp", "depth"), "mp"),
            P(("dp", "depth"), "mp"),
            P("mp", ("dp", "depth")),
            P(("dp", "depth"), "mp"),
            P("mp", ("dp", "depth")),
        ),
        check_vma=False,
    )
```

```python
import functools
import math

import jax
import jax.numpy as jnp
from jax import lax
from jax.experimental import pallas as pl
from jax.experimental.pallas import tpu as pltpu
from jax.sharding import PartitionSpec as P

HDIM = 128
ROT = 32
GEN = 72
MB = 2
MIX = 18
STREAMS = 4
COST = 1

PRECISE = lax.Precision.HIGHEST
NORM_EPSILON = 1e-05
RMS_EPSILON = 1e-06
MASKED = -1e30

bf16 = jnp.bfloat16
f32 = jnp.float32


def dot_nn(a, b):
    return lax.dot_general(a, b, (((1,), (0,)), ((), ())), preferred_element_type=f32)


def dot_nt(a, b):
    return lax.dot_general(a, b, (((1,), (1,)), ((), ())), preferred_element_type=f32)


def dot_tn(a, b):
    return lax.dot_general(a, b, (((0,), (0,)), ((), ())), preferred_element_type=f32)


def dot_exact(a, b):
    return jnp.dot(a, b, precision=PRECISE, preferred_element_type=f32)


def gelu_exact(values):
    return jax.nn.gelu(values, approximate=False)


def gelu_slope(values):
    result, pullback = jax.vjp(gelu_exact, values)
    return pullback(jnp.ones_like(result))[0]


def bit_count(size):
    count = size.bit_length() - 1
    assert 1 << count == size
    return count


def swap_mask(values, axis, mask):
    size = lax.axis_size(axis)
    return lax.ppermute(values, axis, [(i, i ^ mask) for i in range(size)])


def gather_masked(values, axis, order):
    pieces = {0: values}
    for bit in order:
        arrived = {m | (1 << bit): swap_mask(v, axis, 1 << bit) for m, v in pieces.items()}
        pieces.update(arrived)
    return [pieces[m] for m in range(len(pieces))]


def scatter_masked(pieces, axis, order, link=bf16):
    pieces = dict(enumerate(pieces))
    for bit in order:
        flag = 1 << bit
        for m in [m for m in pieces if m & flag]:
            arrived = swap_mask(pieces.pop(m).astype(link), axis, flag)
            pieces[m ^ flag] = pieces[m ^ flag].astype(f32) + arrived.astype(f32)
    return pieces[0]


def core_orders():
    bits = list(range(bit_count(lax.axis_size("dp"))))
    return bits, bits[1:] + bits[:1]


def place_mask(place):
    masks = []
    for order in core_orders():
        masks.append(sum(1 << bit for at, bit in enumerate(order) if (place >> at) & 1))
    return jnp.where(lax.axis_index("mp") % 2 == 0, masks[0], masks[1])


def place_index(place):
    return lax.axis_index("dp") ^ place_mask(place)


def core_hop(values, at):
    orders, cores = core_orders(), lax.axis_size("mp")
    pairs = []
    for i in range(lax.axis_size("dp")):
        for core in range(cores):
            partner = i ^ (1 << orders[core % 2][at])
            pairs.append((i * cores + core, partner * cores + core))
    return lax.ppermute(values, ("dp", "mp"), pairs)


def group_hop(pieces, at):
    return jnp.concatenate([pieces, core_hop(pieces, at)], axis=0)


def group_gather(values):
    pieces = values[None]
    for at in range(bit_count(lax.axis_size("dp"))):
        pieces = group_hop(pieces, at)
    return group_rows_placed(pieces)


def group_rows_placed(pieces):
    buffer = None
    for place in range(pieces.shape[0]):
        buffer = place_block(
            buffer, pieces[place][None], place_index(place), pieces.shape[0]
        )
    return buffer[0]


def group_scatter(blocks):
    count = blocks.shape[0]
    pieces = [
        lax.dynamic_index_in_dim(blocks, place_index(p), 0, keepdims=False) for p in range(count)
    ]
    for at in reversed(range(bit_count(count))):
        half = 1 << at
        arrived = core_hop(jnp.stack(pieces[half : 2 * half]).astype(bf16), at).astype(f32)
        pieces = [pieces[p] + arrived[p] for p in range(half)]
    return pieces[0]


def reorder_masked(stacked, axis):
    count = bit_count(stacked.shape[0])
    here = lax.axis_index(axis)
    shape = stacked.shape
    values = stacked.reshape((2,) * count + shape[1:])
    for bit in range(count):
        turned = jnp.flip(values, count - 1 - bit)
        values = jnp.where(((here >> bit) & 1) == 1, turned, values)
    return values.reshape(shape)


def gather_small(values, axes):
    shape = values.shape
    values = values[None]
    for axis in reversed(axes):
        order = range(bit_count(lax.axis_size(axis)))
        stacked = jnp.stack(gather_masked(values, axis, order))
        values = reorder_masked(stacked, axis)
        values = values.reshape((-1,) + shape)
    return values


def scatter_small(values, axes):
    for axis in axes:
        size = lax.axis_size(axis)
        values = values.reshape((size, values.shape[0] // size) + values.shape[1:])
        turned = reorder_masked(values, axis)
        order = reversed(range(bit_count(size)))
        values = scatter_masked([turned[m] for m in range(size)], axis, order, f32)
    return values[0]


def line_size():
    return lax.axis_size("depth"), lax.axis_index("depth")


def fence(*values):
    return lax.optimization_barrier(values)


class LineGather:

    def __init__(self, values):
        self.up, self.down = [values], [values]

    def step(self):
        size, _ = line_size()
        at = len(self.up)
        if at < size:
            up_pairs = [(i, i + 1) for i in range(at - 1, size - 1)]
            down_pairs = [(i, i - 1) for i in range(1, size - at + 1)]
            self.up.append(lax.ppermute(self.up[-1], "depth", up_pairs))
            self.down.append(lax.ppermute(self.down[-1], "depth", down_pairs))

    def hold(self, *others):
        kept = fence((self.up[1:], self.down[1:]), *others)
        (up, down), rest = kept[0], kept[1:]
        self.up, self.down = self.up[:1] + list(up), self.down[:1] + list(down)
        return rest

    def placed(self):
        size, here = line_size()
        buffer = place_block(None, self.up[0], here, size)
        for at in range(1, size):
            buffer = place_block(
                buffer,
                self.up[at],
                lax.rem(here - at + size, size),
                size,
                self.down[size - at],
                here >= at,
            )
        return buffer


class LineScatter:

    def __init__(self, terms):
        self.terms, self.at = terms, 0
        self.up = self.down = None

    def step(self):
        size, here = line_size()
        self.at += 1
        if self.at >= size:
            return
        goes_up, goes_down = hop_sums(
            self.terms,
            jnp.minimum(size - self.at + here, size - 1),
            jnp.maximum(here - size + self.at, 0),
            self.up,
            self.down,
        )
        up_pairs = [(i, i + 1) for i in range(min(self.at, size - 1))]
        down_pairs = [(size - 1 - i, size - 2 - i) for i in range(min(self.at, size - 1))]
        self.up = lax.ppermute(goes_up, "depth", up_pairs)
        self.down = lax.ppermute(goes_down, "depth", down_pairs)

    def hold(self, *others):
        (self.up, self.down), *rest = fence((self.up, self.down), *others)
        return rest


def other_core(values):
    return swap_mask(values, "mp", 1)


def join_kernel(model_ref, own_ref, other_ref, out_ref):
    width = own_ref.shape[1]
    own_at = pl.multiple_of(model_ref[0] * width, width)
    other_at = pl.multiple_of((1 - model_ref[0]) * width, width)
    out_ref[:, pl.ds(own_at, width)] = own_ref[...]
    out_ref[:, pl.ds(other_at, width)] = other_ref[...]


def join_halves(own, other, model_at):
    tall, width = own.shape
    rows = min(256, tall)
    return pl.pallas_call(
        join_kernel,
        grid_spec=pltpu.PrefetchScalarGridSpec(
            num_scalar_prefetch=1,
            grid=(tall // rows,),
            in_specs=[pl.BlockSpec((rows, width), lambda i, m: (i, 0))] * 2,
            out_specs=pl.BlockSpec((rows, 2 * width), lambda i, m: (i, 0)),
        ),
        out_shape=jax.ShapeDtypeStruct((tall, 2 * width), own.dtype),
        cost_estimate=spent(
            flops=0, bytes_accessed=8 * tall * width, transcendentals=0
        ),
        name="join_halves",
    )(model_at.astype(jnp.int32)[None], own, other)


def spent(flops, bytes_accessed, transcendentals):
    return pl.CostEstimate(
        flops=flops // COST, bytes_accessed=bytes_accessed // COST, transcendentals=transcendentals // COST
    )


def chunk_of(tall, wide):
    rows = tall
    while rows * wide > 1 << 19 and rows % 32 == 0:
        rows //= 2
    return rows


def place_kernel(at_ref, *refs):
    if len(refs) < 4:
        refs[-1][0, 0] = refs[0][0]
        return

    @pl.when(at_ref[1] == 1)
    def _():
        refs[-1][0, 0] = refs[0][0]

    @pl.when(at_ref[1] == 0)
    def _():
        refs[-1][0, 0] = refs[1][0]


def place_block(buffer, block, index, count, instead=None, first=None):
    lead, tall, wide = block.shape
    rows = chunk_of(tall, wide)
    spec = pl.BlockSpec((1, rows, wide), lambda l, i, m: (l, i, 0))
    blocks = [block] if instead is None else [block, instead]
    where = [index, 1 if first is None else first]
    where = jnp.stack([jnp.asarray(v).astype(jnp.int32) for v in where])
    in_specs, operands, aliases = [spec] * len(blocks), list(blocks), {}
    if buffer is not None or instead is not None:
        in_specs.append(pl.BlockSpec(memory_space=pl.ANY))
        operands.append(block if buffer is None else buffer)
        aliases = {} if buffer is None else {len(operands): 0}
    return pl.pallas_call(
        place_kernel,
        grid_spec=pltpu.PrefetchScalarGridSpec(
            num_scalar_prefetch=1,
            grid=(lead, tall // rows),
            in_specs=in_specs,
            out_specs=pl.BlockSpec((1, 1, rows, wide), lambda l, i, m: (l, m[0], i, 0)),
        ),
        out_shape=jax.ShapeDtypeStruct((lead, count, tall, wide), block.dtype),
        input_output_aliases=aliases,
        cost_estimate=spent(
            flops=0, bytes_accessed=4 * lead * tall * wide, transcendentals=0
        ),
        name="place_block",
    )(where, *operands)


def hop_kernel(at_ref, *refs):
    ins, outs = refs[:-2], refs[-2:]
    for way in range(2):
        term = ins[way][0, 0].astype(f32)
        if len(ins) > 2:
            term = term + ins[2 + way][0].astype(f32)
        outs[way][0] = term.astype(bf16)


def hop_sums(terms, up_at, down_at, up, down):
    lead, _, tall, wide = terms.shape
    rows = chunk_of(tall, wide)
    block = pl.BlockSpec((1, rows, wide), lambda l, i, m: (l, i, 0))
    in_specs = [
        pl.BlockSpec((1, 1, rows, wide), lambda l, i, m: (l, m[0], i, 0)),
        pl.BlockSpec((1, 1, rows, wide), lambda l, i, m: (l, m[1], i, 0)),
    ]
    operands = [terms, terms]
    if up is not None:
        in_specs += [block, block]
        operands += [up, down]
    return pl.pallas_call(
        hop_kernel,
        grid_spec=pltpu.PrefetchScalarGridSpec(
            num_scalar_prefetch=1,
            grid=(lead, tall // rows),
            in_specs=in_specs,
            out_specs=[block, block],
        ),
        out_shape=[jax.ShapeDtypeStruct((lead, tall, wide), bf16)] * 2,
        cost_estimate=spent(
            flops=2 * lead * tall * wide, bytes_accessed=12 * lead * tall * wide, transcendentals=0
        ),
        name="hop_sums",
    )(jnp.stack([up_at, down_at]).astype(jnp.int32), *operands)


def end_kernel(at_ref, term_ref, up_ref, down_ref, out_ref):
    total = term_ref[0, 0].astype(f32) + up_ref[0].astype(f32) + down_ref[0].astype(f32)
    out_ref[0] = total.astype(out_ref.dtype)


def end_sums(sums, dtype):
    lead, _, tall, wide = sums.terms.shape
    rows = chunk_of(tall, wide)
    block = pl.BlockSpec((1, rows, wide), lambda l, i, m: (l, i, 0))
    return pl.pallas_call(
        end_kernel,
        grid_spec=pltpu.PrefetchScalarGridSpec(
            num_scalar_prefetch=1,
            grid=(lead, tall // rows),
            in_specs=[
                pl.BlockSpec((1, 1, rows, wide), lambda l, i, m: (l, m[0], i, 0)),
                block,
                block,
            ],
            out_specs=block,
        ),
        out_shape=jax.ShapeDtypeStruct((lead, tall, wide), dtype),
        cost_estimate=spent(
            flops=2 * lead * tall * wide, bytes_accessed=10 * lead * tall * wide, transcendentals=0
        ),
        name="end_sums",
    )(lax.axis_index("depth").astype(jnp.int32)[None], sums.terms, sums.up, sums.down)


def attention_grad_kernel(
    at_ref, x0_ref, x1_ref, cot_ref, g0_ref, g1_ref, out_ref
):
    tall = x0_ref.shape[1]

    def store(total):
        out_ref[...] = total.reshape(out_ref.shape).astype(out_ref.dtype)

    @pl.when(pl.program_id(0) < 3)
    def _():
        store(dot_tn(x0_ref[0], g0_ref[0]) + dot_tn(x1_ref[0], g1_ref[0]))

    @pl.when(pl.program_id(0) == 3)
    def _():
        store(
            dot_tn(cot_ref[0:tall, :], g0_ref[0]) + dot_tn(cot_ref[tall : 2 * tall, :], g1_ref[0])
        )


def attention_grads(normed, cot, flat, place, depth_count, dp_count, dtype):
    _, tall, model = normed[0].shape
    heads_width = flat[0].shape[2]
    block = model // dp_count
    own_rows = block // depth_count
    normed_spec = pl.BlockSpec((1, tall, block), lambda k, m: (jnp.minimum(k, 2), 0, m[0]))
    flat_spec = pl.BlockSpec((1, tall, heads_width), lambda k, m: (lax.rem(k + 1, 4), 0, 0))
    return pl.pallas_call(
        attention_grad_kernel,
        grid_spec=pltpu.PrefetchScalarGridSpec(
            num_scalar_prefetch=1,
            grid=(4,),
            in_specs=[
                normed_spec,
                normed_spec,
                pl.BlockSpec((2 * tall, block), lambda k, m: (0, m[0])),
                flat_spec,
                flat_spec,
            ],
            out_specs=pl.BlockSpec(
                (depth_count, 1, own_rows, heads_width), lambda k, m: (0, k, 0, 0)
            ),
        ),
        out_shape=jax.ShapeDtypeStruct((depth_count, 4, own_rows, heads_width), dtype),
        compiler_params=pltpu.CompilerParams(vmem_limit_bytes=40 << 20),
        cost_estimate=spent(
            flops=16 * tall * block * heads_width,
            bytes_accessed=16 * block * heads_width,
            transcendentals=0,
        ),
        name="attention_grads",
    )(place, *normed, cot, *flat)


def hidden_grad_kernel(x0_ref, x1_ref, c0_ref, c1_ref, u0_ref, u1_ref, h0_ref, h1_ref, out_ref):
    def store(total):
        out_ref[...] = total.reshape(out_ref.shape)

    @pl.when(pl.program_id(0) == 0)
    def _():
        store(dot_tn(x0_ref[...], u0_ref[...]) + dot_tn(x1_ref[...], u1_ref[...]))

    @pl.when(pl.program_id(0) == 1)
    def _():
        store(dot_tn(c0_ref[0], h0_ref[...]) + dot_tn(c1_ref[0], h1_ref[...]))


def hidden_grads(x, cot, up_grads, hidden, dp_count, depth_count):
    tall, model = x[0].shape
    part = hidden[0].shape[1]
    block = model // dp_count
    cols = pl.BlockSpec((tall, block), lambda k, n: (0, n * (1 - k)))
    whole = pl.BlockSpec((tall, part), lambda k, n: (0, 0))
    return pl.pallas_call(
        hidden_grad_kernel,
        grid=(2, dp_count),
        in_specs=[cols, cols]
        + [
            pl.BlockSpec((1, tall, block), lambda k, n: (0, 0, n * k)),
            pl.BlockSpec((1, tall, block), lambda k, n: (1, 0, n * k)),
        ]
        + [whole] * 4,
        out_specs=pl.BlockSpec(
            (1, depth_count, block // depth_count, part), lambda k, n: (k * dp_count + n, 0, 0, 0)
        ),
        out_shape=jax.ShapeDtypeStruct(
            (2 * dp_count, depth_count, block // depth_count, part), f32
        ),
        compiler_params=pltpu.CompilerParams(vmem_limit_bytes=48 << 20),
        cost_estimate=spent(
            flops=8 * tall * model * part, bytes_accessed=8 * model * part, transcendentals=0
        ),
        name="hidden_grads",
    )(*x, cot, cot, *up_grads, *hidden)


def mix_kernel(slots, mix_ref, hist_ref, out_ref):
    rows, width = hist_ref.shape[1], hist_ref.shape[2]
    part = 512 if width % 512 == 0 else width

    def step(at, carry):
        r0 = pl.multiple_of(at * 16, 16)
        weights = mix_ref[pl.ds(r0, 16), :]
        for c0 in range(0, width, part):
            sums = [None] * STREAMS
            for k in range(slots):
                state = hist_ref[k, pl.ds(r0, 16), c0 : c0 + part].astype(f32)
                for s in range(STREAMS):
                    term = weights[:, s * slots + k : s * slots + k + 1] * state
                    sums[s] = term if sums[s] is None else sums[s] + term
            for s in range(STREAMS):
                out_ref[pl.ds(r0, 16), s * width + c0 : s * width + c0 + part] = sums[s].astype(bf16)
        return carry

    lax.fori_loop(0, rows // 16, step, 0)


def mix_streams(slot_mix, history, micro_at, depth_count, rows_mb):
    slots, _, width = history.shape
    rows = min(128, rows_mb)
    per = rows_mb // rows

    def row_block(i):
        return ((i // per) * MB + micro_at) * per + i % per

    return pl.pallas_call(
        functools.partial(mix_kernel, slots),
        grid=(depth_count * per,),
        in_specs=[
            pl.BlockSpec((rows, slot_mix.shape[1]), lambda i: (row_block(i), 0)),
            pl.BlockSpec((slots, rows, width), lambda i: (0, row_block(i), 0)),
        ],
        out_specs=pl.BlockSpec((rows, STREAMS * width), lambda i: (i, 0)),
        out_shape=jax.ShapeDtypeStruct((depth_count * rows_mb, STREAMS * width), bf16),
        cost_estimate=spent(
            flops=2 * slots * STREAMS * depth_count * rows_mb * width,
            bytes_accessed=2 * (slots + STREAMS) * depth_count * rows_mb * width,
            transcendentals=0,
        ),
        name="mix_streams",
    )(slot_mix, history)


def unmix_kernel(slots, mix_ref, hist_ref, grad_ref, *rest):
    hist_grad_ref, slot_grad_ref = rest[-2:]
    rows, width = hist_ref.shape[1], hist_ref.shape[2]
    part = 512 if width % 512 == 0 else width

    def step(at, carry):
        r0 = pl.multiple_of(at * 16, 16)
        weights = mix_ref[pl.ds(r0, 16), :]
        totals = [None] * (STREAMS * slots)
        for c0 in range(0, width, part):
            grads = [
                grad_ref[pl.ds(r0, 16), s * width + c0 : s * width + c0 + part].astype(f32)
                for s in range(STREAMS)
            ]
            for k in range(slots):
                state = hist_ref[k, pl.ds(r0, 16), c0 : c0 + part].astype(f32)
                back = None
                for s in range(STREAMS):
                    at_sk = s * slots + k
                    term = weights[:, at_sk : at_sk + 1] * grads[s]
                    back = term if back is None else back + term
                    product = state * grads[s]
                    folded = product[:, 0:128]
                    for l0 in range(128, part, 128):
                        folded = folded + product[:, l0 : l0 + 128]
                    totals[at_sk] = folded if totals[at_sk] is None else totals[at_sk] + folded
                hist_grad_ref[k, pl.ds(r0, 16), c0 : c0 + part] = back.astype(bf16)
        lane = lax.broadcasted_iota(jnp.int32, (16, 128), 1)
        packed = jnp.zeros((16, 128), f32)
        for at_sk in range(STREAMS * slots):
            column = jnp.sum(totals[at_sk], axis=1, keepdims=True)
            packed = jnp.where(lane == at_sk, column, packed)
        slot_grad_ref[pl.ds(r0, 16), :] = packed
        return carry

    lax.fori_loop(0, rows // 16, step, 0)


def unmix_streams(slot_mix, history, grads, micro_at, depth_count, rows_mb, earlier):
    slots, tokens, width = history.shape
    rows = min(128, rows_mb)
    per = rows_mb // rows

    def row_block(i):
        return ((i // per) * MB + micro_at) * per + i % per

    in_specs = [
        pl.BlockSpec((rows, slot_mix.shape[1]), lambda i: (row_block(i), 0)),
        pl.BlockSpec((slots, rows, width), lambda i: (0, row_block(i), 0)),
        pl.BlockSpec((rows, STREAMS * width), lambda i: (i, 0)),
    ]
    operands = [slot_mix, history, grads]
    aliases = {}
    if earlier is not None:
        in_specs.append(pl.BlockSpec(memory_space=pl.ANY))
        operands.append(earlier)
        aliases = {3: 0}
    return pl.pallas_call(
        functools.partial(unmix_kernel, slots),
        grid=(depth_count * per,),
        in_specs=in_specs,
        out_specs=[
            pl.BlockSpec((slots, rows, width), lambda i: (0, row_block(i), 0)),
            pl.BlockSpec((rows, 128), lambda i: (i, 0)),
        ],
        out_shape=[
            jax.ShapeDtypeStruct((slots, tokens, width), bf16),
            jax.ShapeDtypeStruct((depth_count * rows_mb, 128), f32),
        ],
        input_output_aliases=aliases,
        cost_estimate=spent(
            flops=4 * slots * STREAMS * depth_count * rows_mb * width,
            bytes_accessed=2 * (2 * slots + STREAMS) * depth_count * rows_mb * width,
            transcendentals=0,
        ),
        name="unmix_streams",
    )(*operands)


def own_spans(model_ref, width):
    own_at = pl.multiple_of(model_ref[0] * width, width)
    other_at = pl.multiple_of((1 - model_ref[0]) * width, width)
    return pl.ds(own_at, width), pl.ds(other_at, width)


def ff_split_kernel(at_ref, up_ref, down_ref, out_ref):
    out_ref[0, 0] = up_ref[...]
    out_ref[0, 1] = down_ref[...].T


def ff_split(up_weight, down_weight, partners):
    own_rows, ff_width = up_weight.shape
    count = partners.shape[0]
    part = ff_width // count
    return pl.pallas_call(
        ff_split_kernel,
        grid_spec=pltpu.PrefetchScalarGridSpec(
            num_scalar_prefetch=1,
            grid=(count,),
            in_specs=[
                pl.BlockSpec((own_rows, part), lambda i, m: (0, m[i])),
                pl.BlockSpec((part, own_rows), lambda i, m: (m[i], 0)),
            ],
            out_specs=pl.BlockSpec((1, 2, own_rows, part), lambda i, m: (i, 0, 0, 0)),
        ),
        out_shape=jax.ShapeDtypeStruct((count, 2, own_rows, part), bf16),
        cost_estimate=spent(flops=0, bytes_accessed=8 * own_rows * ff_width, transcendentals=0),
        name="ff_split",
    )(partners, up_weight, down_weight)


def ff_join_kernel(at_ref, piece_ref, up_ref, down_ref):
    up_ref[...] = piece_ref[0, 0].astype(f32)
    down_ref[...] = piece_ref[0, 1].astype(f32).T


def ff_join(pieces, partners):
    count, _, own_rows, part = pieces.shape
    return pl.pallas_call(
        ff_join_kernel,
        grid_spec=pltpu.PrefetchScalarGridSpec(
            num_scalar_prefetch=1,
            grid=(count,),
            in_specs=[pl.BlockSpec((1, 2, own_rows, part), lambda i, m: (i, 0, 0, 0))],
            out_specs=[
                pl.BlockSpec((own_rows, part), lambda i, m: (0, m[i])),
                pl.BlockSpec((part, own_rows), lambda i, m: (m[i], 0)),
            ],
        ),
        out_shape=[
            jax.ShapeDtypeStruct((own_rows, count * part), f32),
            jax.ShapeDtypeStruct((count * part, own_rows), f32),
        ],
        cost_estimate=spent(
            flops=0, bytes_accessed=12 * own_rows * count * part, transcendentals=0
        ),
        name="ff_join",
    )(partners, pieces)


def total_kernel(depth_ref, part_ref, up_ref, down_ref, cur_ref, last_ref, low_ref, resid_ref):
    width = resid_ref.shape[1]
    current = cur_ref[...].astype(f32)
    for s in range(STREAMS):
        lanes = slice(s * width, (s + 1) * width)
        total = part_ref[0, 0, :, lanes].astype(f32)
        total = total + up_ref[0, :, lanes].astype(f32) + down_ref[0, :, lanes].astype(f32)
        total = total + last_ref[:, s : s + 1] * current
        if s == STREAMS - 1:
            resid_ref[...] = total
        low_ref[:, lanes] = total.astype(bf16)


def total_streams(sums, current_half, last, depth_at):
    _, _, tall, wide = sums.terms.shape
    width = wide // STREAMS
    rows = min(64, tall)
    row = lambda i, d: (i, 0)
    return pl.pallas_call(
        total_kernel,
        grid_spec=pltpu.PrefetchScalarGridSpec(
            num_scalar_prefetch=1,
            grid=(tall // rows,),
            in_specs=[
                pl.BlockSpec((1, 1, rows, wide), lambda i, d: (0, d[0], i, 0)),
                pl.BlockSpec((1, rows, wide), lambda i, d: (0, i, 0)),
                pl.BlockSpec((1, rows, wide), lambda i, d: (0, i, 0)),
                pl.BlockSpec((rows, width), row),
                pl.BlockSpec((rows, 128), row),
            ],
            out_specs=[pl.BlockSpec((rows, wide), row), pl.BlockSpec((rows, width), row)],
        ),
        out_shape=[
            jax.ShapeDtypeStruct((tall, wide), bf16),
            jax.ShapeDtypeStruct((tall, width), f32),
        ],
        cost_estimate=spent(flops=5 * tall * wide, bytes_accessed=9 * tall * wide, transcendentals=0),
        name="total_streams",
    )(depth_at, sums.terms, sums.up, sums.down, current_half, last)


def norm_kernel(model_ref, own_ref, other_ref, gain_ref, normed_ref, ff_ref, stat_ref):
    rows, width = ff_ref.shape
    model = 2 * width
    own_span, other_span = own_spans(model_ref, width)
    lane = lax.broadcasted_iota(jnp.int32, (rows, 128), 1)
    stats = jnp.zeros((rows, 128), f32)
    for s in range(STREAMS):
        lanes = slice(s * width, (s + 1) * width)
        own = own_ref[:, lanes].astype(f32)
        other = other_ref[:, lanes].astype(f32)
        average = (
            jnp.sum(own, axis=-1, keepdims=True) + jnp.sum(other, axis=-1, keepdims=True)
        ) / model
        own, other = own - average, other - average
        variance = (
            jnp.sum(own * own, axis=-1, keepdims=True)
            + jnp.sum(other * other, axis=-1, keepdims=True)
        ) / model
        inverse = lax.rsqrt(variance + NORM_EPSILON)
        stats = jnp.where(lane == 2 * s, average, stats)
        stats = jnp.where(lane == 2 * s + 1, inverse, stats)
        norm_own = (own * inverse * gain_ref[s : s + 1, own_span]).astype(bf16)
        if s == STREAMS - 1:
            ff_ref[...] = norm_own
        else:
            normed_ref[s, :, own_span] = norm_own
            norm_other = (other * inverse * gain_ref[s : s + 1, other_span]).astype(bf16)
            normed_ref[s, :, other_span] = norm_other
    stat_ref[...] = stats


def norm_streams(low, low_other, gains, which):
    tall, wide = low.shape
    width = wide // STREAMS
    rows = min(64, tall)
    row = lambda i, m: (i, 0)
    return pl.pallas_call(
        norm_kernel,
        grid_spec=pltpu.PrefetchScalarGridSpec(
            num_scalar_prefetch=1,
            grid=(tall // rows,),
            in_specs=[
                pl.BlockSpec((rows, wide), row),
                pl.BlockSpec((rows, wide), row),
                pl.BlockSpec(gains.shape, lambda i, m: (0, 0)),
            ],
            out_specs=[
                pl.BlockSpec((3, rows, 2 * width), lambda i, m: (0, i, 0)),
                pl.BlockSpec((rows, width), row),
                pl.BlockSpec((rows, 128), row),
            ],
        ),
        out_shape=[
            jax.ShapeDtypeStruct((3, tall, 2 * width), bf16),
            jax.ShapeDtypeStruct((tall, width), bf16),
            jax.ShapeDtypeStruct((tall, 128), f32),
        ],
        cost_estimate=spent(
            flops=20 * tall * wide, bytes_accessed=8 * tall * wide, transcendentals=0
        ),
        name="norm_streams",
    )(which, low, low_other, gains)


def turn(values, cosine, sine_up, sine_down, sign):
    up = pltpu.roll(values, HDIM - ROT // 2, 1)
    down = pltpu.roll(values, ROT // 2, 1)
    return values * cosine + sign * (up * sine_up + down * sine_down)


def project_kernel(
    x_ref, cot_ref, wq_ref, wk_ref, wv_ref, wo_ref, cos_ref, up_ref, down_ref, out_ref
):
    span = wq_ref.shape[-1]
    tables = cos_ref[...], up_ref[...], down_ref[...]
    for kind, w_ref in enumerate((wq_ref, wk_ref, wv_ref, wo_ref)):
        rows = cot_ref[...] if kind == 3 else x_ref[kind]
        product = dot_nn(rows, w_ref[...].reshape(-1, span))
        for begin in range(0, span, HDIM):
            head = product[:, begin : begin + HDIM]
            if kind < 2:
                head = turn(head, *tables, 1.0)
            out_ref[0, :, kind * span + begin : kind * span + begin + HDIM] = head.astype(bf16)


def project_heads(normed, cot, weights, tables, depth_count):
    _, rows, model = normed.shape
    groups, _, _, own_rows, heads_width = weights.shape
    span = heads_width // depth_count
    whole = lambda j: (0, 0)

    def matrix(kind):
        shape = (groups, depth_count, 1, own_rows, span)
        return pl.BlockSpec(shape, lambda j: (0, 0, kind, 0, j))

    return pl.pallas_call(
        project_kernel,
        grid=(depth_count,),
        in_specs=[
            pl.BlockSpec((3, rows, model), lambda j: (0, 0, 0)),
            pl.BlockSpec((rows, model), whole),
        ]
        + [matrix(kind) for kind in range(4)]
        + [pl.BlockSpec((rows, HDIM), whole)] * 3,
        out_specs=pl.BlockSpec((1, rows, 4 * span), lambda j: (j, 0, 0)),
        out_shape=jax.ShapeDtypeStruct((depth_count, rows, 4 * span), bf16),
        compiler_params=pltpu.CompilerParams(vmem_limit_bytes=40 << 20),
        cost_estimate=spent(
            flops=8 * rows * model * span * depth_count,
            bytes_accessed=8 * model * span * depth_count + 8 * rows * model,
            transcendentals=0,
        ),
        name="project_heads",
    )(normed, cot, *[weights] * 4, *tables)


def attend_kernel(
    block, q_ref, k_ref, v_ref, g_ref, doc_col_ref, doc_row_ref, cos_ref, up_ref, down_ref,
    out_ref, dk_sum, dv_sum,
):
    length = q_ref.shape[0]
    scale = HDIM**-0.5
    heads_each = out_ref.shape[1] // (4 * HDIM)

    def lanes(kind):
        return pl.ds(pl.multiple_of((kind * heads_each + pl.program_id(0)) * HDIM, HDIM), HDIM)

    for begin in range(0, length, block):
        end = begin + block
        rows = slice(begin, end)
        queries, grads = q_ref[rows, :], g_ref[rows, :]
        keys, values = k_ref[0:end, :], v_ref[0:end, :]
        scores = dot_nt(queries, keys) * scale
        place_q = begin + lax.broadcasted_iota(jnp.int32, scores.shape, 0)
        place_k = lax.broadcasted_iota(jnp.int32, scores.shape, 1)
        allowed = (doc_col_ref[rows, :] == doc_row_ref[:, 0:end]) & (place_q >= place_k)
        scores = jnp.where(allowed, scores, MASKED)
        highest = jnp.max(scores, axis=-1, keepdims=True)
        exponent = jnp.exp(scores - highest)
        totals = jnp.sum(exponent, axis=-1, keepdims=True)
        attention = exponent * (1.0 / totals)
        low = attention.astype(bf16)
        out_ref[rows, lanes(0)] = dot_nn(low, values).astype(bf16)
        grad_att = dot_nt(grads, values).astype(bf16).astype(f32)
        weighted = jnp.sum(attention * grad_att, axis=-1, keepdims=True)
        grad_scores = (attention * (grad_att - weighted)).astype(bf16)
        grad_q = dot_nn(grad_scores, keys) * scale
        out_ref[rows, lanes(1)] = turn(
            grad_q, cos_ref[rows, :], up_ref[rows, :], down_ref[rows, :], -1.0
        ).astype(bf16)
        part_k = dot_tn(grad_scores, queries)
        part_v = dot_tn(low, grads)
        if begin > 0:
            dk_sum[0:begin, :] += part_k[0:begin]
            dv_sum[0:begin, :] += part_v[0:begin]
        dk_sum[begin:end, :] = part_k[begin:end]
        dv_sum[begin:end, :] = part_v[begin:end]
    grad_k = dk_sum[...] * scale
    out_ref[:, lanes(2)] = turn(grad_k, cos_ref[...], up_ref[...], down_ref[...], -1.0).astype(bf16)
    out_ref[:, lanes(3)] = dv_sum[...].astype(bf16)


def attend(packed, documents, tables, heads_each):
    length = packed.shape[0]
    block = min(256, length)
    whole = lambda h: (0, 0)

    def kind(at):
        return pl.BlockSpec((length, HDIM), lambda h: (0, at * heads_each + h))

    return pl.pallas_call(
        functools.partial(attend_kernel, block),
        grid=(heads_each,),
        in_specs=[kind(0), kind(1), kind(2), kind(3)]
        + [pl.BlockSpec((length, 1), whole), pl.BlockSpec((1, length), whole)]
        + [pl.BlockSpec((length, HDIM), whole)] * 3,
        out_specs=pl.BlockSpec((length, 4 * heads_each * HDIM), whole),
        out_shape=jax.ShapeDtypeStruct((length, 4 * heads_each * HDIM), bf16),
        scratch_shapes=[pltpu.VMEM((length, HDIM), f32)] * 2,
        compiler_params=pltpu.CompilerParams(vmem_limit_bytes=48 << 20),
        cost_estimate=spent(
            flops=9 * heads_each * length * length * HDIM,
            bytes_accessed=16 * length * heads_each * HDIM + 12 * length * HDIM,
            transcendentals=heads_each * length * length,
        ),
        name="attend",
    )(packed, packed, packed, packed, documents[:, None], documents[None, :], *tables)


def gelu_parts(values):
    cdf = 0.5 * (1.0 + lax.erf(values * (0.5**0.5)))
    density = jnp.exp(-0.5 * values * values) * (1.0 / math.sqrt(2.0 * math.pi))
    return values * cdf, cdf + values * density


def ff_kernel(
    model_ref, x_ref, cot_ref, up_ref, down_ref,
    hidden_ref, grad_ref, out_own_ref, out_other_ref, back_own_ref, back_other_ref,
):
    part = up_ref.shape[-1]
    half = up_ref.shape[1] // 2

    def rows_of(ref, which):
        return ref[0, pl.ds(which * half, half)].reshape(-1, part)

    own, other = model_ref[0], 1 - model_ref[0]
    up_pre = dot_nn(x_ref[...], up_ref[...].reshape(-1, part))
    hidden, slope = gelu_parts(up_pre)
    hidden = hidden.astype(bf16)
    grad_up = (dot_nn(cot_ref[0], down_ref[...].reshape(-1, part)) * slope).astype(bf16)
    hidden_ref[...] = hidden
    grad_ref[...] = grad_up
    back_other_ref[...] = dot_nt(grad_up, rows_of(up_ref, other)).astype(bf16)
    back_own_ref[...] = dot_nt(grad_up, rows_of(up_ref, own))
    out_other_ref[...] = dot_nt(hidden, rows_of(down_ref, other)).astype(bf16)
    out_own_ref[...] = dot_nt(hidden, rows_of(down_ref, own))


def feed_forward(x, cot, micro_at, weights, which):
    tall, model = x.shape
    part = weights.shape[-1]
    width = model // 2
    rows = min(256, tall)
    row = lambda i, m: (i, 0)

    def resident(kind):
        return pl.BlockSpec(
            (1,) + weights.shape[1:],
            lambda i, m: (kind, 0, 0, 0, 0),
            pipeline_mode=pl.Buffered(1),
        )

    return pl.pallas_call(
        ff_kernel,
        grid_spec=pltpu.PrefetchScalarGridSpec(
            num_scalar_prefetch=1,
            grid=(tall // rows,),
            in_specs=[
                pl.BlockSpec((rows, model), row),
                pl.BlockSpec((1, rows, model), lambda i, m: (micro_at, i, 0)),
                resident(0),
                resident(1),
            ],
            out_specs=[pl.BlockSpec((rows, part), row)] * 2
            + [pl.BlockSpec((rows, width), row)] * 4,
        ),
        out_shape=[jax.ShapeDtypeStruct((tall, part), bf16)] * 2
        + [
            jax.ShapeDtypeStruct((tall, width), f32),
            jax.ShapeDtypeStruct((tall, width), bf16),
            jax.ShapeDtypeStruct((tall, width), f32),
            jax.ShapeDtypeStruct((tall, width), bf16),
        ],
        compiler_params=pltpu.CompilerParams(vmem_limit_bytes=48 << 20),
        cost_estimate=spent(
            flops=8 * tall * model * part,
            bytes_accessed=4 * model * part + 16 * tall * model,
            transcendentals=2 * tall * part,
        ),
        name="feed_forward",
    )(which, x, cot, weights, weights)


def back_kernel(half_ref, ans_ref, wo_ref, wq_ref, wk_ref, wv_ref, out_ref, *flat):
    count, _, wide = ans_ref.shape
    span = wide // 4
    for kind, w_ref in enumerate((wo_ref, wq_ref, wk_ref, wv_ref)):
        total = None
        for j in range(count):
            term = dot_nt(
                ans_ref[j, :, kind * span : (kind + 1) * span],
                w_ref[:, :, :, :, j * span : (j + 1) * span].reshape(-1, span),
            )
            total = term if total is None else total + term
        out_ref[kind] = total.astype(out_ref.dtype)
    if flat:

        @pl.when(pl.program_id(0) == 0)
        def _():
            for kind in range(4):
                for j in range(count):
                    flat[0][kind, :, j * span : (j + 1) * span] = ans_ref[
                        j, :, kind * span : (kind + 1) * span
                    ]


def back_project(answer, weights, half, dtype, flat):
    count, rows, wide = answer.shape
    groups, _, _, own_rows, heads_width = weights.shape
    part = count * own_rows
    steps = groups // 2
    width = part * steps

    def matrix(kind):
        shape = (1, count, 1, own_rows, heads_width)
        return pl.BlockSpec(shape, lambda i, m: (m[0] * steps + i, 0, kind, 0, 0))

    out_specs = [pl.BlockSpec((4, rows, part), lambda i, m: (0, 0, i))]
    out_shape = [jax.ShapeDtypeStruct((4, rows, width), dtype)]
    if flat:
        out_specs.append(pl.BlockSpec((4, rows, heads_width), lambda i, m: (0, 0, 0)))
        out_shape.append(jax.ShapeDtypeStruct((4, rows, heads_width), bf16))
    return pl.pallas_call(
        back_kernel,
        grid_spec=pltpu.PrefetchScalarGridSpec(
            num_scalar_prefetch=1,
            grid=(steps,),
            in_specs=[pl.BlockSpec((count, rows, wide), lambda i, m: (0, 0, 0))]
            + [matrix(kind) for kind in (3, 0, 1, 2)],
            out_specs=out_specs,
        ),
        out_shape=out_shape,
        compiler_params=pltpu.CompilerParams(vmem_limit_bytes=40 << 20),
        cost_estimate=spent(
            flops=8 * rows * heads_width * width,
            bytes_accessed=8 * heads_width * width + 20 * rows * width,
            transcendentals=0,
        ),
        name="back_project",
    )(half, answer, *[weights] * 4)


def slope_kernel(
    model_ref, own_ref, got_ref, ff_ref, low_ref, stat_ref, gain_ref, scaled_ref, sum_ref, gain_out_ref
):
    rows, width = ff_ref.shape
    own_span, _ = own_spans(model_ref, width)
    lane = lax.broadcasted_iota(jnp.int32, (rows, 128), 1)
    packed = jnp.zeros((rows, 128), f32)
    totals = []
    for s in range(STREAMS):
        lanes = slice(s * width, (s + 1) * width)
        if s < 3:
            grad = own_ref[s + 1] + got_ref[s + 1].astype(f32)
        else:
            grad = ff_ref[...]
        average, inverse = stat_ref[:, 2 * s : 2 * s + 1], stat_ref[:, 2 * s + 1 : 2 * s + 2]
        hat = (low_ref[:, lanes].astype(f32) - average) * inverse
        totals.append(jnp.sum(grad * hat, axis=0, keepdims=True))
        scaled = grad * gain_ref[s : s + 1, own_span]
        scaled_ref[:, lanes] = scaled
        packed = jnp.where(lane == 2 * s, jnp.sum(scaled, axis=-1, keepdims=True), packed)
        packed = jnp.where(
            lane == 2 * s + 1, jnp.sum(scaled * hat, axis=-1, keepdims=True), packed
        )
    sum_ref[...] = packed
    totals = jnp.concatenate(totals, axis=0)

    @pl.when(pl.program_id(0) == 0)
    def _():
        gain_out_ref[...] = totals

    @pl.when(pl.program_id(0) > 0)
    def _():
        gain_out_ref[...] += totals


def norm_slopes(own, got, ff_grad, low, stats, gains, which):
    tall, wide = low.shape
    width = wide // STREAMS
    rows = min(64, tall)
    row = lambda i, m: (i, 0)
    cube = pl.BlockSpec((4, rows, width), lambda i, m: (0, i, 0))
    return pl.pallas_call(
        slope_kernel,
        grid_spec=pltpu.PrefetchScalarGridSpec(
            num_scalar_prefetch=1,
            grid=(tall // rows,),
            in_specs=[
                cube,
                cube,
                pl.BlockSpec((rows, width), row),
                pl.BlockSpec((rows, wide), row),
                pl.BlockSpec((rows, 128), row),
                pl.BlockSpec(gains.shape, lambda i, m: (0, 0)),
            ],
            out_specs=[
                pl.BlockSpec((rows, wide), row),
                pl.BlockSpec((rows, 128), row),
                pl.BlockSpec((STREAMS, width), lambda i, m: (0, 0)),
            ],
        ),
        out_shape=[
            jax.ShapeDtypeStruct((tall, wide), f32),
            jax.ShapeDtypeStruct((tall, 128), f32),
            jax.ShapeDtypeStruct((STREAMS, width), f32),
        ],
        cost_estimate=spent(
            flops=12 * tall * wide, bytes_accessed=12 * tall * wide, transcendentals=0
        ),
        name="norm_slopes",
    )(which, own, got, ff_grad, low, stats, gains)


def grads_kernel(
    scaled_ref, mine_ref, theirs_ref, low_ref, stat_ref, cot_ref, cur_ref, last_ref,
    grad_ref, mix_ref, dot_ref,
):
    rows, width = cot_ref.shape
    lane = lax.broadcasted_iota(jnp.int32, (rows, 128), 1)
    means = (mine_ref[...] + theirs_ref[...]) / (2 * width)
    current = cur_ref[...].astype(f32)
    packed = jnp.zeros((rows, 128), f32)
    mixed = None
    for s in range(STREAMS):
        lanes = slice(s * width, (s + 1) * width)
        average, inverse = stat_ref[:, 2 * s : 2 * s + 1], stat_ref[:, 2 * s + 1 : 2 * s + 2]
        hat = (low_ref[:, lanes].astype(f32) - average) * inverse
        grad = inverse * (
            scaled_ref[:, lanes]
            - means[:, 2 * s : 2 * s + 1]
            - hat * means[:, 2 * s + 1 : 2 * s + 2]
        )
        if s == STREAMS - 1:
            grad = grad + cot_ref[...].astype(f32)
        grad = grad.astype(bf16)
        grad_ref[:, lanes] = grad
        grad = grad.astype(f32)
        term = last_ref[:, s : s + 1] * grad
        mixed = term if mixed is None else mixed + term
        packed = jnp.where(lane == s, jnp.sum(grad * current, axis=-1, keepdims=True), packed)
    mix_ref[...] = mixed
    dot_ref[...] = packed


def stream_grads(scaled, mine, theirs, low, stats, cot, current_half, last):
    tall, wide = low.shape
    width = wide // STREAMS
    rows = min(64, tall)
    row = lambda i: (i, 0)
    return pl.pallas_call(
        grads_kernel,
        grid=(tall // rows,),
        in_specs=[
            pl.BlockSpec((rows, wide), row),
            pl.BlockSpec((rows, 128), row),
            pl.BlockSpec((rows, 128), row),
            pl.BlockSpec((rows, wide), row),
            pl.BlockSpec((rows, 128), row),
            pl.BlockSpec((rows, width), row),
            pl.BlockSpec((rows, width), row),
            pl.BlockSpec((rows, 128), row),
        ],
        out_specs=[
            pl.BlockSpec((rows, wide), row),
            pl.BlockSpec((rows, width), row),
            pl.BlockSpec((rows, 128), row),
        ],
        out_shape=[
            jax.ShapeDtypeStruct((tall, wide), bf16),
            jax.ShapeDtypeStruct((tall, width), f32),
            jax.ShapeDtypeStruct((tall, 128), f32),
        ],
        cost_estimate=spent(
            flops=12 * tall * wide, bytes_accessed=10 * tall * wide, transcendentals=0
        ),
        name="stream_grads",
    )(scaled, mine, theirs, low, stats, cot, current_half, last)


def turning_tables(places):
    half = ROT // 2
    inverse = jnp.exp(jnp.arange(half, dtype=f32) * (-2.0 * math.log(10000.0) / ROT))
    angles = places.astype(f32)[:, None] * inverse[None, :]
    cosine, sine = jnp.cos(angles), jnp.sin(angles)
    rows = places.shape[0]
    rest = jnp.zeros((rows, HDIM - ROT), f32)
    blank = jnp.zeros((rows, half), f32)
    return (
        jnp.concatenate([cosine, cosine, rest + 1.0], axis=1),
        jnp.concatenate([-sine, blank, rest], axis=1),
        jnp.concatenate([blank, sine, rest], axis=1),
    )


def local(
    history,
    slot_layer,
    current,
    positions,
    doc_ids,
    cotangent,
    norm_gains,
    generator_in,
    generator_out,
    query_weight,
    key_weight,
    value_weight,
    out_weight,
    up_weight,
    down_weight,
):
    dp_count = lax.axis_size("dp")
    depth_count = lax.axis_size("depth")
    dp_at = lax.axis_index("dp")
    model_at = lax.axis_index("mp")
    dp_bits = list(range(bit_count(dp_count)))
    slots, tokens_held, width = history.shape
    model = current.shape[1]
    rows_mb = current.shape[0] // MB
    length = depth_count * rows_mb
    heads_width = query_weight.shape[1]
    heads_each = heads_width // HDIM // depth_count
    own_rows = query_weight.shape[0]
    ff_width = up_weight.shape[1]
    ff_part = ff_width // dp_count
    both = ("dp", "depth")

    def half_of(values, axis, which):
        return lax.dynamic_slice_in_dim(values, which * width, width, axis)

    small_cols = jnp.concatenate(
        [generator_in, norm_gains.T, jnp.zeros((own_rows, 128 - GEN - 5), bf16)], axis=1
    )
    small_all = gather_small(small_cols, both).reshape(model, 128)
    gen_first = small_all[:, :GEN]
    gain_float = small_all[:, GEN : GEN + 5].astype(f32).T
    second_rows = generator_out.shape[0]
    second_pad = -second_rows % 128
    second_all = gather_small(jnp.pad(generator_out, (0, second_pad))[None], both)
    gen_second = second_all.reshape(-1, second_rows + second_pad)[:, :second_rows]
    second_low = gen_second.reshape(GEN, STREAMS * MIX)

    stacked = jnp.concatenate([query_weight, key_weight, value_weight, out_weight.T], axis=0)
    over_depth = lax.all_gather(stacked, "depth", axis=0, tiled=True)
    current_f = current.astype(f32)
    current_half = half_of(current, 1, model_at)
    mean_square = jnp.mean(current_f * current_f, axis=-1, keepdims=True)
    inverse_rms = lax.rsqrt(mean_square + RMS_EPSILON)
    unit = current_f * inverse_rms
    gen_normed = (unit * gain_float[4]).astype(bf16)
    gen_pre = dot_nn(gen_normed, gen_first)
    gen_hidden = gelu_exact(gen_pre).astype(bf16)
    column = jnp.arange(STREAMS * MIX)
    last_col = (column % MIX == MIX - 1).astype(f32)
    mixing = (dot_nn(gen_hidden, second_low) + last_col).astype(bf16)
    pick_last = (column[:, None] == (jnp.arange(128) * MIX + MIX - 1)[None, :]).astype(bf16)
    last = dot_nn(mixing, pick_last)

    layer_of = jnp.tile(slot_layer, STREAMS)
    stream_of = jnp.repeat(jnp.arange(STREAMS), slots)
    from_col = jnp.where(layer_of < MIX, stream_of * MIX + layer_of, -1)
    pick = (column[:, None] == from_col[None, :]).astype(f32)
    mix_all = gather_small(mixing, ("depth",)).reshape(depth_count * MB * rows_mb, STREAMS * MIX)
    slot_mix = dot_nn(mix_all, pick.astype(bf16))
    places_all = gather_small(positions, ("depth",))

    def over_depth_swap(values):
        return lax.all_to_all(values, "depth", 0, 0, tiled=True)

    def mix_part(micro_at, slot_mix):
        partial = mix_streams(slot_mix, history, micro_at, depth_count, rows_mb)
        return partial.reshape(1, depth_count, rows_mb, STREAMS * width)

    partners = jnp.stack([dp_at ^ m for m in range(dp_count)]).astype(jnp.int32)
    ff_local = ff_split(up_weight, down_weight, partners)
    ff_local, cotangent, slot_mix = fence(ff_local, cotangent, slot_mix)
    cot_pieces = group_hop(cotangent[None], 0)
    ff_rows = place_block(None, ff_local[0], partners[0], dp_count)
    for m in range(1, dp_count):
        arrived = swap_mask(ff_local[m], "dp", m)
        ff_rows = place_block(ff_rows, arrived, partners[m], dp_count)
    ff_rows = ff_rows.reshape(2 * dp_count, own_rows, ff_part)

    partial = mix_part(0, slot_mix)
    over_depth, partial, slot_mix, ff_rows, cot_pieces, places_all = fence(
        over_depth, partial, slot_mix, ff_rows, cot_pieces, places_all
    )

    weights_line = LineGather(ff_rows)
    weights_line.step()
    flat_rows = depth_count * 4 * own_rows
    pieces = [over_depth.reshape(flat_rows, heads_width)]
    pieces.append(core_hop(pieces[0], 0))
    weights = place_block(None, pieces[0][None], place_index(0), dp_count)
    partial_next = mix_part(1, slot_mix)
    cot_other = other_core(cotangent)
    pieces, partial, partial_next, weights, cot_pieces, cot_other = weights_line.hold(
        pieces, partial, partial_next, weights, cot_pieces, cot_other
    )
    hops_left = [(p, at) for at in range(1, len(dp_bits)) for p in range(1 << at)]
    placed = 1
    cots = None
    sums, sums_next = LineScatter(partial), LineScatter(partial_next)
    for hop in range(1, depth_count):
        sums.step()
        weights_line.step()
        last_hop = hop == depth_count - 1
        for place in range(placed, len(pieces)):
            weights = place_block(weights, pieces[place][None], place_index(place), dp_count)
        placed = len(pieces)
        while hops_left:
            place, at = hops_left.pop(0)
            pieces.append(core_hop(pieces[place], at))
            if len(hops_left) <= depth_count - 2 - hop:
                break
        if last_hop:
            cot_full = join_halves(cotangent, cot_other, model_at)
            for at in range(1, len(dp_bits)):
                cot_pieces = group_hop(cot_pieces, at)
            ff_weights = weights_line.placed()
            sums_next.step()
            cots = cot_full, ff_weights
        (state,) = weights_line.hold(
            (sums.up, sums.down, pieces, weights, cot_pieces, cot_other, cots)
        )
        sums.up, sums.down, pieces, weights, cot_pieces, cot_other, cots = state
    while sums_next.at < depth_count - 3:
        sums_next.hold()
        sums_next.step()
    cot_full, ff_weights = cots
    for place in range(placed, len(pieces)):
        weights = place_block(weights, pieces[place][None], place_index(place), dp_count)
    weights = weights.reshape(dp_count, depth_count, 4, own_rows, heads_width)
    ff_weights = ff_weights.reshape(2, dp_count, depth_count, own_rows, ff_part)

    document_view = doc_ids.reshape(depth_count, MB, rows_mb)
    own_tables = turning_tables(positions)
    which = model_at.astype(jnp.int32)[None]
    depth_at = lax.axis_index("depth").astype(jnp.int32)[None]
    gains = gain_float

    def enter(micro_at, sums):
        span = slice(micro_at * rows_mb, (micro_at + 1) * rows_mb)
        low, resid = total_streams(sums, current_half[span], last[span], depth_at)
        normed, ff_normed, stats = norm_streams(low, other_core(low), gains, which)
        packed = project_heads(
            normed,
            cot_full[span],
            weights,
            [t[span] for t in own_tables],
            depth_count,
        )
        return dict(
            low=low, resid=resid, normed=normed, ff_normed=ff_normed, stats=stats, packed=packed
        )

    def attention(micro_at, by_head):
        span = slice(micro_at * rows_mb, (micro_at + 1) * rows_mb)
        documents = document_view[:, micro_at].reshape(length)
        seq_places = places_all[:, span].reshape(length)
        by_head = by_head.reshape(length, 4 * heads_each * HDIM)
        answer = attend(by_head, documents, turning_tables(seq_places), heads_each)
        return answer.reshape(depth_count, rows_mb, 4 * heads_each * HDIM)

    def group_rows(ff_normed):
        mine = group_gather(ff_normed).reshape(dp_count * rows_mb, width)
        return join_halves(mine, other_core(mine), model_at)

    def hidden_units(micro_at, group_normed):
        hidden, grad_up, out_own, out_other, back_own, back_other = feed_forward(
            group_normed, cot_group, micro_at, ff_weights, which
        )
        return (
            dict(group_normed=group_normed, hidden=hidden, grad_up=grad_up),
            ((back_own, other_core(back_other)), (out_own, other_core(out_other))),
        )

    def reduce_group(own, other):
        total = own + other.astype(f32)
        return group_scatter(total.reshape(dp_count, rows_mb, width))

    def back(kept, answer, ff_parts):
        (theirs,) = back_project(answer, weights, 1 - which, bf16, False)
        got = other_core(theirs)
        own, kept["flat"] = back_project(answer, weights, which, f32, True)
        grad_norm_ff = reduce_group(*ff_parts[0])
        ff_out = reduce_group(*ff_parts[1])
        rows = (kept["resid"] + own[0] + got[0].astype(f32) + ff_out).astype(bf16)
        return own, got, grad_norm_ff, rows

    def leave(micro_at, kept, own, got, grad_norm_ff, rows):
        span = slice(micro_at * rows_mb, (micro_at + 1) * rows_mb)
        low, stats = kept["low"], kept["stats"]
        scaled, sums, gain_part = norm_slopes(own, got, grad_norm_ff, low, stats, gains, which)
        grad_low, current_mix, last_dot = stream_grads(
            scaled, sums, other_core(sums), low, stats, cotangent[span], current_half[span], last[span]
        )
        kept.update(layer_rows=rows, gain=gain_part, current_mix=current_mix, last_dot=last_dot)
        return grad_low

    sums_next.step()
    first = enter(0, sums)
    packed, ff_normed, cot_pieces = sums_next.hold(
        first["packed"], first["ff_normed"], cot_pieces
    )
    sums_next.step()
    cot_mine = group_rows_placed(cot_pieces).reshape(dp_count, MB, rows_mb, width)
    cot_mine = jnp.swapaxes(cot_mine, 0, 1).reshape(MB * dp_count * rows_mb, width)
    cot_group = join_halves(cot_mine, other_core(cot_mine), model_at)
    cot_group = cot_group.reshape(MB, dp_count * rows_mb, model)
    by_head = over_depth_swap(packed)
    group_normed = group_rows(ff_normed)
    by_head, group_normed, cot_group = sums_next.hold(by_head, group_normed, cot_group)
    answer = attention(0, by_head)
    answer, group_normed = sums_next.hold(answer, group_normed)

    answer = over_depth_swap(answer)
    second = enter(1, sums_next)
    kept, ff_parts = hidden_units(0, group_normed)
    first.update(kept)
    answer, packed, ff_normed, ff_parts = fence(
        answer, second["packed"], second["ff_normed"], ff_parts
    )
    by_head = over_depth_swap(packed)
    group_normed = group_rows(ff_normed)
    ways = back(first, answer, ff_parts)
    by_head, group_normed, ways = fence(by_head, group_normed, ways)
    answer = attention(1, by_head)
    answer, group_normed, ways = fence(answer, group_normed, ways)

    answer = over_depth_swap(answer)
    grad_low = leave(0, first, *ways)
    kept, ff_parts = hidden_units(1, group_normed)
    second.update(kept)
    answer, grad_low, ff_parts = fence(answer, grad_low, ff_parts)
    saved = [first, second]

    def each(name):
        return [s[name] for s in saved]

    def rows_of(name):
        return jnp.concatenate(each(name), axis=0)

    grad_line = LineGather(grad_low[None])
    place_list = jnp.stack([place_index(p) for p in range(dp_count)]).astype(jnp.int32)

    def place_grads(place, dtype):
        return attention_grads(
            each("normed"),
            cot_full,
            each("flat"),
            place_list[place : place + 1],
            depth_count,
            dp_count,
            dtype,
        )

    half = dp_count // 2
    hops_left = [
        (p, at) for at in reversed(range(len(dp_bits))) for p in range(1 << at, 2 << at)
    ]
    pieces = {}

    def sums_hop():
        place, at = hops_left.pop(0)
        arrived = core_hop(pieces.pop(place).astype(bf16), at)
        target = place - (1 << at)
        pieces[target] = pieces[target].astype(f32) + arrived.astype(f32)

    grad_line.step()
    ways = back(second, answer, ff_parts)
    ff_products = hidden_grads(
        each("group_normed"), cot_group, each("grad_up"), each("hidden"), dp_count, depth_count
    )
    ways, ff_products = grad_line.hold(ways, ff_products)
    pieces = {p: place_grads(p, bf16) for p in range(half, dp_count)}
    ff_sums = LineScatter(ff_products)
    for hop in range(2, depth_count):
        grad_line.step()
        ff_sums.step()
        if hop == 2:
            arrived = core_hop(pieces.pop(half), hops_left.pop(0)[1])
            grad_low = leave(1, second, *ways)
            (state,) = grad_line.hold((grad_low, ff_sums.up, ff_sums.down, arrived, pieces))
            grad_low, ff_sums.up, ff_sums.down, arrived, pieces = state
        else:
            if hop == 3:
                pieces.update({p: place_grads(p, f32) for p in range(half)})
                pieces[0] = pieces[0] + arrived.astype(f32)
            sums_hop()
            (state,) = grad_line.hold((grad_low, ff_sums.up, ff_sums.down, pieces))
            grad_low, ff_sums.up, ff_sums.down, pieces = state

    last_line = LineGather(grad_low[None])
    last_line.step()
    while hops_left:
        sums_hop()
    grad_first = grad_line.placed().reshape(length, -1)
    history_grad, slot_part = unmix_streams(
        slot_mix, history, grad_first, 0, depth_count, rows_mb, None
    )
    slot_parts = [slot_part.reshape(depth_count, 1, rows_mb, 128)]
    pieces, history_grad = last_line.hold(pieces, history_grad)
    out_sums = LineScatter(pieces[0].reshape(1, depth_count, 4 * own_rows, heads_width))
    for hop in range(2, depth_count):
        last_line.step()
        out_sums.step()
        (state,) = last_line.hold((out_sums.up, out_sums.down))
        out_sums.up, out_sums.down = state
    ff_sums.step()
    out_sums.step()
    last_grads = last_line.placed().reshape(length, -1)
    history_grad, slot_part = unmix_streams(
        slot_mix, history, last_grads, 1, depth_count, rows_mb, history_grad
    )
    slot_parts.append(slot_part.reshape(depth_count, 1, rows_mb, 128))

    slot_grads = jnp.concatenate(slot_parts, axis=1).reshape(-1, 128)[:, : STREAMS * slots]
    mix_grads = dot_exact(slot_grads, pick.T).reshape(depth_count, MB * rows_mb, STREAMS * MIX)
    (state,) = ff_sums.hold((mix_grads, out_sums.up, out_sums.down))
    mix_grads, out_sums.up, out_sums.down = state
    grad_mixing = scatter_small(mix_grads, ("depth",))
    scattered = end_sums(out_sums, f32).reshape(4, own_rows, heads_width)
    ff_grads = end_sums(ff_sums, bf16).reshape(2, dp_count, own_rows, ff_part)
    ff_pieces = [
        lax.dynamic_index_in_dim(ff_grads, partners[m], 1, keepdims=False) for m in range(dp_count)
    ]
    ff_pieces = [ff_pieces[0]] + [swap_mask(ff_pieces[m], "dp", m) for m in range(1, dp_count)]
    up_grad, down_grad = ff_join(jnp.stack(ff_pieces), partners)
    last_dots = rows_of("last_dot")
    grad_mixing = grad_mixing + dot_exact(last_dots, pick_last.astype(f32).T)
    grad_mixing = grad_mixing + other_core(grad_mixing)

    second_float = second_low.astype(f32)
    grad_second = dot_exact(gen_hidden.astype(f32).T, grad_mixing)
    grad_pre = dot_exact(grad_mixing, second_float.T) * gelu_slope(gen_pre)
    grad_first = dot_exact(gen_normed.astype(f32).T, grad_pre)
    grad_gen_normed = dot_exact(grad_pre, gen_first.astype(f32).T)
    gain_gen = jnp.sum(grad_gen_normed * unit, axis=0)
    grad_unit = grad_gen_normed * gain_float[4]
    shared = jnp.mean(grad_unit * unit, axis=-1, keepdims=True)
    current_gen = half_of(inverse_rms * (grad_unit - unit * shared), 1, model_at)
    current_grad = rows_of("current_mix") + current_gen

    gain_own = sum(s["gain"] for s in saved)
    gain_other = other_core(gain_own)
    gain_all = jnp.where(
        model_at == 0,
        jnp.concatenate([gain_own, gain_other], axis=1),
        jnp.concatenate([gain_other, gain_own], axis=1),
    )
    gain_all = jnp.concatenate([gain_all, gain_gen[None]], axis=0)
    small_grads = jnp.concatenate(
        [grad_first, gain_all.T, jnp.zeros((model, 128 - GEN - 5), f32)], axis=1
    )
    small_grads = scatter_small(small_grads.reshape(-1, own_rows, 128), both)
    second_grads = jnp.pad(grad_second.reshape(-1, second_rows), ((0, 0), (0, second_pad)))
    second_grads = scatter_small(second_grads[:, None], both)

    return (
        rows_of("layer_rows"),
        history_grad,
        current_grad,
        small_grads[:, GEN : GEN + 5].T,
        small_grads[:, :GEN],
        second_grads[0, :second_rows],
        scattered[0],
        scattered[1],
        scattered[2],
        scattered[3].T,
        up_grad,
        down_grad,
    )


def solution(mesh):
    return jax.shard_map(
        local,
        mesh=mesh,
        in_specs=(
            P("depth", "dp", "mp"),
            P("depth"),
            P(("dp", "depth"), None),
            P(("dp", "depth")),
            P("dp"),
            P(("dp", "depth"), "mp"),
            P(None, ("dp", "depth")),
            P(("dp", "depth"), None),
            P(("dp", "depth")),
            P(("dp", "depth"), "mp"),
            P(("dp", "depth"), "mp"),
            P(("dp", "depth"), "mp"),
            P("mp", ("dp", "depth")),
            P(("dp", "depth"), "mp"),
            P("mp", ("dp", "depth")),
        ),
        out_specs=(
            P(("dp", "depth"), "mp"),
            P("depth", "dp", "mp"),
            P(("dp", "depth"), "mp"),
            P(None, ("dp", "depth")),
            P(("dp", "depth"), None),
            P(("dp", "depth")),
            P(("dp", "depth"), "mp"),
            P(("dp", "depth"), "mp"),
            P(("dp", "depth"), "mp"),
            P("mp", ("dp", "depth")),
            P(("dp", "depth"), "mp"),
            P("mp", ("dp", "depth")),
        ),
        check_vma=False,
    )
```

```python
import functools
import math

import jax
import jax.numpy as jnp
from jax import lax
from jax.experimental import pallas as pl
from jax.experimental.pallas import tpu as pltpu
from jax.sharding import PartitionSpec as P

HDIM = 128
ROT = 32
GEN = 72
MB = 2
MIX = 18
STREAMS = 4
COST = 20

PRECISE = lax.Precision.HIGHEST
NORM_EPSILON = 1e-05
RMS_EPSILON = 1e-06
MASKED = -1e30

bf16 = jnp.bfloat16
f32 = jnp.float32


def dot_nn(a, b):
    return lax.dot_general(a, b, (((1,), (0,)), ((), ())), preferred_element_type=f32)


def dot_nt(a, b):
    return lax.dot_general(a, b, (((1,), (1,)), ((), ())), preferred_element_type=f32)


def dot_tn(a, b):
    return lax.dot_general(a, b, (((0,), (0,)), ((), ())), preferred_element_type=f32)


def dot_exact(a, b):
    return jnp.dot(a, b, precision=PRECISE, preferred_element_type=f32)


def gelu_exact(values):
    return jax.nn.gelu(values, approximate=False)


def gelu_slope(values):
    result, pullback = jax.vjp(gelu_exact, values)
    return pullback(jnp.ones_like(result))[0]


def bit_count(size):
    count = size.bit_length() - 1
    assert 1 << count == size
    return count


def swap_mask(values, axis, mask):
    size = lax.axis_size(axis)
    return lax.ppermute(values, axis, [(i, i ^ mask) for i in range(size)])


def gather_masked(values, axis, order):
    pieces = {0: values}
    for bit in order:
        arrived = {m | (1 << bit): swap_mask(v, axis, 1 << bit) for m, v in pieces.items()}
        pieces.update(arrived)
    return [pieces[m] for m in range(len(pieces))]


def scatter_masked(pieces, axis, order, link=bf16):
    pieces = dict(enumerate(pieces))
    for bit in order:
        flag = 1 << bit
        for m in [m for m in pieces if m & flag]:
            arrived = swap_mask(pieces.pop(m).astype(link), axis, flag)
            pieces[m ^ flag] = pieces[m ^ flag].astype(f32) + arrived.astype(f32)
    return pieces[0]


def core_orders():
    bits = list(range(bit_count(lax.axis_size("dp"))))
    return bits, bits[1:] + bits[:1]


def place_mask(place):
    masks = []
    for order in core_orders():
        masks.append(sum(1 << bit for at, bit in enumerate(order) if (place >> at) & 1))
    return jnp.where(lax.axis_index("mp") % 2 == 0, masks[0], masks[1])


def place_index(place):
    return lax.axis_index("dp") ^ place_mask(place)


def core_hop(values, at):
    orders, cores = core_orders(), lax.axis_size("mp")
    pairs = []
    for i in range(lax.axis_size("dp")):
        for core in range(cores):
            partner = i ^ (1 << orders[core % 2][at])
            pairs.append((i * cores + core, partner * cores + core))
    return lax.ppermute(values, ("dp", "mp"), pairs)


def group_hop(pieces, at):
    return jnp.concatenate([pieces, core_hop(pieces, at)], axis=0)


def place_of(core):
    partner = jnp.arange(lax.axis_size("dp")) ^ lax.axis_index("dp")
    places = []
    for order in core_orders():
        places.append(sum(((partner >> bit) & 1) << at for at, bit in enumerate(order)))
    return jnp.where(core % 2 == 0, places[0], places[1])


def reorder_masked(stacked, axis):
    count = bit_count(stacked.shape[0])
    here = lax.axis_index(axis)
    shape = stacked.shape
    values = stacked.reshape((2,) * count + shape[1:])
    for bit in range(count):
        turned = jnp.flip(values, count - 1 - bit)
        values = jnp.where(((here >> bit) & 1) == 1, turned, values)
    return values.reshape(shape)


def gather_small(values, axes):
    shape = values.shape
    values = values[None]
    for axis in reversed(axes):
        order = range(bit_count(lax.axis_size(axis)))
        stacked = jnp.stack(gather_masked(values, axis, order))
        values = reorder_masked(stacked, axis)
        values = values.reshape((-1,) + shape)
    return values


def scatter_small(values, axes):
    for axis in axes:
        size = lax.axis_size(axis)
        values = values.reshape((size, values.shape[0] // size) + values.shape[1:])
        turned = reorder_masked(values, axis)
        order = reversed(range(bit_count(size)))
        values = scatter_masked([turned[m] for m in range(size)], axis, order, f32)
    return values[0]


def line_size():
    return lax.axis_size("depth"), lax.axis_index("depth")


def fence(*values):
    return lax.optimization_barrier(values)


class LineGather:

    def __init__(self, values):
        self.up, self.down = [values], [values]

    def step(self):
        size, _ = line_size()
        at = len(self.up)
        if at < size:
            up_pairs = [(i, i + 1) for i in range(at - 1, size - 1)]
            down_pairs = [(i, i - 1) for i in range(1, size - at + 1)]
            self.up.append(lax.ppermute(self.up[-1], "depth", up_pairs))
            self.down.append(lax.ppermute(self.down[-1], "depth", down_pairs))

    def hold(self, *others):
        kept = fence((self.up[1:], self.down[1:]), *others)
        (up, down), rest = kept[0], kept[1:]
        self.up, self.down = self.up[:1] + list(up), self.down[:1] + list(down)
        return rest

    def placed(self):
        size, here = line_size()
        steps = jnp.arange(size)
        index = lax.rem(here - steps + size, size)
        return place_line(index, here >= steps, self.up, self.down[1:][::-1])


class LineScatter:

    def __init__(self, terms):
        self.terms, self.at = terms, 0
        self.up = self.down = None

    def step(self, *later):
        size, here = line_size()
        self.at += 1
        if self.at >= size:
            return later
        goes_up, goes_down = hop_sums(
            self.terms,
            jnp.minimum(size - self.at + here, size - 1),
            jnp.maximum(here - size + self.at, 0),
            self.up,
            self.down,
        )
        (goes_up, goes_down), *later = fence((goes_up, goes_down), *later)
        up_pairs = [(i, i + 1) for i in range(min(self.at, size - 1))]
        down_pairs = [(size - 1 - i, size - 2 - i) for i in range(min(self.at, size - 1))]
        self.up = lax.ppermute(goes_up, "depth", up_pairs)
        self.down = lax.ppermute(goes_down, "depth", down_pairs)
        return later

    def hold(self, *others):
        (self.up, self.down), *rest = fence((self.up, self.down), *others)
        return rest


def other_core(values):
    return swap_mask(values, "mp", 1)


def join_kernel(model_ref, own_ref, other_ref, out_ref):
    width = own_ref.shape[1]
    own_at = pl.multiple_of(model_ref[0] * width, width)
    other_at = pl.multiple_of((1 - model_ref[0]) * width, width)
    out_ref[:, pl.ds(own_at, width)] = own_ref[...]
    out_ref[:, pl.ds(other_at, width)] = other_ref[...]


def join_halves(own, other, model_at):
    tall, width = own.shape
    rows = min(256, tall)
    return pl.pallas_call(
        join_kernel,
        grid_spec=pltpu.PrefetchScalarGridSpec(
            num_scalar_prefetch=1,
            grid=(tall // rows,),
            in_specs=[pl.BlockSpec((rows, width), lambda i, m: (i, 0))] * 2,
            out_specs=pl.BlockSpec((rows, 2 * width), lambda i, m: (i, 0)),
        ),
        out_shape=jax.ShapeDtypeStruct((tall, 2 * width), own.dtype),
        cost_estimate=spent(
            flops=0, bytes_accessed=8 * tall * width, transcendentals=0
        ),
        name="join_halves",
    )(model_at.astype(jnp.int32)[None], own, other)


def spent(flops, bytes_accessed, transcendentals):
    return pl.CostEstimate(
        flops=flops // COST, bytes_accessed=bytes_accessed // COST, transcendentals=transcendentals // COST
    )


def chunk_of(tall, wide):
    rows = tall
    while rows * wide > 1 << 19 and rows % 32 == 0:
        rows //= 2
    return rows


def place_kernel(at_ref, *refs):
    if len(refs) < 4:
        refs[-1][0, 0] = refs[0][0]
        return

    @pl.when(at_ref[1] == 1)
    def _():
        refs[-1][0, 0] = refs[0][0]

    @pl.when(at_ref[1] == 0)
    def _():
        refs[-1][0, 0] = refs[1][0]


def place_block(buffer, block, index, count, instead=None, first=None):
    lead, tall, wide = block.shape
    rows = chunk_of(tall, wide)
    spec = pl.BlockSpec((1, rows, wide), lambda l, i, m: (l, i, 0))
    blocks = [block] if instead is None else [block, instead]
    where = [index, 1 if first is None else first]
    where = jnp.stack([jnp.asarray(v).astype(jnp.int32) for v in where])
    in_specs, operands, aliases = [spec] * len(blocks), list(blocks), {}
    if buffer is not None or instead is not None:
        in_specs.append(pl.BlockSpec(memory_space=pl.ANY))
        operands.append(block if buffer is None else buffer)
        aliases = {} if buffer is None else {len(operands): 0}
    return pl.pallas_call(
        place_kernel,
        grid_spec=pltpu.PrefetchScalarGridSpec(
            num_scalar_prefetch=1,
            grid=(lead, tall // rows),
            in_specs=in_specs,
            out_specs=pl.BlockSpec((1, 1, rows, wide), lambda l, i, m: (l, m[0], i, 0)),
        ),
        out_shape=jax.ShapeDtypeStruct((lead, count, tall, wide), block.dtype),
        input_output_aliases=aliases,
        cost_estimate=spent(
            flops=0, bytes_accessed=4 * lead * tall * wide, transcendentals=0
        ),
        name="place_block",
    )(where, *operands)


def place_line_kernel(size, at_ref, *refs):
    out_ref = refs[-1]
    for step in range(size):
        if step == 0 or len(refs) == size + 1:
            out_ref[0, at_ref[step]] = refs[step][0]
            continue

        @pl.when(at_ref[size + step] == 1)
        def _(step=step):
            out_ref[0, at_ref[step]] = refs[step][0]

        @pl.when(at_ref[size + step] == 0)
        def _(step=step):
            out_ref[0, at_ref[step]] = refs[size + step - 1][0]


def place_line(index, first, blocks, instead):
    size = len(blocks)
    lead, tall, wide = blocks[0].shape
    rows = tall
    while rows * wide > 1 << 18 and rows % 32 == 0:
        rows //= 2
    spec = pl.BlockSpec((1, rows, wide), lambda l, i, m: (l, i, 0))
    where = jnp.concatenate([index, first]).astype(jnp.int32)
    operands = list(blocks) + list(instead)
    return pl.pallas_call(
        functools.partial(place_line_kernel, size),
        grid_spec=pltpu.PrefetchScalarGridSpec(
            num_scalar_prefetch=1,
            grid=(lead, tall // rows),
            in_specs=[spec] * len(operands),
            out_specs=pl.BlockSpec((1, size, rows, wide), lambda l, i, m: (l, 0, i, 0)),
        ),
        out_shape=jax.ShapeDtypeStruct((lead, size, tall, wide), blocks[0].dtype),
        compiler_params=pltpu.CompilerParams(vmem_limit_bytes=40 << 20),
        cost_estimate=spent(
            flops=0, bytes_accessed=6 * size * lead * tall * wide, transcendentals=0
        ),
        name="place_line",
    )(where, *operands)


def place_many(index, blocks):
    ones = jnp.ones(len(blocks), jnp.int32)
    return place_line(index, ones, blocks, [])


def group_join_kernel(at_ref, own_ref, other_ref, out_ref):
    width = own_ref.shape[2]
    own_span, other_span = own_spans(at_ref, width)
    out_ref[:, own_span] = own_ref[0]
    out_ref[:, other_span] = other_ref[0]


def group_join(own, other, model_at):
    count, tall, width = own.shape
    rows = chunk_of(tall, width)
    per = tall // rows
    where = jnp.concatenate([model_at[None], place_of(model_at), place_of(1 - model_at)])
    return pl.pallas_call(
        group_join_kernel,
        grid_spec=pltpu.PrefetchScalarGridSpec(
            num_scalar_prefetch=1,
            grid=(count, per),
            in_specs=[
                pl.BlockSpec((1, rows, width), lambda n, i, m: (m[1 + n], i, 0)),
                pl.BlockSpec((1, rows, width), lambda n, i, m: (m[1 + count + n], i, 0)),
            ],
            out_specs=pl.BlockSpec((rows, 2 * width), lambda n, i, m: (n * per + i, 0)),
        ),
        out_shape=jax.ShapeDtypeStruct((count * tall, 2 * width), own.dtype),
        cost_estimate=spent(
            flops=0, bytes_accessed=8 * count * tall * width, transcendentals=0
        ),
        name="group_join",
    )(where.astype(jnp.int32), own, other)


def group_split_kernel(at_ref, near_own, near_other, far_own, far_other, near_ref, far_ref):
    near_ref[0, 0] = near_own[0] + near_other[0].astype(f32)
    far_ref[0, 0] = (far_own[0] + far_other[0].astype(f32)).astype(bf16)


def group_split(own, other, places):
    _, tall, width = own.shape
    count = places.shape[0]
    half, rows = count // 2, tall // count
    near = pl.BlockSpec((1, rows, width), lambda p, k, m: (k, m[p], 0))
    far = pl.BlockSpec((1, rows, width), lambda p, k, m: (k, m[half + p], 0))
    out = pl.BlockSpec((1, 1, rows, width), lambda p, k, m: (p, k, 0, 0))
    return pl.pallas_call(
        group_split_kernel,
        grid_spec=pltpu.PrefetchScalarGridSpec(
            num_scalar_prefetch=1,
            grid=(half, 2),
            in_specs=[near, near, far, far],
            out_specs=[out, out],
        ),
        out_shape=[
            jax.ShapeDtypeStruct((half, 2, rows, width), f32),
            jax.ShapeDtypeStruct((half, 2, rows, width), bf16),
        ],
        cost_estimate=spent(
            flops=2 * tall * width, bytes_accessed=20 * tall * width, transcendentals=0
        ),
        name="group_split",
    )(places, own, other, own, other)


def hop_kernel(at_ref, *refs):
    ins, outs = refs[:-2], refs[-2:]
    for way in range(2):
        term = ins[way][0, 0].astype(f32)
        if len(ins) > 2:
            term = term + ins[2 + way][0].astype(f32)
        outs[way][0] = term.astype(bf16)


def hop_sums(terms, up_at, down_at, up, down):
    lead, _, tall, wide = terms.shape
    rows = chunk_of(tall, wide)
    block = pl.BlockSpec((1, rows, wide), lambda l, i, m: (l, i, 0))
    in_specs = [
        pl.BlockSpec((1, 1, rows, wide), lambda l, i, m: (l, m[0], i, 0)),
        pl.BlockSpec((1, 1, rows, wide), lambda l, i, m: (l, m[1], i, 0)),
    ]
    operands = [terms, terms]
    if up is not None:
        in_specs += [block, block]
        operands += [up, down]
    return pl.pallas_call(
        hop_kernel,
        grid_spec=pltpu.PrefetchScalarGridSpec(
            num_scalar_prefetch=1,
            grid=(lead, tall // rows),
            in_specs=in_specs,
            out_specs=[block, block],
        ),
        out_shape=[jax.ShapeDtypeStruct((lead, tall, wide), bf16)] * 2,
        cost_estimate=spent(
            flops=2 * lead * tall * wide, bytes_accessed=12 * lead * tall * wide, transcendentals=0
        ),
        name="hop_sums",
    )(jnp.stack([up_at, down_at]).astype(jnp.int32), *operands)


def end_kernel(at_ref, term_ref, up_ref, down_ref, out_ref):
    total = term_ref[0, 0].astype(f32) + up_ref[0].astype(f32) + down_ref[0].astype(f32)
    out_ref[0] = total.astype(out_ref.dtype)


def end_sums(sums, dtype):
    lead, _, tall, wide = sums.terms.shape
    rows = chunk_of(tall, wide)
    block = pl.BlockSpec((1, rows, wide), lambda l, i, m: (l, i, 0))
    return pl.pallas_call(
        end_kernel,
        grid_spec=pltpu.PrefetchScalarGridSpec(
            num_scalar_prefetch=1,
            grid=(lead, tall // rows),
            in_specs=[
                pl.BlockSpec((1, 1, rows, wide), lambda l, i, m: (l, m[0], i, 0)),
                block,
                block,
            ],
            out_specs=block,
        ),
        out_shape=jax.ShapeDtypeStruct((lead, tall, wide), dtype),
        cost_estimate=spent(
            flops=2 * lead * tall * wide, bytes_accessed=10 * lead * tall * wide, transcendentals=0
        ),
        name="end_sums",
    )(lax.axis_index("depth").astype(jnp.int32)[None], sums.terms, sums.up, sums.down)


def attention_grad_kernel(
    at_ref, x0_ref, x1_ref, cot_ref, g0_ref, g1_ref, out_ref
):
    tall = x0_ref.shape[1]

    def store(total):
        out_ref[...] = total.reshape(out_ref.shape).astype(out_ref.dtype)

    @pl.when(pl.program_id(0) < 3)
    def _():
        store(dot_tn(x0_ref[0], g0_ref[0]) + dot_tn(x1_ref[0], g1_ref[0]))

    @pl.when(pl.program_id(0) == 3)
    def _():
        store(
            dot_tn(cot_ref[0:tall, :], g0_ref[0]) + dot_tn(cot_ref[tall : 2 * tall, :], g1_ref[0])
        )


def attention_grads(normed, cot, flat, place, depth_count, dp_count, dtype):
    _, tall, model = normed[0].shape
    heads_width = flat[0].shape[2]
    block = model // dp_count
    own_rows = block // depth_count
    normed_spec = pl.BlockSpec((1, tall, block), lambda k, m: (jnp.minimum(k, 2), 0, m[0]))
    flat_spec = pl.BlockSpec((1, tall, heads_width), lambda k, m: (lax.rem(k + 1, 4), 0, 0))
    return pl.pallas_call(
        attention_grad_kernel,
        grid_spec=pltpu.PrefetchScalarGridSpec(
            num_scalar_prefetch=1,
            grid=(4,),
            in_specs=[
                normed_spec,
                normed_spec,
                pl.BlockSpec((2 * tall, block), lambda k, m: (0, m[0])),
                flat_spec,
                flat_spec,
            ],
            out_specs=pl.BlockSpec(
                (depth_count, 1, own_rows, heads_width), lambda k, m: (0, k, 0, 0)
            ),
        ),
        out_shape=jax.ShapeDtypeStruct((depth_count, 4, own_rows, heads_width), dtype),
        compiler_params=pltpu.CompilerParams(vmem_limit_bytes=40 << 20),
        cost_estimate=spent(
            flops=16 * tall * block * heads_width,
            bytes_accessed=16 * block * heads_width,
            transcendentals=0,
        ),
        name="attention_grads",
    )(place, *normed, cot, *flat)


def hidden_grad_kernel(x0_ref, x1_ref, c0_ref, c1_ref, u0_ref, u1_ref, h0_ref, h1_ref, out_ref):
    def store(total):
        out_ref[...] = total.reshape(out_ref.shape)

    @pl.when(pl.program_id(0) == 0)
    def _():
        store(dot_tn(x0_ref[...], u0_ref[...]) + dot_tn(x1_ref[...], u1_ref[...]))

    @pl.when(pl.program_id(0) == 1)
    def _():
        tall, wide = h0_ref.shape[0], c0_ref.shape[3]
        c0, c1 = c0_ref[:, 0].reshape(tall, wide), c1_ref[:, 0].reshape(tall, wide)
        store(dot_tn(c0, h0_ref[...]) + dot_tn(c1, h1_ref[...]))


def hidden_grads(x, cot, up_grads, hidden, dp_count, depth_count):
    tall, model = x[0].shape
    part = hidden[0].shape[1]
    block = model // dp_count
    cols = pl.BlockSpec((tall, block), lambda k, n: (0, n * (1 - k)))
    whole = pl.BlockSpec((tall, part), lambda k, n: (0, 0))
    return pl.pallas_call(
        hidden_grad_kernel,
        grid=(2, dp_count),
        in_specs=[cols, cols]
        + [
            pl.BlockSpec((dp_count, 1, cot.shape[2], block), lambda k, n: (0, 0, 0, n * k)),
            pl.BlockSpec((dp_count, 1, cot.shape[2], block), lambda k, n: (0, 1, 0, n * k)),
        ]
        + [whole] * 4,
        out_specs=pl.BlockSpec(
            (1, depth_count, block // depth_count, part), lambda k, n: (k * dp_count + n, 0, 0, 0)
        ),
        out_shape=jax.ShapeDtypeStruct(
            (2 * dp_count, depth_count, block // depth_count, part), f32
        ),
        compiler_params=pltpu.CompilerParams(vmem_limit_bytes=48 << 20),
        cost_estimate=spent(
            flops=8 * tall * model * part, bytes_accessed=8 * model * part, transcendentals=0
        ),
        name="hidden_grads",
    )(*x, cot, cot, *up_grads, *hidden)


def mix_kernel(slots, mix_ref, hist_ref, out_ref):
    rows, width = hist_ref.shape[1], hist_ref.shape[2]
    part = 512 if width % 512 == 0 else width

    def step(at, carry):
        r0 = pl.multiple_of(at * 16, 16)
        weights = mix_ref[pl.ds(r0, 16), :]
        for c0 in range(0, width, part):
            sums = [None] * STREAMS
            for k in range(slots):
                state = hist_ref[k, pl.ds(r0, 16), c0 : c0 + part].astype(f32)
                for s in range(STREAMS):
                    term = weights[:, s * slots + k : s * slots + k + 1] * state
                    sums[s] = term if sums[s] is None else sums[s] + term
            for s in range(STREAMS):
                out_ref[pl.ds(r0, 16), s * width + c0 : s * width + c0 + part] = sums[s].astype(bf16)
        return carry

    lax.fori_loop(0, rows // 16, step, 0)


def mix_streams(slot_mix, history, micro_at, depth_count, rows_mb):
    slots, _, width = history.shape
    rows = min(128, rows_mb)
    per = rows_mb // rows

    def row_block(i):
        return ((i // per) * MB + micro_at) * per + i % per

    return pl.pallas_call(
        functools.partial(mix_kernel, slots),
        grid=(depth_count * per,),
        in_specs=[
            pl.BlockSpec((rows, slot_mix.shape[1]), lambda i: (row_block(i), 0)),
            pl.BlockSpec((slots, rows, width), lambda i: (0, row_block(i), 0)),
        ],
        out_specs=pl.BlockSpec((rows, STREAMS * width), lambda i: (i, 0)),
        out_shape=jax.ShapeDtypeStruct((depth_count * rows_mb, STREAMS * width), bf16),
        cost_estimate=spent(
            flops=2 * slots * STREAMS * depth_count * rows_mb * width,
            bytes_accessed=2 * (slots + STREAMS) * depth_count * rows_mb * width,
            transcendentals=0,
        ),
        name="mix_streams",
    )(slot_mix, history)


def unmix_kernel(slots, mix_ref, hist_ref, grad_ref, *rest):
    hist_grad_ref, slot_grad_ref = rest[-2:]
    rows, width = hist_ref.shape[1], hist_ref.shape[2]
    part = 512 if width % 512 == 0 else width

    def step(at, carry):
        r0 = pl.multiple_of(at * 16, 16)
        weights = mix_ref[pl.ds(r0, 16), :]
        totals = [None] * (STREAMS * slots)
        for c0 in range(0, width, part):
            grads = [
                grad_ref[pl.ds(r0, 16), s * width + c0 : s * width + c0 + part].astype(f32)
                for s in range(STREAMS)
            ]
            for k in range(slots):
                state = hist_ref[k, pl.ds(r0, 16), c0 : c0 + part].astype(f32)
                back = None
                for s in range(STREAMS):
                    at_sk = s * slots + k
                    term = weights[:, at_sk : at_sk + 1] * grads[s]
                    back = term if back is None else back + term
                    product = state * grads[s]
                    folded = product[:, 0:128]
                    for l0 in range(128, part, 128):
                        folded = folded + product[:, l0 : l0 + 128]
                    totals[at_sk] = folded if totals[at_sk] is None else totals[at_sk] + folded
                hist_grad_ref[k, pl.ds(r0, 16), c0 : c0 + part] = back.astype(bf16)
        lane = lax.broadcasted_iota(jnp.int32, (16, 128), 1)
        packed = jnp.zeros((16, 128), f32)
        for at_sk in range(STREAMS * slots):
            column = jnp.sum(totals[at_sk], axis=1, keepdims=True)
            packed = jnp.where(lane == at_sk, column, packed)
        slot_grad_ref[pl.ds(r0, 16), :] = packed
        return carry

    lax.fori_loop(0, rows // 16, step, 0)


def unmix_streams(slot_mix, history, grads, micro_at, depth_count, rows_mb, earlier):
    slots, tokens, width = history.shape
    rows = min(128, rows_mb)
    per = rows_mb // rows

    def row_block(i):
        return ((i // per) * MB + micro_at) * per + i % per

    in_specs = [
        pl.BlockSpec((rows, slot_mix.shape[1]), lambda i: (row_block(i), 0)),
        pl.BlockSpec((slots, rows, width), lambda i: (0, row_block(i), 0)),
        pl.BlockSpec((rows, STREAMS * width), lambda i: (i, 0)),
    ]
    operands = [slot_mix, history, grads]
    aliases = {}
    if earlier is not None:
        in_specs.append(pl.BlockSpec(memory_space=pl.ANY))
        operands.append(earlier)
        aliases = {3: 0}
    return pl.pallas_call(
        functools.partial(unmix_kernel, slots),
        grid=(depth_count * per,),
        in_specs=in_specs,
        out_specs=[
            pl.BlockSpec((slots, rows, width), lambda i: (0, row_block(i), 0)),
            pl.BlockSpec((rows, 128), lambda i: (i, 0)),
        ],
        out_shape=[
            jax.ShapeDtypeStruct((slots, tokens, width), bf16),
            jax.ShapeDtypeStruct((depth_count * rows_mb, 128), f32),
        ],
        input_output_aliases=aliases,
        cost_estimate=spent(
            flops=4 * slots * STREAMS * depth_count * rows_mb * width,
            bytes_accessed=2 * (2 * slots + STREAMS) * depth_count * rows_mb * width,
            transcendentals=0,
        ),
        name="unmix_streams",
    )(*operands)


def own_spans(model_ref, width):
    own_at = pl.multiple_of(model_ref[0] * width, width)
    other_at = pl.multiple_of((1 - model_ref[0]) * width, width)
    return pl.ds(own_at, width), pl.ds(other_at, width)


def ff_split_kernel(at_ref, up_ref, down_ref, out_ref):
    out_ref[0, 0] = up_ref[...]
    out_ref[0, 1] = down_ref[...].T


def ff_split(up_weight, down_weight, partners):
    own_rows, ff_width = up_weight.shape
    count = partners.shape[0]
    part = ff_width // count
    return pl.pallas_call(
        ff_split_kernel,
        grid_spec=pltpu.PrefetchScalarGridSpec(
            num_scalar_prefetch=1,
            grid=(count,),
            in_specs=[
                pl.BlockSpec((own_rows, part), lambda i, m: (0, m[i])),
                pl.BlockSpec((part, own_rows), lambda i, m: (m[i], 0)),
            ],
            out_specs=pl.BlockSpec((1, 2, own_rows, part), lambda i, m: (i, 0, 0, 0)),
        ),
        out_shape=jax.ShapeDtypeStruct((count, 2, own_rows, part), bf16),
        cost_estimate=spent(flops=0, bytes_accessed=8 * own_rows * ff_width, transcendentals=0),
        name="ff_split",
    )(partners, up_weight, down_weight)


def ff_join_kernel(at_ref, piece_ref, up_ref, down_ref):
    up_ref[...] = piece_ref[0, 0].astype(f32)
    down_ref[...] = piece_ref[0, 1].astype(f32).T


def ff_join(pieces, partners):
    count, _, own_rows, part = pieces.shape
    return pl.pallas_call(
        ff_join_kernel,
        grid_spec=pltpu.PrefetchScalarGridSpec(
            num_scalar_prefetch=1,
            grid=(count,),
            in_specs=[pl.BlockSpec((1, 2, own_rows, part), lambda i, m: (i, 0, 0, 0))],
            out_specs=[
                pl.BlockSpec((own_rows, part), lambda i, m: (0, m[i])),
                pl.BlockSpec((part, own_rows), lambda i, m: (m[i], 0)),
            ],
        ),
        out_shape=[
            jax.ShapeDtypeStruct((own_rows, count * part), f32),
            jax.ShapeDtypeStruct((count * part, own_rows), f32),
        ],
        cost_estimate=spent(
            flops=0, bytes_accessed=12 * own_rows * count * part, transcendentals=0
        ),
        name="ff_join",
    )(partners, pieces)


def total_kernel(depth_ref, part_ref, up_ref, down_ref, cur_ref, last_ref, low_ref, resid_ref):
    width = resid_ref.shape[1]
    current = cur_ref[...].astype(f32)
    for s in range(STREAMS):
        lanes = slice(s * width, (s + 1) * width)
        total = part_ref[0, 0, :, lanes].astype(f32)
        total = total + up_ref[0, :, lanes].astype(f32) + down_ref[0, :, lanes].astype(f32)
        total = total + last_ref[:, s : s + 1] * current
        if s == STREAMS - 1:
            resid_ref[...] = total
        low_ref[:, lanes] = total.astype(bf16)


def total_streams(sums, current_half, last, depth_at):
    _, _, tall, wide = sums.terms.shape
    width = wide // STREAMS
    rows = min(64, tall)
    row = lambda i, d: (i, 0)
    return pl.pallas_call(
        total_kernel,
        grid_spec=pltpu.PrefetchScalarGridSpec(
            num_scalar_prefetch=1,
            grid=(tall // rows,),
            in_specs=[
                pl.BlockSpec((1, 1, rows, wide), lambda i, d: (0, d[0], i, 0)),
                pl.BlockSpec((1, rows, wide), lambda i, d: (0, i, 0)),
                pl.BlockSpec((1, rows, wide), lambda i, d: (0, i, 0)),
                pl.BlockSpec((rows, width), row),
                pl.BlockSpec((rows, 128), row),
            ],
            out_specs=[pl.BlockSpec((rows, wide), row), pl.BlockSpec((rows, width), row)],
        ),
        out_shape=[
            jax.ShapeDtypeStruct((tall, wide), bf16),
            jax.ShapeDtypeStruct((tall, width), f32),
        ],
        cost_estimate=spent(flops=5 * tall * wide, bytes_accessed=9 * tall * wide, transcendentals=0),
        name="total_streams",
    )(depth_at, sums.terms, sums.up, sums.down, current_half, last)


def norm_kernel(model_ref, own_ref, other_ref, gain_ref, normed_ref, ff_ref, stat_ref):
    rows, width = ff_ref.shape
    model = 2 * width
    own_span, other_span = own_spans(model_ref, width)
    lane = lax.broadcasted_iota(jnp.int32, (rows, 128), 1)
    stats = jnp.zeros((rows, 128), f32)
    for s in range(STREAMS):
        lanes = slice(s * width, (s + 1) * width)
        own = own_ref[:, lanes].astype(f32)
        other = other_ref[:, lanes].astype(f32)
        average = (
            jnp.sum(own, axis=-1, keepdims=True) + jnp.sum(other, axis=-1, keepdims=True)
        ) / model
        own, other = own - average, other - average
        variance = (
            jnp.sum(own * own, axis=-1, keepdims=True)
            + jnp.sum(other * other, axis=-1, keepdims=True)
        ) / model
        inverse = lax.rsqrt(variance + NORM_EPSILON)
        stats = jnp.where(lane == 2 * s, average, stats)
        stats = jnp.where(lane == 2 * s + 1, inverse, stats)
        norm_own = (own * inverse * gain_ref[s : s + 1, own_span]).astype(bf16)
        if s == STREAMS - 1:
            ff_ref[...] = norm_own
        else:
            normed_ref[s, :, own_span] = norm_own
            norm_other = (other * inverse * gain_ref[s : s + 1, other_span]).astype(bf16)
            normed_ref[s, :, other_span] = norm_other
    stat_ref[...] = stats


def norm_streams(low, low_other, gains, which):
    tall, wide = low.shape
    width = wide // STREAMS
    rows = min(64, tall)
    row = lambda i, m: (i, 0)
    return pl.pallas_call(
        norm_kernel,
        grid_spec=pltpu.PrefetchScalarGridSpec(
            num_scalar_prefetch=1,
            grid=(tall // rows,),
            in_specs=[
                pl.BlockSpec((rows, wide), row),
                pl.BlockSpec((rows, wide), row),
                pl.BlockSpec(gains.shape, lambda i, m: (0, 0)),
            ],
            out_specs=[
                pl.BlockSpec((3, rows, 2 * width), lambda i, m: (0, i, 0)),
                pl.BlockSpec((rows, width), row),
                pl.BlockSpec((rows, 128), row),
            ],
        ),
        out_shape=[
            jax.ShapeDtypeStruct((3, tall, 2 * width), bf16),
            jax.ShapeDtypeStruct((tall, width), bf16),
            jax.ShapeDtypeStruct((tall, 128), f32),
        ],
        cost_estimate=spent(
            flops=20 * tall * wide, bytes_accessed=8 * tall * wide, transcendentals=0
        ),
        name="norm_streams",
    )(which, low, low_other, gains)


def turn(values, cosine, sine_up, sine_down, sign):
    up = pltpu.roll(values, HDIM - ROT // 2, 1)
    down = pltpu.roll(values, ROT // 2, 1)
    return values * cosine + sign * (up * sine_up + down * sine_down)


def project_kernel(
    x_ref, cot_ref, wq_ref, wk_ref, wv_ref, wo_ref, cos_ref, up_ref, down_ref, out_ref
):
    span = wq_ref.shape[-1]
    tables = cos_ref[...], up_ref[...], down_ref[...]
    for kind, w_ref in enumerate((wq_ref, wk_ref, wv_ref, wo_ref)):
        rows = cot_ref[...] if kind == 3 else x_ref[kind]
        product = dot_nn(rows, w_ref[...].reshape(-1, span))
        for begin in range(0, span, HDIM):
            head = product[:, begin : begin + HDIM]
            if kind < 2:
                head = turn(head, *tables, 1.0)
            out_ref[0, :, kind * span + begin : kind * span + begin + HDIM] = head.astype(bf16)


def project_heads(normed, cot, weights, tables, depth_count):
    _, rows, model = normed.shape
    groups, _, _, own_rows, heads_width = weights.shape
    span = heads_width // depth_count
    whole = lambda j: (0, 0)

    def matrix(kind):
        shape = (groups, depth_count, 1, own_rows, span)
        return pl.BlockSpec(shape, lambda j: (0, 0, kind, 0, j))

    return pl.pallas_call(
        project_kernel,
        grid=(depth_count,),
        in_specs=[
            pl.BlockSpec((3, rows, model), lambda j: (0, 0, 0)),
            pl.BlockSpec((rows, model), whole),
        ]
        + [matrix(kind) for kind in range(4)]
        + [pl.BlockSpec((rows, HDIM), whole)] * 3,
        out_specs=pl.BlockSpec((1, rows, 4 * span), lambda j: (j, 0, 0)),
        out_shape=jax.ShapeDtypeStruct((depth_count, rows, 4 * span), bf16),
        compiler_params=pltpu.CompilerParams(vmem_limit_bytes=40 << 20),
        cost_estimate=spent(
            flops=8 * rows * model * span * depth_count,
            bytes_accessed=8 * model * span * depth_count + 8 * rows * model,
            transcendentals=0,
        ),
        name="project_heads",
    )(normed, cot, *[weights] * 4, *tables)


def attend_kernel(
    block, q_ref, k_ref, v_ref, g_ref, doc_col_ref, doc_row_ref, cos_ref, up_ref, down_ref,
    out_ref, dk_sum, dv_sum,
):
    length = q_ref.shape[0]
    scale = HDIM**-0.5
    heads_each = out_ref.shape[1] // (4 * HDIM)

    def lanes(kind):
        return pl.ds(pl.multiple_of((kind * heads_each + pl.program_id(0)) * HDIM, HDIM), HDIM)

    for begin in range(0, length, block):
        end = begin + block
        rows = slice(begin, end)
        queries, grads = q_ref[rows, :], g_ref[rows, :]
        keys, values = k_ref[0:end, :], v_ref[0:end, :]
        scores = dot_nt(queries, keys) * scale
        place_q = begin + lax.broadcasted_iota(jnp.int32, scores.shape, 0)
        place_k = lax.broadcasted_iota(jnp.int32, scores.shape, 1)
        allowed = (doc_col_ref[rows, :] == doc_row_ref[:, 0:end]) & (place_q >= place_k)
        scores = jnp.where(allowed, scores, MASKED)
        highest = jnp.max(scores, axis=-1, keepdims=True)
        exponent = jnp.exp(scores - highest)
        totals = jnp.sum(exponent, axis=-1, keepdims=True)
        attention = exponent * (1.0 / totals)
        low = attention.astype(bf16)
        out_ref[rows, lanes(0)] = dot_nn(low, values).astype(bf16)
        grad_att = dot_nt(grads, values).astype(bf16).astype(f32)
        weighted = jnp.sum(attention * grad_att, axis=-1, keepdims=True)
        grad_scores = (attention * (grad_att - weighted)).astype(bf16)
        grad_q = dot_nn(grad_scores, keys) * scale
        out_ref[rows, lanes(1)] = turn(
            grad_q, cos_ref[rows, :], up_ref[rows, :], down_ref[rows, :], -1.0
        ).astype(bf16)
        part_k = dot_tn(grad_scores, queries)
        part_v = dot_tn(low, grads)
        if begin > 0:
            dk_sum[0:begin, :] += part_k[0:begin]
            dv_sum[0:begin, :] += part_v[0:begin]
        dk_sum[begin:end, :] = part_k[begin:end]
        dv_sum[begin:end, :] = part_v[begin:end]
    grad_k = dk_sum[...] * scale
    out_ref[:, lanes(2)] = turn(grad_k, cos_ref[...], up_ref[...], down_ref[...], -1.0).astype(bf16)
    out_ref[:, lanes(3)] = dv_sum[...].astype(bf16)


def attend(packed, documents, tables, heads_each):
    length = packed.shape[0]
    block = min(256, length)
    whole = lambda h: (0, 0)

    def kind(at):
        return pl.BlockSpec((length, HDIM), lambda h: (0, at * heads_each + h))

    return pl.pallas_call(
        functools.partial(attend_kernel, block),
        grid=(heads_each,),
        in_specs=[kind(0), kind(1), kind(2), kind(3)]
        + [pl.BlockSpec((length, 1), whole), pl.BlockSpec((1, length), whole)]
        + [pl.BlockSpec((length, HDIM), whole)] * 3,
        out_specs=pl.BlockSpec((length, 4 * heads_each * HDIM), whole),
        out_shape=jax.ShapeDtypeStruct((length, 4 * heads_each * HDIM), bf16),
        scratch_shapes=[pltpu.VMEM((length, HDIM), f32)] * 2,
        compiler_params=pltpu.CompilerParams(vmem_limit_bytes=48 << 20),
        cost_estimate=spent(
            flops=9 * heads_each * length * length * HDIM,
            bytes_accessed=16 * length * heads_each * HDIM + 12 * length * HDIM,
            transcendentals=heads_each * length * length,
        ),
        name="attend",
    )(packed, packed, packed, packed, documents[:, None], documents[None, :], *tables)


def gelu_parts(values):
    cdf = 0.5 * (1.0 + lax.erf(values * (0.5**0.5)))
    density = jnp.exp(-0.5 * values * values) * (1.0 / math.sqrt(2.0 * math.pi))
    return values * cdf, cdf + values * density


def ff_kernel(
    model_ref, x_ref, cot_ref, up_ref, down_ref,
    hidden_ref, grad_ref, own_ref, other_ref,
):
    part = up_ref.shape[-1]
    half = up_ref.shape[1] // 2

    def rows_of(ref, which):
        return ref[0, pl.ds(which * half, half)].reshape(-1, part)

    own, other = model_ref[0], 1 - model_ref[0]
    up_pre = dot_nn(x_ref[...], up_ref[...].reshape(-1, part))
    hidden, slope = gelu_parts(up_pre)
    hidden = hidden.astype(bf16)
    grad_up = (dot_nn(cot_ref[0, 0], down_ref[...].reshape(-1, part)) * slope).astype(bf16)
    hidden_ref[...] = hidden
    grad_ref[...] = grad_up
    other_ref[0] = dot_nt(grad_up, rows_of(up_ref, other)).astype(bf16)
    own_ref[0] = dot_nt(grad_up, rows_of(up_ref, own))
    other_ref[1] = dot_nt(hidden, rows_of(down_ref, other)).astype(bf16)
    own_ref[1] = dot_nt(hidden, rows_of(down_ref, own))


def feed_forward(x, cot, micro_at, weights, which):
    tall, model = x.shape
    part = weights.shape[-1]
    width = model // 2
    rows = cot.shape[2]
    row = lambda i, m: (i, 0)

    def resident(kind):
        return pl.BlockSpec(
            (1,) + weights.shape[1:],
            lambda i, m: (kind, 0, 0, 0, 0),
            pipeline_mode=pl.Buffered(1),
        )

    return pl.pallas_call(
        ff_kernel,
        grid_spec=pltpu.PrefetchScalarGridSpec(
            num_scalar_prefetch=1,
            grid=(tall // rows,),
            in_specs=[
                pl.BlockSpec((rows, model), row),
                pl.BlockSpec((1, 1, rows, model), lambda i, m: (i, micro_at, 0, 0)),
                resident(0),
                resident(1),
            ],
            out_specs=[pl.BlockSpec((rows, part), row)] * 2
            + [pl.BlockSpec((2, rows, width), lambda i, m: (0, i, 0))] * 2,
        ),
        out_shape=[jax.ShapeDtypeStruct((tall, part), bf16)] * 2
        + [
            jax.ShapeDtypeStruct((2, tall, width), f32),
            jax.ShapeDtypeStruct((2, tall, width), bf16),
        ],
        compiler_params=pltpu.CompilerParams(vmem_limit_bytes=48 << 20),
        cost_estimate=spent(
            flops=8 * tall * model * part,
            bytes_accessed=4 * model * part + 16 * tall * model,
            transcendentals=2 * tall * part,
        ),
        name="feed_forward",
    )(which, x, cot, weights, weights)


def back_kernel(half_ref, ans_ref, wo_ref, wq_ref, wk_ref, wv_ref, out_ref, *flat):
    count, _, wide = ans_ref.shape
    span = wide // 4
    for kind, w_ref in enumerate((wo_ref, wq_ref, wk_ref, wv_ref)):
        total = None
        for j in range(count):
            term = dot_nt(
                ans_ref[j, :, kind * span : (kind + 1) * span],
                w_ref[:, :, :, :, j * span : (j + 1) * span].reshape(-1, span),
            )
            total = term if total is None else total + term
        out_ref[kind] = total.astype(out_ref.dtype)
    if flat:

        @pl.when(pl.program_id(0) == 0)
        def _():
            for kind in range(4):
                for j in range(count):
                    flat[0][kind, :, j * span : (j + 1) * span] = ans_ref[
                        j, :, kind * span : (kind + 1) * span
                    ]


def back_project(answer, weights, half, dtype, flat):
    count, rows, wide = answer.shape
    groups, _, _, own_rows, heads_width = weights.shape
    part = count * own_rows
    steps = groups // 2
    width = part * steps

    def matrix(kind):
        shape = (1, count, 1, own_rows, heads_width)
        return pl.BlockSpec(shape, lambda i, m: (m[0] * steps + i, 0, kind, 0, 0))

    out_specs = [pl.BlockSpec((4, rows, part), lambda i, m: (0, 0, i))]
    out_shape = [jax.ShapeDtypeStruct((4, rows, width), dtype)]
    if flat:
        out_specs.append(pl.BlockSpec((4, rows, heads_width), lambda i, m: (0, 0, 0)))
        out_shape.append(jax.ShapeDtypeStruct((4, rows, heads_width), bf16))
    return pl.pallas_call(
        back_kernel,
        grid_spec=pltpu.PrefetchScalarGridSpec(
            num_scalar_prefetch=1,
            grid=(steps,),
            in_specs=[pl.BlockSpec((count, rows, wide), lambda i, m: (0, 0, 0))]
            + [matrix(kind) for kind in (3, 0, 1, 2)],
            out_specs=out_specs,
        ),
        out_shape=out_shape,
        compiler_params=pltpu.CompilerParams(vmem_limit_bytes=40 << 20),
        cost_estimate=spent(
            flops=8 * rows * heads_width * width,
            bytes_accessed=8 * heads_width * width + 20 * rows * width,
            transcendentals=0,
        ),
        name="back_project",
    )(half, answer, *[weights] * 4)


def slope_kernel(
    model_ref, own_ref, got_ref, ff_ref, low_ref, stat_ref, gain_ref, scaled_ref, sum_ref, gain_out_ref
):
    _, rows, width = ff_ref.shape
    own_span, _ = own_spans(model_ref, width)
    lane = lax.broadcasted_iota(jnp.int32, (rows, 128), 1)
    packed = jnp.zeros((rows, 128), f32)
    totals = []
    for s in range(STREAMS):
        lanes = slice(s * width, (s + 1) * width)
        if s < 3:
            grad = own_ref[s + 1] + got_ref[s + 1].astype(f32)
        else:
            grad = ff_ref[0]
        average, inverse = stat_ref[:, 2 * s : 2 * s + 1], stat_ref[:, 2 * s + 1 : 2 * s + 2]
        hat = (low_ref[:, lanes].astype(f32) - average) * inverse
        totals.append(jnp.sum(grad * hat, axis=0, keepdims=True))
        scaled = grad * gain_ref[s : s + 1, own_span]
        scaled_ref[:, lanes] = scaled
        packed = jnp.where(lane == 2 * s, jnp.sum(scaled, axis=-1, keepdims=True), packed)
        packed = jnp.where(
            lane == 2 * s + 1, jnp.sum(scaled * hat, axis=-1, keepdims=True), packed
        )
    sum_ref[...] = packed
    totals = jnp.concatenate(totals, axis=0)

    @pl.when(pl.program_id(0) == 0)
    def _():
        gain_out_ref[...] = totals

    @pl.when(pl.program_id(0) > 0)
    def _():
        gain_out_ref[...] += totals


def norm_slopes(own, got, ff_grad, low, stats, gains, which):
    tall, wide = low.shape
    width = wide // STREAMS
    rows = min(64, tall)
    row = lambda i, m: (i, 0)
    cube = pl.BlockSpec((4, rows, width), lambda i, m: (0, i, 0))
    return pl.pallas_call(
        slope_kernel,
        grid_spec=pltpu.PrefetchScalarGridSpec(
            num_scalar_prefetch=1,
            grid=(tall // rows,),
            in_specs=[
                cube,
                cube,
                pl.BlockSpec((1, rows, width), lambda i, m: (0, i, 0)),
                pl.BlockSpec((rows, wide), row),
                pl.BlockSpec((rows, 128), row),
                pl.BlockSpec(gains.shape, lambda i, m: (0, 0)),
            ],
            out_specs=[
                pl.BlockSpec((rows, wide), row),
                pl.BlockSpec((rows, 128), row),
                pl.BlockSpec((STREAMS, width), lambda i, m: (0, 0)),
            ],
        ),
        out_shape=[
            jax.ShapeDtypeStruct((tall, wide), f32),
            jax.ShapeDtypeStruct((tall, 128), f32),
            jax.ShapeDtypeStruct((STREAMS, width), f32),
        ],
        cost_estimate=spent(
            flops=12 * tall * wide, bytes_accessed=12 * tall * wide, transcendentals=0
        ),
        name="norm_slopes",
    )(which, own, got, ff_grad, low, stats, gains)


def grads_kernel(
    scaled_ref, mine_ref, theirs_ref, low_ref, stat_ref, cot_ref, cur_ref, last_ref,
    grad_ref, mix_ref, dot_ref,
):
    rows, width = cot_ref.shape
    lane = lax.broadcasted_iota(jnp.int32, (rows, 128), 1)
    means = (mine_ref[...] + theirs_ref[...]) / (2 * width)
    current = cur_ref[...].astype(f32)
    packed = jnp.zeros((rows, 128), f32)
    mixed = None
    for s in range(STREAMS):
        lanes = slice(s * width, (s + 1) * width)
        average, inverse = stat_ref[:, 2 * s : 2 * s + 1], stat_ref[:, 2 * s + 1 : 2 * s + 2]
        hat = (low_ref[:, lanes].astype(f32) - average) * inverse
        grad = inverse * (
            scaled_ref[:, lanes]
            - means[:, 2 * s : 2 * s + 1]
            - hat * means[:, 2 * s + 1 : 2 * s + 2]
        )
        if s == STREAMS - 1:
            grad = grad + cot_ref[...].astype(f32)
        grad = grad.astype(bf16)
        grad_ref[:, lanes] = grad
        grad = grad.astype(f32)
        term = last_ref[:, s : s + 1] * grad
        mixed = term if mixed is None else mixed + term
        packed = jnp.where(lane == s, jnp.sum(grad * current, axis=-1, keepdims=True), packed)
    mix_ref[...] = mixed
    dot_ref[...] = packed


def stream_grads(scaled, mine, theirs, low, stats, cot, current_half, last):
    tall, wide = low.shape
    width = wide // STREAMS
    rows = min(64, tall)
    row = lambda i: (i, 0)
    return pl.pallas_call(
        grads_kernel,
        grid=(tall // rows,),
        in_specs=[
            pl.BlockSpec((rows, wide), row),
            pl.BlockSpec((rows, 128), row),
            pl.BlockSpec((rows, 128), row),
            pl.BlockSpec((rows, wide), row),
            pl.BlockSpec((rows, 128), row),
            pl.BlockSpec((rows, width), row),
            pl.BlockSpec((rows, width), row),
            pl.BlockSpec((rows, 128), row),
        ],
        out_specs=[
            pl.BlockSpec((rows, wide), row),
            pl.BlockSpec((rows, width), row),
            pl.BlockSpec((rows, 128), row),
        ],
        out_shape=[
            jax.ShapeDtypeStruct((tall, wide), bf16),
            jax.ShapeDtypeStruct((tall, width), f32),
            jax.ShapeDtypeStruct((tall, 128), f32),
        ],
        cost_estimate=spent(
            flops=12 * tall * wide, bytes_accessed=10 * tall * wide, transcendentals=0
        ),
        name="stream_grads",
    )(scaled, mine, theirs, low, stats, cot, current_half, last)


def turning_tables(places):
    half = ROT // 2
    inverse = jnp.exp(jnp.arange(half, dtype=f32) * (-2.0 * math.log(10000.0) / ROT))
    angles = places.astype(f32)[:, None] * inverse[None, :]
    cosine, sine = jnp.cos(angles), jnp.sin(angles)
    rows = places.shape[0]
    rest = jnp.zeros((rows, HDIM - ROT), f32)
    blank = jnp.zeros((rows, half), f32)
    return (
        jnp.concatenate([cosine, cosine, rest + 1.0], axis=1),
        jnp.concatenate([-sine, blank, rest], axis=1),
        jnp.concatenate([blank, sine, rest], axis=1),
    )


def local(
    history,
    slot_layer,
    current,
    positions,
    doc_ids,
    cotangent,
    norm_gains,
    generator_in,
    generator_out,
    query_weight,
    key_weight,
    value_weight,
    out_weight,
    up_weight,
    down_weight,
):
    dp_count = lax.axis_size("dp")
    depth_count = lax.axis_size("depth")
    dp_at = lax.axis_index("dp")
    model_at = lax.axis_index("mp")
    dp_bits = list(range(bit_count(dp_count)))
    slots, tokens_held, width = history.shape
    model = current.shape[1]
    rows_mb = current.shape[0] // MB
    length = depth_count * rows_mb
    heads_width = query_weight.shape[1]
    heads_each = heads_width // HDIM // depth_count
    own_rows = query_weight.shape[0]
    ff_width = up_weight.shape[1]
    ff_part = ff_width // dp_count
    both = ("dp", "depth")

    def half_of(values, axis, which):
        return lax.dynamic_slice_in_dim(values, which * width, width, axis)

    partners = jnp.stack([dp_at ^ m for m in range(dp_count)]).astype(jnp.int32)
    ff_local = ff_split(up_weight, down_weight, partners)
    ff_rows = [ff_local[0]] + [swap_mask(ff_local[m], "dp", m) for m in range(1, dp_count)]
    ff_rows = place_many(partners, ff_rows).reshape(2 * dp_count, own_rows, ff_part)

    small_cols = jnp.concatenate(
        [generator_in, norm_gains.T, jnp.zeros((own_rows, 128 - GEN - 5), bf16)], axis=1
    )
    small_all = gather_small(small_cols, both).reshape(model, 128)
    gen_first = small_all[:, :GEN]
    gen_first, ff_rows = fence(gen_first, ff_rows)
    gain_float = small_all[:, GEN : GEN + 5].astype(f32).T
    second_rows = generator_out.shape[0]
    second_pad = -second_rows % 128
    second_all = gather_small(jnp.pad(generator_out, (0, second_pad))[None], both)
    gen_second = second_all.reshape(-1, second_rows + second_pad)[:, :second_rows]
    second_low = gen_second.reshape(GEN, STREAMS * MIX)

    stacked = jnp.concatenate([query_weight, key_weight, value_weight, out_weight.T], axis=0)
    over_depth = lax.all_gather(stacked, "depth", axis=0, tiled=True)
    current_f = current.astype(f32)
    current_half = half_of(current, 1, model_at)
    mean_square = jnp.mean(current_f * current_f, axis=-1, keepdims=True)
    inverse_rms = lax.rsqrt(mean_square + RMS_EPSILON)
    unit = current_f * inverse_rms
    gen_normed = (unit * gain_float[4]).astype(bf16)
    gen_pre = dot_nn(gen_normed, gen_first)
    gen_hidden = gelu_exact(gen_pre).astype(bf16)
    column = jnp.arange(STREAMS * MIX)
    last_col = (column % MIX == MIX - 1).astype(f32)
    mixing = (dot_nn(gen_hidden, second_low) + last_col).astype(bf16)
    pick_last = (column[:, None] == (jnp.arange(128) * MIX + MIX - 1)[None, :]).astype(bf16)
    last = dot_nn(mixing, pick_last)

    layer_of = jnp.tile(slot_layer, STREAMS)
    stream_of = jnp.repeat(jnp.arange(STREAMS), slots)
    from_col = jnp.where(layer_of < MIX, stream_of * MIX + layer_of, -1)
    pick = (column[:, None] == from_col[None, :]).astype(f32)
    mix_all = gather_small(mixing, ("depth",)).reshape(depth_count * MB * rows_mb, STREAMS * MIX)
    slot_mix = dot_nn(mix_all, pick.astype(bf16))
    places_all = gather_small(positions, ("depth",))

    def over_depth_swap(values):
        return lax.all_to_all(values, "depth", 0, 0, tiled=True)

    def mix_part(micro_at, slot_mix):
        partial = mix_streams(slot_mix, history, micro_at, depth_count, rows_mb)
        return partial.reshape(1, depth_count, rows_mb, STREAMS * width)

    slot_mix, ff_rows, cotangent, places_all = fence(slot_mix, ff_rows, cotangent, places_all)
    partial = mix_part(0, slot_mix)
    partial_next = mix_part(1, slot_mix)

    weights_line = LineGather(ff_rows)
    weights_line.step()
    over_depth, partial, partial_next = weights_line.hold(over_depth, partial, partial_next)
    pieces = [over_depth]
    weights = place_block(None, pieces[0][None], place_index(0), dp_count)
    hops_left = [(p, at) for at in range(len(dp_bits)) for p in range(1 << at)]
    placed = 1
    cots = None
    sums, sums_next = LineScatter(partial), LineScatter(partial_next)
    for hop in range(1, depth_count):
        sums.step()
        weights_line.step()
        last_hop = hop == depth_count - 1
        for place in range(placed, len(pieces)):
            weights = place_block(weights, pieces[place][None], place_index(place), dp_count)
        placed = len(pieces)
        while hops_left:
            place, at = hops_left.pop(0)
            pieces.append(core_hop(pieces[place], at))
            if len(hops_left) <= depth_count - 1 - hop:
                break
        if last_hop:
            cot_full = join_halves(cotangent, other_core(cotangent), model_at)
            ff_weights = weights_line.placed()
            cots = cot_full, cotangent, ff_weights
        (state,) = weights_line.hold((sums.up, sums.down, pieces, weights, cots))
        sums.up, sums.down, pieces, weights, cots = state
    cot_full, cotangent, ff_weights = cots
    for place in range(placed, len(pieces)):
        weights = place_block(weights, pieces[place][None], place_index(place), dp_count)
    weights = weights.reshape(dp_count, depth_count, 4, own_rows, heads_width)
    ff_weights = ff_weights.reshape(2, dp_count, depth_count, own_rows, ff_part)

    document_view = doc_ids.reshape(depth_count, MB, rows_mb)
    own_tables = turning_tables(positions)
    which = model_at.astype(jnp.int32)[None]
    depth_at = lax.axis_index("depth").astype(jnp.int32)[None]
    gains = gain_float

    def enter(micro_at, sums):
        span = slice(micro_at * rows_mb, (micro_at + 1) * rows_mb)
        low, resid = total_streams(sums, current_half[span], last[span], depth_at)
        normed, ff_normed, stats = norm_streams(low, other_core(low), gains, which)
        packed = project_heads(
            normed,
            cot_full[span],
            weights,
            [t[span] for t in own_tables],
            depth_count,
        )
        return dict(
            low=low, resid=resid, normed=normed, ff_normed=ff_normed, stats=stats, packed=packed
        )

    def attention(micro_at, by_head):
        span = slice(micro_at * rows_mb, (micro_at + 1) * rows_mb)
        documents = document_view[:, micro_at].reshape(length)
        seq_places = places_all[:, span].reshape(length)
        by_head = by_head.reshape(length, 4 * heads_each * HDIM)
        answer = attend(by_head, documents, turning_tables(seq_places), heads_each)
        return answer.reshape(depth_count, rows_mb, 4 * heads_each * HDIM)

    place_list = jnp.stack([place_index(p) for p in range(dp_count)]).astype(jnp.int32)

    def group_rows(ff_normed):
        return lax.all_gather(ff_normed, "dp", axis=0, tiled=True)

    def group_joined(mine):
        return join_halves(mine, other_core(mine), model_at)

    def hidden_units(micro_at, group_normed):
        hidden, grad_up, own, other = feed_forward(
            group_normed, cot_group, micro_at, ff_weights, which
        )
        return dict(group_normed=group_normed, hidden=hidden, grad_up=grad_up), (own, other)

    def group_back_rest(near):
        for at in reversed(range(len(dp_bits) - 1)):
            half = 1 << at
            near = near[:half] + core_hop(near[half:].astype(bf16), at).astype(f32)
        return near[0]

    def group_back(own, other):
        near, far = group_split(own, other, place_list)
        return group_back_rest(near + core_hop(far, len(dp_bits) - 1).astype(f32))

    def back(kept, answer):
        (theirs,) = back_project(answer, weights, 1 - which, bf16, False)
        got = other_core(theirs)
        own, flat = back_project(answer, weights, which, f32, True)
        return own, got, flat

    def leave(micro_at, kept, own, got, ff_sum):
        span = slice(micro_at * rows_mb, (micro_at + 1) * rows_mb)
        rows = (kept["resid"] + own[0] + got[0].astype(f32) + ff_sum[1]).astype(bf16)
        low, stats = kept["low"], kept["stats"]
        scaled, sums, gain_part = norm_slopes(own, got, ff_sum, low, stats, gains, which)
        grad_low, current_mix, last_dot = stream_grads(
            scaled, sums, other_core(sums), low, stats, cotangent[span], current_half[span], last[span]
        )
        kept.update(layer_rows=rows, gain=gain_part, current_mix=current_mix, last_dot=last_dot)
        return grad_low

    ((sums.up, sums.down),) = sums_next.step((sums.up, sums.down))
    first = enter(0, sums)
    cot_mine = lax.all_gather(cotangent, "dp", axis=0, tiled=True)
    packed, ff_normed, cot_mine = sums_next.hold(first["packed"], first["ff_normed"], cot_mine)
    while sums_next.at < depth_count - 3:
        sums_next.step()
        sums_next.hold()
    packed, ff_normed = sums_next.step(packed, ff_normed)
    by_head = over_depth_swap(packed)
    cot_group = join_halves(cot_mine, other_core(cot_mine), model_at)
    cot_group = cot_group.reshape(dp_count, MB, rows_mb, model)
    by_head, mine, cot_group = sums_next.hold(by_head, group_rows(ff_normed), cot_group)
    by_head, mine = sums_next.step(by_head, mine)
    kept, ff_parts = hidden_units(0, group_joined(mine))
    first.update(kept)
    answer = attention(0, by_head)
    answer, ff_parts = sums_next.hold(answer, ff_parts)

    answer = over_depth_swap(answer)
    second = enter(1, sums_next)
    ff_sum = group_back(ff_parts[0], other_core(ff_parts[1]))
    answer, packed, ff_normed, ff_sum = fence(
        answer, second["packed"], second["ff_normed"], ff_sum
    )
    by_head = over_depth_swap(packed)
    own, got, first["flat"] = back(first, answer)
    grad_low = leave(0, first, own, got, ff_sum)
    by_head, grad_low, group_normed = fence(
        by_head, grad_low, group_joined(group_rows(ff_normed))
    )
    saved = [first, second]

    def each(name):
        return [s[name] for s in saved]

    def rows_of(name):
        return jnp.concatenate(each(name), axis=0)

    def place_grads(place, dtype):
        return attention_grads(
            each("normed"),
            cot_full,
            each("flat"),
            place_list[place : place + 1],
            depth_count,
            dp_count,
            dtype,
        )

    half = dp_count // 2
    hops_left = [
        (p, at) for at in reversed(range(len(dp_bits))) for p in range(1 << at, 2 << at)
    ]
    pieces = {}

    def sums_hop():
        place, at = hops_left.pop(0)
        arrived = core_hop(pieces.pop(place).astype(bf16), at)
        target = place - (1 << at)
        pieces[target] = pieces[target].astype(f32) + arrived.astype(f32)

    grad_line = LineGather(grad_low[None])
    grad_line.step()
    answer = attention(1, by_head)
    kept, ff_parts = hidden_units(1, group_normed)
    second.update(kept)
    answer, ff_parts = grad_line.hold(answer, ff_parts)
    answer = over_depth_swap(answer)
    near, far = group_split(ff_parts[0], other_core(ff_parts[1]), place_list)
    ff_products = hidden_grads(
        each("group_normed"), cot_group, each("grad_up"), each("hidden"), dp_count, depth_count
    )
    near = near + core_hop(far, len(dp_bits) - 1).astype(f32)
    answer, near, ff_products = fence(answer, near, ff_products)

    ff_sums = LineScatter(ff_products)
    grad_line.step()
    (answer,) = ff_sums.step(answer)
    own, got, flat = back(second, answer)
    ff_sum = group_back_rest(near)
    second["flat"] = flat
    far_grads = [place_grads(p, bf16) for p in range(half, dp_count)]
    arrived = core_hop(far_grads[0], hops_left.pop(0)[1])
    (state,) = grad_line.hold(
        (ff_sums.up, ff_sums.down, own, got, flat, ff_sum, far_grads, arrived)
    )
    ff_sums.up, ff_sums.down, own, got, second["flat"], ff_sum, far_grads, arrived = state
    while len(grad_line.up) < depth_count - 1:
        grad_line.step()
        ff_sums.step()
        (state,) = grad_line.hold((ff_sums.up, ff_sums.down))
        ff_sums.up, ff_sums.down = state
    grad_line.step()
    (ff_sum,) = ff_sums.step(ff_sum)
    grad_low = leave(1, second, own, got, ff_sum)
    pieces = {p: place_grads(p, f32) for p in range(half)}
    pieces[0] = pieces[0] + arrived.astype(f32)
    pieces.update({half + at: far_grads[at] for at in range(1, half)})
    sums_hop()
    (state,) = grad_line.hold((ff_sums.up, ff_sums.down, grad_low, pieces))
    ff_sums.up, ff_sums.down, grad_low, pieces = state

    last_line = LineGather(grad_low[None])
    last_line.step()
    while hops_left:
        sums_hop()
    grad_first = grad_line.placed().reshape(length, -1)
    history_grad, slot_part = unmix_streams(
        slot_mix, history, grad_first, 0, depth_count, rows_mb, None
    )
    slot_parts = [slot_part.reshape(depth_count, 1, rows_mb, 128)]
    pieces, history_grad = last_line.hold(pieces, history_grad)
    out_sums = LineScatter(pieces[0].reshape(1, depth_count, 4 * own_rows, heads_width))
    for hop in range(2, depth_count):
        last_line.step()
        out_sums.step()
        (state,) = last_line.hold((out_sums.up, out_sums.down, ff_sums.up, ff_sums.down))
        out_sums.up, out_sums.down, ff_sums.up, ff_sums.down = state
    out_sums.step()
    ff_sums.step()
    last_grads = last_line.placed().reshape(length, -1)
    history_grad, slot_part = unmix_streams(
        slot_mix, history, last_grads, 1, depth_count, rows_mb, history_grad
    )
    slot_parts.append(slot_part.reshape(depth_count, 1, rows_mb, 128))

    slot_grads = jnp.concatenate(slot_parts, axis=1).reshape(-1, 128)[:, : STREAMS * slots]
    mix_grads = dot_exact(slot_grads, pick.T).reshape(depth_count, MB * rows_mb, STREAMS * MIX)
    (state,) = out_sums.hold((mix_grads, ff_sums.up, ff_sums.down))
    mix_grads, ff_sums.up, ff_sums.down = state
    grad_mixing = scatter_small(mix_grads, ("depth",))
    ff_grads = end_sums(ff_sums, bf16).reshape(2, dp_count, own_rows, ff_part)
    ff_pieces = [
        lax.dynamic_index_in_dim(ff_grads, partners[m], 1, keepdims=False) for m in range(dp_count)
    ]
    ff_pieces = [ff_pieces[0]] + [swap_mask(ff_pieces[m], "dp", m) for m in range(1, dp_count)]
    up_grad, down_grad = ff_join(jnp.stack(ff_pieces), partners)
    last_dots = rows_of("last_dot")
    grad_mixing = grad_mixing + dot_exact(last_dots, pick_last.astype(f32).T)
    grad_mixing = grad_mixing + other_core(grad_mixing)

    second_float = second_low.astype(f32)
    grad_second = dot_exact(gen_hidden.astype(f32).T, grad_mixing)
    grad_pre = dot_exact(grad_mixing, second_float.T) * gelu_slope(gen_pre)
    grad_first = dot_exact(gen_normed.astype(f32).T, grad_pre)
    grad_gen_normed = dot_exact(grad_pre, gen_first.astype(f32).T)
    gain_gen = jnp.sum(grad_gen_normed * unit, axis=0)
    scattered = end_sums(out_sums, f32).reshape(4, own_rows, heads_width)
    grad_unit = grad_gen_normed * gain_float[4]
    shared = jnp.mean(grad_unit * unit, axis=-1, keepdims=True)
    current_gen = half_of(inverse_rms * (grad_unit - unit * shared), 1, model_at)
    current_grad = rows_of("current_mix") + current_gen

    gain_own = sum(s["gain"] for s in saved)
    gain_other = other_core(gain_own)
    gain_all = jnp.where(
        model_at == 0,
        jnp.concatenate([gain_own, gain_other], axis=1),
        jnp.concatenate([gain_other, gain_own], axis=1),
    )
    gain_all = jnp.concatenate([gain_all, gain_gen[None]], axis=0)
    small_grads = jnp.concatenate(
        [grad_first, gain_all.T, jnp.zeros((model, 128 - GEN - 5), f32)], axis=1
    )
    small_grads = scatter_small(small_grads.reshape(-1, own_rows, 128), both)
    second_grads = jnp.pad(grad_second.reshape(-1, second_rows), ((0, 0), (0, second_pad)))
    second_grads = scatter_small(second_grads[:, None], both)

    return (
        rows_of("layer_rows"),
        history_grad,
        current_grad,
        small_grads[:, GEN : GEN + 5].T,
        small_grads[:, :GEN],
        second_grads[0, :second_rows],
        scattered[0],
        scattered[1],
        scattered[2],
        scattered[3].T,
        up_grad,
        down_grad,
    )


def solution(mesh):
    return jax.shard_map(
        local,
        mesh=mesh,
        in_specs=(
            P("depth", "dp", "mp"),
            P("depth"),
            P(("dp", "depth"), None),
            P(("dp", "depth")),
            P("dp"),
            P(("dp", "depth"), "mp"),
            P(None, ("dp", "depth")),
            P(("dp", "depth"), None),
            P(("dp", "depth")),
            P(("dp", "depth"), "mp"),
            P(("dp", "depth"), "mp"),
            P(("dp", "depth"), "mp"),
            P("mp", ("dp", "depth")),
            P(("dp", "depth"), "mp"),
            P("mp", ("dp", "depth")),
        ),
        out_specs=(
            P(("dp", "depth"), "mp"),
            P("depth", "dp", "mp"),
            P(("dp", "depth"), "mp"),
            P(None, ("dp", "depth")),
            P(("dp", "depth"), None),
            P(("dp", "depth")),
            P(("dp", "depth"), "mp"),
            P(("dp", "depth"), "mp"),
            P(("dp", "depth"), "mp"),
            P("mp", ("dp", "depth")),
            P(("dp", "depth"), "mp"),
            P("mp", ("dp", "depth")),
        ),
        check_vma=False,
    )
```

```python
import functools
import math

import jax
import jax.numpy as jnp
from jax import lax
from jax.experimental import pallas as pl
from jax.experimental.pallas import tpu as pltpu
from jax.sharding import PartitionSpec as P

HDIM = 128
ROT = 32
GEN = 72
MB = 2
MIX = 18
STREAMS = 4
COST = 20

PRECISE = lax.Precision.HIGHEST
NORM_EPSILON = 1e-05
RMS_EPSILON = 1e-06
MASKED = -1e30

bf16 = jnp.bfloat16
f32 = jnp.float32


def dot_nn(a, b):
    return lax.dot_general(a, b, (((1,), (0,)), ((), ())), preferred_element_type=f32)


def dot_nt(a, b):
    return lax.dot_general(a, b, (((1,), (1,)), ((), ())), preferred_element_type=f32)


def dot_tn(a, b):
    return lax.dot_general(a, b, (((0,), (0,)), ((), ())), preferred_element_type=f32)


def dot_exact(a, b):
    return jnp.dot(a, b, precision=PRECISE, preferred_element_type=f32)


def gelu_exact(values):
    return jax.nn.gelu(values, approximate=False)


def gelu_slope(values):
    result, pullback = jax.vjp(gelu_exact, values)
    return pullback(jnp.ones_like(result))[0]


def bit_count(size):
    count = size.bit_length() - 1
    assert 1 << count == size
    return count


def swap_mask(values, axis, mask):
    size = lax.axis_size(axis)
    return lax.ppermute(values, axis, [(i, i ^ mask) for i in range(size)])


def gather_masked(values, axis, order):
    pieces = {0: values}
    for bit in order:
        arrived = {m | (1 << bit): swap_mask(v, axis, 1 << bit) for m, v in pieces.items()}
        pieces.update(arrived)
    return [pieces[m] for m in range(len(pieces))]


def scatter_masked(pieces, axis, order, link=bf16):
    pieces = dict(enumerate(pieces))
    for bit in order:
        flag = 1 << bit
        for m in [m for m in pieces if m & flag]:
            arrived = swap_mask(pieces.pop(m).astype(link), axis, flag)
            pieces[m ^ flag] = pieces[m ^ flag].astype(f32) + arrived.astype(f32)
    return pieces[0]


def core_orders():
    bits = list(range(bit_count(lax.axis_size("dp"))))
    return bits, bits[1:] + bits[:1]


def place_mask(place):
    masks = []
    for order in core_orders():
        masks.append(sum(1 << bit for at, bit in enumerate(order) if (place >> at) & 1))
    return jnp.where(lax.axis_index("mp") % 2 == 0, masks[0], masks[1])


def place_index(place):
    return lax.axis_index("dp") ^ place_mask(place)


def core_hop(values, at):
    orders, cores = core_orders(), lax.axis_size("mp")
    pairs = []
    for i in range(lax.axis_size("dp")):
        for core in range(cores):
            partner = i ^ (1 << orders[core % 2][at])
            pairs.append((i * cores + core, partner * cores + core))
    return lax.ppermute(values, ("dp", "mp"), pairs)


def group_hop(pieces, at):
    return jnp.concatenate([pieces, core_hop(pieces, at)], axis=0)


def place_of(core):
    partner = jnp.arange(lax.axis_size("dp")) ^ lax.axis_index("dp")
    places = []
    for order in core_orders():
        places.append(sum(((partner >> bit) & 1) << at for at, bit in enumerate(order)))
    return jnp.where(core % 2 == 0, places[0], places[1])


def reorder_masked(stacked, axis):
    count = bit_count(stacked.shape[0])
    here = lax.axis_index(axis)
    shape = stacked.shape
    values = stacked.reshape((2,) * count + shape[1:])
    for bit in range(count):
        turned = jnp.flip(values, count - 1 - bit)
        values = jnp.where(((here >> bit) & 1) == 1, turned, values)
    return values.reshape(shape)


def gather_small(values, axes):
    shape = values.shape
    values = values[None]
    for axis in reversed(axes):
        order = range(bit_count(lax.axis_size(axis)))
        stacked = jnp.stack(gather_masked(values, axis, order))
        values = reorder_masked(stacked, axis)
        values = values.reshape((-1,) + shape)
    return values


def scatter_small(values, axes):
    for axis in axes:
        size = lax.axis_size(axis)
        values = values.reshape((size, values.shape[0] // size) + values.shape[1:])
        turned = reorder_masked(values, axis)
        order = reversed(range(bit_count(size)))
        values = scatter_masked([turned[m] for m in range(size)], axis, order, f32)
    return values[0]


def line_size():
    return lax.axis_size("depth"), lax.axis_index("depth")


def fence(*values):
    return lax.optimization_barrier(values)


class LineGather:

    def __init__(self, values):
        self.up, self.down = [values], [values]

    def step(self):
        size, _ = line_size()
        at = len(self.up)
        if at < size:
            up_pairs = [(i, i + 1) for i in range(at - 1, size - 1)]
            down_pairs = [(i, i - 1) for i in range(1, size - at + 1)]
            self.up.append(lax.ppermute(self.up[-1], "depth", up_pairs))
            self.down.append(lax.ppermute(self.down[-1], "depth", down_pairs))

    def hold(self, *others):
        kept = fence((self.up[1:], self.down[1:]), *others)
        (up, down), rest = kept[0], kept[1:]
        self.up, self.down = self.up[:1] + list(up), self.down[:1] + list(down)
        return rest

    def placed(self):
        size, here = line_size()
        steps = jnp.arange(size)
        index = lax.rem(here - steps + size, size)
        return place_line(index, here >= steps, self.up, self.down[1:][::-1])


class LineScatter:

    def __init__(self, terms):
        self.terms, self.at = terms, 0
        self.up = self.down = None

    def step(self, *later):
        size, here = line_size()
        self.at += 1
        if self.at >= size:
            return later
        goes_up, goes_down = hop_sums(
            self.terms,
            jnp.minimum(size - self.at + here, size - 1),
            jnp.maximum(here - size + self.at, 0),
            self.up,
            self.down,
        )
        (goes_up, goes_down), *later = fence((goes_up, goes_down), *later)
        up_pairs = [(i, i + 1) for i in range(min(self.at, size - 1))]
        down_pairs = [(size - 1 - i, size - 2 - i) for i in range(min(self.at, size - 1))]
        self.up = lax.ppermute(goes_up, "depth", up_pairs)
        self.down = lax.ppermute(goes_down, "depth", down_pairs)
        return later

    def step_with(self, line, *later):
        size, here = line_size()
        lead, _, tall, wide = self.terms.shape
        shape = line.up[0].shape
        if (
            len(line.up) != self.at + 2
            or self.at + 2 > size - 1
            or math.prod(shape) != lead * tall * wide
            or shape[2] != wide
        ):
            line.step()
            return self.step(*later)
        self.at += 1
        goes = hop_sums(
            self.terms,
            jnp.minimum(size - self.at + here, size - 1),
            jnp.maximum(here - size + self.at, 0),
            self.up,
            self.down,
            [v[-1].reshape(lead, tall, wide) for v in (line.up, line.down)],
            [here < self.at, here > size - 1 - self.at],
        )
        goes, *later = fence(goes, *later)
        self.up = lax.ppermute(goes[0], "depth", [(i, i + 1) for i in range(size - 1)])
        self.down = lax.ppermute(goes[1], "depth", [(i, i - 1) for i in range(1, size)])
        line.up.append(self.up.reshape(shape))
        line.down.append(self.down.reshape(shape))
        return later

    def hold(self, *others):
        (self.up, self.down), *rest = fence((self.up, self.down), *others)
        return rest


def other_core(values):
    return swap_mask(values, "mp", 1)


def join_kernel(model_ref, own_ref, other_ref, out_ref):
    width = own_ref.shape[1]
    own_at = pl.multiple_of(model_ref[0] * width, width)
    other_at = pl.multiple_of((1 - model_ref[0]) * width, width)
    out_ref[:, pl.ds(own_at, width)] = own_ref[...]
    out_ref[:, pl.ds(other_at, width)] = other_ref[...]


def join_halves(own, other, model_at):
    tall, width = own.shape
    rows = min(256, tall)
    return pl.pallas_call(
        join_kernel,
        grid_spec=pltpu.PrefetchScalarGridSpec(
            num_scalar_prefetch=1,
            grid=(tall // rows,),
            in_specs=[pl.BlockSpec((rows, width), lambda i, m: (i, 0))] * 2,
            out_specs=pl.BlockSpec((rows, 2 * width), lambda i, m: (i, 0)),
        ),
        out_shape=jax.ShapeDtypeStruct((tall, 2 * width), own.dtype),
        cost_estimate=spent(
            flops=0, bytes_accessed=8 * tall * width, transcendentals=0
        ),
        name="join_halves",
    )(model_at.astype(jnp.int32)[None], own, other)


def spent(flops, bytes_accessed, transcendentals):
    return pl.CostEstimate(
        flops=flops // COST, bytes_accessed=bytes_accessed // COST, transcendentals=transcendentals // COST
    )


def chunk_of(tall, wide):
    rows = tall
    while rows * wide > 1 << 19 and rows % 32 == 0:
        rows //= 2
    return rows


def place_kernel(at_ref, *refs):
    if len(refs) < 4:
        refs[-1][0, 0] = refs[0][0]
        return

    @pl.when(at_ref[1] == 1)
    def _():
        refs[-1][0, 0] = refs[0][0]

    @pl.when(at_ref[1] == 0)
    def _():
        refs[-1][0, 0] = refs[1][0]


def place_block(buffer, block, index, count, instead=None, first=None):
    lead, tall, wide = block.shape
    rows = chunk_of(tall, wide)
    spec = pl.BlockSpec((1, rows, wide), lambda l, i, m: (l, i, 0))
    blocks = [block] if instead is None else [block, instead]
    where = [index, 1 if first is None else first]
    where = jnp.stack([jnp.asarray(v).astype(jnp.int32) for v in where])
    in_specs, operands, aliases = [spec] * len(blocks), list(blocks), {}
    if buffer is not None or instead is not None:
        in_specs.append(pl.BlockSpec(memory_space=pl.ANY))
        operands.append(block if buffer is None else buffer)
        aliases = {} if buffer is None else {len(operands): 0}
    return pl.pallas_call(
        place_kernel,
        grid_spec=pltpu.PrefetchScalarGridSpec(
            num_scalar_prefetch=1,
            grid=(lead, tall // rows),
            in_specs=in_specs,
            out_specs=pl.BlockSpec((1, 1, rows, wide), lambda l, i, m: (l, m[0], i, 0)),
        ),
        out_shape=jax.ShapeDtypeStruct((lead, count, tall, wide), block.dtype),
        input_output_aliases=aliases,
        cost_estimate=spent(
            flops=0, bytes_accessed=4 * lead * tall * wide, transcendentals=0
        ),
        name="place_block",
    )(where, *operands)


def place_line_kernel(size, at_ref, *refs):
    out_ref = refs[-1]
    for step in range(size):
        if step == 0 or len(refs) == size + 1:
            out_ref[0, at_ref[step]] = refs[step][0]
            continue

        @pl.when(at_ref[size + step] == 1)
        def _(step=step):
            out_ref[0, at_ref[step]] = refs[step][0]

        @pl.when(at_ref[size + step] == 0)
        def _(step=step):
            out_ref[0, at_ref[step]] = refs[size + step - 1][0]


def place_line(index, first, blocks, instead):
    size = len(blocks)
    lead, tall, wide = blocks[0].shape
    rows = tall
    while rows * wide > 1 << 18 and rows % 32 == 0:
        rows //= 2
    spec = pl.BlockSpec((1, rows, wide), lambda l, i, m: (l, i, 0))
    where = jnp.concatenate([index, first]).astype(jnp.int32)
    operands = list(blocks) + list(instead)
    return pl.pallas_call(
        functools.partial(place_line_kernel, size),
        grid_spec=pltpu.PrefetchScalarGridSpec(
            num_scalar_prefetch=1,
            grid=(lead, tall // rows),
            in_specs=[spec] * len(operands),
            out_specs=pl.BlockSpec((1, size, rows, wide), lambda l, i, m: (l, 0, i, 0)),
        ),
        out_shape=jax.ShapeDtypeStruct((lead, size, tall, wide), blocks[0].dtype),
        compiler_params=pltpu.CompilerParams(vmem_limit_bytes=40 << 20),
        cost_estimate=spent(
            flops=0, bytes_accessed=6 * size * lead * tall * wide, transcendentals=0
        ),
        name="place_line",
    )(where, *operands)


def place_many(index, blocks):
    ones = jnp.ones(len(blocks), jnp.int32)
    return place_line(index, ones, blocks, [])


def group_join_kernel(at_ref, own_ref, other_ref, out_ref):
    width = own_ref.shape[2]
    own_span, other_span = own_spans(at_ref, width)
    out_ref[:, own_span] = own_ref[0]
    out_ref[:, other_span] = other_ref[0]


def group_join(own, other, model_at):
    count, tall, width = own.shape
    rows = chunk_of(tall, width)
    per = tall // rows
    where = jnp.concatenate([model_at[None], place_of(model_at), place_of(1 - model_at)])
    return pl.pallas_call(
        group_join_kernel,
        grid_spec=pltpu.PrefetchScalarGridSpec(
            num_scalar_prefetch=1,
            grid=(count, per),
            in_specs=[
                pl.BlockSpec((1, rows, width), lambda n, i, m: (m[1 + n], i, 0)),
                pl.BlockSpec((1, rows, width), lambda n, i, m: (m[1 + count + n], i, 0)),
            ],
            out_specs=pl.BlockSpec((rows, 2 * width), lambda n, i, m: (n * per + i, 0)),
        ),
        out_shape=jax.ShapeDtypeStruct((count * tall, 2 * width), own.dtype),
        cost_estimate=spent(
            flops=0, bytes_accessed=8 * count * tall * width, transcendentals=0
        ),
        name="group_join",
    )(where.astype(jnp.int32), own, other)


def group_split_kernel(at_ref, near_own, near_other, far_own, far_other, near_ref, far_ref):
    near_ref[0, 0] = near_own[0] + near_other[0].astype(f32)
    far_ref[0, 0] = (far_own[0] + far_other[0].astype(f32)).astype(bf16)


def group_split(own, other, places):
    _, tall, width = own.shape
    count = places.shape[0]
    half, rows = count // 2, tall // count
    near = pl.BlockSpec((1, rows, width), lambda p, k, m: (k, m[p], 0))
    far = pl.BlockSpec((1, rows, width), lambda p, k, m: (k, m[half + p], 0))
    out = pl.BlockSpec((1, 1, rows, width), lambda p, k, m: (p, k, 0, 0))
    return pl.pallas_call(
        group_split_kernel,
        grid_spec=pltpu.PrefetchScalarGridSpec(
            num_scalar_prefetch=1,
            grid=(half, 2),
            in_specs=[near, near, far, far],
            out_specs=[out, out],
        ),
        out_shape=[
            jax.ShapeDtypeStruct((half, 2, rows, width), f32),
            jax.ShapeDtypeStruct((half, 2, rows, width), bf16),
        ],
        cost_estimate=spent(
            flops=2 * tall * width, bytes_accessed=20 * tall * width, transcendentals=0
        ),
        name="group_split",
    )(places, own, other, own, other)


def hop_kernel(has_sums, has_blocks, at_ref, *refs):
    ins, outs = list(refs[:-2]), refs[-2:]
    terms, ins = ins[:2], ins[2:]
    sums, ins = (ins[:2], ins[2:]) if has_sums else (None, ins)

    def send_sum(way):
        term = terms[way][0, 0].astype(f32)
        if sums is not None:
            term = term + sums[way][0].astype(f32)
        outs[way][0] = term.astype(bf16)

    for way in range(2):
        if not has_blocks:
            send_sum(way)
            continue
        pl.when(at_ref[2 + way] == 1)(functools.partial(send_sum, way))

        @pl.when(at_ref[2 + way] == 0)
        def _(way=way):
            outs[way][0] = ins[way][0]


def hop_sums(terms, up_at, down_at, up, down, blocks=None, first=None):
    lead, _, tall, wide = terms.shape
    rows = chunk_of(tall, wide)
    block = pl.BlockSpec((1, rows, wide), lambda l, i, m: (l, i, 0))
    in_specs = [
        pl.BlockSpec((1, 1, rows, wide), lambda l, i, m: (l, m[0], i, 0)),
        pl.BlockSpec((1, 1, rows, wide), lambda l, i, m: (l, m[1], i, 0)),
    ]
    operands = [terms, terms]
    where = [up_at, down_at]
    if up is not None:
        in_specs += [block, block]
        operands += [up, down]
    if blocks is not None:
        in_specs += [block, block]
        operands += list(blocks)
        where += list(first)
    return pl.pallas_call(
        functools.partial(hop_kernel, up is not None, blocks is not None),
        grid_spec=pltpu.PrefetchScalarGridSpec(
            num_scalar_prefetch=1,
            grid=(lead, tall // rows),
            in_specs=in_specs,
            out_specs=[block, block],
        ),
        out_shape=[jax.ShapeDtypeStruct((lead, tall, wide), bf16)] * 2,
        cost_estimate=spent(
            flops=2 * lead * tall * wide, bytes_accessed=12 * lead * tall * wide, transcendentals=0
        ),
        name="hop_sums",
    )(jnp.stack(where).astype(jnp.int32), *operands)


def end_kernel(at_ref, term_ref, up_ref, down_ref, out_ref):
    total = term_ref[0, 0].astype(f32) + up_ref[0].astype(f32) + down_ref[0].astype(f32)
    out_ref[0] = total.astype(out_ref.dtype)


def end_sums(sums, dtype):
    lead, _, tall, wide = sums.terms.shape
    rows = chunk_of(tall, wide)
    block = pl.BlockSpec((1, rows, wide), lambda l, i, m: (l, i, 0))
    return pl.pallas_call(
        end_kernel,
        grid_spec=pltpu.PrefetchScalarGridSpec(
            num_scalar_prefetch=1,
            grid=(lead, tall // rows),
            in_specs=[
                pl.BlockSpec((1, 1, rows, wide), lambda l, i, m: (l, m[0], i, 0)),
                block,
                block,
            ],
            out_specs=block,
        ),
        out_shape=jax.ShapeDtypeStruct((lead, tall, wide), dtype),
        cost_estimate=spent(
            flops=2 * lead * tall * wide, bytes_accessed=10 * lead * tall * wide, transcendentals=0
        ),
        name="end_sums",
    )(lax.axis_index("depth").astype(jnp.int32)[None], sums.terms, sums.up, sums.down)


def attention_grad_kernel(
    at_ref, x0_ref, x1_ref, cot_ref, g0_ref, g1_ref, out_ref
):
    tall = x0_ref.shape[1]

    def store(total):
        out_ref[...] = total.reshape(out_ref.shape).astype(out_ref.dtype)

    @pl.when(pl.program_id(0) < 3)
    def _():
        store(dot_tn(x0_ref[0], g0_ref[0]) + dot_tn(x1_ref[0], g1_ref[0]))

    @pl.when(pl.program_id(0) == 3)
    def _():
        store(
            dot_tn(cot_ref[0:tall, :], g0_ref[0]) + dot_tn(cot_ref[tall : 2 * tall, :], g1_ref[0])
        )


def attention_grads(normed, cot, flat, place, depth_count, dp_count, dtype):
    _, tall, model = normed[0].shape
    heads_width = flat[0].shape[2]
    block = model // dp_count
    own_rows = block // depth_count
    normed_spec = pl.BlockSpec((1, tall, block), lambda k, m: (jnp.minimum(k, 2), 0, m[0]))
    flat_spec = pl.BlockSpec((1, tall, heads_width), lambda k, m: (lax.rem(k + 1, 4), 0, 0))
    return pl.pallas_call(
        attention_grad_kernel,
        grid_spec=pltpu.PrefetchScalarGridSpec(
            num_scalar_prefetch=1,
            grid=(4,),
            in_specs=[
                normed_spec,
                normed_spec,
                pl.BlockSpec((2 * tall, block), lambda k, m: (0, m[0])),
                flat_spec,
                flat_spec,
            ],
            out_specs=pl.BlockSpec(
                (depth_count, 1, own_rows, heads_width), lambda k, m: (0, k, 0, 0)
            ),
        ),
        out_shape=jax.ShapeDtypeStruct((depth_count, 4, own_rows, heads_width), dtype),
        compiler_params=pltpu.CompilerParams(vmem_limit_bytes=40 << 20),
        cost_estimate=spent(
            flops=16 * tall * block * heads_width,
            bytes_accessed=16 * block * heads_width,
            transcendentals=0,
        ),
        name="attention_grads",
    )(place, *normed, cot, *flat)


def hidden_grad_kernel(x0_ref, x1_ref, c0_ref, c1_ref, u0_ref, u1_ref, h0_ref, h1_ref, out_ref):
    def store(total):
        out_ref[...] = total.reshape(out_ref.shape)

    @pl.when(pl.program_id(0) == 0)
    def _():
        store(dot_tn(x0_ref[...], u0_ref[...]) + dot_tn(x1_ref[...], u1_ref[...]))

    @pl.when(pl.program_id(0) == 1)
    def _():
        tall, wide = h0_ref.shape[0], c0_ref.shape[3]
        c0, c1 = c0_ref[:, 0].reshape(tall, wide), c1_ref[:, 0].reshape(tall, wide)
        store(dot_tn(c0, h0_ref[...]) + dot_tn(c1, h1_ref[...]))


def hidden_grads(x, cot, up_grads, hidden, dp_count, depth_count):
    tall, model = x[0].shape
    part = hidden[0].shape[1]
    block = model // dp_count
    cols = pl.BlockSpec((tall, block), lambda k, n: (0, n * (1 - k)))
    whole = pl.BlockSpec((tall, part), lambda k, n: (0, 0))
    return pl.pallas_call(
        hidden_grad_kernel,
        grid=(2, dp_count),
        in_specs=[cols, cols]
        + [
            pl.BlockSpec((dp_count, 1, cot.shape[2], block), lambda k, n: (0, 0, 0, n * k)),
            pl.BlockSpec((dp_count, 1, cot.shape[2], block), lambda k, n: (0, 1, 0, n * k)),
        ]
        + [whole] * 4,
        out_specs=pl.BlockSpec(
            (1, depth_count, block // depth_count, part), lambda k, n: (k * dp_count + n, 0, 0, 0)
        ),
        out_shape=jax.ShapeDtypeStruct(
            (2 * dp_count, depth_count, block // depth_count, part), f32
        ),
        compiler_params=pltpu.CompilerParams(vmem_limit_bytes=48 << 20),
        cost_estimate=spent(
            flops=8 * tall * model * part, bytes_accessed=8 * model * part, transcendentals=0
        ),
        name="hidden_grads",
    )(*x, cot, cot, *up_grads, *hidden)


def mix_kernel(slots, mix_ref, hist_ref, out_ref):
    rows, width = hist_ref.shape[1], hist_ref.shape[2]
    part = 512 if width % 512 == 0 else width

    def step(at, carry):
        r0 = pl.multiple_of(at * 16, 16)
        weights = mix_ref[pl.ds(r0, 16), :]
        for c0 in range(0, width, part):
            sums = [None] * STREAMS
            for k in range(slots):
                state = hist_ref[k, pl.ds(r0, 16), c0 : c0 + part].astype(f32)
                for s in range(STREAMS):
                    term = weights[:, s * slots + k : s * slots + k + 1] * state
                    sums[s] = term if sums[s] is None else sums[s] + term
            for s in range(STREAMS):
                out_ref[s, pl.ds(r0, 16), c0 : c0 + part] = sums[s].astype(bf16)
        return carry

    lax.fori_loop(0, rows // 16, step, 0)


def mix_streams(slot_mix, history, micro_at, depth_count, rows_mb):
    slots, _, width = history.shape
    rows = min(128, rows_mb)
    per = rows_mb // rows

    def row_block(i):
        return ((i // per) * MB + micro_at) * per + i % per

    return pl.pallas_call(
        functools.partial(mix_kernel, slots),
        grid=(depth_count * per,),
        in_specs=[
            pl.BlockSpec((rows, slot_mix.shape[1]), lambda i: (row_block(i), 0)),
            pl.BlockSpec((slots, rows, width), lambda i: (0, row_block(i), 0)),
        ],
        out_specs=pl.BlockSpec((STREAMS, rows, width), lambda i: (0, i, 0)),
        out_shape=jax.ShapeDtypeStruct((STREAMS, depth_count * rows_mb, width), bf16),
        cost_estimate=spent(
            flops=2 * slots * STREAMS * depth_count * rows_mb * width,
            bytes_accessed=2 * (slots + STREAMS) * depth_count * rows_mb * width,
            transcendentals=0,
        ),
        name="mix_streams",
    )(slot_mix, history)


def unmix_kernel(slots, mix_ref, hist_ref, grad_ref, *rest):
    hist_grad_ref, slot_grad_ref = rest[-2:]
    rows, width = hist_ref.shape[1], hist_ref.shape[2]
    part = 512 if width % 512 == 0 else width

    def step(at, carry):
        r0 = pl.multiple_of(at * 16, 16)
        weights = mix_ref[pl.ds(r0, 16), :]
        totals = [None] * (STREAMS * slots)
        for c0 in range(0, width, part):
            grads = [
                grad_ref[s, pl.ds(r0, 16), c0 : c0 + part].astype(f32)
                for s in range(STREAMS)
            ]
            for k in range(slots):
                state = hist_ref[k, pl.ds(r0, 16), c0 : c0 + part].astype(f32)
                back = None
                for s in range(STREAMS):
                    at_sk = s * slots + k
                    term = weights[:, at_sk : at_sk + 1] * grads[s]
                    back = term if back is None else back + term
                    product = state * grads[s]
                    folded = product[:, 0:128]
                    for l0 in range(128, part, 128):
                        folded = folded + product[:, l0 : l0 + 128]
                    totals[at_sk] = folded if totals[at_sk] is None else totals[at_sk] + folded
                hist_grad_ref[k, pl.ds(r0, 16), c0 : c0 + part] = back.astype(bf16)
        lane = lax.broadcasted_iota(jnp.int32, (16, 128), 1)
        packed = jnp.zeros((16, 128), f32)
        for at_sk in range(STREAMS * slots):
            column = jnp.sum(totals[at_sk], axis=1, keepdims=True)
            packed = jnp.where(lane == at_sk, column, packed)
        slot_grad_ref[pl.ds(r0, 16), :] = packed
        return carry

    lax.fori_loop(0, rows // 16, step, 0)


def unmix_streams(slot_mix, history, grads, micro_at, depth_count, rows_mb, earlier):
    slots, tokens, width = history.shape
    rows = min(128, rows_mb)
    per = rows_mb // rows

    def row_block(i):
        return ((i // per) * MB + micro_at) * per + i % per

    in_specs = [
        pl.BlockSpec((rows, slot_mix.shape[1]), lambda i: (row_block(i), 0)),
        pl.BlockSpec((slots, rows, width), lambda i: (0, row_block(i), 0)),
        pl.BlockSpec((STREAMS, rows, width), lambda i: (0, i, 0)),
    ]
    operands = [slot_mix, history, grads]
    aliases = {}
    if earlier is not None:
        in_specs.append(pl.BlockSpec(memory_space=pl.ANY))
        operands.append(earlier)
        aliases = {3: 0}
    return pl.pallas_call(
        functools.partial(unmix_kernel, slots),
        grid=(depth_count * per,),
        in_specs=in_specs,
        out_specs=[
            pl.BlockSpec((slots, rows, width), lambda i: (0, row_block(i), 0)),
            pl.BlockSpec((rows, 128), lambda i: (i, 0)),
        ],
        out_shape=[
            jax.ShapeDtypeStruct((slots, tokens, width), bf16),
            jax.ShapeDtypeStruct((depth_count * rows_mb, 128), f32),
        ],
        input_output_aliases=aliases,
        cost_estimate=spent(
            flops=4 * slots * STREAMS * depth_count * rows_mb * width,
            bytes_accessed=2 * (2 * slots + STREAMS) * depth_count * rows_mb * width,
            transcendentals=0,
        ),
        name="unmix_streams",
    )(*operands)


def own_spans(model_ref, width):
    own_at = pl.multiple_of(model_ref[0] * width, width)
    other_at = pl.multiple_of((1 - model_ref[0]) * width, width)
    return pl.ds(own_at, width), pl.ds(other_at, width)


def ff_split_kernel(at_ref, up_ref, down_ref, out_ref):
    out_ref[0, 0] = up_ref[...]
    out_ref[0, 1] = down_ref[...].T


def ff_split(up_weight, down_weight, partners):
    own_rows, ff_width = up_weight.shape
    count = partners.shape[0]
    part = ff_width // count
    return pl.pallas_call(
        ff_split_kernel,
        grid_spec=pltpu.PrefetchScalarGridSpec(
            num_scalar_prefetch=1,
            grid=(count,),
            in_specs=[
                pl.BlockSpec((own_rows, part), lambda i, m: (0, m[i])),
                pl.BlockSpec((part, own_rows), lambda i, m: (m[i], 0)),
            ],
            out_specs=pl.BlockSpec((1, 2, own_rows, part), lambda i, m: (i, 0, 0, 0)),
        ),
        out_shape=jax.ShapeDtypeStruct((count, 2, own_rows, part), bf16),
        cost_estimate=spent(flops=0, bytes_accessed=8 * own_rows * ff_width, transcendentals=0),
        name="ff_split",
    )(partners, up_weight, down_weight)


def ff_join_kernel(at_ref, piece_ref, up_ref, down_ref):
    up_ref[...] = piece_ref[0, 0].astype(f32)
    down_ref[...] = piece_ref[0, 1].astype(f32).T


def ff_join(pieces, partners):
    count, _, own_rows, part = pieces.shape
    return pl.pallas_call(
        ff_join_kernel,
        grid_spec=pltpu.PrefetchScalarGridSpec(
            num_scalar_prefetch=1,
            grid=(count,),
            in_specs=[pl.BlockSpec((1, 2, own_rows, part), lambda i, m: (i, 0, 0, 0))],
            out_specs=[
                pl.BlockSpec((own_rows, part), lambda i, m: (0, m[i])),
                pl.BlockSpec((part, own_rows), lambda i, m: (m[i], 0)),
            ],
        ),
        out_shape=[
            jax.ShapeDtypeStruct((own_rows, count * part), f32),
            jax.ShapeDtypeStruct((count * part, own_rows), f32),
        ],
        cost_estimate=spent(
            flops=0, bytes_accessed=12 * own_rows * count * part, transcendentals=0
        ),
        name="ff_join",
    )(partners, pieces)


def total_kernel(depth_ref, part_ref, up_ref, down_ref, cur_ref, last_ref, low_ref, resid_ref):
    width = resid_ref.shape[1]
    current = cur_ref[...].astype(f32)
    for s in range(STREAMS):
        lanes = slice(s * width, (s + 1) * width)
        total = part_ref[s, 0].astype(f32)
        total = total + up_ref[s].astype(f32) + down_ref[s].astype(f32)
        total = total + last_ref[:, s : s + 1] * current
        if s == STREAMS - 1:
            resid_ref[...] = total
        low_ref[:, lanes] = total.astype(bf16)


def total_streams(sums, current_half, last, depth_at):
    _, _, tall, width = sums.terms.shape
    wide = STREAMS * width
    rows = min(64, tall)
    row = lambda i, d: (i, 0)
    return pl.pallas_call(
        total_kernel,
        grid_spec=pltpu.PrefetchScalarGridSpec(
            num_scalar_prefetch=1,
            grid=(tall // rows,),
            in_specs=[
                pl.BlockSpec((STREAMS, 1, rows, width), lambda i, d: (0, d[0], i, 0)),
                pl.BlockSpec((STREAMS, rows, width), lambda i, d: (0, i, 0)),
                pl.BlockSpec((STREAMS, rows, width), lambda i, d: (0, i, 0)),
                pl.BlockSpec((rows, width), row),
                pl.BlockSpec((rows, 128), row),
            ],
            out_specs=[pl.BlockSpec((rows, wide), row), pl.BlockSpec((rows, width), row)],
        ),
        out_shape=[
            jax.ShapeDtypeStruct((tall, wide), bf16),
            jax.ShapeDtypeStruct((tall, width), f32),
        ],
        cost_estimate=spent(flops=5 * tall * wide, bytes_accessed=9 * tall * wide, transcendentals=0),
        name="total_streams",
    )(depth_at, sums.terms, sums.up, sums.down, current_half, last)


def norm_kernel(model_ref, own_ref, other_ref, gain_ref, normed_ref, ff_ref, stat_ref):
    rows, width = ff_ref.shape
    model = 2 * width
    own_span, other_span = own_spans(model_ref, width)
    lane = lax.broadcasted_iota(jnp.int32, (rows, 128), 1)
    stats = jnp.zeros((rows, 128), f32)
    for s in range(STREAMS):
        lanes = slice(s * width, (s + 1) * width)
        own = own_ref[:, lanes].astype(f32)
        other = other_ref[:, lanes].astype(f32)
        average = (
            jnp.sum(own, axis=-1, keepdims=True) + jnp.sum(other, axis=-1, keepdims=True)
        ) / model
        own, other = own - average, other - average
        variance = (
            jnp.sum(own * own, axis=-1, keepdims=True)
            + jnp.sum(other * other, axis=-1, keepdims=True)
        ) / model
        inverse = lax.rsqrt(variance + NORM_EPSILON)
        stats = jnp.where(lane == 2 * s, average, stats)
        stats = jnp.where(lane == 2 * s + 1, inverse, stats)
        norm_own = (own * inverse * gain_ref[s : s + 1, own_span]).astype(bf16)
        if s == STREAMS - 1:
            ff_ref[...] = norm_own
        else:
            normed_ref[s, :, own_span] = norm_own
            norm_other = (other * inverse * gain_ref[s : s + 1, other_span]).astype(bf16)
            normed_ref[s, :, other_span] = norm_other
    stat_ref[...] = stats


def norm_streams(low, low_other, gains, which):
    tall, wide = low.shape
    width = wide // STREAMS
    rows = min(64, tall)
    row = lambda i, m: (i, 0)
    return pl.pallas_call(
        norm_kernel,
        grid_spec=pltpu.PrefetchScalarGridSpec(
            num_scalar_prefetch=1,
            grid=(tall // rows,),
            in_specs=[
                pl.BlockSpec((rows, wide), row),
                pl.BlockSpec((rows, wide), row),
                pl.BlockSpec(gains.shape, lambda i, m: (0, 0)),
            ],
            out_specs=[
                pl.BlockSpec((3, rows, 2 * width), lambda i, m: (0, i, 0)),
                pl.BlockSpec((rows, width), row),
                pl.BlockSpec((rows, 128), row),
            ],
        ),
        out_shape=[
            jax.ShapeDtypeStruct((3, tall, 2 * width), bf16),
            jax.ShapeDtypeStruct((tall, width), bf16),
            jax.ShapeDtypeStruct((tall, 128), f32),
        ],
        cost_estimate=spent(
            flops=20 * tall * wide, bytes_accessed=8 * tall * wide, transcendentals=0
        ),
        name="norm_streams",
    )(which, low, low_other, gains)


def turn(values, cosine, sine_up, sine_down, sign):
    up = pltpu.roll(values, HDIM - ROT // 2, 1)
    down = pltpu.roll(values, ROT // 2, 1)
    return values * cosine + sign * (up * sine_up + down * sine_down)


def project_kernel(
    x_ref, cot_ref, wq_ref, wk_ref, wv_ref, wo_ref, cos_ref, up_ref, down_ref, out_ref
):
    span = wq_ref.shape[-1]
    tables = cos_ref[...], up_ref[...], down_ref[...]
    for kind, w_ref in enumerate((wq_ref, wk_ref, wv_ref, wo_ref)):
        rows = cot_ref[...] if kind == 3 else x_ref[kind]
        product = dot_nn(rows, w_ref[...].reshape(-1, span))
        for begin in range(0, span, HDIM):
            head = product[:, begin : begin + HDIM]
            if kind < 2:
                head = turn(head, *tables, 1.0)
            out_ref[0, :, kind * span + begin : kind * span + begin + HDIM] = head.astype(bf16)


def project_heads(normed, cot, weights, tables, depth_count):
    _, rows, model = normed.shape
    groups, _, _, own_rows, heads_width = weights.shape
    span = heads_width // depth_count
    whole = lambda j: (0, 0)

    def matrix(kind):
        shape = (groups, depth_count, 1, own_rows, span)
        return pl.BlockSpec(shape, lambda j: (0, 0, kind, 0, j))

    return pl.pallas_call(
        project_kernel,
        grid=(depth_count,),
        in_specs=[
            pl.BlockSpec((3, rows, model), lambda j: (0, 0, 0)),
            pl.BlockSpec((rows, model), whole),
        ]
        + [matrix(kind) for kind in range(4)]
        + [pl.BlockSpec((rows, HDIM), whole)] * 3,
        out_specs=pl.BlockSpec((1, rows, 4 * span), lambda j: (j, 0, 0)),
        out_shape=jax.ShapeDtypeStruct((depth_count, rows, 4 * span), bf16),
        compiler_params=pltpu.CompilerParams(vmem_limit_bytes=40 << 20),
        cost_estimate=spent(
            flops=8 * rows * model * span * depth_count,
            bytes_accessed=8 * model * span * depth_count + 8 * rows * model,
            transcendentals=0,
        ),
        name="project_heads",
    )(normed, cot, *[weights] * 4, *tables)


def attend_kernel(
    block, q_ref, k_ref, v_ref, g_ref, doc_col_ref, doc_row_ref, cos_ref, up_ref, down_ref,
    out_ref, dk_sum, dv_sum,
):
    length = q_ref.shape[0]
    scale = HDIM**-0.5
    heads_each = out_ref.shape[1] // (4 * HDIM)

    def lanes(kind):
        return pl.ds(pl.multiple_of((kind * heads_each + pl.program_id(0)) * HDIM, HDIM), HDIM)

    for begin in range(0, length, block):
        end = begin + block
        rows = slice(begin, end)
        queries, grads = q_ref[rows, :], g_ref[rows, :]
        keys, values = k_ref[0:end, :], v_ref[0:end, :]
        scores = dot_nt(queries, keys) * scale
        place_q = begin + lax.broadcasted_iota(jnp.int32, scores.shape, 0)
        place_k = lax.broadcasted_iota(jnp.int32, scores.shape, 1)
        allowed = (doc_col_ref[rows, :] == doc_row_ref[:, 0:end]) & (place_q >= place_k)
        scores = jnp.where(allowed, scores, MASKED)
        highest = jnp.max(scores, axis=-1, keepdims=True)
        exponent = jnp.exp(scores - highest)
        totals = jnp.sum(exponent, axis=-1, keepdims=True)
        attention = exponent * (1.0 / totals)
        low = attention.astype(bf16)
        out_ref[rows, lanes(0)] = dot_nn(low, values).astype(bf16)
        grad_att = dot_nt(grads, values).astype(bf16).astype(f32)
        weighted = jnp.sum(attention * grad_att, axis=-1, keepdims=True)
        grad_scores = (attention * (grad_att - weighted)).astype(bf16)
        grad_q = dot_nn(grad_scores, keys) * scale
        out_ref[rows, lanes(1)] = turn(
            grad_q, cos_ref[rows, :], up_ref[rows, :], down_ref[rows, :], -1.0
        ).astype(bf16)
        part_k = dot_tn(grad_scores, queries)
        part_v = dot_tn(low, grads)
        if begin > 0:
            dk_sum[0:begin, :] += part_k[0:begin]
            dv_sum[0:begin, :] += part_v[0:begin]
        dk_sum[begin:end, :] = part_k[begin:end]
        dv_sum[begin:end, :] = part_v[begin:end]
    grad_k = dk_sum[...] * scale
    out_ref[:, lanes(2)] = turn(grad_k, cos_ref[...], up_ref[...], down_ref[...], -1.0).astype(bf16)
    out_ref[:, lanes(3)] = dv_sum[...].astype(bf16)


def attend(packed, documents, tables, heads_each):
    length = packed.shape[0]
    block = min(256, length)
    whole = lambda h: (0, 0)

    def kind(at):
        return pl.BlockSpec((length, HDIM), lambda h: (0, at * heads_each + h))

    return pl.pallas_call(
        functools.partial(attend_kernel, block),
        grid=(heads_each,),
        in_specs=[kind(0), kind(1), kind(2), kind(3)]
        + [pl.BlockSpec((length, 1), whole), pl.BlockSpec((1, length), whole)]
        + [pl.BlockSpec((length, HDIM), whole)] * 3,
        out_specs=pl.BlockSpec((length, 4 * heads_each * HDIM), whole),
        out_shape=jax.ShapeDtypeStruct((length, 4 * heads_each * HDIM), bf16),
        scratch_shapes=[pltpu.VMEM((length, HDIM), f32)] * 2,
        compiler_params=pltpu.CompilerParams(vmem_limit_bytes=48 << 20),
        cost_estimate=spent(
            flops=9 * heads_each * length * length * HDIM,
            bytes_accessed=16 * length * heads_each * HDIM + 12 * length * HDIM,
            transcendentals=heads_each * length * length,
        ),
        name="attend",
    )(packed, packed, packed, packed, documents[:, None], documents[None, :], *tables)


def gelu_parts(values):
    cdf = 0.5 * (1.0 + lax.erf(values * (0.5**0.5)))
    density = jnp.exp(-0.5 * values * values) * (1.0 / math.sqrt(2.0 * math.pi))
    return values * cdf, cdf + values * density


def ff_kernel(
    model_ref, x_ref, cot_ref, up_ref, down_ref,
    hidden_ref, grad_ref, own_ref, other_ref,
):
    part = up_ref.shape[-1]
    half = up_ref.shape[1] // 2

    def rows_of(ref, which):
        return ref[0, pl.ds(which * half, half)].reshape(-1, part)

    own, other = model_ref[0], 1 - model_ref[0]
    up_pre = dot_nn(x_ref[...], up_ref[...].reshape(-1, part))
    hidden, slope = gelu_parts(up_pre)
    hidden = hidden.astype(bf16)
    grad_up = (dot_nn(cot_ref[0, 0], down_ref[...].reshape(-1, part)) * slope).astype(bf16)
    hidden_ref[...] = hidden
    grad_ref[...] = grad_up
    other_ref[0] = dot_nt(grad_up, rows_of(up_ref, other)).astype(bf16)
    own_ref[0] = dot_nt(grad_up, rows_of(up_ref, own))
    other_ref[1] = dot_nt(hidden, rows_of(down_ref, other)).astype(bf16)
    own_ref[1] = dot_nt(hidden, rows_of(down_ref, own))


def feed_forward(x, cot, micro_at, weights, which):
    tall, model = x.shape
    part = weights.shape[-1]
    width = model // 2
    rows = cot.shape[2]
    row = lambda i, m: (i, 0)

    def resident(kind):
        return pl.BlockSpec(
            (1,) + weights.shape[1:],
            lambda i, m: (kind, 0, 0, 0, 0),
            pipeline_mode=pl.Buffered(1),
        )

    return pl.pallas_call(
        ff_kernel,
        grid_spec=pltpu.PrefetchScalarGridSpec(
            num_scalar_prefetch=1,
            grid=(tall // rows,),
            in_specs=[
                pl.BlockSpec((rows, model), row),
                pl.BlockSpec((1, 1, rows, model), lambda i, m: (i, micro_at, 0, 0)),
                resident(0),
                resident(1),
            ],
            out_specs=[pl.BlockSpec((rows, part), row)] * 2
            + [pl.BlockSpec((2, rows, width), lambda i, m: (0, i, 0))] * 2,
        ),
        out_shape=[jax.ShapeDtypeStruct((tall, part), bf16)] * 2
        + [
            jax.ShapeDtypeStruct((2, tall, width), f32),
            jax.ShapeDtypeStruct((2, tall, width), bf16),
        ],
        compiler_params=pltpu.CompilerParams(vmem_limit_bytes=48 << 20),
        cost_estimate=spent(
            flops=8 * tall * model * part,
            bytes_accessed=4 * model * part + 16 * tall * model,
            transcendentals=2 * tall * part,
        ),
        name="feed_forward",
    )(which, x, cot, weights, weights)


def back_kernel(half_ref, ans_ref, wo_ref, wq_ref, wk_ref, wv_ref, out_ref, *flat):
    count, _, wide = ans_ref.shape
    span = wide // 4
    for kind, w_ref in enumerate((wo_ref, wq_ref, wk_ref, wv_ref)):
        total = None
        for j in range(count):
            term = dot_nt(
                ans_ref[j, :, kind * span : (kind + 1) * span],
                w_ref[:, :, :, :, j * span : (j + 1) * span].reshape(-1, span),
            )
            total = term if total is None else total + term
        out_ref[kind] = total.astype(out_ref.dtype)
    if flat:

        @pl.when(pl.program_id(0) == 0)
        def _():
            for kind in range(4):
                for j in range(count):
                    flat[0][kind, :, j * span : (j + 1) * span] = ans_ref[
                        j, :, kind * span : (kind + 1) * span
                    ]


def back_project(answer, weights, half, dtype, flat):
    count, rows, wide = answer.shape
    groups, _, _, own_rows, heads_width = weights.shape
    part = count * own_rows
    steps = groups // 2
    width = part * steps

    def matrix(kind):
        shape = (1, count, 1, own_rows, heads_width)
        return pl.BlockSpec(shape, lambda i, m: (m[0] * steps + i, 0, kind, 0, 0))

    out_specs = [pl.BlockSpec((4, rows, part), lambda i, m: (0, 0, i))]
    out_shape = [jax.ShapeDtypeStruct((4, rows, width), dtype)]
    if flat:
        out_specs.append(pl.BlockSpec((4, rows, heads_width), lambda i, m: (0, 0, 0)))
        out_shape.append(jax.ShapeDtypeStruct((4, rows, heads_width), bf16))
    return pl.pallas_call(
        back_kernel,
        grid_spec=pltpu.PrefetchScalarGridSpec(
            num_scalar_prefetch=1,
            grid=(steps,),
            in_specs=[pl.BlockSpec((count, rows, wide), lambda i, m: (0, 0, 0))]
            + [matrix(kind) for kind in (3, 0, 1, 2)],
            out_specs=out_specs,
        ),
        out_shape=out_shape,
        compiler_params=pltpu.CompilerParams(vmem_limit_bytes=40 << 20),
        cost_estimate=spent(
            flops=8 * rows * heads_width * width,
            bytes_accessed=8 * heads_width * width + 20 * rows * width,
            transcendentals=0,
        ),
        name="back_project",
    )(half, answer, *[weights] * 4)


def slope_kernel(
    model_ref, own_ref, got_ref, ff_ref, low_ref, stat_ref, gain_ref, scaled_ref, sum_ref, gain_out_ref
):
    _, rows, width = ff_ref.shape
    own_span, _ = own_spans(model_ref, width)
    lane = lax.broadcasted_iota(jnp.int32, (rows, 128), 1)
    packed = jnp.zeros((rows, 128), f32)
    totals = []
    for s in range(STREAMS):
        lanes = slice(s * width, (s + 1) * width)
        if s < 3:
            grad = own_ref[s + 1] + got_ref[s + 1].astype(f32)
        else:
            grad = ff_ref[0]
        average, inverse = stat_ref[:, 2 * s : 2 * s + 1], stat_ref[:, 2 * s + 1 : 2 * s + 2]
        hat = (low_ref[:, lanes].astype(f32) - average) * inverse
        totals.append(jnp.sum(grad * hat, axis=0, keepdims=True))
        scaled = grad * gain_ref[s : s + 1, own_span]
        scaled_ref[:, lanes] = scaled
        packed = jnp.where(lane == 2 * s, jnp.sum(scaled, axis=-1, keepdims=True), packed)
        packed = jnp.where(
            lane == 2 * s + 1, jnp.sum(scaled * hat, axis=-1, keepdims=True), packed
        )
    sum_ref[...] = packed
    totals = jnp.concatenate(totals, axis=0)

    @pl.when(pl.program_id(0) == 0)
    def _():
        gain_out_ref[...] = totals

    @pl.when(pl.program_id(0) > 0)
    def _():
        gain_out_ref[...] += totals


def norm_slopes(own, got, ff_grad, low, stats, gains, which):
    tall, wide = low.shape
    width = wide // STREAMS
    rows = min(64, tall)
    row = lambda i, m: (i, 0)
    cube = pl.BlockSpec((4, rows, width), lambda i, m: (0, i, 0))
    return pl.pallas_call(
        slope_kernel,
        grid_spec=pltpu.PrefetchScalarGridSpec(
            num_scalar_prefetch=1,
            grid=(tall // rows,),
            in_specs=[
                cube,
                cube,
                pl.BlockSpec((1, rows, width), lambda i, m: (0, i, 0)),
                pl.BlockSpec((rows, wide), row),
                pl.BlockSpec((rows, 128), row),
                pl.BlockSpec(gains.shape, lambda i, m: (0, 0)),
            ],
            out_specs=[
                pl.BlockSpec((rows, wide), row),
                pl.BlockSpec((rows, 128), row),
                pl.BlockSpec((STREAMS, width), lambda i, m: (0, 0)),
            ],
        ),
        out_shape=[
            jax.ShapeDtypeStruct((tall, wide), f32),
            jax.ShapeDtypeStruct((tall, 128), f32),
            jax.ShapeDtypeStruct((STREAMS, width), f32),
        ],
        cost_estimate=spent(
            flops=12 * tall * wide, bytes_accessed=12 * tall * wide, transcendentals=0
        ),
        name="norm_slopes",
    )(which, own, got, ff_grad, low, stats, gains)


def grads_kernel(
    scaled_ref, mine_ref, theirs_ref, low_ref, stat_ref, cot_ref, cur_ref, last_ref,
    grad_ref, mix_ref, dot_ref,
):
    rows, width = cot_ref.shape
    lane = lax.broadcasted_iota(jnp.int32, (rows, 128), 1)
    means = (mine_ref[...] + theirs_ref[...]) / (2 * width)
    current = cur_ref[...].astype(f32)
    packed = jnp.zeros((rows, 128), f32)
    mixed = None
    for s in range(STREAMS):
        lanes = slice(s * width, (s + 1) * width)
        average, inverse = stat_ref[:, 2 * s : 2 * s + 1], stat_ref[:, 2 * s + 1 : 2 * s + 2]
        hat = (low_ref[:, lanes].astype(f32) - average) * inverse
        grad = inverse * (
            scaled_ref[:, lanes]
            - means[:, 2 * s : 2 * s + 1]
            - hat * means[:, 2 * s + 1 : 2 * s + 2]
        )
        if s == STREAMS - 1:
            grad = grad + cot_ref[...].astype(f32)
        grad = grad.astype(bf16)
        grad_ref[s] = grad
        grad = grad.astype(f32)
        term = last_ref[:, s : s + 1] * grad
        mixed = term if mixed is None else mixed + term
        packed = jnp.where(lane == s, jnp.sum(grad * current, axis=-1, keepdims=True), packed)
    mix_ref[...] = mixed
    dot_ref[...] = packed


def stream_grads(scaled, mine, theirs, low, stats, cot, current_half, last):
    tall, wide = low.shape
    width = wide // STREAMS
    rows = min(64, tall)
    row = lambda i: (i, 0)
    return pl.pallas_call(
        grads_kernel,
        grid=(tall // rows,),
        in_specs=[
            pl.BlockSpec((rows, wide), row),
            pl.BlockSpec((rows, 128), row),
            pl.BlockSpec((rows, 128), row),
            pl.BlockSpec((rows, wide), row),
            pl.BlockSpec((rows, 128), row),
            pl.BlockSpec((rows, width), row),
            pl.BlockSpec((rows, width), row),
            pl.BlockSpec((rows, 128), row),
        ],
        out_specs=[
            pl.BlockSpec((STREAMS, rows, width), lambda i: (0, i, 0)),
            pl.BlockSpec((rows, width), row),
            pl.BlockSpec((rows, 128), row),
        ],
        out_shape=[
            jax.ShapeDtypeStruct((STREAMS, tall, width), bf16),
            jax.ShapeDtypeStruct((tall, width), f32),
            jax.ShapeDtypeStruct((tall, 128), f32),
        ],
        cost_estimate=spent(
            flops=12 * tall * wide, bytes_accessed=10 * tall * wide, transcendentals=0
        ),
        name="stream_grads",
    )(scaled, mine, theirs, low, stats, cot, current_half, last)


def turning_tables(places):
    half = ROT // 2
    inverse = jnp.exp(jnp.arange(half, dtype=f32) * (-2.0 * math.log(10000.0) / ROT))
    angles = places.astype(f32)[:, None] * inverse[None, :]
    cosine, sine = jnp.cos(angles), jnp.sin(angles)
    rows = places.shape[0]
    rest = jnp.zeros((rows, HDIM - ROT), f32)
    blank = jnp.zeros((rows, half), f32)
    return (
        jnp.concatenate([cosine, cosine, rest + 1.0], axis=1),
        jnp.concatenate([-sine, blank, rest], axis=1),
        jnp.concatenate([blank, sine, rest], axis=1),
    )


def local(
    history,
    slot_layer,
    current,
    positions,
    doc_ids,
    cotangent,
    norm_gains,
    generator_in,
    generator_out,
    query_weight,
    key_weight,
    value_weight,
    out_weight,
    up_weight,
    down_weight,
):
    dp_count = lax.axis_size("dp")
    depth_count = lax.axis_size("depth")
    dp_at = lax.axis_index("dp")
    model_at = lax.axis_index("mp")
    dp_bits = list(range(bit_count(dp_count)))
    slots, tokens_held, width = history.shape
    model = current.shape[1]
    rows_mb = current.shape[0] // MB
    length = depth_count * rows_mb
    heads_width = query_weight.shape[1]
    heads_each = heads_width // HDIM // depth_count
    own_rows = query_weight.shape[0]
    ff_width = up_weight.shape[1]
    ff_part = ff_width // dp_count
    both = ("dp", "depth")

    def half_of(values, axis, which):
        return lax.dynamic_slice_in_dim(values, which * width, width, axis)

    partners = jnp.stack([dp_at ^ m for m in range(dp_count)]).astype(jnp.int32)
    ff_local = ff_split(up_weight, down_weight, partners)
    ff_rows = [ff_local[0]] + [swap_mask(ff_local[m], "dp", m) for m in range(1, dp_count)]
    ff_rows = place_many(partners, ff_rows).reshape(2 * dp_count, own_rows, ff_part)

    small_cols = jnp.concatenate(
        [generator_in, norm_gains.T, jnp.zeros((own_rows, 128 - GEN - 5), bf16)], axis=1
    )
    small_all = gather_small(small_cols, both).reshape(model, 128)
    gen_first = small_all[:, :GEN]
    gen_first, ff_rows = fence(gen_first, ff_rows)
    gain_float = small_all[:, GEN : GEN + 5].astype(f32).T
    second_rows = generator_out.shape[0]
    second_pad = -second_rows % 128
    second_all = gather_small(jnp.pad(generator_out, (0, second_pad))[None], both)
    gen_second = second_all.reshape(-1, second_rows + second_pad)[:, :second_rows]
    second_low = gen_second.reshape(GEN, STREAMS * MIX)

    stacked = jnp.concatenate([query_weight, key_weight, value_weight, out_weight.T], axis=0)
    over_depth = lax.all_gather(stacked, "depth", axis=0, tiled=True)
    current_f = current.astype(f32)
    current_half = half_of(current, 1, model_at)
    mean_square = jnp.mean(current_f * current_f, axis=-1, keepdims=True)
    inverse_rms = lax.rsqrt(mean_square + RMS_EPSILON)
    unit = current_f * inverse_rms
    gen_normed = (unit * gain_float[4]).astype(bf16)
    gen_pre = dot_nn(gen_normed, gen_first)
    gen_hidden = gelu_exact(gen_pre).astype(bf16)
    column = jnp.arange(STREAMS * MIX)
    last_col = (column % MIX == MIX - 1).astype(f32)
    mixing = (dot_nn(gen_hidden, second_low) + last_col).astype(bf16)
    pick_last = (column[:, None] == (jnp.arange(128) * MIX + MIX - 1)[None, :]).astype(bf16)
    last = dot_nn(mixing, pick_last)

    layer_of = jnp.tile(slot_layer, STREAMS)
    stream_of = jnp.repeat(jnp.arange(STREAMS), slots)
    from_col = jnp.where(layer_of < MIX, stream_of * MIX + layer_of, -1)
    pick = (column[:, None] == from_col[None, :]).astype(f32)
    mix_all = gather_small(mixing, ("depth",)).reshape(depth_count * MB * rows_mb, STREAMS * MIX)
    slot_mix = dot_nn(mix_all, pick.astype(bf16))
    places_all = gather_small(positions, ("depth",))

    def over_depth_swap(values):
        return lax.all_to_all(values, "depth", 0, 0, tiled=True)

    def mix_part(micro_at, slot_mix):
        partial = mix_streams(slot_mix, history, micro_at, depth_count, rows_mb)
        return partial.reshape(STREAMS, depth_count, rows_mb, width)

    slot_mix, ff_rows, cotangent, places_all = fence(slot_mix, ff_rows, cotangent, places_all)
    partial = mix_part(0, slot_mix)
    partial_next = mix_part(1, slot_mix)

    weights_line = LineGather(ff_rows)
    weights_line.step()
    over_depth, partial, partial_next = weights_line.hold(over_depth, partial, partial_next)
    pieces = [over_depth]
    weights = place_block(None, pieces[0][None], place_index(0), dp_count)
    hops_left = [(p, at) for at in range(len(dp_bits)) for p in range(1 << at)]
    placed = 1
    cots = None
    sums, sums_next = LineScatter(partial), LineScatter(partial_next)
    for hop in range(1, depth_count):
        sums.step_with(weights_line)
        last_hop = hop == depth_count - 1
        for place in range(placed, len(pieces)):
            weights = place_block(weights, pieces[place][None], place_index(place), dp_count)
        placed = len(pieces)
        while hops_left:
            place, at = hops_left.pop(0)
            pieces.append(core_hop(pieces[place], at))
            if len(hops_left) <= depth_count - 1 - hop:
                break
        if last_hop:
            cot_full = join_halves(cotangent, other_core(cotangent), model_at)
            ff_weights = weights_line.placed()
            cots = cot_full, cotangent, ff_weights
        (state,) = weights_line.hold((sums.up, sums.down, pieces, weights, cots))
        sums.up, sums.down, pieces, weights, cots = state
    cot_full, cotangent, ff_weights = cots
    for place in range(placed, len(pieces)):
        weights = place_block(weights, pieces[place][None], place_index(place), dp_count)
    weights = weights.reshape(dp_count, depth_count, 4, own_rows, heads_width)
    ff_weights = ff_weights.reshape(2, dp_count, depth_count, own_rows, ff_part)

    document_view = doc_ids.reshape(depth_count, MB, rows_mb)
    own_tables = turning_tables(positions)
    which = model_at.astype(jnp.int32)[None]
    depth_at = lax.axis_index("depth").astype(jnp.int32)[None]
    gains = gain_float

    def enter(micro_at, sums):
        span = slice(micro_at * rows_mb, (micro_at + 1) * rows_mb)
        low, resid = total_streams(sums, current_half[span], last[span], depth_at)
        normed, ff_normed, stats = norm_streams(low, other_core(low), gains, which)
        packed = project_heads(
            normed,
            cot_full[span],
            weights,
            [t[span] for t in own_tables],
            depth_count,
        )
        return dict(
            low=low, resid=resid, normed=normed, ff_normed=ff_normed, stats=stats, packed=packed
        )

    def attention(micro_at, by_head):
        span = slice(micro_at * rows_mb, (micro_at + 1) * rows_mb)
        documents = document_view[:, micro_at].reshape(length)
        seq_places = places_all[:, span].reshape(length)
        by_head = by_head.reshape(length, 4 * heads_each * HDIM)
        answer = attend(by_head, documents, turning_tables(seq_places), heads_each)
        return answer.reshape(depth_count, rows_mb, 4 * heads_each * HDIM)

    place_list = jnp.stack([place_index(p) for p in range(dp_count)]).astype(jnp.int32)

    def group_rows(ff_normed):
        return lax.all_gather(ff_normed, "dp", axis=0, tiled=True)

    def group_joined(mine):
        return join_halves(mine, other_core(mine), model_at)

    def hidden_units(micro_at, group_normed):
        hidden, grad_up, own, other = feed_forward(
            group_normed, cot_group, micro_at, ff_weights, which
        )
        return dict(group_normed=group_normed, hidden=hidden, grad_up=grad_up), (own, other)

    def group_back_rest(near):
        for at in reversed(range(len(dp_bits) - 1)):
            half = 1 << at
            near = near[:half] + core_hop(near[half:].astype(bf16), at).astype(f32)
        return near[0]

    def group_back(own, other):
        near, far = group_split(own, other, place_list)
        return group_back_rest(near + core_hop(far, len(dp_bits) - 1).astype(f32))

    def back(kept, answer):
        (theirs,) = back_project(answer, weights, 1 - which, bf16, False)
        got = other_core(theirs)
        own, flat = back_project(answer, weights, which, f32, True)
        return own, got, flat

    def leave(micro_at, kept, own, got, ff_sum):
        span = slice(micro_at * rows_mb, (micro_at + 1) * rows_mb)
        rows = (kept["resid"] + own[0] + got[0].astype(f32) + ff_sum[1]).astype(bf16)
        low, stats = kept["low"], kept["stats"]
        scaled, sums, gain_part = norm_slopes(own, got, ff_sum, low, stats, gains, which)
        grad_low, current_mix, last_dot = stream_grads(
            scaled, sums, other_core(sums), low, stats, cotangent[span], current_half[span], last[span]
        )
        kept.update(layer_rows=rows, gain=gain_part, current_mix=current_mix, last_dot=last_dot)
        return grad_low

    ((sums.up, sums.down),) = sums_next.step((sums.up, sums.down))
    first = enter(0, sums)
    cot_mine = lax.all_gather(cotangent, "dp", axis=0, tiled=True)
    packed, ff_normed, cot_mine = sums_next.hold(first["packed"], first["ff_normed"], cot_mine)
    while sums_next.at < depth_count - 3:
        sums_next.step()
        sums_next.hold()
    packed, ff_normed = sums_next.step(packed, ff_normed)
    by_head = over_depth_swap(packed)
    cot_group = join_halves(cot_mine, other_core(cot_mine), model_at)
    cot_group = cot_group.reshape(dp_count, MB, rows_mb, model)
    by_head, mine, cot_group = sums_next.hold(by_head, group_rows(ff_normed), cot_group)
    by_head, mine = sums_next.step(by_head, mine)
    kept, ff_parts = hidden_units(0, group_joined(mine))
    first.update(kept)
    answer = attention(0, by_head)
    answer, ff_parts = sums_next.hold(answer, ff_parts)

    answer = over_depth_swap(answer)
    second = enter(1, sums_next)
    ff_sum = group_back(ff_parts[0], other_core(ff_parts[1]))
    answer, packed, ff_normed, ff_sum = fence(
        answer, second["packed"], second["ff_normed"], ff_sum
    )
    by_head = over_depth_swap(packed)
    own, got, first["flat"] = back(first, answer)
    grad_low = leave(0, first, own, got, ff_sum)
    by_head, grad_low, group_normed = fence(
        by_head, grad_low, group_joined(group_rows(ff_normed))
    )
    saved = [first, second]

    def each(name):
        return [s[name] for s in saved]

    def rows_of(name):
        return jnp.concatenate(each(name), axis=0)

    def place_grads(place, dtype):
        return attention_grads(
            each("normed"),
            cot_full,
            each("flat"),
            place_list[place : place + 1],
            depth_count,
            dp_count,
            dtype,
        )

    half = dp_count // 2
    hops_left = [
        (p, at) for at in reversed(range(len(dp_bits))) for p in range(1 << at, 2 << at)
    ]
    pieces = {}

    def sums_hop():
        place, at = hops_left.pop(0)
        arrived = core_hop(pieces.pop(place).astype(bf16), at)
        target = place - (1 << at)
        pieces[target] = pieces[target].astype(f32) + arrived.astype(f32)

    grad_line = LineGather(grad_low)
    grad_line.step()
    answer = attention(1, by_head)
    kept, ff_parts = hidden_units(1, group_normed)
    second.update(kept)
    answer, ff_parts = grad_line.hold(answer, ff_parts)
    answer = over_depth_swap(answer)
    near, far = group_split(ff_parts[0], other_core(ff_parts[1]), place_list)
    ff_products = hidden_grads(
        each("group_normed"), cot_group, each("grad_up"), each("hidden"), dp_count, depth_count
    )
    near = near + core_hop(far, len(dp_bits) - 1).astype(f32)
    answer, near, ff_products = fence(answer, near, ff_products)

    ff_sums = LineScatter(ff_products)
    (answer,) = ff_sums.step_with(grad_line, answer)
    own, got, flat = back(second, answer)
    ff_sum = group_back_rest(near)
    second["flat"] = flat
    far_grads = [place_grads(p, bf16) for p in range(half, dp_count)]
    arrived = core_hop(far_grads[0], hops_left.pop(0)[1])
    (state,) = grad_line.hold(
        (ff_sums.up, ff_sums.down, own, got, flat, ff_sum, far_grads, arrived)
    )
    ff_sums.up, ff_sums.down, own, got, second["flat"], ff_sum, far_grads, arrived = state
    while len(grad_line.up) < depth_count - 1:
        ff_sums.step_with(grad_line)
        (state,) = grad_line.hold((ff_sums.up, ff_sums.down))
        ff_sums.up, ff_sums.down = state
    (ff_sum,) = ff_sums.step_with(grad_line, ff_sum)
    grad_low = leave(1, second, own, got, ff_sum)
    pieces = {p: place_grads(p, f32) for p in range(half)}
    pieces[0] = pieces[0] + arrived.astype(f32)
    pieces.update({half + at: far_grads[at] for at in range(1, half)})
    sums_hop()
    (state,) = grad_line.hold((ff_sums.up, ff_sums.down, grad_low, pieces))
    ff_sums.up, ff_sums.down, grad_low, pieces = state

    last_line = LineGather(grad_low)
    last_line.step()
    ff_sums.step()
    while hops_left:
        sums_hop()
    grad_first = grad_line.placed().reshape(STREAMS, length, width)
    history_grad, slot_part = unmix_streams(
        slot_mix, history, grad_first, 0, depth_count, rows_mb, None
    )
    slot_parts = [slot_part.reshape(depth_count, 1, rows_mb, 128)]
    pieces, history_grad, state = last_line.hold(
        pieces, history_grad, (ff_sums.up, ff_sums.down)
    )
    ff_sums.up, ff_sums.down = state
    out_sums = LineScatter(pieces[0].reshape(1, depth_count, 4 * own_rows, heads_width))
    for hop in range(2, depth_count):
        last_line.step()
        out_sums.step()
        (state,) = last_line.hold((out_sums.up, out_sums.down, ff_sums.up, ff_sums.down))
        out_sums.up, out_sums.down, ff_sums.up, ff_sums.down = state
    out_sums.step()
    ff_grads = end_sums(ff_sums, bf16).reshape(2, dp_count, own_rows, ff_part)
    ff_pieces = [
        lax.dynamic_index_in_dim(ff_grads, partners[m], 1, keepdims=False) for m in range(dp_count)
    ]
    ff_pieces = [ff_pieces[0]] + [swap_mask(ff_pieces[m], "dp", m) for m in range(1, dp_count)]
    last_grads = last_line.placed().reshape(STREAMS, length, width)
    history_grad, slot_part = unmix_streams(
        slot_mix, history, last_grads, 1, depth_count, rows_mb, history_grad
    )
    slot_parts.append(slot_part.reshape(depth_count, 1, rows_mb, 128))

    slot_grads = jnp.concatenate(slot_parts, axis=1).reshape(-1, 128)[:, : STREAMS * slots]
    mix_grads = dot_exact(slot_grads, pick.T).reshape(depth_count, MB * rows_mb, STREAMS * MIX)
    mix_grads, ff_pieces = out_sums.hold(mix_grads, ff_pieces)
    grad_mixing = scatter_small(mix_grads, ("depth",))
    up_grad, down_grad = ff_join(jnp.stack(ff_pieces), partners)
    last_dots = rows_of("last_dot")
    grad_mixing = grad_mixing + dot_exact(last_dots, pick_last.astype(f32).T)
    grad_mixing = grad_mixing + other_core(grad_mixing)

    second_float = second_low.astype(f32)
    grad_second = dot_exact(gen_hidden.astype(f32).T, grad_mixing)
    grad_pre = dot_exact(grad_mixing, second_float.T) * gelu_slope(gen_pre)
    grad_first = dot_exact(gen_normed.astype(f32).T, grad_pre)
    grad_gen_normed = dot_exact(grad_pre, gen_first.astype(f32).T)
    gain_gen = jnp.sum(grad_gen_normed * unit, axis=0)
    scattered = end_sums(out_sums, f32).reshape(4, own_rows, heads_width)
    grad_unit = grad_gen_normed * gain_float[4]
    shared = jnp.mean(grad_unit * unit, axis=-1, keepdims=True)
    current_gen = half_of(inverse_rms * (grad_unit - unit * shared), 1, model_at)
    current_grad = rows_of("current_mix") + current_gen

    gain_own = sum(s["gain"] for s in saved)
    gain_other = other_core(gain_own)
    gain_all = jnp.where(
        model_at == 0,
        jnp.concatenate([gain_own, gain_other], axis=1),
        jnp.concatenate([gain_other, gain_own], axis=1),
    )
    gain_all = jnp.concatenate([gain_all, gain_gen[None]], axis=0)
    small_grads = jnp.concatenate(
        [grad_first, gain_all.T, jnp.zeros((model, 128 - GEN - 5), f32)], axis=1
    )
    small_grads = scatter_small(small_grads.reshape(-1, own_rows, 128), both)
    second_grads = jnp.pad(grad_second.reshape(-1, second_rows), ((0, 0), (0, second_pad)))
    second_grads = scatter_small(second_grads[:, None], both)

    return (
        rows_of("layer_rows"),
        history_grad,
        current_grad,
        small_grads[:, GEN : GEN + 5].T,
        small_grads[:, :GEN],
        second_grads[0, :second_rows],
        scattered[0],
        scattered[1],
        scattered[2],
        scattered[3].T,
        up_grad,
        down_grad,
    )


def solution(mesh):
    return jax.shard_map(
        local,
        mesh=mesh,
        in_specs=(
            P("depth", "dp", "mp"),
            P("depth"),
            P(("dp", "depth"), None),
            P(("dp", "depth")),
            P("dp"),
            P(("dp", "depth"), "mp"),
            P(None, ("dp", "depth")),
            P(("dp", "depth"), None),
            P(("dp", "depth")),
            P(("dp", "depth"), "mp"),
            P(("dp", "depth"), "mp"),
            P(("dp", "depth"), "mp"),
            P("mp", ("dp", "depth")),
            P(("dp", "depth"), "mp"),
            P("mp", ("dp", "depth")),
        ),
        out_specs=(
            P(("dp", "depth"), "mp"),
            P("depth", "dp", "mp"),
            P(("dp", "depth"), "mp"),
            P(None, ("dp", "depth")),
            P(("dp", "depth"), None),
            P(("dp", "depth")),
            P(("dp", "depth"), "mp"),
            P(("dp", "depth"), "mp"),
            P(("dp", "depth"), "mp"),
            P("mp", ("dp", "depth")),
            P(("dp", "depth"), "mp"),
            P("mp", ("dp", "depth")),
        ),
        check_vma=False,
    )
```

```python
import functools
import math

import jax
import jax.numpy as jnp
from jax import lax
from jax.experimental import pallas as pl
from jax.experimental.pallas import tpu as pltpu
from jax.sharding import PartitionSpec as P

HDIM = 128
ROT = 32
GEN = 72
MB = 2
MIX = 18
STREAMS = 4
COST = 20

PRECISE = lax.Precision.HIGHEST
NORM_EPSILON = 1e-05
RMS_EPSILON = 1e-06
MASKED = -1e30

bf16 = jnp.bfloat16
f32 = jnp.float32


def dot_nn(a, b):
    return lax.dot_general(a, b, (((1,), (0,)), ((), ())), preferred_element_type=f32)


def dot_nt(a, b):
    return lax.dot_general(a, b, (((1,), (1,)), ((), ())), preferred_element_type=f32)


def dot_tn(a, b):
    return lax.dot_general(a, b, (((0,), (0,)), ((), ())), preferred_element_type=f32)


def dot_exact(a, b):
    return jnp.dot(a, b, precision=PRECISE, preferred_element_type=f32)


def gelu_exact(values):
    return jax.nn.gelu(values, approximate=False)


def gelu_slope(values):
    result, pullback = jax.vjp(gelu_exact, values)
    return pullback(jnp.ones_like(result))[0]


def bit_count(size):
    count = size.bit_length() - 1
    assert 1 << count == size
    return count


def swap_mask(values, axis, mask):
    size = lax.axis_size(axis)
    return lax.ppermute(values, axis, [(i, i ^ mask) for i in range(size)])


def gather_masked(values, axis, order):
    pieces = {0: values}
    for bit in order:
        arrived = {m | (1 << bit): swap_mask(v, axis, 1 << bit) for m, v in pieces.items()}
        pieces.update(arrived)
    return [pieces[m] for m in range(len(pieces))]


def scatter_masked(pieces, axis, order, link=bf16):
    pieces = dict(enumerate(pieces))
    for bit in order:
        flag = 1 << bit
        for m in [m for m in pieces if m & flag]:
            arrived = swap_mask(pieces.pop(m).astype(link), axis, flag)
            pieces[m ^ flag] = pieces[m ^ flag].astype(f32) + arrived.astype(f32)
    return pieces[0]


def core_orders():
    bits = list(range(bit_count(lax.axis_size("dp"))))
    return bits, bits[1:] + bits[:1]


def place_mask(place):
    masks = []
    for order in core_orders():
        masks.append(sum(1 << bit for at, bit in enumerate(order) if (place >> at) & 1))
    return jnp.where(lax.axis_index("mp") % 2 == 0, masks[0], masks[1])


def place_index(place):
    return lax.axis_index("dp") ^ place_mask(place)


def core_hop(values, at):
    orders, cores = core_orders(), lax.axis_size("mp")
    pairs = []
    for i in range(lax.axis_size("dp")):
        for core in range(cores):
            partner = i ^ (1 << orders[core % 2][at])
            pairs.append((i * cores + core, partner * cores + core))
    return lax.ppermute(values, ("dp", "mp"), pairs)


def group_hop(pieces, at):
    return jnp.concatenate([pieces, core_hop(pieces, at)], axis=0)


def place_of(core):
    partner = jnp.arange(lax.axis_size("dp")) ^ lax.axis_index("dp")
    places = []
    for order in core_orders():
        places.append(sum(((partner >> bit) & 1) << at for at, bit in enumerate(order)))
    return jnp.where(core % 2 == 0, places[0], places[1])


def reorder_masked(stacked, axis):
    count = bit_count(stacked.shape[0])
    here = lax.axis_index(axis)
    shape = stacked.shape
    values = stacked.reshape((2,) * count + shape[1:])
    for bit in range(count):
        turned = jnp.flip(values, count - 1 - bit)
        values = jnp.where(((here >> bit) & 1) == 1, turned, values)
    return values.reshape(shape)


def gather_small(values, axes):
    shape = values.shape
    values = values[None]
    for axis in reversed(axes):
        order = range(bit_count(lax.axis_size(axis)))
        stacked = jnp.stack(gather_masked(values, axis, order))
        values = reorder_masked(stacked, axis)
        values = values.reshape((-1,) + shape)
    return values


def scatter_small(values, axes):
    for axis in axes:
        size = lax.axis_size(axis)
        values = values.reshape((size, values.shape[0] // size) + values.shape[1:])
        turned = reorder_masked(values, axis)
        order = reversed(range(bit_count(size)))
        values = scatter_masked([turned[m] for m in range(size)], axis, order, f32)
    return values[0]


def line_size():
    return lax.axis_size("depth"), lax.axis_index("depth")


def fence(*values):
    return lax.optimization_barrier(values)


class LineGather:

    def __init__(self, values):
        self.up, self.down = [values], [values]

    def step(self):
        size, _ = line_size()
        at = len(self.up)
        if at < size:
            up_pairs = [(i, i + 1) for i in range(at - 1, size - 1)]
            down_pairs = [(i, i - 1) for i in range(1, size - at + 1)]
            self.up.append(lax.ppermute(self.up[-1], "depth", up_pairs))
            self.down.append(lax.ppermute(self.down[-1], "depth", down_pairs))

    def hold(self, *others):
        kept = fence((self.up[1:], self.down[1:]), *others)
        (up, down), rest = kept[0], kept[1:]
        self.up, self.down = self.up[:1] + list(up), self.down[:1] + list(down)
        return rest

    def placed(self):
        size, here = line_size()
        steps = jnp.arange(size)
        index = lax.rem(here - steps + size, size)
        return place_line(index, here >= steps, self.up, self.down[1:][::-1])


class LineScatter:

    def __init__(self, terms):
        self.terms, self.at = terms, 0
        self.up = self.down = None

    def step(self, *later):
        size, here = line_size()
        self.at += 1
        if self.at >= size:
            return later
        goes_up, goes_down = hop_sums(
            self.terms,
            jnp.minimum(size - self.at + here, size - 1),
            jnp.maximum(here - size + self.at, 0),
            self.up,
            self.down,
        )
        (goes_up, goes_down), *later = fence((goes_up, goes_down), *later)
        up_pairs = [(i, i + 1) for i in range(min(self.at, size - 1))]
        down_pairs = [(size - 1 - i, size - 2 - i) for i in range(min(self.at, size - 1))]
        self.up = lax.ppermute(goes_up, "depth", up_pairs)
        self.down = lax.ppermute(goes_down, "depth", down_pairs)
        return later

    def step_with(self, line, *later):
        size, here = line_size()
        lead, _, tall, wide = self.terms.shape
        shape = line.up[0].shape
        if (
            len(line.up) != self.at + 2
            or self.at + 2 > size - 1
            or math.prod(shape) != lead * tall * wide
            or shape[2] != wide
        ):
            line.step()
            return self.step(*later)
        self.at += 1
        goes = hop_sums(
            self.terms,
            jnp.minimum(size - self.at + here, size - 1),
            jnp.maximum(here - size + self.at, 0),
            self.up,
            self.down,
            [v[-1].reshape(lead, tall, wide) for v in (line.up, line.down)],
            [here < self.at, here > size - 1 - self.at],
        )
        goes, *later = fence(goes, *later)
        self.up = lax.ppermute(goes[0], "depth", [(i, i + 1) for i in range(size - 1)])
        self.down = lax.ppermute(goes[1], "depth", [(i, i - 1) for i in range(1, size)])
        line.up.append(self.up.reshape(shape))
        line.down.append(self.down.reshape(shape))
        return later

    def hold(self, *others):
        (self.up, self.down), *rest = fence((self.up, self.down), *others)
        return rest


def other_core(values):
    return swap_mask(values, "mp", 1)


def join_kernel(model_ref, own_ref, other_ref, out_ref):
    width = own_ref.shape[1]
    own_at = pl.multiple_of(model_ref[0] * width, width)
    other_at = pl.multiple_of((1 - model_ref[0]) * width, width)
    out_ref[:, pl.ds(own_at, width)] = own_ref[...]
    out_ref[:, pl.ds(other_at, width)] = other_ref[...]


def join_halves(own, other, model_at):
    tall, width = own.shape
    rows = min(256, tall)
    return pl.pallas_call(
        join_kernel,
        grid_spec=pltpu.PrefetchScalarGridSpec(
            num_scalar_prefetch=1,
            grid=(tall // rows,),
            in_specs=[pl.BlockSpec((rows, width), lambda i, m: (i, 0))] * 2,
            out_specs=pl.BlockSpec((rows, 2 * width), lambda i, m: (i, 0)),
        ),
        out_shape=jax.ShapeDtypeStruct((tall, 2 * width), own.dtype),
        cost_estimate=spent(
            flops=0, bytes_accessed=8 * tall * width, transcendentals=0
        ),
        name="join_halves",
    )(model_at.astype(jnp.int32)[None], own, other)


def spent(flops, bytes_accessed, transcendentals):
    return pl.CostEstimate(
        flops=flops // COST, bytes_accessed=bytes_accessed // COST, transcendentals=transcendentals // COST
    )


def chunk_of(tall, wide):
    rows = tall
    while rows * wide > 1 << 19 and rows % 32 == 0:
        rows //= 2
    return rows


def place_kernel(at_ref, *refs):
    if len(refs) < 4:
        refs[-1][0, 0] = refs[0][0]
        return

    @pl.when(at_ref[1] == 1)
    def _():
        refs[-1][0, 0] = refs[0][0]

    @pl.when(at_ref[1] == 0)
    def _():
        refs[-1][0, 0] = refs[1][0]


def place_block(buffer, block, index, count, instead=None, first=None):
    lead, tall, wide = block.shape
    rows = chunk_of(tall, wide)
    spec = pl.BlockSpec((1, rows, wide), lambda l, i, m: (l, i, 0))
    blocks = [block] if instead is None else [block, instead]
    where = [index, 1 if first is None else first]
    where = jnp.stack([jnp.asarray(v).astype(jnp.int32) for v in where])
    in_specs, operands, aliases = [spec] * len(blocks), list(blocks), {}
    if buffer is not None or instead is not None:
        in_specs.append(pl.BlockSpec(memory_space=pl.ANY))
        operands.append(block if buffer is None else buffer)
        aliases = {} if buffer is None else {len(operands): 0}
    return pl.pallas_call(
        place_kernel,
        grid_spec=pltpu.PrefetchScalarGridSpec(
            num_scalar_prefetch=1,
            grid=(lead, tall // rows),
            in_specs=in_specs,
            out_specs=pl.BlockSpec((1, 1, rows, wide), lambda l, i, m: (l, m[0], i, 0)),
        ),
        out_shape=jax.ShapeDtypeStruct((lead, count, tall, wide), block.dtype),
        input_output_aliases=aliases,
        cost_estimate=spent(
            flops=0, bytes_accessed=4 * lead * tall * wide, transcendentals=0
        ),
        name="place_block",
    )(where, *operands)


def place_line_kernel(size, at_ref, *refs):
    out_ref = refs[-1]
    for step in range(size):
        if step == 0 or len(refs) == size + 1:
            out_ref[0, at_ref[step]] = refs[step][0]
            continue

        @pl.when(at_ref[size + step] == 1)
        def _(step=step):
            out_ref[0, at_ref[step]] = refs[step][0]

        @pl.when(at_ref[size + step] == 0)
        def _(step=step):
            out_ref[0, at_ref[step]] = refs[size + step - 1][0]


def place_line(index, first, blocks, instead):
    size = len(blocks)
    lead, tall, wide = blocks[0].shape
    rows = tall
    while rows * wide > 1 << 18 and rows % 32 == 0:
        rows //= 2
    spec = pl.BlockSpec((1, rows, wide), lambda l, i, m: (l, i, 0))
    where = jnp.concatenate([index, first]).astype(jnp.int32)
    operands = list(blocks) + list(instead)
    return pl.pallas_call(
        functools.partial(place_line_kernel, size),
        grid_spec=pltpu.PrefetchScalarGridSpec(
            num_scalar_prefetch=1,
            grid=(lead, tall // rows),
            in_specs=[spec] * len(operands),
            out_specs=pl.BlockSpec((1, size, rows, wide), lambda l, i, m: (l, 0, i, 0)),
        ),
        out_shape=jax.ShapeDtypeStruct((lead, size, tall, wide), blocks[0].dtype),
        compiler_params=pltpu.CompilerParams(vmem_limit_bytes=40 << 20),
        cost_estimate=spent(
            flops=0, bytes_accessed=6 * size * lead * tall * wide, transcendentals=0
        ),
        name="place_line",
    )(where, *operands)


def place_many(index, blocks):
    ones = jnp.ones(len(blocks), jnp.int32)
    return place_line(index, ones, blocks, [])


def group_join_kernel(at_ref, own_ref, other_ref, out_ref):
    width = own_ref.shape[2]
    own_span, other_span = own_spans(at_ref, width)
    out_ref[:, own_span] = own_ref[0]
    out_ref[:, other_span] = other_ref[0]


def group_join(own, other, model_at):
    count, tall, width = own.shape
    rows = chunk_of(tall, width)
    per = tall // rows
    where = jnp.concatenate([model_at[None], place_of(model_at), place_of(1 - model_at)])
    return pl.pallas_call(
        group_join_kernel,
        grid_spec=pltpu.PrefetchScalarGridSpec(
            num_scalar_prefetch=1,
            grid=(count, per),
            in_specs=[
                pl.BlockSpec((1, rows, width), lambda n, i, m: (m[1 + n], i, 0)),
                pl.BlockSpec((1, rows, width), lambda n, i, m: (m[1 + count + n], i, 0)),
            ],
            out_specs=pl.BlockSpec((rows, 2 * width), lambda n, i, m: (n * per + i, 0)),
        ),
        out_shape=jax.ShapeDtypeStruct((count * tall, 2 * width), own.dtype),
        cost_estimate=spent(
            flops=0, bytes_accessed=8 * count * tall * width, transcendentals=0
        ),
        name="group_join",
    )(where.astype(jnp.int32), own, other)


def group_split_kernel(at_ref, near_own, near_other, far_own, far_other, near_ref, far_ref):
    near_ref[0, 0] = near_own[0] + near_other[0].astype(f32)
    far_ref[0, 0] = (far_own[0] + far_other[0].astype(f32)).astype(bf16)


def group_split(own, other, places):
    _, tall, width = own.shape
    count = places.shape[0]
    half, rows = count // 2, tall // count
    near = pl.BlockSpec((1, rows, width), lambda p, k, m: (k, m[p], 0))
    far = pl.BlockSpec((1, rows, width), lambda p, k, m: (k, m[half + p], 0))
    out = pl.BlockSpec((1, 1, rows, width), lambda p, k, m: (p, k, 0, 0))
    return pl.pallas_call(
        group_split_kernel,
        grid_spec=pltpu.PrefetchScalarGridSpec(
            num_scalar_prefetch=1,
            grid=(half, 2),
            in_specs=[near, near, far, far],
            out_specs=[out, out],
        ),
        out_shape=[
            jax.ShapeDtypeStruct((half, 2, rows, width), f32),
            jax.ShapeDtypeStruct((half, 2, rows, width), bf16),
        ],
        cost_estimate=spent(
            flops=2 * tall * width, bytes_accessed=20 * tall * width, transcendentals=0
        ),
        name="group_split",
    )(places, own, other, own, other)


def hop_kernel(has_sums, has_blocks, at_ref, *refs):
    ins, outs = list(refs[:-2]), refs[-2:]
    terms, ins = ins[:2], ins[2:]
    sums, ins = (ins[:2], ins[2:]) if has_sums else (None, ins)

    def send_sum(way):
        term = terms[way][0, 0].astype(f32)
        if sums is not None:
            term = term + sums[way][0].astype(f32)
        outs[way][0] = term.astype(bf16)

    for way in range(2):
        if not has_blocks:
            send_sum(way)
            continue
        pl.when(at_ref[2 + way] == 1)(functools.partial(send_sum, way))

        @pl.when(at_ref[2 + way] == 0)
        def _(way=way):
            outs[way][0] = ins[way][0]


def hop_sums(terms, up_at, down_at, up, down, blocks=None, first=None):
    lead, _, tall, wide = terms.shape
    rows = chunk_of(tall, wide)
    block = pl.BlockSpec((1, rows, wide), lambda l, i, m: (l, i, 0))
    in_specs = [
        pl.BlockSpec((1, 1, rows, wide), lambda l, i, m: (l, m[0], i, 0)),
        pl.BlockSpec((1, 1, rows, wide), lambda l, i, m: (l, m[1], i, 0)),
    ]
    operands = [terms, terms]
    where = [up_at, down_at]
    if up is not None:
        in_specs += [block, block]
        operands += [up, down]
    if blocks is not None:
        in_specs += [block, block]
        operands += list(blocks)
        where += list(first)
    return pl.pallas_call(
        functools.partial(hop_kernel, up is not None, blocks is not None),
        grid_spec=pltpu.PrefetchScalarGridSpec(
            num_scalar_prefetch=1,
            grid=(lead, tall // rows),
            in_specs=in_specs,
            out_specs=[block, block],
        ),
        out_shape=[jax.ShapeDtypeStruct((lead, tall, wide), bf16)] * 2,
        cost_estimate=spent(
            flops=2 * lead * tall * wide, bytes_accessed=12 * lead * tall * wide, transcendentals=0
        ),
        name="hop_sums",
    )(jnp.stack(where).astype(jnp.int32), *operands)


def end_kernel(at_ref, term_ref, up_ref, down_ref, out_ref):
    total = term_ref[0, 0].astype(f32) + up_ref[0].astype(f32) + down_ref[0].astype(f32)
    out_ref[0] = total.astype(out_ref.dtype)


def end_sums(sums, dtype):
    lead, _, tall, wide = sums.terms.shape
    rows = chunk_of(tall, wide)
    block = pl.BlockSpec((1, rows, wide), lambda l, i, m: (l, i, 0))
    return pl.pallas_call(
        end_kernel,
        grid_spec=pltpu.PrefetchScalarGridSpec(
            num_scalar_prefetch=1,
            grid=(lead, tall // rows),
            in_specs=[
                pl.BlockSpec((1, 1, rows, wide), lambda l, i, m: (l, m[0], i, 0)),
                block,
                block,
            ],
            out_specs=block,
        ),
        out_shape=jax.ShapeDtypeStruct((lead, tall, wide), dtype),
        cost_estimate=spent(
            flops=2 * lead * tall * wide, bytes_accessed=10 * lead * tall * wide, transcendentals=0
        ),
        name="end_sums",
    )(lax.axis_index("depth").astype(jnp.int32)[None], sums.terms, sums.up, sums.down)


def attention_grad_kernel(
    at_ref, x0_ref, x1_ref, cot_ref, g0_ref, g1_ref, out_ref
):
    tall = x0_ref.shape[1]

    def store(total):
        out_ref[...] = total.reshape(out_ref.shape).astype(out_ref.dtype)

    @pl.when(pl.program_id(0) < 3)
    def _():
        store(dot_tn(x0_ref[0], g0_ref[0]) + dot_tn(x1_ref[0], g1_ref[0]))

    @pl.when(pl.program_id(0) == 3)
    def _():
        store(
            dot_tn(cot_ref[0:tall, :], g0_ref[0]) + dot_tn(cot_ref[tall : 2 * tall, :], g1_ref[0])
        )


def attention_grads(normed, cot, flat, place, depth_count, dp_count, dtype):
    _, tall, model = normed[0].shape
    heads_width = flat[0].shape[2]
    block = model // dp_count
    own_rows = block // depth_count
    normed_spec = pl.BlockSpec((1, tall, block), lambda k, m: (jnp.minimum(k, 2), 0, m[0]))
    flat_spec = pl.BlockSpec((1, tall, heads_width), lambda k, m: (lax.rem(k + 1, 4), 0, 0))
    return pl.pallas_call(
        attention_grad_kernel,
        grid_spec=pltpu.PrefetchScalarGridSpec(
            num_scalar_prefetch=1,
            grid=(4,),
            in_specs=[
                normed_spec,
                normed_spec,
                pl.BlockSpec((2 * tall, block), lambda k, m: (0, m[0])),
                flat_spec,
                flat_spec,
            ],
            out_specs=pl.BlockSpec(
                (depth_count, 1, own_rows, heads_width), lambda k, m: (0, k, 0, 0)
            ),
        ),
        out_shape=jax.ShapeDtypeStruct((depth_count, 4, own_rows, heads_width), dtype),
        compiler_params=pltpu.CompilerParams(vmem_limit_bytes=40 << 20),
        cost_estimate=spent(
            flops=16 * tall * block * heads_width,
            bytes_accessed=16 * block * heads_width,
            transcendentals=0,
        ),
        name="attention_grads",
    )(place, *normed, cot, *flat)


def hidden_grad_kernel(x0_ref, x1_ref, c0_ref, c1_ref, u0_ref, u1_ref, h0_ref, h1_ref, out_ref):
    def store(total):
        out_ref[...] = total.reshape(out_ref.shape)

    @pl.when(pl.program_id(0) == 0)
    def _():
        store(dot_tn(x0_ref[...], u0_ref[...]) + dot_tn(x1_ref[...], u1_ref[...]))

    @pl.when(pl.program_id(0) == 1)
    def _():
        tall, wide = h0_ref.shape[0], c0_ref.shape[3]
        c0, c1 = c0_ref[:, 0].reshape(tall, wide), c1_ref[:, 0].reshape(tall, wide)
        store(dot_tn(c0, h0_ref[...]) + dot_tn(c1, h1_ref[...]))


def hidden_grads(x, cot, up_grads, hidden, dp_count, depth_count):
    tall, model = x[0].shape
    part = hidden[0].shape[1]
    block = model // dp_count
    cols = pl.BlockSpec((tall, block), lambda k, n: (0, n * (1 - k)))
    whole = pl.BlockSpec((tall, part), lambda k, n: (0, 0))
    return pl.pallas_call(
        hidden_grad_kernel,
        grid=(2, dp_count),
        in_specs=[cols, cols]
        + [
            pl.BlockSpec((dp_count, 1, cot.shape[2], block), lambda k, n: (0, 0, 0, n * k)),
            pl.BlockSpec((dp_count, 1, cot.shape[2], block), lambda k, n: (0, 1, 0, n * k)),
        ]
        + [whole] * 4,
        out_specs=pl.BlockSpec(
            (1, depth_count, block // depth_count, part), lambda k, n: (k * dp_count + n, 0, 0, 0)
        ),
        out_shape=jax.ShapeDtypeStruct(
            (2 * dp_count, depth_count, block // depth_count, part), f32
        ),
        compiler_params=pltpu.CompilerParams(vmem_limit_bytes=48 << 20),
        cost_estimate=spent(
            flops=8 * tall * model * part, bytes_accessed=8 * model * part, transcendentals=0
        ),
        name="hidden_grads",
    )(*x, cot, cot, *up_grads, *hidden)


def mix_kernel(slots, mix_ref, hist_ref, out_ref):
    rows, width = hist_ref.shape[1], hist_ref.shape[2]
    part = 512 if width % 512 == 0 else width

    def step(at, carry):
        r0 = pl.multiple_of(at * 16, 16)
        weights = mix_ref[pl.ds(r0, 16), :]
        for c0 in range(0, width, part):
            sums = [None] * STREAMS
            for k in range(slots):
                state = hist_ref[k, pl.ds(r0, 16), c0 : c0 + part].astype(f32)
                for s in range(STREAMS):
                    term = weights[:, s * slots + k : s * slots + k + 1] * state
                    sums[s] = term if sums[s] is None else sums[s] + term
            for s in range(STREAMS):
                out_ref[s, pl.ds(r0, 16), c0 : c0 + part] = sums[s].astype(bf16)
        return carry

    lax.fori_loop(0, rows // 16, step, 0)


def mix_streams(slot_mix, history, micro_at, depth_count, rows_mb):
    slots, _, width = history.shape
    rows = min(128, rows_mb)
    per = rows_mb // rows

    def row_block(i):
        return ((i // per) * MB + micro_at) * per + i % per

    return pl.pallas_call(
        functools.partial(mix_kernel, slots),
        grid=(depth_count * per,),
        in_specs=[
            pl.BlockSpec((rows, slot_mix.shape[1]), lambda i: (row_block(i), 0)),
            pl.BlockSpec((slots, rows, width), lambda i: (0, row_block(i), 0)),
        ],
        out_specs=pl.BlockSpec((STREAMS, rows, width), lambda i: (0, i, 0)),
        out_shape=jax.ShapeDtypeStruct((STREAMS, depth_count * rows_mb, width), bf16),
        cost_estimate=spent(
            flops=2 * slots * STREAMS * depth_count * rows_mb * width,
            bytes_accessed=2 * (slots + STREAMS) * depth_count * rows_mb * width,
            transcendentals=0,
        ),
        name="mix_streams",
    )(slot_mix, history)


def unmix_kernel(slots, mix_ref, hist_ref, grad_ref, *rest):
    hist_grad_ref, slot_grad_ref = rest[-2:]
    rows, width = hist_ref.shape[1], hist_ref.shape[2]
    part = 512 if width % 512 == 0 else width

    def step(at, carry):
        r0 = pl.multiple_of(at * 16, 16)
        weights = mix_ref[pl.ds(r0, 16), :]
        totals = [None] * (STREAMS * slots)
        for c0 in range(0, width, part):
            grads = [
                grad_ref[s, pl.ds(r0, 16), c0 : c0 + part].astype(f32)
                for s in range(STREAMS)
            ]
            for k in range(slots):
                state = hist_ref[k, pl.ds(r0, 16), c0 : c0 + part].astype(f32)
                back = None
                for s in range(STREAMS):
                    at_sk = s * slots + k
                    term = weights[:, at_sk : at_sk + 1] * grads[s]
                    back = term if back is None else back + term
                    product = state * grads[s]
                    folded = product[:, 0:128]
                    for l0 in range(128, part, 128):
                        folded = folded + product[:, l0 : l0 + 128]
                    totals[at_sk] = folded if totals[at_sk] is None else totals[at_sk] + folded
                hist_grad_ref[k, pl.ds(r0, 16), c0 : c0 + part] = back.astype(bf16)
        lane = lax.broadcasted_iota(jnp.int32, (16, 128), 1)
        packed = jnp.zeros((16, 128), f32)
        for at_sk in range(STREAMS * slots):
            column = jnp.sum(totals[at_sk], axis=1, keepdims=True)
            packed = jnp.where(lane == at_sk, column, packed)
        slot_grad_ref[pl.ds(r0, 16), :] = packed
        return carry

    lax.fori_loop(0, rows // 16, step, 0)


def unmix_streams(slot_mix, history, grads, micro_at, depth_count, rows_mb, earlier):
    slots, tokens, width = history.shape
    rows = min(128, rows_mb)
    per = rows_mb // rows

    def row_block(i):
        return ((i // per) * MB + micro_at) * per + i % per

    in_specs = [
        pl.BlockSpec((rows, slot_mix.shape[1]), lambda i: (row_block(i), 0)),
        pl.BlockSpec((slots, rows, width), lambda i: (0, row_block(i), 0)),
        pl.BlockSpec((STREAMS, rows, width), lambda i: (0, i, 0)),
    ]
    operands = [slot_mix, history, grads]
    aliases = {}
    if earlier is not None:
        in_specs.append(pl.BlockSpec(memory_space=pl.ANY))
        operands.append(earlier)
        aliases = {3: 0}
    return pl.pallas_call(
        functools.partial(unmix_kernel, slots),
        grid=(depth_count * per,),
        in_specs=in_specs,
        out_specs=[
            pl.BlockSpec((slots, rows, width), lambda i: (0, row_block(i), 0)),
            pl.BlockSpec((rows, 128), lambda i: (i, 0)),
        ],
        out_shape=[
            jax.ShapeDtypeStruct((slots, tokens, width), bf16),
            jax.ShapeDtypeStruct((depth_count * rows_mb, 128), f32),
        ],
        input_output_aliases=aliases,
        cost_estimate=spent(
            flops=4 * slots * STREAMS * depth_count * rows_mb * width,
            bytes_accessed=2 * (2 * slots + STREAMS) * depth_count * rows_mb * width,
            transcendentals=0,
        ),
        name="unmix_streams",
    )(*operands)


def own_spans(model_ref, width):
    own_at = pl.multiple_of(model_ref[0] * width, width)
    other_at = pl.multiple_of((1 - model_ref[0]) * width, width)
    return pl.ds(own_at, width), pl.ds(other_at, width)


def ff_split_kernel(at_ref, up_ref, down_ref, out_ref):
    out_ref[0, 0] = up_ref[...]
    out_ref[0, 1] = down_ref[...].T


def ff_split(up_weight, down_weight, partners):
    own_rows, ff_width = up_weight.shape
    count = partners.shape[0]
    part = ff_width // count
    return pl.pallas_call(
        ff_split_kernel,
        grid_spec=pltpu.PrefetchScalarGridSpec(
            num_scalar_prefetch=1,
            grid=(count,),
            in_specs=[
                pl.BlockSpec((own_rows, part), lambda i, m: (0, m[i])),
                pl.BlockSpec((part, own_rows), lambda i, m: (m[i], 0)),
            ],
            out_specs=pl.BlockSpec((1, 2, own_rows, part), lambda i, m: (i, 0, 0, 0)),
        ),
        out_shape=jax.ShapeDtypeStruct((count, 2, own_rows, part), bf16),
        cost_estimate=spent(flops=0, bytes_accessed=8 * own_rows * ff_width, transcendentals=0),
        name="ff_split",
    )(partners, up_weight, down_weight)


def ff_join_kernel(at_ref, piece_ref, up_ref, down_ref):
    up_ref[...] = piece_ref[0, 0].astype(f32)
    down_ref[...] = piece_ref[0, 1].astype(f32).T


def ff_join(pieces, partners):
    count, _, own_rows, part = pieces.shape
    return pl.pallas_call(
        ff_join_kernel,
        grid_spec=pltpu.PrefetchScalarGridSpec(
            num_scalar_prefetch=1,
            grid=(count,),
            in_specs=[pl.BlockSpec((1, 2, own_rows, part), lambda i, m: (i, 0, 0, 0))],
            out_specs=[
                pl.BlockSpec((own_rows, part), lambda i, m: (0, m[i])),
                pl.BlockSpec((part, own_rows), lambda i, m: (m[i], 0)),
            ],
        ),
        out_shape=[
            jax.ShapeDtypeStruct((own_rows, count * part), f32),
            jax.ShapeDtypeStruct((count * part, own_rows), f32),
        ],
        cost_estimate=spent(
            flops=0, bytes_accessed=12 * own_rows * count * part, transcendentals=0
        ),
        name="ff_join",
    )(partners, pieces)


def total_kernel(depth_ref, part_ref, up_ref, down_ref, cur_ref, last_ref, low_ref, resid_ref):
    width = resid_ref.shape[1]
    current = cur_ref[...].astype(f32)
    for s in range(STREAMS):
        lanes = slice(s * width, (s + 1) * width)
        total = part_ref[s, 0].astype(f32)
        total = total + up_ref[s].astype(f32) + down_ref[s].astype(f32)
        total = total + last_ref[:, s : s + 1] * current
        if s == STREAMS - 1:
            resid_ref[...] = total
        low_ref[:, lanes] = total.astype(bf16)


def total_streams(sums, current_half, last, depth_at):
    _, _, tall, width = sums.terms.shape
    wide = STREAMS * width
    rows = min(64, tall)
    row = lambda i, d: (i, 0)
    return pl.pallas_call(
        total_kernel,
        grid_spec=pltpu.PrefetchScalarGridSpec(
            num_scalar_prefetch=1,
            grid=(tall // rows,),
            in_specs=[
                pl.BlockSpec((STREAMS, 1, rows, width), lambda i, d: (0, d[0], i, 0)),
                pl.BlockSpec((STREAMS, rows, width), lambda i, d: (0, i, 0)),
                pl.BlockSpec((STREAMS, rows, width), lambda i, d: (0, i, 0)),
                pl.BlockSpec((rows, width), row),
                pl.BlockSpec((rows, 128), row),
            ],
            out_specs=[pl.BlockSpec((rows, wide), row), pl.BlockSpec((rows, width), row)],
        ),
        out_shape=[
            jax.ShapeDtypeStruct((tall, wide), bf16),
            jax.ShapeDtypeStruct((tall, width), f32),
        ],
        cost_estimate=spent(flops=5 * tall * wide, bytes_accessed=9 * tall * wide, transcendentals=0),
        name="total_streams",
    )(depth_at, sums.terms, sums.up, sums.down, current_half, last)


def norm_kernel(model_ref, own_ref, other_ref, gain_ref, normed_ref, ff_ref, stat_ref):
    rows, width = ff_ref.shape
    model = 2 * width
    own_span, other_span = own_spans(model_ref, width)
    lane = lax.broadcasted_iota(jnp.int32, (rows, 128), 1)
    stats = jnp.zeros((rows, 128), f32)
    for s in range(STREAMS):
        lanes = slice(s * width, (s + 1) * width)
        own = own_ref[:, lanes].astype(f32)
        other = other_ref[:, lanes].astype(f32)
        average = (
            jnp.sum(own, axis=-1, keepdims=True) + jnp.sum(other, axis=-1, keepdims=True)
        ) / model
        own, other = own - average, other - average
        variance = (
            jnp.sum(own * own, axis=-1, keepdims=True)
            + jnp.sum(other * other, axis=-1, keepdims=True)
        ) / model
        inverse = lax.rsqrt(variance + NORM_EPSILON)
        stats = jnp.where(lane == 2 * s, average, stats)
        stats = jnp.where(lane == 2 * s + 1, inverse, stats)
        norm_own = (own * inverse * gain_ref[s : s + 1, own_span]).astype(bf16)
        if s == STREAMS - 1:
            ff_ref[...] = norm_own
        else:
            normed_ref[s, :, own_span] = norm_own
            norm_other = (other * inverse * gain_ref[s : s + 1, other_span]).astype(bf16)
            normed_ref[s, :, other_span] = norm_other
    stat_ref[...] = stats


def norm_streams(low, low_other, gains, which):
    tall, wide = low.shape
    width = wide // STREAMS
    rows = min(64, tall)
    row = lambda i, m: (i, 0)
    return pl.pallas_call(
        norm_kernel,
        grid_spec=pltpu.PrefetchScalarGridSpec(
            num_scalar_prefetch=1,
            grid=(tall // rows,),
            in_specs=[
                pl.BlockSpec((rows, wide), row),
                pl.BlockSpec((rows, wide), row),
                pl.BlockSpec(gains.shape, lambda i, m: (0, 0)),
            ],
            out_specs=[
                pl.BlockSpec((3, rows, 2 * width), lambda i, m: (0, i, 0)),
                pl.BlockSpec((rows, width), row),
                pl.BlockSpec((rows, 128), row),
            ],
        ),
        out_shape=[
            jax.ShapeDtypeStruct((3, tall, 2 * width), bf16),
            jax.ShapeDtypeStruct((tall, width), bf16),
            jax.ShapeDtypeStruct((tall, 128), f32),
        ],
        cost_estimate=spent(
            flops=20 * tall * wide, bytes_accessed=8 * tall * wide, transcendentals=0
        ),
        name="norm_streams",
    )(which, low, low_other, gains)


def turn(values, cosine, sine_up, sine_down, sign):
    up = pltpu.roll(values, HDIM - ROT // 2, 1)
    down = pltpu.roll(values, ROT // 2, 1)
    return values * cosine + sign * (up * sine_up + down * sine_down)


def project_kernel(
    x_ref, cot_ref, wq_ref, wk_ref, wv_ref, wo_ref, cos_ref, up_ref, down_ref, out_ref
):
    span = wq_ref.shape[-1]
    tables = cos_ref[...], up_ref[...], down_ref[...]
    for kind, w_ref in enumerate((wq_ref, wk_ref, wv_ref, wo_ref)):
        rows = cot_ref[...] if kind == 3 else x_ref[kind]
        product = dot_nn(rows, w_ref[...].reshape(-1, span))
        for begin in range(0, span, HDIM):
            head = product[:, begin : begin + HDIM]
            if kind < 2:
                head = turn(head, *tables, 1.0)
            out_ref[0, :, kind * span + begin : kind * span + begin + HDIM] = head.astype(bf16)


def project_heads(normed, cot, weights, tables, depth_count):
    _, rows, model = normed.shape
    groups, _, _, own_rows, heads_width = weights.shape
    span = heads_width // depth_count
    whole = lambda j: (0, 0)

    def matrix(kind):
        shape = (groups, depth_count, 1, own_rows, span)
        return pl.BlockSpec(shape, lambda j: (0, 0, kind, 0, j))

    return pl.pallas_call(
        project_kernel,
        grid=(depth_count,),
        in_specs=[
            pl.BlockSpec((3, rows, model), lambda j: (0, 0, 0)),
            pl.BlockSpec((rows, model), whole),
        ]
        + [matrix(kind) for kind in range(4)]
        + [pl.BlockSpec((rows, HDIM), whole)] * 3,
        out_specs=pl.BlockSpec((1, rows, 4 * span), lambda j: (j, 0, 0)),
        out_shape=jax.ShapeDtypeStruct((depth_count, rows, 4 * span), bf16),
        compiler_params=pltpu.CompilerParams(vmem_limit_bytes=40 << 20),
        cost_estimate=spent(
            flops=8 * rows * model * span * depth_count,
            bytes_accessed=8 * model * span * depth_count + 8 * rows * model,
            transcendentals=0,
        ),
        name="project_heads",
    )(normed, cot, *[weights] * 4, *tables)


def attend_kernel(
    block, q_ref, k_ref, v_ref, g_ref, doc_col_ref, doc_row_ref, cos_ref, up_ref, down_ref,
    out_ref, dk_sum, dv_sum,
):
    length = q_ref.shape[0]
    scale = HDIM**-0.5
    heads_each = out_ref.shape[1] // (4 * HDIM)

    def lanes(kind):
        return pl.ds(pl.multiple_of((kind * heads_each + pl.program_id(0)) * HDIM, HDIM), HDIM)

    for begin in range(0, length, block):
        end = begin + block
        rows = slice(begin, end)
        queries, grads = q_ref[rows, :], g_ref[rows, :]
        keys, values = k_ref[0:end, :], v_ref[0:end, :]
        scores = dot_nt(queries, keys) * scale
        place_q = begin + lax.broadcasted_iota(jnp.int32, scores.shape, 0)
        place_k = lax.broadcasted_iota(jnp.int32, scores.shape, 1)
        allowed = (doc_col_ref[rows, :] == doc_row_ref[:, 0:end]) & (place_q >= place_k)
        scores = jnp.where(allowed, scores, MASKED)
        highest = jnp.max(scores, axis=-1, keepdims=True)
        exponent = jnp.exp(scores - highest)
        totals = jnp.sum(exponent, axis=-1, keepdims=True)
        attention = exponent * (1.0 / totals)
        low = attention.astype(bf16)
        out_ref[rows, lanes(0)] = dot_nn(low, values).astype(bf16)
        grad_att = dot_nt(grads, values).astype(bf16).astype(f32)
        weighted = jnp.sum(attention * grad_att, axis=-1, keepdims=True)
        grad_scores = (attention * (grad_att - weighted)).astype(bf16)
        grad_q = dot_nn(grad_scores, keys) * scale
        out_ref[rows, lanes(1)] = turn(
            grad_q, cos_ref[rows, :], up_ref[rows, :], down_ref[rows, :], -1.0
        ).astype(bf16)
        part_k = dot_tn(grad_scores, queries)
        part_v = dot_tn(low, grads)
        if begin > 0:
            dk_sum[0:begin, :] += part_k[0:begin]
            dv_sum[0:begin, :] += part_v[0:begin]
        dk_sum[begin:end, :] = part_k[begin:end]
        dv_sum[begin:end, :] = part_v[begin:end]
    grad_k = dk_sum[...] * scale
    out_ref[:, lanes(2)] = turn(grad_k, cos_ref[...], up_ref[...], down_ref[...], -1.0).astype(bf16)
    out_ref[:, lanes(3)] = dv_sum[...].astype(bf16)


def attend(packed, documents, tables, heads_each):
    length = packed.shape[0]
    block = min(256, length)
    whole = lambda h: (0, 0)

    def kind(at):
        return pl.BlockSpec((length, HDIM), lambda h: (0, at * heads_each + h))

    return pl.pallas_call(
        functools.partial(attend_kernel, block),
        grid=(heads_each,),
        in_specs=[kind(0), kind(1), kind(2), kind(3)]
        + [pl.BlockSpec((length, 1), whole), pl.BlockSpec((1, length), whole)]
        + [pl.BlockSpec((length, HDIM), whole)] * 3,
        out_specs=pl.BlockSpec((length, 4 * heads_each * HDIM), whole),
        out_shape=jax.ShapeDtypeStruct((length, 4 * heads_each * HDIM), bf16),
        scratch_shapes=[pltpu.VMEM((length, HDIM), f32)] * 2,
        compiler_params=pltpu.CompilerParams(vmem_limit_bytes=48 << 20),
        cost_estimate=spent(
            flops=9 * heads_each * length * length * HDIM,
            bytes_accessed=16 * length * heads_each * HDIM + 12 * length * HDIM,
            transcendentals=heads_each * length * length,
        ),
        name="attend",
    )(packed, packed, packed, packed, documents[:, None], documents[None, :], *tables)


def gelu_parts(values):
    cdf = 0.5 * (1.0 + lax.erf(values * (0.5**0.5)))
    density = jnp.exp(-0.5 * values * values) * (1.0 / math.sqrt(2.0 * math.pi))
    return values * cdf, cdf + values * density


def ff_kernel(
    model_ref, x_ref, cot_ref, up_ref, down_ref,
    hidden_ref, grad_ref, own_ref, other_ref,
):
    part = up_ref.shape[-1]
    half = up_ref.shape[1] // 2

    def rows_of(ref, which):
        return ref[0, pl.ds(which * half, half)].reshape(-1, part)

    own, other = model_ref[0], 1 - model_ref[0]
    up_pre = dot_nn(x_ref[...], up_ref[...].reshape(-1, part))
    hidden, slope = gelu_parts(up_pre)
    hidden = hidden.astype(bf16)
    grad_up = (dot_nn(cot_ref[0, 0], down_ref[...].reshape(-1, part)) * slope).astype(bf16)
    hidden_ref[...] = hidden
    grad_ref[...] = grad_up
    other_ref[0] = dot_nt(grad_up, rows_of(up_ref, other)).astype(bf16)
    own_ref[0] = dot_nt(grad_up, rows_of(up_ref, own))
    other_ref[1] = dot_nt(hidden, rows_of(down_ref, other)).astype(bf16)
    own_ref[1] = dot_nt(hidden, rows_of(down_ref, own))


def feed_forward(x, cot, micro_at, weights, which):
    tall, model = x.shape
    part = weights.shape[-1]
    width = model // 2
    rows = cot.shape[2]
    row = lambda i, m: (i, 0)

    def resident(kind):
        return pl.BlockSpec(
            (1,) + weights.shape[1:],
            lambda i, m: (kind, 0, 0, 0, 0),
            pipeline_mode=pl.Buffered(1),
        )

    return pl.pallas_call(
        ff_kernel,
        grid_spec=pltpu.PrefetchScalarGridSpec(
            num_scalar_prefetch=1,
            grid=(tall // rows,),
            in_specs=[
                pl.BlockSpec((rows, model), row),
                pl.BlockSpec((1, 1, rows, model), lambda i, m: (i, micro_at, 0, 0)),
                resident(0),
                resident(1),
            ],
            out_specs=[pl.BlockSpec((rows, part), row)] * 2
            + [pl.BlockSpec((2, rows, width), lambda i, m: (0, i, 0))] * 2,
        ),
        out_shape=[jax.ShapeDtypeStruct((tall, part), bf16)] * 2
        + [
            jax.ShapeDtypeStruct((2, tall, width), f32),
            jax.ShapeDtypeStruct((2, tall, width), bf16),
        ],
        compiler_params=pltpu.CompilerParams(vmem_limit_bytes=48 << 20),
        cost_estimate=spent(
            flops=8 * tall * model * part,
            bytes_accessed=4 * model * part + 16 * tall * model,
            transcendentals=2 * tall * part,
        ),
        name="feed_forward",
    )(which, x, cot, weights, weights)


def back_kernel(half_ref, ans_ref, wo_ref, wq_ref, wk_ref, wv_ref, out_ref, *flat):
    count, _, wide = ans_ref.shape
    span = wide // 4
    for kind, w_ref in enumerate((wo_ref, wq_ref, wk_ref, wv_ref)):
        total = None
        for j in range(count):
            term = dot_nt(
                ans_ref[j, :, kind * span : (kind + 1) * span],
                w_ref[:, :, :, :, j * span : (j + 1) * span].reshape(-1, span),
            )
            total = term if total is None else total + term
        out_ref[kind] = total.astype(out_ref.dtype)
    if flat:

        @pl.when(pl.program_id(0) == 0)
        def _():
            for kind in range(4):
                for j in range(count):
                    flat[0][kind, :, j * span : (j + 1) * span] = ans_ref[
                        j, :, kind * span : (kind + 1) * span
                    ]


def back_project(answer, weights, half, dtype, flat):
    count, rows, wide = answer.shape
    groups, _, _, own_rows, heads_width = weights.shape
    part = count * own_rows
    steps = groups // 2
    width = part * steps

    def matrix(kind):
        shape = (1, count, 1, own_rows, heads_width)
        return pl.BlockSpec(shape, lambda i, m: (m[0] * steps + i, 0, kind, 0, 0))

    out_specs = [pl.BlockSpec((4, rows, part), lambda i, m: (0, 0, i))]
    out_shape = [jax.ShapeDtypeStruct((4, rows, width), dtype)]
    if flat:
        out_specs.append(pl.BlockSpec((4, rows, heads_width), lambda i, m: (0, 0, 0)))
        out_shape.append(jax.ShapeDtypeStruct((4, rows, heads_width), bf16))
    return pl.pallas_call(
        back_kernel,
        grid_spec=pltpu.PrefetchScalarGridSpec(
            num_scalar_prefetch=1,
            grid=(steps,),
            in_specs=[pl.BlockSpec((count, rows, wide), lambda i, m: (0, 0, 0))]
            + [matrix(kind) for kind in (3, 0, 1, 2)],
            out_specs=out_specs,
        ),
        out_shape=out_shape,
        compiler_params=pltpu.CompilerParams(vmem_limit_bytes=40 << 20),
        cost_estimate=spent(
            flops=8 * rows * heads_width * width,
            bytes_accessed=8 * heads_width * width + 20 * rows * width,
            transcendentals=0,
        ),
        name="back_project",
    )(half, answer, *[weights] * 4)


def slope_kernel(
    model_ref, own_ref, got_ref, ff_ref, low_ref, stat_ref, gain_ref, scaled_ref, sum_ref, gain_out_ref
):
    _, rows, width = ff_ref.shape
    own_span, _ = own_spans(model_ref, width)
    lane = lax.broadcasted_iota(jnp.int32, (rows, 128), 1)
    packed = jnp.zeros((rows, 128), f32)
    totals = []
    for s in range(STREAMS):
        lanes = slice(s * width, (s + 1) * width)
        if s < 3:
            grad = own_ref[s + 1] + got_ref[s + 1].astype(f32)
        else:
            grad = ff_ref[0]
        average, inverse = stat_ref[:, 2 * s : 2 * s + 1], stat_ref[:, 2 * s + 1 : 2 * s + 2]
        hat = (low_ref[:, lanes].astype(f32) - average) * inverse
        totals.append(jnp.sum(grad * hat, axis=0, keepdims=True))
        scaled = grad * gain_ref[s : s + 1, own_span]
        scaled_ref[:, lanes] = scaled
        packed = jnp.where(lane == 2 * s, jnp.sum(scaled, axis=-1, keepdims=True), packed)
        packed = jnp.where(
            lane == 2 * s + 1, jnp.sum(scaled * hat, axis=-1, keepdims=True), packed
        )
    sum_ref[...] = packed
    totals = jnp.concatenate(totals, axis=0)

    @pl.when(pl.program_id(0) == 0)
    def _():
        gain_out_ref[...] = totals

    @pl.when(pl.program_id(0) > 0)
    def _():
        gain_out_ref[...] += totals


def norm_slopes(own, got, ff_grad, low, stats, gains, which):
    tall, wide = low.shape
    width = wide // STREAMS
    rows = min(64, tall)
    row = lambda i, m: (i, 0)
    cube = pl.BlockSpec((4, rows, width), lambda i, m: (0, i, 0))
    return pl.pallas_call(
        slope_kernel,
        grid_spec=pltpu.PrefetchScalarGridSpec(
            num_scalar_prefetch=1,
            grid=(tall // rows,),
            in_specs=[
                cube,
                cube,
                pl.BlockSpec((1, rows, width), lambda i, m: (0, i, 0)),
                pl.BlockSpec((rows, wide), row),
                pl.BlockSpec((rows, 128), row),
                pl.BlockSpec(gains.shape, lambda i, m: (0, 0)),
            ],
            out_specs=[
                pl.BlockSpec((rows, wide), row),
                pl.BlockSpec((rows, 128), row),
                pl.BlockSpec((STREAMS, width), lambda i, m: (0, 0)),
            ],
        ),
        out_shape=[
            jax.ShapeDtypeStruct((tall, wide), f32),
            jax.ShapeDtypeStruct((tall, 128), f32),
            jax.ShapeDtypeStruct((STREAMS, width), f32),
        ],
        cost_estimate=spent(
            flops=12 * tall * wide, bytes_accessed=12 * tall * wide, transcendentals=0
        ),
        name="norm_slopes",
    )(which, own, got, ff_grad, low, stats, gains)


def grads_kernel(
    scaled_ref, mine_ref, theirs_ref, low_ref, stat_ref, cot_ref, cur_ref, last_ref,
    grad_ref, mix_ref, dot_ref,
):
    rows, width = cot_ref.shape
    lane = lax.broadcasted_iota(jnp.int32, (rows, 128), 1)
    means = (mine_ref[...] + theirs_ref[...]) / (2 * width)
    current = cur_ref[...].astype(f32)
    packed = jnp.zeros((rows, 128), f32)
    mixed = None
    for s in range(STREAMS):
        lanes = slice(s * width, (s + 1) * width)
        average, inverse = stat_ref[:, 2 * s : 2 * s + 1], stat_ref[:, 2 * s + 1 : 2 * s + 2]
        hat = (low_ref[:, lanes].astype(f32) - average) * inverse
        grad = inverse * (
            scaled_ref[:, lanes]
            - means[:, 2 * s : 2 * s + 1]
            - hat * means[:, 2 * s + 1 : 2 * s + 2]
        )
        if s == STREAMS - 1:
            grad = grad + cot_ref[...].astype(f32)
        grad = grad.astype(bf16)
        grad_ref[s] = grad
        grad = grad.astype(f32)
        term = last_ref[:, s : s + 1] * grad
        mixed = term if mixed is None else mixed + term
        packed = jnp.where(lane == s, jnp.sum(grad * current, axis=-1, keepdims=True), packed)
    mix_ref[...] = mixed
    dot_ref[...] = packed


def stream_grads(scaled, mine, theirs, low, stats, cot, current_half, last):
    tall, wide = low.shape
    width = wide // STREAMS
    rows = min(64, tall)
    row = lambda i: (i, 0)
    return pl.pallas_call(
        grads_kernel,
        grid=(tall // rows,),
        in_specs=[
            pl.BlockSpec((rows, wide), row),
            pl.BlockSpec((rows, 128), row),
            pl.BlockSpec((rows, 128), row),
            pl.BlockSpec((rows, wide), row),
            pl.BlockSpec((rows, 128), row),
            pl.BlockSpec((rows, width), row),
            pl.BlockSpec((rows, width), row),
            pl.BlockSpec((rows, 128), row),
        ],
        out_specs=[
            pl.BlockSpec((STREAMS, rows, width), lambda i: (0, i, 0)),
            pl.BlockSpec((rows, width), row),
            pl.BlockSpec((rows, 128), row),
        ],
        out_shape=[
            jax.ShapeDtypeStruct((STREAMS, tall, width), bf16),
            jax.ShapeDtypeStruct((tall, width), f32),
            jax.ShapeDtypeStruct((tall, 128), f32),
        ],
        cost_estimate=spent(
            flops=12 * tall * wide, bytes_accessed=10 * tall * wide, transcendentals=0
        ),
        name="stream_grads",
    )(scaled, mine, theirs, low, stats, cot, current_half, last)


def turning_tables(places):
    half = ROT // 2
    inverse = jnp.exp(jnp.arange(half, dtype=f32) * (-2.0 * math.log(10000.0) / ROT))
    angles = places.astype(f32)[:, None] * inverse[None, :]
    cosine, sine = jnp.cos(angles), jnp.sin(angles)
    rows = places.shape[0]
    rest = jnp.zeros((rows, HDIM - ROT), f32)
    blank = jnp.zeros((rows, half), f32)
    return (
        jnp.concatenate([cosine, cosine, rest + 1.0], axis=1),
        jnp.concatenate([-sine, blank, rest], axis=1),
        jnp.concatenate([blank, sine, rest], axis=1),
    )


def local(
    history,
    slot_layer,
    current,
    positions,
    doc_ids,
    cotangent,
    norm_gains,
    generator_in,
    generator_out,
    query_weight,
    key_weight,
    value_weight,
    out_weight,
    up_weight,
    down_weight,
):
    dp_count = lax.axis_size("dp")
    depth_count = lax.axis_size("depth")
    dp_at = lax.axis_index("dp")
    model_at = lax.axis_index("mp")
    dp_bits = list(range(bit_count(dp_count)))
    slots, tokens_held, width = history.shape
    model = current.shape[1]
    rows_mb = current.shape[0] // MB
    length = depth_count * rows_mb
    heads_width = query_weight.shape[1]
    heads_each = heads_width // HDIM // depth_count
    own_rows = query_weight.shape[0]
    ff_width = up_weight.shape[1]
    ff_part = ff_width // dp_count
    both = ("dp", "depth")

    def half_of(values, axis, which):
        return lax.dynamic_slice_in_dim(values, which * width, width, axis)

    partners = jnp.stack([dp_at ^ m for m in range(dp_count)]).astype(jnp.int32)
    ff_local = ff_split(up_weight, down_weight, partners)
    ff_rows = [ff_local[0]] + [swap_mask(ff_local[m], "dp", m) for m in range(1, dp_count)]
    ff_rows = place_many(partners, ff_rows).reshape(2 * dp_count, own_rows, ff_part)

    small_cols = jnp.concatenate(
        [generator_in, norm_gains.T, jnp.zeros((own_rows, 128 - GEN - 5), bf16)], axis=1
    )
    small_all = gather_small(small_cols, both).reshape(model, 128)
    gen_first = small_all[:, :GEN]
    gen_first, ff_rows = fence(gen_first, ff_rows)
    gain_float = small_all[:, GEN : GEN + 5].astype(f32).T
    second_rows = generator_out.shape[0]
    second_pad = -second_rows % 128
    second_all = gather_small(jnp.pad(generator_out, (0, second_pad))[None], both)
    gen_second = second_all.reshape(-1, second_rows + second_pad)[:, :second_rows]
    second_low = gen_second.reshape(GEN, STREAMS * MIX)

    stacked = jnp.concatenate([query_weight, key_weight, value_weight, out_weight.T], axis=0)
    over_depth = lax.all_gather(stacked, "depth", axis=0, tiled=True)
    current_f = current.astype(f32)
    current_half = half_of(current, 1, model_at)
    mean_square = jnp.mean(current_f * current_f, axis=-1, keepdims=True)
    inverse_rms = lax.rsqrt(mean_square + RMS_EPSILON)
    unit = current_f * inverse_rms
    gen_normed = (unit * gain_float[4]).astype(bf16)
    gen_pre = dot_nn(gen_normed, gen_first)
    gen_hidden = gelu_exact(gen_pre).astype(bf16)
    column = jnp.arange(STREAMS * MIX)
    last_col = (column % MIX == MIX - 1).astype(f32)
    mixing = (dot_nn(gen_hidden, second_low) + last_col).astype(bf16)
    pick_last = (column[:, None] == (jnp.arange(128) * MIX + MIX - 1)[None, :]).astype(bf16)
    last = dot_nn(mixing, pick_last)

    layer_of = jnp.tile(slot_layer, STREAMS)
    stream_of = jnp.repeat(jnp.arange(STREAMS), slots)
    from_col = jnp.where(layer_of < MIX, stream_of * MIX + layer_of, -1)
    pick = (column[:, None] == from_col[None, :]).astype(f32)
    mix_all = gather_small(mixing, ("depth",)).reshape(depth_count * MB * rows_mb, STREAMS * MIX)
    slot_mix = dot_nn(mix_all, pick.astype(bf16))
    places_all = gather_small(positions, ("depth",))

    def over_depth_swap(values):
        return lax.all_to_all(values, "depth", 0, 0, tiled=True)

    def mix_part(micro_at, slot_mix):
        partial = mix_streams(slot_mix, history, micro_at, depth_count, rows_mb)
        return partial.reshape(STREAMS, depth_count, rows_mb, width)

    slot_mix, ff_rows, cotangent, places_all = fence(slot_mix, ff_rows, cotangent, places_all)
    partial = mix_part(0, slot_mix)
    partial_next = mix_part(1, slot_mix)

    weights_line = LineGather(ff_rows)
    weights_line.step()
    cot_pieces = lax.all_gather(cotangent, "dp", axis=0, tiled=True)
    over_depth, partial, partial_next, cot_pieces = weights_line.hold(
        over_depth, partial, partial_next, cot_pieces
    )
    pieces = [over_depth]
    weights = place_block(None, pieces[0][None], place_index(0), dp_count)
    hops_left = [(p, at) for at in range(len(dp_bits)) for p in range(1 << at)]
    placed = 1
    cots = None
    sums, sums_next = LineScatter(partial), LineScatter(partial_next)
    own_tables = turning_tables(positions)
    tables = [
        turning_tables(places_all[:, m * rows_mb : (m + 1) * rows_mb].reshape(length))
        for m in range(MB)
    ]
    for hop in range(1, depth_count):
        sums.step_with(weights_line)
        last_hop = hop == depth_count - 1
        for place in range(placed, len(pieces)):
            weights = place_block(weights, pieces[place][None], place_index(place), dp_count)
        placed = len(pieces)
        while hops_left:
            place, at = hops_left.pop(0)
            pieces.append(core_hop(pieces[place], at))
            if len(hops_left) <= depth_count - 1 - hop:
                break
        if last_hop:
            cot_full = join_halves(cotangent, other_core(cotangent), model_at)
            ff_weights = weights_line.placed()
            cots = cot_full, cotangent, cot_pieces, ff_weights
        (state,) = weights_line.hold(
            (sums.up, sums.down, pieces, weights, cots, own_tables, tables)
        )
        sums.up, sums.down, pieces, weights, cots, own_tables, tables = state
    cot_full, cotangent, cot_pieces, ff_weights = cots
    for place in range(placed, len(pieces)):
        weights = place_block(weights, pieces[place][None], place_index(place), dp_count)
    weights = weights.reshape(dp_count, depth_count, 4, own_rows, heads_width)
    ff_weights = ff_weights.reshape(2, dp_count, depth_count, own_rows, ff_part)

    document_view = doc_ids.reshape(depth_count, MB, rows_mb)
    which = model_at.astype(jnp.int32)[None]
    depth_at = lax.axis_index("depth").astype(jnp.int32)[None]
    gains = gain_float

    def enter(micro_at, sums):
        span = slice(micro_at * rows_mb, (micro_at + 1) * rows_mb)
        low, resid = total_streams(sums, current_half[span], last[span], depth_at)
        normed, ff_normed, stats = norm_streams(low, other_core(low), gains, which)
        packed = project_heads(
            normed,
            cot_full[span],
            weights,
            [t[span] for t in own_tables],
            depth_count,
        )
        return dict(
            low=low, resid=resid, normed=normed, ff_normed=ff_normed, stats=stats, packed=packed
        )

    def attention(micro_at, by_head):
        documents = document_view[:, micro_at].reshape(length)
        by_head = by_head.reshape(length, 4 * heads_each * HDIM)
        answer = attend(by_head, documents, tables[micro_at], heads_each)
        return answer.reshape(depth_count, rows_mb, 4 * heads_each * HDIM)

    place_list = jnp.stack([place_index(p) for p in range(dp_count)]).astype(jnp.int32)

    def group_rows(ff_normed):
        return lax.all_gather(ff_normed, "dp", axis=0, tiled=True)

    def group_joined(mine):
        return join_halves(mine, other_core(mine), model_at)

    def hidden_units(micro_at, group_normed):
        hidden, grad_up, own, other = feed_forward(
            group_normed, cot_group, micro_at, ff_weights, which
        )
        return dict(group_normed=group_normed, hidden=hidden, grad_up=grad_up), (own, other)

    def group_back_rest(near):
        for at in reversed(range(len(dp_bits) - 1)):
            half = 1 << at
            near = near[:half] + core_hop(near[half:].astype(bf16), at).astype(f32)
        return near[0]

    def group_back(own, other):
        near, far = group_split(own, other, place_list)
        return group_back_rest(near + core_hop(far, len(dp_bits) - 1).astype(f32))

    def back(kept, answer):
        (theirs,) = back_project(answer, weights, 1 - which, bf16, False)
        got = other_core(theirs)
        own, flat = back_project(answer, weights, which, f32, True)
        return own, got, flat

    def leave(micro_at, kept, own, got, ff_sum):
        span = slice(micro_at * rows_mb, (micro_at + 1) * rows_mb)
        rows = (kept["resid"] + own[0] + got[0].astype(f32) + ff_sum[1]).astype(bf16)
        low, stats = kept["low"], kept["stats"]
        scaled, sums, gain_part = norm_slopes(own, got, ff_sum, low, stats, gains, which)
        grad_low, current_mix, last_dot = stream_grads(
            scaled, sums, other_core(sums), low, stats, cotangent[span], current_half[span], last[span]
        )
        kept.update(layer_rows=rows, gain=gain_part, current_mix=current_mix, last_dot=last_dot)
        return grad_low

    ((sums.up, sums.down),) = sums_next.step((sums.up, sums.down))
    first = enter(0, sums)
    mine = group_rows(first["ff_normed"])
    packed, mine, cot_pieces = sums_next.hold(first["packed"], mine, cot_pieces)
    while sums_next.at < depth_count - 3:
        sums_next.step()
        sums_next.hold()
    packed, mine, cot_pieces = sums_next.step(packed, mine, cot_pieces)
    by_head = over_depth_swap(packed)
    cot_group = join_halves(cot_pieces, other_core(cot_pieces), model_at)
    cot_group = cot_group.reshape(dp_count, MB, rows_mb, model)
    kept, ff_parts = hidden_units(0, group_joined(mine))
    first.update(kept)
    by_head, ff_parts, cot_group = sums_next.hold(by_head, ff_parts, cot_group)
    by_head, ff_parts = sums_next.step(by_head, ff_parts)
    answer = attention(0, by_head)
    near, far = group_split(ff_parts[0], other_core(ff_parts[1]), place_list)
    near = near + core_hop(far, len(dp_bits) - 1).astype(f32)
    answer, near = sums_next.hold(answer, near)

    answer = over_depth_swap(answer)
    second = enter(1, sums_next)
    answer, packed, ff_normed, ff_sum = fence(
        answer, second["packed"], second["ff_normed"], group_back_rest(near)
    )
    by_head = over_depth_swap(packed)
    mine = group_rows(ff_normed)
    own, got, first["flat"] = back(first, answer)
    grad_low = leave(0, first, own, got, ff_sum)
    by_head, grad_low, mine = fence(by_head, grad_low, mine)
    saved = [first, second]

    def each(name):
        return [s[name] for s in saved]

    def rows_of(name):
        return jnp.concatenate(each(name), axis=0)

    def place_grads(place, dtype):
        return attention_grads(
            each("normed"),
            cot_full,
            each("flat"),
            place_list[place : place + 1],
            depth_count,
            dp_count,
            dtype,
        )

    half = dp_count // 2
    hops_left = [
        (p, at) for at in reversed(range(len(dp_bits))) for p in range(1 << at, 2 << at)
    ]
    pieces = {}

    def sums_hop():
        place, at = hops_left.pop(0)
        arrived = core_hop(pieces.pop(place).astype(bf16), at)
        target = place - (1 << at)
        pieces[target] = pieces[target].astype(f32) + arrived.astype(f32)

    grad_line = LineGather(grad_low)
    grad_line.step()
    answer = attention(1, by_head)
    kept, ff_parts = hidden_units(1, group_joined(mine))
    second.update(kept)
    answer, ff_parts = grad_line.hold(answer, ff_parts)
    answer = over_depth_swap(answer)
    near, far = group_split(ff_parts[0], other_core(ff_parts[1]), place_list)
    ff_products = hidden_grads(
        each("group_normed"), cot_group, each("grad_up"), each("hidden"), dp_count, depth_count
    )
    near = near + core_hop(far, len(dp_bits) - 1).astype(f32)
    answer, near, ff_products = fence(answer, near, ff_products)

    ff_sums = LineScatter(ff_products)
    (answer,) = ff_sums.step_with(grad_line, answer)
    own, got, flat = back(second, answer)
    ff_sum = group_back_rest(near)
    second["flat"] = flat
    (state,) = grad_line.hold((ff_sums.up, ff_sums.down, own, got, flat, ff_sum))
    ff_sums.up, ff_sums.down, own, got, second["flat"], ff_sum = state
    while len(grad_line.up) < depth_count - 1:
        ff_sums.step_with(grad_line)
        (state,) = grad_line.hold((ff_sums.up, ff_sums.down))
        ff_sums.up, ff_sums.down = state
    (ff_sum,) = ff_sums.step_with(grad_line, ff_sum)
    grad_low = leave(1, second, own, got, ff_sum)
    pieces = {p: place_grads(p, bf16 if p >= half else f32) for p in range(dp_count)}
    sums_hop()
    (state,) = grad_line.hold((ff_sums.up, ff_sums.down, grad_low, pieces))
    ff_sums.up, ff_sums.down, grad_low, pieces = state

    last_line = LineGather(grad_low)
    last_line.step()
    if hops_left:
        sums_hop()
    grad_first = grad_line.placed().reshape(STREAMS, length, width)
    history_grad, slot_part = unmix_streams(
        slot_mix, history, grad_first, 0, depth_count, rows_mb, None
    )
    slot_parts = [slot_part.reshape(depth_count, 1, rows_mb, 128)]
    pieces, history_grad = last_line.hold(pieces, history_grad)
    (pieces,) = ff_sums.step(pieces)
    while hops_left:
        sums_hop()
    (pieces,) = ff_sums.hold(pieces)
    out_sums = LineScatter(pieces[0].reshape(1, depth_count, 4 * own_rows, heads_width))
    for hop in range(2, depth_count):
        last_line.step()
        out_sums.step()
        if hop == depth_count - 1:
            ff_grads = end_sums(ff_sums, bf16).reshape(2, dp_count, own_rows, ff_part)
            ff_pieces = [
                lax.dynamic_index_in_dim(ff_grads, partners[m], 1, keepdims=False)
                for m in range(dp_count)
            ]
            ff_pieces = ff_pieces[:1] + [
                swap_mask(ff_pieces[m], "dp", m) for m in range(1, dp_count)
            ]
            ff_sums.up = ff_sums.down = ff_pieces
        (state,) = last_line.hold((out_sums.up, out_sums.down, ff_sums.up, ff_sums.down))
        out_sums.up, out_sums.down, ff_sums.up, ff_sums.down = state
    out_sums.step()
    ff_pieces = ff_sums.up
    last_grads = last_line.placed().reshape(STREAMS, length, width)
    history_grad, slot_part = unmix_streams(
        slot_mix, history, last_grads, 1, depth_count, rows_mb, history_grad
    )
    slot_parts.append(slot_part.reshape(depth_count, 1, rows_mb, 128))

    slot_grads = jnp.concatenate(slot_parts, axis=1).reshape(-1, 128)[:, : STREAMS * slots]
    mix_grads = dot_exact(slot_grads, pick.T).reshape(depth_count, MB * rows_mb, STREAMS * MIX)
    mix_grads, ff_pieces = out_sums.hold(mix_grads, ff_pieces)
    grad_mixing = scatter_small(mix_grads, ("depth",))
    up_grad, down_grad = ff_join(jnp.stack(ff_pieces), partners)
    last_dots = rows_of("last_dot")
    grad_mixing = grad_mixing + dot_exact(last_dots, pick_last.astype(f32).T)
    grad_mixing = grad_mixing + other_core(grad_mixing)

    second_float = second_low.astype(f32)
    grad_second = dot_exact(gen_hidden.astype(f32).T, grad_mixing)
    grad_pre = dot_exact(grad_mixing, second_float.T) * gelu_slope(gen_pre)
    grad_first = dot_exact(gen_normed.astype(f32).T, grad_pre)
    grad_gen_normed = dot_exact(grad_pre, gen_first.astype(f32).T)
    gain_gen = jnp.sum(grad_gen_normed * unit, axis=0)
    scattered = end_sums(out_sums, f32).reshape(4, own_rows, heads_width)
    grad_unit = grad_gen_normed * gain_float[4]
    shared = jnp.mean(grad_unit * unit, axis=-1, keepdims=True)
    current_gen = half_of(inverse_rms * (grad_unit - unit * shared), 1, model_at)
    current_grad = rows_of("current_mix") + current_gen

    gain_own = sum(s["gain"] for s in saved)
    gain_other = other_core(gain_own)
    gain_all = jnp.where(
        model_at == 0,
        jnp.concatenate([gain_own, gain_other], axis=1),
        jnp.concatenate([gain_other, gain_own], axis=1),
    )
    gain_all = jnp.concatenate([gain_all, gain_gen[None]], axis=0)
    small_grads = jnp.concatenate(
        [grad_first, gain_all.T, jnp.zeros((model, 128 - GEN - 5), f32)], axis=1
    )
    small_grads = scatter_small(small_grads.reshape(-1, own_rows, 128), both)
    second_grads = jnp.pad(grad_second.reshape(-1, second_rows), ((0, 0), (0, second_pad)))
    second_grads = scatter_small(second_grads[:, None], both)

    return (
        rows_of("layer_rows"),
        history_grad,
        current_grad,
        small_grads[:, GEN : GEN + 5].T,
        small_grads[:, :GEN],
        second_grads[0, :second_rows],
        scattered[0],
        scattered[1],
        scattered[2],
        scattered[3].T,
        up_grad,
        down_grad,
    )


def solution(mesh):
    return jax.shard_map(
        local,
        mesh=mesh,
        in_specs=(
            P("depth", "dp", "mp"),
            P("depth"),
            P(("dp", "depth"), None),
            P(("dp", "depth")),
            P("dp"),
            P(("dp", "depth"), "mp"),
            P(None, ("dp", "depth")),
            P(("dp", "depth"), None),
            P(("dp", "depth")),
            P(("dp", "depth"), "mp"),
            P(("dp", "depth"), "mp"),
            P(("dp", "depth"), "mp"),
            P("mp", ("dp", "depth")),
            P(("dp", "depth"), "mp"),
            P("mp", ("dp", "depth")),
        ),
        out_specs=(
            P(("dp", "depth"), "mp"),
            P("depth", "dp", "mp"),
            P(("dp", "depth"), "mp"),
            P(None, ("dp", "depth")),
            P(("dp", "depth"), None),
            P(("dp", "depth")),
            P(("dp", "depth"), "mp"),
            P(("dp", "depth"), "mp"),
            P(("dp", "depth"), "mp"),
            P("mp", ("dp", "depth")),
            P(("dp", "depth"), "mp"),
            P("mp", ("dp", "depth")),
        ),
        check_vma=False,
    )
```

```python
import functools
import math

import jax
import jax.numpy as jnp
from jax import lax
from jax.experimental import pallas as pl
from jax.experimental.pallas import tpu as pltpu
from jax.sharding import PartitionSpec as P

HDIM = 128
ROT = 32
GEN = 72
MB = 2
MIX = 18
STREAMS = 4
COST = 20

PRECISE = lax.Precision.HIGHEST
NORM_EPSILON = 1e-05
RMS_EPSILON = 1e-06
MASKED = -1e30

bf16 = jnp.bfloat16
f32 = jnp.float32


def dot_nn(a, b):
    return lax.dot_general(a, b, (((1,), (0,)), ((), ())), preferred_element_type=f32)


def dot_nt(a, b):
    return lax.dot_general(a, b, (((1,), (1,)), ((), ())), preferred_element_type=f32)


def dot_tn(a, b):
    return lax.dot_general(a, b, (((0,), (0,)), ((), ())), preferred_element_type=f32)


def dot_exact(a, b):
    return jnp.dot(a, b, precision=PRECISE, preferred_element_type=f32)


def gelu_exact(values):
    return jax.nn.gelu(values, approximate=False)


def gelu_slope(values):
    result, pullback = jax.vjp(gelu_exact, values)
    return pullback(jnp.ones_like(result))[0]


def bit_count(size):
    count = size.bit_length() - 1
    assert 1 << count == size
    return count


def swap_mask(values, axis, mask):
    size = lax.axis_size(axis)
    return lax.ppermute(values, axis, [(i, i ^ mask) for i in range(size)])


def gather_masked(values, axis, order):
    pieces = {0: values}
    for bit in order:
        arrived = {m | (1 << bit): swap_mask(v, axis, 1 << bit) for m, v in pieces.items()}
        pieces.update(arrived)
    return [pieces[m] for m in range(len(pieces))]


def scatter_masked(pieces, axis, order, link=bf16):
    pieces = dict(enumerate(pieces))
    for bit in order:
        flag = 1 << bit
        for m in [m for m in pieces if m & flag]:
            arrived = swap_mask(pieces.pop(m).astype(link), axis, flag)
            pieces[m ^ flag] = pieces[m ^ flag].astype(f32) + arrived.astype(f32)
    return pieces[0]


def core_orders():
    bits = list(range(bit_count(lax.axis_size("dp"))))
    return bits, bits[1:] + bits[:1]


def place_mask(place):
    masks = []
    for order in core_orders():
        masks.append(sum(1 << bit for at, bit in enumerate(order) if (place >> at) & 1))
    return jnp.where(lax.axis_index("mp") % 2 == 0, masks[0], masks[1])


def place_index(place):
    return lax.axis_index("dp") ^ place_mask(place)


def core_hop(values, at):
    orders, cores = core_orders(), lax.axis_size("mp")
    pairs = []
    for i in range(lax.axis_size("dp")):
        for core in range(cores):
            partner = i ^ (1 << orders[core % 2][at])
            pairs.append((i * cores + core, partner * cores + core))
    return lax.ppermute(values, ("dp", "mp"), pairs)


def group_hop(pieces, at):
    return jnp.concatenate([pieces, core_hop(pieces, at)], axis=0)


def place_of(core):
    partner = jnp.arange(lax.axis_size("dp")) ^ lax.axis_index("dp")
    places = []
    for order in core_orders():
        places.append(sum(((partner >> bit) & 1) << at for at, bit in enumerate(order)))
    return jnp.where(core % 2 == 0, places[0], places[1])


def reorder_masked(stacked, axis):
    count = bit_count(stacked.shape[0])
    here = lax.axis_index(axis)
    shape = stacked.shape
    values = stacked.reshape((2,) * count + shape[1:])
    for bit in range(count):
        turned = jnp.flip(values, count - 1 - bit)
        values = jnp.where(((here >> bit) & 1) == 1, turned, values)
    return values.reshape(shape)


def gather_small(values, axes):
    shape = values.shape
    values = values[None]
    for axis in reversed(axes):
        order = range(bit_count(lax.axis_size(axis)))
        stacked = jnp.stack(gather_masked(values, axis, order))
        values = reorder_masked(stacked, axis)
        values = values.reshape((-1,) + shape)
    return values


def scatter_small(values, axes):
    for axis in axes:
        size = lax.axis_size(axis)
        values = values.reshape((size, values.shape[0] // size) + values.shape[1:])
        turned = reorder_masked(values, axis)
        order = reversed(range(bit_count(size)))
        values = scatter_masked([turned[m] for m in range(size)], axis, order, f32)
    return values[0]


def line_size():
    return lax.axis_size("depth"), lax.axis_index("depth")


def fence(*values):
    return lax.optimization_barrier(values)


class LineGather:

    def __init__(self, values):
        self.up, self.down = [values], [values]

    def step(self):
        size, _ = line_size()
        at = len(self.up)
        if at < size:
            up_pairs = [(i, i + 1) for i in range(at - 1, size - 1)]
            down_pairs = [(i, i - 1) for i in range(1, size - at + 1)]
            self.up.append(lax.ppermute(self.up[-1], "depth", up_pairs))
            self.down.append(lax.ppermute(self.down[-1], "depth", down_pairs))

    def hold(self, *others):
        kept = fence((self.up[1:], self.down[1:]), *others)
        (up, down), rest = kept[0], kept[1:]
        self.up, self.down = self.up[:1] + list(up), self.down[:1] + list(down)
        return rest

    def placed_early(self):
        size, here = line_size()
        steps = jnp.arange(size)
        index = lax.rem(here - steps + size, size)
        own = self.up[0]
        blocks = self.up[: size - 1] + [own]
        instead = [own] + self.down[1 : size - 1][::-1]
        return place_line(index, here >= steps, blocks, instead)

    def farthest(self, early):
        size, here = line_size()
        last = jnp.where(here == size - 1, self.up[size - 1], early[:, 0])
        return jnp.where(here == 0, self.down[size - 1], last), jnp.where(here == 0, size - 1, 0)

    def placed(self):
        size, here = line_size()
        steps = jnp.arange(size)
        index = lax.rem(here - steps + size, size)
        return place_line(index, here >= steps, self.up, self.down[1:][::-1])


class LineScatter:

    def __init__(self, terms):
        self.terms, self.at = terms, 0
        self.up = self.down = None

    def step(self, *later):
        size, here = line_size()
        self.at += 1
        if self.at >= size:
            return later
        goes_up, goes_down = hop_sums(
            self.terms,
            jnp.minimum(size - self.at + here, size - 1),
            jnp.maximum(here - size + self.at, 0),
            self.up,
            self.down,
        )
        (goes_up, goes_down), *later = fence((goes_up, goes_down), *later)
        up_pairs = [(i, i + 1) for i in range(min(self.at, size - 1))]
        down_pairs = [(size - 1 - i, size - 2 - i) for i in range(min(self.at, size - 1))]
        self.up = lax.ppermute(goes_up, "depth", up_pairs)
        self.down = lax.ppermute(goes_down, "depth", down_pairs)
        return later

    def step_with(self, line, *later):
        size, here = line_size()
        lead, _, tall, wide = self.terms.shape
        shape = line.up[0].shape
        if (
            len(line.up) != self.at + 2
            or self.at + 2 > size - 1
            or math.prod(shape) != lead * tall * wide
            or shape[2] != wide
        ):
            line.step()
            return self.step(*later)
        self.at += 1
        goes = hop_sums(
            self.terms,
            jnp.minimum(size - self.at + here, size - 1),
            jnp.maximum(here - size + self.at, 0),
            self.up,
            self.down,
            [v[-1].reshape(lead, tall, wide) for v in (line.up, line.down)],
            [here < self.at, here > size - 1 - self.at],
        )
        goes, *later = fence(goes, *later)
        self.up = lax.ppermute(goes[0], "depth", [(i, i + 1) for i in range(size - 1)])
        self.down = lax.ppermute(goes[1], "depth", [(i, i - 1) for i in range(1, size)])
        line.up.append(self.up.reshape(shape))
        line.down.append(self.down.reshape(shape))
        return later

    def hold(self, *others):
        (self.up, self.down), *rest = fence((self.up, self.down), *others)
        return rest


def other_core(values):
    return swap_mask(values, "mp", 1)


def join_kernel(model_ref, own_ref, other_ref, out_ref):
    width = own_ref.shape[1]
    own_at = pl.multiple_of(model_ref[0] * width, width)
    other_at = pl.multiple_of((1 - model_ref[0]) * width, width)
    out_ref[:, pl.ds(own_at, width)] = own_ref[...]
    out_ref[:, pl.ds(other_at, width)] = other_ref[...]


def join_halves(own, other, model_at):
    tall, width = own.shape
    rows = min(256, tall)
    return pl.pallas_call(
        join_kernel,
        grid_spec=pltpu.PrefetchScalarGridSpec(
            num_scalar_prefetch=1,
            grid=(tall // rows,),
            in_specs=[pl.BlockSpec((rows, width), lambda i, m: (i, 0))] * 2,
            out_specs=pl.BlockSpec((rows, 2 * width), lambda i, m: (i, 0)),
        ),
        out_shape=jax.ShapeDtypeStruct((tall, 2 * width), own.dtype),
        cost_estimate=spent(
            flops=0, bytes_accessed=8 * tall * width, transcendentals=0
        ),
        name="join_halves",
    )(model_at.astype(jnp.int32)[None], own, other)


def spent(flops, bytes_accessed, transcendentals):
    return pl.CostEstimate(
        flops=flops // COST, bytes_accessed=bytes_accessed // COST, transcendentals=transcendentals // COST
    )


def chunk_of(tall, wide):
    rows = tall
    while rows * wide > 1 << 19 and rows % 32 == 0:
        rows //= 2
    return rows


def place_kernel(at_ref, *refs):
    if len(refs) < 4:
        refs[-1][0, 0] = refs[0][0]
        return

    @pl.when(at_ref[1] == 1)
    def _():
        refs[-1][0, 0] = refs[0][0]

    @pl.when(at_ref[1] == 0)
    def _():
        refs[-1][0, 0] = refs[1][0]


def place_block(buffer, block, index, count, instead=None, first=None):
    lead, tall, wide = block.shape
    rows = chunk_of(tall, wide)
    spec = pl.BlockSpec((1, rows, wide), lambda l, i, m: (l, i, 0))
    blocks = [block] if instead is None else [block, instead]
    where = [index, 1 if first is None else first]
    where = jnp.stack([jnp.asarray(v).astype(jnp.int32) for v in where])
    in_specs, operands, aliases = [spec] * len(blocks), list(blocks), {}
    if buffer is not None or instead is not None:
        in_specs.append(pl.BlockSpec(memory_space=pl.ANY))
        operands.append(block if buffer is None else buffer)
        aliases = {} if buffer is None else {len(operands): 0}
    return pl.pallas_call(
        place_kernel,
        grid_spec=pltpu.PrefetchScalarGridSpec(
            num_scalar_prefetch=1,
            grid=(lead, tall // rows),
            in_specs=in_specs,
            out_specs=pl.BlockSpec((1, 1, rows, wide), lambda l, i, m: (l, m[0], i, 0)),
        ),
        out_shape=jax.ShapeDtypeStruct((lead, count, tall, wide), block.dtype),
        input_output_aliases=aliases,
        cost_estimate=spent(
            flops=0, bytes_accessed=4 * lead * tall * wide, transcendentals=0
        ),
        name="place_block",
    )(where, *operands)


def place_line_kernel(size, at_ref, *refs):
    out_ref = refs[-1]
    for step in range(size):
        if step == 0 or len(refs) == size + 1:
            out_ref[0, at_ref[step]] = refs[step][0]
            continue

        @pl.when(at_ref[size + step] == 1)
        def _(step=step):
            out_ref[0, at_ref[step]] = refs[step][0]

        @pl.when(at_ref[size + step] == 0)
        def _(step=step):
            out_ref[0, at_ref[step]] = refs[size + step - 1][0]


def place_line(index, first, blocks, instead):
    size = len(blocks)
    lead, tall, wide = blocks[0].shape
    rows = tall
    while rows * wide > 1 << 18 and rows % 32 == 0:
        rows //= 2
    spec = pl.BlockSpec((1, rows, wide), lambda l, i, m: (l, i, 0))
    where = jnp.concatenate([index, first]).astype(jnp.int32)
    operands = list(blocks) + list(instead)
    return pl.pallas_call(
        functools.partial(place_line_kernel, size),
        grid_spec=pltpu.PrefetchScalarGridSpec(
            num_scalar_prefetch=1,
            grid=(lead, tall // rows),
            in_specs=[spec] * len(operands),
            out_specs=pl.BlockSpec((1, size, rows, wide), lambda l, i, m: (l, 0, i, 0)),
        ),
        out_shape=jax.ShapeDtypeStruct((lead, size, tall, wide), blocks[0].dtype),
        compiler_params=pltpu.CompilerParams(vmem_limit_bytes=40 << 20),
        cost_estimate=spent(
            flops=0, bytes_accessed=6 * size * lead * tall * wide, transcendentals=0
        ),
        name="place_line",
    )(where, *operands)


def place_many(index, blocks):
    ones = jnp.ones(len(blocks), jnp.int32)
    return place_line(index, ones, blocks, [])


def group_join_kernel(at_ref, own_ref, other_ref, out_ref):
    width = own_ref.shape[2]
    own_span, other_span = own_spans(at_ref, width)
    out_ref[:, own_span] = own_ref[0]
    out_ref[:, other_span] = other_ref[0]


def group_join(own, other, model_at):
    count, tall, width = own.shape
    rows = chunk_of(tall, width)
    per = tall // rows
    where = jnp.concatenate([model_at[None], place_of(model_at), place_of(1 - model_at)])
    return pl.pallas_call(
        group_join_kernel,
        grid_spec=pltpu.PrefetchScalarGridSpec(
            num_scalar_prefetch=1,
            grid=(count, per),
            in_specs=[
                pl.BlockSpec((1, rows, width), lambda n, i, m: (m[1 + n], i, 0)),
                pl.BlockSpec((1, rows, width), lambda n, i, m: (m[1 + count + n], i, 0)),
            ],
            out_specs=pl.BlockSpec((rows, 2 * width), lambda n, i, m: (n * per + i, 0)),
        ),
        out_shape=jax.ShapeDtypeStruct((count * tall, 2 * width), own.dtype),
        cost_estimate=spent(
            flops=0, bytes_accessed=8 * count * tall * width, transcendentals=0
        ),
        name="group_join",
    )(where.astype(jnp.int32), own, other)


def group_split_kernel(at_ref, near_own, near_other, far_own, far_other, near_ref, far_ref):
    near_ref[0, 0] = near_own[0] + near_other[0].astype(f32)
    far_ref[0, 0] = (far_own[0] + far_other[0].astype(f32)).astype(bf16)


def group_split(own, other, places):
    _, tall, width = own.shape
    count = places.shape[0]
    half, rows = count // 2, tall // count
    near = pl.BlockSpec((1, rows, width), lambda p, k, m: (k, m[p], 0))
    far = pl.BlockSpec((1, rows, width), lambda p, k, m: (k, m[half + p], 0))
    out = pl.BlockSpec((1, 1, rows, width), lambda p, k, m: (p, k, 0, 0))
    return pl.pallas_call(
        group_split_kernel,
        grid_spec=pltpu.PrefetchScalarGridSpec(
            num_scalar_prefetch=1,
            grid=(half, 2),
            in_specs=[near, near, far, far],
            out_specs=[out, out],
        ),
        out_shape=[
            jax.ShapeDtypeStruct((half, 2, rows, width), f32),
            jax.ShapeDtypeStruct((half, 2, rows, width), bf16),
        ],
        cost_estimate=spent(
            flops=2 * tall * width, bytes_accessed=20 * tall * width, transcendentals=0
        ),
        name="group_split",
    )(places, own, other, own, other)


def hop_kernel(has_sums, has_blocks, at_ref, *refs):
    ins, outs = list(refs[:-2]), refs[-2:]
    terms, ins = ins[:2], ins[2:]
    sums, ins = (ins[:2], ins[2:]) if has_sums else (None, ins)

    def send_sum(way):
        term = terms[way][0, 0].astype(f32)
        if sums is not None:
            term = term + sums[way][0].astype(f32)
        outs[way][0] = term.astype(bf16)

    for way in range(2):
        if not has_blocks:
            send_sum(way)
            continue
        pl.when(at_ref[2 + way] == 1)(functools.partial(send_sum, way))

        @pl.when(at_ref[2 + way] == 0)
        def _(way=way):
            outs[way][0] = ins[way][0]


def hop_sums(terms, up_at, down_at, up, down, blocks=None, first=None):
    lead, _, tall, wide = terms.shape
    rows = chunk_of(tall, wide)
    block = pl.BlockSpec((1, rows, wide), lambda l, i, m: (l, i, 0))
    in_specs = [
        pl.BlockSpec((1, 1, rows, wide), lambda l, i, m: (l, m[0], i, 0)),
        pl.BlockSpec((1, 1, rows, wide), lambda l, i, m: (l, m[1], i, 0)),
    ]
    operands = [terms, terms]
    where = [up_at, down_at]
    if up is not None:
        in_specs += [block, block]
        operands += [up, down]
    if blocks is not None:
        in_specs += [block, block]
        operands += list(blocks)
        where += list(first)
    return pl.pallas_call(
        functools.partial(hop_kernel, up is not None, blocks is not None),
        grid_spec=pltpu.PrefetchScalarGridSpec(
            num_scalar_prefetch=1,
            grid=(lead, tall // rows),
            in_specs=in_specs,
            out_specs=[block, block],
        ),
        out_shape=[jax.ShapeDtypeStruct((lead, tall, wide), bf16)] * 2,
        cost_estimate=spent(
            flops=2 * lead * tall * wide, bytes_accessed=12 * lead * tall * wide, transcendentals=0
        ),
        name="hop_sums",
    )(jnp.stack(where).astype(jnp.int32), *operands)


def end_kernel(at_ref, term_ref, up_ref, down_ref, out_ref):
    total = term_ref[0, 0].astype(f32) + up_ref[0].astype(f32) + down_ref[0].astype(f32)
    out_ref[0] = total.astype(out_ref.dtype)


def end_sums(sums, dtype):
    lead, _, tall, wide = sums.terms.shape
    rows = chunk_of(tall, wide)
    block = pl.BlockSpec((1, rows, wide), lambda l, i, m: (l, i, 0))
    return pl.pallas_call(
        end_kernel,
        grid_spec=pltpu.PrefetchScalarGridSpec(
            num_scalar_prefetch=1,
            grid=(lead, tall // rows),
            in_specs=[
                pl.BlockSpec((1, 1, rows, wide), lambda l, i, m: (l, m[0], i, 0)),
                block,
                block,
            ],
            out_specs=block,
        ),
        out_shape=jax.ShapeDtypeStruct((lead, tall, wide), dtype),
        cost_estimate=spent(
            flops=2 * lead * tall * wide, bytes_accessed=10 * lead * tall * wide, transcendentals=0
        ),
        name="end_sums",
    )(lax.axis_index("depth").astype(jnp.int32)[None], sums.terms, sums.up, sums.down)


def attention_grad_kernel(
    at_ref, x0_ref, x1_ref, cot_ref, g0_ref, g1_ref, out_ref
):
    tall = x0_ref.shape[1]

    def store(total):
        out_ref[...] = total.reshape(out_ref.shape).astype(out_ref.dtype)

    @pl.when(pl.program_id(0) < 3)
    def _():
        store(dot_tn(x0_ref[0], g0_ref[0]) + dot_tn(x1_ref[0], g1_ref[0]))

    @pl.when(pl.program_id(0) == 3)
    def _():
        store(
            dot_tn(cot_ref[0:tall, :], g0_ref[0]) + dot_tn(cot_ref[tall : 2 * tall, :], g1_ref[0])
        )


def attention_grads(normed, cot, flat, place, depth_count, dp_count, dtype):
    _, tall, model = normed[0].shape
    heads_width = flat[0].shape[2]
    block = model // dp_count
    own_rows = block // depth_count
    normed_spec = pl.BlockSpec((1, tall, block), lambda k, m: (jnp.minimum(k, 2), 0, m[0]))
    flat_spec = pl.BlockSpec((1, tall, heads_width), lambda k, m: (lax.rem(k + 1, 4), 0, 0))
    return pl.pallas_call(
        attention_grad_kernel,
        grid_spec=pltpu.PrefetchScalarGridSpec(
            num_scalar_prefetch=1,
            grid=(4,),
            in_specs=[
                normed_spec,
                normed_spec,
                pl.BlockSpec((2 * tall, block), lambda k, m: (0, m[0])),
                flat_spec,
                flat_spec,
            ],
            out_specs=pl.BlockSpec(
                (depth_count, 1, own_rows, heads_width), lambda k, m: (0, k, 0, 0)
            ),
        ),
        out_shape=jax.ShapeDtypeStruct((depth_count, 4, own_rows, heads_width), dtype),
        compiler_params=pltpu.CompilerParams(vmem_limit_bytes=40 << 20),
        cost_estimate=spent(
            flops=16 * tall * block * heads_width,
            bytes_accessed=16 * block * heads_width,
            transcendentals=0,
        ),
        name="attention_grads",
    )(place, *normed, cot, *flat)


def hidden_grad_kernel(x0_ref, x1_ref, c0_ref, c1_ref, u0_ref, u1_ref, h0_ref, h1_ref, out_ref):
    def store(total):
        out_ref[...] = total.reshape(out_ref.shape)

    @pl.when(pl.program_id(0) == 0)
    def _():
        store(dot_tn(x0_ref[...], u0_ref[...]) + dot_tn(x1_ref[...], u1_ref[...]))

    @pl.when(pl.program_id(0) == 1)
    def _():
        tall, wide = h0_ref.shape[0], c0_ref.shape[3]
        c0, c1 = c0_ref[:, 0].reshape(tall, wide), c1_ref[:, 0].reshape(tall, wide)
        store(dot_tn(c0, h0_ref[...]) + dot_tn(c1, h1_ref[...]))


def hidden_grads(x, cot, up_grads, hidden, dp_count, depth_count):
    tall, model = x[0].shape
    part = hidden[0].shape[1]
    block = model // dp_count
    cols = pl.BlockSpec((tall, block), lambda k, n: (0, n * (1 - k)))
    whole = pl.BlockSpec((tall, part), lambda k, n: (0, 0))
    return pl.pallas_call(
        hidden_grad_kernel,
        grid=(2, dp_count),
        in_specs=[cols, cols]
        + [
            pl.BlockSpec((dp_count, 1, cot.shape[2], block), lambda k, n: (0, 0, 0, n * k)),
            pl.BlockSpec((dp_count, 1, cot.shape[2], block), lambda k, n: (0, 1, 0, n * k)),
        ]
        + [whole] * 4,
        out_specs=pl.BlockSpec(
            (1, depth_count, block // depth_count, part), lambda k, n: (k * dp_count + n, 0, 0, 0)
        ),
        out_shape=jax.ShapeDtypeStruct(
            (2 * dp_count, depth_count, block // depth_count, part), f32
        ),
        compiler_params=pltpu.CompilerParams(vmem_limit_bytes=48 << 20),
        cost_estimate=spent(
            flops=8 * tall * model * part, bytes_accessed=8 * model * part, transcendentals=0
        ),
        name="hidden_grads",
    )(*x, cot, cot, *up_grads, *hidden)


def mix_kernel(slots, mix_ref, hist_ref, out_ref):
    rows, width = hist_ref.shape[1], hist_ref.shape[2]
    part = 512 if width % 512 == 0 else width

    def step(at, carry):
        r0 = pl.multiple_of(at * 16, 16)
        weights = mix_ref[pl.ds(r0, 16), :]
        for c0 in range(0, width, part):
            sums = [None] * STREAMS
            for k in range(slots):
                state = hist_ref[k, pl.ds(r0, 16), c0 : c0 + part].astype(f32)
                for s in range(STREAMS):
                    term = weights[:, s * slots + k : s * slots + k + 1] * state
                    sums[s] = term if sums[s] is None else sums[s] + term
            for s in range(STREAMS):
                out_ref[s, pl.ds(r0, 16), c0 : c0 + part] = sums[s].astype(bf16)
        return carry

    lax.fori_loop(0, rows // 16, step, 0)


def mix_streams(slot_mix, history, micro_at, depth_count, rows_mb):
    slots, _, width = history.shape
    rows = min(128, rows_mb)
    per = rows_mb // rows

    def row_block(i):
        return ((i // per) * MB + micro_at) * per + i % per

    return pl.pallas_call(
        functools.partial(mix_kernel, slots),
        grid=(depth_count * per,),
        in_specs=[
            pl.BlockSpec((rows, slot_mix.shape[1]), lambda i: (row_block(i), 0)),
            pl.BlockSpec((slots, rows, width), lambda i: (0, row_block(i), 0)),
        ],
        out_specs=pl.BlockSpec((STREAMS, rows, width), lambda i: (0, i, 0)),
        out_shape=jax.ShapeDtypeStruct((STREAMS, depth_count * rows_mb, width), bf16),
        cost_estimate=spent(
            flops=2 * slots * STREAMS * depth_count * rows_mb * width,
            bytes_accessed=2 * (slots + STREAMS) * depth_count * rows_mb * width,
            transcendentals=0,
        ),
        name="mix_streams",
    )(slot_mix, history)


def unmix_kernel(slots, mix_ref, hist_ref, grad_ref, *rest):
    hist_grad_ref, slot_grad_ref = rest[-2:]
    rows, width = hist_ref.shape[1], hist_ref.shape[2]
    part = 512 if width % 512 == 0 else width

    def step(at, carry):
        r0 = pl.multiple_of(at * 16, 16)
        weights = mix_ref[pl.ds(r0, 16), :]
        totals = [None] * (STREAMS * slots)
        for c0 in range(0, width, part):
            grads = [
                grad_ref[s, pl.ds(r0, 16), c0 : c0 + part].astype(f32)
                for s in range(STREAMS)
            ]
            for k in range(slots):
                state = hist_ref[k, pl.ds(r0, 16), c0 : c0 + part].astype(f32)
                back = None
                for s in range(STREAMS):
                    at_sk = s * slots + k
                    term = weights[:, at_sk : at_sk + 1] * grads[s]
                    back = term if back is None else back + term
                    product = state * grads[s]
                    folded = product[:, 0:128]
                    for l0 in range(128, part, 128):
                        folded = folded + product[:, l0 : l0 + 128]
                    totals[at_sk] = folded if totals[at_sk] is None else totals[at_sk] + folded
                hist_grad_ref[k, pl.ds(r0, 16), c0 : c0 + part] = back.astype(bf16)
        lane = lax.broadcasted_iota(jnp.int32, (16, 128), 1)
        packed = jnp.zeros((16, 128), f32)
        for at_sk in range(STREAMS * slots):
            column = jnp.sum(totals[at_sk], axis=1, keepdims=True)
            packed = jnp.where(lane == at_sk, column, packed)
        slot_grad_ref[pl.ds(r0, 16), :] = packed
        return carry

    lax.fori_loop(0, rows // 16, step, 0)


def unmix_streams(slot_mix, history, grads, micro_at, depth_count, rows_mb, earlier):
    slots, tokens, width = history.shape
    rows = min(128, rows_mb)
    per = rows_mb // rows

    def row_block(i):
        return ((i // per) * MB + micro_at) * per + i % per

    in_specs = [
        pl.BlockSpec((rows, slot_mix.shape[1]), lambda i: (row_block(i), 0)),
        pl.BlockSpec((slots, rows, width), lambda i: (0, row_block(i), 0)),
        pl.BlockSpec((STREAMS, rows, width), lambda i: (0, i, 0)),
    ]
    operands = [slot_mix, history, grads]
    aliases = {}
    if earlier is not None:
        in_specs.append(pl.BlockSpec(memory_space=pl.ANY))
        operands.append(earlier)
        aliases = {3: 0}
    return pl.pallas_call(
        functools.partial(unmix_kernel, slots),
        grid=(depth_count * per,),
        in_specs=in_specs,
        out_specs=[
            pl.BlockSpec((slots, rows, width), lambda i: (0, row_block(i), 0)),
            pl.BlockSpec((rows, 128), lambda i: (i, 0)),
        ],
        out_shape=[
            jax.ShapeDtypeStruct((slots, tokens, width), bf16),
            jax.ShapeDtypeStruct((depth_count * rows_mb, 128), f32),
        ],
        input_output_aliases=aliases,
        cost_estimate=spent(
            flops=4 * slots * STREAMS * depth_count * rows_mb * width,
            bytes_accessed=2 * (2 * slots + STREAMS) * depth_count * rows_mb * width,
            transcendentals=0,
        ),
        name="unmix_streams",
    )(*operands)


def unmix_one(slot_mix, history, grads, micro_at, index, rows_mb, earlier):
    slots, tokens, width = history.shape
    rows = min(128, rows_mb)
    per = rows_mb // rows

    def row_block(i, m):
        return (m[0] * MB + micro_at) * per + i

    def kernel(at_ref, *refs):
        unmix_kernel(slots, *refs)

    return pl.pallas_call(
        kernel,
        grid_spec=pltpu.PrefetchScalarGridSpec(
            num_scalar_prefetch=1,
            grid=(per,),
            in_specs=[
                pl.BlockSpec((rows, slot_mix.shape[1]), lambda i, m: (row_block(i, m), 0)),
                pl.BlockSpec((slots, rows, width), lambda i, m: (0, row_block(i, m), 0)),
                pl.BlockSpec((STREAMS, rows, width), lambda i, m: (0, i, 0)),
                pl.BlockSpec(memory_space=pl.ANY),
            ],
            out_specs=[
                pl.BlockSpec((slots, rows, width), lambda i, m: (0, row_block(i, m), 0)),
                pl.BlockSpec((rows, 128), lambda i, m: (i, 0)),
            ],
        ),
        out_shape=[
            jax.ShapeDtypeStruct((slots, tokens, width), bf16),
            jax.ShapeDtypeStruct((rows_mb, 128), f32),
        ],
        input_output_aliases={4: 0},
        cost_estimate=spent(
            flops=4 * slots * STREAMS * rows_mb * width,
            bytes_accessed=2 * (2 * slots + STREAMS) * rows_mb * width,
            transcendentals=0,
        ),
        name="unmix_one",
    )(index.astype(jnp.int32)[None], slot_mix, history, grads, earlier)


def own_spans(model_ref, width):
    own_at = pl.multiple_of(model_ref[0] * width, width)
    other_at = pl.multiple_of((1 - model_ref[0]) * width, width)
    return pl.ds(own_at, width), pl.ds(other_at, width)


def ff_split_kernel(at_ref, up_ref, down_ref, out_ref):
    out_ref[0, 0] = up_ref[...]
    out_ref[0, 1] = down_ref[...].T


def ff_split(up_weight, down_weight, partners):
    own_rows, ff_width = up_weight.shape
    count = partners.shape[0]
    part = ff_width // count
    return pl.pallas_call(
        ff_split_kernel,
        grid_spec=pltpu.PrefetchScalarGridSpec(
            num_scalar_prefetch=1,
            grid=(count,),
            in_specs=[
                pl.BlockSpec((own_rows, part), lambda i, m: (0, m[i])),
                pl.BlockSpec((part, own_rows), lambda i, m: (m[i], 0)),
            ],
            out_specs=pl.BlockSpec((1, 2, own_rows, part), lambda i, m: (i, 0, 0, 0)),
        ),
        out_shape=jax.ShapeDtypeStruct((count, 2, own_rows, part), bf16),
        cost_estimate=spent(flops=0, bytes_accessed=8 * own_rows * ff_width, transcendentals=0),
        name="ff_split",
    )(partners, up_weight, down_weight)


def ff_join_kernel(at_ref, piece_ref, up_ref, down_ref):
    up_ref[...] = piece_ref[0, 0].astype(f32)
    down_ref[...] = piece_ref[0, 1].astype(f32).T


def ff_join(pieces, partners):
    count, _, own_rows, part = pieces.shape
    return pl.pallas_call(
        ff_join_kernel,
        grid_spec=pltpu.PrefetchScalarGridSpec(
            num_scalar_prefetch=1,
            grid=(count,),
            in_specs=[pl.BlockSpec((1, 2, own_rows, part), lambda i, m: (i, 0, 0, 0))],
            out_specs=[
                pl.BlockSpec((own_rows, part), lambda i, m: (0, m[i])),
                pl.BlockSpec((part, own_rows), lambda i, m: (m[i], 0)),
            ],
        ),
        out_shape=[
            jax.ShapeDtypeStruct((own_rows, count * part), f32),
            jax.ShapeDtypeStruct((count * part, own_rows), f32),
        ],
        cost_estimate=spent(
            flops=0, bytes_accessed=12 * own_rows * count * part, transcendentals=0
        ),
        name="ff_join",
    )(partners, pieces)


def total_kernel(depth_ref, part_ref, up_ref, down_ref, cur_ref, last_ref, low_ref, resid_ref):
    width = resid_ref.shape[1]
    current = cur_ref[...].astype(f32)
    for s in range(STREAMS):
        lanes = slice(s * width, (s + 1) * width)
        total = part_ref[s, 0].astype(f32)
        total = total + up_ref[s].astype(f32) + down_ref[s].astype(f32)
        total = total + last_ref[:, s : s + 1] * current
        if s == STREAMS - 1:
            resid_ref[...] = total
        low_ref[:, lanes] = total.astype(bf16)


def total_streams(sums, current_half, last, depth_at):
    _, _, tall, width = sums.terms.shape
    wide = STREAMS * width
    rows = min(64, tall)
    row = lambda i, d: (i, 0)
    return pl.pallas_call(
        total_kernel,
        grid_spec=pltpu.PrefetchScalarGridSpec(
            num_scalar_prefetch=1,
            grid=(tall // rows,),
            in_specs=[
                pl.BlockSpec((STREAMS, 1, rows, width), lambda i, d: (0, d[0], i, 0)),
                pl.BlockSpec((STREAMS, rows, width), lambda i, d: (0, i, 0)),
                pl.BlockSpec((STREAMS, rows, width), lambda i, d: (0, i, 0)),
                pl.BlockSpec((rows, width), row),
                pl.BlockSpec((rows, 128), row),
            ],
            out_specs=[pl.BlockSpec((rows, wide), row), pl.BlockSpec((rows, width), row)],
        ),
        out_shape=[
            jax.ShapeDtypeStruct((tall, wide), bf16),
            jax.ShapeDtypeStruct((tall, width), f32),
        ],
        cost_estimate=spent(flops=5 * tall * wide, bytes_accessed=9 * tall * wide, transcendentals=0),
        name="total_streams",
    )(depth_at, sums.terms, sums.up, sums.down, current_half, last)


def norm_kernel(model_ref, own_ref, other_ref, gain_ref, normed_ref, ff_ref, stat_ref):
    rows, width = ff_ref.shape
    model = 2 * width
    own_span, other_span = own_spans(model_ref, width)
    lane = lax.broadcasted_iota(jnp.int32, (rows, 128), 1)
    stats = jnp.zeros((rows, 128), f32)
    for s in range(STREAMS):
        lanes = slice(s * width, (s + 1) * width)
        own = own_ref[:, lanes].astype(f32)
        other = other_ref[:, lanes].astype(f32)
        average = (
            jnp.sum(own, axis=-1, keepdims=True) + jnp.sum(other, axis=-1, keepdims=True)
        ) / model
        own, other = own - average, other - average
        variance = (
            jnp.sum(own * own, axis=-1, keepdims=True)
            + jnp.sum(other * other, axis=-1, keepdims=True)
        ) / model
        inverse = lax.rsqrt(variance + NORM_EPSILON)
        stats = jnp.where(lane == 2 * s, average, stats)
        stats = jnp.where(lane == 2 * s + 1, inverse, stats)
        norm_own = (own * inverse * gain_ref[s : s + 1, own_span]).astype(bf16)
        if s == STREAMS - 1:
            ff_ref[...] = norm_own
        else:
            normed_ref[s, :, own_span] = norm_own
            norm_other = (other * inverse * gain_ref[s : s + 1, other_span]).astype(bf16)
            normed_ref[s, :, other_span] = norm_other
    stat_ref[...] = stats


def norm_streams(low, low_other, gains, which):
    tall, wide = low.shape
    width = wide // STREAMS
    rows = min(64, tall)
    row = lambda i, m: (i, 0)
    return pl.pallas_call(
        norm_kernel,
        grid_spec=pltpu.PrefetchScalarGridSpec(
            num_scalar_prefetch=1,
            grid=(tall // rows,),
            in_specs=[
                pl.BlockSpec((rows, wide), row),
                pl.BlockSpec((rows, wide), row),
                pl.BlockSpec(gains.shape, lambda i, m: (0, 0)),
            ],
            out_specs=[
                pl.BlockSpec((3, rows, 2 * width), lambda i, m: (0, i, 0)),
                pl.BlockSpec((rows, width), row),
                pl.BlockSpec((rows, 128), row),
            ],
        ),
        out_shape=[
            jax.ShapeDtypeStruct((3, tall, 2 * width), bf16),
            jax.ShapeDtypeStruct((tall, width), bf16),
            jax.ShapeDtypeStruct((tall, 128), f32),
        ],
        cost_estimate=spent(
            flops=20 * tall * wide, bytes_accessed=8 * tall * wide, transcendentals=0
        ),
        name="norm_streams",
    )(which, low, low_other, gains)


def turn(values, cosine, sine_up, sine_down, sign):
    up = pltpu.roll(values, HDIM - ROT // 2, 1)
    down = pltpu.roll(values, ROT // 2, 1)
    return values * cosine + sign * (up * sine_up + down * sine_down)


def project_kernel(
    x_ref, cot_ref, wq_ref, wk_ref, wv_ref, wo_ref, cos_ref, up_ref, down_ref, out_ref
):
    span = wq_ref.shape[-1]
    tables = cos_ref[...], up_ref[...], down_ref[...]
    for kind, w_ref in enumerate((wq_ref, wk_ref, wv_ref, wo_ref)):
        rows = cot_ref[...] if kind == 3 else x_ref[kind]
        product = dot_nn(rows, w_ref[...].reshape(-1, span))
        for begin in range(0, span, HDIM):
            head = product[:, begin : begin + HDIM]
            if kind < 2:
                head = turn(head, *tables, 1.0)
            out_ref[0, :, kind * span + begin : kind * span + begin + HDIM] = head.astype(bf16)


def project_heads(normed, cot, weights, tables, depth_count):
    _, rows, model = normed.shape
    groups, _, _, own_rows, heads_width = weights.shape
    span = heads_width // depth_count
    whole = lambda j: (0, 0)

    def matrix(kind):
        shape = (groups, depth_count, 1, own_rows, span)
        return pl.BlockSpec(shape, lambda j: (0, 0, kind, 0, j))

    return pl.pallas_call(
        project_kernel,
        grid=(depth_count,),
        in_specs=[
            pl.BlockSpec((3, rows, model), lambda j: (0, 0, 0)),
            pl.BlockSpec((rows, model), whole),
        ]
        + [matrix(kind) for kind in range(4)]
        + [pl.BlockSpec((rows, HDIM), whole)] * 3,
        out_specs=pl.BlockSpec((1, rows, 4 * span), lambda j: (j, 0, 0)),
        out_shape=jax.ShapeDtypeStruct((depth_count, rows, 4 * span), bf16),
        compiler_params=pltpu.CompilerParams(vmem_limit_bytes=40 << 20),
        cost_estimate=spent(
            flops=8 * rows * model * span * depth_count,
            bytes_accessed=8 * model * span * depth_count + 8 * rows * model,
            transcendentals=0,
        ),
        name="project_heads",
    )(normed, cot, *[weights] * 4, *tables)


def attend_kernel(
    block, q_ref, k_ref, v_ref, g_ref, doc_col_ref, doc_row_ref, cos_ref, up_ref, down_ref,
    out_ref, dk_sum, dv_sum,
):
    length = q_ref.shape[0]
    scale = HDIM**-0.5
    heads_each = out_ref.shape[1] // (4 * HDIM)

    def lanes(kind):
        return pl.ds(pl.multiple_of((kind * heads_each + pl.program_id(0)) * HDIM, HDIM), HDIM)

    for begin in range(0, length, block):
        end = begin + block
        rows = slice(begin, end)
        queries, grads = q_ref[rows, :], g_ref[rows, :]
        keys, values = k_ref[0:end, :], v_ref[0:end, :]
        scores = dot_nt(queries, keys) * scale
        place_q = begin + lax.broadcasted_iota(jnp.int32, scores.shape, 0)
        place_k = lax.broadcasted_iota(jnp.int32, scores.shape, 1)
        allowed = (doc_col_ref[rows, :] == doc_row_ref[:, 0:end]) & (place_q >= place_k)
        scores = jnp.where(allowed, scores, MASKED)
        highest = jnp.max(scores, axis=-1, keepdims=True)
        exponent = jnp.exp(scores - highest)
        totals = jnp.sum(exponent, axis=-1, keepdims=True)
        attention = exponent * (1.0 / totals)
        low = attention.astype(bf16)
        out_ref[rows, lanes(0)] = dot_nn(low, values).astype(bf16)
        grad_att = dot_nt(grads, values).astype(bf16).astype(f32)
        weighted = jnp.sum(attention * grad_att, axis=-1, keepdims=True)
        grad_scores = (attention * (grad_att - weighted)).astype(bf16)
        grad_q = dot_nn(grad_scores, keys) * scale
        out_ref[rows, lanes(1)] = turn(
            grad_q, cos_ref[rows, :], up_ref[rows, :], down_ref[rows, :], -1.0
        ).astype(bf16)
        part_k = dot_tn(grad_scores, queries)
        part_v = dot_tn(low, grads)
        if begin > 0:
            dk_sum[0:begin, :] += part_k[0:begin]
            dv_sum[0:begin, :] += part_v[0:begin]
        dk_sum[begin:end, :] = part_k[begin:end]
        dv_sum[begin:end, :] = part_v[begin:end]
    grad_k = dk_sum[...] * scale
    out_ref[:, lanes(2)] = turn(grad_k, cos_ref[...], up_ref[...], down_ref[...], -1.0).astype(bf16)
    out_ref[:, lanes(3)] = dv_sum[...].astype(bf16)


def attend(packed, documents, tables, heads_each):
    length = packed.shape[0]
    block = min(256, length)
    whole = lambda h: (0, 0)

    def kind(at):
        return pl.BlockSpec((length, HDIM), lambda h: (0, at * heads_each + h))

    return pl.pallas_call(
        functools.partial(attend_kernel, block),
        grid=(heads_each,),
        in_specs=[kind(0), kind(1), kind(2), kind(3)]
        + [pl.BlockSpec((length, 1), whole), pl.BlockSpec((1, length), whole)]
        + [pl.BlockSpec((length, HDIM), whole)] * 3,
        out_specs=pl.BlockSpec((length, 4 * heads_each * HDIM), whole),
        out_shape=jax.ShapeDtypeStruct((length, 4 * heads_each * HDIM), bf16),
        scratch_shapes=[pltpu.VMEM((length, HDIM), f32)] * 2,
        compiler_params=pltpu.CompilerParams(vmem_limit_bytes=48 << 20),
        cost_estimate=spent(
            flops=9 * heads_each * length * length * HDIM,
            bytes_accessed=16 * length * heads_each * HDIM + 12 * length * HDIM,
            transcendentals=heads_each * length * length,
        ),
        name="attend",
    )(packed, packed, packed, packed, documents[:, None], documents[None, :], *tables)


def gelu_parts(values):
    cdf = 0.5 * (1.0 + lax.erf(values * (0.5**0.5)))
    density = jnp.exp(-0.5 * values * values) * (1.0 / math.sqrt(2.0 * math.pi))
    return values * cdf, cdf + values * density


def ff_kernel(
    model_ref, x_ref, cot_ref, up_ref, down_ref,
    hidden_ref, grad_ref, own_ref, other_ref,
):
    part = up_ref.shape[-1]
    half = up_ref.shape[1] // 2

    def rows_of(ref, which):
        return ref[0, pl.ds(which * half, half)].reshape(-1, part)

    own, other = model_ref[0], 1 - model_ref[0]
    up_pre = dot_nn(x_ref[...], up_ref[...].reshape(-1, part))
    hidden, slope = gelu_parts(up_pre)
    hidden = hidden.astype(bf16)
    grad_up = (dot_nn(cot_ref[0, 0], down_ref[...].reshape(-1, part)) * slope).astype(bf16)
    hidden_ref[...] = hidden
    grad_ref[...] = grad_up
    other_ref[0] = dot_nt(grad_up, rows_of(up_ref, other)).astype(bf16)
    own_ref[0] = dot_nt(grad_up, rows_of(up_ref, own))
    other_ref[1] = dot_nt(hidden, rows_of(down_ref, other)).astype(bf16)
    own_ref[1] = dot_nt(hidden, rows_of(down_ref, own))


def feed_forward(x, cot, micro_at, weights, which):
    tall, model = x.shape
    part = weights.shape[-1]
    width = model // 2
    rows = cot.shape[2]
    row = lambda i, m: (i, 0)

    def resident(kind):
        return pl.BlockSpec(
            (1,) + weights.shape[1:],
            lambda i, m: (kind, 0, 0, 0, 0),
            pipeline_mode=pl.Buffered(1),
        )

    return pl.pallas_call(
        ff_kernel,
        grid_spec=pltpu.PrefetchScalarGridSpec(
            num_scalar_prefetch=1,
            grid=(tall // rows,),
            in_specs=[
                pl.BlockSpec((rows, model), row),
                pl.BlockSpec((1, 1, rows, model), lambda i, m: (i, micro_at, 0, 0)),
                resident(0),
                resident(1),
            ],
            out_specs=[pl.BlockSpec((rows, part), row)] * 2
            + [pl.BlockSpec((2, rows, width), lambda i, m: (0, i, 0))] * 2,
        ),
        out_shape=[jax.ShapeDtypeStruct((tall, part), bf16)] * 2
        + [
            jax.ShapeDtypeStruct((2, tall, width), f32),
            jax.ShapeDtypeStruct((2, tall, width), bf16),
        ],
        compiler_params=pltpu.CompilerParams(vmem_limit_bytes=48 << 20),
        cost_estimate=spent(
            flops=8 * tall * model * part,
            bytes_accessed=4 * model * part + 16 * tall * model,
            transcendentals=2 * tall * part,
        ),
        name="feed_forward",
    )(which, x, cot, weights, weights)


def back_kernel(half_ref, ans_ref, wo_ref, wq_ref, wk_ref, wv_ref, out_ref, *flat):
    count, _, wide = ans_ref.shape
    span = wide // 4
    for kind, w_ref in enumerate((wo_ref, wq_ref, wk_ref, wv_ref)):
        total = None
        for j in range(count):
            term = dot_nt(
                ans_ref[j, :, kind * span : (kind + 1) * span],
                w_ref[:, :, :, :, j * span : (j + 1) * span].reshape(-1, span),
            )
            total = term if total is None else total + term
        out_ref[kind] = total.astype(out_ref.dtype)
    if flat:

        @pl.when(pl.program_id(0) == 0)
        def _():
            for kind in range(4):
                for j in range(count):
                    flat[0][kind, :, j * span : (j + 1) * span] = ans_ref[
                        j, :, kind * span : (kind + 1) * span
                    ]


def back_project(answer, weights, half, dtype, flat):
    count, rows, wide = answer.shape
    groups, _, _, own_rows, heads_width = weights.shape
    part = count * own_rows
    steps = groups // 2
    width = part * steps

    def matrix(kind):
        shape = (1, count, 1, own_rows, heads_width)
        return pl.BlockSpec(shape, lambda i, m: (m[0] * steps + i, 0, kind, 0, 0))

    out_specs = [pl.BlockSpec((4, rows, part), lambda i, m: (0, 0, i))]
    out_shape = [jax.ShapeDtypeStruct((4, rows, width), dtype)]
    if flat:
        out_specs.append(pl.BlockSpec((4, rows, heads_width), lambda i, m: (0, 0, 0)))
        out_shape.append(jax.ShapeDtypeStruct((4, rows, heads_width), bf16))
    return pl.pallas_call(
        back_kernel,
        grid_spec=pltpu.PrefetchScalarGridSpec(
            num_scalar_prefetch=1,
            grid=(steps,),
            in_specs=[pl.BlockSpec((count, rows, wide), lambda i, m: (0, 0, 0))]
            + [matrix(kind) for kind in (3, 0, 1, 2)],
            out_specs=out_specs,
        ),
        out_shape=out_shape,
        compiler_params=pltpu.CompilerParams(vmem_limit_bytes=40 << 20),
        cost_estimate=spent(
            flops=8 * rows * heads_width * width,
            bytes_accessed=8 * heads_width * width + 20 * rows * width,
            transcendentals=0,
        ),
        name="back_project",
    )(half, answer, *[weights] * 4)


def slope_kernel(
    model_ref, own_ref, got_ref, ff_ref, low_ref, stat_ref, gain_ref, scaled_ref, sum_ref, gain_out_ref
):
    _, rows, width = ff_ref.shape
    own_span, _ = own_spans(model_ref, width)
    lane = lax.broadcasted_iota(jnp.int32, (rows, 128), 1)
    packed = jnp.zeros((rows, 128), f32)
    totals = []
    for s in range(STREAMS):
        lanes = slice(s * width, (s + 1) * width)
        if s < 3:
            grad = own_ref[s + 1] + got_ref[s + 1].astype(f32)
        else:
            grad = ff_ref[0]
        average, inverse = stat_ref[:, 2 * s : 2 * s + 1], stat_ref[:, 2 * s + 1 : 2 * s + 2]
        hat = (low_ref[:, lanes].astype(f32) - average) * inverse
        totals.append(jnp.sum(grad * hat, axis=0, keepdims=True))
        scaled = grad * gain_ref[s : s + 1, own_span]
        scaled_ref[:, lanes] = scaled
        packed = jnp.where(lane == 2 * s, jnp.sum(scaled, axis=-1, keepdims=True), packed)
        packed = jnp.where(
            lane == 2 * s + 1, jnp.sum(scaled * hat, axis=-1, keepdims=True), packed
        )
    sum_ref[...] = packed
    totals = jnp.concatenate(totals, axis=0)

    @pl.when(pl.program_id(0) == 0)
    def _():
        gain_out_ref[...] = totals

    @pl.when(pl.program_id(0) > 0)
    def _():
        gain_out_ref[...] += totals


def norm_slopes(own, got, ff_grad, low, stats, gains, which):
    tall, wide = low.shape
    width = wide // STREAMS
    rows = min(64, tall)
    row = lambda i, m: (i, 0)
    cube = pl.BlockSpec((4, rows, width), lambda i, m: (0, i, 0))
    return pl.pallas_call(
        slope_kernel,
        grid_spec=pltpu.PrefetchScalarGridSpec(
            num_scalar_prefetch=1,
            grid=(tall // rows,),
            in_specs=[
                cube,
                cube,
                pl.BlockSpec((1, rows, width), lambda i, m: (0, i, 0)),
                pl.BlockSpec((rows, wide), row),
                pl.BlockSpec((rows, 128), row),
                pl.BlockSpec(gains.shape, lambda i, m: (0, 0)),
            ],
            out_specs=[
                pl.BlockSpec((rows, wide), row),
                pl.BlockSpec((rows, 128), row),
                pl.BlockSpec((STREAMS, width), lambda i, m: (0, 0)),
            ],
        ),
        out_shape=[
            jax.ShapeDtypeStruct((tall, wide), f32),
            jax.ShapeDtypeStruct((tall, 128), f32),
            jax.ShapeDtypeStruct((STREAMS, width), f32),
        ],
        cost_estimate=spent(
            flops=12 * tall * wide, bytes_accessed=12 * tall * wide, transcendentals=0
        ),
        name="norm_slopes",
    )(which, own, got, ff_grad, low, stats, gains)


def grads_kernel(
    scaled_ref, mine_ref, theirs_ref, low_ref, stat_ref, cot_ref, cur_ref, last_ref,
    grad_ref, mix_ref, dot_ref,
):
    rows, width = cot_ref.shape
    lane = lax.broadcasted_iota(jnp.int32, (rows, 128), 1)
    means = (mine_ref[...] + theirs_ref[...]) / (2 * width)
    current = cur_ref[...].astype(f32)
    packed = jnp.zeros((rows, 128), f32)
    mixed = None
    for s in range(STREAMS):
        lanes = slice(s * width, (s + 1) * width)
        average, inverse = stat_ref[:, 2 * s : 2 * s + 1], stat_ref[:, 2 * s + 1 : 2 * s + 2]
        hat = (low_ref[:, lanes].astype(f32) - average) * inverse
        grad = inverse * (
            scaled_ref[:, lanes]
            - means[:, 2 * s : 2 * s + 1]
            - hat * means[:, 2 * s + 1 : 2 * s + 2]
        )
        if s == STREAMS - 1:
            grad = grad + cot_ref[...].astype(f32)
        grad = grad.astype(bf16)
        grad_ref[s] = grad
        grad = grad.astype(f32)
        term = last_ref[:, s : s + 1] * grad
        mixed = term if mixed is None else mixed + term
        packed = jnp.where(lane == s, jnp.sum(grad * current, axis=-1, keepdims=True), packed)
    mix_ref[...] = mixed
    dot_ref[...] = packed


def stream_grads(scaled, mine, theirs, low, stats, cot, current_half, last):
    tall, wide = low.shape
    width = wide // STREAMS
    rows = min(64, tall)
    row = lambda i: (i, 0)
    return pl.pallas_call(
        grads_kernel,
        grid=(tall // rows,),
        in_specs=[
            pl.BlockSpec((rows, wide), row),
            pl.BlockSpec((rows, 128), row),
            pl.BlockSpec((rows, 128), row),
            pl.BlockSpec((rows, wide), row),
            pl.BlockSpec((rows, 128), row),
            pl.BlockSpec((rows, width), row),
            pl.BlockSpec((rows, width), row),
            pl.BlockSpec((rows, 128), row),
        ],
        out_specs=[
            pl.BlockSpec((STREAMS, rows, width), lambda i: (0, i, 0)),
            pl.BlockSpec((rows, width), row),
            pl.BlockSpec((rows, 128), row),
        ],
        out_shape=[
            jax.ShapeDtypeStruct((STREAMS, tall, width), bf16),
            jax.ShapeDtypeStruct((tall, width), f32),
            jax.ShapeDtypeStruct((tall, 128), f32),
        ],
        cost_estimate=spent(
            flops=12 * tall * wide, bytes_accessed=10 * tall * wide, transcendentals=0
        ),
        name="stream_grads",
    )(scaled, mine, theirs, low, stats, cot, current_half, last)


def turning_tables(places):
    half = ROT // 2
    inverse = jnp.exp(jnp.arange(half, dtype=f32) * (-2.0 * math.log(10000.0) / ROT))
    angles = places.astype(f32)[:, None] * inverse[None, :]
    cosine, sine = jnp.cos(angles), jnp.sin(angles)
    rows = places.shape[0]
    rest = jnp.zeros((rows, HDIM - ROT), f32)
    blank = jnp.zeros((rows, half), f32)
    return (
        jnp.concatenate([cosine, cosine, rest + 1.0], axis=1),
        jnp.concatenate([-sine, blank, rest], axis=1),
        jnp.concatenate([blank, sine, rest], axis=1),
    )


def local(
    history,
    slot_layer,
    current,
    positions,
    doc_ids,
    cotangent,
    norm_gains,
    generator_in,
    generator_out,
    query_weight,
    key_weight,
    value_weight,
    out_weight,
    up_weight,
    down_weight,
):
    dp_count = lax.axis_size("dp")
    depth_count = lax.axis_size("depth")
    dp_at = lax.axis_index("dp")
    model_at = lax.axis_index("mp")
    dp_bits = list(range(bit_count(dp_count)))
    slots, tokens_held, width = history.shape
    model = current.shape[1]
    rows_mb = current.shape[0] // MB
    length = depth_count * rows_mb
    heads_width = query_weight.shape[1]
    heads_each = heads_width // HDIM // depth_count
    own_rows = query_weight.shape[0]
    ff_width = up_weight.shape[1]
    ff_part = ff_width // dp_count
    both = ("dp", "depth")

    def half_of(values, axis, which):
        return lax.dynamic_slice_in_dim(values, which * width, width, axis)

    partners = jnp.stack([dp_at ^ m for m in range(dp_count)]).astype(jnp.int32)
    ff_local = ff_split(up_weight, down_weight, partners)
    ff_rows = [ff_local[0]] + [swap_mask(ff_local[m], "dp", m) for m in range(1, dp_count)]
    ff_rows = place_many(partners, ff_rows).reshape(2 * dp_count, own_rows, ff_part)

    small_cols = jnp.concatenate(
        [generator_in, norm_gains.T, jnp.zeros((own_rows, 128 - GEN - 5), bf16)], axis=1
    )
    small_all = gather_small(small_cols, both).reshape(model, 128)
    gen_first = small_all[:, :GEN]
    gen_first, ff_rows = fence(gen_first, ff_rows)
    gain_float = small_all[:, GEN : GEN + 5].astype(f32).T
    second_rows = generator_out.shape[0]
    second_pad = -second_rows % 128
    second_all = gather_small(jnp.pad(generator_out, (0, second_pad))[None], both)
    gen_second = second_all.reshape(-1, second_rows + second_pad)[:, :second_rows]
    second_low = gen_second.reshape(GEN, STREAMS * MIX)

    stacked = jnp.concatenate([query_weight, key_weight, value_weight, out_weight.T], axis=0)
    over_depth = lax.all_gather(stacked, "depth", axis=0, tiled=True)
    current_f = current.astype(f32)
    current_half = half_of(current, 1, model_at)
    mean_square = jnp.mean(current_f * current_f, axis=-1, keepdims=True)
    inverse_rms = lax.rsqrt(mean_square + RMS_EPSILON)
    unit = current_f * inverse_rms
    gen_normed = (unit * gain_float[4]).astype(bf16)
    gen_pre = dot_nn(gen_normed, gen_first)
    gen_hidden = gelu_exact(gen_pre).astype(bf16)
    column = jnp.arange(STREAMS * MIX)
    last_col = (column % MIX == MIX - 1).astype(f32)
    mixing = (dot_nn(gen_hidden, second_low) + last_col).astype(bf16)
    pick_last = (column[:, None] == (jnp.arange(128) * MIX + MIX - 1)[None, :]).astype(bf16)
    last = dot_nn(mixing, pick_last)

    layer_of = jnp.tile(slot_layer, STREAMS)
    stream_of = jnp.repeat(jnp.arange(STREAMS), slots)
    from_col = jnp.where(layer_of < MIX, stream_of * MIX + layer_of, -1)
    pick = (column[:, None] == from_col[None, :]).astype(f32)
    mix_all = gather_small(mixing, ("depth",)).reshape(depth_count * MB * rows_mb, STREAMS * MIX)
    slot_mix = dot_nn(mix_all, pick.astype(bf16))
    places_all = gather_small(positions, ("depth",))

    def over_depth_swap(values):
        return lax.all_to_all(values, "depth", 0, 0, tiled=True)

    def mix_part(micro_at, slot_mix):
        partial = mix_streams(slot_mix, history, micro_at, depth_count, rows_mb)
        return partial.reshape(STREAMS, depth_count, rows_mb, width)

    slot_mix, ff_rows, cotangent, places_all = fence(slot_mix, ff_rows, cotangent, places_all)
    partial = mix_part(0, slot_mix)
    partial_next = mix_part(1, slot_mix)

    weights_line = LineGather(ff_rows)
    weights_line.step()
    cot_pieces = lax.all_gather(cotangent, "dp", axis=0, tiled=True)
    over_depth, partial, partial_next = weights_line.hold(over_depth, partial, partial_next)
    pieces = [over_depth]
    weights = place_block(None, pieces[0][None], place_index(0), dp_count)
    hops_left = [(p, at) for at in range(len(dp_bits)) for p in range(1 << at)]
    placed = 1
    cots = None
    sums, sums_next = LineScatter(partial), LineScatter(partial_next)
    own_tables = turning_tables(positions)
    tables = [
        turning_tables(places_all[:, m * rows_mb : (m + 1) * rows_mb].reshape(length))
        for m in range(MB)
    ]
    for hop in range(1, depth_count):
        sums.step_with(weights_line)
        last_hop = hop == depth_count - 1
        for place in range(placed, len(pieces)):
            weights = place_block(weights, pieces[place][None], place_index(place), dp_count)
        placed = len(pieces)
        while hops_left:
            place, at = hops_left.pop(0)
            pieces.append(core_hop(pieces[place], at))
            if len(hops_left) <= depth_count - 1 - hop:
                break
        if last_hop:
            cot_full = join_halves(cotangent, other_core(cotangent), model_at)
            ff_weights = weights_line.placed()
            cots = cot_full, cotangent, ff_weights
        (state,) = weights_line.hold(
            (sums.up, sums.down, pieces, weights, cots, own_tables, tables, cot_pieces)
        )
        sums.up, sums.down, pieces, weights, cots, own_tables, tables, cot_pieces = state
    cot_full, cotangent, ff_weights = cots
    for place in range(placed, len(pieces)):
        weights = place_block(weights, pieces[place][None], place_index(place), dp_count)
    weights = weights.reshape(dp_count, depth_count, 4, own_rows, heads_width)
    ff_weights = ff_weights.reshape(2, dp_count, depth_count, own_rows, ff_part)

    document_view = doc_ids.reshape(depth_count, MB, rows_mb)
    which = model_at.astype(jnp.int32)[None]
    depth_at = lax.axis_index("depth").astype(jnp.int32)[None]
    gains = gain_float

    def enter(micro_at, sums):
        span = slice(micro_at * rows_mb, (micro_at + 1) * rows_mb)
        low, resid = total_streams(sums, current_half[span], last[span], depth_at)
        normed, ff_normed, stats = norm_streams(low, other_core(low), gains, which)
        packed = project_heads(
            normed,
            cot_full[span],
            weights,
            [t[span] for t in own_tables],
            depth_count,
        )
        return dict(
            low=low, resid=resid, normed=normed, ff_normed=ff_normed, stats=stats, packed=packed
        )

    def attention(micro_at, by_head):
        documents = document_view[:, micro_at].reshape(length)
        by_head = by_head.reshape(length, 4 * heads_each * HDIM)
        answer = attend(by_head, documents, tables[micro_at], heads_each)
        return answer.reshape(depth_count, rows_mb, 4 * heads_each * HDIM)

    place_list = jnp.stack([place_index(p) for p in range(dp_count)]).astype(jnp.int32)

    def group_rows(ff_normed):
        return lax.all_gather(ff_normed, "dp", axis=0, tiled=True)

    def group_joined(mine):
        return join_halves(mine, other_core(mine), model_at)

    def hidden_units(micro_at, group_normed):
        hidden, grad_up, own, other = feed_forward(
            group_normed, cot_group, micro_at, ff_weights, which
        )
        return dict(group_normed=group_normed, hidden=hidden, grad_up=grad_up), (own, other)

    def group_back_rest(near):
        for at in reversed(range(len(dp_bits) - 1)):
            half = 1 << at
            near = near[:half] + core_hop(near[half:].astype(bf16), at).astype(f32)
        return near[0]

    def group_back(own, other):
        near, far = group_split(own, other, place_list)
        return group_back_rest(near + core_hop(far, len(dp_bits) - 1).astype(f32))

    def back(kept, answer):
        (theirs,) = back_project(answer, weights, 1 - which, bf16, False)
        got = other_core(theirs)
        own, flat = back_project(answer, weights, which, f32, True)
        return own, got, flat

    def leave(micro_at, kept, own, got, ff_sum):
        span = slice(micro_at * rows_mb, (micro_at + 1) * rows_mb)
        rows = (kept["resid"] + own[0] + got[0].astype(f32) + ff_sum[1]).astype(bf16)
        low, stats = kept["low"], kept["stats"]
        scaled, sums, gain_part = norm_slopes(own, got, ff_sum, low, stats, gains, which)
        grad_low, current_mix, last_dot = stream_grads(
            scaled, sums, other_core(sums), low, stats, cotangent[span], current_half[span], last[span]
        )
        kept.update(layer_rows=rows, gain=gain_part, current_mix=current_mix, last_dot=last_dot)
        return grad_low

    ((sums.up, sums.down),) = sums_next.step((sums.up, sums.down))
    first = enter(0, sums)
    mine = group_rows(first["ff_normed"])
    packed, mine, cot_pieces = sums_next.hold(first["packed"], mine, cot_pieces)
    while sums_next.at < depth_count - 3:
        sums_next.step()
        sums_next.hold()
    packed, mine, cot_pieces = sums_next.step(packed, mine, cot_pieces)
    by_head = over_depth_swap(packed)
    cot_group = join_halves(cot_pieces, other_core(cot_pieces), model_at)
    cot_group = cot_group.reshape(dp_count, MB, rows_mb, model)
    kept, ff_parts = hidden_units(0, group_joined(mine))
    first.update(kept)
    by_head, ff_parts, cot_group = sums_next.hold(by_head, ff_parts, cot_group)
    by_head, ff_parts = sums_next.step(by_head, ff_parts)
    answer = attention(0, by_head)
    answer, ff_parts = sums_next.hold(answer, ff_parts)

    answer = over_depth_swap(answer)
    second = enter(1, sums_next)
    near, far = group_split(ff_parts[0], other_core(ff_parts[1]), place_list)
    near = near + core_hop(far, len(dp_bits) - 1).astype(f32)
    answer, packed, ff_normed, near = fence(
        answer, second["packed"], second["ff_normed"], near
    )
    by_head = over_depth_swap(packed)
    mine = group_rows(ff_normed)
    own, got, first["flat"] = back(first, answer)
    grad_low = leave(0, first, own, got, group_back_rest(near))
    by_head, grad_low, mine, first["layer_rows"] = fence(
        by_head, grad_low, mine, first["layer_rows"]
    )
    saved = [first, second]

    def each(name):
        return [s[name] for s in saved]

    def rows_of(name):
        return jnp.concatenate(each(name), axis=0)

    def place_grads(place, dtype):
        return attention_grads(
            each("normed"),
            cot_full,
            each("flat"),
            place_list[place : place + 1],
            depth_count,
            dp_count,
            dtype,
        )

    half = dp_count // 2
    hops_left = [
        (p, at) for at in reversed(range(len(dp_bits))) for p in range(1 << at, 2 << at)
    ]
    pieces = {}

    def sums_hop():
        place, at = hops_left.pop(0)
        arrived = core_hop(pieces.pop(place).astype(bf16), at)
        target = place - (1 << at)
        pieces[target] = pieces[target].astype(f32) + arrived.astype(f32)

    grad_line = LineGather(grad_low)
    grad_line.step()
    answer = attention(1, by_head)
    kept, ff_parts = hidden_units(1, group_joined(mine))
    second.update(kept)
    answer, ff_parts = grad_line.hold(answer, ff_parts)
    answer = over_depth_swap(answer)
    near, far = group_split(ff_parts[0], other_core(ff_parts[1]), place_list)
    ff_products = hidden_grads(
        each("group_normed"), cot_group, each("grad_up"), each("hidden"), dp_count, depth_count
    )
    near = near + core_hop(far, len(dp_bits) - 1).astype(f32)
    answer, near, ff_products = fence(answer, near, ff_products)

    ff_sums = LineScatter(ff_products)
    (answer,) = ff_sums.step_with(grad_line, answer)
    own, got, flat = back(second, answer)
    ff_sum = group_back_rest(near)
    second["flat"] = flat
    (state,) = grad_line.hold((ff_sums.up, ff_sums.down, own, got, flat, ff_sum))
    ff_sums.up, ff_sums.down, own, got, second["flat"], ff_sum = state
    while len(grad_line.up) < depth_count - 1:
        ff_sums.step_with(grad_line)
        (state,) = grad_line.hold((ff_sums.up, ff_sums.down))
        ff_sums.up, ff_sums.down = state
    (ff_sum,) = ff_sums.step_with(grad_line, ff_sum)
    grad_low = leave(1, second, own, got, ff_sum)
    pieces = {p: place_grads(p, bf16 if p >= half else f32) for p in range(dp_count)}
    sums_hop()
    (state,) = grad_line.hold((ff_sums.up, ff_sums.down, grad_low, pieces, second["layer_rows"]))
    ff_sums.up, ff_sums.down, grad_low, pieces, second["layer_rows"] = state

    last_line = LineGather(grad_low)
    last_line.step()
    if hops_left:
        sums_hop()
    grad_first = grad_line.placed().reshape(STREAMS, length, width)
    history_grad, slot_part = unmix_streams(
        slot_mix, history, grad_first, 0, depth_count, rows_mb, None
    )
    slot_parts = [slot_part.reshape(depth_count, 1, rows_mb, 128)]
    pieces, history_grad = last_line.hold(pieces, history_grad)
    (pieces,) = ff_sums.step(pieces)
    while hops_left:
        sums_hop()
    (pieces,) = ff_sums.hold(pieces)
    out_sums = LineScatter(pieces[0].reshape(1, depth_count, 4 * own_rows, heads_width))
    for hop in range(2, depth_count):
        last_line.step()
        out_sums.step()
        if hop == depth_count - 1:
            ff_grads = end_sums(ff_sums, bf16).reshape(2, dp_count, own_rows, ff_part)
            ff_pieces = [
                lax.dynamic_index_in_dim(ff_grads, partners[m], 1, keepdims=False)
                for m in range(dp_count)
            ]
            ff_pieces = ff_pieces[:1] + [
                swap_mask(ff_pieces[m], "dp", m) for m in range(1, dp_count)
            ]
            ff_sums.up = ff_sums.down = ff_pieces
            early = last_line.placed_early()
            history_grad, slot_part = unmix_streams(
                slot_mix,
                history,
                early.reshape(STREAMS, length, width),
                1,
                depth_count,
                rows_mb,
                history_grad,
            )
        (state,) = last_line.hold(
            (out_sums.up, out_sums.down, ff_sums.up, ff_sums.down, history_grad, slot_part)
        )
        out_sums.up, out_sums.down, ff_sums.up, ff_sums.down, history_grad, slot_part = state
    out_sums.step()
    ff_pieces = ff_sums.up
    far_grads, far_index = last_line.farthest(early)
    history_grad, far_part = unmix_one(
        slot_mix, history, far_grads, 1, far_index, rows_mb, history_grad
    )
    slot_part = slot_part.reshape(depth_count, rows_mb, 128)
    slot_part = lax.dynamic_update_index_in_dim(slot_part, far_part, far_index, 0)
    slot_parts.append(slot_part[:, None])

    slot_grads = jnp.concatenate(slot_parts, axis=1).reshape(-1, 128)[:, : STREAMS * slots]
    mix_grads = dot_exact(slot_grads, pick.T).reshape(depth_count, MB * rows_mb, STREAMS * MIX)
    mix_grads, ff_pieces = out_sums.hold(mix_grads, ff_pieces)
    grad_mixing = scatter_small(mix_grads, ("depth",))
    up_grad, down_grad = ff_join(jnp.stack(ff_pieces), partners)
    last_dots = rows_of("last_dot")
    grad_mixing = grad_mixing + dot_exact(last_dots, pick_last.astype(f32).T)
    grad_mixing = grad_mixing + other_core(grad_mixing)

    second_float = second_low.astype(f32)
    grad_second = dot_exact(gen_hidden.astype(f32).T, grad_mixing)
    grad_pre = dot_exact(grad_mixing, second_float.T) * gelu_slope(gen_pre)
    grad_first = dot_exact(gen_normed.astype(f32).T, grad_pre)
    grad_gen_normed = dot_exact(grad_pre, gen_first.astype(f32).T)
    gain_gen = jnp.sum(grad_gen_normed * unit, axis=0)
    scattered = end_sums(out_sums, f32).reshape(4, own_rows, heads_width)
    grad_unit = grad_gen_normed * gain_float[4]
    shared = jnp.mean(grad_unit * unit, axis=-1, keepdims=True)
    current_gen = half_of(inverse_rms * (grad_unit - unit * shared), 1, model_at)
    current_grad = rows_of("current_mix") + current_gen

    gain_own = sum(s["gain"] for s in saved)
    gain_other = other_core(gain_own)
    gain_all = jnp.where(
        model_at == 0,
        jnp.concatenate([gain_own, gain_other], axis=1),
        jnp.concatenate([gain_other, gain_own], axis=1),
    )
    gain_all = jnp.concatenate([gain_all, gain_gen[None]], axis=0)
    small_grads = jnp.concatenate(
        [grad_first, gain_all.T, jnp.zeros((model, 128 - GEN - 5), f32)], axis=1
    )
    small_grads = scatter_small(small_grads.reshape(-1, own_rows, 128), both)
    second_grads = jnp.pad(grad_second.reshape(-1, second_rows), ((0, 0), (0, second_pad)))
    second_grads = scatter_small(second_grads[:, None], both)

    return (
        rows_of("layer_rows"),
        history_grad,
        current_grad,
        small_grads[:, GEN : GEN + 5].T,
        small_grads[:, :GEN],
        second_grads[0, :second_rows],
        scattered[0],
        scattered[1],
        scattered[2],
        scattered[3].T,
        up_grad,
        down_grad,
    )


def solution(mesh):
    return jax.shard_map(
        local,
        mesh=mesh,
        in_specs=(
            P("depth", "dp", "mp"),
            P("depth"),
            P(("dp", "depth"), None),
            P(("dp", "depth")),
            P("dp"),
            P(("dp", "depth"), "mp"),
            P(None, ("dp", "depth")),
            P(("dp", "depth"), None),
            P(("dp", "depth")),
            P(("dp", "depth"), "mp"),
            P(("dp", "depth"), "mp"),
            P(("dp", "depth"), "mp"),
            P("mp", ("dp", "depth")),
            P(("dp", "depth"), "mp"),
            P("mp", ("dp", "depth")),
        ),
        out_specs=(
            P(("dp", "depth"), "mp"),
            P("depth", "dp", "mp"),
            P(("dp", "depth"), "mp"),
            P(None, ("dp", "depth")),
            P(("dp", "depth"), None),
            P(("dp", "depth")),
            P(("dp", "depth"), "mp"),
            P(("dp", "depth"), "mp"),
            P(("dp", "depth"), "mp"),
            P("mp", ("dp", "depth")),
            P(("dp", "depth"), "mp"),
            P("mp", ("dp", "depth")),
        ),
        check_vma=False,
    )
```

```python
import functools
import math

import jax
import jax.numpy as jnp
from jax import lax
from jax.experimental import pallas as pl
from jax.experimental.pallas import tpu as pltpu
from jax.sharding import PartitionSpec as P

HDIM = 128
ROT = 32
GEN = 72
MB = 2
MIX = 18
STREAMS = 4
COST = 20

PRECISE = lax.Precision.HIGHEST
NORM_EPSILON = 1e-05
RMS_EPSILON = 1e-06
MASKED = -1e30

bf16 = jnp.bfloat16
f32 = jnp.float32


def dot_nn(a, b):
    return lax.dot_general(a, b, (((1,), (0,)), ((), ())), preferred_element_type=f32)


def dot_nt(a, b):
    return lax.dot_general(a, b, (((1,), (1,)), ((), ())), preferred_element_type=f32)


def dot_tn(a, b):
    return lax.dot_general(a, b, (((0,), (0,)), ((), ())), preferred_element_type=f32)


def dot_exact(a, b):
    return jnp.dot(a, b, precision=PRECISE, preferred_element_type=f32)


def gelu_exact(values):
    return jax.nn.gelu(values, approximate=False)


def gelu_slope(values):
    result, pullback = jax.vjp(gelu_exact, values)
    return pullback(jnp.ones_like(result))[0]


def bit_count(size):
    count = size.bit_length() - 1
    assert 1 << count == size
    return count


def swap_mask(values, axis, mask):
    size = lax.axis_size(axis)
    return lax.ppermute(values, axis, [(i, i ^ mask) for i in range(size)])


def gather_masked(values, axis, order):
    pieces = {0: values}
    for bit in order:
        arrived = {m | (1 << bit): swap_mask(v, axis, 1 << bit) for m, v in pieces.items()}
        pieces.update(arrived)
    return [pieces[m] for m in range(len(pieces))]


def scatter_masked(pieces, axis, order, link=bf16):
    pieces = dict(enumerate(pieces))
    for bit in order:
        flag = 1 << bit
        for m in [m for m in pieces if m & flag]:
            arrived = swap_mask(pieces.pop(m).astype(link), axis, flag)
            pieces[m ^ flag] = pieces[m ^ flag].astype(f32) + arrived.astype(f32)
    return pieces[0]


def core_orders():
    bits = list(range(bit_count(lax.axis_size("dp"))))
    return bits, bits[1:] + bits[:1]


def place_mask(place):
    masks = []
    for order in core_orders():
        masks.append(sum(1 << bit for at, bit in enumerate(order) if (place >> at) & 1))
    return jnp.where(lax.axis_index("mp") % 2 == 0, masks[0], masks[1])


def place_index(place):
    return lax.axis_index("dp") ^ place_mask(place)


def core_hop(values, at):
    orders, cores = core_orders(), lax.axis_size("mp")
    pairs = []
    for i in range(lax.axis_size("dp")):
        for core in range(cores):
            partner = i ^ (1 << orders[core % 2][at])
            pairs.append((i * cores + core, partner * cores + core))
    return lax.ppermute(values, ("dp", "mp"), pairs)


def group_hop(pieces, at):
    return jnp.concatenate([pieces, core_hop(pieces, at)], axis=0)


def place_of(core):
    partner = jnp.arange(lax.axis_size("dp")) ^ lax.axis_index("dp")
    places = []
    for order in core_orders():
        places.append(sum(((partner >> bit) & 1) << at for at, bit in enumerate(order)))
    return jnp.where(core % 2 == 0, places[0], places[1])


def reorder_masked(stacked, axis):
    count = bit_count(stacked.shape[0])
    here = lax.axis_index(axis)
    shape = stacked.shape
    values = stacked.reshape((2,) * count + shape[1:])
    for bit in range(count):
        turned = jnp.flip(values, count - 1 - bit)
        values = jnp.where(((here >> bit) & 1) == 1, turned, values)
    return values.reshape(shape)


def gather_small(values, axes):
    shape = values.shape
    values = values[None]
    for axis in reversed(axes):
        order = range(bit_count(lax.axis_size(axis)))
        stacked = jnp.stack(gather_masked(values, axis, order))
        values = reorder_masked(stacked, axis)
        values = values.reshape((-1,) + shape)
    return values


def scatter_small(values, axes):
    for axis in axes:
        size = lax.axis_size(axis)
        values = values.reshape((size, values.shape[0] // size) + values.shape[1:])
        turned = reorder_masked(values, axis)
        order = reversed(range(bit_count(size)))
        values = scatter_masked([turned[m] for m in range(size)], axis, order, f32)
    return values[0]


def line_size():
    return lax.axis_size("depth"), lax.axis_index("depth")


def fence(*values):
    return lax.optimization_barrier(values)


class LineGather:

    def __init__(self, values):
        self.up, self.down = [values], [values]

    def step(self):
        size, _ = line_size()
        at = len(self.up)
        if at < size:
            up_pairs = [(i, i + 1) for i in range(at - 1, size - 1)]
            down_pairs = [(i, i - 1) for i in range(1, size - at + 1)]
            self.up.append(lax.ppermute(self.up[-1], "depth", up_pairs))
            self.down.append(lax.ppermute(self.down[-1], "depth", down_pairs))

    def hold(self, *others):
        kept = fence((self.up[1:], self.down[1:]), *others)
        (up, down), rest = kept[0], kept[1:]
        self.up, self.down = self.up[:1] + list(up), self.down[:1] + list(down)
        return rest

    def placed_early(self):
        size, here = line_size()
        steps = jnp.arange(size)
        index = lax.rem(here - steps + size, size)
        own = self.up[0]
        blocks = self.up[: size - 1] + [own]
        instead = [own] + self.down[1 : size - 1][::-1]
        return place_line(index, here >= steps, blocks, instead)

    def farthest(self, early):
        size, here = line_size()
        last = jnp.where(here == size - 1, self.up[size - 1], early[:, 0])
        return jnp.where(here == 0, self.down[size - 1], last), jnp.where(here == 0, size - 1, 0)

    def placed(self):
        size, here = line_size()
        steps = jnp.arange(size)
        index = lax.rem(here - steps + size, size)
        return place_line(index, here >= steps, self.up, self.down[1:][::-1])


class LineScatter:

    def __init__(self, terms):
        self.terms, self.at = terms, 0
        self.up = self.down = None

    def step(self, *later):
        size, here = line_size()
        self.at += 1
        if self.at >= size:
            return later
        goes_up, goes_down = hop_sums(
            self.terms,
            jnp.minimum(size - self.at + here, size - 1),
            jnp.maximum(here - size + self.at, 0),
            self.up,
            self.down,
        )
        (goes_up, goes_down), *later = fence((goes_up, goes_down), *later)
        up_pairs = [(i, i + 1) for i in range(min(self.at, size - 1))]
        down_pairs = [(size - 1 - i, size - 2 - i) for i in range(min(self.at, size - 1))]
        self.up = lax.ppermute(goes_up, "depth", up_pairs)
        self.down = lax.ppermute(goes_down, "depth", down_pairs)
        return later

    def step_with(self, line, *later):
        size, here = line_size()
        lead, _, tall, wide = self.terms.shape
        shape = line.up[0].shape
        if (
            len(line.up) != self.at + 2
            or self.at + 2 > size - 1
            or math.prod(shape) != lead * tall * wide
            or shape[2] != wide
        ):
            line.step()
            return self.step(*later)
        self.at += 1
        goes = hop_sums(
            self.terms,
            jnp.minimum(size - self.at + here, size - 1),
            jnp.maximum(here - size + self.at, 0),
            self.up,
            self.down,
            [v[-1].reshape(lead, tall, wide) for v in (line.up, line.down)],
            [here < self.at, here > size - 1 - self.at],
        )
        goes, *later = fence(goes, *later)
        self.up = lax.ppermute(goes[0], "depth", [(i, i + 1) for i in range(size - 1)])
        self.down = lax.ppermute(goes[1], "depth", [(i, i - 1) for i in range(1, size)])
        line.up.append(self.up.reshape(shape))
        line.down.append(self.down.reshape(shape))
        return later

    def hold(self, *others):
        (self.up, self.down), *rest = fence((self.up, self.down), *others)
        return rest


def other_core(values):
    return swap_mask(values, "mp", 1)


def join_kernel(model_ref, own_ref, other_ref, out_ref):
    width = own_ref.shape[1]
    own_at = pl.multiple_of(model_ref[0] * width, width)
    other_at = pl.multiple_of((1 - model_ref[0]) * width, width)
    out_ref[:, pl.ds(own_at, width)] = own_ref[...]
    out_ref[:, pl.ds(other_at, width)] = other_ref[...]


def join_halves(own, other, model_at):
    tall, width = own.shape
    rows = min(256, tall)
    return pl.pallas_call(
        join_kernel,
        grid_spec=pltpu.PrefetchScalarGridSpec(
            num_scalar_prefetch=1,
            grid=(tall // rows,),
            in_specs=[pl.BlockSpec((rows, width), lambda i, m: (i, 0))] * 2,
            out_specs=pl.BlockSpec((rows, 2 * width), lambda i, m: (i, 0)),
        ),
        out_shape=jax.ShapeDtypeStruct((tall, 2 * width), own.dtype),
        cost_estimate=spent(
            flops=0, bytes_accessed=8 * tall * width, transcendentals=0
        ),
        name="join_halves",
    )(model_at.astype(jnp.int32)[None], own, other)


def spent(flops, bytes_accessed, transcendentals):
    return pl.CostEstimate(
        flops=flops // COST, bytes_accessed=bytes_accessed // COST, transcendentals=transcendentals // COST
    )


def chunk_of(tall, wide):
    rows = tall
    while rows * wide > 1 << 19 and rows % 32 == 0:
        rows //= 2
    return rows


def place_kernel(at_ref, *refs):
    if len(refs) < 4:
        refs[-1][0, 0] = refs[0][0]
        return

    @pl.when(at_ref[1] == 1)
    def _():
        refs[-1][0, 0] = refs[0][0]

    @pl.when(at_ref[1] == 0)
    def _():
        refs[-1][0, 0] = refs[1][0]


def place_block(buffer, block, index, count, instead=None, first=None):
    lead, tall, wide = block.shape
    rows = chunk_of(tall, wide)
    spec = pl.BlockSpec((1, rows, wide), lambda l, i, m: (l, i, 0))
    blocks = [block] if instead is None else [block, instead]
    where = [index, 1 if first is None else first]
    where = jnp.stack([jnp.asarray(v).astype(jnp.int32) for v in where])
    in_specs, operands, aliases = [spec] * len(blocks), list(blocks), {}
    if buffer is not None or instead is not None:
        in_specs.append(pl.BlockSpec(memory_space=pl.ANY))
        operands.append(block if buffer is None else buffer)
        aliases = {} if buffer is None else {len(operands): 0}
    return pl.pallas_call(
        place_kernel,
        grid_spec=pltpu.PrefetchScalarGridSpec(
            num_scalar_prefetch=1,
            grid=(lead, tall // rows),
            in_specs=in_specs,
            out_specs=pl.BlockSpec((1, 1, rows, wide), lambda l, i, m: (l, m[0], i, 0)),
        ),
        out_shape=jax.ShapeDtypeStruct((lead, count, tall, wide), block.dtype),
        input_output_aliases=aliases,
        cost_estimate=spent(
            flops=0, bytes_accessed=4 * lead * tall * wide, transcendentals=0
        ),
        name="place_block",
    )(where, *operands)


def place_line_kernel(size, at_ref, *refs):
    out_ref = refs[-1]
    for step in range(size):
        if step == 0 or len(refs) == size + 1:
            out_ref[0, at_ref[step]] = refs[step][0]
            continue

        @pl.when(at_ref[size + step] == 1)
        def _(step=step):
            out_ref[0, at_ref[step]] = refs[step][0]

        @pl.when(at_ref[size + step] == 0)
        def _(step=step):
            out_ref[0, at_ref[step]] = refs[size + step - 1][0]


def place_line(index, first, blocks, instead):
    size = len(blocks)
    lead, tall, wide = blocks[0].shape
    rows = tall
    while rows * wide > 1 << 18 and rows % 32 == 0:
        rows //= 2
    spec = pl.BlockSpec((1, rows, wide), lambda l, i, m: (l, i, 0))
    where = jnp.concatenate([index, first]).astype(jnp.int32)
    operands = list(blocks) + list(instead)
    return pl.pallas_call(
        functools.partial(place_line_kernel, size),
        grid_spec=pltpu.PrefetchScalarGridSpec(
            num_scalar_prefetch=1,
            grid=(lead, tall // rows),
            in_specs=[spec] * len(operands),
            out_specs=pl.BlockSpec((1, size, rows, wide), lambda l, i, m: (l, 0, i, 0)),
        ),
        out_shape=jax.ShapeDtypeStruct((lead, size, tall, wide), blocks[0].dtype),
        compiler_params=pltpu.CompilerParams(vmem_limit_bytes=40 << 20),
        cost_estimate=spent(
            flops=0, bytes_accessed=6 * size * lead * tall * wide, transcendentals=0
        ),
        name="place_line",
    )(where, *operands)


def place_many(index, blocks):
    ones = jnp.ones(len(blocks), jnp.int32)
    return place_line(index, ones, blocks, [])


def group_join_kernel(at_ref, own_ref, other_ref, out_ref):
    width = own_ref.shape[2]
    own_span, other_span = own_spans(at_ref, width)
    out_ref[:, own_span] = own_ref[0]
    out_ref[:, other_span] = other_ref[0]


def group_join(own, other, model_at):
    count, tall, width = own.shape
    rows = chunk_of(tall, width)
    per = tall // rows
    where = jnp.concatenate([model_at[None], place_of(model_at), place_of(1 - model_at)])
    return pl.pallas_call(
        group_join_kernel,
        grid_spec=pltpu.PrefetchScalarGridSpec(
            num_scalar_prefetch=1,
            grid=(count, per),
            in_specs=[
                pl.BlockSpec((1, rows, width), lambda n, i, m: (m[1 + n], i, 0)),
                pl.BlockSpec((1, rows, width), lambda n, i, m: (m[1 + count + n], i, 0)),
            ],
            out_specs=pl.BlockSpec((rows, 2 * width), lambda n, i, m: (n * per + i, 0)),
        ),
        out_shape=jax.ShapeDtypeStruct((count * tall, 2 * width), own.dtype),
        cost_estimate=spent(
            flops=0, bytes_accessed=8 * count * tall * width, transcendentals=0
        ),
        name="group_join",
    )(where.astype(jnp.int32), own, other)


def group_split_kernel(at_ref, near_own, near_other, far_own, far_other, near_ref, far_ref):
    near_ref[0, 0] = near_own[0] + near_other[0].astype(f32)
    far_ref[0, 0] = (far_own[0] + far_other[0].astype(f32)).astype(bf16)


def group_split(own, other, places):
    _, tall, width = own.shape
    count = places.shape[0]
    half, rows = count // 2, tall // count
    near = pl.BlockSpec((1, rows, width), lambda p, k, m: (k, m[p], 0))
    far = pl.BlockSpec((1, rows, width), lambda p, k, m: (k, m[half + p], 0))
    out = pl.BlockSpec((1, 1, rows, width), lambda p, k, m: (p, k, 0, 0))
    return pl.pallas_call(
        group_split_kernel,
        grid_spec=pltpu.PrefetchScalarGridSpec(
            num_scalar_prefetch=1,
            grid=(half, 2),
            in_specs=[near, near, far, far],
            out_specs=[out, out],
        ),
        out_shape=[
            jax.ShapeDtypeStruct((half, 2, rows, width), f32),
            jax.ShapeDtypeStruct((half, 2, rows, width), bf16),
        ],
        cost_estimate=spent(
            flops=2 * tall * width, bytes_accessed=20 * tall * width, transcendentals=0
        ),
        name="group_split",
    )(places, own, other, own, other)


def hop_kernel(has_sums, has_blocks, at_ref, *refs):
    ins, outs = list(refs[:-2]), refs[-2:]
    terms, ins = ins[:2], ins[2:]
    sums, ins = (ins[:2], ins[2:]) if has_sums else (None, ins)

    def send_sum(way):
        term = terms[way][0, 0].astype(f32)
        if sums is not None:
            term = term + sums[way][0].astype(f32)
        outs[way][0] = term.astype(bf16)

    for way in range(2):
        if not has_blocks:
            send_sum(way)
            continue
        pl.when(at_ref[2 + way] == 1)(functools.partial(send_sum, way))

        @pl.when(at_ref[2 + way] == 0)
        def _(way=way):
            outs[way][0] = ins[way][0]


def hop_sums(terms, up_at, down_at, up, down, blocks=None, first=None):
    lead, _, tall, wide = terms.shape
    rows = chunk_of(tall, wide)
    block = pl.BlockSpec((1, rows, wide), lambda l, i, m: (l, i, 0))
    in_specs = [
        pl.BlockSpec((1, 1, rows, wide), lambda l, i, m: (l, m[0], i, 0)),
        pl.BlockSpec((1, 1, rows, wide), lambda l, i, m: (l, m[1], i, 0)),
    ]
    operands = [terms, terms]
    where = [up_at, down_at]
    if up is not None:
        in_specs += [block, block]
        operands += [up, down]
    if blocks is not None:
        in_specs += [block, block]
        operands += list(blocks)
        where += list(first)
    return pl.pallas_call(
        functools.partial(hop_kernel, up is not None, blocks is not None),
        grid_spec=pltpu.PrefetchScalarGridSpec(
            num_scalar_prefetch=1,
            grid=(lead, tall // rows),
            in_specs=in_specs,
            out_specs=[block, block],
        ),
        out_shape=[jax.ShapeDtypeStruct((lead, tall, wide), bf16)] * 2,
        cost_estimate=spent(
            flops=2 * lead * tall * wide, bytes_accessed=12 * lead * tall * wide, transcendentals=0
        ),
        name="hop_sums",
    )(jnp.stack(where).astype(jnp.int32), *operands)


def end_kernel(at_ref, term_ref, up_ref, down_ref, out_ref):
    total = term_ref[0, 0].astype(f32) + up_ref[0].astype(f32) + down_ref[0].astype(f32)
    out_ref[0] = total.astype(out_ref.dtype)


def end_sums(sums, dtype):
    lead, _, tall, wide = sums.terms.shape
    rows = chunk_of(tall, wide)
    block = pl.BlockSpec((1, rows, wide), lambda l, i, m: (l, i, 0))
    return pl.pallas_call(
        end_kernel,
        grid_spec=pltpu.PrefetchScalarGridSpec(
            num_scalar_prefetch=1,
            grid=(lead, tall // rows),
            in_specs=[
                pl.BlockSpec((1, 1, rows, wide), lambda l, i, m: (l, m[0], i, 0)),
                block,
                block,
            ],
            out_specs=block,
        ),
        out_shape=jax.ShapeDtypeStruct((lead, tall, wide), dtype),
        cost_estimate=spent(
            flops=2 * lead * tall * wide, bytes_accessed=10 * lead * tall * wide, transcendentals=0
        ),
        name="end_sums",
    )(lax.axis_index("depth").astype(jnp.int32)[None], sums.terms, sums.up, sums.down)


def attention_grad_kernel(
    at_ref, x0_ref, x1_ref, cot_ref, g0_ref, g1_ref, out_ref
):
    tall = x0_ref.shape[1]

    def store(total):
        out_ref[...] = total.reshape(out_ref.shape).astype(out_ref.dtype)

    @pl.when(pl.program_id(0) < 3)
    def _():
        store(dot_tn(x0_ref[0], g0_ref[0]) + dot_tn(x1_ref[0], g1_ref[0]))

    @pl.when(pl.program_id(0) == 3)
    def _():
        store(
            dot_tn(cot_ref[0:tall, :], g0_ref[0]) + dot_tn(cot_ref[tall : 2 * tall, :], g1_ref[0])
        )


def attention_grads(normed, cot, flat, place, depth_count, dp_count, dtype):
    _, tall, model = normed[0].shape
    heads_width = flat[0].shape[2]
    block = model // dp_count
    own_rows = block // depth_count
    normed_spec = pl.BlockSpec((1, tall, block), lambda k, m: (jnp.minimum(k, 2), 0, m[0]))
    flat_spec = pl.BlockSpec((1, tall, heads_width), lambda k, m: (lax.rem(k + 1, 4), 0, 0))
    return pl.pallas_call(
        attention_grad_kernel,
        grid_spec=pltpu.PrefetchScalarGridSpec(
            num_scalar_prefetch=1,
            grid=(4,),
            in_specs=[
                normed_spec,
                normed_spec,
                pl.BlockSpec((2 * tall, block), lambda k, m: (0, m[0])),
                flat_spec,
                flat_spec,
            ],
            out_specs=pl.BlockSpec(
                (depth_count, 1, own_rows, heads_width), lambda k, m: (0, k, 0, 0)
            ),
        ),
        out_shape=jax.ShapeDtypeStruct((depth_count, 4, own_rows, heads_width), dtype),
        compiler_params=pltpu.CompilerParams(vmem_limit_bytes=40 << 20),
        cost_estimate=spent(
            flops=16 * tall * block * heads_width,
            bytes_accessed=16 * block * heads_width,
            transcendentals=0,
        ),
        name="attention_grads",
    )(place, *normed, cot, *flat)


def hidden_grad_kernel(x0_ref, x1_ref, c0_ref, c1_ref, u0_ref, u1_ref, h0_ref, h1_ref, out_ref):
    def store(total):
        out_ref[...] = total.reshape(out_ref.shape).astype(bf16)

    @pl.when(pl.program_id(0) == 0)
    def _():
        store(dot_tn(x0_ref[...], u0_ref[...]) + dot_tn(x1_ref[...], u1_ref[...]))

    @pl.when(pl.program_id(0) == 1)
    def _():
        tall, wide = h0_ref.shape[0], c0_ref.shape[3]
        c0, c1 = c0_ref[:, 0].reshape(tall, wide), c1_ref[:, 0].reshape(tall, wide)
        store(dot_tn(c0, h0_ref[...]) + dot_tn(c1, h1_ref[...]))


def hidden_grads(x, cot, up_grads, hidden, dp_count, depth_count):
    tall, model = x[0].shape
    part = hidden[0].shape[1]
    block = model // dp_count
    cols = pl.BlockSpec((tall, block), lambda k, n: (0, n * (1 - k)))
    whole = pl.BlockSpec((tall, part), lambda k, n: (0, 0))
    return pl.pallas_call(
        hidden_grad_kernel,
        grid=(2, dp_count),
        in_specs=[cols, cols]
        + [
            pl.BlockSpec((dp_count, 1, cot.shape[2], block), lambda k, n: (0, 0, 0, n * k)),
            pl.BlockSpec((dp_count, 1, cot.shape[2], block), lambda k, n: (0, 1, 0, n * k)),
        ]
        + [whole] * 4,
        out_specs=pl.BlockSpec(
            (1, depth_count, block // depth_count, part), lambda k, n: (k * dp_count + n, 0, 0, 0)
        ),
        out_shape=jax.ShapeDtypeStruct(
            (2 * dp_count, depth_count, block // depth_count, part), bf16
        ),
        compiler_params=pltpu.CompilerParams(vmem_limit_bytes=48 << 20),
        cost_estimate=spent(
            flops=8 * tall * model * part, bytes_accessed=8 * model * part, transcendentals=0
        ),
        name="hidden_grads",
    )(*x, cot, cot, *up_grads, *hidden)


def mix_kernel(slots, mix_ref, hist_ref, out_ref):
    rows, width = hist_ref.shape[1], hist_ref.shape[2]
    part = 512 if width % 512 == 0 else width

    def step(at, carry):
        r0 = pl.multiple_of(at * 16, 16)
        weights = mix_ref[pl.ds(r0, 16), :]
        for c0 in range(0, width, part):
            sums = [None] * STREAMS
            for k in range(slots):
                state = hist_ref[k, pl.ds(r0, 16), c0 : c0 + part].astype(f32)
                for s in range(STREAMS):
                    term = weights[:, s * slots + k : s * slots + k + 1] * state
                    sums[s] = term if sums[s] is None else sums[s] + term
            for s in range(STREAMS):
                out_ref[s, pl.ds(r0, 16), c0 : c0 + part] = sums[s].astype(bf16)
        return carry

    lax.fori_loop(0, rows // 16, step, 0)


def mix_streams(slot_mix, history, micro_at, depth_count, rows_mb):
    slots, _, width = history.shape
    rows = min(128, rows_mb)
    per = rows_mb // rows

    def row_block(i):
        return ((i // per) * MB + micro_at) * per + i % per

    return pl.pallas_call(
        functools.partial(mix_kernel, slots),
        grid=(depth_count * per,),
        in_specs=[
            pl.BlockSpec((rows, slot_mix.shape[1]), lambda i: (row_block(i), 0)),
            pl.BlockSpec((slots, rows, width), lambda i: (0, row_block(i), 0)),
        ],
        out_specs=pl.BlockSpec((STREAMS, rows, width), lambda i: (0, i, 0)),
        out_shape=jax.ShapeDtypeStruct((STREAMS, depth_count * rows_mb, width), bf16),
        cost_estimate=spent(
            flops=2 * slots * STREAMS * depth_count * rows_mb * width,
            bytes_accessed=2 * (slots + STREAMS) * depth_count * rows_mb * width,
            transcendentals=0,
        ),
        name="mix_streams",
    )(slot_mix, history)


def unmix_kernel(slots, mix_ref, hist_ref, grad_ref, *rest):
    hist_grad_ref, slot_grad_ref = rest[-2:]
    rows, width = hist_ref.shape[1], hist_ref.shape[2]
    part = 512 if width % 512 == 0 else width

    def step(at, carry):
        r0 = pl.multiple_of(at * 16, 16)
        weights = mix_ref[pl.ds(r0, 16), :]
        totals = [None] * (STREAMS * slots)
        for c0 in range(0, width, part):
            grads = [
                grad_ref[s, pl.ds(r0, 16), c0 : c0 + part].astype(f32)
                for s in range(STREAMS)
            ]
            for k in range(slots):
                state = hist_ref[k, pl.ds(r0, 16), c0 : c0 + part].astype(f32)
                back = None
                for s in range(STREAMS):
                    at_sk = s * slots + k
                    term = weights[:, at_sk : at_sk + 1] * grads[s]
                    back = term if back is None else back + term
                    product = state * grads[s]
                    folded = product[:, 0:128]
                    for l0 in range(128, part, 128):
                        folded = folded + product[:, l0 : l0 + 128]
                    totals[at_sk] = folded if totals[at_sk] is None else totals[at_sk] + folded
                hist_grad_ref[k, pl.ds(r0, 16), c0 : c0 + part] = back.astype(bf16)
        lane = lax.broadcasted_iota(jnp.int32, (16, 128), 1)
        packed = jnp.zeros((16, 128), f32)
        for at_sk in range(STREAMS * slots):
            column = jnp.sum(totals[at_sk], axis=1, keepdims=True)
            packed = jnp.where(lane == at_sk, column, packed)
        slot_grad_ref[pl.ds(r0, 16), :] = packed
        return carry

    lax.fori_loop(0, rows // 16, step, 0)


def unmix_streams(slot_mix, history, grads, micro_at, depth_count, rows_mb, earlier):
    slots, tokens, width = history.shape
    rows = min(128, rows_mb)
    per = rows_mb // rows

    def row_block(i):
        return ((i // per) * MB + micro_at) * per + i % per

    in_specs = [
        pl.BlockSpec((rows, slot_mix.shape[1]), lambda i: (row_block(i), 0)),
        pl.BlockSpec((slots, rows, width), lambda i: (0, row_block(i), 0)),
        pl.BlockSpec((STREAMS, rows, width), lambda i: (0, i, 0)),
    ]
    operands = [slot_mix, history, grads]
    aliases = {}
    if earlier is not None:
        in_specs.append(pl.BlockSpec(memory_space=pl.ANY))
        operands.append(earlier)
        aliases = {3: 0}
    return pl.pallas_call(
        functools.partial(unmix_kernel, slots),
        grid=(depth_count * per,),
        in_specs=in_specs,
        out_specs=[
            pl.BlockSpec((slots, rows, width), lambda i: (0, row_block(i), 0)),
            pl.BlockSpec((rows, 128), lambda i: (i, 0)),
        ],
        out_shape=[
            jax.ShapeDtypeStruct((slots, tokens, width), bf16),
            jax.ShapeDtypeStruct((depth_count * rows_mb, 128), f32),
        ],
        input_output_aliases=aliases,
        cost_estimate=spent(
            flops=4 * slots * STREAMS * depth_count * rows_mb * width,
            bytes_accessed=2 * (2 * slots + STREAMS) * depth_count * rows_mb * width,
            transcendentals=0,
        ),
        name="unmix_streams",
    )(*operands)


def unmix_one(slot_mix, history, grads, micro_at, index, rows_mb, earlier):
    slots, tokens, width = history.shape
    rows = min(128, rows_mb)
    per = rows_mb // rows

    def row_block(i, m):
        return (m[0] * MB + micro_at) * per + i

    def kernel(at_ref, *refs):
        unmix_kernel(slots, *refs)

    return pl.pallas_call(
        kernel,
        grid_spec=pltpu.PrefetchScalarGridSpec(
            num_scalar_prefetch=1,
            grid=(per,),
            in_specs=[
                pl.BlockSpec((rows, slot_mix.shape[1]), lambda i, m: (row_block(i, m), 0)),
                pl.BlockSpec((slots, rows, width), lambda i, m: (0, row_block(i, m), 0)),
                pl.BlockSpec((STREAMS, rows, width), lambda i, m: (0, i, 0)),
                pl.BlockSpec(memory_space=pl.ANY),
            ],
            out_specs=[
                pl.BlockSpec((slots, rows, width), lambda i, m: (0, row_block(i, m), 0)),
                pl.BlockSpec((rows, 128), lambda i, m: (i, 0)),
            ],
        ),
        out_shape=[
            jax.ShapeDtypeStruct((slots, tokens, width), bf16),
            jax.ShapeDtypeStruct((rows_mb, 128), f32),
        ],
        input_output_aliases={4: 0},
        cost_estimate=spent(
            flops=4 * slots * STREAMS * rows_mb * width,
            bytes_accessed=2 * (2 * slots + STREAMS) * rows_mb * width,
            transcendentals=0,
        ),
        name="unmix_one",
    )(index.astype(jnp.int32)[None], slot_mix, history, grads, earlier)


def own_spans(model_ref, width):
    own_at = pl.multiple_of(model_ref[0] * width, width)
    other_at = pl.multiple_of((1 - model_ref[0]) * width, width)
    return pl.ds(own_at, width), pl.ds(other_at, width)


def ff_split_kernel(at_ref, up_ref, down_ref, out_ref):
    out_ref[0, 0] = up_ref[...]
    out_ref[0, 1] = down_ref[...].T


def ff_split(up_weight, down_weight, partners):
    own_rows, ff_width = up_weight.shape
    count = partners.shape[0]
    part = ff_width // count
    return pl.pallas_call(
        ff_split_kernel,
        grid_spec=pltpu.PrefetchScalarGridSpec(
            num_scalar_prefetch=1,
            grid=(count,),
            in_specs=[
                pl.BlockSpec((own_rows, part), lambda i, m: (0, m[i])),
                pl.BlockSpec((part, own_rows), lambda i, m: (m[i], 0)),
            ],
            out_specs=pl.BlockSpec((1, 2, own_rows, part), lambda i, m: (i, 0, 0, 0)),
        ),
        out_shape=jax.ShapeDtypeStruct((count, 2, own_rows, part), bf16),
        cost_estimate=spent(flops=0, bytes_accessed=8 * own_rows * ff_width, transcendentals=0),
        name="ff_split",
    )(partners, up_weight, down_weight)


def ff_join_kernel(at_ref, piece_ref, up_ref, down_ref):
    up_ref[...] = piece_ref[0, 0].astype(f32)
    down_ref[...] = piece_ref[0, 1].astype(f32).T


def ff_join(pieces, partners):
    count, _, own_rows, part = pieces.shape
    return pl.pallas_call(
        ff_join_kernel,
        grid_spec=pltpu.PrefetchScalarGridSpec(
            num_scalar_prefetch=1,
            grid=(count,),
            in_specs=[pl.BlockSpec((1, 2, own_rows, part), lambda i, m: (i, 0, 0, 0))],
            out_specs=[
                pl.BlockSpec((own_rows, part), lambda i, m: (0, m[i])),
                pl.BlockSpec((part, own_rows), lambda i, m: (m[i], 0)),
            ],
        ),
        out_shape=[
            jax.ShapeDtypeStruct((own_rows, count * part), f32),
            jax.ShapeDtypeStruct((count * part, own_rows), f32),
        ],
        cost_estimate=spent(
            flops=0, bytes_accessed=12 * own_rows * count * part, transcendentals=0
        ),
        name="ff_join",
    )(partners, pieces)


def total_kernel(depth_ref, part_ref, up_ref, down_ref, cur_ref, last_ref, low_ref, resid_ref):
    width = resid_ref.shape[1]
    current = cur_ref[...].astype(f32)
    for s in range(STREAMS):
        lanes = slice(s * width, (s + 1) * width)
        total = part_ref[s, 0].astype(f32)
        total = total + up_ref[s].astype(f32) + down_ref[s].astype(f32)
        total = total + last_ref[:, s : s + 1] * current
        if s == STREAMS - 1:
            resid_ref[...] = total
        low_ref[:, lanes] = total.astype(bf16)


def total_streams(sums, current_half, last, depth_at):
    _, _, tall, width = sums.terms.shape
    wide = STREAMS * width
    rows = min(64, tall)
    row = lambda i, d: (i, 0)
    return pl.pallas_call(
        total_kernel,
        grid_spec=pltpu.PrefetchScalarGridSpec(
            num_scalar_prefetch=1,
            grid=(tall // rows,),
            in_specs=[
                pl.BlockSpec((STREAMS, 1, rows, width), lambda i, d: (0, d[0], i, 0)),
                pl.BlockSpec((STREAMS, rows, width), lambda i, d: (0, i, 0)),
                pl.BlockSpec((STREAMS, rows, width), lambda i, d: (0, i, 0)),
                pl.BlockSpec((rows, width), row),
                pl.BlockSpec((rows, 128), row),
            ],
            out_specs=[pl.BlockSpec((rows, wide), row), pl.BlockSpec((rows, width), row)],
        ),
        out_shape=[
            jax.ShapeDtypeStruct((tall, wide), bf16),
            jax.ShapeDtypeStruct((tall, width), f32),
        ],
        cost_estimate=spent(flops=5 * tall * wide, bytes_accessed=9 * tall * wide, transcendentals=0),
        name="total_streams",
    )(depth_at, sums.terms, sums.up, sums.down, current_half, last)


def norm_kernel(model_ref, own_ref, other_ref, gain_ref, normed_ref, ff_ref, stat_ref):
    rows, width = ff_ref.shape
    model = 2 * width
    own_span, other_span = own_spans(model_ref, width)
    lane = lax.broadcasted_iota(jnp.int32, (rows, 128), 1)
    stats = jnp.zeros((rows, 128), f32)
    for s in range(STREAMS):
        lanes = slice(s * width, (s + 1) * width)
        own = own_ref[:, lanes].astype(f32)
        other = other_ref[:, lanes].astype(f32)
        average = (
            jnp.sum(own, axis=-1, keepdims=True) + jnp.sum(other, axis=-1, keepdims=True)
        ) / model
        own, other = own - average, other - average
        variance = (
            jnp.sum(own * own, axis=-1, keepdims=True)
            + jnp.sum(other * other, axis=-1, keepdims=True)
        ) / model
        inverse = lax.rsqrt(variance + NORM_EPSILON)
        stats = jnp.where(lane == 2 * s, average, stats)
        stats = jnp.where(lane == 2 * s + 1, inverse, stats)
        norm_own = (own * inverse * gain_ref[s : s + 1, own_span]).astype(bf16)
        if s == STREAMS - 1:
            ff_ref[...] = norm_own
        else:
            normed_ref[s, :, own_span] = norm_own
            norm_other = (other * inverse * gain_ref[s : s + 1, other_span]).astype(bf16)
            normed_ref[s, :, other_span] = norm_other
    stat_ref[...] = stats


def norm_streams(low, low_other, gains, which):
    tall, wide = low.shape
    width = wide // STREAMS
    rows = min(64, tall)
    row = lambda i, m: (i, 0)
    return pl.pallas_call(
        norm_kernel,
        grid_spec=pltpu.PrefetchScalarGridSpec(
            num_scalar_prefetch=1,
            grid=(tall // rows,),
            in_specs=[
                pl.BlockSpec((rows, wide), row),
                pl.BlockSpec((rows, wide), row),
                pl.BlockSpec(gains.shape, lambda i, m: (0, 0)),
            ],
            out_specs=[
                pl.BlockSpec((3, rows, 2 * width), lambda i, m: (0, i, 0)),
                pl.BlockSpec((rows, width), row),
                pl.BlockSpec((rows, 128), row),
            ],
        ),
        out_shape=[
            jax.ShapeDtypeStruct((3, tall, 2 * width), bf16),
            jax.ShapeDtypeStruct((tall, width), bf16),
            jax.ShapeDtypeStruct((tall, 128), f32),
        ],
        cost_estimate=spent(
            flops=20 * tall * wide, bytes_accessed=8 * tall * wide, transcendentals=0
        ),
        name="norm_streams",
    )(which, low, low_other, gains)


def turn(values, cosine, sine_up, sine_down, sign):
    up = pltpu.roll(values, HDIM - ROT // 2, 1)
    down = pltpu.roll(values, ROT // 2, 1)
    return values * cosine + sign * (up * sine_up + down * sine_down)


def project_kernel(
    x_ref, cot_ref, wq_ref, wk_ref, wv_ref, wo_ref, cos_ref, up_ref, down_ref, out_ref
):
    span = wq_ref.shape[-1]
    tables = cos_ref[...], up_ref[...], down_ref[...]
    for kind, w_ref in enumerate((wq_ref, wk_ref, wv_ref, wo_ref)):
        rows = cot_ref[...] if kind == 3 else x_ref[kind]
        product = dot_nn(rows, w_ref[...].reshape(-1, span))
        for begin in range(0, span, HDIM):
            head = product[:, begin : begin + HDIM]
            if kind < 2:
                head = turn(head, *tables, 1.0)
            out_ref[0, :, kind * span + begin : kind * span + begin + HDIM] = head.astype(bf16)


def project_heads(normed, cot, weights, tables, depth_count):
    _, rows, model = normed.shape
    groups, _, _, own_rows, heads_width = weights.shape
    span = heads_width // depth_count
    whole = lambda j: (0, 0)

    def matrix(kind):
        shape = (groups, depth_count, 1, own_rows, span)
        return pl.BlockSpec(shape, lambda j: (0, 0, kind, 0, j))

    return pl.pallas_call(
        project_kernel,
        grid=(depth_count,),
        in_specs=[
            pl.BlockSpec((3, rows, model), lambda j: (0, 0, 0)),
            pl.BlockSpec((rows, model), whole),
        ]
        + [matrix(kind) for kind in range(4)]
        + [pl.BlockSpec((rows, HDIM), whole)] * 3,
        out_specs=pl.BlockSpec((1, rows, 4 * span), lambda j: (j, 0, 0)),
        out_shape=jax.ShapeDtypeStruct((depth_count, rows, 4 * span), bf16),
        compiler_params=pltpu.CompilerParams(vmem_limit_bytes=40 << 20),
        cost_estimate=spent(
            flops=8 * rows * model * span * depth_count,
            bytes_accessed=8 * model * span * depth_count + 8 * rows * model,
            transcendentals=0,
        ),
        name="project_heads",
    )(normed, cot, *[weights] * 4, *tables)


def attend_kernel(
    block, q_ref, k_ref, v_ref, g_ref, doc_col_ref, doc_row_ref, cos_ref, up_ref, down_ref,
    out_ref, dk_sum, dv_sum,
):
    length = q_ref.shape[0]
    scale = HDIM**-0.5
    heads_each = out_ref.shape[1] // (4 * HDIM)

    def lanes(kind):
        return pl.ds(pl.multiple_of((kind * heads_each + pl.program_id(0)) * HDIM, HDIM), HDIM)

    for begin in range(0, length, block):
        end = begin + block
        rows = slice(begin, end)
        queries, grads = q_ref[rows, :], g_ref[rows, :]
        keys, values = k_ref[0:end, :], v_ref[0:end, :]
        scores = dot_nt(queries, keys) * scale
        place_q = begin + lax.broadcasted_iota(jnp.int32, scores.shape, 0)
        place_k = lax.broadcasted_iota(jnp.int32, scores.shape, 1)
        allowed = (doc_col_ref[rows, :] == doc_row_ref[:, 0:end]) & (place_q >= place_k)
        scores = jnp.where(allowed, scores, MASKED)
        highest = jnp.max(scores, axis=-1, keepdims=True)
        exponent = jnp.exp(scores - highest)
        totals = jnp.sum(exponent, axis=-1, keepdims=True)
        attention = exponent * (1.0 / totals)
        low = attention.astype(bf16)
        out_ref[rows, lanes(0)] = dot_nn(low, values).astype(bf16)
        grad_att = dot_nt(grads, values).astype(bf16).astype(f32)
        weighted = jnp.sum(attention * grad_att, axis=-1, keepdims=True)
        grad_scores = (attention * (grad_att - weighted)).astype(bf16)
        grad_q = dot_nn(grad_scores, keys) * scale
        out_ref[rows, lanes(1)] = turn(
            grad_q, cos_ref[rows, :], up_ref[rows, :], down_ref[rows, :], -1.0
        ).astype(bf16)
        part_k = dot_tn(grad_scores, queries)
        part_v = dot_tn(low, grads)
        if begin > 0:
            dk_sum[0:begin, :] += part_k[0:begin]
            dv_sum[0:begin, :] += part_v[0:begin]
        dk_sum[begin:end, :] = part_k[begin:end]
        dv_sum[begin:end, :] = part_v[begin:end]
    grad_k = dk_sum[...] * scale
    out_ref[:, lanes(2)] = turn(grad_k, cos_ref[...], up_ref[...], down_ref[...], -1.0).astype(bf16)
    out_ref[:, lanes(3)] = dv_sum[...].astype(bf16)


def attend(packed, documents, tables, heads_each):
    length = packed.shape[0]
    block = min(256, length)
    whole = lambda h: (0, 0)

    def kind(at):
        return pl.BlockSpec((length, HDIM), lambda h: (0, at * heads_each + h))

    return pl.pallas_call(
        functools.partial(attend_kernel, block),
        grid=(heads_each,),
        in_specs=[kind(0), kind(1), kind(2), kind(3)]
        + [pl.BlockSpec((length, 1), whole), pl.BlockSpec((1, length), whole)]
        + [pl.BlockSpec((length, HDIM), whole)] * 3,
        out_specs=pl.BlockSpec((length, 4 * heads_each * HDIM), whole),
        out_shape=jax.ShapeDtypeStruct((length, 4 * heads_each * HDIM), bf16),
        scratch_shapes=[pltpu.VMEM((length, HDIM), f32)] * 2,
        compiler_params=pltpu.CompilerParams(vmem_limit_bytes=48 << 20),
        cost_estimate=spent(
            flops=9 * heads_each * length * length * HDIM,
            bytes_accessed=16 * length * heads_each * HDIM + 12 * length * HDIM,
            transcendentals=heads_each * length * length,
        ),
        name="attend",
    )(packed, packed, packed, packed, documents[:, None], documents[None, :], *tables)


def gelu_parts(values):
    cdf = 0.5 * (1.0 + lax.erf(values * (0.5**0.5)))
    density = jnp.exp(-0.5 * values * values) * (1.0 / math.sqrt(2.0 * math.pi))
    return values * cdf, cdf + values * density


def ff_kernel(
    model_ref, x_ref, cot_ref, up_ref, down_ref,
    hidden_ref, grad_ref, own_ref, other_ref,
):
    part = up_ref.shape[-1]
    half = up_ref.shape[1] // 2

    def rows_of(ref, which):
        return ref[0, pl.ds(which * half, half)].reshape(-1, part)

    own, other = model_ref[0], 1 - model_ref[0]
    up_pre = dot_nn(x_ref[...], up_ref[...].reshape(-1, part))
    hidden, slope = gelu_parts(up_pre)
    hidden = hidden.astype(bf16)
    grad_up = (dot_nn(cot_ref[0, 0], down_ref[...].reshape(-1, part)) * slope).astype(bf16)
    hidden_ref[...] = hidden
    grad_ref[...] = grad_up
    other_ref[0] = dot_nt(grad_up, rows_of(up_ref, other)).astype(bf16)
    own_ref[0] = dot_nt(grad_up, rows_of(up_ref, own))
    other_ref[1] = dot_nt(hidden, rows_of(down_ref, other)).astype(bf16)
    own_ref[1] = dot_nt(hidden, rows_of(down_ref, own))


def feed_forward(x, cot, micro_at, weights, which):
    tall, model = x.shape
    part = weights.shape[-1]
    width = model // 2
    rows = cot.shape[2]
    row = lambda i, m: (i, 0)

    def resident(kind):
        return pl.BlockSpec(
            (1,) + weights.shape[1:],
            lambda i, m: (kind, 0, 0, 0, 0),
            pipeline_mode=pl.Buffered(1),
        )

    return pl.pallas_call(
        ff_kernel,
        grid_spec=pltpu.PrefetchScalarGridSpec(
            num_scalar_prefetch=1,
            grid=(tall // rows,),
            in_specs=[
                pl.BlockSpec((rows, model), row),
                pl.BlockSpec((1, 1, rows, model), lambda i, m: (i, micro_at, 0, 0)),
                resident(0),
                resident(1),
            ],
            out_specs=[pl.BlockSpec((rows, part), row)] * 2
            + [pl.BlockSpec((2, rows, width), lambda i, m: (0, i, 0))] * 2,
        ),
        out_shape=[jax.ShapeDtypeStruct((tall, part), bf16)] * 2
        + [
            jax.ShapeDtypeStruct((2, tall, width), f32),
            jax.ShapeDtypeStruct((2, tall, width), bf16),
        ],
        compiler_params=pltpu.CompilerParams(vmem_limit_bytes=48 << 20),
        cost_estimate=spent(
            flops=8 * tall * model * part,
            bytes_accessed=4 * model * part + 16 * tall * model,
            transcendentals=2 * tall * part,
        ),
        name="feed_forward",
    )(which, x, cot, weights, weights)


def back_kernel(half_ref, ans_ref, wo_ref, wq_ref, wk_ref, wv_ref, out_ref, *flat):
    count, _, wide = ans_ref.shape
    span = wide // 4
    for kind, w_ref in enumerate((wo_ref, wq_ref, wk_ref, wv_ref)):
        total = None
        for j in range(count):
            term = dot_nt(
                ans_ref[j, :, kind * span : (kind + 1) * span],
                w_ref[:, :, :, :, j * span : (j + 1) * span].reshape(-1, span),
            )
            total = term if total is None else total + term
        out_ref[kind] = total.astype(out_ref.dtype)
    if flat:

        @pl.when(pl.program_id(0) == 0)
        def _():
            for kind in range(4):
                for j in range(count):
                    flat[0][kind, :, j * span : (j + 1) * span] = ans_ref[
                        j, :, kind * span : (kind + 1) * span
                    ]


def back_project(answer, weights, half, dtype, flat):
    count, rows, wide = answer.shape
    groups, _, _, own_rows, heads_width = weights.shape
    part = count * own_rows
    steps = groups // 2
    width = part * steps

    def matrix(kind):
        shape = (1, count, 1, own_rows, heads_width)
        return pl.BlockSpec(shape, lambda i, m: (m[0] * steps + i, 0, kind, 0, 0))

    out_specs = [pl.BlockSpec((4, rows, part), lambda i, m: (0, 0, i))]
    out_shape = [jax.ShapeDtypeStruct((4, rows, width), dtype)]
    if flat:
        out_specs.append(pl.BlockSpec((4, rows, heads_width), lambda i, m: (0, 0, 0)))
        out_shape.append(jax.ShapeDtypeStruct((4, rows, heads_width), bf16))
    return pl.pallas_call(
        back_kernel,
        grid_spec=pltpu.PrefetchScalarGridSpec(
            num_scalar_prefetch=1,
            grid=(steps,),
            in_specs=[pl.BlockSpec((count, rows, wide), lambda i, m: (0, 0, 0))]
            + [matrix(kind) for kind in (3, 0, 1, 2)],
            out_specs=out_specs,
        ),
        out_shape=out_shape,
        compiler_params=pltpu.CompilerParams(vmem_limit_bytes=40 << 20),
        cost_estimate=spent(
            flops=8 * rows * heads_width * width,
            bytes_accessed=8 * heads_width * width + 20 * rows * width,
            transcendentals=0,
        ),
        name="back_project",
    )(half, answer, *[weights] * 4)


def slope_kernel(
    model_ref, own_ref, got_ref, ff_ref, low_ref, stat_ref, gain_ref, scaled_ref, sum_ref, gain_out_ref
):
    _, rows, width = ff_ref.shape
    own_span, _ = own_spans(model_ref, width)
    lane = lax.broadcasted_iota(jnp.int32, (rows, 128), 1)
    packed = jnp.zeros((rows, 128), f32)
    totals = []
    for s in range(STREAMS):
        lanes = slice(s * width, (s + 1) * width)
        if s < 3:
            grad = own_ref[s + 1] + got_ref[s + 1].astype(f32)
        else:
            grad = ff_ref[0]
        average, inverse = stat_ref[:, 2 * s : 2 * s + 1], stat_ref[:, 2 * s + 1 : 2 * s + 2]
        hat = (low_ref[:, lanes].astype(f32) - average) * inverse
        totals.append(jnp.sum(grad * hat, axis=0, keepdims=True))
        scaled = grad * gain_ref[s : s + 1, own_span]
        scaled_ref[:, lanes] = scaled
        packed = jnp.where(lane == 2 * s, jnp.sum(scaled, axis=-1, keepdims=True), packed)
        packed = jnp.where(
            lane == 2 * s + 1, jnp.sum(scaled * hat, axis=-1, keepdims=True), packed
        )
    sum_ref[...] = packed
    totals = jnp.concatenate(totals, axis=0)

    @pl.when(pl.program_id(0) == 0)
    def _():
        gain_out_ref[...] = totals

    @pl.when(pl.program_id(0) > 0)
    def _():
        gain_out_ref[...] += totals


def norm_slopes(own, got, ff_grad, low, stats, gains, which):
    tall, wide = low.shape
    width = wide // STREAMS
    rows = min(64, tall)
    row = lambda i, m: (i, 0)
    cube = pl.BlockSpec((4, rows, width), lambda i, m: (0, i, 0))
    return pl.pallas_call(
        slope_kernel,
        grid_spec=pltpu.PrefetchScalarGridSpec(
            num_scalar_prefetch=1,
            grid=(tall // rows,),
            in_specs=[
                cube,
                cube,
                pl.BlockSpec((1, rows, width), lambda i, m: (0, i, 0)),
                pl.BlockSpec((rows, wide), row),
                pl.BlockSpec((rows, 128), row),
                pl.BlockSpec(gains.shape, lambda i, m: (0, 0)),
            ],
            out_specs=[
                pl.BlockSpec((rows, wide), row),
                pl.BlockSpec((rows, 128), row),
                pl.BlockSpec((STREAMS, width), lambda i, m: (0, 0)),
            ],
        ),
        out_shape=[
            jax.ShapeDtypeStruct((tall, wide), f32),
            jax.ShapeDtypeStruct((tall, 128), f32),
            jax.ShapeDtypeStruct((STREAMS, width), f32),
        ],
        cost_estimate=spent(
            flops=12 * tall * wide, bytes_accessed=12 * tall * wide, transcendentals=0
        ),
        name="norm_slopes",
    )(which, own, got, ff_grad, low, stats, gains)


def grads_kernel(
    scaled_ref, mine_ref, theirs_ref, low_ref, stat_ref, cot_ref, cur_ref, last_ref,
    grad_ref, mix_ref, dot_ref,
):
    rows, width = cot_ref.shape
    lane = lax.broadcasted_iota(jnp.int32, (rows, 128), 1)
    means = (mine_ref[...] + theirs_ref[...]) / (2 * width)
    current = cur_ref[...].astype(f32)
    packed = jnp.zeros((rows, 128), f32)
    mixed = None
    for s in range(STREAMS):
        lanes = slice(s * width, (s + 1) * width)
        average, inverse = stat_ref[:, 2 * s : 2 * s + 1], stat_ref[:, 2 * s + 1 : 2 * s + 2]
        hat = (low_ref[:, lanes].astype(f32) - average) * inverse
        grad = inverse * (
            scaled_ref[:, lanes]
            - means[:, 2 * s : 2 * s + 1]
            - hat * means[:, 2 * s + 1 : 2 * s + 2]
        )
        if s == STREAMS - 1:
            grad = grad + cot_ref[...].astype(f32)
        grad = grad.astype(bf16)
        grad_ref[s] = grad
        grad = grad.astype(f32)
        term = last_ref[:, s : s + 1] * grad
        mixed = term if mixed is None else mixed + term
        packed = jnp.where(lane == s, jnp.sum(grad * current, axis=-1, keepdims=True), packed)
    mix_ref[...] = mixed
    dot_ref[...] = packed


def stream_grads(scaled, mine, theirs, low, stats, cot, current_half, last):
    tall, wide = low.shape
    width = wide // STREAMS
    rows = min(64, tall)
    row = lambda i: (i, 0)
    return pl.pallas_call(
        grads_kernel,
        grid=(tall // rows,),
        in_specs=[
            pl.BlockSpec((rows, wide), row),
            pl.BlockSpec((rows, 128), row),
            pl.BlockSpec((rows, 128), row),
            pl.BlockSpec((rows, wide), row),
            pl.BlockSpec((rows, 128), row),
            pl.BlockSpec((rows, width), row),
            pl.BlockSpec((rows, width), row),
            pl.BlockSpec((rows, 128), row),
        ],
        out_specs=[
            pl.BlockSpec((STREAMS, rows, width), lambda i: (0, i, 0)),
            pl.BlockSpec((rows, width), row),
            pl.BlockSpec((rows, 128), row),
        ],
        out_shape=[
            jax.ShapeDtypeStruct((STREAMS, tall, width), bf16),
            jax.ShapeDtypeStruct((tall, width), f32),
            jax.ShapeDtypeStruct((tall, 128), f32),
        ],
        cost_estimate=spent(
            flops=12 * tall * wide, bytes_accessed=10 * tall * wide, transcendentals=0
        ),
        name="stream_grads",
    )(scaled, mine, theirs, low, stats, cot, current_half, last)


def turning_tables(places):
    half = ROT // 2
    inverse = jnp.exp(jnp.arange(half, dtype=f32) * (-2.0 * math.log(10000.0) / ROT))
    angles = places.astype(f32)[:, None] * inverse[None, :]
    cosine, sine = jnp.cos(angles), jnp.sin(angles)
    rows = places.shape[0]
    rest = jnp.zeros((rows, HDIM - ROT), f32)
    blank = jnp.zeros((rows, half), f32)
    return (
        jnp.concatenate([cosine, cosine, rest + 1.0], axis=1),
        jnp.concatenate([-sine, blank, rest], axis=1),
        jnp.concatenate([blank, sine, rest], axis=1),
    )


def local(
    history,
    slot_layer,
    current,
    positions,
    doc_ids,
    cotangent,
    norm_gains,
    generator_in,
    generator_out,
    query_weight,
    key_weight,
    value_weight,
    out_weight,
    up_weight,
    down_weight,
):
    dp_count = lax.axis_size("dp")
    depth_count = lax.axis_size("depth")
    dp_at = lax.axis_index("dp")
    model_at = lax.axis_index("mp")
    dp_bits = list(range(bit_count(dp_count)))
    slots, tokens_held, width = history.shape
    model = current.shape[1]
    rows_mb = current.shape[0] // MB
    length = depth_count * rows_mb
    heads_width = query_weight.shape[1]
    heads_each = heads_width // HDIM // depth_count
    own_rows = query_weight.shape[0]
    ff_width = up_weight.shape[1]
    ff_part = ff_width // dp_count
    both = ("dp", "depth")

    def half_of(values, axis, which):
        return lax.dynamic_slice_in_dim(values, which * width, width, axis)

    partners = jnp.stack([dp_at ^ m for m in range(dp_count)]).astype(jnp.int32)
    ff_local = ff_split(up_weight, down_weight, partners)
    ff_rows = [ff_local[0]] + [swap_mask(ff_local[m], "dp", m) for m in range(1, dp_count)]
    ff_rows = place_many(partners, ff_rows).reshape(2 * dp_count, own_rows, ff_part)

    small_cols = jnp.concatenate(
        [generator_in, norm_gains.T, jnp.zeros((own_rows, 128 - GEN - 5), bf16)], axis=1
    )
    small_all = gather_small(small_cols, both).reshape(model, 128)
    gen_first = small_all[:, :GEN]
    gen_first, ff_rows = fence(gen_first, ff_rows)
    gain_float = small_all[:, GEN : GEN + 5].astype(f32).T
    second_rows = generator_out.shape[0]
    second_pad = -second_rows % 128
    second_all = gather_small(jnp.pad(generator_out, (0, second_pad))[None], both)
    gen_second = second_all.reshape(-1, second_rows + second_pad)[:, :second_rows]
    second_low = gen_second.reshape(GEN, STREAMS * MIX)

    stacked = jnp.concatenate([query_weight, key_weight, value_weight, out_weight.T], axis=0)
    over_depth = lax.all_gather(stacked, "depth", axis=0, tiled=True)
    current_f = current.astype(f32)
    current_half = half_of(current, 1, model_at)
    mean_square = jnp.mean(current_f * current_f, axis=-1, keepdims=True)
    inverse_rms = lax.rsqrt(mean_square + RMS_EPSILON)
    unit = current_f * inverse_rms
    gen_normed = (unit * gain_float[4]).astype(bf16)
    gen_pre = dot_nn(gen_normed, gen_first)
    gen_hidden = gelu_exact(gen_pre).astype(bf16)
    column = jnp.arange(STREAMS * MIX)
    last_col = (column % MIX == MIX - 1).astype(f32)
    mixing = (dot_nn(gen_hidden, second_low) + last_col).astype(bf16)
    pick_last = (column[:, None] == (jnp.arange(128) * MIX + MIX - 1)[None, :]).astype(bf16)
    last = dot_nn(mixing, pick_last)

    layer_of = jnp.tile(slot_layer, STREAMS)
    stream_of = jnp.repeat(jnp.arange(STREAMS), slots)
    from_col = jnp.where(layer_of < MIX, stream_of * MIX + layer_of, -1)
    pick = (column[:, None] == from_col[None, :]).astype(f32)
    mix_all = gather_small(mixing, ("depth",)).reshape(depth_count * MB * rows_mb, STREAMS * MIX)
    slot_mix = dot_nn(mix_all, pick.astype(bf16))
    places_all = gather_small(positions, ("depth",))

    def over_depth_swap(values):
        return lax.all_to_all(values, "depth", 0, 0, tiled=True)

    def mix_part(micro_at, slot_mix):
        partial = mix_streams(slot_mix, history, micro_at, depth_count, rows_mb)
        return partial.reshape(STREAMS, depth_count, rows_mb, width)

    slot_mix, ff_rows, cotangent, places_all = fence(slot_mix, ff_rows, cotangent, places_all)
    partial = mix_part(0, slot_mix)
    partial_next = mix_part(1, slot_mix)

    weights_line = LineGather(ff_rows)
    weights_line.step()
    cot_pieces = lax.all_gather(cotangent, "dp", axis=0, tiled=True)
    over_depth, partial, partial_next = weights_line.hold(over_depth, partial, partial_next)
    pieces = [over_depth]
    weights = place_block(None, pieces[0][None], place_index(0), dp_count)
    hops_left = [(p, at) for at in range(len(dp_bits)) for p in range(1 << at)]
    placed = 1
    cots = None
    sums, sums_next = LineScatter(partial), LineScatter(partial_next)
    own_tables = turning_tables(positions)
    tables = [
        turning_tables(places_all[:, m * rows_mb : (m + 1) * rows_mb].reshape(length))
        for m in range(MB)
    ]
    for hop in range(1, depth_count):
        sums.step_with(weights_line)
        last_hop = hop == depth_count - 1
        for place in range(placed, len(pieces)):
            weights = place_block(weights, pieces[place][None], place_index(place), dp_count)
        placed = len(pieces)
        while hops_left:
            place, at = hops_left.pop(0)
            pieces.append(core_hop(pieces[place], at))
            if len(hops_left) <= depth_count - 1 - hop:
                break
        if last_hop:
            cot_full = join_halves(cotangent, other_core(cotangent), model_at)
            ff_weights = weights_line.placed()
            cots = cot_full, cotangent, ff_weights
        (state,) = weights_line.hold(
            (sums.up, sums.down, pieces, weights, cots, own_tables, tables, cot_pieces)
        )
        sums.up, sums.down, pieces, weights, cots, own_tables, tables, cot_pieces = state
    cot_full, cotangent, ff_weights = cots
    for place in range(placed, len(pieces)):
        weights = place_block(weights, pieces[place][None], place_index(place), dp_count)
    weights = weights.reshape(dp_count, depth_count, 4, own_rows, heads_width)
    ff_weights = ff_weights.reshape(2, dp_count, depth_count, own_rows, ff_part)

    document_view = doc_ids.reshape(depth_count, MB, rows_mb)
    which = model_at.astype(jnp.int32)[None]
    depth_at = lax.axis_index("depth").astype(jnp.int32)[None]
    gains = gain_float

    def enter(micro_at, sums):
        span = slice(micro_at * rows_mb, (micro_at + 1) * rows_mb)
        low, resid = total_streams(sums, current_half[span], last[span], depth_at)
        normed, ff_normed, stats = norm_streams(low, other_core(low), gains, which)
        packed = project_heads(
            normed,
            cot_full[span],
            weights,
            [t[span] for t in own_tables],
            depth_count,
        )
        return dict(
            low=low, resid=resid, normed=normed, ff_normed=ff_normed, stats=stats, packed=packed
        )

    def attention(micro_at, by_head):
        documents = document_view[:, micro_at].reshape(length)
        by_head = by_head.reshape(length, 4 * heads_each * HDIM)
        answer = attend(by_head, documents, tables[micro_at], heads_each)
        return answer.reshape(depth_count, rows_mb, 4 * heads_each * HDIM)

    place_list = jnp.stack([place_index(p) for p in range(dp_count)]).astype(jnp.int32)

    def group_rows(ff_normed):
        return lax.all_gather(ff_normed, "dp", axis=0, tiled=True)

    def group_joined(mine):
        return join_halves(mine, other_core(mine), model_at)

    def hidden_units(micro_at, group_normed):
        hidden, grad_up, own, other = feed_forward(
            group_normed, cot_group, micro_at, ff_weights, which
        )
        return dict(group_normed=group_normed, hidden=hidden, grad_up=grad_up), (own, other)

    def group_back_rest(near):
        for at in reversed(range(len(dp_bits) - 1)):
            half = 1 << at
            near = near[:half] + core_hop(near[half:].astype(bf16), at).astype(f32)
        return near[0]

    def group_back(own, other):
        near, far = group_split(own, other, place_list)
        return group_back_rest(near + core_hop(far, len(dp_bits) - 1).astype(f32))

    def back(kept, answer):
        (theirs,) = back_project(answer, weights, 1 - which, bf16, False)
        got = other_core(theirs)
        own, flat = back_project(answer, weights, which, f32, True)
        return own, got, flat

    def leave(micro_at, kept, own, got, ff_sum):
        span = slice(micro_at * rows_mb, (micro_at + 1) * rows_mb)
        rows = (kept["resid"] + own[0] + got[0].astype(f32) + ff_sum[1]).astype(bf16)
        low, stats = kept["low"], kept["stats"]
        scaled, sums, gain_part = norm_slopes(own, got, ff_sum, low, stats, gains, which)
        grad_low, current_mix, last_dot = stream_grads(
            scaled, sums, other_core(sums), low, stats, cotangent[span], current_half[span], last[span]
        )
        kept.update(layer_rows=rows, gain=gain_part, current_mix=current_mix, last_dot=last_dot)
        return grad_low

    ((sums.up, sums.down),) = sums_next.step((sums.up, sums.down))
    first = enter(0, sums)
    mine = group_rows(first["ff_normed"])
    packed, mine, cot_pieces = sums_next.hold(first["packed"], mine, cot_pieces)
    while sums_next.at < depth_count - 3:
        sums_next.step()
        sums_next.hold()
    packed, mine, cot_pieces = sums_next.step(packed, mine, cot_pieces)
    by_head = over_depth_swap(packed)
    cot_group = join_halves(cot_pieces, other_core(cot_pieces), model_at)
    cot_group = cot_group.reshape(dp_count, MB, rows_mb, model)
    kept, ff_parts = hidden_units(0, group_joined(mine))
    first.update(kept)
    by_head, ff_parts, cot_group = sums_next.hold(by_head, ff_parts, cot_group)
    by_head, ff_parts = sums_next.step(by_head, ff_parts)
    answer = attention(0, by_head)
    answer, ff_parts = sums_next.hold(answer, ff_parts)

    answer = over_depth_swap(answer)
    second = enter(1, sums_next)
    near, far = group_split(ff_parts[0], other_core(ff_parts[1]), place_list)
    near = near + core_hop(far, len(dp_bits) - 1).astype(f32)
    answer, packed, ff_normed, near = fence(
        answer, second["packed"], second["ff_normed"], near
    )
    by_head = over_depth_swap(packed)
    mine = group_rows(ff_normed)
    own, got, first["flat"] = back(first, answer)
    grad_low = leave(0, first, own, got, group_back_rest(near))
    by_head, grad_low, mine, first["layer_rows"] = fence(
        by_head, grad_low, mine, first["layer_rows"]
    )
    saved = [first, second]

    def each(name):
        return [s[name] for s in saved]

    def rows_of(name):
        return jnp.concatenate(each(name), axis=0)

    def place_grads(place, dtype):
        return attention_grads(
            each("normed"),
            cot_full,
            each("flat"),
            place_list[place : place + 1],
            depth_count,
            dp_count,
            dtype,
        )

    half = dp_count // 2
    hops_left = [
        (p, at) for at in reversed(range(len(dp_bits))) for p in range(1 << at, 2 << at)
    ]
    pieces = {}

    def sums_hop():
        place, at = hops_left.pop(0)
        arrived = core_hop(pieces.pop(place).astype(bf16), at)
        target = place - (1 << at)
        pieces[target] = pieces[target].astype(f32) + arrived.astype(f32)

    grad_line = LineGather(grad_low)
    grad_line.step()
    answer = attention(1, by_head)
    kept, ff_parts = hidden_units(1, group_joined(mine))
    second.update(kept)
    answer, ff_parts = grad_line.hold(answer, ff_parts)
    answer = over_depth_swap(answer)
    near, far = group_split(ff_parts[0], other_core(ff_parts[1]), place_list)
    ff_products = hidden_grads(
        each("group_normed"), cot_group, each("grad_up"), each("hidden"), dp_count, depth_count
    )
    near = near + core_hop(far, len(dp_bits) - 1).astype(f32)
    answer, near, ff_products = fence(answer, near, ff_products)

    ff_sums = LineScatter(ff_products)
    (answer,) = ff_sums.step_with(grad_line, answer)
    own, got, flat = back(second, answer)
    ff_sum = group_back_rest(near)
    second["flat"] = flat
    (state,) = grad_line.hold((ff_sums.up, ff_sums.down, own, got, flat, ff_sum))
    ff_sums.up, ff_sums.down, own, got, second["flat"], ff_sum = state
    while len(grad_line.up) < depth_count - 1:
        ff_sums.step_with(grad_line)
        (state,) = grad_line.hold((ff_sums.up, ff_sums.down))
        ff_sums.up, ff_sums.down = state
    (ff_sum,) = ff_sums.step_with(grad_line, ff_sum)
    grad_low = leave(1, second, own, got, ff_sum)
    pieces = {p: place_grads(p, bf16) for p in range(dp_count)}
    sums_hop()
    (state,) = grad_line.hold((ff_sums.up, ff_sums.down, grad_low, pieces))
    ff_sums.up, ff_sums.down, grad_low, pieces = state

    last_line = LineGather(grad_low)
    last_line.step()
    if hops_left:
        sums_hop()
    grad_first = grad_line.placed().reshape(STREAMS, length, width)
    history_grad, slot_part = unmix_streams(
        slot_mix, history, grad_first, 0, depth_count, rows_mb, None
    )
    slot_parts = [slot_part.reshape(depth_count, 1, rows_mb, 128)]
    pieces, history_grad, second["layer_rows"] = last_line.hold(
        pieces, history_grad, second["layer_rows"]
    )
    (pieces,) = ff_sums.step(pieces)
    while hops_left:
        sums_hop()
    (pieces,) = ff_sums.hold(pieces)
    out_sums = LineScatter(pieces[0].reshape(1, depth_count, 4 * own_rows, heads_width))
    for hop in range(2, depth_count):
        last_line.step()
        ((ff_sums.up, ff_sums.down),) = out_sums.step((ff_sums.up, ff_sums.down))
        if hop == depth_count - 1:
            ff_sums.up = ff_sums.down = end_sums(ff_sums, bf16)
            early = last_line.placed_early()
            history_grad, slot_part = unmix_streams(
                slot_mix,
                history,
                early.reshape(STREAMS, length, width),
                1,
                depth_count,
                rows_mb,
                history_grad,
            )
        (state,) = last_line.hold(
            (out_sums.up, out_sums.down, ff_sums.up, ff_sums.down, history_grad, slot_part)
        )
        out_sums.up, out_sums.down, ff_sums.up, ff_sums.down, history_grad, slot_part = state
    early, ff_grads = out_sums.step(early, ff_sums.up)
    ff_grads = ff_grads.reshape(2, dp_count, own_rows, ff_part)
    ff_pieces = [
        lax.dynamic_index_in_dim(ff_grads, partners[m], 1, keepdims=False) for m in range(dp_count)
    ]
    ff_pieces = ff_pieces[:1] + [swap_mask(ff_pieces[m], "dp", m) for m in range(1, dp_count)]
    far_grads, far_index = last_line.farthest(early)
    history_grad, far_part = unmix_one(
        slot_mix, history, far_grads, 1, far_index, rows_mb, history_grad
    )
    slot_part = slot_part.reshape(depth_count, rows_mb, 128)
    slot_part = lax.dynamic_update_index_in_dim(slot_part, far_part, far_index, 0)
    slot_parts.append(slot_part[:, None])

    slot_grads = jnp.concatenate(slot_parts, axis=1).reshape(-1, 128)[:, : STREAMS * slots]
    mix_grads = dot_exact(slot_grads, pick.T).reshape(depth_count, MB * rows_mb, STREAMS * MIX)
    mix_grads, ff_pieces = out_sums.hold(mix_grads, ff_pieces)
    grad_mixing = scatter_small(mix_grads, ("depth",))
    up_grad, down_grad = ff_join(jnp.stack(ff_pieces), partners)
    last_dots = rows_of("last_dot")
    grad_mixing = grad_mixing + dot_exact(last_dots, pick_last.astype(f32).T)
    grad_mixing = grad_mixing + other_core(grad_mixing)

    second_float = second_low.astype(f32)
    grad_second = dot_exact(gen_hidden.astype(f32).T, grad_mixing)
    grad_pre = dot_exact(grad_mixing, second_float.T) * gelu_slope(gen_pre)
    grad_first = dot_exact(gen_normed.astype(f32).T, grad_pre)
    grad_gen_normed = dot_exact(grad_pre, gen_first.astype(f32).T)
    gain_gen = jnp.sum(grad_gen_normed * unit, axis=0)
    scattered = end_sums(out_sums, f32).reshape(4, own_rows, heads_width)
    grad_unit = grad_gen_normed * gain_float[4]
    shared = jnp.mean(grad_unit * unit, axis=-1, keepdims=True)
    current_gen = half_of(inverse_rms * (grad_unit - unit * shared), 1, model_at)
    current_grad = rows_of("current_mix") + current_gen

    gain_own = sum(s["gain"] for s in saved)
    gain_other = other_core(gain_own)
    gain_all = jnp.where(
        model_at == 0,
        jnp.concatenate([gain_own, gain_other], axis=1),
        jnp.concatenate([gain_other, gain_own], axis=1),
    )
    gain_all = jnp.concatenate([gain_all, gain_gen[None]], axis=0)
    small_grads = jnp.concatenate(
        [grad_first, gain_all.T, jnp.zeros((model, 128 - GEN - 5), f32)], axis=1
    )
    small_grads = scatter_small(small_grads.reshape(-1, own_rows, 128), both)
    second_grads = jnp.pad(grad_second.reshape(-1, second_rows), ((0, 0), (0, second_pad)))
    second_grads = scatter_small(second_grads[:, None], both)

    return (
        rows_of("layer_rows"),
        history_grad,
        current_grad,
        small_grads[:, GEN : GEN + 5].T,
        small_grads[:, :GEN],
        second_grads[0, :second_rows],
        scattered[0],
        scattered[1],
        scattered[2],
        scattered[3].T,
        up_grad,
        down_grad,
    )


def solution(mesh):
    return jax.shard_map(
        local,
        mesh=mesh,
        in_specs=(
            P("depth", "dp", "mp"),
            P("depth"),
            P(("dp", "depth"), None),
            P(("dp", "depth")),
            P("dp"),
            P(("dp", "depth"), "mp"),
            P(None, ("dp", "depth")),
            P(("dp", "depth"), None),
            P(("dp", "depth")),
            P(("dp", "depth"), "mp"),
            P(("dp", "depth"), "mp"),
            P(("dp", "depth"), "mp"),
            P("mp", ("dp", "depth")),
            P(("dp", "depth"), "mp"),
            P("mp", ("dp", "depth")),
        ),
        out_specs=(
            P(("dp", "depth"), "mp"),
            P("depth", "dp", "mp"),
            P(("dp", "depth"), "mp"),
            P(None, ("dp", "depth")),
            P(("dp", "depth"), None),
            P(("dp", "depth")),
            P(("dp", "depth"), "mp"),
            P(("dp", "depth"), "mp"),
            P(("dp", "depth"), "mp"),
            P("mp", ("dp", "depth")),
            P(("dp", "depth"), "mp"),
            P("mp", ("dp", "depth")),
        ),
        check_vma=False,
    )
```

```python
import functools
import math

import jax
import jax.numpy as jnp
from jax import lax
from jax.experimental import pallas as pl
from jax.experimental.pallas import tpu as pltpu
from jax.sharding import PartitionSpec as P

HDIM = 128
ROT = 32
GEN = 72
MB = 2
MIX = 18
STREAMS = 4
COST = 20

PRECISE = lax.Precision.HIGHEST
NORM_EPSILON = 1e-05
RMS_EPSILON = 1e-06
MASKED = -1e30

bf16 = jnp.bfloat16
f32 = jnp.float32


def dot_nn(a, b):
    return lax.dot_general(a, b, (((1,), (0,)), ((), ())), preferred_element_type=f32)


def dot_nt(a, b):
    return lax.dot_general(a, b, (((1,), (1,)), ((), ())), preferred_element_type=f32)


def dot_tn(a, b):
    return lax.dot_general(a, b, (((0,), (0,)), ((), ())), preferred_element_type=f32)


def dot_exact(a, b):
    return jnp.dot(a, b, precision=PRECISE, preferred_element_type=f32)


def gelu_exact(values):
    return jax.nn.gelu(values, approximate=False)


def gelu_slope(values):
    result, pullback = jax.vjp(gelu_exact, values)
    return pullback(jnp.ones_like(result))[0]


def bit_count(size):
    count = size.bit_length() - 1
    assert 1 << count == size
    return count


def swap_mask(values, axis, mask):
    size = lax.axis_size(axis)
    return lax.ppermute(values, axis, [(i, i ^ mask) for i in range(size)])


def gather_masked(values, axis, order):
    pieces = {0: values}
    for bit in order:
        arrived = {m | (1 << bit): swap_mask(v, axis, 1 << bit) for m, v in pieces.items()}
        pieces.update(arrived)
    return [pieces[m] for m in range(len(pieces))]


def scatter_masked(pieces, axis, order, link=bf16):
    pieces = dict(enumerate(pieces))
    for bit in order:
        flag = 1 << bit
        for m in [m for m in pieces if m & flag]:
            arrived = swap_mask(pieces.pop(m).astype(link), axis, flag)
            pieces[m ^ flag] = pieces[m ^ flag].astype(f32) + arrived.astype(f32)
    return pieces[0]


def core_orders():
    bits = list(range(bit_count(lax.axis_size("dp"))))
    return bits, bits[1:] + bits[:1]


def place_mask(place):
    masks = []
    for order in core_orders():
        masks.append(sum(1 << bit for at, bit in enumerate(order) if (place >> at) & 1))
    return jnp.where(lax.axis_index("mp") % 2 == 0, masks[0], masks[1])


def place_index(place):
    return lax.axis_index("dp") ^ place_mask(place)


def core_hop(values, at):
    orders, cores = core_orders(), lax.axis_size("mp")
    pairs = []
    for i in range(lax.axis_size("dp")):
        for core in range(cores):
            partner = i ^ (1 << orders[core % 2][at])
            pairs.append((i * cores + core, partner * cores + core))
    return lax.ppermute(values, ("dp", "mp"), pairs)


def group_hop(pieces, at):
    return jnp.concatenate([pieces, core_hop(pieces, at)], axis=0)


def place_of(core):
    partner = jnp.arange(lax.axis_size("dp")) ^ lax.axis_index("dp")
    places = []
    for order in core_orders():
        places.append(sum(((partner >> bit) & 1) << at for at, bit in enumerate(order)))
    return jnp.where(core % 2 == 0, places[0], places[1])


def reorder_masked(stacked, axis):
    count = bit_count(stacked.shape[0])
    here = lax.axis_index(axis)
    shape = stacked.shape
    values = stacked.reshape((2,) * count + shape[1:])
    for bit in range(count):
        turned = jnp.flip(values, count - 1 - bit)
        values = jnp.where(((here >> bit) & 1) == 1, turned, values)
    return values.reshape(shape)


def gather_small(values, axes):
    shape = values.shape
    values = values[None]
    for axis in reversed(axes):
        order = range(bit_count(lax.axis_size(axis)))
        stacked = jnp.stack(gather_masked(values, axis, order))
        values = reorder_masked(stacked, axis)
        values = values.reshape((-1,) + shape)
    return values


def scatter_small(values, axes):
    for axis in axes:
        size = lax.axis_size(axis)
        values = values.reshape((size, values.shape[0] // size) + values.shape[1:])
        turned = reorder_masked(values, axis)
        order = reversed(range(bit_count(size)))
        values = scatter_masked([turned[m] for m in range(size)], axis, order, f32)
    return values[0]


def line_size():
    return lax.axis_size("depth"), lax.axis_index("depth")


def fence(*values):
    return lax.optimization_barrier(values)


class LineGather:

    def __init__(self, values):
        self.up, self.down = [values], [values]

    def step(self):
        size, _ = line_size()
        at = len(self.up)
        if at < size:
            up_pairs = [(i, i + 1) for i in range(at - 1, size - 1)]
            down_pairs = [(i, i - 1) for i in range(1, size - at + 1)]
            self.up.append(lax.ppermute(self.up[-1], "depth", up_pairs))
            self.down.append(lax.ppermute(self.down[-1], "depth", down_pairs))

    def hold(self, *others):
        kept = fence((self.up[1:], self.down[1:]), *others)
        (up, down), rest = kept[0], kept[1:]
        self.up, self.down = self.up[:1] + list(up), self.down[:1] + list(down)
        return rest

    def placed_early(self):
        size, here = line_size()
        steps = jnp.arange(size)
        index = lax.rem(here - steps + size, size)
        own = self.up[0]
        blocks = self.up[: size - 1] + [own]
        instead = [own] + self.down[1 : size - 1][::-1]
        return place_line(index, here >= steps, blocks, instead)

    def farthest(self, early):
        size, here = line_size()
        last = jnp.where(here == size - 1, self.up[size - 1], early[:, 0])
        return jnp.where(here == 0, self.down[size - 1], last), jnp.where(here == 0, size - 1, 0)

    def placed(self):
        size, here = line_size()
        steps = jnp.arange(size)
        index = lax.rem(here - steps + size, size)
        return place_line(index, here >= steps, self.up, self.down[1:][::-1])


class LineScatter:

    def __init__(self, terms):
        self.terms, self.at = terms, 0
        self.up = self.down = None

    def step(self, *later):
        size, here = line_size()
        self.at += 1
        if self.at >= size:
            return later
        goes_up, goes_down = hop_sums(
            self.terms,
            jnp.minimum(size - self.at + here, size - 1),
            jnp.maximum(here - size + self.at, 0),
            self.up,
            self.down,
            [here < self.at, here > size - 1 - self.at],
        )
        (goes_up, goes_down), *later = fence((goes_up, goes_down), *later)
        up_pairs = [(i, i + 1) for i in range(min(self.at, size - 1))]
        down_pairs = [(size - 1 - i, size - 2 - i) for i in range(min(self.at, size - 1))]
        self.up = lax.ppermute(goes_up, "depth", up_pairs)
        self.down = lax.ppermute(goes_down, "depth", down_pairs)
        return later

    def step_with(self, line, *later):
        size, here = line_size()
        lead, _, tall, wide = self.terms.shape
        shape = line.up[0].shape
        if (
            len(line.up) != self.at + 2
            or self.at + 2 > size - 1
            or math.prod(shape) != lead * tall * wide
            or shape[2] != wide
        ):
            line.step()
            return self.step(*later)
        self.at += 1
        goes = hop_sums(
            self.terms,
            jnp.minimum(size - self.at + here, size - 1),
            jnp.maximum(here - size + self.at, 0),
            self.up,
            self.down,
            [here < self.at, here > size - 1 - self.at],
            [v[-1].reshape(lead, tall, wide) for v in (line.up, line.down)],
        )
        goes, *later = fence(goes, *later)
        self.up = lax.ppermute(goes[0], "depth", [(i, i + 1) for i in range(size - 1)])
        self.down = lax.ppermute(goes[1], "depth", [(i, i - 1) for i in range(1, size)])
        line.up.append(self.up.reshape(shape))
        line.down.append(self.down.reshape(shape))
        return later

    def hold(self, *others):
        (self.up, self.down), *rest = fence((self.up, self.down), *others)
        return rest


def other_core(values):
    return swap_mask(values, "mp", 1)


def join_kernel(model_ref, own_ref, other_ref, out_ref):
    width = own_ref.shape[1]
    own_at = pl.multiple_of(model_ref[0] * width, width)
    other_at = pl.multiple_of((1 - model_ref[0]) * width, width)
    out_ref[:, pl.ds(own_at, width)] = own_ref[...]
    out_ref[:, pl.ds(other_at, width)] = other_ref[...]


def join_halves(own, other, model_at):
    tall, width = own.shape
    rows = min(256, tall)
    return pl.pallas_call(
        join_kernel,
        grid_spec=pltpu.PrefetchScalarGridSpec(
            num_scalar_prefetch=1,
            grid=(tall // rows,),
            in_specs=[pl.BlockSpec((rows, width), lambda i, m: (i, 0))] * 2,
            out_specs=pl.BlockSpec((rows, 2 * width), lambda i, m: (i, 0)),
        ),
        out_shape=jax.ShapeDtypeStruct((tall, 2 * width), own.dtype),
        cost_estimate=spent(
            flops=0, bytes_accessed=8 * tall * width, transcendentals=0
        ),
        name="join_halves",
    )(model_at.astype(jnp.int32)[None], own, other)


def spent(flops, bytes_accessed, transcendentals):
    return pl.CostEstimate(
        flops=flops // COST, bytes_accessed=bytes_accessed // COST, transcendentals=transcendentals // COST
    )


def chunk_of(tall, wide):
    rows = tall
    while rows * wide > 1 << 19 and rows % 32 == 0:
        rows //= 2
    return rows


def place_kernel(at_ref, *refs):
    if len(refs) < 4:
        refs[-1][0, 0] = refs[0][0]
        return

    @pl.when(at_ref[1] == 1)
    def _():
        refs[-1][0, 0] = refs[0][0]

    @pl.when(at_ref[1] == 0)
    def _():
        refs[-1][0, 0] = refs[1][0]


def place_block(buffer, block, index, count, instead=None, first=None):
    lead, tall, wide = block.shape
    rows = chunk_of(tall, wide)
    spec = pl.BlockSpec((1, rows, wide), lambda l, i, m: (l, i, 0))
    blocks = [block] if instead is None else [block, instead]
    where = [index, 1 if first is None else first]
    where = jnp.stack([jnp.asarray(v).astype(jnp.int32) for v in where])
    in_specs, operands, aliases = [spec] * len(blocks), list(blocks), {}
    if buffer is not None or instead is not None:
        in_specs.append(pl.BlockSpec(memory_space=pl.ANY))
        operands.append(block if buffer is None else buffer)
        aliases = {} if buffer is None else {len(operands): 0}
    return pl.pallas_call(
        place_kernel,
        grid_spec=pltpu.PrefetchScalarGridSpec(
            num_scalar_prefetch=1,
            grid=(lead, tall // rows),
            in_specs=in_specs,
            out_specs=pl.BlockSpec((1, 1, rows, wide), lambda l, i, m: (l, m[0], i, 0)),
        ),
        out_shape=jax.ShapeDtypeStruct((lead, count, tall, wide), block.dtype),
        input_output_aliases=aliases,
        cost_estimate=spent(
            flops=0, bytes_accessed=4 * lead * tall * wide, transcendentals=0
        ),
        name="place_block",
    )(where, *operands)


def place_line_kernel(size, at_ref, *refs):
    out_ref = refs[-1]
    for step in range(size):
        if step == 0 or len(refs) == size + 1:
            out_ref[0, at_ref[step]] = refs[step][0]
            continue

        @pl.when(at_ref[size + step] == 1)
        def _(step=step):
            out_ref[0, at_ref[step]] = refs[step][0]

        @pl.when(at_ref[size + step] == 0)
        def _(step=step):
            out_ref[0, at_ref[step]] = refs[size + step - 1][0]


def place_line(index, first, blocks, instead):
    size = len(blocks)
    lead, tall, wide = blocks[0].shape
    rows = tall
    while rows * wide > 1 << 18 and rows % 32 == 0:
        rows //= 2
    spec = pl.BlockSpec((1, rows, wide), lambda l, i, m: (l, i, 0))
    where = jnp.concatenate([index, first]).astype(jnp.int32)
    operands = list(blocks) + list(instead)
    return pl.pallas_call(
        functools.partial(place_line_kernel, size),
        grid_spec=pltpu.PrefetchScalarGridSpec(
            num_scalar_prefetch=1,
            grid=(lead, tall // rows),
            in_specs=[spec] * len(operands),
            out_specs=pl.BlockSpec((1, size, rows, wide), lambda l, i, m: (l, 0, i, 0)),
        ),
        out_shape=jax.ShapeDtypeStruct((lead, size, tall, wide), blocks[0].dtype),
        compiler_params=pltpu.CompilerParams(vmem_limit_bytes=40 << 20),
        cost_estimate=spent(
            flops=0, bytes_accessed=6 * size * lead * tall * wide, transcendentals=0
        ),
        name="place_line",
    )(where, *operands)


def place_many(index, blocks):
    ones = jnp.ones(len(blocks), jnp.int32)
    return place_line(index, ones, blocks, [])


def group_join_kernel(at_ref, own_ref, other_ref, out_ref):
    width = own_ref.shape[2]
    own_span, other_span = own_spans(at_ref, width)
    out_ref[:, own_span] = own_ref[0]
    out_ref[:, other_span] = other_ref[0]


def group_join(own, other, model_at):
    count, tall, width = own.shape
    rows = chunk_of(tall, width)
    per = tall // rows
    where = jnp.concatenate([model_at[None], place_of(model_at), place_of(1 - model_at)])
    return pl.pallas_call(
        group_join_kernel,
        grid_spec=pltpu.PrefetchScalarGridSpec(
            num_scalar_prefetch=1,
            grid=(count, per),
            in_specs=[
                pl.BlockSpec((1, rows, width), lambda n, i, m: (m[1 + n], i, 0)),
                pl.BlockSpec((1, rows, width), lambda n, i, m: (m[1 + count + n], i, 0)),
            ],
            out_specs=pl.BlockSpec((rows, 2 * width), lambda n, i, m: (n * per + i, 0)),
        ),
        out_shape=jax.ShapeDtypeStruct((count * tall, 2 * width), own.dtype),
        cost_estimate=spent(
            flops=0, bytes_accessed=8 * count * tall * width, transcendentals=0
        ),
        name="group_join",
    )(where.astype(jnp.int32), own, other)


def group_split_kernel(at_ref, near_own, near_other, far_own, far_other, near_ref, far_ref):
    near_ref[0, 0] = near_own[0] + near_other[0].astype(f32)
    far_ref[0, 0] = (far_own[0] + far_other[0].astype(f32)).astype(bf16)


def group_split(own, other, places):
    _, tall, width = own.shape
    count = places.shape[0]
    half, rows = count // 2, tall // count
    near = pl.BlockSpec((1, rows, width), lambda p, k, m: (k, m[p], 0))
    far = pl.BlockSpec((1, rows, width), lambda p, k, m: (k, m[half + p], 0))
    out = pl.BlockSpec((1, 1, rows, width), lambda p, k, m: (p, k, 0, 0))
    return pl.pallas_call(
        group_split_kernel,
        grid_spec=pltpu.PrefetchScalarGridSpec(
            num_scalar_prefetch=1,
            grid=(half, 2),
            in_specs=[near, near, far, far],
            out_specs=[out, out],
        ),
        out_shape=[
            jax.ShapeDtypeStruct((half, 2, rows, width), f32),
            jax.ShapeDtypeStruct((half, 2, rows, width), bf16),
        ],
        cost_estimate=spent(
            flops=2 * tall * width, bytes_accessed=20 * tall * width, transcendentals=0
        ),
        name="group_split",
    )(places, own, other, own, other)


def hop_kernel(has_sums, has_blocks, at_ref, *refs):
    ins, outs = list(refs[:-2]), refs[-2:]
    terms, ins = ins[:2], ins[2:]
    sums, ins = (ins[:2], ins[2:]) if has_sums else (None, ins)

    def send_sum(way):
        term = terms[way][0, 0].astype(f32)
        if sums is not None:
            term = term + sums[way][0].astype(f32)
        outs[way][0] = term.astype(bf16)

    for way in range(2):
        if not has_blocks:
            send_sum(way)
            continue
        pl.when(at_ref[2 + way] == 1)(functools.partial(send_sum, way))

        @pl.when(at_ref[2 + way] == 0)
        def _(way=way):
            outs[way][0] = ins[way][0]


def hop_sums(terms, up_at, down_at, up, down, sends, blocks=None):
    lead, _, tall, wide = terms.shape
    rows = chunk_of(tall, wide)
    block = pl.BlockSpec((1, rows, wide), lambda l, i, m: (l, i, 0))

    def term_spec(way):
        return pl.BlockSpec(
            (1, 1, rows, wide), lambda l, i, m: (l * m[2 + way], m[way], i * m[2 + way], 0)
        )

    def block_spec(way, sign):
        def index(l, i, m):
            need = m[2 + way] if sign else 1 - m[2 + way]
            return (l * need, i * need, 0)

        return pl.BlockSpec((1, rows, wide), index)

    in_specs = [term_spec(0), term_spec(1)]
    operands = [terms, terms]
    if up is not None:
        in_specs += [block_spec(0, True), block_spec(1, True)]
        operands += [up, down]
    if blocks is not None:
        in_specs += [block_spec(0, False), block_spec(1, False)]
        operands += list(blocks)
    return pl.pallas_call(
        functools.partial(hop_kernel, up is not None, blocks is not None),
        grid_spec=pltpu.PrefetchScalarGridSpec(
            num_scalar_prefetch=1,
            grid=(lead, tall // rows),
            in_specs=in_specs,
            out_specs=[block, block],
        ),
        out_shape=[jax.ShapeDtypeStruct((lead, tall, wide), bf16)] * 2,
        cost_estimate=spent(
            flops=2 * lead * tall * wide, bytes_accessed=12 * lead * tall * wide, transcendentals=0
        ),
        name="hop_sums",
    )(jnp.stack([up_at, down_at, *sends]).astype(jnp.int32), *operands)


def end_kernel(at_ref, term_ref, up_ref, down_ref, out_ref):
    total = term_ref[0, 0].astype(f32) + up_ref[0].astype(f32) + down_ref[0].astype(f32)
    out_ref[0] = total.astype(out_ref.dtype)


def end_sums(sums, dtype):
    lead, _, tall, wide = sums.terms.shape
    rows = chunk_of(tall, wide)
    block = pl.BlockSpec((1, rows, wide), lambda l, i, m: (l, i, 0))
    return pl.pallas_call(
        end_kernel,
        grid_spec=pltpu.PrefetchScalarGridSpec(
            num_scalar_prefetch=1,
            grid=(lead, tall // rows),
            in_specs=[
                pl.BlockSpec((1, 1, rows, wide), lambda l, i, m: (l, m[0], i, 0)),
                block,
                block,
            ],
            out_specs=block,
        ),
        out_shape=jax.ShapeDtypeStruct((lead, tall, wide), dtype),
        cost_estimate=spent(
            flops=2 * lead * tall * wide, bytes_accessed=10 * lead * tall * wide, transcendentals=0
        ),
        name="end_sums",
    )(lax.axis_index("depth").astype(jnp.int32)[None], sums.terms, sums.up, sums.down)


def attention_grad_kernel(
    at_ref, x0_ref, x1_ref, cot_ref, g0_ref, g1_ref, out_ref
):
    tall = x0_ref.shape[1]

    def store(total):
        out_ref[...] = total.reshape(out_ref.shape).astype(out_ref.dtype)

    @pl.when(pl.program_id(0) < 3)
    def _():
        store(dot_tn(x0_ref[0], g0_ref[0]) + dot_tn(x1_ref[0], g1_ref[0]))

    @pl.when(pl.program_id(0) == 3)
    def _():
        store(
            dot_tn(cot_ref[0:tall, :], g0_ref[0]) + dot_tn(cot_ref[tall : 2 * tall, :], g1_ref[0])
        )


def attention_grads(normed, cot, flat, place, depth_count, dp_count, dtype):
    _, tall, model = normed[0].shape
    heads_width = flat[0].shape[2]
    block = model // dp_count
    own_rows = block // depth_count
    normed_spec = pl.BlockSpec((1, tall, block), lambda k, m: (jnp.minimum(k, 2), 0, m[0]))
    flat_spec = pl.BlockSpec((1, tall, heads_width), lambda k, m: (lax.rem(k + 1, 4), 0, 0))
    return pl.pallas_call(
        attention_grad_kernel,
        grid_spec=pltpu.PrefetchScalarGridSpec(
            num_scalar_prefetch=1,
            grid=(4,),
            in_specs=[
                normed_spec,
                normed_spec,
                pl.BlockSpec((2 * tall, block), lambda k, m: (0, m[0])),
                flat_spec,
                flat_spec,
            ],
            out_specs=pl.BlockSpec(
                (depth_count, 1, own_rows, heads_width), lambda k, m: (0, k, 0, 0)
            ),
        ),
        out_shape=jax.ShapeDtypeStruct((depth_count, 4, own_rows, heads_width), dtype),
        compiler_params=pltpu.CompilerParams(vmem_limit_bytes=40 << 20),
        cost_estimate=spent(
            flops=16 * tall * block * heads_width,
            bytes_accessed=16 * block * heads_width,
            transcendentals=0,
        ),
        name="attention_grads",
    )(place, *normed, cot, *flat)


def hidden_grad_kernel(x0_ref, x1_ref, c0_ref, c1_ref, u0_ref, u1_ref, h0_ref, h1_ref, out_ref):
    def store(total):
        out_ref[...] = total.reshape(out_ref.shape).astype(bf16)

    @pl.when(pl.program_id(0) == 0)
    def _():
        store(dot_tn(x0_ref[...], u0_ref[...]) + dot_tn(x1_ref[...], u1_ref[...]))

    @pl.when(pl.program_id(0) == 1)
    def _():
        tall, wide = h0_ref.shape[0], c0_ref.shape[3]
        c0, c1 = c0_ref[:, 0].reshape(tall, wide), c1_ref[:, 0].reshape(tall, wide)
        store(dot_tn(c0, h0_ref[...]) + dot_tn(c1, h1_ref[...]))


def hidden_grads(x, cot, up_grads, hidden, dp_count, depth_count):
    tall, model = x[0].shape
    part = hidden[0].shape[1]
    block = model // dp_count
    cols = pl.BlockSpec((tall, block), lambda k, n: (0, n * (1 - k)))
    whole = pl.BlockSpec((tall, part), lambda k, n: (0, 0))
    return pl.pallas_call(
        hidden_grad_kernel,
        grid=(2, dp_count),
        in_specs=[cols, cols]
        + [
            pl.BlockSpec((dp_count, 1, cot.shape[2], block), lambda k, n: (0, 0, 0, n * k)),
            pl.BlockSpec((dp_count, 1, cot.shape[2], block), lambda k, n: (0, 1, 0, n * k)),
        ]
        + [whole] * 4,
        out_specs=pl.BlockSpec(
            (1, depth_count, block // depth_count, part), lambda k, n: (k * dp_count + n, 0, 0, 0)
        ),
        out_shape=jax.ShapeDtypeStruct(
            (2 * dp_count, depth_count, block // depth_count, part), bf16
        ),
        compiler_params=pltpu.CompilerParams(vmem_limit_bytes=48 << 20),
        cost_estimate=spent(
            flops=8 * tall * model * part, bytes_accessed=8 * model * part, transcendentals=0
        ),
        name="hidden_grads",
    )(*x, cot, cot, *up_grads, *hidden)


def mix_kernel(slots, mix_ref, hist_ref, out_ref):
    rows, width = hist_ref.shape[1], hist_ref.shape[2]
    part = 512 if width % 512 == 0 else width

    def step(at, carry):
        r0 = pl.multiple_of(at * 16, 16)
        weights = mix_ref[pl.ds(r0, 16), :]
        for c0 in range(0, width, part):
            sums = [None] * STREAMS
            for k in range(slots):
                state = hist_ref[k, pl.ds(r0, 16), c0 : c0 + part].astype(f32)
                for s in range(STREAMS):
                    term = weights[:, s * slots + k : s * slots + k + 1] * state
                    sums[s] = term if sums[s] is None else sums[s] + term
            for s in range(STREAMS):
                out_ref[s, pl.ds(r0, 16), c0 : c0 + part] = sums[s].astype(bf16)
        return carry

    lax.fori_loop(0, rows // 16, step, 0)


def mix_streams(slot_mix, history, micro_at, depth_count, rows_mb):
    slots, _, width = history.shape
    rows = min(128, rows_mb)
    per = rows_mb // rows

    def row_block(i):
        return ((i // per) * MB + micro_at) * per + i % per

    return pl.pallas_call(
        functools.partial(mix_kernel, slots),
        grid=(depth_count * per,),
        in_specs=[
            pl.BlockSpec((rows, slot_mix.shape[1]), lambda i: (row_block(i), 0)),
            pl.BlockSpec((slots, rows, width), lambda i: (0, row_block(i), 0)),
        ],
        out_specs=pl.BlockSpec((STREAMS, rows, width), lambda i: (0, i, 0)),
        out_shape=jax.ShapeDtypeStruct((STREAMS, depth_count * rows_mb, width), bf16),
        cost_estimate=spent(
            flops=2 * slots * STREAMS * depth_count * rows_mb * width,
            bytes_accessed=2 * (slots + STREAMS) * depth_count * rows_mb * width,
            transcendentals=0,
        ),
        name="mix_streams",
    )(slot_mix, history)


def unmix_kernel(slots, mix_ref, hist_ref, grad_ref, *rest):
    hist_grad_ref, slot_grad_ref = rest[-2:]
    rows, width = hist_ref.shape[1], hist_ref.shape[2]
    part = 512 if width % 512 == 0 else width

    def step(at, carry):
        r0 = pl.multiple_of(at * 16, 16)
        weights = mix_ref[pl.ds(r0, 16), :]
        totals = [None] * (STREAMS * slots)
        for c0 in range(0, width, part):
            grads = [
                grad_ref[s, pl.ds(r0, 16), c0 : c0 + part].astype(f32)
                for s in range(STREAMS)
            ]
            for k in range(slots):
                state = hist_ref[k, pl.ds(r0, 16), c0 : c0 + part].astype(f32)
                back = None
                for s in range(STREAMS):
                    at_sk = s * slots + k
                    term = weights[:, at_sk : at_sk + 1] * grads[s]
                    back = term if back is None else back + term
                    product = state * grads[s]
                    folded = product[:, 0:128]
                    for l0 in range(128, part, 128):
                        folded = folded + product[:, l0 : l0 + 128]
                    totals[at_sk] = folded if totals[at_sk] is None else totals[at_sk] + folded
                hist_grad_ref[k, pl.ds(r0, 16), c0 : c0 + part] = back.astype(bf16)
        lane = lax.broadcasted_iota(jnp.int32, (16, 128), 1)
        packed = jnp.zeros((16, 128), f32)
        for at_sk in range(STREAMS * slots):
            column = jnp.sum(totals[at_sk], axis=1, keepdims=True)
            packed = jnp.where(lane == at_sk, column, packed)
        slot_grad_ref[pl.ds(r0, 16), :] = packed
        return carry

    lax.fori_loop(0, rows // 16, step, 0)


def unmix_streams(slot_mix, history, grads, micro_at, depth_count, rows_mb, earlier):
    slots, tokens, width = history.shape
    rows = min(128, rows_mb)
    per = rows_mb // rows

    def row_block(i):
        return ((i // per) * MB + micro_at) * per + i % per

    in_specs = [
        pl.BlockSpec((rows, slot_mix.shape[1]), lambda i: (row_block(i), 0)),
        pl.BlockSpec((slots, rows, width), lambda i: (0, row_block(i), 0)),
        pl.BlockSpec((STREAMS, rows, width), lambda i: (0, i, 0)),
    ]
    operands = [slot_mix, history, grads]
    aliases = {}
    if earlier is not None:
        in_specs.append(pl.BlockSpec(memory_space=pl.ANY))
        operands.append(earlier)
        aliases = {3: 0}
    return pl.pallas_call(
        functools.partial(unmix_kernel, slots),
        grid=(depth_count * per,),
        in_specs=in_specs,
        out_specs=[
            pl.BlockSpec((slots, rows, width), lambda i: (0, row_block(i), 0)),
            pl.BlockSpec((rows, 128), lambda i: (i, 0)),
        ],
        out_shape=[
            jax.ShapeDtypeStruct((slots, tokens, width), bf16),
            jax.ShapeDtypeStruct((depth_count * rows_mb, 128), f32),
        ],
        input_output_aliases=aliases,
        cost_estimate=spent(
            flops=4 * slots * STREAMS * depth_count * rows_mb * width,
            bytes_accessed=2 * (2 * slots + STREAMS) * depth_count * rows_mb * width,
            transcendentals=0,
        ),
        name="unmix_streams",
    )(*operands)


def unmix_one(slot_mix, history, grads, micro_at, index, rows_mb, earlier):
    slots, tokens, width = history.shape
    rows = min(128, rows_mb)
    per = rows_mb // rows

    def row_block(i, m):
        return (m[0] * MB + micro_at) * per + i

    def kernel(at_ref, *refs):
        unmix_kernel(slots, *refs)

    return pl.pallas_call(
        kernel,
        grid_spec=pltpu.PrefetchScalarGridSpec(
            num_scalar_prefetch=1,
            grid=(per,),
            in_specs=[
                pl.BlockSpec((rows, slot_mix.shape[1]), lambda i, m: (row_block(i, m), 0)),
                pl.BlockSpec((slots, rows, width), lambda i, m: (0, row_block(i, m), 0)),
                pl.BlockSpec((STREAMS, rows, width), lambda i, m: (0, i, 0)),
                pl.BlockSpec(memory_space=pl.ANY),
            ],
            out_specs=[
                pl.BlockSpec((slots, rows, width), lambda i, m: (0, row_block(i, m), 0)),
                pl.BlockSpec((rows, 128), lambda i, m: (i, 0)),
            ],
        ),
        out_shape=[
            jax.ShapeDtypeStruct((slots, tokens, width), bf16),
            jax.ShapeDtypeStruct((rows_mb, 128), f32),
        ],
        input_output_aliases={4: 0},
        cost_estimate=spent(
            flops=4 * slots * STREAMS * rows_mb * width,
            bytes_accessed=2 * (2 * slots + STREAMS) * rows_mb * width,
            transcendentals=0,
        ),
        name="unmix_one",
    )(index.astype(jnp.int32)[None], slot_mix, history, grads, earlier)


def own_spans(model_ref, width):
    own_at = pl.multiple_of(model_ref[0] * width, width)
    other_at = pl.multiple_of((1 - model_ref[0]) * width, width)
    return pl.ds(own_at, width), pl.ds(other_at, width)


def ff_split_kernel(at_ref, up_ref, down_ref, out_ref):
    out_ref[0, 0] = up_ref[...]
    out_ref[0, 1] = down_ref[...].T


def ff_split(up_weight, down_weight, partners):
    own_rows, ff_width = up_weight.shape
    count = partners.shape[0]
    part = ff_width // count
    return pl.pallas_call(
        ff_split_kernel,
        grid_spec=pltpu.PrefetchScalarGridSpec(
            num_scalar_prefetch=1,
            grid=(count,),
            in_specs=[
                pl.BlockSpec((own_rows, part), lambda i, m: (0, m[i])),
                pl.BlockSpec((part, own_rows), lambda i, m: (m[i], 0)),
            ],
            out_specs=pl.BlockSpec((1, 2, own_rows, part), lambda i, m: (i, 0, 0, 0)),
        ),
        out_shape=jax.ShapeDtypeStruct((count, 2, own_rows, part), bf16),
        cost_estimate=spent(flops=0, bytes_accessed=8 * own_rows * ff_width, transcendentals=0),
        name="ff_split",
    )(partners, up_weight, down_weight)


def ff_join_kernel(at_ref, piece_ref, up_ref, down_ref):
    up_ref[...] = piece_ref[0, 0].astype(f32)
    down_ref[...] = piece_ref[0, 1].astype(f32).T


def ff_join(pieces, partners):
    count, _, own_rows, part = pieces.shape
    return pl.pallas_call(
        ff_join_kernel,
        grid_spec=pltpu.PrefetchScalarGridSpec(
            num_scalar_prefetch=1,
            grid=(count,),
            in_specs=[pl.BlockSpec((1, 2, own_rows, part), lambda i, m: (i, 0, 0, 0))],
            out_specs=[
                pl.BlockSpec((own_rows, part), lambda i, m: (0, m[i])),
                pl.BlockSpec((part, own_rows), lambda i, m: (m[i], 0)),
            ],
        ),
        out_shape=[
            jax.ShapeDtypeStruct((own_rows, count * part), f32),
            jax.ShapeDtypeStruct((count * part, own_rows), f32),
        ],
        cost_estimate=spent(
            flops=0, bytes_accessed=12 * own_rows * count * part, transcendentals=0
        ),
        name="ff_join",
    )(partners, pieces)


def total_kernel(depth_ref, part_ref, up_ref, down_ref, cur_ref, last_ref, low_ref, resid_ref):
    width = resid_ref.shape[1]
    current = cur_ref[...].astype(f32)
    for s in range(STREAMS):
        lanes = slice(s * width, (s + 1) * width)
        total = part_ref[s, 0].astype(f32)
        total = total + up_ref[s].astype(f32) + down_ref[s].astype(f32)
        total = total + last_ref[:, s : s + 1] * current
        if s == STREAMS - 1:
            resid_ref[...] = total
        low_ref[:, lanes] = total.astype(bf16)


def total_streams(sums, current_half, last, depth_at):
    _, _, tall, width = sums.terms.shape
    wide = STREAMS * width
    rows = min(64, tall)
    row = lambda i, d: (i, 0)
    return pl.pallas_call(
        total_kernel,
        grid_spec=pltpu.PrefetchScalarGridSpec(
            num_scalar_prefetch=1,
            grid=(tall // rows,),
            in_specs=[
                pl.BlockSpec((STREAMS, 1, rows, width), lambda i, d: (0, d[0], i, 0)),
                pl.BlockSpec((STREAMS, rows, width), lambda i, d: (0, i, 0)),
                pl.BlockSpec((STREAMS, rows, width), lambda i, d: (0, i, 0)),
                pl.BlockSpec((rows, width), row),
                pl.BlockSpec((rows, 128), row),
            ],
            out_specs=[pl.BlockSpec((rows, wide), row), pl.BlockSpec((rows, width), row)],
        ),
        out_shape=[
            jax.ShapeDtypeStruct((tall, wide), bf16),
            jax.ShapeDtypeStruct((tall, width), f32),
        ],
        cost_estimate=spent(flops=5 * tall * wide, bytes_accessed=9 * tall * wide, transcendentals=0),
        name="total_streams",
    )(depth_at, sums.terms, sums.up, sums.down, current_half, last)


def norm_kernel(model_ref, own_ref, other_ref, gain_ref, normed_ref, ff_ref, stat_ref):
    rows, width = ff_ref.shape
    model = 2 * width
    own_span, other_span = own_spans(model_ref, width)
    lane = lax.broadcasted_iota(jnp.int32, (rows, 128), 1)
    stats = jnp.zeros((rows, 128), f32)
    for s in range(STREAMS):
        lanes = slice(s * width, (s + 1) * width)
        own = own_ref[:, lanes].astype(f32)
        other = other_ref[:, lanes].astype(f32)
        average = (
            jnp.sum(own, axis=-1, keepdims=True) + jnp.sum(other, axis=-1, keepdims=True)
        ) / model
        own, other = own - average, other - average
        variance = (
            jnp.sum(own * own, axis=-1, keepdims=True)
            + jnp.sum(other * other, axis=-1, keepdims=True)
        ) / model
        inverse = lax.rsqrt(variance + NORM_EPSILON)
        stats = jnp.where(lane == 2 * s, average, stats)
        stats = jnp.where(lane == 2 * s + 1, inverse, stats)
        norm_own = (own * inverse * gain_ref[s : s + 1, own_span]).astype(bf16)
        if s == STREAMS - 1:
            ff_ref[...] = norm_own
        else:
            normed_ref[s, :, own_span] = norm_own
            norm_other = (other * inverse * gain_ref[s : s + 1, other_span]).astype(bf16)
            normed_ref[s, :, other_span] = norm_other
    stat_ref[...] = stats


def norm_streams(low, low_other, gains, which):
    tall, wide = low.shape
    width = wide // STREAMS
    rows = min(64, tall)
    row = lambda i, m: (i, 0)
    return pl.pallas_call(
        norm_kernel,
        grid_spec=pltpu.PrefetchScalarGridSpec(
            num_scalar_prefetch=1,
            grid=(tall // rows,),
            in_specs=[
                pl.BlockSpec((rows, wide), row),
                pl.BlockSpec((rows, wide), row),
                pl.BlockSpec(gains.shape, lambda i, m: (0, 0)),
            ],
            out_specs=[
                pl.BlockSpec((3, rows, 2 * width), lambda i, m: (0, i, 0)),
                pl.BlockSpec((rows, width), row),
                pl.BlockSpec((rows, 128), row),
            ],
        ),
        out_shape=[
            jax.ShapeDtypeStruct((3, tall, 2 * width), bf16),
            jax.ShapeDtypeStruct((tall, width), bf16),
            jax.ShapeDtypeStruct((tall, 128), f32),
        ],
        cost_estimate=spent(
            flops=20 * tall * wide, bytes_accessed=8 * tall * wide, transcendentals=0
        ),
        name="norm_streams",
    )(which, low, low_other, gains)


def turn(values, cosine, sine_up, sine_down, sign):
    up = pltpu.roll(values, HDIM - ROT // 2, 1)
    down = pltpu.roll(values, ROT // 2, 1)
    return values * cosine + sign * (up * sine_up + down * sine_down)


def project_kernel(
    x_ref, cot_ref, wq_ref, wk_ref, wv_ref, wo_ref, cos_ref, up_ref, down_ref, out_ref
):
    span = wq_ref.shape[-1]
    tables = cos_ref[...], up_ref[...], down_ref[...]
    for kind, w_ref in enumerate((wq_ref, wk_ref, wv_ref, wo_ref)):
        rows = cot_ref[...] if kind == 3 else x_ref[kind]
        product = dot_nn(rows, w_ref[...].reshape(-1, span))
        for begin in range(0, span, HDIM):
            head = product[:, begin : begin + HDIM]
            if kind < 2:
                head = turn(head, *tables, 1.0)
            out_ref[0, :, kind * span + begin : kind * span + begin + HDIM] = head.astype(bf16)


def project_heads(normed, cot, weights, tables, depth_count):
    _, rows, model = normed.shape
    groups, _, _, own_rows, heads_width = weights.shape
    span = heads_width // depth_count
    whole = lambda j: (0, 0)

    def matrix(kind):
        shape = (groups, depth_count, 1, own_rows, span)
        return pl.BlockSpec(shape, lambda j: (0, 0, kind, 0, j))

    return pl.pallas_call(
        project_kernel,
        grid=(depth_count,),
        in_specs=[
            pl.BlockSpec((3, rows, model), lambda j: (0, 0, 0)),
            pl.BlockSpec((rows, model), whole),
        ]
        + [matrix(kind) for kind in range(4)]
        + [pl.BlockSpec((rows, HDIM), whole)] * 3,
        out_specs=pl.BlockSpec((1, rows, 4 * span), lambda j: (j, 0, 0)),
        out_shape=jax.ShapeDtypeStruct((depth_count, rows, 4 * span), bf16),
        compiler_params=pltpu.CompilerParams(vmem_limit_bytes=40 << 20),
        cost_estimate=spent(
            flops=8 * rows * model * span * depth_count,
            bytes_accessed=8 * model * span * depth_count + 8 * rows * model,
            transcendentals=0,
        ),
        name="project_heads",
    )(normed, cot, *[weights] * 4, *tables)


def attend_kernel(
    block, q_ref, k_ref, v_ref, g_ref, doc_col_ref, doc_row_ref, cos_ref, up_ref, down_ref,
    out_ref, dk_sum, dv_sum,
):
    length = q_ref.shape[0]
    scale = HDIM**-0.5
    heads_each = out_ref.shape[1] // (4 * HDIM)

    def lanes(kind):
        return pl.ds(pl.multiple_of((kind * heads_each + pl.program_id(0)) * HDIM, HDIM), HDIM)

    for begin in range(0, length, block):
        end = begin + block
        rows = slice(begin, end)
        queries, grads = q_ref[rows, :], g_ref[rows, :]
        keys, values = k_ref[0:end, :], v_ref[0:end, :]
        scores = dot_nt(queries, keys) * scale
        place_q = begin + lax.broadcasted_iota(jnp.int32, scores.shape, 0)
        place_k = lax.broadcasted_iota(jnp.int32, scores.shape, 1)
        allowed = (doc_col_ref[rows, :] == doc_row_ref[:, 0:end]) & (place_q >= place_k)
        scores = jnp.where(allowed, scores, MASKED)
        highest = jnp.max(scores, axis=-1, keepdims=True)
        exponent = jnp.exp(scores - highest)
        totals = jnp.sum(exponent, axis=-1, keepdims=True)
        attention = exponent * (1.0 / totals)
        low = attention.astype(bf16)
        out_ref[rows, lanes(0)] = dot_nn(low, values).astype(bf16)
        grad_att = dot_nt(grads, values).astype(bf16).astype(f32)
        weighted = jnp.sum(attention * grad_att, axis=-1, keepdims=True)
        grad_scores = (attention * (grad_att - weighted)).astype(bf16)
        grad_q = dot_nn(grad_scores, keys) * scale
        out_ref[rows, lanes(1)] = turn(
            grad_q, cos_ref[rows, :], up_ref[rows, :], down_ref[rows, :], -1.0
        ).astype(bf16)
        part_k = dot_tn(grad_scores, queries)
        part_v = dot_tn(low, grads)
        if begin > 0:
            dk_sum[0:begin, :] += part_k[0:begin]
            dv_sum[0:begin, :] += part_v[0:begin]
        dk_sum[begin:end, :] = part_k[begin:end]
        dv_sum[begin:end, :] = part_v[begin:end]
    grad_k = dk_sum[...] * scale
    out_ref[:, lanes(2)] = turn(grad_k, cos_ref[...], up_ref[...], down_ref[...], -1.0).astype(bf16)
    out_ref[:, lanes(3)] = dv_sum[...].astype(bf16)


def attend(packed, documents, tables, heads_each):
    length = packed.shape[0]
    block = min(256, length)
    whole = lambda h: (0, 0)

    def kind(at):
        return pl.BlockSpec((length, HDIM), lambda h: (0, at * heads_each + h))

    return pl.pallas_call(
        functools.partial(attend_kernel, block),
        grid=(heads_each,),
        in_specs=[kind(0), kind(1), kind(2), kind(3)]
        + [pl.BlockSpec((length, 1), whole), pl.BlockSpec((1, length), whole)]
        + [pl.BlockSpec((length, HDIM), whole)] * 3,
        out_specs=pl.BlockSpec((length, 4 * heads_each * HDIM), whole),
        out_shape=jax.ShapeDtypeStruct((length, 4 * heads_each * HDIM), bf16),
        scratch_shapes=[pltpu.VMEM((length, HDIM), f32)] * 2,
        compiler_params=pltpu.CompilerParams(vmem_limit_bytes=48 << 20),
        cost_estimate=spent(
            flops=9 * heads_each * length * length * HDIM,
            bytes_accessed=16 * length * heads_each * HDIM + 12 * length * HDIM,
            transcendentals=heads_each * length * length,
        ),
        name="attend",
    )(packed, packed, packed, packed, documents[:, None], documents[None, :], *tables)


def gelu_parts(values):
    cdf = 0.5 * (1.0 + lax.erf(values * (0.5**0.5)))
    density = jnp.exp(-0.5 * values * values) * (1.0 / math.sqrt(2.0 * math.pi))
    return values * cdf, cdf + values * density


def ff_kernel(
    model_ref, x_ref, cot_ref, up_ref, down_ref,
    hidden_ref, grad_ref, own_ref, other_ref,
):
    part = up_ref.shape[-1]
    half = up_ref.shape[1] // 2

    def rows_of(ref, which):
        return ref[0, pl.ds(which * half, half)].reshape(-1, part)

    own, other = model_ref[0], 1 - model_ref[0]
    up_pre = dot_nn(x_ref[...], up_ref[...].reshape(-1, part))
    hidden, slope = gelu_parts(up_pre)
    hidden = hidden.astype(bf16)
    grad_up = (dot_nn(cot_ref[0, 0], down_ref[...].reshape(-1, part)) * slope).astype(bf16)
    hidden_ref[...] = hidden
    grad_ref[...] = grad_up
    other_ref[0] = dot_nt(grad_up, rows_of(up_ref, other)).astype(bf16)
    own_ref[0] = dot_nt(grad_up, rows_of(up_ref, own))
    other_ref[1] = dot_nt(hidden, rows_of(down_ref, other)).astype(bf16)
    own_ref[1] = dot_nt(hidden, rows_of(down_ref, own))


def feed_forward(x, cot, micro_at, weights, which):
    tall, model = x.shape
    part = weights.shape[-1]
    width = model // 2
    rows = cot.shape[2]
    row = lambda i, m: (i, 0)

    def resident(kind):
        return pl.BlockSpec(
            (1,) + weights.shape[1:],
            lambda i, m: (kind, 0, 0, 0, 0),
            pipeline_mode=pl.Buffered(1),
        )

    return pl.pallas_call(
        ff_kernel,
        grid_spec=pltpu.PrefetchScalarGridSpec(
            num_scalar_prefetch=1,
            grid=(tall // rows,),
            in_specs=[
                pl.BlockSpec((rows, model), row),
                pl.BlockSpec((1, 1, rows, model), lambda i, m: (i, micro_at, 0, 0)),
                resident(0),
                resident(1),
            ],
            out_specs=[pl.BlockSpec((rows, part), row)] * 2
            + [pl.BlockSpec((2, rows, width), lambda i, m: (0, i, 0))] * 2,
        ),
        out_shape=[jax.ShapeDtypeStruct((tall, part), bf16)] * 2
        + [
            jax.ShapeDtypeStruct((2, tall, width), f32),
            jax.ShapeDtypeStruct((2, tall, width), bf16),
        ],
        compiler_params=pltpu.CompilerParams(vmem_limit_bytes=48 << 20),
        cost_estimate=spent(
            flops=8 * tall * model * part,
            bytes_accessed=4 * model * part + 16 * tall * model,
            transcendentals=2 * tall * part,
        ),
        name="feed_forward",
    )(which, x, cot, weights, weights)


def back_kernel(half_ref, ans_ref, wo_ref, wq_ref, wk_ref, wv_ref, out_ref, *flat):
    count, _, wide = ans_ref.shape
    span = wide // 4
    for kind, w_ref in enumerate((wo_ref, wq_ref, wk_ref, wv_ref)):
        total = None
        for j in range(count):
            term = dot_nt(
                ans_ref[j, :, kind * span : (kind + 1) * span],
                w_ref[:, :, :, :, j * span : (j + 1) * span].reshape(-1, span),
            )
            total = term if total is None else total + term
        out_ref[kind] = total.astype(out_ref.dtype)
    if flat:

        @pl.when(pl.program_id(0) == 0)
        def _():
            for kind in range(4):
                for j in range(count):
                    flat[0][kind, :, j * span : (j + 1) * span] = ans_ref[
                        j, :, kind * span : (kind + 1) * span
                    ]


def back_project(answer, weights, half, dtype, flat):
    count, rows, wide = answer.shape
    groups, _, _, own_rows, heads_width = weights.shape
    part = count * own_rows
    steps = groups // 2
    width = part * steps

    def matrix(kind):
        shape = (1, count, 1, own_rows, heads_width)
        return pl.BlockSpec(shape, lambda i, m: (m[0] * steps + i, 0, kind, 0, 0))

    out_specs = [pl.BlockSpec((4, rows, part), lambda i, m: (0, 0, i))]
    out_shape = [jax.ShapeDtypeStruct((4, rows, width), dtype)]
    if flat:
        out_specs.append(pl.BlockSpec((4, rows, heads_width), lambda i, m: (0, 0, 0)))
        out_shape.append(jax.ShapeDtypeStruct((4, rows, heads_width), bf16))
    return pl.pallas_call(
        back_kernel,
        grid_spec=pltpu.PrefetchScalarGridSpec(
            num_scalar_prefetch=1,
            grid=(steps,),
            in_specs=[pl.BlockSpec((count, rows, wide), lambda i, m: (0, 0, 0))]
            + [matrix(kind) for kind in (3, 0, 1, 2)],
            out_specs=out_specs,
        ),
        out_shape=out_shape,
        compiler_params=pltpu.CompilerParams(vmem_limit_bytes=40 << 20),
        cost_estimate=spent(
            flops=8 * rows * heads_width * width,
            bytes_accessed=8 * heads_width * width + 20 * rows * width,
            transcendentals=0,
        ),
        name="back_project",
    )(half, answer, *[weights] * 4)


def slope_kernel(
    model_ref, own_ref, got_ref, ff_ref, low_ref, stat_ref, gain_ref, scaled_ref, sum_ref, gain_out_ref
):
    _, rows, width = ff_ref.shape
    own_span, _ = own_spans(model_ref, width)
    lane = lax.broadcasted_iota(jnp.int32, (rows, 128), 1)
    packed = jnp.zeros((rows, 128), f32)
    totals = []
    for s in range(STREAMS):
        lanes = slice(s * width, (s + 1) * width)
        if s < 3:
            grad = own_ref[s + 1] + got_ref[s + 1].astype(f32)
        else:
            grad = ff_ref[0]
        average, inverse = stat_ref[:, 2 * s : 2 * s + 1], stat_ref[:, 2 * s + 1 : 2 * s + 2]
        hat = (low_ref[:, lanes].astype(f32) - average) * inverse
        totals.append(jnp.sum(grad * hat, axis=0, keepdims=True))
        scaled = grad * gain_ref[s : s + 1, own_span]
        scaled_ref[:, lanes] = scaled
        packed = jnp.where(lane == 2 * s, jnp.sum(scaled, axis=-1, keepdims=True), packed)
        packed = jnp.where(
            lane == 2 * s + 1, jnp.sum(scaled * hat, axis=-1, keepdims=True), packed
        )
    sum_ref[...] = packed
    totals = jnp.concatenate(totals, axis=0)

    @pl.when(pl.program_id(0) == 0)
    def _():
        gain_out_ref[...] = totals

    @pl.when(pl.program_id(0) > 0)
    def _():
        gain_out_ref[...] += totals


def norm_slopes(own, got, ff_grad, low, stats, gains, which):
    tall, wide = low.shape
    width = wide // STREAMS
    rows = min(64, tall)
    row = lambda i, m: (i, 0)
    cube = pl.BlockSpec((4, rows, width), lambda i, m: (0, i, 0))
    return pl.pallas_call(
        slope_kernel,
        grid_spec=pltpu.PrefetchScalarGridSpec(
            num_scalar_prefetch=1,
            grid=(tall // rows,),
            in_specs=[
                cube,
                cube,
                pl.BlockSpec((1, rows, width), lambda i, m: (0, i, 0)),
                pl.BlockSpec((rows, wide), row),
                pl.BlockSpec((rows, 128), row),
                pl.BlockSpec(gains.shape, lambda i, m: (0, 0)),
            ],
            out_specs=[
                pl.BlockSpec((rows, wide), row),
                pl.BlockSpec((rows, 128), row),
                pl.BlockSpec((STREAMS, width), lambda i, m: (0, 0)),
            ],
        ),
        out_shape=[
            jax.ShapeDtypeStruct((tall, wide), f32),
            jax.ShapeDtypeStruct((tall, 128), f32),
            jax.ShapeDtypeStruct((STREAMS, width), f32),
        ],
        cost_estimate=spent(
            flops=12 * tall * wide, bytes_accessed=12 * tall * wide, transcendentals=0
        ),
        name="norm_slopes",
    )(which, own, got, ff_grad, low, stats, gains)


def grads_kernel(
    scaled_ref, mine_ref, theirs_ref, low_ref, stat_ref, cot_ref, cur_ref, last_ref,
    grad_ref, mix_ref, dot_ref,
):
    rows, width = cot_ref.shape
    lane = lax.broadcasted_iota(jnp.int32, (rows, 128), 1)
    means = (mine_ref[...] + theirs_ref[...]) / (2 * width)
    current = cur_ref[...].astype(f32)
    packed = jnp.zeros((rows, 128), f32)
    mixed = None
    for s in range(STREAMS):
        lanes = slice(s * width, (s + 1) * width)
        average, inverse = stat_ref[:, 2 * s : 2 * s + 1], stat_ref[:, 2 * s + 1 : 2 * s + 2]
        hat = (low_ref[:, lanes].astype(f32) - average) * inverse
        grad = inverse * (
            scaled_ref[:, lanes]
            - means[:, 2 * s : 2 * s + 1]
            - hat * means[:, 2 * s + 1 : 2 * s + 2]
        )
        if s == STREAMS - 1:
            grad = grad + cot_ref[...].astype(f32)
        grad = grad.astype(bf16)
        grad_ref[s] = grad
        grad = grad.astype(f32)
        term = last_ref[:, s : s + 1] * grad
        mixed = term if mixed is None else mixed + term
        packed = jnp.where(lane == s, jnp.sum(grad * current, axis=-1, keepdims=True), packed)
    mix_ref[...] = mixed
    dot_ref[...] = packed


def stream_grads(scaled, mine, theirs, low, stats, cot, current_half, last):
    tall, wide = low.shape
    width = wide // STREAMS
    rows = min(64, tall)
    row = lambda i: (i, 0)
    return pl.pallas_call(
        grads_kernel,
        grid=(tall // rows,),
        in_specs=[
            pl.BlockSpec((rows, wide), row),
            pl.BlockSpec((rows, 128), row),
            pl.BlockSpec((rows, 128), row),
            pl.BlockSpec((rows, wide), row),
            pl.BlockSpec((rows, 128), row),
            pl.BlockSpec((rows, width), row),
            pl.BlockSpec((rows, width), row),
            pl.BlockSpec((rows, 128), row),
        ],
        out_specs=[
            pl.BlockSpec((STREAMS, rows, width), lambda i: (0, i, 0)),
            pl.BlockSpec((rows, width), row),
            pl.BlockSpec((rows, 128), row),
        ],
        out_shape=[
            jax.ShapeDtypeStruct((STREAMS, tall, width), bf16),
            jax.ShapeDtypeStruct((tall, width), f32),
            jax.ShapeDtypeStruct((tall, 128), f32),
        ],
        cost_estimate=spent(
            flops=12 * tall * wide, bytes_accessed=10 * tall * wide, transcendentals=0
        ),
        name="stream_grads",
    )(scaled, mine, theirs, low, stats, cot, current_half, last)


def turning_tables(places):
    half = ROT // 2
    inverse = jnp.exp(jnp.arange(half, dtype=f32) * (-2.0 * math.log(10000.0) / ROT))
    angles = places.astype(f32)[:, None] * inverse[None, :]
    cosine, sine = jnp.cos(angles), jnp.sin(angles)
    rows = places.shape[0]
    rest = jnp.zeros((rows, HDIM - ROT), f32)
    blank = jnp.zeros((rows, half), f32)
    return (
        jnp.concatenate([cosine, cosine, rest + 1.0], axis=1),
        jnp.concatenate([-sine, blank, rest], axis=1),
        jnp.concatenate([blank, sine, rest], axis=1),
    )


def local(
    history,
    slot_layer,
    current,
    positions,
    doc_ids,
    cotangent,
    norm_gains,
    generator_in,
    generator_out,
    query_weight,
    key_weight,
    value_weight,
    out_weight,
    up_weight,
    down_weight,
):
    dp_count = lax.axis_size("dp")
    depth_count = lax.axis_size("depth")
    dp_at = lax.axis_index("dp")
    model_at = lax.axis_index("mp")
    dp_bits = list(range(bit_count(dp_count)))
    slots, tokens_held, width = history.shape
    model = current.shape[1]
    rows_mb = current.shape[0] // MB
    length = depth_count * rows_mb
    heads_width = query_weight.shape[1]
    heads_each = heads_width // HDIM // depth_count
    own_rows = query_weight.shape[0]
    ff_width = up_weight.shape[1]
    ff_part = ff_width // dp_count
    both = ("dp", "depth")

    def half_of(values, axis, which):
        return lax.dynamic_slice_in_dim(values, which * width, width, axis)

    partners = jnp.stack([dp_at ^ m for m in range(dp_count)]).astype(jnp.int32)
    ff_local = ff_split(up_weight, down_weight, partners)
    ff_rows = [ff_local[0]] + [swap_mask(ff_local[m], "dp", m) for m in range(1, dp_count)]
    ff_rows = place_many(partners, ff_rows).reshape(2 * dp_count, own_rows, ff_part)

    small_cols = jnp.concatenate(
        [generator_in, norm_gains.T, jnp.zeros((own_rows, 128 - GEN - 5), bf16)], axis=1
    )
    small_all = gather_small(small_cols, both).reshape(model, 128)
    gen_first = small_all[:, :GEN]
    gen_first, ff_rows = fence(gen_first, ff_rows)
    gain_float = small_all[:, GEN : GEN + 5].astype(f32).T
    second_rows = generator_out.shape[0]
    second_pad = -second_rows % 128
    second_all = gather_small(jnp.pad(generator_out, (0, second_pad))[None], both)
    gen_second = second_all.reshape(-1, second_rows + second_pad)[:, :second_rows]
    second_low = gen_second.reshape(GEN, STREAMS * MIX)

    stacked = jnp.concatenate([query_weight, key_weight, value_weight, out_weight.T], axis=0)
    over_depth = lax.all_gather(stacked, "depth", axis=0, tiled=True)
    current_f = current.astype(f32)
    current_half = half_of(current, 1, model_at)
    mean_square = jnp.mean(current_f * current_f, axis=-1, keepdims=True)
    inverse_rms = lax.rsqrt(mean_square + RMS_EPSILON)
    unit = current_f * inverse_rms
    gen_normed = (unit * gain_float[4]).astype(bf16)
    gen_pre = dot_nn(gen_normed, gen_first)
    gen_hidden = gelu_exact(gen_pre).astype(bf16)
    column = jnp.arange(STREAMS * MIX)
    last_col = (column % MIX == MIX - 1).astype(f32)
    mixing = (dot_nn(gen_hidden, second_low) + last_col).astype(bf16)
    pick_last = (column[:, None] == (jnp.arange(128) * MIX + MIX - 1)[None, :]).astype(bf16)
    last = dot_nn(mixing, pick_last)

    layer_of = jnp.tile(slot_layer, STREAMS)
    stream_of = jnp.repeat(jnp.arange(STREAMS), slots)
    from_col = jnp.where(layer_of < MIX, stream_of * MIX + layer_of, -1)
    pick = (column[:, None] == from_col[None, :]).astype(f32)
    mix_all = gather_small(mixing, ("depth",)).reshape(depth_count * MB * rows_mb, STREAMS * MIX)
    slot_mix = dot_nn(mix_all, pick.astype(bf16))
    places_all = gather_small(positions, ("depth",))

    def over_depth_swap(values):
        return lax.all_to_all(values, "depth", 0, 0, tiled=True)

    def mix_part(micro_at, slot_mix):
        partial = mix_streams(slot_mix, history, micro_at, depth_count, rows_mb)
        return partial.reshape(STREAMS, depth_count, rows_mb, width)

    slot_mix, ff_rows, cotangent, places_all = fence(slot_mix, ff_rows, cotangent, places_all)
    partial = mix_part(0, slot_mix)
    partial_next = mix_part(1, slot_mix)

    weights_line = LineGather(ff_rows)
    weights_line.step()
    cot_pieces = lax.all_gather(cotangent, "dp", axis=0, tiled=True)
    over_depth, partial, partial_next = weights_line.hold(over_depth, partial, partial_next)
    pieces = [over_depth]
    weights = place_block(None, pieces[0][None], place_index(0), dp_count)
    hops_left = [(p, at) for at in range(len(dp_bits)) for p in range(1 << at)]
    placed = 1
    cots = None
    sums, sums_next = LineScatter(partial), LineScatter(partial_next)
    own_tables = turning_tables(positions)
    tables = [
        turning_tables(places_all[:, m * rows_mb : (m + 1) * rows_mb].reshape(length))
        for m in range(MB)
    ]
    for hop in range(1, depth_count):
        sums.step_with(weights_line)
        last_hop = hop == depth_count - 1
        for place in range(placed, len(pieces)):
            weights = place_block(weights, pieces[place][None], place_index(place), dp_count)
        placed = len(pieces)
        while hops_left:
            place, at = hops_left.pop(0)
            pieces.append(core_hop(pieces[place], at))
            if len(hops_left) <= depth_count - 1 - hop:
                break
        if last_hop:
            cot_full = join_halves(cotangent, other_core(cotangent), model_at)
            ff_weights = weights_line.placed()
            cots = cot_full, cotangent, ff_weights
        (state,) = weights_line.hold(
            (sums.up, sums.down, pieces, weights, cots, own_tables, tables, cot_pieces)
        )
        sums.up, sums.down, pieces, weights, cots, own_tables, tables, cot_pieces = state
    cot_full, cotangent, ff_weights = cots
    for place in range(placed, len(pieces)):
        weights = place_block(weights, pieces[place][None], place_index(place), dp_count)
    weights = weights.reshape(dp_count, depth_count, 4, own_rows, heads_width)
    ff_weights = ff_weights.reshape(2, dp_count, depth_count, own_rows, ff_part)

    document_view = doc_ids.reshape(depth_count, MB, rows_mb)
    which = model_at.astype(jnp.int32)[None]
    depth_at = lax.axis_index("depth").astype(jnp.int32)[None]
    gains = gain_float

    def enter(micro_at, sums):
        span = slice(micro_at * rows_mb, (micro_at + 1) * rows_mb)
        low, resid = total_streams(sums, current_half[span], last[span], depth_at)
        normed, ff_normed, stats = norm_streams(low, other_core(low), gains, which)
        packed = project_heads(
            normed,
            cot_full[span],
            weights,
            [t[span] for t in own_tables],
            depth_count,
        )
        return dict(
            low=low, resid=resid, normed=normed, ff_normed=ff_normed, stats=stats, packed=packed
        )

    def attention(micro_at, by_head):
        documents = document_view[:, micro_at].reshape(length)
        by_head = by_head.reshape(length, 4 * heads_each * HDIM)
        answer = attend(by_head, documents, tables[micro_at], heads_each)
        return answer.reshape(depth_count, rows_mb, 4 * heads_each * HDIM)

    place_list = jnp.stack([place_index(p) for p in range(dp_count)]).astype(jnp.int32)

    def group_rows(ff_normed):
        return lax.all_gather(ff_normed, "dp", axis=0, tiled=True)

    def group_joined(mine):
        return join_halves(mine, other_core(mine), model_at)

    def hidden_units(micro_at, group_normed):
        hidden, grad_up, own, other = feed_forward(
            group_normed, cot_group, micro_at, ff_weights, which
        )
        return dict(group_normed=group_normed, hidden=hidden, grad_up=grad_up), (own, other)

    def group_back_rest(near):
        for at in reversed(range(len(dp_bits) - 1)):
            half = 1 << at
            near = near[:half] + core_hop(near[half:].astype(bf16), at).astype(f32)
        return near[0]

    def group_back(own, other):
        near, far = group_split(own, other, place_list)
        return group_back_rest(near + core_hop(far, len(dp_bits) - 1).astype(f32))

    def back(kept, answer):
        (theirs,) = back_project(answer, weights, 1 - which, bf16, False)
        got = other_core(theirs)
        own, flat = back_project(answer, weights, which, f32, True)
        return own, got, flat

    def leave(micro_at, kept, own, got, ff_sum):
        span = slice(micro_at * rows_mb, (micro_at + 1) * rows_mb)
        rows = (kept["resid"] + own[0] + got[0].astype(f32) + ff_sum[1]).astype(bf16)
        low, stats = kept["low"], kept["stats"]
        scaled, sums, gain_part = norm_slopes(own, got, ff_sum, low, stats, gains, which)
        grad_low, current_mix, last_dot = stream_grads(
            scaled, sums, other_core(sums), low, stats, cotangent[span], current_half[span], last[span]
        )
        kept.update(layer_rows=rows, gain=gain_part, current_mix=current_mix, last_dot=last_dot)
        return grad_low

    ((sums.up, sums.down),) = sums_next.step((sums.up, sums.down))
    first = enter(0, sums)
    mine = group_rows(first["ff_normed"])
    packed, mine, cot_pieces = sums_next.hold(first["packed"], mine, cot_pieces)
    while sums_next.at < depth_count - 3:
        sums_next.step()
        sums_next.hold()
    packed, mine, cot_pieces = sums_next.step(packed, mine, cot_pieces)
    by_head = over_depth_swap(packed)
    cot_group = join_halves(cot_pieces, other_core(cot_pieces), model_at)
    cot_group = cot_group.reshape(dp_count, MB, rows_mb, model)
    kept, ff_parts = hidden_units(0, group_joined(mine))
    first.update(kept)
    by_head, ff_parts, cot_group = sums_next.hold(by_head, ff_parts, cot_group)
    by_head, ff_parts = sums_next.step(by_head, ff_parts)
    answer = attention(0, by_head)
    answer, ff_parts = sums_next.hold(answer, ff_parts)

    answer = over_depth_swap(answer)
    second = enter(1, sums_next)
    near, far = group_split(ff_parts[0], other_core(ff_parts[1]), place_list)
    near = near + core_hop(far, len(dp_bits) - 1).astype(f32)
    answer, packed, ff_normed, near = fence(
        answer, second["packed"], second["ff_normed"], near
    )
    by_head = over_depth_swap(packed)
    mine = group_rows(ff_normed)
    own, got, first["flat"] = back(first, answer)
    grad_low = leave(0, first, own, got, group_back_rest(near))
    by_head, grad_low, mine, first["layer_rows"] = fence(
        by_head, grad_low, mine, first["layer_rows"]
    )
    saved = [first, second]

    def each(name):
        return [s[name] for s in saved]

    def rows_of(name):
        return jnp.concatenate(each(name), axis=0)

    def place_grads(place, dtype):
        return attention_grads(
            each("normed"),
            cot_full,
            each("flat"),
            place_list[place : place + 1],
            depth_count,
            dp_count,
            dtype,
        )

    half = dp_count // 2
    hops_left = [
        (p, at) for at in reversed(range(len(dp_bits))) for p in range(1 << at, 2 << at)
    ]
    pieces = {}

    def sums_hop():
        place, at = hops_left.pop(0)
        arrived = core_hop(pieces.pop(place), at)
        target = place - (1 << at)
        pieces[target] = (pieces[target].astype(f32) + arrived.astype(f32)).astype(bf16)

    grad_line = LineGather(grad_low)
    grad_line.step()
    answer = attention(1, by_head)
    kept, ff_parts = hidden_units(1, group_joined(mine))
    second.update(kept)
    answer, ff_parts = grad_line.hold(answer, ff_parts)
    answer = over_depth_swap(answer)
    near, far = group_split(ff_parts[0], other_core(ff_parts[1]), place_list)
    ff_products = hidden_grads(
        each("group_normed"), cot_group, each("grad_up"), each("hidden"), dp_count, depth_count
    )
    near = near + core_hop(far, len(dp_bits) - 1).astype(f32)
    answer, near, ff_products = fence(answer, near, ff_products)

    ff_sums = LineScatter(ff_products)
    (answer,) = ff_sums.step_with(grad_line, answer)
    own, got, flat = back(second, answer)
    ff_sum = group_back_rest(near)
    second["flat"] = flat
    (state,) = grad_line.hold((ff_sums.up, ff_sums.down, own, got, flat, ff_sum))
    ff_sums.up, ff_sums.down, own, got, second["flat"], ff_sum = state
    while len(grad_line.up) < depth_count - 1:
        ff_sums.step_with(grad_line)
        (state,) = grad_line.hold((ff_sums.up, ff_sums.down))
        ff_sums.up, ff_sums.down = state
    (ff_sum,) = ff_sums.step_with(grad_line, ff_sum)
    grad_low = leave(1, second, own, got, ff_sum)
    pieces = {p: place_grads(p, bf16) for p in range(dp_count)}
    sums_hop()
    (state,) = grad_line.hold((ff_sums.up, ff_sums.down, grad_low, pieces))
    ff_sums.up, ff_sums.down, grad_low, pieces = state

    last_line = LineGather(grad_low)
    last_line.step()
    if hops_left:
        sums_hop()
    grad_first = grad_line.placed().reshape(STREAMS, length, width)
    history_grad, slot_part = unmix_streams(
        slot_mix, history, grad_first, 0, depth_count, rows_mb, None
    )
    slot_parts = [slot_part.reshape(depth_count, 1, rows_mb, 128)]
    pieces, history_grad, second["layer_rows"] = last_line.hold(
        pieces, history_grad, second["layer_rows"]
    )
    (pieces,) = ff_sums.step(pieces)
    while hops_left:
        sums_hop()
    (pieces,) = ff_sums.hold(pieces)
    out_sums = LineScatter(pieces[0].reshape(1, depth_count, 4 * own_rows, heads_width))
    for hop in range(2, depth_count):
        last_line.step()
        ((ff_sums.up, ff_sums.down),) = out_sums.step((ff_sums.up, ff_sums.down))
        if hop == depth_count - 1:
            ff_sums.up = ff_sums.down = end_sums(ff_sums, bf16)
            early = last_line.placed_early()
            history_grad, slot_part = unmix_streams(
                slot_mix,
                history,
                early.reshape(STREAMS, length, width),
                1,
                depth_count,
                rows_mb,
                history_grad,
            )
        (state,) = last_line.hold(
            (out_sums.up, out_sums.down, ff_sums.up, ff_sums.down, history_grad, slot_part)
        )
        out_sums.up, out_sums.down, ff_sums.up, ff_sums.down, history_grad, slot_part = state
    early, ff_grads = out_sums.step(early, ff_sums.up)
    ff_grads = ff_grads.reshape(2, dp_count, own_rows, ff_part)
    ff_pieces = [
        lax.dynamic_index_in_dim(ff_grads, partners[m], 1, keepdims=False) for m in range(dp_count)
    ]
    ff_pieces = ff_pieces[:1] + [swap_mask(ff_pieces[m], "dp", m) for m in range(1, dp_count)]
    far_grads, far_index = last_line.farthest(early)
    history_grad, far_part = unmix_one(
        slot_mix, history, far_grads, 1, far_index, rows_mb, history_grad
    )
    slot_part = slot_part.reshape(depth_count, rows_mb, 128)
    slot_part = lax.dynamic_update_index_in_dim(slot_part, far_part, far_index, 0)
    slot_parts.append(slot_part[:, None])

    slot_grads = jnp.concatenate(slot_parts, axis=1).reshape(-1, 128)[:, : STREAMS * slots]
    mix_grads = dot_exact(slot_grads, pick.T).reshape(depth_count, MB * rows_mb, STREAMS * MIX)
    mix_grads, ff_pieces = out_sums.hold(mix_grads, ff_pieces)
    grad_mixing = scatter_small(mix_grads, ("depth",))
    up_grad, down_grad = ff_join(jnp.stack(ff_pieces), partners)
    last_dots = rows_of("last_dot")
    grad_mixing = grad_mixing + dot_exact(last_dots, pick_last.astype(f32).T)
    grad_mixing = grad_mixing + other_core(grad_mixing)

    second_float = second_low.astype(f32)
    grad_second = dot_exact(gen_hidden.astype(f32).T, grad_mixing)
    grad_pre = dot_exact(grad_mixing, second_float.T) * gelu_slope(gen_pre)
    grad_first = dot_exact(gen_normed.astype(f32).T, grad_pre)
    grad_gen_normed = dot_exact(grad_pre, gen_first.astype(f32).T)
    gain_gen = jnp.sum(grad_gen_normed * unit, axis=0)
    scattered = end_sums(out_sums, f32).reshape(4, own_rows, heads_width)
    grad_unit = grad_gen_normed * gain_float[4]
    shared = jnp.mean(grad_unit * unit, axis=-1, keepdims=True)
    current_gen = half_of(inverse_rms * (grad_unit - unit * shared), 1, model_at)
    current_grad = rows_of("current_mix") + current_gen

    gain_own = sum(s["gain"] for s in saved)
    gain_other = other_core(gain_own)
    gain_all = jnp.where(
        model_at == 0,
        jnp.concatenate([gain_own, gain_other], axis=1),
        jnp.concatenate([gain_other, gain_own], axis=1),
    )
    gain_all = jnp.concatenate([gain_all, gain_gen[None]], axis=0)
    small_grads = jnp.concatenate(
        [grad_first, gain_all.T, jnp.zeros((model, 128 - GEN - 5), f32)], axis=1
    )
    small_grads = scatter_small(small_grads.reshape(-1, own_rows, 128), both)
    second_grads = jnp.pad(grad_second.reshape(-1, second_rows), ((0, 0), (0, second_pad)))
    second_grads = scatter_small(second_grads[:, None], both)

    return (
        rows_of("layer_rows"),
        history_grad,
        current_grad,
        small_grads[:, GEN : GEN + 5].T,
        small_grads[:, :GEN],
        second_grads[0, :second_rows],
        scattered[0],
        scattered[1],
        scattered[2],
        scattered[3].T,
        up_grad,
        down_grad,
    )


def solution(mesh):
    return jax.shard_map(
        local,
        mesh=mesh,
        in_specs=(
            P("depth", "dp", "mp"),
            P("depth"),
            P(("dp", "depth"), None),
            P(("dp", "depth")),
            P("dp"),
            P(("dp", "depth"), "mp"),
            P(None, ("dp", "depth")),
            P(("dp", "depth"), None),
            P(("dp", "depth")),
            P(("dp", "depth"), "mp"),
            P(("dp", "depth"), "mp"),
            P(("dp", "depth"), "mp"),
            P("mp", ("dp", "depth")),
            P(("dp", "depth"), "mp"),
            P("mp", ("dp", "depth")),
        ),
        out_specs=(
            P(("dp", "depth"), "mp"),
            P("depth", "dp", "mp"),
            P(("dp", "depth"), "mp"),
            P(None, ("dp", "depth")),
            P(("dp", "depth"), None),
            P(("dp", "depth")),
            P(("dp", "depth"), "mp"),
            P(("dp", "depth"), "mp"),
            P(("dp", "depth"), "mp"),
            P("mp", ("dp", "depth")),
            P(("dp", "depth"), "mp"),
            P("mp", ("dp", "depth")),
        ),
        check_vma=False,
    )
```

```python
import functools
import math

import jax
import jax.numpy as jnp
from jax import lax
from jax.experimental import pallas as pl
from jax.experimental.pallas import tpu as pltpu
from jax.sharding import PartitionSpec as P

HDIM = 128
ROT = 32
GEN = 72
MB = 2
MIX = 18
STREAMS = 4
COST = 20

PRECISE = lax.Precision.HIGHEST
NORM_EPSILON = 1e-05
RMS_EPSILON = 1e-06
MASKED = -1e30

bf16 = jnp.bfloat16
f32 = jnp.float32


def dot_nn(a, b):
    return lax.dot_general(a, b, (((1,), (0,)), ((), ())), preferred_element_type=f32)


def dot_nt(a, b):
    return lax.dot_general(a, b, (((1,), (1,)), ((), ())), preferred_element_type=f32)


def dot_tn(a, b):
    return lax.dot_general(a, b, (((0,), (0,)), ((), ())), preferred_element_type=f32)


def dot_exact(a, b):
    return jnp.dot(a, b, precision=PRECISE, preferred_element_type=f32)


def gelu_exact(values):
    return jax.nn.gelu(values, approximate=False)


def gelu_slope(values):
    result, pullback = jax.vjp(gelu_exact, values)
    return pullback(jnp.ones_like(result))[0]


def bit_count(size):
    count = size.bit_length() - 1
    assert 1 << count == size
    return count


def swap_mask(values, axis, mask):
    size = lax.axis_size(axis)
    return lax.ppermute(values, axis, [(i, i ^ mask) for i in range(size)])


def gather_masked(values, axis, order):
    pieces = {0: values}
    for bit in order:
        arrived = {m | (1 << bit): swap_mask(v, axis, 1 << bit) for m, v in pieces.items()}
        pieces.update(arrived)
    return [pieces[m] for m in range(len(pieces))]


def scatter_masked(pieces, axis, order, link=bf16):
    pieces = dict(enumerate(pieces))
    for bit in order:
        flag = 1 << bit
        for m in [m for m in pieces if m & flag]:
            arrived = swap_mask(pieces.pop(m).astype(link), axis, flag)
            pieces[m ^ flag] = pieces[m ^ flag].astype(f32) + arrived.astype(f32)
    return pieces[0]


def core_orders():
    bits = list(range(bit_count(lax.axis_size("dp"))))
    return bits, bits[1:] + bits[:1]


def place_mask(place):
    masks = []
    for order in core_orders():
        masks.append(sum(1 << bit for at, bit in enumerate(order) if (place >> at) & 1))
    return jnp.where(lax.axis_index("mp") % 2 == 0, masks[0], masks[1])


def place_index(place):
    return lax.axis_index("dp") ^ place_mask(place)


def core_hop(values, at):
    orders, cores = core_orders(), lax.axis_size("mp")
    pairs = []
    for i in range(lax.axis_size("dp")):
        for core in range(cores):
            partner = i ^ (1 << orders[core % 2][at])
            pairs.append((i * cores + core, partner * cores + core))
    return lax.ppermute(values, ("dp", "mp"), pairs)


def group_hop(pieces, at):
    return jnp.concatenate([pieces, core_hop(pieces, at)], axis=0)


def place_of(core):
    partner = jnp.arange(lax.axis_size("dp")) ^ lax.axis_index("dp")
    places = []
    for order in core_orders():
        places.append(sum(((partner >> bit) & 1) << at for at, bit in enumerate(order)))
    return jnp.where(core % 2 == 0, places[0], places[1])


def reorder_masked(stacked, axis):
    count = bit_count(stacked.shape[0])
    here = lax.axis_index(axis)
    shape = stacked.shape
    values = stacked.reshape((2,) * count + shape[1:])
    for bit in range(count):
        turned = jnp.flip(values, count - 1 - bit)
        values = jnp.where(((here >> bit) & 1) == 1, turned, values)
    return values.reshape(shape)


def gather_small(values, axes):
    shape = values.shape
    values = values[None]
    for axis in reversed(axes):
        order = range(bit_count(lax.axis_size(axis)))
        stacked = jnp.stack(gather_masked(values, axis, order))
        values = reorder_masked(stacked, axis)
        values = values.reshape((-1,) + shape)
    return values


def scatter_small(values, axes):
    for axis in axes:
        size = lax.axis_size(axis)
        values = values.reshape((size, values.shape[0] // size) + values.shape[1:])
        turned = reorder_masked(values, axis)
        order = reversed(range(bit_count(size)))
        values = scatter_masked([turned[m] for m in range(size)], axis, order, f32)
    return values[0]


def line_size():
    return lax.axis_size("depth"), lax.axis_index("depth")


def fence(*values):
    return lax.optimization_barrier(values)


class LineGather:

    def __init__(self, values):
        self.up, self.down = [values], [values]

    def step(self):
        size, _ = line_size()
        at = len(self.up)
        if at < size:
            up_pairs = [(i, i + 1) for i in range(at - 1, size - 1)]
            down_pairs = [(i, i - 1) for i in range(1, size - at + 1)]
            self.up.append(lax.ppermute(self.up[-1], "depth", up_pairs))
            self.down.append(lax.ppermute(self.down[-1], "depth", down_pairs))

    def hold(self, *others):
        kept = fence((self.up[1:], self.down[1:]), *others)
        (up, down), rest = kept[0], kept[1:]
        self.up, self.down = self.up[:1] + list(up), self.down[:1] + list(down)
        return rest

    def placed_early(self):
        size, here = line_size()
        steps = jnp.arange(size)
        index = lax.rem(here - steps + size, size)
        own = self.up[0]
        blocks = self.up[: size - 1] + [own]
        instead = [own] + self.down[1 : size - 1][::-1]
        return place_line(index, here >= steps, blocks, instead)

    def farthest(self, early):
        size, here = line_size()
        last = jnp.where(here == size - 1, self.up[size - 1], early[:, 0])
        return jnp.where(here == 0, self.down[size - 1], last), jnp.where(here == 0, size - 1, 0)

    def placed(self):
        size, here = line_size()
        steps = jnp.arange(size)
        index = lax.rem(here - steps + size, size)
        return place_line(index, here >= steps, self.up, self.down[1:][::-1])


class LineScatter:

    def __init__(self, terms):
        self.terms, self.at = terms, 0
        self.up = self.down = None

    def step(self, *later):
        size, here = line_size()
        self.at += 1
        if self.at >= size:
            return later
        goes_up, goes_down = hop_sums(
            self.terms,
            jnp.minimum(size - self.at + here, size - 1),
            jnp.maximum(here - size + self.at, 0),
            self.up,
            self.down,
            [here < self.at, here > size - 1 - self.at],
        )
        (goes_up, goes_down), *later = fence((goes_up, goes_down), *later)
        up_pairs = [(i, i + 1) for i in range(min(self.at, size - 1))]
        down_pairs = [(size - 1 - i, size - 2 - i) for i in range(min(self.at, size - 1))]
        self.up = lax.ppermute(goes_up, "depth", up_pairs)
        self.down = lax.ppermute(goes_down, "depth", down_pairs)
        return later

    def step_with(self, line, *later):
        size, here = line_size()
        lead, _, tall, wide = self.terms.shape
        shape = line.up[0].shape
        if (
            len(line.up) != self.at + 2
            or self.at + 2 > size - 1
            or math.prod(shape) != lead * tall * wide
            or shape[2] != wide
        ):
            line.step()
            return self.step(*later)
        self.at += 1
        goes = hop_sums(
            self.terms,
            jnp.minimum(size - self.at + here, size - 1),
            jnp.maximum(here - size + self.at, 0),
            self.up,
            self.down,
            [here < self.at, here > size - 1 - self.at],
            [v[-1].reshape(lead, tall, wide) for v in (line.up, line.down)],
        )
        goes, *later = fence(goes, *later)
        self.up = lax.ppermute(goes[0], "depth", [(i, i + 1) for i in range(size - 1)])
        self.down = lax.ppermute(goes[1], "depth", [(i, i - 1) for i in range(1, size)])
        line.up.append(self.up.reshape(shape))
        line.down.append(self.down.reshape(shape))
        return later

    def hold(self, *others):
        (self.up, self.down), *rest = fence((self.up, self.down), *others)
        return rest


def other_core(values):
    return swap_mask(values, "mp", 1)


def join_kernel(model_ref, own_ref, other_ref, out_ref):
    width = own_ref.shape[1]
    own_at = pl.multiple_of(model_ref[0] * width, width)
    other_at = pl.multiple_of((1 - model_ref[0]) * width, width)
    out_ref[:, pl.ds(own_at, width)] = own_ref[...]
    out_ref[:, pl.ds(other_at, width)] = other_ref[...]


def join_halves(own, other, model_at):
    tall, width = own.shape
    rows = min(256, tall)
    return pl.pallas_call(
        join_kernel,
        grid_spec=pltpu.PrefetchScalarGridSpec(
            num_scalar_prefetch=1,
            grid=(tall // rows,),
            in_specs=[pl.BlockSpec((rows, width), lambda i, m: (i, 0))] * 2,
            out_specs=pl.BlockSpec((rows, 2 * width), lambda i, m: (i, 0)),
        ),
        out_shape=jax.ShapeDtypeStruct((tall, 2 * width), own.dtype),
        cost_estimate=spent(
            flops=0, bytes_accessed=8 * tall * width, transcendentals=0
        ),
        name="join_halves",
    )(model_at.astype(jnp.int32)[None], own, other)


def spent(flops, bytes_accessed, transcendentals):
    return pl.CostEstimate(
        flops=flops // COST, bytes_accessed=bytes_accessed // COST, transcendentals=transcendentals // COST
    )


def chunk_of(tall, wide, most=1 << 19):
    rows = tall
    while rows * wide > most and rows % 32 == 0:
        rows //= 2
    return rows


def place_kernel(at_ref, *refs):
    if len(refs) < 4:
        refs[-1][0, 0] = refs[0][0]
        return

    @pl.when(at_ref[1] == 1)
    def _():
        refs[-1][0, 0] = refs[0][0]

    @pl.when(at_ref[1] == 0)
    def _():
        refs[-1][0, 0] = refs[1][0]


def place_block(buffer, block, index, count, instead=None, first=None):
    lead, tall, wide = block.shape
    rows = chunk_of(tall, wide)
    spec = pl.BlockSpec((1, rows, wide), lambda l, i, m: (l, i, 0))
    blocks = [block] if instead is None else [block, instead]
    where = [index, 1 if first is None else first]
    where = jnp.stack([jnp.asarray(v).astype(jnp.int32) for v in where])
    in_specs, operands, aliases = [spec] * len(blocks), list(blocks), {}
    if buffer is not None or instead is not None:
        in_specs.append(pl.BlockSpec(memory_space=pl.ANY))
        operands.append(block if buffer is None else buffer)
        aliases = {} if buffer is None else {len(operands): 0}
    return pl.pallas_call(
        place_kernel,
        grid_spec=pltpu.PrefetchScalarGridSpec(
            num_scalar_prefetch=1,
            grid=(lead, tall // rows),
            in_specs=in_specs,
            out_specs=pl.BlockSpec((1, 1, rows, wide), lambda l, i, m: (l, m[0], i, 0)),
        ),
        out_shape=jax.ShapeDtypeStruct((lead, count, tall, wide), block.dtype),
        input_output_aliases=aliases,
        cost_estimate=spent(
            flops=0, bytes_accessed=4 * lead * tall * wide, transcendentals=0
        ),
        name="place_block",
    )(where, *operands)


def place_line_kernel(size, at_ref, *refs):
    out_ref = refs[-1]
    for step in range(size):
        if step == 0 or len(refs) == size + 1:
            out_ref[0, at_ref[step]] = refs[step][0]
            continue

        @pl.when(at_ref[size + step] == 1)
        def _(step=step):
            out_ref[0, at_ref[step]] = refs[step][0]

        @pl.when(at_ref[size + step] == 0)
        def _(step=step):
            out_ref[0, at_ref[step]] = refs[size + step - 1][0]


def place_line(index, first, blocks, instead):
    size = len(blocks)
    lead, tall, wide = blocks[0].shape
    rows = tall
    while rows * wide > 1 << 18 and rows % 32 == 0:
        rows //= 2
    spec = pl.BlockSpec((1, rows, wide), lambda l, i, m: (l, i, 0))
    where = jnp.concatenate([index, first]).astype(jnp.int32)
    operands = list(blocks) + list(instead)
    return pl.pallas_call(
        functools.partial(place_line_kernel, size),
        grid_spec=pltpu.PrefetchScalarGridSpec(
            num_scalar_prefetch=1,
            grid=(lead, tall // rows),
            in_specs=[spec] * len(operands),
            out_specs=pl.BlockSpec((1, size, rows, wide), lambda l, i, m: (l, 0, i, 0)),
        ),
        out_shape=jax.ShapeDtypeStruct((lead, size, tall, wide), blocks[0].dtype),
        compiler_params=pltpu.CompilerParams(vmem_limit_bytes=40 << 20),
        cost_estimate=spent(
            flops=0, bytes_accessed=6 * size * lead * tall * wide, transcendentals=0
        ),
        name="place_line",
    )(where, *operands)


def place_many(index, blocks):
    ones = jnp.ones(len(blocks), jnp.int32)
    return place_line(index, ones, blocks, [])


def group_join_kernel(at_ref, own_ref, other_ref, out_ref):
    width = own_ref.shape[2]
    own_span, other_span = own_spans(at_ref, width)
    out_ref[:, own_span] = own_ref[0]
    out_ref[:, other_span] = other_ref[0]


def group_join(own, other, model_at):
    count, tall, width = own.shape
    rows = chunk_of(tall, width)
    per = tall // rows
    where = jnp.concatenate([model_at[None], place_of(model_at), place_of(1 - model_at)])
    return pl.pallas_call(
        group_join_kernel,
        grid_spec=pltpu.PrefetchScalarGridSpec(
            num_scalar_prefetch=1,
            grid=(count, per),
            in_specs=[
                pl.BlockSpec((1, rows, width), lambda n, i, m: (m[1 + n], i, 0)),
                pl.BlockSpec((1, rows, width), lambda n, i, m: (m[1 + count + n], i, 0)),
            ],
            out_specs=pl.BlockSpec((rows, 2 * width), lambda n, i, m: (n * per + i, 0)),
        ),
        out_shape=jax.ShapeDtypeStruct((count * tall, 2 * width), own.dtype),
        cost_estimate=spent(
            flops=0, bytes_accessed=8 * count * tall * width, transcendentals=0
        ),
        name="group_join",
    )(where.astype(jnp.int32), own, other)


def group_split_kernel(at_ref, near_own, near_other, far_own, far_other, near_ref, far_ref):
    near_ref[0, 0] = near_own[0] + near_other[0].astype(f32)
    far_ref[0, 0] = (far_own[0] + far_other[0].astype(f32)).astype(bf16)


def group_split(own, other, places):
    _, tall, width = own.shape
    count = places.shape[0]
    half, rows = count // 2, tall // count
    near = pl.BlockSpec((1, rows, width), lambda p, k, m: (k, m[p], 0))
    far = pl.BlockSpec((1, rows, width), lambda p, k, m: (k, m[half + p], 0))
    out = pl.BlockSpec((1, 1, rows, width), lambda p, k, m: (p, k, 0, 0))
    return pl.pallas_call(
        group_split_kernel,
        grid_spec=pltpu.PrefetchScalarGridSpec(
            num_scalar_prefetch=1,
            grid=(half, 2),
            in_specs=[near, near, far, far],
            out_specs=[out, out],
        ),
        out_shape=[
            jax.ShapeDtypeStruct((half, 2, rows, width), f32),
            jax.ShapeDtypeStruct((half, 2, rows, width), bf16),
        ],
        cost_estimate=spent(
            flops=2 * tall * width, bytes_accessed=20 * tall * width, transcendentals=0
        ),
        name="group_split",
    )(places, own, other, own, other)


def hop_kernel(has_sums, has_blocks, at_ref, *refs):
    ins, outs = list(refs[:-2]), refs[-2:]
    terms, ins = ins[:2], ins[2:]
    sums, ins = (ins[:2], ins[2:]) if has_sums else (None, ins)

    def send_sum(way):
        term = terms[way][0, 0].astype(f32)
        if sums is not None:
            term = term + sums[way][0].astype(f32)
        outs[way][0] = term.astype(bf16)

    for way in range(2):
        if not has_blocks:
            send_sum(way)
            continue
        pl.when(at_ref[2 + way] == 1)(functools.partial(send_sum, way))

        @pl.when(at_ref[2 + way] == 0)
        def _(way=way):
            outs[way][0] = ins[way][0]


def hop_sums(terms, up_at, down_at, up, down, sends, blocks=None):
    lead, _, tall, wide = terms.shape
    rows = chunk_of(tall, wide, 1 << 17)
    block = pl.BlockSpec((1, rows, wide), lambda l, i, m: (l, i, 0))

    def term_spec(way):
        return pl.BlockSpec(
            (1, 1, rows, wide), lambda l, i, m: (l * m[2 + way], m[way], i * m[2 + way], 0)
        )

    def block_spec(way, sign):
        def index(l, i, m):
            need = m[2 + way] if sign else 1 - m[2 + way]
            return (l * need, i * need, 0)

        return pl.BlockSpec((1, rows, wide), index)

    in_specs = [term_spec(0), term_spec(1)]
    operands = [terms, terms]
    if up is not None:
        in_specs += [block_spec(0, True), block_spec(1, True)]
        operands += [up, down]
    if blocks is not None:
        in_specs += [block_spec(0, False), block_spec(1, False)]
        operands += list(blocks)
    return pl.pallas_call(
        functools.partial(hop_kernel, up is not None, blocks is not None),
        grid_spec=pltpu.PrefetchScalarGridSpec(
            num_scalar_prefetch=1,
            grid=(lead, tall // rows),
            in_specs=in_specs,
            out_specs=[block, block],
        ),
        out_shape=[jax.ShapeDtypeStruct((lead, tall, wide), bf16)] * 2,
        cost_estimate=spent(
            flops=2 * lead * tall * wide, bytes_accessed=12 * lead * tall * wide, transcendentals=0
        ),
        name="hop_sums",
    )(jnp.stack([up_at, down_at, *sends]).astype(jnp.int32), *operands)


def end_kernel(at_ref, term_ref, up_ref, down_ref, out_ref):
    total = term_ref[0, 0].astype(f32) + up_ref[0].astype(f32) + down_ref[0].astype(f32)
    out_ref[0] = total.astype(out_ref.dtype)


def end_sums(sums, dtype):
    lead, _, tall, wide = sums.terms.shape
    rows = chunk_of(tall, wide)
    block = pl.BlockSpec((1, rows, wide), lambda l, i, m: (l, i, 0))
    return pl.pallas_call(
        end_kernel,
        grid_spec=pltpu.PrefetchScalarGridSpec(
            num_scalar_prefetch=1,
            grid=(lead, tall // rows),
            in_specs=[
                pl.BlockSpec((1, 1, rows, wide), lambda l, i, m: (l, m[0], i, 0)),
                block,
                block,
            ],
            out_specs=block,
        ),
        out_shape=jax.ShapeDtypeStruct((lead, tall, wide), dtype),
        cost_estimate=spent(
            flops=2 * lead * tall * wide, bytes_accessed=10 * lead * tall * wide, transcendentals=0
        ),
        name="end_sums",
    )(lax.axis_index("depth").astype(jnp.int32)[None], sums.terms, sums.up, sums.down)


def attention_grad_kernel(
    at_ref, x0_ref, x1_ref, cot_ref, g0_ref, g1_ref, out_ref
):
    tall = x0_ref.shape[1]

    def store(total):
        out_ref[...] = total.reshape(out_ref.shape).astype(out_ref.dtype)

    @pl.when(pl.program_id(0) < 3)
    def _():
        store(dot_tn(x0_ref[0], g0_ref[0]) + dot_tn(x1_ref[0], g1_ref[0]))

    @pl.when(pl.program_id(0) == 3)
    def _():
        store(
            dot_tn(cot_ref[0:tall, :], g0_ref[0]) + dot_tn(cot_ref[tall : 2 * tall, :], g1_ref[0])
        )


def attention_grads(normed, cot, flat, place, depth_count, dp_count, dtype):
    _, tall, model = normed[0].shape
    heads_width = flat[0].shape[2]
    block = model // dp_count
    own_rows = block // depth_count
    normed_spec = pl.BlockSpec((1, tall, block), lambda k, m: (jnp.minimum(k, 2), 0, m[0]))
    flat_spec = pl.BlockSpec((1, tall, heads_width), lambda k, m: (lax.rem(k + 1, 4), 0, 0))
    return pl.pallas_call(
        attention_grad_kernel,
        grid_spec=pltpu.PrefetchScalarGridSpec(
            num_scalar_prefetch=1,
            grid=(4,),
            in_specs=[
                normed_spec,
                normed_spec,
                pl.BlockSpec((2 * tall, block), lambda k, m: (0, m[0])),
                flat_spec,
                flat_spec,
            ],
            out_specs=pl.BlockSpec(
                (depth_count, 1, own_rows, heads_width), lambda k, m: (0, k, 0, 0)
            ),
        ),
        out_shape=jax.ShapeDtypeStruct((depth_count, 4, own_rows, heads_width), dtype),
        compiler_params=pltpu.CompilerParams(vmem_limit_bytes=40 << 20),
        cost_estimate=spent(
            flops=16 * tall * block * heads_width,
            bytes_accessed=16 * block * heads_width,
            transcendentals=0,
        ),
        name="attention_grads",
    )(place, *normed, cot, *flat)


def hidden_grad_kernel(x0_ref, x1_ref, c0_ref, c1_ref, u0_ref, u1_ref, h0_ref, h1_ref, out_ref):
    def store(total):
        out_ref[...] = total.reshape(out_ref.shape).astype(bf16)

    @pl.when(pl.program_id(0) == 0)
    def _():
        store(dot_tn(x0_ref[...], u0_ref[...]) + dot_tn(x1_ref[...], u1_ref[...]))

    @pl.when(pl.program_id(0) == 1)
    def _():
        tall, wide = h0_ref.shape[0], c0_ref.shape[3]
        c0, c1 = c0_ref[:, 0].reshape(tall, wide), c1_ref[:, 0].reshape(tall, wide)
        store(dot_tn(c0, h0_ref[...]) + dot_tn(c1, h1_ref[...]))


def hidden_grads(x, cot, up_grads, hidden, dp_count, depth_count):
    tall, model = x[0].shape
    part = hidden[0].shape[1]
    block = model // dp_count
    cols = pl.BlockSpec((tall, block), lambda k, n: (0, n * (1 - k)))
    whole = pl.BlockSpec((tall, part), lambda k, n: (0, 0))
    return pl.pallas_call(
        hidden_grad_kernel,
        grid=(2, dp_count),
        in_specs=[cols, cols]
        + [
            pl.BlockSpec((dp_count, 1, cot.shape[2], block), lambda k, n: (0, 0, 0, n * k)),
            pl.BlockSpec((dp_count, 1, cot.shape[2], block), lambda k, n: (0, 1, 0, n * k)),
        ]
        + [whole] * 4,
        out_specs=pl.BlockSpec(
            (1, depth_count, block // depth_count, part), lambda k, n: (k * dp_count + n, 0, 0, 0)
        ),
        out_shape=jax.ShapeDtypeStruct(
            (2 * dp_count, depth_count, block // depth_count, part), bf16
        ),
        compiler_params=pltpu.CompilerParams(vmem_limit_bytes=48 << 20),
        cost_estimate=spent(
            flops=8 * tall * model * part, bytes_accessed=8 * model * part, transcendentals=0
        ),
        name="hidden_grads",
    )(*x, cot, cot, *up_grads, *hidden)


def mix_kernel(slots, mix_ref, hist_ref, out_ref):
    rows, width = hist_ref.shape[1], hist_ref.shape[2]
    part = 512 if width % 512 == 0 else width

    def step(at, carry):
        r0 = pl.multiple_of(at * 16, 16)
        weights = mix_ref[pl.ds(r0, 16), :]
        for c0 in range(0, width, part):
            sums = [None] * STREAMS
            for k in range(slots):
                state = hist_ref[k, pl.ds(r0, 16), c0 : c0 + part].astype(f32)
                for s in range(STREAMS):
                    term = weights[:, s * slots + k : s * slots + k + 1] * state
                    sums[s] = term if sums[s] is None else sums[s] + term
            for s in range(STREAMS):
                out_ref[s, pl.ds(r0, 16), c0 : c0 + part] = sums[s].astype(bf16)
        return carry

    lax.fori_loop(0, rows // 16, step, 0)


def mix_streams(slot_mix, history, micro_at, depth_count, rows_mb):
    slots, _, width = history.shape
    rows = min(128, rows_mb)
    per = rows_mb // rows

    def row_block(i):
        return ((i // per) * MB + micro_at) * per + i % per

    return pl.pallas_call(
        functools.partial(mix_kernel, slots),
        grid=(depth_count * per,),
        in_specs=[
            pl.BlockSpec((rows, slot_mix.shape[1]), lambda i: (row_block(i), 0)),
            pl.BlockSpec((slots, rows, width), lambda i: (0, row_block(i), 0)),
        ],
        out_specs=pl.BlockSpec((STREAMS, rows, width), lambda i: (0, i, 0)),
        out_shape=jax.ShapeDtypeStruct((STREAMS, depth_count * rows_mb, width), bf16),
        cost_estimate=spent(
            flops=2 * slots * STREAMS * depth_count * rows_mb * width,
            bytes_accessed=2 * (slots + STREAMS) * depth_count * rows_mb * width,
            transcendentals=0,
        ),
        name="mix_streams",
    )(slot_mix, history)


def unmix_kernel(slots, mix_ref, hist_ref, grad_ref, *rest):
    hist_grad_ref, slot_grad_ref = rest[-2:]
    rows, width = hist_ref.shape[1], hist_ref.shape[2]
    part = 512 if width % 512 == 0 else width

    def step(at, carry):
        r0 = pl.multiple_of(at * 16, 16)
        weights = mix_ref[pl.ds(r0, 16), :]
        totals = [None] * (STREAMS * slots)
        for c0 in range(0, width, part):
            grads = [
                grad_ref[s, pl.ds(r0, 16), c0 : c0 + part].astype(f32)
                for s in range(STREAMS)
            ]
            for k in range(slots):
                state = hist_ref[k, pl.ds(r0, 16), c0 : c0 + part].astype(f32)
                back = None
                for s in range(STREAMS):
                    at_sk = s * slots + k
                    term = weights[:, at_sk : at_sk + 1] * grads[s]
                    back = term if back is None else back + term
                    product = state * grads[s]
                    folded = product[:, 0:128]
                    for l0 in range(128, part, 128):
                        folded = folded + product[:, l0 : l0 + 128]
                    totals[at_sk] = folded if totals[at_sk] is None else totals[at_sk] + folded
                hist_grad_ref[k, pl.ds(r0, 16), c0 : c0 + part] = back.astype(bf16)
        lane = lax.broadcasted_iota(jnp.int32, (16, 128), 1)
        packed = jnp.zeros((16, 128), f32)
        for at_sk in range(STREAMS * slots):
            column = jnp.sum(totals[at_sk], axis=1, keepdims=True)
            packed = jnp.where(lane == at_sk, column, packed)
        slot_grad_ref[pl.ds(r0, 16), :] = packed
        return carry

    lax.fori_loop(0, rows // 16, step, 0)


def unmix_streams(slot_mix, history, grads, micro_at, depth_count, rows_mb, earlier):
    slots, tokens, width = history.shape
    rows = min(128, rows_mb)
    per = rows_mb // rows

    def row_block(i):
        return ((i // per) * MB + micro_at) * per + i % per

    in_specs = [
        pl.BlockSpec((rows, slot_mix.shape[1]), lambda i: (row_block(i), 0)),
        pl.BlockSpec((slots, rows, width), lambda i: (0, row_block(i), 0)),
        pl.BlockSpec((STREAMS, rows, width), lambda i: (0, i, 0)),
    ]
    operands = [slot_mix, history, grads]
    aliases = {}
    if earlier is not None:
        in_specs.append(pl.BlockSpec(memory_space=pl.ANY))
        operands.append(earlier)
        aliases = {3: 0}
    return pl.pallas_call(
        functools.partial(unmix_kernel, slots),
        grid=(depth_count * per,),
        in_specs=in_specs,
        out_specs=[
            pl.BlockSpec((slots, rows, width), lambda i: (0, row_block(i), 0)),
            pl.BlockSpec((rows, 128), lambda i: (i, 0)),
        ],
        out_shape=[
            jax.ShapeDtypeStruct((slots, tokens, width), bf16),
            jax.ShapeDtypeStruct((depth_count * rows_mb, 128), f32),
        ],
        input_output_aliases=aliases,
        cost_estimate=spent(
            flops=4 * slots * STREAMS * depth_count * rows_mb * width,
            bytes_accessed=2 * (2 * slots + STREAMS) * depth_count * rows_mb * width,
            transcendentals=0,
        ),
        name="unmix_streams",
    )(*operands)


def unmix_one(slot_mix, history, grads, micro_at, index, rows_mb, earlier):
    slots, tokens, width = history.shape
    rows = min(128, rows_mb)
    per = rows_mb // rows

    def row_block(i, m):
        return (m[0] * MB + micro_at) * per + i

    def kernel(at_ref, *refs):
        unmix_kernel(slots, *refs)

    return pl.pallas_call(
        kernel,
        grid_spec=pltpu.PrefetchScalarGridSpec(
            num_scalar_prefetch=1,
            grid=(per,),
            in_specs=[
                pl.BlockSpec((rows, slot_mix.shape[1]), lambda i, m: (row_block(i, m), 0)),
                pl.BlockSpec((slots, rows, width), lambda i, m: (0, row_block(i, m), 0)),
                pl.BlockSpec((STREAMS, rows, width), lambda i, m: (0, i, 0)),
                pl.BlockSpec(memory_space=pl.ANY),
            ],
            out_specs=[
                pl.BlockSpec((slots, rows, width), lambda i, m: (0, row_block(i, m), 0)),
                pl.BlockSpec((rows, 128), lambda i, m: (i, 0)),
            ],
        ),
        out_shape=[
            jax.ShapeDtypeStruct((slots, tokens, width), bf16),
            jax.ShapeDtypeStruct((rows_mb, 128), f32),
        ],
        input_output_aliases={4: 0},
        cost_estimate=spent(
            flops=4 * slots * STREAMS * rows_mb * width,
            bytes_accessed=2 * (2 * slots + STREAMS) * rows_mb * width,
            transcendentals=0,
        ),
        name="unmix_one",
    )(index.astype(jnp.int32)[None], slot_mix, history, grads, earlier)


def own_spans(model_ref, width):
    own_at = pl.multiple_of(model_ref[0] * width, width)
    other_at = pl.multiple_of((1 - model_ref[0]) * width, width)
    return pl.ds(own_at, width), pl.ds(other_at, width)


def ff_split_kernel(at_ref, up_ref, down_ref, out_ref):
    out_ref[0, 0] = up_ref[...]
    out_ref[0, 1] = down_ref[...].T


def ff_split(up_weight, down_weight, partners):
    own_rows, ff_width = up_weight.shape
    count = partners.shape[0]
    part = ff_width // count
    return pl.pallas_call(
        ff_split_kernel,
        grid_spec=pltpu.PrefetchScalarGridSpec(
            num_scalar_prefetch=1,
            grid=(count,),
            in_specs=[
                pl.BlockSpec((own_rows, part), lambda i, m: (0, m[i])),
                pl.BlockSpec((part, own_rows), lambda i, m: (m[i], 0)),
            ],
            out_specs=pl.BlockSpec((1, 2, own_rows, part), lambda i, m: (i, 0, 0, 0)),
        ),
        out_shape=jax.ShapeDtypeStruct((count, 2, own_rows, part), bf16),
        cost_estimate=spent(flops=0, bytes_accessed=8 * own_rows * ff_width, transcendentals=0),
        name="ff_split",
    )(partners, up_weight, down_weight)


def ff_join_kernel(at_ref, piece_ref, up_ref, down_ref):
    up_ref[...] = piece_ref[0, 0].astype(f32)
    down_ref[...] = piece_ref[0, 1].astype(f32).T


def ff_join(pieces, partners):
    count, _, own_rows, part = pieces.shape
    return pl.pallas_call(
        ff_join_kernel,
        grid_spec=pltpu.PrefetchScalarGridSpec(
            num_scalar_prefetch=1,
            grid=(count,),
            in_specs=[pl.BlockSpec((1, 2, own_rows, part), lambda i, m: (i, 0, 0, 0))],
            out_specs=[
                pl.BlockSpec((own_rows, part), lambda i, m: (0, m[i])),
                pl.BlockSpec((part, own_rows), lambda i, m: (m[i], 0)),
            ],
        ),
        out_shape=[
            jax.ShapeDtypeStruct((own_rows, count * part), f32),
            jax.ShapeDtypeStruct((count * part, own_rows), f32),
        ],
        cost_estimate=spent(
            flops=0, bytes_accessed=12 * own_rows * count * part, transcendentals=0
        ),
        name="ff_join",
    )(partners, pieces)


def total_kernel(depth_ref, part_ref, up_ref, down_ref, cur_ref, last_ref, low_ref, resid_ref):
    width = resid_ref.shape[1]
    current = cur_ref[...].astype(f32)
    for s in range(STREAMS):
        lanes = slice(s * width, (s + 1) * width)
        total = part_ref[s, 0].astype(f32)
        total = total + up_ref[s].astype(f32) + down_ref[s].astype(f32)
        total = total + last_ref[:, s : s + 1] * current
        if s == STREAMS - 1:
            resid_ref[...] = total
        low_ref[:, lanes] = total.astype(bf16)


def total_streams(sums, current_half, last, depth_at):
    _, _, tall, width = sums.terms.shape
    wide = STREAMS * width
    rows = min(64, tall)
    row = lambda i, d: (i, 0)
    return pl.pallas_call(
        total_kernel,
        grid_spec=pltpu.PrefetchScalarGridSpec(
            num_scalar_prefetch=1,
            grid=(tall // rows,),
            in_specs=[
                pl.BlockSpec((STREAMS, 1, rows, width), lambda i, d: (0, d[0], i, 0)),
                pl.BlockSpec((STREAMS, rows, width), lambda i, d: (0, i, 0)),
                pl.BlockSpec((STREAMS, rows, width), lambda i, d: (0, i, 0)),
                pl.BlockSpec((rows, width), row),
                pl.BlockSpec((rows, 128), row),
            ],
            out_specs=[pl.BlockSpec((rows, wide), row), pl.BlockSpec((rows, width), row)],
        ),
        out_shape=[
            jax.ShapeDtypeStruct((tall, wide), bf16),
            jax.ShapeDtypeStruct((tall, width), f32),
        ],
        cost_estimate=spent(flops=5 * tall * wide, bytes_accessed=9 * tall * wide, transcendentals=0),
        name="total_streams",
    )(depth_at, sums.terms, sums.up, sums.down, current_half, last)


def norm_kernel(model_ref, own_ref, other_ref, gain_ref, normed_ref, ff_ref, stat_ref):
    rows, width = ff_ref.shape
    model = 2 * width
    own_span, other_span = own_spans(model_ref, width)
    lane = lax.broadcasted_iota(jnp.int32, (rows, 128), 1)
    stats = jnp.zeros((rows, 128), f32)
    for s in range(STREAMS):
        lanes = slice(s * width, (s + 1) * width)
        own = own_ref[:, lanes].astype(f32)
        other = other_ref[:, lanes].astype(f32)
        average = (
            jnp.sum(own, axis=-1, keepdims=True) + jnp.sum(other, axis=-1, keepdims=True)
        ) / model
        own, other = own - average, other - average
        variance = (
            jnp.sum(own * own, axis=-1, keepdims=True)
            + jnp.sum(other * other, axis=-1, keepdims=True)
        ) / model
        inverse = lax.rsqrt(variance + NORM_EPSILON)
        stats = jnp.where(lane == 2 * s, average, stats)
        stats = jnp.where(lane == 2 * s + 1, inverse, stats)
        norm_own = (own * inverse * gain_ref[s : s + 1, own_span]).astype(bf16)
        if s == STREAMS - 1:
            ff_ref[...] = norm_own
        else:
            normed_ref[s, :, own_span] = norm_own
            norm_other = (other * inverse * gain_ref[s : s + 1, other_span]).astype(bf16)
            normed_ref[s, :, other_span] = norm_other
    stat_ref[...] = stats


def norm_streams(low, low_other, gains, which):
    tall, wide = low.shape
    width = wide // STREAMS
    rows = min(64, tall)
    row = lambda i, m: (i, 0)
    return pl.pallas_call(
        norm_kernel,
        grid_spec=pltpu.PrefetchScalarGridSpec(
            num_scalar_prefetch=1,
            grid=(tall // rows,),
            in_specs=[
                pl.BlockSpec((rows, wide), row),
                pl.BlockSpec((rows, wide), row),
                pl.BlockSpec(gains.shape, lambda i, m: (0, 0)),
            ],
            out_specs=[
                pl.BlockSpec((3, rows, 2 * width), lambda i, m: (0, i, 0)),
                pl.BlockSpec((rows, width), row),
                pl.BlockSpec((rows, 128), row),
            ],
        ),
        out_shape=[
            jax.ShapeDtypeStruct((3, tall, 2 * width), bf16),
            jax.ShapeDtypeStruct((tall, width), bf16),
            jax.ShapeDtypeStruct((tall, 128), f32),
        ],
        cost_estimate=spent(
            flops=20 * tall * wide, bytes_accessed=8 * tall * wide, transcendentals=0
        ),
        name="norm_streams",
    )(which, low, low_other, gains)


def turn(values, cosine, sine_up, sine_down, sign):
    up = pltpu.roll(values, HDIM - ROT // 2, 1)
    down = pltpu.roll(values, ROT // 2, 1)
    return values * cosine + sign * (up * sine_up + down * sine_down)


def project_kernel(
    x_ref, cot_ref, wq_ref, wk_ref, wv_ref, wo_ref, cos_ref, up_ref, down_ref, out_ref
):
    span = wq_ref.shape[-1]
    tables = cos_ref[...], up_ref[...], down_ref[...]
    for kind, w_ref in enumerate((wq_ref, wk_ref, wv_ref, wo_ref)):
        rows = cot_ref[...] if kind == 3 else x_ref[kind]
        product = dot_nn(rows, w_ref[...].reshape(-1, span))
        for begin in range(0, span, HDIM):
            head = product[:, begin : begin + HDIM]
            if kind < 2:
                head = turn(head, *tables, 1.0)
            out_ref[0, :, kind * span + begin : kind * span + begin + HDIM] = head.astype(bf16)


def project_heads(normed, cot, weights, tables, depth_count):
    _, rows, model = normed.shape
    groups, _, _, own_rows, heads_width = weights.shape
    span = heads_width // depth_count
    whole = lambda j: (0, 0)

    def matrix(kind):
        shape = (groups, depth_count, 1, own_rows, span)
        return pl.BlockSpec(shape, lambda j: (0, 0, kind, 0, j))

    return pl.pallas_call(
        project_kernel,
        grid=(depth_count,),
        in_specs=[
            pl.BlockSpec((3, rows, model), lambda j: (0, 0, 0)),
            pl.BlockSpec((rows, model), whole),
        ]
        + [matrix(kind) for kind in range(4)]
        + [pl.BlockSpec((rows, HDIM), whole)] * 3,
        out_specs=pl.BlockSpec((1, rows, 4 * span), lambda j: (j, 0, 0)),
        out_shape=jax.ShapeDtypeStruct((depth_count, rows, 4 * span), bf16),
        compiler_params=pltpu.CompilerParams(vmem_limit_bytes=40 << 20),
        cost_estimate=spent(
            flops=8 * rows * model * span * depth_count,
            bytes_accessed=8 * model * span * depth_count + 8 * rows * model,
            transcendentals=0,
        ),
        name="project_heads",
    )(normed, cot, *[weights] * 4, *tables)


def attend_kernel(
    block, q_ref, k_ref, v_ref, g_ref, doc_col_ref, doc_row_ref, cos_ref, up_ref, down_ref,
    out_ref, dk_sum, dv_sum,
):
    length = q_ref.shape[0]
    scale = HDIM**-0.5
    heads_each = out_ref.shape[1] // (4 * HDIM)

    def lanes(kind):
        return pl.ds(pl.multiple_of((kind * heads_each + pl.program_id(0)) * HDIM, HDIM), HDIM)

    for begin in range(0, length, block):
        end = begin + block
        rows = slice(begin, end)
        queries, grads = q_ref[rows, :], g_ref[rows, :]
        keys, values = k_ref[0:end, :], v_ref[0:end, :]
        scores = dot_nt(queries, keys) * scale
        place_q = begin + lax.broadcasted_iota(jnp.int32, scores.shape, 0)
        place_k = lax.broadcasted_iota(jnp.int32, scores.shape, 1)
        allowed = (doc_col_ref[rows, :] == doc_row_ref[:, 0:end]) & (place_q >= place_k)
        scores = jnp.where(allowed, scores, MASKED)
        highest = jnp.max(scores, axis=-1, keepdims=True)
        exponent = jnp.exp(scores - highest)
        totals = jnp.sum(exponent, axis=-1, keepdims=True)
        attention = exponent * (1.0 / totals)
        low = attention.astype(bf16)
        out_ref[rows, lanes(0)] = dot_nn(low, values).astype(bf16)
        grad_att = dot_nt(grads, values).astype(bf16).astype(f32)
        weighted = jnp.sum(attention * grad_att, axis=-1, keepdims=True)
        grad_scores = (attention * (grad_att - weighted)).astype(bf16)
        grad_q = dot_nn(grad_scores, keys) * scale
        out_ref[rows, lanes(1)] = turn(
            grad_q, cos_ref[rows, :], up_ref[rows, :], down_ref[rows, :], -1.0
        ).astype(bf16)
        part_k = dot_tn(grad_scores, queries)
        part_v = dot_tn(low, grads)
        if begin > 0:
            dk_sum[0:begin, :] += part_k[0:begin]
            dv_sum[0:begin, :] += part_v[0:begin]
        dk_sum[begin:end, :] = part_k[begin:end]
        dv_sum[begin:end, :] = part_v[begin:end]
    grad_k = dk_sum[...] * scale
    out_ref[:, lanes(2)] = turn(grad_k, cos_ref[...], up_ref[...], down_ref[...], -1.0).astype(bf16)
    out_ref[:, lanes(3)] = dv_sum[...].astype(bf16)


def attend(packed, documents, tables, heads_each):
    length = packed.shape[0]
    block = min(256, length)
    whole = lambda h: (0, 0)

    def kind(at):
        return pl.BlockSpec((length, HDIM), lambda h: (0, at * heads_each + h))

    return pl.pallas_call(
        functools.partial(attend_kernel, block),
        grid=(heads_each,),
        in_specs=[kind(0), kind(1), kind(2), kind(3)]
        + [pl.BlockSpec((length, 1), whole), pl.BlockSpec((1, length), whole)]
        + [pl.BlockSpec((length, HDIM), whole)] * 3,
        out_specs=pl.BlockSpec((length, 4 * heads_each * HDIM), whole),
        out_shape=jax.ShapeDtypeStruct((length, 4 * heads_each * HDIM), bf16),
        scratch_shapes=[pltpu.VMEM((length, HDIM), f32)] * 2,
        compiler_params=pltpu.CompilerParams(vmem_limit_bytes=48 << 20),
        cost_estimate=spent(
            flops=9 * heads_each * length * length * HDIM,
            bytes_accessed=16 * length * heads_each * HDIM + 12 * length * HDIM,
            transcendentals=heads_each * length * length,
        ),
        name="attend",
    )(packed, packed, packed, packed, documents[:, None], documents[None, :], *tables)


def gelu_parts(values):
    cdf = 0.5 * (1.0 + lax.erf(values * (0.5**0.5)))
    density = jnp.exp(-0.5 * values * values) * (1.0 / math.sqrt(2.0 * math.pi))
    return values * cdf, cdf + values * density


def ff_kernel(
    model_ref, x_ref, cot_ref, up_ref, down_ref,
    hidden_ref, grad_ref, own_ref, other_ref,
):
    part = up_ref.shape[-1]
    half = up_ref.shape[1] // 2

    def rows_of(ref, which):
        return ref[0, pl.ds(which * half, half)].reshape(-1, part)

    own, other = model_ref[0], 1 - model_ref[0]
    up_pre = dot_nn(x_ref[...], up_ref[...].reshape(-1, part))
    hidden, slope = gelu_parts(up_pre)
    hidden = hidden.astype(bf16)
    grad_up = (dot_nn(cot_ref[0, 0], down_ref[...].reshape(-1, part)) * slope).astype(bf16)
    hidden_ref[...] = hidden
    grad_ref[...] = grad_up
    other_ref[0] = dot_nt(grad_up, rows_of(up_ref, other)).astype(bf16)
    own_ref[0] = dot_nt(grad_up, rows_of(up_ref, own))
    other_ref[1] = dot_nt(hidden, rows_of(down_ref, other)).astype(bf16)
    own_ref[1] = dot_nt(hidden, rows_of(down_ref, own))


def feed_forward(x, cot, micro_at, weights, which):
    tall, model = x.shape
    part = weights.shape[-1]
    width = model // 2
    rows = cot.shape[2]
    row = lambda i, m: (i, 0)

    def resident(kind):
        return pl.BlockSpec(
            (1,) + weights.shape[1:],
            lambda i, m: (kind, 0, 0, 0, 0),
            pipeline_mode=pl.Buffered(1),
        )

    return pl.pallas_call(
        ff_kernel,
        grid_spec=pltpu.PrefetchScalarGridSpec(
            num_scalar_prefetch=1,
            grid=(tall // rows,),
            in_specs=[
                pl.BlockSpec((rows, model), row),
                pl.BlockSpec((1, 1, rows, model), lambda i, m: (i, micro_at, 0, 0)),
                resident(0),
                resident(1),
            ],
            out_specs=[pl.BlockSpec((rows, part), row)] * 2
            + [pl.BlockSpec((2, rows, width), lambda i, m: (0, i, 0))] * 2,
        ),
        out_shape=[jax.ShapeDtypeStruct((tall, part), bf16)] * 2
        + [
            jax.ShapeDtypeStruct((2, tall, width), f32),
            jax.ShapeDtypeStruct((2, tall, width), bf16),
        ],
        compiler_params=pltpu.CompilerParams(vmem_limit_bytes=48 << 20),
        cost_estimate=spent(
            flops=8 * tall * model * part,
            bytes_accessed=4 * model * part + 16 * tall * model,
            transcendentals=2 * tall * part,
        ),
        name="feed_forward",
    )(which, x, cot, weights, weights)


def back_kernel(half_ref, ans_ref, wo_ref, wq_ref, wk_ref, wv_ref, out_ref, *flat):
    count, _, wide = ans_ref.shape
    span = wide // 4
    for kind, w_ref in enumerate((wo_ref, wq_ref, wk_ref, wv_ref)):
        total = None
        for j in range(count):
            term = dot_nt(
                ans_ref[j, :, kind * span : (kind + 1) * span],
                w_ref[:, :, :, :, j * span : (j + 1) * span].reshape(-1, span),
            )
            total = term if total is None else total + term
        out_ref[kind] = total.astype(out_ref.dtype)
    if flat:

        @pl.when(pl.program_id(0) == 0)
        def _():
            for kind in range(4):
                for j in range(count):
                    flat[0][kind, :, j * span : (j + 1) * span] = ans_ref[
                        j, :, kind * span : (kind + 1) * span
                    ]


def back_project(answer, weights, half, dtype, flat):
    count, rows, wide = answer.shape
    groups, _, _, own_rows, heads_width = weights.shape
    part = count * own_rows
    steps = groups // 2
    width = part * steps

    def matrix(kind):
        shape = (1, count, 1, own_rows, heads_width)
        return pl.BlockSpec(shape, lambda i, m: (m[0] * steps + i, 0, kind, 0, 0))

    out_specs = [pl.BlockSpec((4, rows, part), lambda i, m: (0, 0, i))]
    out_shape = [jax.ShapeDtypeStruct((4, rows, width), dtype)]
    if flat:
        out_specs.append(pl.BlockSpec((4, rows, heads_width), lambda i, m: (0, 0, 0)))
        out_shape.append(jax.ShapeDtypeStruct((4, rows, heads_width), bf16))
    return pl.pallas_call(
        back_kernel,
        grid_spec=pltpu.PrefetchScalarGridSpec(
            num_scalar_prefetch=1,
            grid=(steps,),
            in_specs=[pl.BlockSpec((count, rows, wide), lambda i, m: (0, 0, 0))]
            + [matrix(kind) for kind in (3, 0, 1, 2)],
            out_specs=out_specs,
        ),
        out_shape=out_shape,
        compiler_params=pltpu.CompilerParams(vmem_limit_bytes=40 << 20),
        cost_estimate=spent(
            flops=8 * rows * heads_width * width,
            bytes_accessed=8 * heads_width * width + 20 * rows * width,
            transcendentals=0,
        ),
        name="back_project",
    )(half, answer, *[weights] * 4)


def slope_kernel(
    model_ref, own_ref, got_ref, ff_ref, low_ref, stat_ref, gain_ref, scaled_ref, sum_ref, gain_out_ref
):
    _, rows, width = ff_ref.shape
    own_span, _ = own_spans(model_ref, width)
    lane = lax.broadcasted_iota(jnp.int32, (rows, 128), 1)
    packed = jnp.zeros((rows, 128), f32)
    totals = []
    for s in range(STREAMS):
        lanes = slice(s * width, (s + 1) * width)
        if s < 3:
            grad = own_ref[s + 1] + got_ref[s + 1].astype(f32)
        else:
            grad = ff_ref[0]
        average, inverse = stat_ref[:, 2 * s : 2 * s + 1], stat_ref[:, 2 * s + 1 : 2 * s + 2]
        hat = (low_ref[:, lanes].astype(f32) - average) * inverse
        totals.append(jnp.sum(grad * hat, axis=0, keepdims=True))
        scaled = grad * gain_ref[s : s + 1, own_span]
        scaled_ref[:, lanes] = scaled
        packed = jnp.where(lane == 2 * s, jnp.sum(scaled, axis=-1, keepdims=True), packed)
        packed = jnp.where(
            lane == 2 * s + 1, jnp.sum(scaled * hat, axis=-1, keepdims=True), packed
        )
    sum_ref[...] = packed
    totals = jnp.concatenate(totals, axis=0)

    @pl.when(pl.program_id(0) == 0)
    def _():
        gain_out_ref[...] = totals

    @pl.when(pl.program_id(0) > 0)
    def _():
        gain_out_ref[...] += totals


def norm_slopes(own, got, ff_grad, low, stats, gains, which):
    tall, wide = low.shape
    width = wide // STREAMS
    rows = min(64, tall)
    row = lambda i, m: (i, 0)
    cube = pl.BlockSpec((4, rows, width), lambda i, m: (0, i, 0))
    return pl.pallas_call(
        slope_kernel,
        grid_spec=pltpu.PrefetchScalarGridSpec(
            num_scalar_prefetch=1,
            grid=(tall // rows,),
            in_specs=[
                cube,
                cube,
                pl.BlockSpec((1, rows, width), lambda i, m: (0, i, 0)),
                pl.BlockSpec((rows, wide), row),
                pl.BlockSpec((rows, 128), row),
                pl.BlockSpec(gains.shape, lambda i, m: (0, 0)),
            ],
            out_specs=[
                pl.BlockSpec((rows, wide), row),
                pl.BlockSpec((rows, 128), row),
                pl.BlockSpec((STREAMS, width), lambda i, m: (0, 0)),
            ],
        ),
        out_shape=[
            jax.ShapeDtypeStruct((tall, wide), f32),
            jax.ShapeDtypeStruct((tall, 128), f32),
            jax.ShapeDtypeStruct((STREAMS, width), f32),
        ],
        cost_estimate=spent(
            flops=12 * tall * wide, bytes_accessed=12 * tall * wide, transcendentals=0
        ),
        name="norm_slopes",
    )(which, own, got, ff_grad, low, stats, gains)


def grads_kernel(
    scaled_ref, mine_ref, theirs_ref, low_ref, stat_ref, cot_ref, cur_ref, last_ref,
    grad_ref, mix_ref, dot_ref,
):
    rows, width = cot_ref.shape
    lane = lax.broadcasted_iota(jnp.int32, (rows, 128), 1)
    means = (mine_ref[...] + theirs_ref[...]) / (2 * width)
    current = cur_ref[...].astype(f32)
    packed = jnp.zeros((rows, 128), f32)
    mixed = None
    for s in range(STREAMS):
        lanes = slice(s * width, (s + 1) * width)
        average, inverse = stat_ref[:, 2 * s : 2 * s + 1], stat_ref[:, 2 * s + 1 : 2 * s + 2]
        hat = (low_ref[:, lanes].astype(f32) - average) * inverse
        grad = inverse * (
            scaled_ref[:, lanes]
            - means[:, 2 * s : 2 * s + 1]
            - hat * means[:, 2 * s + 1 : 2 * s + 2]
        )
        if s == STREAMS - 1:
            grad = grad + cot_ref[...].astype(f32)
        grad = grad.astype(bf16)
        grad_ref[s] = grad
        grad = grad.astype(f32)
        term = last_ref[:, s : s + 1] * grad
        mixed = term if mixed is None else mixed + term
        packed = jnp.where(lane == s, jnp.sum(grad * current, axis=-1, keepdims=True), packed)
    mix_ref[...] = mixed
    dot_ref[...] = packed


def stream_grads(scaled, mine, theirs, low, stats, cot, current_half, last):
    tall, wide = low.shape
    width = wide // STREAMS
    rows = min(64, tall)
    row = lambda i: (i, 0)
    return pl.pallas_call(
        grads_kernel,
        grid=(tall // rows,),
        in_specs=[
            pl.BlockSpec((rows, wide), row),
            pl.BlockSpec((rows, 128), row),
            pl.BlockSpec((rows, 128), row),
            pl.BlockSpec((rows, wide), row),
            pl.BlockSpec((rows, 128), row),
            pl.BlockSpec((rows, width), row),
            pl.BlockSpec((rows, width), row),
            pl.BlockSpec((rows, 128), row),
        ],
        out_specs=[
            pl.BlockSpec((STREAMS, rows, width), lambda i: (0, i, 0)),
            pl.BlockSpec((rows, width), row),
            pl.BlockSpec((rows, 128), row),
        ],
        out_shape=[
            jax.ShapeDtypeStruct((STREAMS, tall, width), bf16),
            jax.ShapeDtypeStruct((tall, width), f32),
            jax.ShapeDtypeStruct((tall, 128), f32),
        ],
        cost_estimate=spent(
            flops=12 * tall * wide, bytes_accessed=10 * tall * wide, transcendentals=0
        ),
        name="stream_grads",
    )(scaled, mine, theirs, low, stats, cot, current_half, last)


def turning_tables(places):
    half = ROT // 2
    inverse = jnp.exp(jnp.arange(half, dtype=f32) * (-2.0 * math.log(10000.0) / ROT))
    angles = places.astype(f32)[:, None] * inverse[None, :]
    cosine, sine = jnp.cos(angles), jnp.sin(angles)
    rows = places.shape[0]
    rest = jnp.zeros((rows, HDIM - ROT), f32)
    blank = jnp.zeros((rows, half), f32)
    return (
        jnp.concatenate([cosine, cosine, rest + 1.0], axis=1),
        jnp.concatenate([-sine, blank, rest], axis=1),
        jnp.concatenate([blank, sine, rest], axis=1),
    )


def local(
    history,
    slot_layer,
    current,
    positions,
    doc_ids,
    cotangent,
    norm_gains,
    generator_in,
    generator_out,
    query_weight,
    key_weight,
    value_weight,
    out_weight,
    up_weight,
    down_weight,
):
    dp_count = lax.axis_size("dp")
    depth_count = lax.axis_size("depth")
    dp_at = lax.axis_index("dp")
    model_at = lax.axis_index("mp")
    dp_bits = list(range(bit_count(dp_count)))
    slots, tokens_held, width = history.shape
    model = current.shape[1]
    rows_mb = current.shape[0] // MB
    length = depth_count * rows_mb
    heads_width = query_weight.shape[1]
    heads_each = heads_width // HDIM // depth_count
    own_rows = query_weight.shape[0]
    ff_width = up_weight.shape[1]
    ff_part = ff_width // dp_count
    both = ("dp", "depth")

    def half_of(values, axis, which):
        return lax.dynamic_slice_in_dim(values, which * width, width, axis)

    partners = jnp.stack([dp_at ^ m for m in range(dp_count)]).astype(jnp.int32)
    ff_local = ff_split(up_weight, down_weight, partners)
    small_cols = jnp.concatenate(
        [generator_in, norm_gains.T, jnp.zeros((own_rows, 128 - GEN - 5), bf16)], axis=1
    )
    small_all = gather_small(small_cols, both).reshape(model, 128)
    gen_first = small_all[:, :GEN]
    gen_first, ff_local = fence(gen_first, ff_local)
    ff_rows = [ff_local[0]] + [swap_mask(ff_local[m], "dp", m) for m in range(1, dp_count)]
    ff_rows = place_many(partners, ff_rows).reshape(2 * dp_count, own_rows, ff_part)

    gain_float = small_all[:, GEN : GEN + 5].astype(f32).T
    second_rows = generator_out.shape[0]
    second_pad = -second_rows % 128
    second_all = gather_small(jnp.pad(generator_out, (0, second_pad))[None], both)
    gen_second = second_all.reshape(-1, second_rows + second_pad)[:, :second_rows]
    second_low = gen_second.reshape(GEN, STREAMS * MIX)

    stacked = jnp.concatenate([query_weight, key_weight, value_weight, out_weight.T], axis=0)
    over_depth = lax.all_gather(stacked, "depth", axis=0, tiled=True)
    current_f = current.astype(f32)
    current_half = half_of(current, 1, model_at)
    mean_square = jnp.mean(current_f * current_f, axis=-1, keepdims=True)
    inverse_rms = lax.rsqrt(mean_square + RMS_EPSILON)
    unit = current_f * inverse_rms
    gen_normed = (unit * gain_float[4]).astype(bf16)
    gen_pre = dot_nn(gen_normed, gen_first)
    gen_hidden = gelu_exact(gen_pre).astype(bf16)
    column = jnp.arange(STREAMS * MIX)
    last_col = (column % MIX == MIX - 1).astype(f32)
    mixing = (dot_nn(gen_hidden, second_low) + last_col).astype(bf16)
    pick_last = (column[:, None] == (jnp.arange(128) * MIX + MIX - 1)[None, :]).astype(bf16)
    last = dot_nn(mixing, pick_last)

    layer_of = jnp.tile(slot_layer, STREAMS)
    stream_of = jnp.repeat(jnp.arange(STREAMS), slots)
    from_col = jnp.where(layer_of < MIX, stream_of * MIX + layer_of, -1)
    pick = (column[:, None] == from_col[None, :]).astype(f32)
    mix_all = gather_small(mixing, ("depth",)).reshape(depth_count * MB * rows_mb, STREAMS * MIX)
    slot_mix = dot_nn(mix_all, pick.astype(bf16))
    places_all = gather_small(positions, ("depth",))

    def over_depth_swap(values):
        return lax.all_to_all(values, "depth", 0, 0, tiled=True)

    def mix_part(micro_at, slot_mix):
        partial = mix_streams(slot_mix, history, micro_at, depth_count, rows_mb)
        return partial.reshape(STREAMS, depth_count, rows_mb, width)

    slot_mix, ff_rows, cotangent, places_all = fence(slot_mix, ff_rows, cotangent, places_all)
    partial = mix_part(0, slot_mix)
    partial_next = mix_part(1, slot_mix)

    weights_line = LineGather(ff_rows)
    weights_line.step()
    cot_pieces = lax.all_gather(cotangent, "dp", axis=0, tiled=True)
    over_depth, partial, partial_next = weights_line.hold(over_depth, partial, partial_next)
    pieces = [over_depth]
    weights = place_block(None, pieces[0][None], place_index(0), dp_count)
    hops_left = [(p, at) for at in range(len(dp_bits)) for p in range(1 << at)]
    placed = 1
    cots = None
    sums, sums_next = LineScatter(partial), LineScatter(partial_next)
    own_tables = turning_tables(positions)
    tables = [
        turning_tables(places_all[:, m * rows_mb : (m + 1) * rows_mb].reshape(length))
        for m in range(MB)
    ]
    for hop in range(1, depth_count):
        sums.step_with(weights_line)
        last_hop = hop == depth_count - 1
        for place in range(placed, len(pieces)):
            weights = place_block(weights, pieces[place][None], place_index(place), dp_count)
        placed = len(pieces)
        while hops_left:
            place, at = hops_left.pop(0)
            pieces.append(core_hop(pieces[place], at))
            if len(hops_left) <= depth_count - 1 - hop:
                break
        if last_hop:
            cot_full = join_halves(cotangent, other_core(cotangent), model_at)
            ff_weights = weights_line.placed()
            cots = cot_full, cotangent, ff_weights
        (state,) = weights_line.hold(
            (sums.up, sums.down, pieces, weights, cots, own_tables, tables, cot_pieces)
        )
        sums.up, sums.down, pieces, weights, cots, own_tables, tables, cot_pieces = state
    cot_full, cotangent, ff_weights = cots
    for place in range(placed, len(pieces)):
        weights = place_block(weights, pieces[place][None], place_index(place), dp_count)
    weights = weights.reshape(dp_count, depth_count, 4, own_rows, heads_width)
    ff_weights = ff_weights.reshape(2, dp_count, depth_count, own_rows, ff_part)

    document_view = doc_ids.reshape(depth_count, MB, rows_mb)
    which = model_at.astype(jnp.int32)[None]
    depth_at = lax.axis_index("depth").astype(jnp.int32)[None]
    gains = gain_float

    def enter(micro_at, sums):
        span = slice(micro_at * rows_mb, (micro_at + 1) * rows_mb)
        low, resid = total_streams(sums, current_half[span], last[span], depth_at)
        normed, ff_normed, stats = norm_streams(low, other_core(low), gains, which)
        packed = project_heads(
            normed,
            cot_full[span],
            weights,
            [t[span] for t in own_tables],
            depth_count,
        )
        return dict(
            low=low, resid=resid, normed=normed, ff_normed=ff_normed, stats=stats, packed=packed
        )

    def attention(micro_at, by_head):
        documents = document_view[:, micro_at].reshape(length)
        by_head = by_head.reshape(length, 4 * heads_each * HDIM)
        answer = attend(by_head, documents, tables[micro_at], heads_each)
        return answer.reshape(depth_count, rows_mb, 4 * heads_each * HDIM)

    place_list = jnp.stack([place_index(p) for p in range(dp_count)]).astype(jnp.int32)

    def group_rows(ff_normed):
        return lax.all_gather(ff_normed, "dp", axis=0, tiled=True)

    def group_joined(mine):
        return join_halves(mine, other_core(mine), model_at)

    def hidden_units(micro_at, group_normed):
        hidden, grad_up, own, other = feed_forward(
            group_normed, cot_group, micro_at, ff_weights, which
        )
        return dict(group_normed=group_normed, hidden=hidden, grad_up=grad_up), (own, other)

    def group_back_rest(near):
        for at in reversed(range(len(dp_bits) - 1)):
            half = 1 << at
            near = near[:half] + core_hop(near[half:].astype(bf16), at).astype(f32)
        return near[0]

    def group_back(own, other):
        near, far = group_split(own, other, place_list)
        return group_back_rest(near + core_hop(far, len(dp_bits) - 1).astype(f32))

    def back(kept, answer):
        (theirs,) = back_project(answer, weights, 1 - which, bf16, False)
        got = other_core(theirs)
        own, flat = back_project(answer, weights, which, f32, True)
        return own, got, flat

    def leave(micro_at, kept, own, got, ff_sum):
        span = slice(micro_at * rows_mb, (micro_at + 1) * rows_mb)
        rows = (kept["resid"] + own[0] + got[0].astype(f32) + ff_sum[1]).astype(bf16)
        low, stats = kept["low"], kept["stats"]
        scaled, sums, gain_part = norm_slopes(own, got, ff_sum, low, stats, gains, which)
        grad_low, current_mix, last_dot = stream_grads(
            scaled, sums, other_core(sums), low, stats, cotangent[span], current_half[span], last[span]
        )
        kept.update(layer_rows=rows, gain=gain_part, current_mix=current_mix, last_dot=last_dot)
        return grad_low

    ((sums.up, sums.down),) = sums_next.step((sums.up, sums.down))
    first = enter(0, sums)
    mine = group_rows(first["ff_normed"])
    packed, mine, cot_pieces = sums_next.hold(first["packed"], mine, cot_pieces)
    while sums_next.at < depth_count - 3:
        sums_next.step()
        sums_next.hold()
    packed, mine, cot_pieces = sums_next.step(packed, mine, cot_pieces)
    by_head = over_depth_swap(packed)
    cot_group = join_halves(cot_pieces, other_core(cot_pieces), model_at)
    cot_group = cot_group.reshape(dp_count, MB, rows_mb, model)
    kept, ff_parts = hidden_units(0, group_joined(mine))
    first.update(kept)
    by_head, ff_parts, cot_group = sums_next.hold(by_head, ff_parts, cot_group)
    by_head, ff_parts = sums_next.step(by_head, ff_parts)
    answer = attention(0, by_head)
    answer, ff_parts = sums_next.hold(answer, ff_parts)

    answer = over_depth_swap(answer)
    second = enter(1, sums_next)
    near, far = group_split(ff_parts[0], other_core(ff_parts[1]), place_list)
    near = near + core_hop(far, len(dp_bits) - 1).astype(f32)
    answer, packed, ff_normed, near = fence(
        answer, second["packed"], second["ff_normed"], near
    )
    by_head = over_depth_swap(packed)
    mine = group_rows(ff_normed)
    own, got, first["flat"] = back(first, answer)
    grad_low = leave(0, first, own, got, group_back_rest(near))
    by_head, grad_low, mine, first["layer_rows"] = fence(
        by_head, grad_low, mine, first["layer_rows"]
    )
    saved = [first, second]

    def each(name):
        return [s[name] for s in saved]

    def rows_of(name):
        return jnp.concatenate(each(name), axis=0)

    def place_grads(place, dtype):
        return attention_grads(
            each("normed"),
            cot_full,
            each("flat"),
            place_list[place : place + 1],
            depth_count,
            dp_count,
            dtype,
        )

    half = dp_count // 2
    hops_left = [
        (p, at) for at in reversed(range(len(dp_bits))) for p in range(1 << at, 2 << at)
    ]
    pieces = {}

    def sums_hop():
        place, at = hops_left.pop(0)
        arrived = core_hop(pieces.pop(place), at)
        target = place - (1 << at)
        pieces[target] = (pieces[target].astype(f32) + arrived.astype(f32)).astype(bf16)

    grad_line = LineGather(grad_low)
    grad_line.step()
    answer = attention(1, by_head)
    kept, ff_parts = hidden_units(1, group_joined(mine))
    second.update(kept)
    answer, ff_parts = grad_line.hold(answer, ff_parts)
    answer = over_depth_swap(answer)
    near, far = group_split(ff_parts[0], other_core(ff_parts[1]), place_list)
    ff_products = hidden_grads(
        each("group_normed"), cot_group, each("grad_up"), each("hidden"), dp_count, depth_count
    )
    near = near + core_hop(far, len(dp_bits) - 1).astype(f32)
    answer, near, ff_products = fence(answer, near, ff_products)

    ff_sums = LineScatter(ff_products)
    (answer,) = ff_sums.step_with(grad_line, answer)
    own, got, flat = back(second, answer)
    ff_sum = group_back_rest(near)
    second["flat"] = flat
    (state,) = grad_line.hold((ff_sums.up, ff_sums.down, own, got, flat, ff_sum))
    ff_sums.up, ff_sums.down, own, got, second["flat"], ff_sum = state
    while len(grad_line.up) < depth_count - 1:
        ff_sums.step_with(grad_line)
        (state,) = grad_line.hold((ff_sums.up, ff_sums.down))
        ff_sums.up, ff_sums.down = state
    (ff_sum,) = ff_sums.step_with(grad_line, ff_sum)
    grad_low = leave(1, second, own, got, ff_sum)
    pieces = {p: place_grads(p, bf16) for p in range(dp_count)}
    sums_hop()
    (state,) = grad_line.hold((ff_sums.up, ff_sums.down, grad_low, pieces))
    ff_sums.up, ff_sums.down, grad_low, pieces = state

    last_line = LineGather(grad_low)
    last_line.step()
    if hops_left:
        sums_hop()
    grad_first = grad_line.placed().reshape(STREAMS, length, width)
    history_grad, slot_part = unmix_streams(
        slot_mix, history, grad_first, 0, depth_count, rows_mb, None
    )
    slot_parts = [slot_part.reshape(depth_count, 1, rows_mb, 128)]
    pieces, history_grad, second["layer_rows"] = last_line.hold(
        pieces, history_grad, second["layer_rows"]
    )
    (pieces,) = ff_sums.step(pieces)
    while hops_left:
        sums_hop()
    (pieces,) = ff_sums.hold(pieces)
    out_sums = LineScatter(pieces[0].reshape(1, depth_count, 4 * own_rows, heads_width))
    for hop in range(2, depth_count):
        last_line.step()
        ((ff_sums.up, ff_sums.down),) = out_sums.step((ff_sums.up, ff_sums.down))
        if hop == depth_count - 1:
            ff_sums.up = ff_sums.down = end_sums(ff_sums, bf16)
            early = last_line.placed_early()
            history_grad, slot_part = unmix_streams(
                slot_mix,
                history,
                early.reshape(STREAMS, length, width),
                1,
                depth_count,
                rows_mb,
                history_grad,
            )
        (state,) = last_line.hold(
            (out_sums.up, out_sums.down, ff_sums.up, ff_sums.down, history_grad, slot_part)
        )
        out_sums.up, out_sums.down, ff_sums.up, ff_sums.down, history_grad, slot_part = state
    early, ff_grads = out_sums.step(early, ff_sums.up)
    ff_grads = ff_grads.reshape(2, dp_count, own_rows, ff_part)
    ff_pieces = [
        lax.dynamic_index_in_dim(ff_grads, partners[m], 1, keepdims=False) for m in range(dp_count)
    ]
    ff_pieces = ff_pieces[:1] + [swap_mask(ff_pieces[m], "dp", m) for m in range(1, dp_count)]
    far_grads, far_index = last_line.farthest(early)
    history_grad, far_part = unmix_one(
        slot_mix, history, far_grads, 1, far_index, rows_mb, history_grad
    )
    slot_part = slot_part.reshape(depth_count, rows_mb, 128)
    slot_part = lax.dynamic_update_index_in_dim(slot_part, far_part, far_index, 0)
    slot_parts.append(slot_part[:, None])

    slot_grads = jnp.concatenate(slot_parts, axis=1).reshape(-1, 128)[:, : STREAMS * slots]
    mix_grads = dot_exact(slot_grads, pick.T).reshape(depth_count, MB * rows_mb, STREAMS * MIX)
    mix_grads, ff_pieces = out_sums.hold(mix_grads, ff_pieces)
    grad_mixing = scatter_small(mix_grads, ("depth",))
    up_grad, down_grad = ff_join(jnp.stack(ff_pieces), partners)
    last_dots = rows_of("last_dot")
    grad_mixing = grad_mixing + dot_exact(last_dots, pick_last.astype(f32).T)
    grad_mixing = grad_mixing + other_core(grad_mixing)

    second_float = second_low.astype(f32)
    grad_second = dot_exact(gen_hidden.astype(f32).T, grad_mixing)
    grad_pre = dot_exact(grad_mixing, second_float.T) * gelu_slope(gen_pre)
    grad_first = dot_exact(gen_normed.astype(f32).T, grad_pre)
    grad_gen_normed = dot_exact(grad_pre, gen_first.astype(f32).T)
    gain_gen = jnp.sum(grad_gen_normed * unit, axis=0)
    scattered = end_sums(out_sums, f32).reshape(4, own_rows, heads_width)
    grad_unit = grad_gen_normed * gain_float[4]
    shared = jnp.mean(grad_unit * unit, axis=-1, keepdims=True)
    current_gen = half_of(inverse_rms * (grad_unit - unit * shared), 1, model_at)
    current_grad = rows_of("current_mix") + current_gen

    gain_own = sum(s["gain"] for s in saved)
    gain_other = other_core(gain_own)
    gain_all = jnp.where(
        model_at == 0,
        jnp.concatenate([gain_own, gain_other], axis=1),
        jnp.concatenate([gain_other, gain_own], axis=1),
    )
    gain_all = jnp.concatenate([gain_all, gain_gen[None]], axis=0)
    small_grads = jnp.concatenate(
        [grad_first, gain_all.T, jnp.zeros((model, 128 - GEN - 5), f32)], axis=1
    )
    small_grads = scatter_small(small_grads.reshape(-1, own_rows, 128), both)
    second_grads = jnp.pad(grad_second.reshape(-1, second_rows), ((0, 0), (0, second_pad)))
    second_grads = scatter_small(second_grads[:, None], both)

    return (
        rows_of("layer_rows"),
        history_grad,
        current_grad,
        small_grads[:, GEN : GEN + 5].T,
        small_grads[:, :GEN],
        second_grads[0, :second_rows],
        scattered[0],
        scattered[1],
        scattered[2],
        scattered[3].T,
        up_grad,
        down_grad,
    )


def solution(mesh):
    return jax.shard_map(
        local,
        mesh=mesh,
        in_specs=(
            P("depth", "dp", "mp"),
            P("depth"),
            P(("dp", "depth"), None),
            P(("dp", "depth")),
            P("dp"),
            P(("dp", "depth"), "mp"),
            P(None, ("dp", "depth")),
            P(("dp", "depth"), None),
            P(("dp", "depth")),
            P(("dp", "depth"), "mp"),
            P(("dp", "depth"), "mp"),
            P(("dp", "depth"), "mp"),
            P("mp", ("dp", "depth")),
            P(("dp", "depth"), "mp"),
            P("mp", ("dp", "depth")),
        ),
        out_specs=(
            P(("dp", "depth"), "mp"),
            P("depth", "dp", "mp"),
            P(("dp", "depth"), "mp"),
            P(None, ("dp", "depth")),
            P(("dp", "depth"), None),
            P(("dp", "depth")),
            P(("dp", "depth"), "mp"),
            P(("dp", "depth"), "mp"),
            P(("dp", "depth"), "mp"),
            P("mp", ("dp", "depth")),
            P(("dp", "depth"), "mp"),
            P("mp", ("dp", "depth")),
        ),
        check_vma=False,
    )
```

```python
import functools
import math

import jax
import jax.numpy as jnp
from jax import lax
from jax.experimental import pallas as pl
from jax.experimental.pallas import tpu as pltpu
from jax.sharding import PartitionSpec as P

HDIM = 128
ROT = 32
GEN = 72
MB = 2
MIX = 18
STREAMS = 4
COST = 20

PRECISE = lax.Precision.HIGHEST
NORM_EPSILON = 1e-05
RMS_EPSILON = 1e-06
MASKED = -1e30

bf16 = jnp.bfloat16
f32 = jnp.float32


def dot_nn(a, b):
    return lax.dot_general(a, b, (((1,), (0,)), ((), ())), preferred_element_type=f32)


def dot_nt(a, b):
    return lax.dot_general(a, b, (((1,), (1,)), ((), ())), preferred_element_type=f32)


def dot_tn(a, b):
    return lax.dot_general(a, b, (((0,), (0,)), ((), ())), preferred_element_type=f32)


def dot_exact(a, b):
    return jnp.dot(a, b, precision=PRECISE, preferred_element_type=f32)


def gelu_exact(values):
    return jax.nn.gelu(values, approximate=False)


def gelu_slope(values):
    result, pullback = jax.vjp(gelu_exact, values)
    return pullback(jnp.ones_like(result))[0]


def bit_count(size):
    count = size.bit_length() - 1
    assert 1 << count == size
    return count


def swap_mask(values, axis, mask):
    size = lax.axis_size(axis)
    return lax.ppermute(values, axis, [(i, i ^ mask) for i in range(size)])


def gather_masked(values, axis, order):
    pieces = {0: values}
    for bit in order:
        arrived = {m | (1 << bit): swap_mask(v, axis, 1 << bit) for m, v in pieces.items()}
        pieces.update(arrived)
    return [pieces[m] for m in range(len(pieces))]


def scatter_masked(pieces, axis, order, link=bf16):
    pieces = dict(enumerate(pieces))
    for bit in order:
        flag = 1 << bit
        for m in [m for m in pieces if m & flag]:
            arrived = swap_mask(pieces.pop(m).astype(link), axis, flag)
            pieces[m ^ flag] = pieces[m ^ flag].astype(f32) + arrived.astype(f32)
    return pieces[0]


def core_orders():
    bits = list(range(bit_count(lax.axis_size("dp"))))
    return bits, bits[1:] + bits[:1]


def place_mask(place):
    masks = []
    for order in core_orders():
        masks.append(sum(1 << bit for at, bit in enumerate(order) if (place >> at) & 1))
    return jnp.where(lax.axis_index("mp") % 2 == 0, masks[0], masks[1])


def place_index(place):
    return lax.axis_index("dp") ^ place_mask(place)


def core_hop(values, at):
    orders, cores = core_orders(), lax.axis_size("mp")
    pairs = []
    for i in range(lax.axis_size("dp")):
        for core in range(cores):
            partner = i ^ (1 << orders[core % 2][at])
            pairs.append((i * cores + core, partner * cores + core))
    return lax.ppermute(values, ("dp", "mp"), pairs)


def group_hop(pieces, at):
    return jnp.concatenate([pieces, core_hop(pieces, at)], axis=0)


def place_of(core):
    partner = jnp.arange(lax.axis_size("dp")) ^ lax.axis_index("dp")
    places = []
    for order in core_orders():
        places.append(sum(((partner >> bit) & 1) << at for at, bit in enumerate(order)))
    return jnp.where(core % 2 == 0, places[0], places[1])


def reorder_masked(stacked, axis):
    count = bit_count(stacked.shape[0])
    here = lax.axis_index(axis)
    shape = stacked.shape
    values = stacked.reshape((2,) * count + shape[1:])
    for bit in range(count):
        turned = jnp.flip(values, count - 1 - bit)
        values = jnp.where(((here >> bit) & 1) == 1, turned, values)
    return values.reshape(shape)


def gather_small(values, axes):
    shape = values.shape
    values = values[None]
    for axis in reversed(axes):
        order = range(bit_count(lax.axis_size(axis)))
        stacked = jnp.stack(gather_masked(values, axis, order))
        values = reorder_masked(stacked, axis)
        values = values.reshape((-1,) + shape)
    return values


def scatter_small(values, axes):
    for axis in axes:
        size = lax.axis_size(axis)
        values = values.reshape((size, values.shape[0] // size) + values.shape[1:])
        turned = reorder_masked(values, axis)
        order = reversed(range(bit_count(size)))
        values = scatter_masked([turned[m] for m in range(size)], axis, order, f32)
    return values[0]


def line_size():
    return lax.axis_size("depth"), lax.axis_index("depth")


def fence(*values):
    return lax.optimization_barrier(values)


class LineGather:

    def __init__(self, values):
        self.up, self.down = [values], [values]

    def step(self):
        size, _ = line_size()
        at = len(self.up)
        if at < size:
            up_pairs = [(i, i + 1) for i in range(at - 1, size - 1)]
            down_pairs = [(i, i - 1) for i in range(1, size - at + 1)]
            self.up.append(lax.ppermute(self.up[-1], "depth", up_pairs))
            self.down.append(lax.ppermute(self.down[-1], "depth", down_pairs))

    def hold(self, *others):
        kept = fence((self.up[1:], self.down[1:]), *others)
        (up, down), rest = kept[0], kept[1:]
        self.up, self.down = self.up[:1] + list(up), self.down[:1] + list(down)
        return rest

    def placed_early(self):
        size, here = line_size()
        steps = jnp.arange(size)
        index = lax.rem(here - steps + size, size)
        own = self.up[0]
        blocks = self.up[: size - 1] + [own]
        instead = [own] + self.down[1 : size - 1][::-1]
        return place_line(index, here >= steps, blocks, instead)

    def farthest(self, early):
        size, here = line_size()
        last = jnp.where(here == size - 1, self.up[size - 1], early[:, 0])
        return jnp.where(here == 0, self.down[size - 1], last), jnp.where(here == 0, size - 1, 0)

    def placed(self):
        size, here = line_size()
        steps = jnp.arange(size)
        index = lax.rem(here - steps + size, size)
        return place_line(index, here >= steps, self.up, self.down[1:][::-1])


class LineScatter:

    def __init__(self, terms):
        self.terms, self.at = terms, 0
        self.up = self.down = None

    def step(self, *later):
        size, here = line_size()
        self.at += 1
        if self.at >= size:
            return later
        goes_up, goes_down = hop_sums(
            self.terms,
            jnp.minimum(size - self.at + here, size - 1),
            jnp.maximum(here - size + self.at, 0),
            self.up,
            self.down,
            [here < self.at, here > size - 1 - self.at],
        )
        (goes_up, goes_down), *later = fence((goes_up, goes_down), *later)
        up_pairs = [(i, i + 1) for i in range(min(self.at, size - 1))]
        down_pairs = [(size - 1 - i, size - 2 - i) for i in range(min(self.at, size - 1))]
        self.up = lax.ppermute(goes_up, "depth", up_pairs)
        self.down = lax.ppermute(goes_down, "depth", down_pairs)
        return later

    def step_with(self, line, *later):
        size, here = line_size()
        lead, _, tall, wide = self.terms.shape
        shape = line.up[0].shape
        if (
            len(line.up) != self.at + 2
            or self.at + 2 > size - 1
            or math.prod(shape) != lead * tall * wide
            or shape[2] != wide
        ):
            line.step()
            return self.step(*later)
        self.at += 1
        goes = hop_sums(
            self.terms,
            jnp.minimum(size - self.at + here, size - 1),
            jnp.maximum(here - size + self.at, 0),
            self.up,
            self.down,
            [here < self.at, here > size - 1 - self.at],
            [v[-1].reshape(lead, tall, wide) for v in (line.up, line.down)],
        )
        goes, *later = fence(goes, *later)
        self.up = lax.ppermute(goes[0], "depth", [(i, i + 1) for i in range(size - 1)])
        self.down = lax.ppermute(goes[1], "depth", [(i, i - 1) for i in range(1, size)])
        line.up.append(self.up.reshape(shape))
        line.down.append(self.down.reshape(shape))
        return later

    def hold(self, *others):
        (self.up, self.down), *rest = fence((self.up, self.down), *others)
        return rest


def other_core(values):
    return swap_mask(values, "mp", 1)


def join_kernel(model_ref, own_ref, other_ref, out_ref):
    width = own_ref.shape[1]
    own_at = pl.multiple_of(model_ref[0] * width, width)
    other_at = pl.multiple_of((1 - model_ref[0]) * width, width)
    out_ref[:, pl.ds(own_at, width)] = own_ref[...]
    out_ref[:, pl.ds(other_at, width)] = other_ref[...]


def join_halves(own, other, model_at):
    tall, width = own.shape
    rows = min(256, tall)
    return pl.pallas_call(
        join_kernel,
        grid_spec=pltpu.PrefetchScalarGridSpec(
            num_scalar_prefetch=1,
            grid=(tall // rows,),
            in_specs=[pl.BlockSpec((rows, width), lambda i, m: (i, 0))] * 2,
            out_specs=pl.BlockSpec((rows, 2 * width), lambda i, m: (i, 0)),
        ),
        out_shape=jax.ShapeDtypeStruct((tall, 2 * width), own.dtype),
        cost_estimate=spent(
            flops=0, bytes_accessed=8 * tall * width, transcendentals=0
        ),
        name="join_halves",
    )(model_at.astype(jnp.int32)[None], own, other)


def spent(flops, bytes_accessed, transcendentals):
    return pl.CostEstimate(
        flops=flops // COST, bytes_accessed=bytes_accessed // COST, transcendentals=transcendentals // COST
    )


def chunk_of(tall, wide):
    rows = tall
    while rows * wide > 1 << 19 and rows % 32 == 0:
        rows //= 2
    return rows


def place_kernel(at_ref, *refs):
    if len(refs) < 4:
        refs[-1][0, 0] = refs[0][0]
        return

    @pl.when(at_ref[1] == 1)
    def _():
        refs[-1][0, 0] = refs[0][0]

    @pl.when(at_ref[1] == 0)
    def _():
        refs[-1][0, 0] = refs[1][0]


def place_block(buffer, block, index, count, instead=None, first=None):
    lead, tall, wide = block.shape
    rows = chunk_of(tall, wide)
    spec = pl.BlockSpec((1, rows, wide), lambda l, i, m: (l, i, 0))
    blocks = [block] if instead is None else [block, instead]
    where = [index, 1 if first is None else first]
    where = jnp.stack([jnp.asarray(v).astype(jnp.int32) for v in where])
    in_specs, operands, aliases = [spec] * len(blocks), list(blocks), {}
    if buffer is not None or instead is not None:
        in_specs.append(pl.BlockSpec(memory_space=pl.ANY))
        operands.append(block if buffer is None else buffer)
        aliases = {} if buffer is None else {len(operands): 0}
    return pl.pallas_call(
        place_kernel,
        grid_spec=pltpu.PrefetchScalarGridSpec(
            num_scalar_prefetch=1,
            grid=(lead, tall // rows),
            in_specs=in_specs,
            out_specs=pl.BlockSpec((1, 1, rows, wide), lambda l, i, m: (l, m[0], i, 0)),
        ),
        out_shape=jax.ShapeDtypeStruct((lead, count, tall, wide), block.dtype),
        input_output_aliases=aliases,
        cost_estimate=spent(
            flops=0, bytes_accessed=4 * lead * tall * wide, transcendentals=0
        ),
        name="place_block",
    )(where, *operands)


def place_line_kernel(size, at_ref, *refs):
    out_ref = refs[-1]
    for step in range(size):
        if step == 0 or len(refs) == size + 1:
            out_ref[0, at_ref[step]] = refs[step][0]
            continue

        @pl.when(at_ref[size + step] == 1)
        def _(step=step):
            out_ref[0, at_ref[step]] = refs[step][0]

        @pl.when(at_ref[size + step] == 0)
        def _(step=step):
            out_ref[0, at_ref[step]] = refs[size + step - 1][0]


def place_line(index, first, blocks, instead):
    size = len(blocks)
    lead, tall, wide = blocks[0].shape
    rows = tall
    while rows * wide > 1 << 18 and rows % 32 == 0:
        rows //= 2
    spec = pl.BlockSpec((1, rows, wide), lambda l, i, m: (l, i, 0))
    where = jnp.concatenate([index, first]).astype(jnp.int32)
    operands = list(blocks) + list(instead)
    return pl.pallas_call(
        functools.partial(place_line_kernel, size),
        grid_spec=pltpu.PrefetchScalarGridSpec(
            num_scalar_prefetch=1,
            grid=(lead, tall // rows),
            in_specs=[spec] * len(operands),
            out_specs=pl.BlockSpec((1, size, rows, wide), lambda l, i, m: (l, 0, i, 0)),
        ),
        out_shape=jax.ShapeDtypeStruct((lead, size, tall, wide), blocks[0].dtype),
        compiler_params=pltpu.CompilerParams(vmem_limit_bytes=40 << 20),
        cost_estimate=spent(
            flops=0, bytes_accessed=6 * size * lead * tall * wide, transcendentals=0
        ),
        name="place_line",
    )(where, *operands)


def place_many(index, blocks):
    ones = jnp.ones(len(blocks), jnp.int32)
    return place_line(index, ones, blocks, [])


def group_join_kernel(at_ref, own_ref, other_ref, out_ref):
    width = own_ref.shape[2]
    own_span, other_span = own_spans(at_ref, width)
    out_ref[:, own_span] = own_ref[0]
    out_ref[:, other_span] = other_ref[0]


def group_join(own, other, model_at):
    count, tall, width = own.shape
    rows = chunk_of(tall, width)
    per = tall // rows
    where = jnp.concatenate([model_at[None], place_of(model_at), place_of(1 - model_at)])
    return pl.pallas_call(
        group_join_kernel,
        grid_spec=pltpu.PrefetchScalarGridSpec(
            num_scalar_prefetch=1,
            grid=(count, per),
            in_specs=[
                pl.BlockSpec((1, rows, width), lambda n, i, m: (m[1 + n], i, 0)),
                pl.BlockSpec((1, rows, width), lambda n, i, m: (m[1 + count + n], i, 0)),
            ],
            out_specs=pl.BlockSpec((rows, 2 * width), lambda n, i, m: (n * per + i, 0)),
        ),
        out_shape=jax.ShapeDtypeStruct((count * tall, 2 * width), own.dtype),
        cost_estimate=spent(
            flops=0, bytes_accessed=8 * count * tall * width, transcendentals=0
        ),
        name="group_join",
    )(where.astype(jnp.int32), own, other)


def group_split_kernel(at_ref, near_own, near_other, far_own, far_other, near_ref, far_ref):
    near_ref[0, 0] = near_own[0] + near_other[0].astype(f32)
    far_ref[0, 0] = (far_own[0] + far_other[0].astype(f32)).astype(bf16)


def group_split(own, other, places):
    _, tall, width = own.shape
    count = places.shape[0]
    half, rows = count // 2, tall // count
    near = pl.BlockSpec((1, rows, width), lambda p, k, m: (k, m[p], 0))
    far = pl.BlockSpec((1, rows, width), lambda p, k, m: (k, m[half + p], 0))
    out = pl.BlockSpec((1, 1, rows, width), lambda p, k, m: (p, k, 0, 0))
    return pl.pallas_call(
        group_split_kernel,
        grid_spec=pltpu.PrefetchScalarGridSpec(
            num_scalar_prefetch=1,
            grid=(half, 2),
            in_specs=[near, near, far, far],
            out_specs=[out, out],
        ),
        out_shape=[
            jax.ShapeDtypeStruct((half, 2, rows, width), f32),
            jax.ShapeDtypeStruct((half, 2, rows, width), bf16),
        ],
        cost_estimate=spent(
            flops=2 * tall * width, bytes_accessed=20 * tall * width, transcendentals=0
        ),
        name="group_split",
    )(places, own, other, own, other)


def hop_kernel(has_sums, has_blocks, at_ref, *refs):
    ins, outs = list(refs[:-2]), refs[-2:]
    terms, ins = ins[:2], ins[2:]
    sums, ins = (ins[:2], ins[2:]) if has_sums else (None, ins)

    def send_sum(way):
        term = terms[way][:, 0].astype(f32)
        if sums is not None:
            term = term + sums[way][...].astype(f32)
        outs[way][...] = term.astype(bf16)

    for way in range(2):
        if not has_blocks:
            send_sum(way)
            continue
        pl.when(at_ref[2 + way] == 1)(functools.partial(send_sum, way))

        @pl.when(at_ref[2 + way] == 0)
        def _(way=way):
            outs[way][...] = ins[way][...]


def hop_sums(terms, up_at, down_at, up, down, sends, blocks=None):
    lead, _, tall, wide = terms.shape
    rows = chunk_of(tall, wide)
    deep = lead
    while deep * rows * wide > 1 << 19 and deep % 2 == 0:
        deep //= 2
    block = pl.BlockSpec((deep, rows, wide), lambda l, i, m: (l, i, 0))

    def term_spec(way):
        return pl.BlockSpec(
            (deep, 1, rows, wide), lambda l, i, m: (l * m[2 + way], m[way], i * m[2 + way], 0)
        )

    def block_spec(way, sign):
        def index(l, i, m):
            need = m[2 + way] if sign else 1 - m[2 + way]
            return (l * need, i * need, 0)

        return pl.BlockSpec((deep, rows, wide), index)

    in_specs = [term_spec(0), term_spec(1)]
    operands = [terms, terms]
    if up is not None:
        in_specs += [block_spec(0, True), block_spec(1, True)]
        operands += [up, down]
    if blocks is not None:
        in_specs += [block_spec(0, False), block_spec(1, False)]
        operands += list(blocks)
    return pl.pallas_call(
        functools.partial(hop_kernel, up is not None, blocks is not None),
        grid_spec=pltpu.PrefetchScalarGridSpec(
            num_scalar_prefetch=1,
            grid=(lead // deep, tall // rows),
            in_specs=in_specs,
            out_specs=[block, block],
        ),
        out_shape=[jax.ShapeDtypeStruct((lead, tall, wide), bf16)] * 2,
        cost_estimate=spent(
            flops=2 * lead * tall * wide, bytes_accessed=12 * lead * tall * wide, transcendentals=0
        ),
        compiler_params=pltpu.CompilerParams(vmem_limit_bytes=40 << 20),
        name="hop_sums",
    )(jnp.stack([up_at, down_at, *sends]).astype(jnp.int32), *operands)


def end_kernel(at_ref, term_ref, up_ref, down_ref, out_ref):
    total = term_ref[0, 0].astype(f32) + up_ref[0].astype(f32) + down_ref[0].astype(f32)
    out_ref[0] = total.astype(out_ref.dtype)


def end_sums(sums, dtype):
    lead, _, tall, wide = sums.terms.shape
    rows = chunk_of(tall, wide)
    block = pl.BlockSpec((1, rows, wide), lambda l, i, m: (l, i, 0))
    return pl.pallas_call(
        end_kernel,
        grid_spec=pltpu.PrefetchScalarGridSpec(
            num_scalar_prefetch=1,
            grid=(lead, tall // rows),
            in_specs=[
                pl.BlockSpec((1, 1, rows, wide), lambda l, i, m: (l, m[0], i, 0)),
                block,
                block,
            ],
            out_specs=block,
        ),
        out_shape=jax.ShapeDtypeStruct((lead, tall, wide), dtype),
        cost_estimate=spent(
            flops=2 * lead * tall * wide, bytes_accessed=10 * lead * tall * wide, transcendentals=0
        ),
        name="end_sums",
    )(lax.axis_index("depth").astype(jnp.int32)[None], sums.terms, sums.up, sums.down)


def attention_grad_kernel(
    at_ref, x0_ref, x1_ref, cot_ref, g0_ref, g1_ref, out_ref
):
    tall = x0_ref.shape[1]

    def store(total):
        out_ref[...] = total.reshape(out_ref.shape).astype(out_ref.dtype)

    @pl.when(pl.program_id(0) < 3)
    def _():
        store(dot_tn(x0_ref[0], g0_ref[0]) + dot_tn(x1_ref[0], g1_ref[0]))

    @pl.when(pl.program_id(0) == 3)
    def _():
        store(
            dot_tn(cot_ref[0:tall, :], g0_ref[0]) + dot_tn(cot_ref[tall : 2 * tall, :], g1_ref[0])
        )


def attention_grads(normed, cot, flat, place, depth_count, dp_count, dtype):
    _, tall, model = normed[0].shape
    heads_width = flat[0].shape[2]
    block = model // dp_count
    own_rows = block // depth_count
    normed_spec = pl.BlockSpec((1, tall, block), lambda k, m: (jnp.minimum(k, 2), 0, m[0]))
    flat_spec = pl.BlockSpec((1, tall, heads_width), lambda k, m: (lax.rem(k + 1, 4), 0, 0))
    return pl.pallas_call(
        attention_grad_kernel,
        grid_spec=pltpu.PrefetchScalarGridSpec(
            num_scalar_prefetch=1,
            grid=(4,),
            in_specs=[
                normed_spec,
                normed_spec,
                pl.BlockSpec((2 * tall, block), lambda k, m: (0, m[0])),
                flat_spec,
                flat_spec,
            ],
            out_specs=pl.BlockSpec(
                (depth_count, 1, own_rows, heads_width), lambda k, m: (0, k, 0, 0)
            ),
        ),
        out_shape=jax.ShapeDtypeStruct((depth_count, 4, own_rows, heads_width), dtype),
        compiler_params=pltpu.CompilerParams(vmem_limit_bytes=40 << 20),
        cost_estimate=spent(
            flops=16 * tall * block * heads_width,
            bytes_accessed=16 * block * heads_width,
            transcendentals=0,
        ),
        name="attention_grads",
    )(place, *normed, cot, *flat)


def hidden_grad_kernel(x0_ref, x1_ref, c0_ref, c1_ref, u0_ref, u1_ref, h0_ref, h1_ref, out_ref):
    def store(total):
        out_ref[...] = total.reshape(out_ref.shape).astype(bf16)

    @pl.when(pl.program_id(0) == 0)
    def _():
        store(dot_tn(x0_ref[...], u0_ref[...]) + dot_tn(x1_ref[...], u1_ref[...]))

    @pl.when(pl.program_id(0) == 1)
    def _():
        tall, wide = h0_ref.shape[0], c0_ref.shape[3]
        c0, c1 = c0_ref[:, 0].reshape(tall, wide), c1_ref[:, 0].reshape(tall, wide)
        store(dot_tn(c0, h0_ref[...]) + dot_tn(c1, h1_ref[...]))


def hidden_grads(x, cot, up_grads, hidden, dp_count, depth_count):
    tall, model = x[0].shape
    part = hidden[0].shape[1]
    block = model // dp_count
    cols = pl.BlockSpec((tall, block), lambda k, n: (0, n * (1 - k)))
    whole = pl.BlockSpec((tall, part), lambda k, n: (0, 0))
    return pl.pallas_call(
        hidden_grad_kernel,
        grid=(2, dp_count),
        in_specs=[cols, cols]
        + [
            pl.BlockSpec((dp_count, 1, cot.shape[2], block), lambda k, n: (0, 0, 0, n * k)),
            pl.BlockSpec((dp_count, 1, cot.shape[2], block), lambda k, n: (0, 1, 0, n * k)),
        ]
        + [whole] * 4,
        out_specs=pl.BlockSpec(
            (1, depth_count, block // depth_count, part), lambda k, n: (k * dp_count + n, 0, 0, 0)
        ),
        out_shape=jax.ShapeDtypeStruct(
            (2 * dp_count, depth_count, block // depth_count, part), bf16
        ),
        compiler_params=pltpu.CompilerParams(vmem_limit_bytes=48 << 20),
        cost_estimate=spent(
            flops=8 * tall * model * part, bytes_accessed=8 * model * part, transcendentals=0
        ),
        name="hidden_grads",
    )(*x, cot, cot, *up_grads, *hidden)


def mix_kernel(slots, mix_ref, hist_ref, out_ref):
    rows, width = hist_ref.shape[1], hist_ref.shape[2]
    part = 512 if width % 512 == 0 else width

    def step(at, carry):
        r0 = pl.multiple_of(at * 16, 16)
        weights = mix_ref[pl.ds(r0, 16), :]
        for c0 in range(0, width, part):
            sums = [None] * STREAMS
            for k in range(slots):
                state = hist_ref[k, pl.ds(r0, 16), c0 : c0 + part].astype(f32)
                for s in range(STREAMS):
                    term = weights[:, s * slots + k : s * slots + k + 1] * state
                    sums[s] = term if sums[s] is None else sums[s] + term
            for s in range(STREAMS):
                out_ref[s, pl.ds(r0, 16), c0 : c0 + part] = sums[s].astype(bf16)
        return carry

    lax.fori_loop(0, rows // 16, step, 0)


def mix_streams(slot_mix, history, micro_at, depth_count, rows_mb):
    slots, _, width = history.shape
    rows = min(128, rows_mb)
    per = rows_mb // rows

    def row_block(i):
        return ((i // per) * MB + micro_at) * per + i % per

    return pl.pallas_call(
        functools.partial(mix_kernel, slots),
        grid=(depth_count * per,),
        in_specs=[
            pl.BlockSpec((rows, slot_mix.shape[1]), lambda i: (row_block(i), 0)),
            pl.BlockSpec((slots, rows, width), lambda i: (0, row_block(i), 0)),
        ],
        out_specs=pl.BlockSpec((STREAMS, rows, width), lambda i: (0, i, 0)),
        out_shape=jax.ShapeDtypeStruct((STREAMS, depth_count * rows_mb, width), bf16),
        cost_estimate=spent(
            flops=2 * slots * STREAMS * depth_count * rows_mb * width,
            bytes_accessed=2 * (slots + STREAMS) * depth_count * rows_mb * width,
            transcendentals=0,
        ),
        name="mix_streams",
    )(slot_mix, history)


def unmix_kernel(slots, mix_ref, hist_ref, grad_ref, *rest):
    hist_grad_ref, slot_grad_ref = rest[-2:]
    rows, width = hist_ref.shape[1], hist_ref.shape[2]
    part = 512 if width % 512 == 0 else width

    def step(at, carry):
        r0 = pl.multiple_of(at * 16, 16)
        weights = mix_ref[pl.ds(r0, 16), :]
        totals = [None] * (STREAMS * slots)
        for c0 in range(0, width, part):
            grads = [
                grad_ref[s, pl.ds(r0, 16), c0 : c0 + part].astype(f32)
                for s in range(STREAMS)
            ]
            for k in range(slots):
                state = hist_ref[k, pl.ds(r0, 16), c0 : c0 + part].astype(f32)
                back = None
                for s in range(STREAMS):
                    at_sk = s * slots + k
                    term = weights[:, at_sk : at_sk + 1] * grads[s]
                    back = term if back is None else back + term
                    product = state * grads[s]
                    folded = product[:, 0:128]
                    for l0 in range(128, part, 128):
                        folded = folded + product[:, l0 : l0 + 128]
                    totals[at_sk] = folded if totals[at_sk] is None else totals[at_sk] + folded
                hist_grad_ref[k, pl.ds(r0, 16), c0 : c0 + part] = back.astype(bf16)
        lane = lax.broadcasted_iota(jnp.int32, (16, 128), 1)
        packed = jnp.zeros((16, 128), f32)
        for at_sk in range(STREAMS * slots):
            column = jnp.sum(totals[at_sk], axis=1, keepdims=True)
            packed = jnp.where(lane == at_sk, column, packed)
        slot_grad_ref[pl.ds(r0, 16), :] = packed
        return carry

    lax.fori_loop(0, rows // 16, step, 0)


def unmix_streams(slot_mix, history, grads, micro_at, depth_count, rows_mb, earlier):
    slots, tokens, width = history.shape
    rows = min(128, rows_mb)
    per = rows_mb // rows

    def row_block(i):
        return ((i // per) * MB + micro_at) * per + i % per

    in_specs = [
        pl.BlockSpec((rows, slot_mix.shape[1]), lambda i: (row_block(i), 0)),
        pl.BlockSpec((slots, rows, width), lambda i: (0, row_block(i), 0)),
        pl.BlockSpec((STREAMS, rows, width), lambda i: (0, i, 0)),
    ]
    operands = [slot_mix, history, grads]
    aliases = {}
    if earlier is not None:
        in_specs.append(pl.BlockSpec(memory_space=pl.ANY))
        operands.append(earlier)
        aliases = {3: 0}
    return pl.pallas_call(
        functools.partial(unmix_kernel, slots),
        grid=(depth_count * per,),
        in_specs=in_specs,
        out_specs=[
            pl.BlockSpec((slots, rows, width), lambda i: (0, row_block(i), 0)),
            pl.BlockSpec((rows, 128), lambda i: (i, 0)),
        ],
        out_shape=[
            jax.ShapeDtypeStruct((slots, tokens, width), bf16),
            jax.ShapeDtypeStruct((depth_count * rows_mb, 128), f32),
        ],
        input_output_aliases=aliases,
        cost_estimate=spent(
            flops=4 * slots * STREAMS * depth_count * rows_mb * width,
            bytes_accessed=2 * (2 * slots + STREAMS) * depth_count * rows_mb * width,
            transcendentals=0,
        ),
        name="unmix_streams",
    )(*operands)


def unmix_one(slot_mix, history, grads, micro_at, index, rows_mb, earlier):
    slots, tokens, width = history.shape
    rows = min(128, rows_mb)
    per = rows_mb // rows

    def row_block(i, m):
        return (m[0] * MB + micro_at) * per + i

    def kernel(at_ref, *refs):
        unmix_kernel(slots, *refs)

    return pl.pallas_call(
        kernel,
        grid_spec=pltpu.PrefetchScalarGridSpec(
            num_scalar_prefetch=1,
            grid=(per,),
            in_specs=[
                pl.BlockSpec((rows, slot_mix.shape[1]), lambda i, m: (row_block(i, m), 0)),
                pl.BlockSpec((slots, rows, width), lambda i, m: (0, row_block(i, m), 0)),
                pl.BlockSpec((STREAMS, rows, width), lambda i, m: (0, i, 0)),
                pl.BlockSpec(memory_space=pl.ANY),
            ],
            out_specs=[
                pl.BlockSpec((slots, rows, width), lambda i, m: (0, row_block(i, m), 0)),
                pl.BlockSpec((rows, 128), lambda i, m: (i, 0)),
            ],
        ),
        out_shape=[
            jax.ShapeDtypeStruct((slots, tokens, width), bf16),
            jax.ShapeDtypeStruct((rows_mb, 128), f32),
        ],
        input_output_aliases={4: 0},
        cost_estimate=spent(
            flops=4 * slots * STREAMS * rows_mb * width,
            bytes_accessed=2 * (2 * slots + STREAMS) * rows_mb * width,
            transcendentals=0,
        ),
        name="unmix_one",
    )(index.astype(jnp.int32)[None], slot_mix, history, grads, earlier)


def own_spans(model_ref, width):
    own_at = pl.multiple_of(model_ref[0] * width, width)
    other_at = pl.multiple_of((1 - model_ref[0]) * width, width)
    return pl.ds(own_at, width), pl.ds(other_at, width)


def ff_split_kernel(at_ref, up_ref, down_ref, out_ref):
    out_ref[0, 0] = up_ref[...]
    out_ref[0, 1] = down_ref[...].T


def ff_split(up_weight, down_weight, partners):
    own_rows, ff_width = up_weight.shape
    count = partners.shape[0]
    part = ff_width // count
    return pl.pallas_call(
        ff_split_kernel,
        grid_spec=pltpu.PrefetchScalarGridSpec(
            num_scalar_prefetch=1,
            grid=(count,),
            in_specs=[
                pl.BlockSpec((own_rows, part), lambda i, m: (0, m[i])),
                pl.BlockSpec((part, own_rows), lambda i, m: (m[i], 0)),
            ],
            out_specs=pl.BlockSpec((1, 2, own_rows, part), lambda i, m: (i, 0, 0, 0)),
        ),
        out_shape=jax.ShapeDtypeStruct((count, 2, own_rows, part), bf16),
        cost_estimate=spent(flops=0, bytes_accessed=8 * own_rows * ff_width, transcendentals=0),
        name="ff_split",
    )(partners, up_weight, down_weight)


def ff_join_kernel(at_ref, piece_ref, up_ref, down_ref):
    up_ref[...] = piece_ref[0, 0].astype(f32)
    down_ref[...] = piece_ref[0, 1].astype(f32).T


def ff_join(pieces, partners):
    count, _, own_rows, part = pieces.shape
    return pl.pallas_call(
        ff_join_kernel,
        grid_spec=pltpu.PrefetchScalarGridSpec(
            num_scalar_prefetch=1,
            grid=(count,),
            in_specs=[pl.BlockSpec((1, 2, own_rows, part), lambda i, m: (i, 0, 0, 0))],
            out_specs=[
                pl.BlockSpec((own_rows, part), lambda i, m: (0, m[i])),
                pl.BlockSpec((part, own_rows), lambda i, m: (m[i], 0)),
            ],
        ),
        out_shape=[
            jax.ShapeDtypeStruct((own_rows, count * part), f32),
            jax.ShapeDtypeStruct((count * part, own_rows), f32),
        ],
        cost_estimate=spent(
            flops=0, bytes_accessed=12 * own_rows * count * part, transcendentals=0
        ),
        name="ff_join",
    )(partners, pieces)


def total_kernel(depth_ref, part_ref, up_ref, down_ref, cur_ref, last_ref, low_ref, resid_ref):
    width = resid_ref.shape[1]
    current = cur_ref[...].astype(f32)
    for s in range(STREAMS):
        lanes = slice(s * width, (s + 1) * width)
        total = part_ref[s, 0].astype(f32)
        total = total + up_ref[s].astype(f32) + down_ref[s].astype(f32)
        total = total + last_ref[:, s : s + 1] * current
        if s == STREAMS - 1:
            resid_ref[...] = total
        low_ref[:, lanes] = total.astype(bf16)


def total_streams(sums, current_half, last, depth_at):
    _, _, tall, width = sums.terms.shape
    wide = STREAMS * width
    rows = min(64, tall)
    row = lambda i, d: (i, 0)
    return pl.pallas_call(
        total_kernel,
        grid_spec=pltpu.PrefetchScalarGridSpec(
            num_scalar_prefetch=1,
            grid=(tall // rows,),
            in_specs=[
                pl.BlockSpec((STREAMS, 1, rows, width), lambda i, d: (0, d[0], i, 0)),
                pl.BlockSpec((STREAMS, rows, width), lambda i, d: (0, i, 0)),
                pl.BlockSpec((STREAMS, rows, width), lambda i, d: (0, i, 0)),
                pl.BlockSpec((rows, width), row),
                pl.BlockSpec((rows, 128), row),
            ],
            out_specs=[pl.BlockSpec((rows, wide), row), pl.BlockSpec((rows, width), row)],
        ),
        out_shape=[
            jax.ShapeDtypeStruct((tall, wide), bf16),
            jax.ShapeDtypeStruct((tall, width), f32),
        ],
        cost_estimate=spent(flops=5 * tall * wide, bytes_accessed=9 * tall * wide, transcendentals=0),
        name="total_streams",
    )(depth_at, sums.terms, sums.up, sums.down, current_half, last)


def norm_kernel(model_ref, own_ref, other_ref, gain_ref, normed_ref, ff_ref, stat_ref):
    rows, width = ff_ref.shape
    model = 2 * width
    own_span, other_span = own_spans(model_ref, width)
    lane = lax.broadcasted_iota(jnp.int32, (rows, 128), 1)
    stats = jnp.zeros((rows, 128), f32)
    for s in range(STREAMS):
        lanes = slice(s * width, (s + 1) * width)
        own = own_ref[:, lanes].astype(f32)
        other = other_ref[:, lanes].astype(f32)
        average = (
            jnp.sum(own, axis=-1, keepdims=True) + jnp.sum(other, axis=-1, keepdims=True)
        ) / model
        own, other = own - average, other - average
        variance = (
            jnp.sum(own * own, axis=-1, keepdims=True)
            + jnp.sum(other * other, axis=-1, keepdims=True)
        ) / model
        inverse = lax.rsqrt(variance + NORM_EPSILON)
        stats = jnp.where(lane == 2 * s, average, stats)
        stats = jnp.where(lane == 2 * s + 1, inverse, stats)
        norm_own = (own * inverse * gain_ref[s : s + 1, own_span]).astype(bf16)
        if s == STREAMS - 1:
            ff_ref[...] = norm_own
        else:
            normed_ref[s, :, own_span] = norm_own
            norm_other = (other * inverse * gain_ref[s : s + 1, other_span]).astype(bf16)
            normed_ref[s, :, other_span] = norm_other
    stat_ref[...] = stats


def norm_streams(low, low_other, gains, which):
    tall, wide = low.shape
    width = wide // STREAMS
    rows = min(64, tall)
    row = lambda i, m: (i, 0)
    return pl.pallas_call(
        norm_kernel,
        grid_spec=pltpu.PrefetchScalarGridSpec(
            num_scalar_prefetch=1,
            grid=(tall // rows,),
            in_specs=[
                pl.BlockSpec((rows, wide), row),
                pl.BlockSpec((rows, wide), row),
                pl.BlockSpec(gains.shape, lambda i, m: (0, 0)),
            ],
            out_specs=[
                pl.BlockSpec((3, rows, 2 * width), lambda i, m: (0, i, 0)),
                pl.BlockSpec((rows, width), row),
                pl.BlockSpec((rows, 128), row),
            ],
        ),
        out_shape=[
            jax.ShapeDtypeStruct((3, tall, 2 * width), bf16),
            jax.ShapeDtypeStruct((tall, width), bf16),
            jax.ShapeDtypeStruct((tall, 128), f32),
        ],
        cost_estimate=spent(
            flops=20 * tall * wide, bytes_accessed=8 * tall * wide, transcendentals=0
        ),
        name="norm_streams",
    )(which, low, low_other, gains)


def turn(values, cosine, sine_up, sine_down, sign):
    up = pltpu.roll(values, HDIM - ROT // 2, 1)
    down = pltpu.roll(values, ROT // 2, 1)
    return values * cosine + sign * (up * sine_up + down * sine_down)


def project_kernel(
    x_ref, cot_ref, wq_ref, wk_ref, wv_ref, wo_ref, cos_ref, up_ref, down_ref, out_ref
):
    span = wq_ref.shape[-1]
    tables = cos_ref[...], up_ref[...], down_ref[...]
    for kind, w_ref in enumerate((wq_ref, wk_ref, wv_ref, wo_ref)):
        rows = cot_ref[...] if kind == 3 else x_ref[kind]
        product = dot_nn(rows, w_ref[...].reshape(-1, span))
        for begin in range(0, span, HDIM):
            head = product[:, begin : begin + HDIM]
            if kind < 2:
                head = turn(head, *tables, 1.0)
            out_ref[0, :, kind * span + begin : kind * span + begin + HDIM] = head.astype(bf16)


def project_heads(normed, cot, weights, tables, depth_count):
    _, rows, model = normed.shape
    groups, _, _, own_rows, heads_width = weights.shape
    span = heads_width // depth_count
    whole = lambda j: (0, 0)

    def matrix(kind):
        shape = (groups, depth_count, 1, own_rows, span)
        return pl.BlockSpec(shape, lambda j: (0, 0, kind, 0, j))

    return pl.pallas_call(
        project_kernel,
        grid=(depth_count,),
        in_specs=[
            pl.BlockSpec((3, rows, model), lambda j: (0, 0, 0)),
            pl.BlockSpec((rows, model), whole),
        ]
        + [matrix(kind) for kind in range(4)]
        + [pl.BlockSpec((rows, HDIM), whole)] * 3,
        out_specs=pl.BlockSpec((1, rows, 4 * span), lambda j: (j, 0, 0)),
        out_shape=jax.ShapeDtypeStruct((depth_count, rows, 4 * span), bf16),
        compiler_params=pltpu.CompilerParams(vmem_limit_bytes=40 << 20),
        cost_estimate=spent(
            flops=8 * rows * model * span * depth_count,
            bytes_accessed=8 * model * span * depth_count + 8 * rows * model,
            transcendentals=0,
        ),
        name="project_heads",
    )(normed, cot, *[weights] * 4, *tables)


def attend_kernel(
    block, q_ref, k_ref, v_ref, g_ref, doc_col_ref, doc_row_ref, cos_ref, up_ref, down_ref,
    out_ref, dk_sum, dv_sum,
):
    length = q_ref.shape[0]
    scale = HDIM**-0.5
    heads_each = out_ref.shape[1] // (4 * HDIM)

    def lanes(kind):
        return pl.ds(pl.multiple_of((kind * heads_each + pl.program_id(0)) * HDIM, HDIM), HDIM)

    for begin in range(0, length, block):
        end = begin + block
        rows = slice(begin, end)
        queries, grads = q_ref[rows, :], g_ref[rows, :]
        keys, values = k_ref[0:end, :], v_ref[0:end, :]
        scores = dot_nt(queries, keys) * scale
        place_q = begin + lax.broadcasted_iota(jnp.int32, scores.shape, 0)
        place_k = lax.broadcasted_iota(jnp.int32, scores.shape, 1)
        allowed = (doc_col_ref[rows, :] == doc_row_ref[:, 0:end]) & (place_q >= place_k)
        scores = jnp.where(allowed, scores, MASKED)
        highest = jnp.max(scores, axis=-1, keepdims=True)
        exponent = jnp.exp(scores - highest)
        totals = jnp.sum(exponent, axis=-1, keepdims=True)
        attention = exponent * (1.0 / totals)
        low = attention.astype(bf16)
        out_ref[rows, lanes(0)] = dot_nn(low, values).astype(bf16)
        grad_att = dot_nt(grads, values).astype(bf16).astype(f32)
        weighted = jnp.sum(attention * grad_att, axis=-1, keepdims=True)
        grad_scores = (attention * (grad_att - weighted)).astype(bf16)
        grad_q = dot_nn(grad_scores, keys) * scale
        out_ref[rows, lanes(1)] = turn(
            grad_q, cos_ref[rows, :], up_ref[rows, :], down_ref[rows, :], -1.0
        ).astype(bf16)
        part_k = dot_tn(grad_scores, queries)
        part_v = dot_tn(low, grads)
        if begin > 0:
            dk_sum[0:begin, :] += part_k[0:begin]
            dv_sum[0:begin, :] += part_v[0:begin]
        dk_sum[begin:end, :] = part_k[begin:end]
        dv_sum[begin:end, :] = part_v[begin:end]
    grad_k = dk_sum[...] * scale
    out_ref[:, lanes(2)] = turn(grad_k, cos_ref[...], up_ref[...], down_ref[...], -1.0).astype(bf16)
    out_ref[:, lanes(3)] = dv_sum[...].astype(bf16)


def attend(packed, documents, tables, heads_each):
    length = packed.shape[0]
    block = min(256, length)
    whole = lambda h: (0, 0)

    def kind(at):
        return pl.BlockSpec((length, HDIM), lambda h: (0, at * heads_each + h))

    return pl.pallas_call(
        functools.partial(attend_kernel, block),
        grid=(heads_each,),
        in_specs=[kind(0), kind(1), kind(2), kind(3)]
        + [pl.BlockSpec((length, 1), whole), pl.BlockSpec((1, length), whole)]
        + [pl.BlockSpec((length, HDIM), whole)] * 3,
        out_specs=pl.BlockSpec((length, 4 * heads_each * HDIM), whole),
        out_shape=jax.ShapeDtypeStruct((length, 4 * heads_each * HDIM), bf16),
        scratch_shapes=[pltpu.VMEM((length, HDIM), f32)] * 2,
        compiler_params=pltpu.CompilerParams(vmem_limit_bytes=48 << 20),
        cost_estimate=spent(
            flops=9 * heads_each * length * length * HDIM,
            bytes_accessed=16 * length * heads_each * HDIM + 12 * length * HDIM,
            transcendentals=heads_each * length * length,
        ),
        name="attend",
    )(packed, packed, packed, packed, documents[:, None], documents[None, :], *tables)


def gelu_parts(values):
    cdf = 0.5 * (1.0 + lax.erf(values * (0.5**0.5)))
    density = jnp.exp(-0.5 * values * values) * (1.0 / math.sqrt(2.0 * math.pi))
    return values * cdf, cdf + values * density


def ff_kernel(
    model_ref, x_ref, cot_ref, up_ref, down_ref,
    hidden_ref, grad_ref, own_ref, other_ref,
):
    part = up_ref.shape[-1]
    half = up_ref.shape[1] // 2

    def rows_of(ref, which):
        return ref[0, pl.ds(which * half, half)].reshape(-1, part)

    own, other = model_ref[0], 1 - model_ref[0]
    up_pre = dot_nn(x_ref[...], up_ref[...].reshape(-1, part))
    hidden, slope = gelu_parts(up_pre)
    hidden = hidden.astype(bf16)
    grad_up = (dot_nn(cot_ref[0, 0], down_ref[...].reshape(-1, part)) * slope).astype(bf16)
    hidden_ref[...] = hidden
    grad_ref[...] = grad_up
    other_ref[0] = dot_nt(grad_up, rows_of(up_ref, other)).astype(bf16)
    own_ref[0] = dot_nt(grad_up, rows_of(up_ref, own))
    other_ref[1] = dot_nt(hidden, rows_of(down_ref, other)).astype(bf16)
    own_ref[1] = dot_nt(hidden, rows_of(down_ref, own))


def feed_forward(x, cot, micro_at, weights, which):
    tall, model = x.shape
    part = weights.shape[-1]
    width = model // 2
    rows = cot.shape[2]
    row = lambda i, m: (i, 0)

    def resident(kind):
        return pl.BlockSpec(
            (1,) + weights.shape[1:],
            lambda i, m: (kind, 0, 0, 0, 0),
            pipeline_mode=pl.Buffered(1),
        )

    return pl.pallas_call(
        ff_kernel,
        grid_spec=pltpu.PrefetchScalarGridSpec(
            num_scalar_prefetch=1,
            grid=(tall // rows,),
            in_specs=[
                pl.BlockSpec((rows, model), row),
                pl.BlockSpec((1, 1, rows, model), lambda i, m: (i, micro_at, 0, 0)),
                resident(0),
                resident(1),
            ],
            out_specs=[pl.BlockSpec((rows, part), row)] * 2
            + [pl.BlockSpec((2, rows, width), lambda i, m: (0, i, 0))] * 2,
        ),
        out_shape=[jax.ShapeDtypeStruct((tall, part), bf16)] * 2
        + [
            jax.ShapeDtypeStruct((2, tall, width), f32),
            jax.ShapeDtypeStruct((2, tall, width), bf16),
        ],
        compiler_params=pltpu.CompilerParams(vmem_limit_bytes=48 << 20),
        cost_estimate=spent(
            flops=8 * tall * model * part,
            bytes_accessed=4 * model * part + 16 * tall * model,
            transcendentals=2 * tall * part,
        ),
        name="feed_forward",
    )(which, x, cot, weights, weights)


def back_kernel(half_ref, ans_ref, wo_ref, wq_ref, wk_ref, wv_ref, out_ref, *flat):
    count, _, wide = ans_ref.shape
    span = wide // 4
    for kind, w_ref in enumerate((wo_ref, wq_ref, wk_ref, wv_ref)):
        total = None
        for j in range(count):
            term = dot_nt(
                ans_ref[j, :, kind * span : (kind + 1) * span],
                w_ref[:, :, :, :, j * span : (j + 1) * span].reshape(-1, span),
            )
            total = term if total is None else total + term
        out_ref[kind] = total.astype(out_ref.dtype)
    if flat:

        @pl.when(pl.program_id(0) == 0)
        def _():
            for kind in range(4):
                for j in range(count):
                    flat[0][kind, :, j * span : (j + 1) * span] = ans_ref[
                        j, :, kind * span : (kind + 1) * span
                    ]


def back_project(answer, weights, half, dtype, flat):
    count, rows, wide = answer.shape
    groups, _, _, own_rows, heads_width = weights.shape
    part = count * own_rows
    steps = groups // 2
    width = part * steps

    def matrix(kind):
        shape = (1, count, 1, own_rows, heads_width)
        return pl.BlockSpec(shape, lambda i, m: (m[0] * steps + i, 0, kind, 0, 0))

    out_specs = [pl.BlockSpec((4, rows, part), lambda i, m: (0, 0, i))]
    out_shape = [jax.ShapeDtypeStruct((4, rows, width), dtype)]
    if flat:
        out_specs.append(pl.BlockSpec((4, rows, heads_width), lambda i, m: (0, 0, 0)))
        out_shape.append(jax.ShapeDtypeStruct((4, rows, heads_width), bf16))
    return pl.pallas_call(
        back_kernel,
        grid_spec=pltpu.PrefetchScalarGridSpec(
            num_scalar_prefetch=1,
            grid=(steps,),
            in_specs=[pl.BlockSpec((count, rows, wide), lambda i, m: (0, 0, 0))]
            + [matrix(kind) for kind in (3, 0, 1, 2)],
            out_specs=out_specs,
        ),
        out_shape=out_shape,
        compiler_params=pltpu.CompilerParams(vmem_limit_bytes=40 << 20),
        cost_estimate=spent(
            flops=8 * rows * heads_width * width,
            bytes_accessed=8 * heads_width * width + 20 * rows * width,
            transcendentals=0,
        ),
        name="back_project",
    )(half, answer, *[weights] * 4)


def slope_kernel(
    model_ref, own_ref, got_ref, ff_ref, low_ref, stat_ref, gain_ref, scaled_ref, sum_ref, gain_out_ref
):
    _, rows, width = ff_ref.shape
    own_span, _ = own_spans(model_ref, width)
    lane = lax.broadcasted_iota(jnp.int32, (rows, 128), 1)
    packed = jnp.zeros((rows, 128), f32)
    totals = []
    for s in range(STREAMS):
        lanes = slice(s * width, (s + 1) * width)
        if s < 3:
            grad = own_ref[s + 1] + got_ref[s + 1].astype(f32)
        else:
            grad = ff_ref[0]
        average, inverse = stat_ref[:, 2 * s : 2 * s + 1], stat_ref[:, 2 * s + 1 : 2 * s + 2]
        hat = (low_ref[:, lanes].astype(f32) - average) * inverse
        totals.append(jnp.sum(grad * hat, axis=0, keepdims=True))
        scaled = grad * gain_ref[s : s + 1, own_span]
        scaled_ref[:, lanes] = scaled
        packed = jnp.where(lane == 2 * s, jnp.sum(scaled, axis=-1, keepdims=True), packed)
        packed = jnp.where(
            lane == 2 * s + 1, jnp.sum(scaled * hat, axis=-1, keepdims=True), packed
        )
    sum_ref[...] = packed
    totals = jnp.concatenate(totals, axis=0)

    @pl.when(pl.program_id(0) == 0)
    def _():
        gain_out_ref[...] = totals

    @pl.when(pl.program_id(0) > 0)
    def _():
        gain_out_ref[...] += totals


def norm_slopes(own, got, ff_grad, low, stats, gains, which):
    tall, wide = low.shape
    width = wide // STREAMS
    rows = min(64, tall)
    row = lambda i, m: (i, 0)
    cube = pl.BlockSpec((4, rows, width), lambda i, m: (0, i, 0))
    return pl.pallas_call(
        slope_kernel,
        grid_spec=pltpu.PrefetchScalarGridSpec(
            num_scalar_prefetch=1,
            grid=(tall // rows,),
            in_specs=[
                cube,
                cube,
                pl.BlockSpec((1, rows, width), lambda i, m: (0, i, 0)),
                pl.BlockSpec((rows, wide), row),
                pl.BlockSpec((rows, 128), row),
                pl.BlockSpec(gains.shape, lambda i, m: (0, 0)),
            ],
            out_specs=[
                pl.BlockSpec((rows, wide), row),
                pl.BlockSpec((rows, 128), row),
                pl.BlockSpec((STREAMS, width), lambda i, m: (0, 0)),
            ],
        ),
        out_shape=[
            jax.ShapeDtypeStruct((tall, wide), f32),
            jax.ShapeDtypeStruct((tall, 128), f32),
            jax.ShapeDtypeStruct((STREAMS, width), f32),
        ],
        cost_estimate=spent(
            flops=12 * tall * wide, bytes_accessed=12 * tall * wide, transcendentals=0
        ),
        name="norm_slopes",
    )(which, own, got, ff_grad, low, stats, gains)


def grads_kernel(
    scaled_ref, mine_ref, theirs_ref, low_ref, stat_ref, cot_ref, cur_ref, last_ref,
    grad_ref, mix_ref, dot_ref,
):
    rows, width = cot_ref.shape
    lane = lax.broadcasted_iota(jnp.int32, (rows, 128), 1)
    means = (mine_ref[...] + theirs_ref[...]) / (2 * width)
    current = cur_ref[...].astype(f32)
    packed = jnp.zeros((rows, 128), f32)
    mixed = None
    for s in range(STREAMS):
        lanes = slice(s * width, (s + 1) * width)
        average, inverse = stat_ref[:, 2 * s : 2 * s + 1], stat_ref[:, 2 * s + 1 : 2 * s + 2]
        hat = (low_ref[:, lanes].astype(f32) - average) * inverse
        grad = inverse * (
            scaled_ref[:, lanes]
            - means[:, 2 * s : 2 * s + 1]
            - hat * means[:, 2 * s + 1 : 2 * s + 2]
        )
        if s == STREAMS - 1:
            grad = grad + cot_ref[...].astype(f32)
        grad = grad.astype(bf16)
        grad_ref[s] = grad
        grad = grad.astype(f32)
        term = last_ref[:, s : s + 1] * grad
        mixed = term if mixed is None else mixed + term
        packed = jnp.where(lane == s, jnp.sum(grad * current, axis=-1, keepdims=True), packed)
    mix_ref[...] = mixed
    dot_ref[...] = packed


def stream_grads(scaled, mine, theirs, low, stats, cot, current_half, last):
    tall, wide = low.shape
    width = wide // STREAMS
    rows = min(64, tall)
    row = lambda i: (i, 0)
    return pl.pallas_call(
        grads_kernel,
        grid=(tall // rows,),
        in_specs=[
            pl.BlockSpec((rows, wide), row),
            pl.BlockSpec((rows, 128), row),
            pl.BlockSpec((rows, 128), row),
            pl.BlockSpec((rows, wide), row),
            pl.BlockSpec((rows, 128), row),
            pl.BlockSpec((rows, width), row),
            pl.BlockSpec((rows, width), row),
            pl.BlockSpec((rows, 128), row),
        ],
        out_specs=[
            pl.BlockSpec((STREAMS, rows, width), lambda i: (0, i, 0)),
            pl.BlockSpec((rows, width), row),
            pl.BlockSpec((rows, 128), row),
        ],
        out_shape=[
            jax.ShapeDtypeStruct((STREAMS, tall, width), bf16),
            jax.ShapeDtypeStruct((tall, width), f32),
            jax.ShapeDtypeStruct((tall, 128), f32),
        ],
        cost_estimate=spent(
            flops=12 * tall * wide, bytes_accessed=10 * tall * wide, transcendentals=0
        ),
        name="stream_grads",
    )(scaled, mine, theirs, low, stats, cot, current_half, last)


def turning_tables(places):
    half = ROT // 2
    inverse = jnp.exp(jnp.arange(half, dtype=f32) * (-2.0 * math.log(10000.0) / ROT))
    angles = places.astype(f32)[:, None] * inverse[None, :]
    cosine, sine = jnp.cos(angles), jnp.sin(angles)
    rows = places.shape[0]
    rest = jnp.zeros((rows, HDIM - ROT), f32)
    blank = jnp.zeros((rows, half), f32)
    return (
        jnp.concatenate([cosine, cosine, rest + 1.0], axis=1),
        jnp.concatenate([-sine, blank, rest], axis=1),
        jnp.concatenate([blank, sine, rest], axis=1),
    )


def local(
    history,
    slot_layer,
    current,
    positions,
    doc_ids,
    cotangent,
    norm_gains,
    generator_in,
    generator_out,
    query_weight,
    key_weight,
    value_weight,
    out_weight,
    up_weight,
    down_weight,
):
    dp_count = lax.axis_size("dp")
    depth_count = lax.axis_size("depth")
    dp_at = lax.axis_index("dp")
    model_at = lax.axis_index("mp")
    dp_bits = list(range(bit_count(dp_count)))
    slots, tokens_held, width = history.shape
    model = current.shape[1]
    rows_mb = current.shape[0] // MB
    length = depth_count * rows_mb
    heads_width = query_weight.shape[1]
    heads_each = heads_width // HDIM // depth_count
    own_rows = query_weight.shape[0]
    ff_width = up_weight.shape[1]
    ff_part = ff_width // dp_count
    both = ("dp", "depth")

    def half_of(values, axis, which):
        return lax.dynamic_slice_in_dim(values, which * width, width, axis)

    partners = jnp.stack([dp_at ^ m for m in range(dp_count)]).astype(jnp.int32)
    ff_local = ff_split(up_weight, down_weight, partners)
    small_cols = jnp.concatenate(
        [generator_in, norm_gains.T, jnp.zeros((own_rows, 128 - GEN - 5), bf16)], axis=1
    )
    small_all = gather_small(small_cols, both).reshape(model, 128)
    gen_first = small_all[:, :GEN]
    gen_first, ff_local = fence(gen_first, ff_local)
    ff_rows = [ff_local[0]] + [swap_mask(ff_local[m], "dp", m) for m in range(1, dp_count)]
    ff_rows = place_many(partners, ff_rows).reshape(2 * dp_count, own_rows, ff_part)

    gain_float = small_all[:, GEN : GEN + 5].astype(f32).T
    second_rows = generator_out.shape[0]
    second_pad = -second_rows % 128
    second_all = gather_small(jnp.pad(generator_out, (0, second_pad))[None], both)
    gen_second = second_all.reshape(-1, second_rows + second_pad)[:, :second_rows]
    second_low = gen_second.reshape(GEN, STREAMS * MIX)

    stacked = jnp.concatenate([query_weight, key_weight, value_weight, out_weight.T], axis=0)
    over_depth = lax.all_gather(stacked, "depth", axis=0, tiled=True)
    current_f = current.astype(f32)
    current_half = half_of(current, 1, model_at)
    mean_square = jnp.mean(current_f * current_f, axis=-1, keepdims=True)
    inverse_rms = lax.rsqrt(mean_square + RMS_EPSILON)
    unit = current_f * inverse_rms
    gen_normed = (unit * gain_float[4]).astype(bf16)
    gen_pre = dot_nn(gen_normed, gen_first)
    gen_hidden = gelu_exact(gen_pre).astype(bf16)
    column = jnp.arange(STREAMS * MIX)
    last_col = (column % MIX == MIX - 1).astype(f32)
    mixing = (dot_nn(gen_hidden, second_low) + last_col).astype(bf16)
    pick_last = (column[:, None] == (jnp.arange(128) * MIX + MIX - 1)[None, :]).astype(bf16)
    last = dot_nn(mixing, pick_last)

    layer_of = jnp.tile(slot_layer, STREAMS)
    stream_of = jnp.repeat(jnp.arange(STREAMS), slots)
    from_col = jnp.where(layer_of < MIX, stream_of * MIX + layer_of, -1)
    pick = (column[:, None] == from_col[None, :]).astype(f32)
    mix_all = gather_small(mixing, ("depth",)).reshape(depth_count * MB * rows_mb, STREAMS * MIX)
    slot_mix = dot_nn(mix_all, pick.astype(bf16))
    places_all = gather_small(positions, ("depth",))

    def over_depth_swap(values):
        return lax.all_to_all(values, "depth", 0, 0, tiled=True)

    def mix_part(micro_at, slot_mix):
        partial = mix_streams(slot_mix, history, micro_at, depth_count, rows_mb)
        return partial.reshape(STREAMS, depth_count, rows_mb, width)

    slot_mix, ff_rows, cotangent, places_all = fence(slot_mix, ff_rows, cotangent, places_all)
    partial = mix_part(0, slot_mix)
    partial_next = mix_part(1, slot_mix)

    weights_line = LineGather(ff_rows)
    weights_line.step()
    cot_pieces = lax.all_gather(cotangent, "dp", axis=0, tiled=True)
    over_depth, partial, partial_next = weights_line.hold(over_depth, partial, partial_next)
    pieces = [over_depth]
    weights = place_block(None, pieces[0][None], place_index(0), dp_count)
    hops_left = [(p, at) for at in range(len(dp_bits)) for p in range(1 << at)]
    placed = 1
    cots = None
    sums, sums_next = LineScatter(partial), LineScatter(partial_next)
    own_tables = turning_tables(positions)
    tables = [
        turning_tables(places_all[:, m * rows_mb : (m + 1) * rows_mb].reshape(length))
        for m in range(MB)
    ]
    for hop in range(1, depth_count):
        sums.step_with(weights_line)
        last_hop = hop == depth_count - 1
        for place in range(placed, len(pieces)):
            weights = place_block(weights, pieces[place][None], place_index(place), dp_count)
        placed = len(pieces)
        while hops_left:
            place, at = hops_left.pop(0)
            pieces.append(core_hop(pieces[place], at))
            if len(hops_left) <= depth_count - 1 - hop:
                break
        if last_hop:
            cot_full = join_halves(cotangent, other_core(cotangent), model_at)
            ff_weights = weights_line.placed()
            cots = cot_full, cotangent, ff_weights
        (state,) = weights_line.hold(
            (sums.up, sums.down, pieces, weights, cots, own_tables, tables, cot_pieces)
        )
        sums.up, sums.down, pieces, weights, cots, own_tables, tables, cot_pieces = state
    cot_full, cotangent, ff_weights = cots
    for place in range(placed, len(pieces)):
        weights = place_block(weights, pieces[place][None], place_index(place), dp_count)
    weights = weights.reshape(dp_count, depth_count, 4, own_rows, heads_width)
    ff_weights = ff_weights.reshape(2, dp_count, depth_count, own_rows, ff_part)

    document_view = doc_ids.reshape(depth_count, MB, rows_mb)
    which = model_at.astype(jnp.int32)[None]
    depth_at = lax.axis_index("depth").astype(jnp.int32)[None]
    gains = gain_float

    def enter(micro_at, sums):
        span = slice(micro_at * rows_mb, (micro_at + 1) * rows_mb)
        low, resid = total_streams(sums, current_half[span], last[span], depth_at)
        normed, ff_normed, stats = norm_streams(low, other_core(low), gains, which)
        packed = project_heads(
            normed,
            cot_full[span],
            weights,
            [t[span] for t in own_tables],
            depth_count,
        )
        return dict(
            low=low, resid=resid, normed=normed, ff_normed=ff_normed, stats=stats, packed=packed
        )

    def attention(micro_at, by_head):
        documents = document_view[:, micro_at].reshape(length)
        by_head = by_head.reshape(length, 4 * heads_each * HDIM)
        answer = attend(by_head, documents, tables[micro_at], heads_each)
        return answer.reshape(depth_count, rows_mb, 4 * heads_each * HDIM)

    place_list = jnp.stack([place_index(p) for p in range(dp_count)]).astype(jnp.int32)

    def group_rows(ff_normed):
        return lax.all_gather(ff_normed, "dp", axis=0, tiled=True)

    def group_joined(mine):
        return join_halves(mine, other_core(mine), model_at)

    def hidden_units(micro_at, group_normed):
        hidden, grad_up, own, other = feed_forward(
            group_normed, cot_group, micro_at, ff_weights, which
        )
        return dict(group_normed=group_normed, hidden=hidden, grad_up=grad_up), (own, other)

    def group_back_rest(near):
        for at in reversed(range(len(dp_bits) - 1)):
            half = 1 << at
            near = near[:half] + core_hop(near[half:].astype(bf16), at).astype(f32)
        return near[0]

    def group_back(own, other):
        near, far = group_split(own, other, place_list)
        return group_back_rest(near + core_hop(far, len(dp_bits) - 1).astype(f32))

    def back(kept, answer):
        (theirs,) = back_project(answer, weights, 1 - which, bf16, False)
        got = other_core(theirs)
        own, flat = back_project(answer, weights, which, f32, True)
        return own, got, flat

    def leave(micro_at, kept, own, got, ff_sum):
        span = slice(micro_at * rows_mb, (micro_at + 1) * rows_mb)
        rows = (kept["resid"] + own[0] + got[0].astype(f32) + ff_sum[1]).astype(bf16)
        low, stats = kept["low"], kept["stats"]
        scaled, sums, gain_part = norm_slopes(own, got, ff_sum, low, stats, gains, which)
        grad_low, current_mix, last_dot = stream_grads(
            scaled, sums, other_core(sums), low, stats, cotangent[span], current_half[span], last[span]
        )
        kept.update(layer_rows=rows, gain=gain_part, current_mix=current_mix, last_dot=last_dot)
        return grad_low

    ((sums.up, sums.down),) = sums_next.step((sums.up, sums.down))
    first = enter(0, sums)
    mine = group_rows(first["ff_normed"])
    packed, mine, cot_pieces = sums_next.hold(first["packed"], mine, cot_pieces)
    while sums_next.at < depth_count - 3:
        sums_next.step()
        sums_next.hold()
    packed, mine, cot_pieces = sums_next.step(packed, mine, cot_pieces)
    by_head = over_depth_swap(packed)
    cot_group = join_halves(cot_pieces, other_core(cot_pieces), model_at)
    cot_group = cot_group.reshape(dp_count, MB, rows_mb, model)
    kept, ff_parts = hidden_units(0, group_joined(mine))
    first.update(kept)
    by_head, ff_parts, cot_group = sums_next.hold(by_head, ff_parts, cot_group)
    by_head, ff_parts = sums_next.step(by_head, ff_parts)
    answer = attention(0, by_head)
    answer, ff_parts = sums_next.hold(answer, ff_parts)

    answer = over_depth_swap(answer)
    second = enter(1, sums_next)
    near, far = group_split(ff_parts[0], other_core(ff_parts[1]), place_list)
    near = near + core_hop(far, len(dp_bits) - 1).astype(f32)
    answer, packed, ff_normed, near = fence(
        answer, second["packed"], second["ff_normed"], near
    )
    by_head = over_depth_swap(packed)
    mine = group_rows(ff_normed)
    own, got, first["flat"] = back(first, answer)
    grad_low = leave(0, first, own, got, group_back_rest(near))
    by_head, grad_low, mine, first["layer_rows"] = fence(
        by_head, grad_low, mine, first["layer_rows"]
    )
    saved = [first, second]

    def each(name):
        return [s[name] for s in saved]

    def rows_of(name):
        return jnp.concatenate(each(name), axis=0)

    def place_grads(place, dtype):
        return attention_grads(
            each("normed"),
            cot_full,
            each("flat"),
            place_list[place : place + 1],
            depth_count,
            dp_count,
            dtype,
        )

    half = dp_count // 2
    hops_left = [
        (p, at) for at in reversed(range(len(dp_bits))) for p in range(1 << at, 2 << at)
    ]
    pieces = {}

    def sums_hop():
        place, at = hops_left.pop(0)
        arrived = core_hop(pieces.pop(place), at)
        target = place - (1 << at)
        pieces[target] = (pieces[target].astype(f32) + arrived.astype(f32)).astype(bf16)

    grad_line = LineGather(grad_low)
    grad_line.step()
    answer = attention(1, by_head)
    kept, ff_parts = hidden_units(1, group_joined(mine))
    second.update(kept)
    answer, ff_parts = grad_line.hold(answer, ff_parts)
    answer = over_depth_swap(answer)
    near, far = group_split(ff_parts[0], other_core(ff_parts[1]), place_list)
    ff_products = hidden_grads(
        each("group_normed"), cot_group, each("grad_up"), each("hidden"), dp_count, depth_count
    )
    near = near + core_hop(far, len(dp_bits) - 1).astype(f32)
    answer, near, ff_products = fence(answer, near, ff_products)

    ff_sums = LineScatter(ff_products)
    (answer,) = ff_sums.step_with(grad_line, answer)
    own, got, flat = back(second, answer)
    ff_sum = group_back_rest(near)
    second["flat"] = flat
    (state,) = grad_line.hold((ff_sums.up, ff_sums.down, own, got, flat, ff_sum))
    ff_sums.up, ff_sums.down, own, got, second["flat"], ff_sum = state
    while len(grad_line.up) < depth_count - 1:
        ff_sums.step_with(grad_line)
        (state,) = grad_line.hold((ff_sums.up, ff_sums.down))
        ff_sums.up, ff_sums.down = state
    (ff_sum,) = ff_sums.step_with(grad_line, ff_sum)
    grad_low = leave(1, second, own, got, ff_sum)
    pieces = {p: place_grads(p, bf16) for p in range(dp_count)}
    sums_hop()
    (state,) = grad_line.hold((ff_sums.up, ff_sums.down, grad_low, pieces))
    ff_sums.up, ff_sums.down, grad_low, pieces = state

    last_line = LineGather(grad_low)
    last_line.step()
    if hops_left:
        sums_hop()
    grad_first = grad_line.placed().reshape(STREAMS, length, width)
    history_grad, slot_part = unmix_streams(
        slot_mix, history, grad_first, 0, depth_count, rows_mb, None
    )
    slot_parts = [slot_part.reshape(depth_count, 1, rows_mb, 128)]
    pieces, history_grad, second["layer_rows"] = last_line.hold(
        pieces, history_grad, second["layer_rows"]
    )
    (pieces,) = ff_sums.step(pieces)
    while hops_left:
        sums_hop()
    (pieces,) = ff_sums.hold(pieces)
    out_sums = LineScatter(pieces[0].reshape(1, depth_count, 4 * own_rows, heads_width))
    for hop in range(2, depth_count):
        last_line.step()
        ((ff_sums.up, ff_sums.down),) = out_sums.step((ff_sums.up, ff_sums.down))
        if hop == depth_count - 1:
            ff_sums.up = ff_sums.down = end_sums(ff_sums, bf16)
            early = last_line.placed_early()
            history_grad, slot_part = unmix_streams(
                slot_mix,
                history,
                early.reshape(STREAMS, length, width),
                1,
                depth_count,
                rows_mb,
                history_grad,
            )
        (state,) = last_line.hold(
            (out_sums.up, out_sums.down, ff_sums.up, ff_sums.down, history_grad, slot_part)
        )
        out_sums.up, out_sums.down, ff_sums.up, ff_sums.down, history_grad, slot_part = state
    early, ff_grads = out_sums.step(early, ff_sums.up)
    ff_grads = ff_grads.reshape(2, dp_count, own_rows, ff_part)
    ff_pieces = [
        lax.dynamic_index_in_dim(ff_grads, partners[m], 1, keepdims=False) for m in range(dp_count)
    ]
    ff_pieces = ff_pieces[:1] + [swap_mask(ff_pieces[m], "dp", m) for m in range(1, dp_count)]
    far_grads, far_index = last_line.farthest(early)
    history_grad, far_part = unmix_one(
        slot_mix, history, far_grads, 1, far_index, rows_mb, history_grad
    )
    slot_part = slot_part.reshape(depth_count, rows_mb, 128)
    slot_part = lax.dynamic_update_index_in_dim(slot_part, far_part, far_index, 0)
    slot_parts.append(slot_part[:, None])

    slot_grads = jnp.concatenate(slot_parts, axis=1).reshape(-1, 128)[:, : STREAMS * slots]
    mix_grads = dot_exact(slot_grads, pick.T).reshape(depth_count, MB * rows_mb, STREAMS * MIX)
    mix_grads, ff_pieces = out_sums.hold(mix_grads, ff_pieces)
    grad_mixing = scatter_small(mix_grads, ("depth",))
    up_grad, down_grad = ff_join(jnp.stack(ff_pieces), partners)
    last_dots = rows_of("last_dot")
    grad_mixing = grad_mixing + dot_exact(last_dots, pick_last.astype(f32).T)
    grad_mixing = grad_mixing + other_core(grad_mixing)

    second_float = second_low.astype(f32)
    grad_second = dot_exact(gen_hidden.astype(f32).T, grad_mixing)
    grad_pre = dot_exact(grad_mixing, second_float.T) * gelu_slope(gen_pre)
    grad_first = dot_exact(gen_normed.astype(f32).T, grad_pre)
    grad_gen_normed = dot_exact(grad_pre, gen_first.astype(f32).T)
    gain_gen = jnp.sum(grad_gen_normed * unit, axis=0)
    scattered = end_sums(out_sums, f32).reshape(4, own_rows, heads_width)
    grad_unit = grad_gen_normed * gain_float[4]
    shared = jnp.mean(grad_unit * unit, axis=-1, keepdims=True)
    current_gen = half_of(inverse_rms * (grad_unit - unit * shared), 1, model_at)
    current_grad = rows_of("current_mix") + current_gen

    gain_own = sum(s["gain"] for s in saved)
    gain_other = other_core(gain_own)
    gain_all = jnp.where(
        model_at == 0,
        jnp.concatenate([gain_own, gain_other], axis=1),
        jnp.concatenate([gain_other, gain_own], axis=1),
    )
    gain_all = jnp.concatenate([gain_all, gain_gen[None]], axis=0)
    small_grads = jnp.concatenate(
        [grad_first, gain_all.T, jnp.zeros((model, 128 - GEN - 5), f32)], axis=1
    )
    small_grads = scatter_small(small_grads.reshape(-1, own_rows, 128), both)
    second_grads = jnp.pad(grad_second.reshape(-1, second_rows), ((0, 0), (0, second_pad)))
    second_grads = scatter_small(second_grads[:, None], both)

    return (
        rows_of("layer_rows"),
        history_grad,
        current_grad,
        small_grads[:, GEN : GEN + 5].T,
        small_grads[:, :GEN],
        second_grads[0, :second_rows],
        scattered[0],
        scattered[1],
        scattered[2],
        scattered[3].T,
        up_grad,
        down_grad,
    )


def solution(mesh):
    return jax.shard_map(
        local,
        mesh=mesh,
        in_specs=(
            P("depth", "dp", "mp"),
            P("depth"),
            P(("dp", "depth"), None),
            P(("dp", "depth")),
            P("dp"),
            P(("dp", "depth"), "mp"),
            P(None, ("dp", "depth")),
            P(("dp", "depth"), None),
            P(("dp", "depth")),
            P(("dp", "depth"), "mp"),
            P(("dp", "depth"), "mp"),
            P(("dp", "depth"), "mp"),
            P("mp", ("dp", "depth")),
            P(("dp", "depth"), "mp"),
            P("mp", ("dp", "depth")),
        ),
        out_specs=(
            P(("dp", "depth"), "mp"),
            P("depth", "dp", "mp"),
            P(("dp", "depth"), "mp"),
            P(None, ("dp", "depth")),
            P(("dp", "depth"), None),
            P(("dp", "depth")),
            P(("dp", "depth"), "mp"),
            P(("dp", "depth"), "mp"),
            P(("dp", "depth"), "mp"),
            P("mp", ("dp", "depth")),
            P(("dp", "depth"), "mp"),
            P("mp", ("dp", "depth")),
        ),
        check_vma=False,
    )
```

```python
import functools
import math

import jax
import jax.numpy as jnp
from jax import lax
from jax.experimental import pallas as pl
from jax.experimental.pallas import tpu as pltpu
from jax.sharding import PartitionSpec as P

HDIM = 128
ROT = 32
GEN = 72
MB = 2
MIX = 18
STREAMS = 4
COST = 20

PRECISE = lax.Precision.HIGHEST
NORM_EPSILON = 1e-05
RMS_EPSILON = 1e-06
MASKED = -1e30

bf16 = jnp.bfloat16
f32 = jnp.float32


def dot_nn(a, b):
    return lax.dot_general(a, b, (((1,), (0,)), ((), ())), preferred_element_type=f32)


def dot_nt(a, b):
    return lax.dot_general(a, b, (((1,), (1,)), ((), ())), preferred_element_type=f32)


def dot_tn(a, b):
    return lax.dot_general(a, b, (((0,), (0,)), ((), ())), preferred_element_type=f32)


def dot_exact(a, b):
    return jnp.dot(a, b, precision=PRECISE, preferred_element_type=f32)


def gelu_exact(values):
    return jax.nn.gelu(values, approximate=False)


def gelu_slope(values):
    result, pullback = jax.vjp(gelu_exact, values)
    return pullback(jnp.ones_like(result))[0]


def bit_count(size):
    count = size.bit_length() - 1
    assert 1 << count == size
    return count


def swap_mask(values, axis, mask):
    size = lax.axis_size(axis)
    return lax.ppermute(values, axis, [(i, i ^ mask) for i in range(size)])


def gather_masked(values, axis, order):
    pieces = {0: values}
    for bit in order:
        arrived = {m | (1 << bit): swap_mask(v, axis, 1 << bit) for m, v in pieces.items()}
        pieces.update(arrived)
    return [pieces[m] for m in range(len(pieces))]


def scatter_masked(pieces, axis, order, link=bf16):
    pieces = dict(enumerate(pieces))
    for bit in order:
        flag = 1 << bit
        for m in [m for m in pieces if m & flag]:
            arrived = swap_mask(pieces.pop(m).astype(link), axis, flag)
            pieces[m ^ flag] = pieces[m ^ flag].astype(f32) + arrived.astype(f32)
    return pieces[0]


def core_orders():
    bits = list(range(bit_count(lax.axis_size("dp"))))
    return bits, bits[1:] + bits[:1]


def place_mask(place):
    masks = []
    for order in core_orders():
        masks.append(sum(1 << bit for at, bit in enumerate(order) if (place >> at) & 1))
    return jnp.where(lax.axis_index("mp") % 2 == 0, masks[0], masks[1])


def place_index(place):
    return lax.axis_index("dp") ^ place_mask(place)


def core_hop(values, at):
    orders, cores = core_orders(), lax.axis_size("mp")
    pairs = []
    for i in range(lax.axis_size("dp")):
        for core in range(cores):
            partner = i ^ (1 << orders[core % 2][at])
            pairs.append((i * cores + core, partner * cores + core))
    return lax.ppermute(values, ("dp", "mp"), pairs)


def group_hop(pieces, at):
    return jnp.concatenate([pieces, core_hop(pieces, at)], axis=0)


def place_of(core):
    partner = jnp.arange(lax.axis_size("dp")) ^ lax.axis_index("dp")
    places = []
    for order in core_orders():
        places.append(sum(((partner >> bit) & 1) << at for at, bit in enumerate(order)))
    return jnp.where(core % 2 == 0, places[0], places[1])


def reorder_masked(stacked, axis):
    count = bit_count(stacked.shape[0])
    here = lax.axis_index(axis)
    shape = stacked.shape
    values = stacked.reshape((2,) * count + shape[1:])
    for bit in range(count):
        turned = jnp.flip(values, count - 1 - bit)
        values = jnp.where(((here >> bit) & 1) == 1, turned, values)
    return values.reshape(shape)


def gather_small(values, axes):
    shape = values.shape
    values = values[None]
    for axis in reversed(axes):
        order = range(bit_count(lax.axis_size(axis)))
        stacked = jnp.stack(gather_masked(values, axis, order))
        values = reorder_masked(stacked, axis)
        values = values.reshape((-1,) + shape)
    return values


def scatter_small(values, axes):
    for axis in axes:
        size = lax.axis_size(axis)
        values = values.reshape((size, values.shape[0] // size) + values.shape[1:])
        turned = reorder_masked(values, axis)
        order = reversed(range(bit_count(size)))
        values = scatter_masked([turned[m] for m in range(size)], axis, order, f32)
    return values[0]


def line_size():
    return lax.axis_size("depth"), lax.axis_index("depth")


def fence(*values):
    return lax.optimization_barrier(values)


class LineGather:

    def __init__(self, values):
        self.up, self.down = [values], [values]

    def step(self):
        size, _ = line_size()
        at = len(self.up)
        if at < size:
            up_pairs = [(i, i + 1) for i in range(at - 1, size - 1)]
            down_pairs = [(i, i - 1) for i in range(1, size - at + 1)]
            self.up.append(lax.ppermute(self.up[-1], "depth", up_pairs))
            self.down.append(lax.ppermute(self.down[-1], "depth", down_pairs))

    def hold(self, *others):
        kept = fence((self.up[1:], self.down[1:]), *others)
        (up, down), rest = kept[0], kept[1:]
        self.up, self.down = self.up[:1] + list(up), self.down[:1] + list(down)
        return rest

    def placed_early(self):
        size, here = line_size()
        steps = jnp.arange(size)
        index = lax.rem(here - steps + size, size)
        own = self.up[0]
        blocks = self.up[: size - 1] + [own]
        instead = [own] + self.down[1 : size - 1][::-1]
        return place_line(index, here >= steps, blocks, instead)

    def farthest(self, early):
        size, here = line_size()
        last = jnp.where(here == size - 1, self.up[size - 1], early[:, 0])
        return jnp.where(here == 0, self.down[size - 1], last), jnp.where(here == 0, size - 1, 0)

    def placed(self):
        size, here = line_size()
        steps = jnp.arange(size)
        index = lax.rem(here - steps + size, size)
        return place_line(index, here >= steps, self.up, self.down[1:][::-1])


class LineScatter:

    def __init__(self, terms):
        self.terms, self.at = terms, 0
        self.up = self.down = None

    def step(self, *later):
        size, here = line_size()
        self.at += 1
        if self.at >= size:
            return later
        goes_up, goes_down = hop_sums(
            self.terms,
            jnp.minimum(size - self.at + here, size - 1),
            jnp.maximum(here - size + self.at, 0),
            self.up,
            self.down,
            [here < self.at, here > size - 1 - self.at],
        )
        (goes_up, goes_down), *later = fence((goes_up, goes_down), *later)
        up_pairs = [(i, i + 1) for i in range(min(self.at, size - 1))]
        down_pairs = [(size - 1 - i, size - 2 - i) for i in range(min(self.at, size - 1))]
        self.up = lax.ppermute(goes_up, "depth", up_pairs)
        self.down = lax.ppermute(goes_down, "depth", down_pairs)
        return later

    def step_with(self, line, *later):
        size, here = line_size()
        lead, _, tall, wide = self.terms.shape
        shape = line.up[0].shape
        if (
            len(line.up) != self.at + 2
            or self.at + 2 > size - 1
            or math.prod(shape) != lead * tall * wide
            or shape[2] != wide
        ):
            line.step()
            return self.step(*later)
        self.at += 1
        goes = hop_sums(
            self.terms,
            jnp.minimum(size - self.at + here, size - 1),
            jnp.maximum(here - size + self.at, 0),
            self.up,
            self.down,
            [here < self.at, here > size - 1 - self.at],
            [v[-1].reshape(lead, tall, wide) for v in (line.up, line.down)],
        )
        goes, *later = fence(goes, *later)
        self.up = lax.ppermute(goes[0], "depth", [(i, i + 1) for i in range(size - 1)])
        self.down = lax.ppermute(goes[1], "depth", [(i, i - 1) for i in range(1, size)])
        line.up.append(self.up.reshape(shape))
        line.down.append(self.down.reshape(shape))
        return later

    def hold(self, *others):
        (self.up, self.down), *rest = fence((self.up, self.down), *others)
        return rest


def other_core(values):
    return swap_mask(values, "mp", 1)


def join_kernel(model_ref, own_ref, other_ref, out_ref):
    width = own_ref.shape[1]
    own_at = pl.multiple_of(model_ref[0] * width, width)
    other_at = pl.multiple_of((1 - model_ref[0]) * width, width)
    out_ref[:, pl.ds(own_at, width)] = own_ref[...]
    out_ref[:, pl.ds(other_at, width)] = other_ref[...]


def join_halves(own, other, model_at):
    tall, width = own.shape
    rows = min(256, tall)
    return pl.pallas_call(
        join_kernel,
        grid_spec=pltpu.PrefetchScalarGridSpec(
            num_scalar_prefetch=1,
            grid=(tall // rows,),
            in_specs=[pl.BlockSpec((rows, width), lambda i, m: (i, 0))] * 2,
            out_specs=pl.BlockSpec((rows, 2 * width), lambda i, m: (i, 0)),
        ),
        out_shape=jax.ShapeDtypeStruct((tall, 2 * width), own.dtype),
        cost_estimate=spent(
            flops=0, bytes_accessed=8 * tall * width, transcendentals=0
        ),
        name="join_halves",
    )(model_at.astype(jnp.int32)[None], own, other)


def spent(flops, bytes_accessed, transcendentals):
    return pl.CostEstimate(
        flops=flops // COST, bytes_accessed=bytes_accessed // COST, transcendentals=transcendentals // COST
    )


def chunk_of(tall, wide):
    rows = tall
    while rows * wide > 1 << 19 and rows % 32 == 0:
        rows //= 2
    return rows


def place_kernel(at_ref, *refs):
    if len(refs) < 4:
        refs[-1][0, 0] = refs[0][0]
        return

    @pl.when(at_ref[1] == 1)
    def _():
        refs[-1][0, 0] = refs[0][0]

    @pl.when(at_ref[1] == 0)
    def _():
        refs[-1][0, 0] = refs[1][0]


def place_block(buffer, block, index, count, instead=None, first=None):
    lead, tall, wide = block.shape
    rows = chunk_of(tall, wide)
    spec = pl.BlockSpec((1, rows, wide), lambda l, i, m: (l, i, 0))
    blocks = [block] if instead is None else [block, instead]
    where = [index, 1 if first is None else first]
    where = jnp.stack([jnp.asarray(v).astype(jnp.int32) for v in where])
    in_specs, operands, aliases = [spec] * len(blocks), list(blocks), {}
    if buffer is not None or instead is not None:
        in_specs.append(pl.BlockSpec(memory_space=pl.ANY))
        operands.append(block if buffer is None else buffer)
        aliases = {} if buffer is None else {len(operands): 0}
    return pl.pallas_call(
        place_kernel,
        grid_spec=pltpu.PrefetchScalarGridSpec(
            num_scalar_prefetch=1,
            grid=(lead, tall // rows),
            in_specs=in_specs,
            out_specs=pl.BlockSpec((1, 1, rows, wide), lambda l, i, m: (l, m[0], i, 0)),
        ),
        out_shape=jax.ShapeDtypeStruct((lead, count, tall, wide), block.dtype),
        input_output_aliases=aliases,
        cost_estimate=spent(
            flops=0, bytes_accessed=4 * lead * tall * wide, transcendentals=0
        ),
        name="place_block",
    )(where, *operands)


def place_line_kernel(size, at_ref, *refs):
    out_ref = refs[-1]
    for step in range(size):
        if step == 0 or len(refs) == size + 1:
            out_ref[0, at_ref[step]] = refs[step][0]
            continue

        @pl.when(at_ref[size + step] == 1)
        def _(step=step):
            out_ref[0, at_ref[step]] = refs[step][0]

        @pl.when(at_ref[size + step] == 0)
        def _(step=step):
            out_ref[0, at_ref[step]] = refs[size + step - 1][0]


def place_line(index, first, blocks, instead):
    size = len(blocks)
    lead, tall, wide = blocks[0].shape
    rows = tall
    while rows * wide > 1 << 18 and rows % 32 == 0:
        rows //= 2
    spec = pl.BlockSpec((1, rows, wide), lambda l, i, m: (l, i, 0))
    where = jnp.concatenate([index, first]).astype(jnp.int32)
    operands = list(blocks) + list(instead)
    return pl.pallas_call(
        functools.partial(place_line_kernel, size),
        grid_spec=pltpu.PrefetchScalarGridSpec(
            num_scalar_prefetch=1,
            grid=(lead, tall // rows),
            in_specs=[spec] * len(operands),
            out_specs=pl.BlockSpec((1, size, rows, wide), lambda l, i, m: (l, 0, i, 0)),
        ),
        out_shape=jax.ShapeDtypeStruct((lead, size, tall, wide), blocks[0].dtype),
        compiler_params=pltpu.CompilerParams(vmem_limit_bytes=40 << 20),
        cost_estimate=spent(
            flops=0, bytes_accessed=6 * size * lead * tall * wide, transcendentals=0
        ),
        name="place_line",
    )(where, *operands)


def place_many(index, blocks):
    ones = jnp.ones(len(blocks), jnp.int32)
    return place_line(index, ones, blocks, [])


def group_join_kernel(at_ref, own_ref, other_ref, out_ref):
    width = own_ref.shape[2]
    own_span, other_span = own_spans(at_ref, width)
    out_ref[:, own_span] = own_ref[0]
    out_ref[:, other_span] = other_ref[0]


def group_join(own, other, model_at):
    count, tall, width = own.shape
    rows = chunk_of(tall, width)
    per = tall // rows
    where = jnp.concatenate([model_at[None], place_of(model_at), place_of(1 - model_at)])
    return pl.pallas_call(
        group_join_kernel,
        grid_spec=pltpu.PrefetchScalarGridSpec(
            num_scalar_prefetch=1,
            grid=(count, per),
            in_specs=[
                pl.BlockSpec((1, rows, width), lambda n, i, m: (m[1 + n], i, 0)),
                pl.BlockSpec((1, rows, width), lambda n, i, m: (m[1 + count + n], i, 0)),
            ],
            out_specs=pl.BlockSpec((rows, 2 * width), lambda n, i, m: (n * per + i, 0)),
        ),
        out_shape=jax.ShapeDtypeStruct((count * tall, 2 * width), own.dtype),
        cost_estimate=spent(
            flops=0, bytes_accessed=8 * count * tall * width, transcendentals=0
        ),
        name="group_join",
    )(where.astype(jnp.int32), own, other)


def group_split_kernel(at_ref, near_own, near_other, far_own, far_other, near_ref, far_ref):
    near_ref[0, 0] = near_own[0] + near_other[0].astype(f32)
    far_ref[0, 0] = (far_own[0] + far_other[0].astype(f32)).astype(bf16)


def group_split(own, other, places):
    _, tall, width = own.shape
    count = places.shape[0]
    half, rows = count // 2, tall // count
    near = pl.BlockSpec((1, rows, width), lambda p, k, m: (k, m[p], 0))
    far = pl.BlockSpec((1, rows, width), lambda p, k, m: (k, m[half + p], 0))
    out = pl.BlockSpec((1, 1, rows, width), lambda p, k, m: (p, k, 0, 0))
    return pl.pallas_call(
        group_split_kernel,
        grid_spec=pltpu.PrefetchScalarGridSpec(
            num_scalar_prefetch=1,
            grid=(half, 2),
            in_specs=[near, near, far, far],
            out_specs=[out, out],
        ),
        out_shape=[
            jax.ShapeDtypeStruct((half, 2, rows, width), f32),
            jax.ShapeDtypeStruct((half, 2, rows, width), bf16),
        ],
        cost_estimate=spent(
            flops=2 * tall * width, bytes_accessed=20 * tall * width, transcendentals=0
        ),
        name="group_split",
    )(places, own, other, own, other)


def hop_kernel(has_sums, has_blocks, at_ref, *refs):
    ins, outs = list(refs[:-2]), refs[-2:]
    terms, ins = ins[:2], ins[2:]
    sums, ins = (ins[:2], ins[2:]) if has_sums else (None, ins)

    def send_sum(way):
        term = terms[way][:, 0].astype(f32)
        if sums is not None:
            term = term + sums[way][...].astype(f32)
        outs[way][...] = term.astype(bf16)

    for way in range(2):
        if not has_blocks:
            send_sum(way)
            continue
        pl.when(at_ref[2 + way] == 1)(functools.partial(send_sum, way))

        @pl.when(at_ref[2 + way] == 0)
        def _(way=way):
            outs[way][...] = ins[way][...]


def hop_sums(terms, up_at, down_at, up, down, sends, blocks=None):
    lead, _, tall, wide = terms.shape
    rows = chunk_of(tall, wide)
    deep = lead
    while deep * rows * wide > 1 << 19 and deep % 2 == 0:
        deep //= 2
    block = pl.BlockSpec((deep, rows, wide), lambda l, i, m: (l, i, 0))

    def term_spec(way):
        return pl.BlockSpec(
            (deep, 1, rows, wide), lambda l, i, m: (l * m[2 + way], m[way], i * m[2 + way], 0)
        )

    def block_spec(way, sign):
        def index(l, i, m):
            need = m[2 + way] if sign else 1 - m[2 + way]
            return (l * need, i * need, 0)

        return pl.BlockSpec((deep, rows, wide), index)

    in_specs = [term_spec(0), term_spec(1)]
    operands = [terms, terms]
    if up is not None:
        in_specs += [block_spec(0, True), block_spec(1, True)]
        operands += [up, down]
    if blocks is not None:
        in_specs += [block_spec(0, False), block_spec(1, False)]
        operands += list(blocks)
    return pl.pallas_call(
        functools.partial(hop_kernel, up is not None, blocks is not None),
        grid_spec=pltpu.PrefetchScalarGridSpec(
            num_scalar_prefetch=1,
            grid=(lead // deep, tall // rows),
            in_specs=in_specs,
            out_specs=[block, block],
        ),
        out_shape=[jax.ShapeDtypeStruct((lead, tall, wide), bf16)] * 2,
        cost_estimate=spent(
            flops=2 * lead * tall * wide, bytes_accessed=12 * lead * tall * wide, transcendentals=0
        ),
        compiler_params=pltpu.CompilerParams(vmem_limit_bytes=40 << 20),
        name="hop_sums",
    )(jnp.stack([up_at, down_at, *sends]).astype(jnp.int32), *operands)


def end_kernel(at_ref, term_ref, up_ref, down_ref, out_ref):
    total = term_ref[0, 0].astype(f32) + up_ref[0].astype(f32) + down_ref[0].astype(f32)
    out_ref[0] = total.astype(out_ref.dtype)


def end_sums(sums, dtype):
    lead, _, tall, wide = sums.terms.shape
    rows = chunk_of(tall, wide)
    block = pl.BlockSpec((1, rows, wide), lambda l, i, m: (l, i, 0))
    return pl.pallas_call(
        end_kernel,
        grid_spec=pltpu.PrefetchScalarGridSpec(
            num_scalar_prefetch=1,
            grid=(lead, tall // rows),
            in_specs=[
                pl.BlockSpec((1, 1, rows, wide), lambda l, i, m: (l, m[0], i, 0)),
                block,
                block,
            ],
            out_specs=block,
        ),
        out_shape=jax.ShapeDtypeStruct((lead, tall, wide), dtype),
        cost_estimate=spent(
            flops=2 * lead * tall * wide, bytes_accessed=10 * lead * tall * wide, transcendentals=0
        ),
        name="end_sums",
    )(lax.axis_index("depth").astype(jnp.int32)[None], sums.terms, sums.up, sums.down)


def attention_grad_kernel(
    at_ref, x0_ref, x1_ref, cot_ref, g0_ref, g1_ref, out_ref
):
    tall = x0_ref.shape[1]

    def store(total):
        out_ref[...] = total.reshape(out_ref.shape).astype(out_ref.dtype)

    @pl.when(pl.program_id(0) < 3)
    def _():
        store(dot_tn(x0_ref[0], g0_ref[0]) + dot_tn(x1_ref[0], g1_ref[0]))

    @pl.when(pl.program_id(0) == 3)
    def _():
        store(
            dot_tn(cot_ref[0:tall, :], g0_ref[0]) + dot_tn(cot_ref[tall : 2 * tall, :], g1_ref[0])
        )


def attention_grads(normed, cot, flat, place, depth_count, dp_count, dtype):
    _, tall, model = normed[0].shape
    heads_width = flat[0].shape[2]
    block = model // dp_count
    own_rows = block // depth_count
    normed_spec = pl.BlockSpec((1, tall, block), lambda k, m: (jnp.minimum(k, 2), 0, m[0]))
    flat_spec = pl.BlockSpec((1, tall, heads_width), lambda k, m: (lax.rem(k + 1, 4), 0, 0))
    return pl.pallas_call(
        attention_grad_kernel,
        grid_spec=pltpu.PrefetchScalarGridSpec(
            num_scalar_prefetch=1,
            grid=(4,),
            in_specs=[
                normed_spec,
                normed_spec,
                pl.BlockSpec((2 * tall, block), lambda k, m: (0, m[0])),
                flat_spec,
                flat_spec,
            ],
            out_specs=pl.BlockSpec(
                (depth_count, 1, own_rows, heads_width), lambda k, m: (0, k, 0, 0)
            ),
        ),
        out_shape=jax.ShapeDtypeStruct((depth_count, 4, own_rows, heads_width), dtype),
        compiler_params=pltpu.CompilerParams(vmem_limit_bytes=40 << 20),
        cost_estimate=spent(
            flops=16 * tall * block * heads_width,
            bytes_accessed=16 * block * heads_width,
            transcendentals=0,
        ),
        name="attention_grads",
    )(place, *normed, cot, *flat)


def hidden_grad_kernel(x0_ref, x1_ref, c0_ref, c1_ref, u0_ref, u1_ref, h0_ref, h1_ref, out_ref):
    def store(total):
        out_ref[...] = total.reshape(out_ref.shape).astype(bf16)

    @pl.when(pl.program_id(0) == 0)
    def _():
        store(dot_tn(x0_ref[...], u0_ref[...]) + dot_tn(x1_ref[...], u1_ref[...]))

    @pl.when(pl.program_id(0) == 1)
    def _():
        tall, wide = h0_ref.shape[0], c0_ref.shape[3]
        c0, c1 = c0_ref[:, 0].reshape(tall, wide), c1_ref[:, 0].reshape(tall, wide)
        store(dot_tn(c0, h0_ref[...]) + dot_tn(c1, h1_ref[...]))


def hidden_grads(x, cot, up_grads, hidden, dp_count, depth_count):
    tall, model = x[0].shape
    part = hidden[0].shape[1]
    block = model // dp_count
    cols = pl.BlockSpec((tall, block), lambda k, n: (0, n * (1 - k)))
    whole = pl.BlockSpec((tall, part), lambda k, n: (0, 0))
    return pl.pallas_call(
        hidden_grad_kernel,
        grid=(2, dp_count),
        in_specs=[cols, cols]
        + [
            pl.BlockSpec((dp_count, 1, cot.shape[2], block), lambda k, n: (0, 0, 0, n * k)),
            pl.BlockSpec((dp_count, 1, cot.shape[2], block), lambda k, n: (0, 1, 0, n * k)),
        ]
        + [whole] * 4,
        out_specs=pl.BlockSpec(
            (1, depth_count, block // depth_count, part), lambda k, n: (k * dp_count + n, 0, 0, 0)
        ),
        out_shape=jax.ShapeDtypeStruct(
            (2 * dp_count, depth_count, block // depth_count, part), bf16
        ),
        compiler_params=pltpu.CompilerParams(vmem_limit_bytes=48 << 20),
        cost_estimate=spent(
            flops=8 * tall * model * part, bytes_accessed=8 * model * part, transcendentals=0
        ),
        name="hidden_grads",
    )(*x, cot, cot, *up_grads, *hidden)


def mix_kernel(slots, mix_ref, hist_ref, out_ref):
    rows, width = hist_ref.shape[1], hist_ref.shape[2]
    part = 512 if width % 512 == 0 else width

    def step(at, carry):
        r0 = pl.multiple_of(at * 16, 16)
        weights = mix_ref[pl.ds(r0, 16), :]
        for c0 in range(0, width, part):
            sums = [None] * STREAMS
            for k in range(slots):
                state = hist_ref[k, pl.ds(r0, 16), c0 : c0 + part].astype(f32)
                for s in range(STREAMS):
                    term = weights[:, s * slots + k : s * slots + k + 1] * state
                    sums[s] = term if sums[s] is None else sums[s] + term
            for s in range(STREAMS):
                out_ref[s, pl.ds(r0, 16), c0 : c0 + part] = sums[s].astype(bf16)
        return carry

    lax.fori_loop(0, rows // 16, step, 0)


def mix_streams(slot_mix, history, micro_at, depth_count, rows_mb):
    slots, _, width = history.shape
    rows = min(128, rows_mb)
    per = rows_mb // rows

    def row_block(i):
        return ((i // per) * MB + micro_at) * per + i % per

    return pl.pallas_call(
        functools.partial(mix_kernel, slots),
        grid=(depth_count * per,),
        in_specs=[
            pl.BlockSpec((rows, slot_mix.shape[1]), lambda i: (row_block(i), 0)),
            pl.BlockSpec((slots, rows, width), lambda i: (0, row_block(i), 0)),
        ],
        out_specs=pl.BlockSpec((STREAMS, rows, width), lambda i: (0, i, 0)),
        out_shape=jax.ShapeDtypeStruct((STREAMS, depth_count * rows_mb, width), bf16),
        cost_estimate=spent(
            flops=2 * slots * STREAMS * depth_count * rows_mb * width,
            bytes_accessed=2 * (slots + STREAMS) * depth_count * rows_mb * width,
            transcendentals=0,
        ),
        name="mix_streams",
    )(slot_mix, history)


def unmix_kernel(slots, mix_ref, hist_ref, grad_ref, *rest):
    hist_grad_ref, slot_grad_ref = rest[-2:]
    rows, width = hist_ref.shape[1], hist_ref.shape[2]
    part = 512 if width % 512 == 0 else width

    def step(at, carry):
        r0 = pl.multiple_of(at * 16, 16)
        weights = mix_ref[pl.ds(r0, 16), :]
        totals = [None] * (STREAMS * slots)
        for c0 in range(0, width, part):
            grads = [
                grad_ref[s, pl.ds(r0, 16), c0 : c0 + part].astype(f32)
                for s in range(STREAMS)
            ]
            for k in range(slots):
                state = hist_ref[k, pl.ds(r0, 16), c0 : c0 + part].astype(f32)
                back = None
                for s in range(STREAMS):
                    at_sk = s * slots + k
                    term = weights[:, at_sk : at_sk + 1] * grads[s]
                    back = term if back is None else back + term
                    product = state * grads[s]
                    folded = product[:, 0:128]
                    for l0 in range(128, part, 128):
                        folded = folded + product[:, l0 : l0 + 128]
                    totals[at_sk] = folded if totals[at_sk] is None else totals[at_sk] + folded
                hist_grad_ref[k, pl.ds(r0, 16), c0 : c0 + part] = back.astype(bf16)
        lane = lax.broadcasted_iota(jnp.int32, (16, 128), 1)
        packed = jnp.zeros((16, 128), f32)
        for at_sk in range(STREAMS * slots):
            column = jnp.sum(totals[at_sk], axis=1, keepdims=True)
            packed = jnp.where(lane == at_sk, column, packed)
        slot_grad_ref[pl.ds(r0, 16), :] = packed
        return carry

    lax.fori_loop(0, rows // 16, step, 0)


def unmix_streams(slot_mix, history, grads, micro_at, depth_count, rows_mb, earlier):
    slots, tokens, width = history.shape
    rows = min(128, rows_mb)
    per = rows_mb // rows

    def row_block(i):
        return ((i // per) * MB + micro_at) * per + i % per

    in_specs = [
        pl.BlockSpec((rows, slot_mix.shape[1]), lambda i: (row_block(i), 0)),
        pl.BlockSpec((slots, rows, width), lambda i: (0, row_block(i), 0)),
        pl.BlockSpec((STREAMS, rows, width), lambda i: (0, i, 0)),
    ]
    operands = [slot_mix, history, grads]
    aliases = {}
    if earlier is not None:
        in_specs.append(pl.BlockSpec(memory_space=pl.ANY))
        operands.append(earlier)
        aliases = {3: 0}
    return pl.pallas_call(
        functools.partial(unmix_kernel, slots),
        grid=(depth_count * per,),
        in_specs=in_specs,
        out_specs=[
            pl.BlockSpec((slots, rows, width), lambda i: (0, row_block(i), 0)),
            pl.BlockSpec((rows, 128), lambda i: (i, 0)),
        ],
        out_shape=[
            jax.ShapeDtypeStruct((slots, tokens, width), bf16),
            jax.ShapeDtypeStruct((depth_count * rows_mb, 128), f32),
        ],
        input_output_aliases=aliases,
        cost_estimate=spent(
            flops=4 * slots * STREAMS * depth_count * rows_mb * width,
            bytes_accessed=2 * (2 * slots + STREAMS) * depth_count * rows_mb * width,
            transcendentals=0,
        ),
        name="unmix_streams",
    )(*operands)


def unmix_one(slot_mix, history, grads, micro_at, index, rows_mb, earlier):
    slots, tokens, width = history.shape
    rows = min(128, rows_mb)
    per = rows_mb // rows

    def row_block(i, m):
        return (m[0] * MB + micro_at) * per + i

    def kernel(at_ref, *refs):
        unmix_kernel(slots, *refs)

    return pl.pallas_call(
        kernel,
        grid_spec=pltpu.PrefetchScalarGridSpec(
            num_scalar_prefetch=1,
            grid=(per,),
            in_specs=[
                pl.BlockSpec((rows, slot_mix.shape[1]), lambda i, m: (row_block(i, m), 0)),
                pl.BlockSpec((slots, rows, width), lambda i, m: (0, row_block(i, m), 0)),
                pl.BlockSpec((STREAMS, rows, width), lambda i, m: (0, i, 0)),
                pl.BlockSpec(memory_space=pl.ANY),
            ],
            out_specs=[
                pl.BlockSpec((slots, rows, width), lambda i, m: (0, row_block(i, m), 0)),
                pl.BlockSpec((rows, 128), lambda i, m: (i, 0)),
            ],
        ),
        out_shape=[
            jax.ShapeDtypeStruct((slots, tokens, width), bf16),
            jax.ShapeDtypeStruct((rows_mb, 128), f32),
        ],
        input_output_aliases={4: 0},
        cost_estimate=spent(
            flops=4 * slots * STREAMS * rows_mb * width,
            bytes_accessed=2 * (2 * slots + STREAMS) * rows_mb * width,
            transcendentals=0,
        ),
        name="unmix_one",
    )(index.astype(jnp.int32)[None], slot_mix, history, grads, earlier)


def own_spans(model_ref, width):
    own_at = pl.multiple_of(model_ref[0] * width, width)
    other_at = pl.multiple_of((1 - model_ref[0]) * width, width)
    return pl.ds(own_at, width), pl.ds(other_at, width)


def ff_split_kernel(at_ref, up_ref, down_ref, out_ref):
    out_ref[0, 0] = up_ref[...]
    out_ref[0, 1] = down_ref[...].T


def ff_split(up_weight, down_weight, partners):
    own_rows, ff_width = up_weight.shape
    count = partners.shape[0]
    part = ff_width // count
    return pl.pallas_call(
        ff_split_kernel,
        grid_spec=pltpu.PrefetchScalarGridSpec(
            num_scalar_prefetch=1,
            grid=(count,),
            in_specs=[
                pl.BlockSpec((own_rows, part), lambda i, m: (0, m[i])),
                pl.BlockSpec((part, own_rows), lambda i, m: (m[i], 0)),
            ],
            out_specs=pl.BlockSpec((1, 2, own_rows, part), lambda i, m: (i, 0, 0, 0)),
        ),
        out_shape=jax.ShapeDtypeStruct((count, 2, own_rows, part), bf16),
        cost_estimate=spent(flops=0, bytes_accessed=8 * own_rows * ff_width, transcendentals=0),
        name="ff_split",
    )(partners, up_weight, down_weight)


def ff_join_kernel(at_ref, piece_ref, up_ref, down_ref):
    up_ref[...] = piece_ref[0, 0].astype(f32)
    down_ref[...] = piece_ref[0, 1].astype(f32).T


def ff_join(pieces, partners):
    count, _, own_rows, part = pieces.shape
    return pl.pallas_call(
        ff_join_kernel,
        grid_spec=pltpu.PrefetchScalarGridSpec(
            num_scalar_prefetch=1,
            grid=(count,),
            in_specs=[pl.BlockSpec((1, 2, own_rows, part), lambda i, m: (i, 0, 0, 0))],
            out_specs=[
                pl.BlockSpec((own_rows, part), lambda i, m: (0, m[i])),
                pl.BlockSpec((part, own_rows), lambda i, m: (m[i], 0)),
            ],
        ),
        out_shape=[
            jax.ShapeDtypeStruct((own_rows, count * part), f32),
            jax.ShapeDtypeStruct((count * part, own_rows), f32),
        ],
        cost_estimate=spent(
            flops=0, bytes_accessed=12 * own_rows * count * part, transcendentals=0
        ),
        name="ff_join",
    )(partners, pieces)


def total_kernel(depth_ref, part_ref, up_ref, down_ref, cur_ref, last_ref, low_ref, resid_ref):
    width = resid_ref.shape[1]
    current = cur_ref[...].astype(f32)
    for s in range(STREAMS):
        lanes = slice(s * width, (s + 1) * width)
        total = part_ref[s, 0].astype(f32)
        total = total + up_ref[s].astype(f32) + down_ref[s].astype(f32)
        total = total + last_ref[:, s : s + 1] * current
        if s == STREAMS - 1:
            resid_ref[...] = total
        low_ref[:, lanes] = total.astype(bf16)


def total_streams(sums, current_half, last, depth_at):
    _, _, tall, width = sums.terms.shape
    wide = STREAMS * width
    rows = min(128, tall)
    row = lambda i, d: (i, 0)
    return pl.pallas_call(
        total_kernel,
        grid_spec=pltpu.PrefetchScalarGridSpec(
            num_scalar_prefetch=1,
            grid=(tall // rows,),
            in_specs=[
                pl.BlockSpec((STREAMS, 1, rows, width), lambda i, d: (0, d[0], i, 0)),
                pl.BlockSpec((STREAMS, rows, width), lambda i, d: (0, i, 0)),
                pl.BlockSpec((STREAMS, rows, width), lambda i, d: (0, i, 0)),
                pl.BlockSpec((rows, width), row),
                pl.BlockSpec((rows, 128), row),
            ],
            out_specs=[pl.BlockSpec((rows, wide), row), pl.BlockSpec((rows, width), row)],
        ),
        out_shape=[
            jax.ShapeDtypeStruct((tall, wide), bf16),
            jax.ShapeDtypeStruct((tall, width), f32),
        ],
        cost_estimate=spent(flops=5 * tall * wide, bytes_accessed=9 * tall * wide, transcendentals=0),
        compiler_params=pltpu.CompilerParams(vmem_limit_bytes=40 << 20),
        name="total_streams",
    )(depth_at, sums.terms, sums.up, sums.down, current_half, last)


def norm_kernel(model_ref, own_ref, other_ref, gain_ref, normed_ref, ff_ref, stat_ref):
    rows, width = ff_ref.shape
    model = 2 * width
    own_span, other_span = own_spans(model_ref, width)
    lane = lax.broadcasted_iota(jnp.int32, (rows, 128), 1)
    stats = jnp.zeros((rows, 128), f32)
    for s in range(STREAMS):
        lanes = slice(s * width, (s + 1) * width)
        own = own_ref[:, lanes].astype(f32)
        other = other_ref[:, lanes].astype(f32)
        average = (
            jnp.sum(own, axis=-1, keepdims=True) + jnp.sum(other, axis=-1, keepdims=True)
        ) / model
        own, other = own - average, other - average
        variance = (
            jnp.sum(own * own, axis=-1, keepdims=True)
            + jnp.sum(other * other, axis=-1, keepdims=True)
        ) / model
        inverse = lax.rsqrt(variance + NORM_EPSILON)
        stats = jnp.where(lane == 2 * s, average, stats)
        stats = jnp.where(lane == 2 * s + 1, inverse, stats)
        norm_own = (own * inverse * gain_ref[s : s + 1, own_span]).astype(bf16)
        if s == STREAMS - 1:
            ff_ref[...] = norm_own
        else:
            normed_ref[s, :, own_span] = norm_own
            norm_other = (other * inverse * gain_ref[s : s + 1, other_span]).astype(bf16)
            normed_ref[s, :, other_span] = norm_other
    stat_ref[...] = stats


def norm_streams(low, low_other, gains, which):
    tall, wide = low.shape
    width = wide // STREAMS
    rows = min(128, tall)
    row = lambda i, m: (i, 0)
    return pl.pallas_call(
        norm_kernel,
        grid_spec=pltpu.PrefetchScalarGridSpec(
            num_scalar_prefetch=1,
            grid=(tall // rows,),
            in_specs=[
                pl.BlockSpec((rows, wide), row),
                pl.BlockSpec((rows, wide), row),
                pl.BlockSpec(gains.shape, lambda i, m: (0, 0)),
            ],
            out_specs=[
                pl.BlockSpec((3, rows, 2 * width), lambda i, m: (0, i, 0)),
                pl.BlockSpec((rows, width), row),
                pl.BlockSpec((rows, 128), row),
            ],
        ),
        out_shape=[
            jax.ShapeDtypeStruct((3, tall, 2 * width), bf16),
            jax.ShapeDtypeStruct((tall, width), bf16),
            jax.ShapeDtypeStruct((tall, 128), f32),
        ],
        cost_estimate=spent(
            flops=20 * tall * wide, bytes_accessed=8 * tall * wide, transcendentals=0
        ),
        compiler_params=pltpu.CompilerParams(vmem_limit_bytes=40 << 20),
        name="norm_streams",
    )(which, low, low_other, gains)


def turn(values, cosine, sine_up, sine_down, sign):
    up = pltpu.roll(values, HDIM - ROT // 2, 1)
    down = pltpu.roll(values, ROT // 2, 1)
    return values * cosine + sign * (up * sine_up + down * sine_down)


def project_kernel(
    x_ref, cot_ref, wq_ref, wk_ref, wv_ref, wo_ref, cos_ref, up_ref, down_ref, out_ref
):
    span = wq_ref.shape[-1]
    tables = cos_ref[...], up_ref[...], down_ref[...]
    for kind, w_ref in enumerate((wq_ref, wk_ref, wv_ref, wo_ref)):
        rows = cot_ref[...] if kind == 3 else x_ref[kind]
        product = dot_nn(rows, w_ref[...].reshape(-1, span))
        for begin in range(0, span, HDIM):
            head = product[:, begin : begin + HDIM]
            if kind < 2:
                head = turn(head, *tables, 1.0)
            out_ref[0, :, kind * span + begin : kind * span + begin + HDIM] = head.astype(bf16)


def project_heads(normed, cot, weights, tables, depth_count):
    _, rows, model = normed.shape
    groups, _, _, own_rows, heads_width = weights.shape
    span = heads_width // depth_count
    whole = lambda j: (0, 0)

    def matrix(kind):
        shape = (groups, depth_count, 1, own_rows, span)
        return pl.BlockSpec(shape, lambda j: (0, 0, kind, 0, j))

    return pl.pallas_call(
        project_kernel,
        grid=(depth_count,),
        in_specs=[
            pl.BlockSpec((3, rows, model), lambda j: (0, 0, 0)),
            pl.BlockSpec((rows, model), whole),
        ]
        + [matrix(kind) for kind in range(4)]
        + [pl.BlockSpec((rows, HDIM), whole)] * 3,
        out_specs=pl.BlockSpec((1, rows, 4 * span), lambda j: (j, 0, 0)),
        out_shape=jax.ShapeDtypeStruct((depth_count, rows, 4 * span), bf16),
        compiler_params=pltpu.CompilerParams(vmem_limit_bytes=40 << 20),
        cost_estimate=spent(
            flops=8 * rows * model * span * depth_count,
            bytes_accessed=8 * model * span * depth_count + 8 * rows * model,
            transcendentals=0,
        ),
        name="project_heads",
    )(normed, cot, *[weights] * 4, *tables)


def attend_kernel(
    block, q_ref, k_ref, v_ref, g_ref, doc_col_ref, doc_row_ref, cos_ref, up_ref, down_ref,
    out_ref, dk_sum, dv_sum,
):
    length = q_ref.shape[0]
    scale = HDIM**-0.5
    heads_each = out_ref.shape[1] // (4 * HDIM)

    def lanes(kind):
        return pl.ds(pl.multiple_of((kind * heads_each + pl.program_id(0)) * HDIM, HDIM), HDIM)

    for begin in range(0, length, block):
        end = begin + block
        rows = slice(begin, end)
        queries, grads = q_ref[rows, :], g_ref[rows, :]
        keys, values = k_ref[0:end, :], v_ref[0:end, :]
        scores = dot_nt(queries, keys) * scale
        place_q = begin + lax.broadcasted_iota(jnp.int32, scores.shape, 0)
        place_k = lax.broadcasted_iota(jnp.int32, scores.shape, 1)
        allowed = (doc_col_ref[rows, :] == doc_row_ref[:, 0:end]) & (place_q >= place_k)
        scores = jnp.where(allowed, scores, MASKED)
        highest = jnp.max(scores, axis=-1, keepdims=True)
        exponent = jnp.exp(scores - highest)
        totals = jnp.sum(exponent, axis=-1, keepdims=True)
        attention = exponent * (1.0 / totals)
        low = attention.astype(bf16)
        out_ref[rows, lanes(0)] = dot_nn(low, values).astype(bf16)
        grad_att = dot_nt(grads, values).astype(bf16).astype(f32)
        weighted = jnp.sum(attention * grad_att, axis=-1, keepdims=True)
        grad_scores = (attention * (grad_att - weighted)).astype(bf16)
        grad_q = dot_nn(grad_scores, keys) * scale
        out_ref[rows, lanes(1)] = turn(
            grad_q, cos_ref[rows, :], up_ref[rows, :], down_ref[rows, :], -1.0
        ).astype(bf16)
        part_k = dot_tn(grad_scores, queries)
        part_v = dot_tn(low, grads)
        if begin > 0:
            dk_sum[0:begin, :] += part_k[0:begin]
            dv_sum[0:begin, :] += part_v[0:begin]
        dk_sum[begin:end, :] = part_k[begin:end]
        dv_sum[begin:end, :] = part_v[begin:end]
    grad_k = dk_sum[...] * scale
    out_ref[:, lanes(2)] = turn(grad_k, cos_ref[...], up_ref[...], down_ref[...], -1.0).astype(bf16)
    out_ref[:, lanes(3)] = dv_sum[...].astype(bf16)


def attend(packed, documents, tables, heads_each):
    length = packed.shape[0]
    block = min(256, length)
    whole = lambda h: (0, 0)

    def kind(at):
        return pl.BlockSpec((length, HDIM), lambda h: (0, at * heads_each + h))

    return pl.pallas_call(
        functools.partial(attend_kernel, block),
        grid=(heads_each,),
        in_specs=[kind(0), kind(1), kind(2), kind(3)]
        + [pl.BlockSpec((length, 1), whole), pl.BlockSpec((1, length), whole)]
        + [pl.BlockSpec((length, HDIM), whole)] * 3,
        out_specs=pl.BlockSpec((length, 4 * heads_each * HDIM), whole),
        out_shape=jax.ShapeDtypeStruct((length, 4 * heads_each * HDIM), bf16),
        scratch_shapes=[pltpu.VMEM((length, HDIM), f32)] * 2,
        compiler_params=pltpu.CompilerParams(vmem_limit_bytes=48 << 20),
        cost_estimate=spent(
            flops=9 * heads_each * length * length * HDIM,
            bytes_accessed=16 * length * heads_each * HDIM + 12 * length * HDIM,
            transcendentals=heads_each * length * length,
        ),
        name="attend",
    )(packed, packed, packed, packed, documents[:, None], documents[None, :], *tables)


def gelu_parts(values):
    cdf = 0.5 * (1.0 + lax.erf(values * (0.5**0.5)))
    density = jnp.exp(-0.5 * values * values) * (1.0 / math.sqrt(2.0 * math.pi))
    return values * cdf, cdf + values * density


def ff_kernel(
    model_ref, x_ref, cot_ref, up_ref, down_ref,
    hidden_ref, grad_ref, own_ref, other_ref,
):
    part = up_ref.shape[-1]
    half = up_ref.shape[1] // 2

    def rows_of(ref, which):
        return ref[0, pl.ds(which * half, half)].reshape(-1, part)

    own, other = model_ref[0], 1 - model_ref[0]
    up_pre = dot_nn(x_ref[...], up_ref[...].reshape(-1, part))
    hidden, slope = gelu_parts(up_pre)
    hidden = hidden.astype(bf16)
    grad_up = (dot_nn(cot_ref[0, 0], down_ref[...].reshape(-1, part)) * slope).astype(bf16)
    hidden_ref[...] = hidden
    grad_ref[...] = grad_up
    other_ref[0] = dot_nt(grad_up, rows_of(up_ref, other)).astype(bf16)
    own_ref[0] = dot_nt(grad_up, rows_of(up_ref, own))
    other_ref[1] = dot_nt(hidden, rows_of(down_ref, other)).astype(bf16)
    own_ref[1] = dot_nt(hidden, rows_of(down_ref, own))


def feed_forward(x, cot, micro_at, weights, which):
    tall, model = x.shape
    part = weights.shape[-1]
    width = model // 2
    rows = cot.shape[2]
    row = lambda i, m: (i, 0)

    def resident(kind):
        return pl.BlockSpec(
            (1,) + weights.shape[1:],
            lambda i, m: (kind, 0, 0, 0, 0),
            pipeline_mode=pl.Buffered(1),
        )

    return pl.pallas_call(
        ff_kernel,
        grid_spec=pltpu.PrefetchScalarGridSpec(
            num_scalar_prefetch=1,
            grid=(tall // rows,),
            in_specs=[
                pl.BlockSpec((rows, model), row),
                pl.BlockSpec((1, 1, rows, model), lambda i, m: (i, micro_at, 0, 0)),
                resident(0),
                resident(1),
            ],
            out_specs=[pl.BlockSpec((rows, part), row)] * 2
            + [pl.BlockSpec((2, rows, width), lambda i, m: (0, i, 0))] * 2,
        ),
        out_shape=[jax.ShapeDtypeStruct((tall, part), bf16)] * 2
        + [
            jax.ShapeDtypeStruct((2, tall, width), f32),
            jax.ShapeDtypeStruct((2, tall, width), bf16),
        ],
        compiler_params=pltpu.CompilerParams(vmem_limit_bytes=48 << 20),
        cost_estimate=spent(
            flops=8 * tall * model * part,
            bytes_accessed=4 * model * part + 16 * tall * model,
            transcendentals=2 * tall * part,
        ),
        name="feed_forward",
    )(which, x, cot, weights, weights)


def back_kernel(half_ref, ans_ref, wo_ref, wq_ref, wk_ref, wv_ref, out_ref, *flat):
    count, _, wide = ans_ref.shape
    span = wide // 4
    for kind, w_ref in enumerate((wo_ref, wq_ref, wk_ref, wv_ref)):
        total = None
        for j in range(count):
            term = dot_nt(
                ans_ref[j, :, kind * span : (kind + 1) * span],
                w_ref[:, :, :, :, j * span : (j + 1) * span].reshape(-1, span),
            )
            total = term if total is None else total + term
        out_ref[kind] = total.astype(out_ref.dtype)
    if flat:

        @pl.when(pl.program_id(0) == 0)
        def _():
            for kind in range(4):
                for j in range(count):
                    flat[0][kind, :, j * span : (j + 1) * span] = ans_ref[
                        j, :, kind * span : (kind + 1) * span
                    ]


def back_project(answer, weights, half, dtype, flat):
    count, rows, wide = answer.shape
    groups, _, _, own_rows, heads_width = weights.shape
    part = count * own_rows
    steps = groups // 2
    width = part * steps

    def matrix(kind):
        shape = (1, count, 1, own_rows, heads_width)
        return pl.BlockSpec(shape, lambda i, m: (m[0] * steps + i, 0, kind, 0, 0))

    out_specs = [pl.BlockSpec((4, rows, part), lambda i, m: (0, 0, i))]
    out_shape = [jax.ShapeDtypeStruct((4, rows, width), dtype)]
    if flat:
        out_specs.append(pl.BlockSpec((4, rows, heads_width), lambda i, m: (0, 0, 0)))
        out_shape.append(jax.ShapeDtypeStruct((4, rows, heads_width), bf16))
    return pl.pallas_call(
        back_kernel,
        grid_spec=pltpu.PrefetchScalarGridSpec(
            num_scalar_prefetch=1,
            grid=(steps,),
            in_specs=[pl.BlockSpec((count, rows, wide), lambda i, m: (0, 0, 0))]
            + [matrix(kind) for kind in (3, 0, 1, 2)],
            out_specs=out_specs,
        ),
        out_shape=out_shape,
        compiler_params=pltpu.CompilerParams(vmem_limit_bytes=40 << 20),
        cost_estimate=spent(
            flops=8 * rows * heads_width * width,
            bytes_accessed=8 * heads_width * width + 20 * rows * width,
            transcendentals=0,
        ),
        name="back_project",
    )(half, answer, *[weights] * 4)


def slope_kernel(
    model_ref, own_ref, got_ref, ff_ref, low_ref, stat_ref, gain_ref, scaled_ref, sum_ref, gain_out_ref
):
    _, rows, width = ff_ref.shape
    own_span, _ = own_spans(model_ref, width)
    lane = lax.broadcasted_iota(jnp.int32, (rows, 128), 1)
    packed = jnp.zeros((rows, 128), f32)
    totals = []
    for s in range(STREAMS):
        lanes = slice(s * width, (s + 1) * width)
        if s < 3:
            grad = own_ref[s + 1] + got_ref[s + 1].astype(f32)
        else:
            grad = ff_ref[0]
        average, inverse = stat_ref[:, 2 * s : 2 * s + 1], stat_ref[:, 2 * s + 1 : 2 * s + 2]
        hat = (low_ref[:, lanes].astype(f32) - average) * inverse
        totals.append(jnp.sum(grad * hat, axis=0, keepdims=True))
        scaled = grad * gain_ref[s : s + 1, own_span]
        scaled_ref[:, lanes] = scaled
        packed = jnp.where(lane == 2 * s, jnp.sum(scaled, axis=-1, keepdims=True), packed)
        packed = jnp.where(
            lane == 2 * s + 1, jnp.sum(scaled * hat, axis=-1, keepdims=True), packed
        )
    sum_ref[...] = packed
    totals = jnp.concatenate(totals, axis=0)

    @pl.when(pl.program_id(0) == 0)
    def _():
        gain_out_ref[...] = totals

    @pl.when(pl.program_id(0) > 0)
    def _():
        gain_out_ref[...] += totals


def norm_slopes(own, got, ff_grad, low, stats, gains, which):
    tall, wide = low.shape
    width = wide // STREAMS
    rows = min(128, tall)
    row = lambda i, m: (i, 0)
    cube = pl.BlockSpec((4, rows, width), lambda i, m: (0, i, 0))
    return pl.pallas_call(
        slope_kernel,
        grid_spec=pltpu.PrefetchScalarGridSpec(
            num_scalar_prefetch=1,
            grid=(tall // rows,),
            in_specs=[
                cube,
                cube,
                pl.BlockSpec((1, rows, width), lambda i, m: (0, i, 0)),
                pl.BlockSpec((rows, wide), row),
                pl.BlockSpec((rows, 128), row),
                pl.BlockSpec(gains.shape, lambda i, m: (0, 0)),
            ],
            out_specs=[
                pl.BlockSpec((rows, wide), row),
                pl.BlockSpec((rows, 128), row),
                pl.BlockSpec((STREAMS, width), lambda i, m: (0, 0)),
            ],
        ),
        out_shape=[
            jax.ShapeDtypeStruct((tall, wide), f32),
            jax.ShapeDtypeStruct((tall, 128), f32),
            jax.ShapeDtypeStruct((STREAMS, width), f32),
        ],
        cost_estimate=spent(
            flops=12 * tall * wide, bytes_accessed=12 * tall * wide, transcendentals=0
        ),
        compiler_params=pltpu.CompilerParams(vmem_limit_bytes=40 << 20),
        name="norm_slopes",
    )(which, own, got, ff_grad, low, stats, gains)


def grads_kernel(
    scaled_ref, mine_ref, theirs_ref, low_ref, stat_ref, cot_ref, cur_ref, last_ref,
    grad_ref, mix_ref, dot_ref,
):
    rows, width = cot_ref.shape
    lane = lax.broadcasted_iota(jnp.int32, (rows, 128), 1)
    means = (mine_ref[...] + theirs_ref[...]) / (2 * width)
    current = cur_ref[...].astype(f32)
    packed = jnp.zeros((rows, 128), f32)
    mixed = None
    for s in range(STREAMS):
        lanes = slice(s * width, (s + 1) * width)
        average, inverse = stat_ref[:, 2 * s : 2 * s + 1], stat_ref[:, 2 * s + 1 : 2 * s + 2]
        hat = (low_ref[:, lanes].astype(f32) - average) * inverse
        grad = inverse * (
            scaled_ref[:, lanes]
            - means[:, 2 * s : 2 * s + 1]
            - hat * means[:, 2 * s + 1 : 2 * s + 2]
        )
        if s == STREAMS - 1:
            grad = grad + cot_ref[...].astype(f32)
        grad = grad.astype(bf16)
        grad_ref[s] = grad
        grad = grad.astype(f32)
        term = last_ref[:, s : s + 1] * grad
        mixed = term if mixed is None else mixed + term
        packed = jnp.where(lane == s, jnp.sum(grad * current, axis=-1, keepdims=True), packed)
    mix_ref[...] = mixed
    dot_ref[...] = packed


def stream_grads(scaled, mine, theirs, low, stats, cot, current_half, last):
    tall, wide = low.shape
    width = wide // STREAMS
    rows = min(128, tall)
    row = lambda i: (i, 0)
    return pl.pallas_call(
        grads_kernel,
        grid=(tall // rows,),
        in_specs=[
            pl.BlockSpec((rows, wide), row),
            pl.BlockSpec((rows, 128), row),
            pl.BlockSpec((rows, 128), row),
            pl.BlockSpec((rows, wide), row),
            pl.BlockSpec((rows, 128), row),
            pl.BlockSpec((rows, width), row),
            pl.BlockSpec((rows, width), row),
            pl.BlockSpec((rows, 128), row),
        ],
        out_specs=[
            pl.BlockSpec((STREAMS, rows, width), lambda i: (0, i, 0)),
            pl.BlockSpec((rows, width), row),
            pl.BlockSpec((rows, 128), row),
        ],
        out_shape=[
            jax.ShapeDtypeStruct((STREAMS, tall, width), bf16),
            jax.ShapeDtypeStruct((tall, width), f32),
            jax.ShapeDtypeStruct((tall, 128), f32),
        ],
        cost_estimate=spent(
            flops=12 * tall * wide, bytes_accessed=10 * tall * wide, transcendentals=0
        ),
        compiler_params=pltpu.CompilerParams(vmem_limit_bytes=40 << 20),
        name="stream_grads",
    )(scaled, mine, theirs, low, stats, cot, current_half, last)


def turning_tables(places):
    half = ROT // 2
    inverse = jnp.exp(jnp.arange(half, dtype=f32) * (-2.0 * math.log(10000.0) / ROT))
    angles = places.astype(f32)[:, None] * inverse[None, :]
    cosine, sine = jnp.cos(angles), jnp.sin(angles)
    rows = places.shape[0]
    rest = jnp.zeros((rows, HDIM - ROT), f32)
    blank = jnp.zeros((rows, half), f32)
    return (
        jnp.concatenate([cosine, cosine, rest + 1.0], axis=1),
        jnp.concatenate([-sine, blank, rest], axis=1),
        jnp.concatenate([blank, sine, rest], axis=1),
    )


def local(
    history,
    slot_layer,
    current,
    positions,
    doc_ids,
    cotangent,
    norm_gains,
    generator_in,
    generator_out,
    query_weight,
    key_weight,
    value_weight,
    out_weight,
    up_weight,
    down_weight,
):
    dp_count = lax.axis_size("dp")
    depth_count = lax.axis_size("depth")
    dp_at = lax.axis_index("dp")
    model_at = lax.axis_index("mp")
    dp_bits = list(range(bit_count(dp_count)))
    slots, tokens_held, width = history.shape
    model = current.shape[1]
    rows_mb = current.shape[0] // MB
    length = depth_count * rows_mb
    heads_width = query_weight.shape[1]
    heads_each = heads_width // HDIM // depth_count
    own_rows = query_weight.shape[0]
    ff_width = up_weight.shape[1]
    ff_part = ff_width // dp_count
    both = ("dp", "depth")

    def half_of(values, axis, which):
        return lax.dynamic_slice_in_dim(values, which * width, width, axis)

    partners = jnp.stack([dp_at ^ m for m in range(dp_count)]).astype(jnp.int32)
    ff_local = ff_split(up_weight, down_weight, partners)
    small_cols = jnp.concatenate(
        [generator_in, norm_gains.T, jnp.zeros((own_rows, 128 - GEN - 5), bf16)], axis=1
    )
    small_all = gather_small(small_cols, both).reshape(model, 128)
    gen_first = small_all[:, :GEN]
    gen_first, ff_local = fence(gen_first, ff_local)
    ff_rows = [ff_local[0]] + [swap_mask(ff_local[m], "dp", m) for m in range(1, dp_count)]
    ff_rows = place_many(partners, ff_rows).reshape(2 * dp_count, own_rows, ff_part)

    gain_float = small_all[:, GEN : GEN + 5].astype(f32).T
    second_rows = generator_out.shape[0]
    second_pad = -second_rows % 128
    second_all = gather_small(jnp.pad(generator_out, (0, second_pad))[None], both)
    gen_second = second_all.reshape(-1, second_rows + second_pad)[:, :second_rows]
    second_low = gen_second.reshape(GEN, STREAMS * MIX)

    stacked = jnp.concatenate([query_weight, key_weight, value_weight, out_weight.T], axis=0)
    over_depth = lax.all_gather(stacked, "depth", axis=0, tiled=True)
    current_f = current.astype(f32)
    current_half = half_of(current, 1, model_at)
    mean_square = jnp.mean(current_f * current_f, axis=-1, keepdims=True)
    inverse_rms = lax.rsqrt(mean_square + RMS_EPSILON)
    unit = current_f * inverse_rms
    gen_normed = (unit * gain_float[4]).astype(bf16)
    gen_pre = dot_nn(gen_normed, gen_first)
    gen_hidden = gelu_exact(gen_pre).astype(bf16)
    column = jnp.arange(STREAMS * MIX)
    last_col = (column % MIX == MIX - 1).astype(f32)
    mixing = (dot_nn(gen_hidden, second_low) + last_col).astype(bf16)
    pick_last = (column[:, None] == (jnp.arange(128) * MIX + MIX - 1)[None, :]).astype(bf16)
    last = dot_nn(mixing, pick_last)

    layer_of = jnp.tile(slot_layer, STREAMS)
    stream_of = jnp.repeat(jnp.arange(STREAMS), slots)
    from_col = jnp.where(layer_of < MIX, stream_of * MIX + layer_of, -1)
    pick = (column[:, None] == from_col[None, :]).astype(f32)
    mix_all = gather_small(mixing, ("depth",)).reshape(depth_count * MB * rows_mb, STREAMS * MIX)
    slot_mix = dot_nn(mix_all, pick.astype(bf16))
    places_all = gather_small(positions, ("depth",))

    def over_depth_swap(values):
        return lax.all_to_all(values, "depth", 0, 0, tiled=True)

    def mix_part(micro_at, slot_mix):
        partial = mix_streams(slot_mix, history, micro_at, depth_count, rows_mb)
        return partial.reshape(STREAMS, depth_count, rows_mb, width)

    slot_mix, ff_rows, cotangent, places_all = fence(slot_mix, ff_rows, cotangent, places_all)
    partial = mix_part(0, slot_mix)
    partial_next = mix_part(1, slot_mix)

    weights_line = LineGather(ff_rows)
    weights_line.step()
    cot_pieces = lax.all_gather(cotangent, "dp", axis=0, tiled=True)
    over_depth, partial, partial_next = weights_line.hold(over_depth, partial, partial_next)
    pieces = [over_depth]
    weights = place_block(None, pieces[0][None], place_index(0), dp_count)
    hops_left = [(p, at) for at in range(len(dp_bits)) for p in range(1 << at)]
    placed = 1
    cots = None
    sums, sums_next = LineScatter(partial), LineScatter(partial_next)
    own_tables = turning_tables(positions)
    tables = [
        turning_tables(places_all[:, m * rows_mb : (m + 1) * rows_mb].reshape(length))
        for m in range(MB)
    ]
    for hop in range(1, depth_count):
        sums.step_with(weights_line)
        last_hop = hop == depth_count - 1
        for place in range(placed, len(pieces)):
            weights = place_block(weights, pieces[place][None], place_index(place), dp_count)
        placed = len(pieces)
        while hops_left:
            place, at = hops_left.pop(0)
            pieces.append(core_hop(pieces[place], at))
            if len(hops_left) <= depth_count - 1 - hop:
                break
        if last_hop:
            cot_full = join_halves(cotangent, other_core(cotangent), model_at)
            ff_weights = weights_line.placed()
            cots = cot_full, cotangent, ff_weights
        (state,) = weights_line.hold(
            (sums.up, sums.down, pieces, weights, cots, own_tables, tables, cot_pieces)
        )
        sums.up, sums.down, pieces, weights, cots, own_tables, tables, cot_pieces = state
    cot_full, cotangent, ff_weights = cots
    for place in range(placed, len(pieces)):
        weights = place_block(weights, pieces[place][None], place_index(place), dp_count)
    weights = weights.reshape(dp_count, depth_count, 4, own_rows, heads_width)
    ff_weights = ff_weights.reshape(2, dp_count, depth_count, own_rows, ff_part)

    document_view = doc_ids.reshape(depth_count, MB, rows_mb)
    which = model_at.astype(jnp.int32)[None]
    depth_at = lax.axis_index("depth").astype(jnp.int32)[None]
    gains = gain_float

    def enter(micro_at, sums):
        span = slice(micro_at * rows_mb, (micro_at + 1) * rows_mb)
        low, resid = total_streams(sums, current_half[span], last[span], depth_at)
        normed, ff_normed, stats = norm_streams(low, other_core(low), gains, which)
        packed = project_heads(
            normed,
            cot_full[span],
            weights,
            [t[span] for t in own_tables],
            depth_count,
        )
        return dict(
            low=low, resid=resid, normed=normed, ff_normed=ff_normed, stats=stats, packed=packed
        )

    def attention(micro_at, by_head):
        documents = document_view[:, micro_at].reshape(length)
        by_head = by_head.reshape(length, 4 * heads_each * HDIM)
        answer = attend(by_head, documents, tables[micro_at], heads_each)
        return answer.reshape(depth_count, rows_mb, 4 * heads_each * HDIM)

    place_list = jnp.stack([place_index(p) for p in range(dp_count)]).astype(jnp.int32)

    def group_rows(ff_normed):
        return lax.all_gather(ff_normed, "dp", axis=0, tiled=True)

    def group_joined(mine):
        return join_halves(mine, other_core(mine), model_at)

    def hidden_units(micro_at, group_normed):
        hidden, grad_up, own, other = feed_forward(
            group_normed, cot_group, micro_at, ff_weights, which
        )
        return dict(group_normed=group_normed, hidden=hidden, grad_up=grad_up), (own, other)

    def group_back_rest(near):
        for at in reversed(range(len(dp_bits) - 1)):
            half = 1 << at
            near = near[:half] + core_hop(near[half:].astype(bf16), at).astype(f32)
        return near[0]

    def group_back(own, other):
        near, far = group_split(own, other, place_list)
        return group_back_rest(near + core_hop(far, len(dp_bits) - 1).astype(f32))

    def back(kept, answer):
        (theirs,) = back_project(answer, weights, 1 - which, bf16, False)
        got = other_core(theirs)
        own, flat = back_project(answer, weights, which, f32, True)
        return own, got, flat

    def leave(micro_at, kept, own, got, ff_sum):
        span = slice(micro_at * rows_mb, (micro_at + 1) * rows_mb)
        rows = (kept["resid"] + own[0] + got[0].astype(f32) + ff_sum[1]).astype(bf16)
        low, stats = kept["low"], kept["stats"]
        scaled, sums, gain_part = norm_slopes(own, got, ff_sum, low, stats, gains, which)
        grad_low, current_mix, last_dot = stream_grads(
            scaled, sums, other_core(sums), low, stats, cotangent[span], current_half[span], last[span]
        )
        kept.update(layer_rows=rows, gain=gain_part, current_mix=current_mix, last_dot=last_dot)
        return grad_low

    ((sums.up, sums.down),) = sums_next.step((sums.up, sums.down))
    first = enter(0, sums)
    mine = group_rows(first["ff_normed"])
    packed, mine, cot_pieces = sums_next.hold(first["packed"], mine, cot_pieces)
    while sums_next.at < depth_count - 3:
        sums_next.step()
        sums_next.hold()
    packed, mine, cot_pieces = sums_next.step(packed, mine, cot_pieces)
    by_head = over_depth_swap(packed)
    cot_group = join_halves(cot_pieces, other_core(cot_pieces), model_at)
    cot_group = cot_group.reshape(dp_count, MB, rows_mb, model)
    kept, ff_parts = hidden_units(0, group_joined(mine))
    first.update(kept)
    by_head, ff_parts, cot_group = sums_next.hold(by_head, ff_parts, cot_group)
    by_head, ff_parts = sums_next.step(by_head, ff_parts)
    answer = attention(0, by_head)
    answer, ff_parts = sums_next.hold(answer, ff_parts)

    answer = over_depth_swap(answer)
    second = enter(1, sums_next)
    near, far = group_split(ff_parts[0], other_core(ff_parts[1]), place_list)
    near = near + core_hop(far, len(dp_bits) - 1).astype(f32)
    answer, packed, ff_normed, near = fence(
        answer, second["packed"], second["ff_normed"], near
    )
    by_head = over_depth_swap(packed)
    mine = group_rows(ff_normed)
    own, got, first["flat"] = back(first, answer)
    grad_low = leave(0, first, own, got, group_back_rest(near))
    by_head, grad_low, mine, first["layer_rows"] = fence(
        by_head, grad_low, mine, first["layer_rows"]
    )
    saved = [first, second]

    def each(name):
        return [s[name] for s in saved]

    def rows_of(name):
        return jnp.concatenate(each(name), axis=0)

    def place_grads(place, dtype):
        return attention_grads(
            each("normed"),
            cot_full,
            each("flat"),
            place_list[place : place + 1],
            depth_count,
            dp_count,
            dtype,
        )

    half = dp_count // 2
    hops_left = [
        (p, at) for at in reversed(range(len(dp_bits))) for p in range(1 << at, 2 << at)
    ]
    pieces = {}

    def sums_hop():
        place, at = hops_left.pop(0)
        arrived = core_hop(pieces.pop(place), at)
        target = place - (1 << at)
        pieces[target] = (pieces[target].astype(f32) + arrived.astype(f32)).astype(bf16)

    grad_line = LineGather(grad_low)
    grad_line.step()
    answer = attention(1, by_head)
    kept, ff_parts = hidden_units(1, group_joined(mine))
    second.update(kept)
    answer, ff_parts = grad_line.hold(answer, ff_parts)
    answer = over_depth_swap(answer)
    near, far = group_split(ff_parts[0], other_core(ff_parts[1]), place_list)
    ff_products = hidden_grads(
        each("group_normed"), cot_group, each("grad_up"), each("hidden"), dp_count, depth_count
    )
    near = near + core_hop(far, len(dp_bits) - 1).astype(f32)
    answer, near, ff_products = fence(answer, near, ff_products)

    ff_sums = LineScatter(ff_products)
    (answer,) = ff_sums.step_with(grad_line, answer)
    own, got, flat = back(second, answer)
    ff_sum = group_back_rest(near)
    second["flat"] = flat
    (state,) = grad_line.hold((ff_sums.up, ff_sums.down, own, got, flat, ff_sum))
    ff_sums.up, ff_sums.down, own, got, second["flat"], ff_sum = state
    while len(grad_line.up) < depth_count - 1:
        ff_sums.step_with(grad_line)
        (state,) = grad_line.hold((ff_sums.up, ff_sums.down))
        ff_sums.up, ff_sums.down = state
    (ff_sum,) = ff_sums.step_with(grad_line, ff_sum)
    grad_low = leave(1, second, own, got, ff_sum)
    pieces = {p: place_grads(p, bf16) for p in range(dp_count)}
    sums_hop()
    (state,) = grad_line.hold((ff_sums.up, ff_sums.down, grad_low, pieces))
    ff_sums.up, ff_sums.down, grad_low, pieces = state

    last_line = LineGather(grad_low)
    last_line.step()
    if hops_left:
        sums_hop()
    grad_first = grad_line.placed().reshape(STREAMS, length, width)
    history_grad, slot_part = unmix_streams(
        slot_mix, history, grad_first, 0, depth_count, rows_mb, None
    )
    slot_parts = [slot_part.reshape(depth_count, 1, rows_mb, 128)]
    pieces, history_grad, second["layer_rows"] = last_line.hold(
        pieces, history_grad, second["layer_rows"]
    )
    (pieces,) = ff_sums.step(pieces)
    while hops_left:
        sums_hop()
    (pieces,) = ff_sums.hold(pieces)
    out_sums = LineScatter(pieces[0].reshape(1, depth_count, 4 * own_rows, heads_width))
    for hop in range(2, depth_count):
        last_line.step()
        ((ff_sums.up, ff_sums.down),) = out_sums.step((ff_sums.up, ff_sums.down))
        if hop == depth_count - 1:
            ff_sums.up = ff_sums.down = end_sums(ff_sums, bf16)
            early = last_line.placed_early()
            history_grad, slot_part = unmix_streams(
                slot_mix,
                history,
                early.reshape(STREAMS, length, width),
                1,
                depth_count,
                rows_mb,
                history_grad,
            )
        (state,) = last_line.hold(
            (out_sums.up, out_sums.down, ff_sums.up, ff_sums.down, history_grad, slot_part)
        )
        out_sums.up, out_sums.down, ff_sums.up, ff_sums.down, history_grad, slot_part = state
    early, ff_grads = out_sums.step(early, ff_sums.up)
    ff_grads = ff_grads.reshape(2, dp_count, own_rows, ff_part)
    ff_pieces = [
        lax.dynamic_index_in_dim(ff_grads, partners[m], 1, keepdims=False) for m in range(dp_count)
    ]
    ff_pieces = ff_pieces[:1] + [swap_mask(ff_pieces[m], "dp", m) for m in range(1, dp_count)]
    far_grads, far_index = last_line.farthest(early)
    history_grad, far_part = unmix_one(
        slot_mix, history, far_grads, 1, far_index, rows_mb, history_grad
    )
    slot_part = slot_part.reshape(depth_count, rows_mb, 128)
    slot_part = lax.dynamic_update_index_in_dim(slot_part, far_part, far_index, 0)
    slot_parts.append(slot_part[:, None])

    slot_grads = jnp.concatenate(slot_parts, axis=1).reshape(-1, 128)[:, : STREAMS * slots]
    mix_grads = dot_exact(slot_grads, pick.T).reshape(depth_count, MB * rows_mb, STREAMS * MIX)
    mix_grads, ff_pieces = out_sums.hold(mix_grads, ff_pieces)
    grad_mixing = scatter_small(mix_grads, ("depth",))
    up_grad, down_grad = ff_join(jnp.stack(ff_pieces), partners)
    last_dots = rows_of("last_dot")
    grad_mixing = grad_mixing + dot_exact(last_dots, pick_last.astype(f32).T)
    grad_mixing = grad_mixing + other_core(grad_mixing)

    second_float = second_low.astype(f32)
    grad_second = dot_exact(gen_hidden.astype(f32).T, grad_mixing)
    grad_pre = dot_exact(grad_mixing, second_float.T) * gelu_slope(gen_pre)
    grad_first = dot_exact(gen_normed.astype(f32).T, grad_pre)
    grad_gen_normed = dot_exact(grad_pre, gen_first.astype(f32).T)
    gain_gen = jnp.sum(grad_gen_normed * unit, axis=0)
    scattered = end_sums(out_sums, f32).reshape(4, own_rows, heads_width)
    grad_unit = grad_gen_normed * gain_float[4]
    shared = jnp.mean(grad_unit * unit, axis=-1, keepdims=True)
    current_gen = half_of(inverse_rms * (grad_unit - unit * shared), 1, model_at)
    current_grad = rows_of("current_mix") + current_gen

    gain_own = sum(s["gain"] for s in saved)
    gain_other = other_core(gain_own)
    gain_all = jnp.where(
        model_at == 0,
        jnp.concatenate([gain_own, gain_other], axis=1),
        jnp.concatenate([gain_other, gain_own], axis=1),
    )
    gain_all = jnp.concatenate([gain_all, gain_gen[None]], axis=0)
    small_grads = jnp.concatenate(
        [grad_first, gain_all.T, jnp.zeros((model, 128 - GEN - 5), f32)], axis=1
    )
    small_grads = scatter_small(small_grads.reshape(-1, own_rows, 128), both)
    second_grads = jnp.pad(grad_second.reshape(-1, second_rows), ((0, 0), (0, second_pad)))
    second_grads = scatter_small(second_grads[:, None], both)

    return (
        rows_of("layer_rows"),
        history_grad,
        current_grad,
        small_grads[:, GEN : GEN + 5].T,
        small_grads[:, :GEN],
        second_grads[0, :second_rows],
        scattered[0],
        scattered[1],
        scattered[2],
        scattered[3].T,
        up_grad,
        down_grad,
    )


def solution(mesh):
    return jax.shard_map(
        local,
        mesh=mesh,
        in_specs=(
            P("depth", "dp", "mp"),
            P("depth"),
            P(("dp", "depth"), None),
            P(("dp", "depth")),
            P("dp"),
            P(("dp", "depth"), "mp"),
            P(None, ("dp", "depth")),
            P(("dp", "depth"), None),
            P(("dp", "depth")),
            P(("dp", "depth"), "mp"),
            P(("dp", "depth"), "mp"),
            P(("dp", "depth"), "mp"),
            P("mp", ("dp", "depth")),
            P(("dp", "depth"), "mp"),
            P("mp", ("dp", "depth")),
        ),
        out_specs=(
            P(("dp", "depth"), "mp"),
            P("depth", "dp", "mp"),
            P(("dp", "depth"), "mp"),
            P(None, ("dp", "depth")),
            P(("dp", "depth"), None),
            P(("dp", "depth")),
            P(("dp", "depth"), "mp"),
            P(("dp", "depth"), "mp"),
            P(("dp", "depth"), "mp"),
            P("mp", ("dp", "depth")),
            P(("dp", "depth"), "mp"),
            P("mp", ("dp", "depth")),
        ),
        check_vma=False,
    )
```
